32 devices in a mesh: section: 2 (over x), dp: 4 (over y, core), tensor: 4 (over z).
Axes of the slice: x: 2, y: 2, z: 4, core: 2. Of those that a mesh axis runs over, the one named last changes fastest.
Arguments:
- inputs: bfloat16 [8, 1024, 1024], P('dp', 'tensor'), may hold values from -6 to 6
- out_cotangent: bfloat16 [8, 1024, 1024], P('dp', 'tensor'), may hold values from -6 to 6
- group_ids: int32 [8, 1024], P('dp', 'tensor'), may hold values from 0 to 7
- group_weights: float32 [8], replicated, may hold values from 0.25 to 4
- gains: float32 [2, 4, 1024], P('section'), may hold values from 0.1 to 1.9
- qkv_weight: bfloat16 [2, 1024, 3, 1024], P('section', None, None, 'tensor'), may hold values from -0.1875 to 0.1875
- out_weight: bfloat16 [2, 1024, 1024], P('section', 'tensor'), may hold values from -0.1875 to 0.1875
- up_weight: bfloat16 [2, 1024, 4096], P('section', None, 'tensor'), may hold values from -0.1875 to 0.1875
- down_weight: bfloat16 [2, 4096, 1024], P('section', 'tensor'), may hold values from -0.09375 to 0.09375
Outputs:
- layer_outputs: bfloat16 [2, 8, 1024, 1024], P('section', 'dp', 'tensor')
- input_grads: bfloat16 [2, 8, 1024, 1024], P('section', 'dp', 'tensor')
- gains_grad: float32 [2, 4, 1024], P('section', None, ('dp', 'tensor'))
- qkv_grad: float32 [2, 1024, 3, 1024], P('section', 'dp', None, 'tensor')
- out_grad: float32 [2, 1024, 1024], P('section', 'tensor', 'dp')
- up_grad: float32 [2, 1024, 4096], P('section', 'dp', 'tensor')
- down_grad: float32 [2, 4096, 1024], P('section', 'tensor', 'dp')
The draws below stay inside these ranges and needn't reach their ends.
All inputs are finite; a program needn't handle non-finite values.
Results may differ from the reference program's by a relative error of at most 0.02.
Values may be sent and summed in bfloat16 or wider, within the bound.
No kernel may reach another device: no remote copies, remote signals or barrier semaphores. Data moves between devices by JAX's collectives and lax.ppermute only.
A program may use at most 192 MiB of HBM per device.

```python
import math
import jax
import jax.numpy as jnp
from jax import lax

D = 1024
HEAD_DIM = 64
FF = 4096
LEN = 1024
GROUPS = 8
HD = 1024
SEQS = 8


def touch_ends(values, stream_key, low, top_value):
    extent = values.shape
    index_at = [jax.random.randint(jax.random.fold_in(stream_key, axis), (), 0, extent[axis]) for axis in range(len(extent))]
    values = values.at[tuple(index_at)].set(low)
    longest = extent.index(max(extent))
    index_at[longest] = (index_at[longest] + 1) % extent[longest]
    return values.at[tuple(index_at)].set(top_value)


def steps_of(key, shape, cuts, low, high):
    def one(axis_at, blocks):
        heights = jax.random.uniform(jax.random.fold_in(jax.random.fold_in(key, 6), axis_at), (blocks,), jnp.float32, low / len(cuts), high / len(cuts))
        return jnp.repeat(jnp.exp(heights), shape[axis_at] // blocks).reshape((-1,) + (1,) * (len(shape) - axis_at - 1))

    loudness = one(*cuts[0])
    for cut in cuts[1:]:
        loudness = loudness * one(*cut)
    return loudness


def noise(rng, dims, scale, limit, pieces=(), kind=jnp.bfloat16):
    values = jax.random.normal(rng, dims, jnp.float32) * scale
    if len(pieces) > 0:
        values = steps_of(rng, dims, pieces, -0.22, 0.18) * values
    return jnp.clip(values, min=-limit, max=limit).astype(kind)


def setup_inputs(seed: int = 0) -> dict:
    key_list = jax.random.split(jax.random.key(seed), 10)
    return {
        "inputs": noise(key_list[0], (SEQS, LEN, D), 1.0, 6.0, ((0, 4), (1, 4))),
        "out_cotangent": noise(key_list[1], (SEQS, LEN, D), 1.0, 6.0, ((0, 4), (1, 4))),
        "group_ids": touch_ends(jax.random.randint(key_list[2], (SEQS, LEN), 0, GROUPS), jax.random.fold_in(key_list[2], 1), 0, GROUPS - 1).astype(jnp.int32),
        "group_weights": jnp.clip(jnp.exp(jax.random.uniform(key_list[3], (GROUPS,), jnp.float32, math.log(0.25), math.log(4.0))), 0.25, 4.0),
        "gains": jnp.clip(1.0 + 0.18 * jax.random.normal(key_list[4], (2, 4, D), jnp.float32), 0.1, 1.9),
        "qkv_weight": noise(key_list[5], (2, D, 3, HD), D ** -0.5, 0.1875, ((0, 2), (3, 4))),
        "out_weight": noise(key_list[6], (2, HD, D), HD ** -0.5, 0.1875, ((0, 2), (1, 4))),
        "up_weight": noise(key_list[7], (2, D, FF), D ** -0.5, 0.1875, ((0, 2), (2, 4))),
        "down_weight": noise(key_list[8], (2, FF, D), FF ** -0.5, 0.09375, ((0, 2), (1, 4))),
    }


NORM_EPSILON = 1e-06
PRECISE = lax.Precision.HIGHEST

@jax.custom_vjp
def low(v):
    return lax.optimization_barrier(v.astype(jnp.bfloat16)).astype(jnp.float32)

@jax.custom_vjp
def low_back(v):
    return v

def low_keep(v):
    return (low(v), None)

def low_pass(kept, grad):
    return (grad,)

def back_keep(v):
    return (v, None)

def back_low(kept, grad):
    return (low(grad),)
low.defvjp(low_keep, low_pass)
low_back.defvjp(back_keep, back_low)

def norm_rows(vector, weight_gain):
    return vector * lax.rsqrt(lax.optimization_barrier(jnp.mean(vector * vector, axis=-1, keepdims=True)) + NORM_EPSILON) * weight_gain

def rotary_tables(seq_len, head_width):
    half_width = head_width // 2
    freqs = 10000.0 ** (-2.0 * jnp.arange(half_width, dtype=jnp.float32) / head_width)
    angles = jnp.arange(seq_len, dtype=jnp.float32)[:, None] * freqs[None, :]
    return (jnp.cos(angles), jnp.sin(angles))

def rotate(vector, cos_table, sin_table):
    first_half, second_half = jnp.split(vector, 2, axis=-1)
    cos_part = cos_table[:, None, :]
    sin_part = sin_table[:, None, :]
    return jnp.concatenate([first_half * cos_part - second_half * sin_part, second_half * cos_part + first_half * sin_part], axis=-1)

def layer(seq_input, params):
    gains, w_qkv, w_out, w_up, w_down = params
    length = seq_input.shape[0]
    model_width = seq_input.shape[1]
    head_count = w_qkv.shape[2] // HEAD_DIM
    attn_in = low(norm_rows(seq_input, gains[0]))
    qkv = low_back(jnp.dot(attn_in, w_qkv.reshape(model_width, -1), precision=PRECISE))
    qkv = qkv.reshape(length, 3, head_count, HEAD_DIM)
    cos_table, sin_table = rotary_tables(length, HEAD_DIM)
    queries = low(rotate(qkv[:, 0], cos_table, sin_table))
    key_rows = low(rotate(qkv[:, 1], cos_table, sin_table))
    values = low(qkv[:, 2])
    scores = low_back(jnp.einsum('qhd,khd->hqk', queries, key_rows, precision=PRECISE) * HEAD_DIM ** (-0.5))
    positions = jnp.arange(length, dtype=jnp.int32)
    causal = positions[:, None] >= positions[None, :]
    scores = jnp.where(causal[None], scores, -1e+30)
    shifted = scores - lax.optimization_barrier(jnp.max(scores, axis=-1, keepdims=True))
    expos = jnp.exp(shifted)
    attn_probs = low(expos / lax.optimization_barrier(jnp.sum(expos, axis=-1, keepdims=True)))
    mixed = jnp.einsum('hqk,khd->qhd', attn_probs, values, precision=PRECISE).reshape(length, -1)
    mixed = low_back(low(mixed))
    attn_branch = low_back(jnp.dot(mixed, w_out, precision=PRECISE))
    hidden = seq_input + norm_rows(attn_branch, gains[1])
    mlp_in = low(norm_rows(hidden, gains[2]))
    up_act = low_back(jnp.dot(mlp_in, w_up, precision=PRECISE))
    gelu_out = low(jax.nn.gelu(up_act, approximate=True))
    down_branch = low_back(jnp.dot(gelu_out, w_down, precision=PRECISE))
    return hidden + norm_rows(down_branch, gains[3])

def reference(inputs, out_cotangent, group_ids, group_weights, gains, qkv_weight, out_weight, up_weight, down_weight):
    params = tuple((weight.astype(jnp.float32) for weight in (gains, qkv_weight, out_weight, up_weight, down_weight)))
    section_zero = tuple((weight[0] for weight in params))
    section_one = tuple((weight[1] for weight in params))
    row_scale = group_weights.astype(jnp.float32)[group_ids]
    scaled = out_cotangent.astype(jnp.float32) * row_scale[..., None]

    def full_model(seq_input, probe, params_zero, params_one):
        first_out = layer(seq_input, params_zero)
        passed = low_back(low(first_out))
        return (layer(passed + probe, params_one), first_out)

    def one_sequence(totals, step_item):
        seq_input, cotangent = step_item
        probe = jnp.zeros_like(seq_input)
        result, pullback, first_out = jax.vjp(full_model, seq_input, probe, section_zero, section_one, has_aux=True)
        grad_input, grad_probe, grads_zero, grads_one = pullback(cotangent)
        totals = jax.tree.map(lambda total, left, right: total + jnp.stack([left, right]), totals, grads_zero, grads_one)
        return (totals, (first_out.astype(jnp.bfloat16), result.astype(jnp.bfloat16), grad_probe.astype(jnp.bfloat16), grad_input.astype(jnp.bfloat16)))
    start_totals = tuple((jnp.zeros_like(weight) for weight in params))
    totals, stacked = lax.scan(one_sequence, start_totals, (inputs.astype(jnp.float32), scaled))
    first_outs, second_outs, second_grads, first_grads = stacked
    layer_outputs = jnp.stack([first_outs, second_outs])
    input_grads = jnp.stack([first_grads, second_grads])
    return (layer_outputs, input_grads, totals[0], totals[1], totals[2], totals[3], totals[4])
```

```python
import math

import jax
import jax.numpy as jnp
from jax import lax
from jax.experimental import pallas as pl
from jax.experimental.pallas import tpu as pltpu
from jax.sharding import PartitionSpec as P

HEAD_DIM = 64


NORM_EPSILON = 1e-06
TILE = 128
KERNEL_VMEM = 32 << 20


def shifted(block, axis, distance):
    devices = range(lax.axis_size(axis))
    route = [(i - distance, i) for i in devices if i - distance in devices]
    return lax.ppermute(block, axis, route)


def norm_rows(vector, weight_gain):
    return (
        vector
        * lax.rsqrt(jnp.mean(vector * vector, axis=-1, keepdims=True) + NORM_EPSILON)
        * weight_gain
    )


def rotary_tables(seq_len, head_width):
    half_width = head_width // 2
    freqs = 10000.0 ** (-2.0 * jnp.arange(half_width, dtype=jnp.float32) / head_width)
    angles = jnp.arange(seq_len, dtype=jnp.float32)[:, None] * freqs[None, :]
    return (jnp.cos(angles), jnp.sin(angles))


def rotate(vector, cos_table, sin_table):
    first_half, second_half = jnp.split(vector, 2, axis=-1)
    cos_part = cos_table[:, None, :]
    sin_part = sin_table[:, None, :]
    return jnp.concatenate(
        [
            first_half * cos_part - second_half * sin_part,
            second_half * cos_part + first_half * sin_part,
        ],
        axis=-1,
    )


def contract(left_rows, right_rows):
    return lax.dot_general(
        left_rows, right_rows, (((0,), (0,)), ((), ())), preferred_element_type=jnp.float32
    )


def gather_rows(row_values, weight):

    def project(shard_rows, offset):
        return (shard_rows, jnp.dot(shard_rows, weight, preferred_element_type=jnp.float32))

    return project(lax.all_gather(row_values, "tensor", axis=0, tiled=True), jnp.int32(0))


def scatter_rows(row_values, weight, row_count):

    def partial_term(offset, span):
        return jnp.dot(row_values, weight, preferred_element_type=jnp.float32)

    return lax.psum_scatter(
        partial_term(jnp.int32(0), lax.axis_size("tensor") * row_count),
        "tensor",
        scatter_dimension=0,
        tiled=True,
    )


def gather_grads(row_values, weight):

    def project(shard_rows, offset):
        return (shard_rows, jnp.dot(shard_rows, weight.T, preferred_element_type=jnp.float32))

    return project(lax.all_gather(row_values, "tensor", axis=0, tiled=True), jnp.int32(0))


def scatter_grads(row_values, weight, row_count):

    def partial_term(offset, span):
        return jnp.dot(row_values, weight.T, preferred_element_type=jnp.float32)

    return lax.psum_scatter(
        partial_term(jnp.int32(0), lax.axis_size("tensor") * row_count),
        "tensor",
        scatter_dimension=0,
        tiled=True,
    )


def attention_probs(queries, key_rows):
    scores = jnp.einsum(
        "qhd,khd->hqk", queries, key_rows, preferred_element_type=jnp.float32
    ) * HEAD_DIM ** (-0.5)
    length = queries.shape[0]
    positions = jnp.arange(length, dtype=jnp.int32)
    causal = positions[:, None] >= positions[None, :]
    scores = jnp.where(causal[None], scores, -1e30)
    expos = jnp.exp(scores - jnp.max(scores, axis=-1, keepdims=True))
    return expos / jnp.sum(expos, axis=-1, keepdims=True)


def layer_forward(layer_input, weights):
    gains, w_qkv, w_out, w_up, w_down = weights
    row_count, model_width = layer_input.shape
    attn_in = norm_rows(layer_input, gains[0]).astype(jnp.bfloat16)
    gathered_a, qkv = gather_rows(attn_in, w_qkv.reshape(model_width, -1))
    length = qkv.shape[0]
    head_count = w_qkv.shape[2] // HEAD_DIM
    qkv = qkv.reshape(length, 3, head_count, HEAD_DIM)
    cos_table, sin_table = rotary_tables(length, HEAD_DIM)
    queries = rotate(qkv[:, 0], cos_table, sin_table).astype(jnp.bfloat16)
    key_rows = rotate(qkv[:, 1], cos_table, sin_table).astype(jnp.bfloat16)
    values = qkv[:, 2].astype(jnp.bfloat16)
    attn_probs = attention_probs(queries, key_rows).astype(jnp.bfloat16)
    mixed = jnp.einsum("hqk,khd->qhd", attn_probs, values, preferred_element_type=jnp.float32)
    mixed = mixed.reshape(length, -1).astype(jnp.bfloat16)
    attn_branch = scatter_rows(mixed, w_out, row_count)
    hidden = layer_input + norm_rows(attn_branch, gains[1])
    mlp_in = norm_rows(hidden, gains[2]).astype(jnp.bfloat16)
    gathered_c, up_act = gather_rows(mlp_in, w_up)
    gelu_out = jax.nn.gelu(up_act, approximate=True).astype(jnp.bfloat16)
    down_branch = scatter_rows(gelu_out, w_down, row_count)
    result = hidden + norm_rows(down_branch, gains[3])
    kept_values = (
        gathered_a,
        queries,
        key_rows,
        values,
        mixed,
        attn_branch,
        hidden,
        gathered_c,
        up_act,
        gelu_out,
        down_branch,
    )
    return (result, kept_values)


def layer_backward(layer_input, grad_result, kept_values, weights):
    gains, w_qkv, w_out, w_up, w_down = weights
    (
        gathered_a,
        queries,
        key_rows,
        values,
        mixed,
        attn_branch,
        hidden,
        gathered_c,
        up_act,
        gelu_out,
        down_branch,
    ) = kept_values
    row_count, model_width = layer_input.shape
    pullback = jax.vjp(norm_rows, down_branch, gains[3])[1]
    grad_down, gain_three = pullback(grad_result)
    gathered_dd, grad_gelu = gather_grads(grad_down.astype(jnp.bfloat16), w_down)
    down_total = contract(gelu_out, gathered_dd)
    pullback = jax.vjp(lambda vector: jax.nn.gelu(vector, approximate=True), up_act)[1]
    grad_up = pullback(grad_gelu)[0].astype(jnp.bfloat16)
    up_total = contract(gathered_c, grad_up)
    grad_mlp = scatter_grads(grad_up, w_up, row_count)
    pullback = jax.vjp(norm_rows, hidden, gains[2])[1]
    grad_norm_mlp, gain_two = pullback(grad_mlp)
    grad_hidden = grad_result + grad_norm_mlp
    pullback = jax.vjp(norm_rows, attn_branch, gains[1])[1]
    grad_attn, gain_one = pullback(grad_hidden)
    gathered_da, grad_mixed = gather_grads(grad_attn.astype(jnp.bfloat16), w_out)
    out_total = contract(mixed, gathered_da)
    length = grad_mixed.shape[0]
    head_count = w_qkv.shape[2] // HEAD_DIM
    grad_mixed = grad_mixed.astype(jnp.bfloat16).reshape(length, head_count, HEAD_DIM)
    attn_probs = attention_probs(queries, key_rows)
    probs_low = attn_probs.astype(jnp.bfloat16)
    grad_probs = jnp.einsum("qhd,khd->hqk", grad_mixed, values, preferred_element_type=jnp.float32)
    grad_values = jnp.einsum(
        "hqk,qhd->khd", probs_low, grad_mixed, preferred_element_type=jnp.float32
    )
    row_dots = jnp.sum(grad_probs * attn_probs, axis=-1, keepdims=True)
    grad_scores = (attn_probs * (grad_probs - row_dots)).astype(jnp.bfloat16)
    scale_value = HEAD_DIM ** (-0.5)
    grad_queries = (
        jnp.einsum("hqk,khd->qhd", grad_scores, key_rows, preferred_element_type=jnp.float32)
        * scale_value
    )
    grad_keys = (
        jnp.einsum("hqk,qhd->khd", grad_scores, queries, preferred_element_type=jnp.float32)
        * scale_value
    )
    cos_table, sin_table = rotary_tables(length, HEAD_DIM)
    pullback = jax.vjp(lambda vector: rotate(vector, cos_table, sin_table), grad_queries)[1]
    grad_q_raw = pullback(grad_queries)[0]
    grad_k_raw = pullback(grad_keys)[0]
    grad_qkv = (
        jnp.stack([grad_q_raw, grad_k_raw, grad_values], axis=1)
        .reshape(length, -1)
        .astype(jnp.bfloat16)
    )
    qkv_total = contract(gathered_a, grad_qkv).reshape(model_width, 3, -1)
    grad_attn_in = scatter_grads(grad_qkv, w_qkv.reshape(model_width, -1), row_count)
    pullback = jax.vjp(norm_rows, layer_input, gains[0])[1]
    grad_norm_in, gain_zero = pullback(grad_attn_in)
    grad_input = grad_hidden + grad_norm_in
    gain_total = jnp.stack([gain_zero, gain_one, gain_two, gain_three])
    return (grad_input, (gain_total, qkv_total, out_total, up_total, down_total))


def lagged(first_section, stacked):
    blank = jnp.zeros_like(stacked[:1])
    earlier = jnp.concatenate([blank, stacked[:-1]])
    later = jnp.concatenate([stacked[1:], blank])
    return jnp.where(first_section, earlier, later)


def per_device(
    inputs,
    out_cotangent,
    group_ids,
    group_weights,
    gains,
    qkv_weight,
    out_weight,
    up_weight,
    down_weight,
):
    weights = (gains[0], qkv_weight[0], out_weight[0], up_weight[0], down_weight[0])
    micro_count, row_count, model_width = inputs.shape
    first_section = lax.axis_index("section") == 0
    group_count = group_weights.shape[0]
    matches = group_ids[..., None] == jnp.arange(group_count, dtype=jnp.int32)
    row_scale = jnp.sum(jnp.where(matches, group_weights, 0.0), axis=-1)
    scaled = out_cotangent.astype(jnp.float32) * row_scale[..., None]
    padded = jnp.concatenate([inputs, jnp.zeros((1, row_count, model_width), jnp.bfloat16)])

    def forward_tick(received, fresh_input):
        layer_input = jnp.where(first_section, fresh_input, received)
        result, kept_values = layer_forward(layer_input.astype(jnp.float32), weights)
        result_low = result.astype(jnp.bfloat16)
        outgoing = shifted(result_low, "section", 1)
        stashed = ()
        return (outgoing, (layer_input, result_low, stashed))

    start_rows = jnp.zeros((row_count, model_width), jnp.bfloat16)
    _, (layer_inputs, layer_results, stashed) = lax.scan(forward_tick, start_rows, padded)
    layer_outputs = jnp.where(first_section, layer_results[:-1], layer_results[1:])[None]
    back_inputs = lagged(first_section, layer_inputs)
    back_stash = jax.tree.map(lambda stacked: lagged(first_section, stacked), stashed)
    grad_padded = jnp.concatenate([scaled, jnp.zeros((1, row_count, model_width), jnp.float32)])
    tick_index = jnp.arange(micro_count + 1, dtype=jnp.int32)
    tick_valid = jnp.where(first_section, tick_index >= 1, tick_index < micro_count).astype(
        jnp.float32
    )

    def backward_tick(carry, step_item):
        received, totals = carry
        layer_input, cotangent, valid_now, stash_now = step_item
        grad_now = jnp.where(first_section, received.astype(jnp.float32), cotangent)
        input_now = layer_input.astype(jnp.float32)
        kept_values = layer_forward(input_now, weights)[1]
        grad_input, layer_grads = layer_backward(input_now, grad_now, kept_values, weights)
        totals = jax.tree.map(lambda total, update: total + valid_now * update, totals, layer_grads)
        grad_low = grad_input.astype(jnp.bfloat16)
        outgoing = shifted(grad_low, "section", -1)
        return ((outgoing, totals), grad_low)

    start_totals = (
        jnp.zeros((4, model_width), jnp.float32),
        jnp.zeros(qkv_weight.shape[1:], jnp.float32),
        jnp.zeros(out_weight.shape[1:], jnp.float32),
        jnp.zeros(up_weight.shape[1:], jnp.float32),
        jnp.zeros(down_weight.shape[1:], jnp.float32),
    )
    (_, totals), grad_lows = lax.scan(
        backward_tick,
        (start_rows, start_totals),
        (back_inputs, grad_padded, tick_valid, back_stash),
    )
    input_grads = jnp.where(first_section, grad_lows[1:], grad_lows[:-1])[None]
    gain_total, qkv_total, out_total, up_total, down_total = totals
    gains_grad = lax.psum_scatter(gain_total, ("dp", "tensor"), scatter_dimension=1, tiled=True)
    qkv_grad, out_grad, up_grad, down_grad = (
        lax.psum_scatter(
            qkv_total.astype(jnp.bfloat16), "dp", scatter_dimension=0, tiled=True
        ).astype(jnp.float32),
        lax.psum_scatter(
            out_total.astype(jnp.bfloat16), "dp", scatter_dimension=1, tiled=True
        ).astype(jnp.float32),
        lax.psum_scatter(
            up_total.astype(jnp.bfloat16), "dp", scatter_dimension=0, tiled=True
        ).astype(jnp.float32),
        lax.psum_scatter(
            down_total.astype(jnp.bfloat16), "dp", scatter_dimension=1, tiled=True
        ).astype(jnp.float32),
    )
    return (
        layer_outputs,
        input_grads,
        gains_grad[None],
        qkv_grad[None],
        out_grad[None],
        up_grad[None],
        down_grad[None],
    )


def rotated(block, cos_rows, sin_rows):
    lane = lax.broadcasted_iota(jnp.int32, block.shape, 1)
    ahead = pltpu.roll(block, 96, 1)
    behind = pltpu.roll(block, 32, 1)
    swapped = jnp.where(lane % 64 < 32, ahead, behind)
    return block * cos_rows + swapped * sin_rows


def dot_nt(left, right):
    return lax.dot_general(
        left, right, (((1,), (1,)), ((), ())), preferred_element_type=jnp.float32
    )


def dot_nn(left, right):
    return jnp.dot(left, right, preferred_element_type=jnp.float32)


def edge_masks(core, rows):
    key = lax.broadcasted_iota(jnp.int32, (rows, 2 * rows), 0)
    query = lax.broadcasted_iota(jnp.int32, (rows, 2 * rows), 1)
    mine = query < rows
    place = jnp.where(mine, query + core * rows, query - rows + (1 - core) * rows)
    return (key + core * rows <= place, key + (1 - core) * rows <= place)


def both_sides(value, half, start, stop, axis=0):
    if axis == 0:
        return jnp.concatenate([value[start:stop], value[half + start : half + stop]], axis=0)
    return jnp.concatenate([value[:, start:stop], value[:, half + start : half + stop]], axis=1)


def hidden_scores(scores, masks, tile, step):
    seen = step * tile
    pieces = []
    for side in range(2):
        base = side * (seen + tile)
        if seen:
            pieces.append(scores[base : base + seen])
        pieces.append(jnp.where(masks[side], scores[base + seen : base + seen + tile], -1e30))
    return jnp.concatenate(pieces, axis=0)


def attend_kernel(core_ref, cos_ref, sin_ref, rows_ref, w_ref, q_ref, k_ref, v_ref, lse_ref, mix_ref):
    length = rows_ref.shape[0]
    half = length // 2
    tile = TILE
    proj = dot_nn(rows_ref[...], w_ref[...])
    cos_rows, sin_rows = cos_ref[...], sin_ref[...]
    q = (rotated(proj[:, :128], cos_rows, sin_rows) * HEAD_DIM ** (-0.5)).astype(jnp.bfloat16)
    k = rotated(proj[:, 128:256], cos_rows, sin_rows).astype(jnp.bfloat16)
    v32 = proj[:, 256:]
    v = v32.astype(jnp.bfloat16)
    q_ref[0] = q
    k_ref[0] = k
    v_ref[0] = v
    v_flip = v32.T.astype(jnp.bfloat16)
    masks = edge_masks(core_ref[0], tile)
    lane = lax.broadcasted_iota(jnp.int32, (2 * tile, 128), 1)
    for step in range(half // tile):
        stop = (step + 1) * tile
        q_rows = both_sides(q, half, step * tile, stop)
        k_rows = both_sides(k, half, 0, stop)
        v_cols = both_sides(v_flip, half, 0, stop, axis=1)
        outs = []
        for head in range(2):
            q_head = jnp.where(lane // 64 == head, q_rows, jnp.zeros_like(q_rows))
            scores = hidden_scores(dot_nt(k_rows, q_head), masks, tile, step)
            top = jnp.max(scores, axis=0, keepdims=True)
            expos = jnp.exp(scores - top)
            total = jnp.sum(expos, axis=0, keepdims=True)
            lse = top + jnp.log(total)
            lse_ref[0, head : head + 1, step * tile : stop] = lse[:, :tile]
            lse_ref[0, head : head + 1, half + step * tile : half + stop] = lse[:, tile:]
            out = dot_nn(v_cols[64 * head : 64 * head + 64], expos.astype(jnp.bfloat16))
            outs.append(out * (1.0 / total))
        mixed = jnp.concatenate(outs, axis=0).T.astype(jnp.bfloat16)
        mix_ref[step * tile : stop, :] = mixed[:tile]
        mix_ref[half + step * tile : half + stop, :] = mixed[tile:]


def attend_back_kernel(
    core_ref, cos_ref, sin_ref, grad_ref, w_ref, q_ref, k_ref, v_ref, lse_ref, out_ref, dq, dk, dv
):
    length = grad_ref.shape[0]
    half = length // 2
    tile = TILE
    d_mixed = dot_nt(grad_ref[...], w_ref[...]).astype(jnp.bfloat16)
    q, k, v = q_ref[0], k_ref[0], v_ref[0]
    k_flip = k.astype(jnp.float32).T.astype(jnp.bfloat16)
    masks = edge_masks(core_ref[0], tile)
    lane = lax.broadcasted_iota(jnp.int32, (2 * tile, 128), 1)
    steps = half // tile
    for step in reversed(range(steps)):
        stop = (step + 1) * tile
        q_rows = both_sides(q, half, step * tile, stop)
        g_rows = both_sides(d_mixed, half, step * tile, stop)
        k_rows = both_sides(k, half, 0, stop)
        v_rows = both_sides(v, half, 0, stop)
        k_cols = both_sides(k_flip, half, 0, stop, axis=1)
        lse = both_sides(lse_ref[0], half, step * tile, stop, axis=1)
        dq_flips = []
        dk_sum = dv_sum = None
        for head in range(2):
            q_head = jnp.where(lane // 64 == head, q_rows, jnp.zeros_like(q_rows))
            g_head = jnp.where(lane // 64 == head, g_rows, jnp.zeros_like(g_rows))
            scores = hidden_scores(dot_nt(k_rows, q_head), masks, tile, step)
            probs = jnp.exp(scores - lse[head : head + 1])
            d_probs = dot_nt(v_rows, g_head)
            dots = jnp.sum(probs * d_probs, axis=0, keepdims=True)
            d_scores = (probs * (d_probs - dots)).astype(jnp.bfloat16)
            dv_part = dot_nn(probs.astype(jnp.bfloat16), g_head)
            dk_part = dot_nn(d_scores, q_head)
            dv_sum = dv_part if dv_sum is None else dv_sum + dv_part
            dk_sum = dk_part if dk_sum is None else dk_sum + dk_part
            dq_flips.append(dot_nn(k_cols[64 * head : 64 * head + 64], d_scores))
        dq_rows = jnp.concatenate(dq_flips, axis=0).T * HEAD_DIM ** (-0.5)
        dq[step * tile : stop] = dq_rows[:tile]
        dq[half + step * tile : half + stop] = dq_rows[tile:]
        for base, part in ((0, slice(0, stop)), (half, slice(stop, 2 * stop))):
            if step == steps - 1:
                dk[base : base + stop] = dk_sum[part]
                dv[base : base + stop] = dv_sum[part]
            else:
                dk[base : base + stop] += dk_sum[part]
                dv[base : base + stop] += dv_sum[part]
    cos_rows, sin_rows = cos_ref[...], -sin_ref[...]
    out_ref[:, :128] = rotated(dq[...], cos_rows, sin_rows).astype(jnp.bfloat16)
    out_ref[:, 128:256] = rotated(dk[...], cos_rows, sin_rows).astype(jnp.bfloat16)
    out_ref[:, 256:] = dv[...].astype(jnp.bfloat16)


def whole_block(array):
    return pl.BlockSpec(array.shape, lambda j: (0,) * array.ndim)


def attend(core, tables, rows, w_qkv):
    length, width = rows.shape
    pairs = w_qkv.shape[1] // 384
    per_pair = pl.BlockSpec((1, length, 128), lambda j: (j, 0, 0))
    return pl.pallas_call(
        attend_kernel,
        grid=(pairs,),
        in_specs=[
            pl.BlockSpec(memory_space=pltpu.SMEM),
            whole_block(tables[0]),
            whole_block(tables[1]),
            whole_block(rows),
            pl.BlockSpec((width, 384), lambda j: (0, j)),
        ],
        out_specs=[
            per_pair,
            per_pair,
            per_pair,
            pl.BlockSpec((1, 2, length), lambda j: (j, 0, 0)),
            pl.BlockSpec((length, 128), lambda j: (0, j)),
        ],
        out_shape=[
            jax.ShapeDtypeStruct((pairs, length, 128), jnp.bfloat16),
            jax.ShapeDtypeStruct((pairs, length, 128), jnp.bfloat16),
            jax.ShapeDtypeStruct((pairs, length, 128), jnp.bfloat16),
            jax.ShapeDtypeStruct((pairs, 2, length), jnp.float32),
            jax.ShapeDtypeStruct((length, pairs * 128), jnp.bfloat16),
        ],
        compiler_params=pltpu.CompilerParams(vmem_limit_bytes=KERNEL_VMEM),
        name="attend",
    )(core, *tables, rows, w_qkv)


def attend_back(core, tables, grads, w_out, q, k, v, lse):
    length, width = grads.shape
    pairs = q.shape[0]
    per_pair = pl.BlockSpec((1, length, 128), lambda j: (j, 0, 0))
    return pl.pallas_call(
        attend_back_kernel,
        grid=(pairs,),
        in_specs=[
            pl.BlockSpec(memory_space=pltpu.SMEM),
            whole_block(tables[0]),
            whole_block(tables[1]),
            whole_block(grads),
            pl.BlockSpec((128, width), lambda j: (j, 0)),
            per_pair,
            per_pair,
            per_pair,
            pl.BlockSpec((1, 2, length), lambda j: (j, 0, 0)),
        ],
        out_specs=pl.BlockSpec((length, 384), lambda j: (0, j)),
        out_shape=jax.ShapeDtypeStruct((length, pairs * 384), jnp.bfloat16),
        scratch_shapes=[pltpu.VMEM((length, 128), jnp.float32)] * 3,
        compiler_params=pltpu.CompilerParams(vmem_limit_bytes=KERNEL_VMEM),
        name="attend_back",
    )(core, *tables, grads, w_out, q, k, v, lse)


def flip_pairs(block, distance):
    size = lax.axis_size("dp")
    return lax.ppermute(block, "dp", [(i, i ^ distance) for i in range(size)])


def passed_on(block, step):
    size = lax.axis_size("tensor")
    return lax.ppermute(block, "tensor", [(i, (i + step) % size) for i in range(size)])


def spread(piece):
    pieces = [piece]
    for _ in range(lax.axis_size("tensor") - 1):
        pieces.append(passed_on(pieces[-1], 1))
    return pieces


def collected(pieces):
    total = pieces[-1]
    for piece in reversed(pieces[:-1]):
        total = piece + passed_on(total.astype(jnp.bfloat16), -1).astype(jnp.float32)
    return total


def norm_back(vector, gain, grad):
    scale = lax.rsqrt(jnp.mean(vector * vector, axis=-1, keepdims=True) + NORM_EPSILON)
    weighted = grad * gain
    inner = jnp.mean(vector * weighted, axis=-1, keepdims=True)
    d_vector = scale * weighted - vector * (scale * scale * scale * inner)
    return d_vector, jnp.sum(vector * scale * grad, axis=0)


def gelu_both(up_act):
    root = math.sqrt(2.0 / math.pi)
    square = up_act * up_act
    bent = jnp.tanh(root * up_act * (1.0 + 0.044715 * square))
    value = 0.5 * up_act * (1.0 + bent)
    slope = 0.5 * (1.0 + bent) + 0.5 * up_act * (1.0 - bent * bent) * root * (
        1.0 + 3 * 0.044715 * square
    )
    return value, slope


def per_chip(
    inputs,
    out_cotangent,
    group_ids,
    group_weights,
    gains,
    qkv_weight,
    out_weight,
    up_weight,
    down_weight,
):
    micro, row_count, width = inputs.shape
    tensor = lax.axis_size("tensor")
    part = row_count // 2
    wide = width // 2
    length = tensor * row_count
    half = length // 2
    first = lax.axis_index("section") == 0
    place = lax.axis_index("dp")
    core = place % 2
    upper = place // 2 % 2
    core_zero = core == 0
    low_half = upper == 0

    def ordered(mine, other):
        return jnp.where(core_zero, mine, other), jnp.where(core_zero, other, mine)

    def own_first(values):
        return jnp.where(low_half, values, jnp.roll(values, wide, axis=-1))

    def full_rows(own):
        return jnp.concatenate([own, flip_pairs(own, 1)], axis=0)

    def summed_rows(partial):
        return partial[:half] + flip_pairs(partial[half:].astype(jnp.bfloat16), 1).astype(
            jnp.float32
        )

    def to_chip(block):
        split = block.reshape((micro, 2, part) + block.shape[2:])
        mine = lax.dynamic_index_in_dim(split, core, 1, keepdims=False)
        other = lax.dynamic_index_in_dim(split, 1 - core, 1, keepdims=False)
        return lax.all_to_all(
            jnp.concatenate(ordered(mine, flip_pairs(other, 1))), "tensor", 0, 0, tiled=True
        )

    def from_chip(block):
        spread_out = lax.all_to_all(block, "tensor", 0, 0, tiled=True)
        grouped = spread_out.reshape((2, micro, part) + block.shape[2:])
        mine = lax.dynamic_index_in_dim(grouped, core, 0, keepdims=False)
        other = lax.dynamic_index_in_dim(grouped, 1 - core, 0, keepdims=False)
        pair = ordered(mine, flip_pairs(other, 1))
        return jnp.stack(pair, axis=1).reshape((micro, row_count) + block.shape[2:])

    start = to_chip(own_first(jnp.where(first, inputs, out_cotangent))).reshape(half, width)
    start = start.astype(jnp.float32)
    group_count = group_weights.shape[0]
    matches = group_ids[..., None] == jnp.arange(group_count, dtype=jnp.int32)
    row_scale = jnp.sum(jnp.where(matches, group_weights, 0.0), axis=-1)
    row_scale = to_chip(row_scale).reshape(half, 1)

    def columns(local):
        piece = lax.dynamic_slice(
            local, (wide * upper, local.shape[1] // 2 * core), (wide, local.shape[1] // 2)
        )
        pieces = spread(piece)
        others = [flip_pairs(p, 2) for p in pieces]
        return jnp.concatenate(
            [jnp.concatenate(pieces, axis=1), jnp.concatenate(others, axis=1)], axis=0
        )

    def rows(local):
        piece = lax.dynamic_slice(
            local, (local.shape[0] // 2 * core, wide * upper), (local.shape[0] // 2, wide)
        )
        pieces = spread(piece)
        others = [flip_pairs(p, 2) for p in pieces]
        return jnp.concatenate(
            [jnp.concatenate(pieces, axis=0), jnp.concatenate(others, axis=0)], axis=1
        )

    head_cols = qkv_weight.shape[3]
    local_qkv = jnp.concatenate(
        [
            qkv_weight[0, :, i, h * head_cols // 2 : (h + 1) * head_cols // 2]
            for h in range(2)
            for i in range(3)
        ],
        axis=1,
    )
    w_qkv = columns(local_qkv)
    w_out = rows(out_weight[0])
    w_up = columns(up_weight[0])
    w_down = rows(down_weight[0])
    gain = own_first(gains[0])

    turns = jnp.arange(half, dtype=jnp.int32)
    turns = turns // part * row_count + turns % part
    positions = jnp.concatenate([turns + core * part, turns + (1 - core) * part])
    freqs = 10000.0 ** (-2.0 * jnp.arange(HEAD_DIM // 2, dtype=jnp.float32) / HEAD_DIM)
    angles = positions.astype(jnp.float32)[:, None] * freqs[None, :]
    cos_part, sin_part = jnp.cos(angles), jnp.sin(angles)
    tables = (
        jnp.concatenate([cos_part] * 4, axis=1),
        jnp.concatenate([-sin_part, sin_part] * 2, axis=1),
    )
    core_word = core.astype(jnp.int32).reshape(1)

    def forward(layer_input):
        attn_in = full_rows(norm_rows(layer_input, gain[0]).astype(jnp.bfloat16))
        q, k, v, lse, mixed = attend(core_word, tables, attn_in, w_qkv)
        attn_branch = summed_rows(dot_nn(mixed, w_out))
        hidden = layer_input + norm_rows(attn_branch, gain[1])
        mlp_in = full_rows(norm_rows(hidden, gain[2]).astype(jnp.bfloat16))
        gelu_out, slope = (t.astype(jnp.bfloat16) for t in gelu_both(dot_nn(mlp_in, w_up)))
        down_branch = summed_rows(dot_nn(gelu_out, w_down))
        result = hidden + norm_rows(down_branch, gain[3])
        chain = (layer_input, q, k, v, lse, attn_branch, hidden, slope, down_branch)
        return result.astype(jnp.bfloat16), chain, (attn_in, mixed, mlp_in, gelu_out)

    def backward(grad, chain):
        layer_input, q, k, v, lse, attn_branch, hidden, slope, down_branch = chain
        d_down, gain_three = norm_back(down_branch, gain[3], grad)
        d_down = full_rows(d_down.astype(jnp.bfloat16))
        d_up = (dot_nt(d_down, w_down) * slope.astype(jnp.float32)).astype(jnp.bfloat16)
        d_mlp = summed_rows(dot_nt(d_up, w_up))
        d_norm, gain_two = norm_back(hidden, gain[2], d_mlp)
        d_hidden = grad + d_norm
        d_attn, gain_one = norm_back(attn_branch, gain[1], d_hidden)
        d_attn = full_rows(d_attn.astype(jnp.bfloat16))
        d_qkv = attend_back(core_word, tables, d_attn, w_out, q, k, v, lse)
        d_in = summed_rows(dot_nt(d_qkv, w_qkv))
        d_norm, gain_zero = norm_back(layer_input, gain[0], d_in)
        d_input = (d_hidden + d_norm).astype(jnp.bfloat16)
        gain_rows = jnp.stack([gain_zero, gain_one, gain_two, gain_three])
        return d_input, (d_qkv, d_attn, d_up, d_down), gain_rows

    low_zero, chain_zero, lefts_zero = forward(start)
    low_one, chain_one, lefts_one = forward(shifted(low_zero, "section", 1).astype(jnp.float32))
    outputs = from_chip(own_first(jnp.where(first, low_zero, low_one)).reshape(tensor, part, width))
    grad_one, rights_one, gain_one = backward(start * row_scale, chain_one)
    grad_zero, rights_zero, gain_zero = backward(
        shifted(grad_one, "section", -1).astype(jnp.float32), chain_zero
    )
    grads = from_chip(own_first(jnp.where(first, grad_zero, grad_one)).reshape(tensor, part, width))

    attn_in, mixed, mlp_in, gelu_out = (
        jnp.where(first, zero, one) for zero, one in zip(lefts_zero, lefts_one)
    )
    d_qkv, d_attn, d_up, d_down = (
        jnp.where(first, zero, one) for zero, one in zip(rights_zero, rights_one)
    )

    def sum_columns(left, right, count):
        total = contract(left, right)
        size = total.shape[1] // tensor
        pieces = [
            total[:wide, j * size : (j + 1) * size]
            + flip_pairs(
                total[wide:, j * size : (j + 1) * size].astype(jnp.bfloat16), 2
            ).astype(jnp.float32)
            for j in range(tensor)
        ]
        kept = collected(pieces).reshape(2, wide // 2, size)
        mine = lax.dynamic_index_in_dim(kept, core, 0, keepdims=False)
        other = lax.dynamic_index_in_dim(kept, 1 - core, 0, keepdims=False)
        pair = ordered(mine, flip_pairs(other, 1))
        pair = [side.reshape(wide // 2, count, size // count) for side in pair]
        return jnp.concatenate(pair, axis=2)

    def sum_rows(left, right):
        total = contract(left, right)
        size = total.shape[0] // tensor
        pieces = [
            total[j * size : (j + 1) * size, :wide]
            + flip_pairs(
                total[j * size : (j + 1) * size, wide:].astype(jnp.bfloat16), 2
            ).astype(jnp.float32)
            for j in range(tensor)
        ]
        kept = collected(pieces)
        sides = (kept[:, : wide // 2], kept[:, wide // 2 :])
        mine = jnp.where(core_zero, sides[0], sides[1])
        other = jnp.where(core_zero, sides[1], sides[0])
        return jnp.concatenate(ordered(mine, flip_pairs(other, 1)), axis=0)

    down_grad = sum_rows(gelu_out, d_down)
    up_grad = sum_columns(mlp_in, d_up, 1)[:, 0]
    out_grad = sum_rows(mixed, d_attn)
    qkv_grad = sum_columns(attn_in, d_qkv, 3)
    gain_total = own_first(jnp.where(first, gain_zero, gain_one))
    gains_grad = lax.psum_scatter(gain_total, ("dp", "tensor"), scatter_dimension=1, tiled=True)
    return (
        outputs[None],
        grads[None],
        gains_grad[None],
        qkv_grad[None],
        out_grad[None],
        up_grad[None],
        down_grad[None],
    )


def takes_chips(sizes):
    return sizes["section"] == 2 and sizes["dp"] == 4 and sizes["tensor"] == 4


def solution(mesh):
    placed = (
        P("dp", "tensor", None),
        P("dp", "tensor", None),
        P("dp", "tensor"),
        P(),
        P("section", None, None),
        P("section", None, None, "tensor"),
        P("section", "tensor", None),
        P("section", None, "tensor"),
        P("section", "tensor", None),
    )
    body = per_chip if takes_chips(dict(mesh.shape)) else per_device
    return jax.shard_map(
        body,
        mesh=mesh,
        in_specs=placed,
        out_specs=(
            P("section", "dp", "tensor", None),
            P("section", "dp", "tensor", None),
            P("section", None, ("dp", "tensor")),
            P("section", "dp", None, "tensor"),
            P("section", "tensor", "dp"),
            P("section", "dp", "tensor"),
            P("section", "tensor", "dp"),
        ),
        check_vma=False,
    )
```

```python
import functools
import math

import jax
import jax.numpy as jnp
from jax import lax
from jax.experimental import pallas as pl
from jax.experimental.pallas import tpu as pltpu
from jax.sharding import PartitionSpec as P

HEAD_DIM = 64


NORM_EPSILON = 1e-06
TILE = 128
CHUNK = 32
KERNEL_VMEM = 40 << 20


def shifted(block, axis, distance):
    devices = range(lax.axis_size(axis))
    route = [(i - distance, i) for i in devices if i - distance in devices]
    return lax.ppermute(block, axis, route)


def norm_rows(vector, weight_gain):
    return (
        vector
        * lax.rsqrt(jnp.mean(vector * vector, axis=-1, keepdims=True) + NORM_EPSILON)
        * weight_gain
    )


def rotary_tables(seq_len, head_width):
    half_width = head_width // 2
    freqs = 10000.0 ** (-2.0 * jnp.arange(half_width, dtype=jnp.float32) / head_width)
    angles = jnp.arange(seq_len, dtype=jnp.float32)[:, None] * freqs[None, :]
    return (jnp.cos(angles), jnp.sin(angles))


def rotate(vector, cos_table, sin_table):
    first_half, second_half = jnp.split(vector, 2, axis=-1)
    cos_part = cos_table[:, None, :]
    sin_part = sin_table[:, None, :]
    return jnp.concatenate(
        [
            first_half * cos_part - second_half * sin_part,
            second_half * cos_part + first_half * sin_part,
        ],
        axis=-1,
    )


def contract(left_rows, right_rows):
    return lax.dot_general(
        left_rows, right_rows, (((0,), (0,)), ((), ())), preferred_element_type=jnp.float32
    )


def gather_rows(row_values, weight):

    def project(shard_rows, offset):
        return (shard_rows, jnp.dot(shard_rows, weight, preferred_element_type=jnp.float32))

    return project(lax.all_gather(row_values, "tensor", axis=0, tiled=True), jnp.int32(0))


def scatter_rows(row_values, weight, row_count):

    def partial_term(offset, span):
        return jnp.dot(row_values, weight, preferred_element_type=jnp.float32)

    return lax.psum_scatter(
        partial_term(jnp.int32(0), lax.axis_size("tensor") * row_count),
        "tensor",
        scatter_dimension=0,
        tiled=True,
    )


def gather_grads(row_values, weight):

    def project(shard_rows, offset):
        return (shard_rows, jnp.dot(shard_rows, weight.T, preferred_element_type=jnp.float32))

    return project(lax.all_gather(row_values, "tensor", axis=0, tiled=True), jnp.int32(0))


def scatter_grads(row_values, weight, row_count):

    def partial_term(offset, span):
        return jnp.dot(row_values, weight.T, preferred_element_type=jnp.float32)

    return lax.psum_scatter(
        partial_term(jnp.int32(0), lax.axis_size("tensor") * row_count),
        "tensor",
        scatter_dimension=0,
        tiled=True,
    )


def attention_probs(queries, key_rows):
    scores = jnp.einsum(
        "qhd,khd->hqk", queries, key_rows, preferred_element_type=jnp.float32
    ) * HEAD_DIM ** (-0.5)
    length = queries.shape[0]
    positions = jnp.arange(length, dtype=jnp.int32)
    causal = positions[:, None] >= positions[None, :]
    scores = jnp.where(causal[None], scores, -1e30)
    expos = jnp.exp(scores - jnp.max(scores, axis=-1, keepdims=True))
    return expos / jnp.sum(expos, axis=-1, keepdims=True)


def layer_forward(layer_input, weights):
    gains, w_qkv, w_out, w_up, w_down = weights
    row_count, model_width = layer_input.shape
    attn_in = norm_rows(layer_input, gains[0]).astype(jnp.bfloat16)
    gathered_a, qkv = gather_rows(attn_in, w_qkv.reshape(model_width, -1))
    length = qkv.shape[0]
    head_count = w_qkv.shape[2] // HEAD_DIM
    qkv = qkv.reshape(length, 3, head_count, HEAD_DIM)
    cos_table, sin_table = rotary_tables(length, HEAD_DIM)
    queries = rotate(qkv[:, 0], cos_table, sin_table).astype(jnp.bfloat16)
    key_rows = rotate(qkv[:, 1], cos_table, sin_table).astype(jnp.bfloat16)
    values = qkv[:, 2].astype(jnp.bfloat16)
    attn_probs = attention_probs(queries, key_rows).astype(jnp.bfloat16)
    mixed = jnp.einsum("hqk,khd->qhd", attn_probs, values, preferred_element_type=jnp.float32)
    mixed = mixed.reshape(length, -1).astype(jnp.bfloat16)
    attn_branch = scatter_rows(mixed, w_out, row_count)
    hidden = layer_input + norm_rows(attn_branch, gains[1])
    mlp_in = norm_rows(hidden, gains[2]).astype(jnp.bfloat16)
    gathered_c, up_act = gather_rows(mlp_in, w_up)
    gelu_out = jax.nn.gelu(up_act, approximate=True).astype(jnp.bfloat16)
    down_branch = scatter_rows(gelu_out, w_down, row_count)
    result = hidden + norm_rows(down_branch, gains[3])
    kept_values = (
        gathered_a,
        queries,
        key_rows,
        values,
        mixed,
        attn_branch,
        hidden,
        gathered_c,
        up_act,
        gelu_out,
        down_branch,
    )
    return (result, kept_values)


def layer_backward(layer_input, grad_result, kept_values, weights):
    gains, w_qkv, w_out, w_up, w_down = weights
    (
        gathered_a,
        queries,
        key_rows,
        values,
        mixed,
        attn_branch,
        hidden,
        gathered_c,
        up_act,
        gelu_out,
        down_branch,
    ) = kept_values
    row_count, model_width = layer_input.shape
    pullback = jax.vjp(norm_rows, down_branch, gains[3])[1]
    grad_down, gain_three = pullback(grad_result)
    gathered_dd, grad_gelu = gather_grads(grad_down.astype(jnp.bfloat16), w_down)
    down_total = contract(gelu_out, gathered_dd)
    pullback = jax.vjp(lambda vector: jax.nn.gelu(vector, approximate=True), up_act)[1]
    grad_up = pullback(grad_gelu)[0].astype(jnp.bfloat16)
    up_total = contract(gathered_c, grad_up)
    grad_mlp = scatter_grads(grad_up, w_up, row_count)
    pullback = jax.vjp(norm_rows, hidden, gains[2])[1]
    grad_norm_mlp, gain_two = pullback(grad_mlp)
    grad_hidden = grad_result + grad_norm_mlp
    pullback = jax.vjp(norm_rows, attn_branch, gains[1])[1]
    grad_attn, gain_one = pullback(grad_hidden)
    gathered_da, grad_mixed = gather_grads(grad_attn.astype(jnp.bfloat16), w_out)
    out_total = contract(mixed, gathered_da)
    length = grad_mixed.shape[0]
    head_count = w_qkv.shape[2] // HEAD_DIM
    grad_mixed = grad_mixed.astype(jnp.bfloat16).reshape(length, head_count, HEAD_DIM)
    attn_probs = attention_probs(queries, key_rows)
    probs_low = attn_probs.astype(jnp.bfloat16)
    grad_probs = jnp.einsum("qhd,khd->hqk", grad_mixed, values, preferred_element_type=jnp.float32)
    grad_values = jnp.einsum(
        "hqk,qhd->khd", probs_low, grad_mixed, preferred_element_type=jnp.float32
    )
    row_dots = jnp.sum(grad_probs * attn_probs, axis=-1, keepdims=True)
    grad_scores = (attn_probs * (grad_probs - row_dots)).astype(jnp.bfloat16)
    scale_value = HEAD_DIM ** (-0.5)
    grad_queries = (
        jnp.einsum("hqk,khd->qhd", grad_scores, key_rows, preferred_element_type=jnp.float32)
        * scale_value
    )
    grad_keys = (
        jnp.einsum("hqk,qhd->khd", grad_scores, queries, preferred_element_type=jnp.float32)
        * scale_value
    )
    cos_table, sin_table = rotary_tables(length, HEAD_DIM)
    pullback = jax.vjp(lambda vector: rotate(vector, cos_table, sin_table), grad_queries)[1]
    grad_q_raw = pullback(grad_queries)[0]
    grad_k_raw = pullback(grad_keys)[0]
    grad_qkv = (
        jnp.stack([grad_q_raw, grad_k_raw, grad_values], axis=1)
        .reshape(length, -1)
        .astype(jnp.bfloat16)
    )
    qkv_total = contract(gathered_a, grad_qkv).reshape(model_width, 3, -1)
    grad_attn_in = scatter_grads(grad_qkv, w_qkv.reshape(model_width, -1), row_count)
    pullback = jax.vjp(norm_rows, layer_input, gains[0])[1]
    grad_norm_in, gain_zero = pullback(grad_attn_in)
    grad_input = grad_hidden + grad_norm_in
    gain_total = jnp.stack([gain_zero, gain_one, gain_two, gain_three])
    return (grad_input, (gain_total, qkv_total, out_total, up_total, down_total))


def lagged(first_section, stacked):
    blank = jnp.zeros_like(stacked[:1])
    earlier = jnp.concatenate([blank, stacked[:-1]])
    later = jnp.concatenate([stacked[1:], blank])
    return jnp.where(first_section, earlier, later)


def per_device(
    inputs,
    out_cotangent,
    group_ids,
    group_weights,
    gains,
    qkv_weight,
    out_weight,
    up_weight,
    down_weight,
):
    weights = (gains[0], qkv_weight[0], out_weight[0], up_weight[0], down_weight[0])
    micro_count, row_count, model_width = inputs.shape
    first_section = lax.axis_index("section") == 0
    group_count = group_weights.shape[0]
    matches = group_ids[..., None] == jnp.arange(group_count, dtype=jnp.int32)
    row_scale = jnp.sum(jnp.where(matches, group_weights, 0.0), axis=-1)
    scaled = out_cotangent.astype(jnp.float32) * row_scale[..., None]
    padded = jnp.concatenate([inputs, jnp.zeros((1, row_count, model_width), jnp.bfloat16)])

    def forward_tick(received, fresh_input):
        layer_input = jnp.where(first_section, fresh_input, received)
        result, kept_values = layer_forward(layer_input.astype(jnp.float32), weights)
        result_low = result.astype(jnp.bfloat16)
        outgoing = shifted(result_low, "section", 1)
        stashed = ()
        return (outgoing, (layer_input, result_low, stashed))

    start_rows = jnp.zeros((row_count, model_width), jnp.bfloat16)
    _, (layer_inputs, layer_results, stashed) = lax.scan(forward_tick, start_rows, padded)
    layer_outputs = jnp.where(first_section, layer_results[:-1], layer_results[1:])[None]
    back_inputs = lagged(first_section, layer_inputs)
    back_stash = jax.tree.map(lambda stacked: lagged(first_section, stacked), stashed)
    grad_padded = jnp.concatenate([scaled, jnp.zeros((1, row_count, model_width), jnp.float32)])
    tick_index = jnp.arange(micro_count + 1, dtype=jnp.int32)
    tick_valid = jnp.where(first_section, tick_index >= 1, tick_index < micro_count).astype(
        jnp.float32
    )

    def backward_tick(carry, step_item):
        received, totals = carry
        layer_input, cotangent, valid_now, stash_now = step_item
        grad_now = jnp.where(first_section, received.astype(jnp.float32), cotangent)
        input_now = layer_input.astype(jnp.float32)
        kept_values = layer_forward(input_now, weights)[1]
        grad_input, layer_grads = layer_backward(input_now, grad_now, kept_values, weights)
        totals = jax.tree.map(lambda total, update: total + valid_now * update, totals, layer_grads)
        grad_low = grad_input.astype(jnp.bfloat16)
        outgoing = shifted(grad_low, "section", -1)
        return ((outgoing, totals), grad_low)

    start_totals = (
        jnp.zeros((4, model_width), jnp.float32),
        jnp.zeros(qkv_weight.shape[1:], jnp.float32),
        jnp.zeros(out_weight.shape[1:], jnp.float32),
        jnp.zeros(up_weight.shape[1:], jnp.float32),
        jnp.zeros(down_weight.shape[1:], jnp.float32),
    )
    (_, totals), grad_lows = lax.scan(
        backward_tick,
        (start_rows, start_totals),
        (back_inputs, grad_padded, tick_valid, back_stash),
    )
    input_grads = jnp.where(first_section, grad_lows[1:], grad_lows[:-1])[None]
    gain_total, qkv_total, out_total, up_total, down_total = totals
    gains_grad = lax.psum_scatter(gain_total, ("dp", "tensor"), scatter_dimension=1, tiled=True)
    qkv_grad, out_grad, up_grad, down_grad = (
        lax.psum_scatter(
            qkv_total.astype(jnp.bfloat16), "dp", scatter_dimension=0, tiled=True
        ).astype(jnp.float32),
        lax.psum_scatter(
            out_total.astype(jnp.bfloat16), "dp", scatter_dimension=1, tiled=True
        ).astype(jnp.float32),
        lax.psum_scatter(
            up_total.astype(jnp.bfloat16), "dp", scatter_dimension=0, tiled=True
        ).astype(jnp.float32),
        lax.psum_scatter(
            down_total.astype(jnp.bfloat16), "dp", scatter_dimension=1, tiled=True
        ).astype(jnp.float32),
    )
    return (
        layer_outputs,
        input_grads,
        gains_grad[None],
        qkv_grad[None],
        out_grad[None],
        up_grad[None],
        down_grad[None],
    )


def rotated(block, cos_rows, sin_rows):
    lane = lax.broadcasted_iota(jnp.int32, block.shape, 1)
    ahead = pltpu.roll(block, 96, 1)
    behind = pltpu.roll(block, 32, 1)
    swapped = jnp.where(lane % 64 < 32, ahead, behind)
    return block * cos_rows + swapped * sin_rows


def dot_nt(left, right):
    return lax.dot_general(
        left, right, (((1,), (1,)), ((), ())), preferred_element_type=jnp.float32
    )


def dot_nn(left, right):
    return jnp.dot(left, right, preferred_element_type=jnp.float32)


def side_by_side(refs):
    return jnp.concatenate([ref[...] for ref in refs], axis=1)


def stacked_up(refs):
    return jnp.concatenate([ref[...] for ref in refs], axis=0)


def edge_masks(core, rows):
    key = lax.broadcasted_iota(jnp.int32, (rows, 2 * rows), 0)
    query = lax.broadcasted_iota(jnp.int32, (rows, 2 * rows), 1)
    mine = query < rows
    place = jnp.where(mine, query + core * rows, query - rows + (1 - core) * rows)
    return (key + core * rows <= place, key + (1 - core) * rows <= place)


def both_sides(value, half, start, stop, axis=0):
    if axis == 0:
        return jnp.concatenate([value[start:stop], value[half + start : half + stop]], axis=0)
    return jnp.concatenate([value[:, start:stop], value[:, half + start : half + stop]], axis=1)


def hidden_scores(scores, masks, tile, step):
    seen = step * tile
    pieces = []
    for side in range(2):
        base = side * (seen + tile)
        if seen:
            pieces.append(scores[base : base + seen])
        pieces.append(jnp.where(masks[side], scores[base + seen : base + seen + tile], -1e30))
    return jnp.concatenate(pieces, axis=0)


def one_head(rows, head):
    lane = lax.broadcasted_iota(jnp.int32, rows.shape, 1)
    return jnp.where(lane // 64 == head, rows, jnp.zeros_like(rows))


def pick_piece(weight, owns, others, axis):
    for j, (own, other) in enumerate(zip(owns, others)):

        @pl.when(pl.program_id(0) == j)
        def _():
            size = own.shape[axis]
            if axis == 0:
                weight[:size] = own[...]
                weight[size:] = other[...]
            else:
                weight[:, :size] = own[...]
                weight[:, size:] = other[...]


def attend_kernel(pieces, core_ref, cos_ref, sin_ref, own_rows, other_rows, *refs):
    owns, others = refs[:pieces], refs[pieces : 2 * pieces]
    q_ref, k_ref, v_ref, lse_ref, mix_ref, weight = refs[2 * pieces :]
    half = own_rows.shape[0]
    tile = TILE
    pick_piece(weight, owns, others, 0)
    proj = dot_nn(stacked_up([own_rows, other_rows]), weight[...])
    cos_rows, sin_rows = cos_ref[...], sin_ref[...]
    q = (rotated(proj[:, :128], cos_rows, sin_rows) * HEAD_DIM ** (-0.5)).astype(jnp.bfloat16)
    k = rotated(proj[:, 128:256], cos_rows, sin_rows).astype(jnp.bfloat16)
    v32 = proj[:, 256:]
    q_ref[0] = q
    k_ref[0] = k
    v_ref[0] = v32.astype(jnp.bfloat16)
    v_flip = v32.T.astype(jnp.bfloat16)
    masks = edge_masks(core_ref[0], tile)

    def scored(step, head):
        stop = (step + 1) * tile
        q_head = one_head(both_sides(q, half, step * tile, stop), head)
        return hidden_scores(dot_nt(both_sides(k, half, 0, stop), q_head), masks, tile, step)

    units = [(step, head) for step in range(half // tile) for head in range(2)]
    ahead = scored(*units[0])
    outs = []
    for spot, (step, head) in enumerate(units):
        scores = ahead
        if spot + 1 < len(units):
            ahead = scored(*units[spot + 1])
        stop = (step + 1) * tile
        top = jnp.max(scores, axis=0, keepdims=True)
        expos = jnp.exp(scores - top)
        total = jnp.sum(expos, axis=0, keepdims=True)
        lse = top + jnp.log(total)
        lse_ref[0, head : head + 1, step * tile : stop] = lse[:, :tile]
        lse_ref[0, head : head + 1, half + step * tile : half + stop] = lse[:, tile:]
        v_cols = both_sides(v_flip, half, 0, stop, axis=1)
        out = dot_nn(v_cols[64 * head : 64 * head + 64], expos.astype(jnp.bfloat16))
        outs.append(out * (1.0 / total))
        if head == 1:
            mixed = jnp.concatenate(outs, axis=0).T.astype(jnp.bfloat16)
            outs = []
            mix_ref[step * tile : stop, :] = mixed[:tile]
            mix_ref[half + step * tile : half + stop, :] = mixed[tile:]


def attend_back_kernel(pieces, core_ref, cos_ref, sin_ref, own_rows, other_rows, *refs):
    owns, others = refs[:pieces], refs[pieces : 2 * pieces]
    q_ref, k_ref, v_ref, lse_ref, out_ref, weight, dq, dk, dv = refs[2 * pieces :]
    half = own_rows.shape[0]
    tile = TILE
    pick_piece(weight, owns, others, 1)
    d_mixed = dot_nt(stacked_up([own_rows, other_rows]), weight[...]).astype(jnp.bfloat16)
    q, k, v = q_ref[0], k_ref[0], v_ref[0]
    k_flip = k.astype(jnp.float32).T.astype(jnp.bfloat16)
    masks = edge_masks(core_ref[0], tile)
    steps = half // tile

    def scored(step, head):
        stop = (step + 1) * tile
        q_head = one_head(both_sides(q, half, step * tile, stop), head)
        g_head = one_head(both_sides(d_mixed, half, step * tile, stop), head)
        scores = hidden_scores(dot_nt(both_sides(k, half, 0, stop), q_head), masks, tile, step)
        return q_head, g_head, scores, dot_nt(both_sides(v, half, 0, stop), g_head)

    units = [(step, head) for step in reversed(range(steps)) for head in range(2)]
    ahead = scored(*units[0])
    dq_flips = []
    dk_sum = dv_sum = None
    for spot, (step, head) in enumerate(units):
        q_head, g_head, scores, d_probs = ahead
        if spot + 1 < len(units):
            ahead = scored(*units[spot + 1])
        stop = (step + 1) * tile
        lse = both_sides(lse_ref[0], half, step * tile, stop, axis=1)
        probs = jnp.exp(scores - lse[head : head + 1])
        dots = jnp.sum(probs * d_probs, axis=0, keepdims=True)
        d_scores = (probs * (d_probs - dots)).astype(jnp.bfloat16)
        dv_part = dot_nn(probs.astype(jnp.bfloat16), g_head)
        dk_part = dot_nn(d_scores, q_head)
        k_cols = both_sides(k_flip, half, 0, stop, axis=1)
        dq_flips.append(dot_nn(k_cols[64 * head : 64 * head + 64], d_scores))
        if head == 0:
            dv_sum, dk_sum = dv_part, dk_part
            continue
        dv_sum, dk_sum = dv_sum + dv_part, dk_sum + dk_part
        dq_rows = jnp.concatenate(dq_flips, axis=0).T * HEAD_DIM ** (-0.5)
        dq_flips = []
        dq[step * tile : stop] = dq_rows[:tile]
        dq[half + step * tile : half + stop] = dq_rows[tile:]
        for base, part in ((0, slice(0, stop)), (half, slice(stop, 2 * stop))):
            if step == steps - 1:
                dk[base : base + stop] = dk_sum[part]
                dv[base : base + stop] = dv_sum[part]
            else:
                dk[base : base + stop] += dk_sum[part]
                dv[base : base + stop] += dv_sum[part]
    cos_rows, sin_rows = cos_ref[...], -sin_ref[...]
    out_ref[:, :128] = rotated(dq[...], cos_rows, sin_rows).astype(jnp.bfloat16)
    out_ref[:, 128:256] = rotated(dk[...], cos_rows, sin_rows).astype(jnp.bfloat16)
    out_ref[:, 256:] = dv[...].astype(jnp.bfloat16)


def split_rows(total, own_ref, other_ref):
    half = own_ref.shape[0]
    own_ref[...] = total[:half]
    other_ref[...] = total[half:].astype(jnp.bfloat16)


def into_model_kernel(pieces, left_ref, *refs):
    owns, others = refs[:pieces], refs[pieces : 2 * pieces]
    weight = jnp.concatenate([stacked_up(owns), stacked_up(others)], axis=1)
    split_rows(dot_nn(left_ref[...], weight), *refs[2 * pieces :])


def back_to_model_kernel(pieces, left_ref, *refs):
    owns, others = refs[:pieces], refs[pieces : 2 * pieces]
    weight = jnp.concatenate([side_by_side(owns), side_by_side(others)], axis=0)
    split_rows(dot_nt(left_ref[...], weight), *refs[2 * pieces :])


def gelu_both(up_act):
    root = math.sqrt(2.0 / math.pi)
    square = up_act * up_act
    rise = 0.5 + 0.5 * jnp.tanh(up_act * (root + root * 0.044715 * square))
    value = up_act * rise
    slope = rise + value * (1.0 - rise) * (2.0 * root + 6.0 * root * 0.044715 * square)
    return value, slope


def mlp_up_kernel(pieces, own_rows, other_rows, *refs):
    owns, others = refs[:pieces], refs[pieces : 2 * pieces]
    gelu_ref, slope_ref = refs[2 * pieces :]
    half = own_rows.shape[0]
    size = owns[0].shape[1]
    step = half // 2
    units = [(j, i) for j in range(pieces) for i in range(4)]

    def product(j, i):
        rows = (own_rows, other_rows)[i // 2][i % 2 * step : (i % 2 + 1) * step]
        return dot_nn(rows, stacked_up([owns[j], others[j]]))

    ahead = product(*units[0])
    for spot, (j, i) in enumerate(units):
        up_act = ahead
        if spot + 1 < len(units):
            ahead = product(*units[spot + 1])
        value, slope = gelu_both(up_act)
        gelu_ref[i * step : (i + 1) * step, j * size : (j + 1) * size] = value.astype(jnp.bfloat16)
        slope_ref[i * step : (i + 1) * step, j * size : (j + 1) * size] = slope.astype(
            jnp.bfloat16
        )


def mlp_up_back_kernel(pieces, own_rows, other_rows, slope_ref, *refs):
    owns, others = refs[:pieces], refs[pieces : 2 * pieces]
    out_ref = refs[-1]
    size = owns[0].shape[0]
    rows = stacked_up([own_rows, other_rows])
    for j in range(pieces):
        cols = slice(j * size, (j + 1) * size)
        d_gelu = dot_nt(rows, side_by_side([owns[j], others[j]]))
        out_ref[:, cols] = (d_gelu * slope_ref[:, cols].astype(jnp.float32)).astype(jnp.bfloat16)


def inverse_size(rows):
    return lax.rsqrt(jnp.mean(rows * rows, axis=-1, keepdims=True) + NORM_EPSILON)


def norm_back(rows, gain, grad):
    scale = inverse_size(rows)
    weighted = grad * gain
    inner = jnp.mean(rows * weighted, axis=-1, keepdims=True)
    return scale * weighted - rows * (scale * scale * scale * inner), rows * scale * grad


def folded(rows):
    return jnp.sum(rows.reshape(rows.shape[0] // 8, 8, rows.shape[1]), axis=0)


def wide(ref, spot):
    return ref[spot, :].astype(jnp.float32)


def by_chunks(count, body, sums=0, width=0):
    def one(i, carry):
        more = body(pl.ds(pl.multiple_of(i * CHUNK, CHUNK), CHUNK))
        return tuple(old + folded(new) for old, new in zip(carry, more))

    start = tuple(jnp.zeros((8, width), jnp.float32) for _ in range(sums))
    totals = lax.fori_loop(0, count // CHUNK, one, start)
    return [jnp.sum(total, axis=0, keepdims=True) for total in totals]


def norm_in_kernel(gain_ref, rows_ref, out_ref):
    def body(spot):
        rows = wide(rows_ref, spot)
        out_ref[spot, :] = (rows * inverse_size(rows) * gain_ref[0:1]).astype(jnp.bfloat16)
        return ()

    by_chunks(rows_ref.shape[0], body)


def after_attention_kernel(
    gain_ref, rows_ref, own_ref, other_ref, branch_ref, hidden_ref, out_ref
):
    def body(spot):
        branch = own_ref[spot, :] + wide(other_ref, spot)
        hidden = wide(rows_ref, spot) + branch * inverse_size(branch) * gain_ref[1:2]
        branch_ref[spot, :] = branch
        hidden_ref[spot, :] = hidden
        out_ref[spot, :] = (hidden * inverse_size(hidden) * gain_ref[2:3]).astype(jnp.bfloat16)
        return ()

    by_chunks(rows_ref.shape[0], body)


def after_mlp_kernel(gain_ref, hidden_ref, own_ref, other_ref, branch_ref, out_ref):
    def body(spot):
        branch = own_ref[spot, :] + wide(other_ref, spot)
        branch_ref[spot, :] = branch
        result = hidden_ref[spot, :] + branch * inverse_size(branch) * gain_ref[3:4]
        out_ref[spot, :] = result.astype(jnp.bfloat16)
        return ()

    by_chunks(hidden_ref.shape[0], body)


def into_mlp_back_kernel(gain_ref, grad_ref, branch_ref, out_ref, sum_ref):
    def body(spot):
        d_rows, d_gain = norm_back(branch_ref[spot, :], gain_ref[3:4], wide(grad_ref, spot))
        out_ref[spot, :] = d_rows.astype(jnp.bfloat16)
        return (d_gain,)

    (sum_ref[...],) = by_chunks(grad_ref.shape[0], body, 1, grad_ref.shape[1])


def into_attention_back_kernel(
    gain_ref, grad_ref, own_ref, other_ref, hidden_ref, branch_ref, d_hidden_ref, out_ref, *sums
):
    def body(spot):
        d_rows = own_ref[spot, :] + wide(other_ref, spot)
        d_rows, d_gain = norm_back(hidden_ref[spot, :], gain_ref[2:3], d_rows)
        d_hidden = wide(grad_ref, spot) + d_rows
        d_hidden_ref[spot, :] = d_hidden
        d_rows, d_first = norm_back(branch_ref[spot, :], gain_ref[1:2], d_hidden)
        out_ref[spot, :] = d_rows.astype(jnp.bfloat16)
        return (d_first, d_gain)

    totals = by_chunks(grad_ref.shape[0], body, 2, grad_ref.shape[1])
    sums[0][...], sums[1][...] = totals


def out_of_layer_kernel(gain_ref, rows_ref, own_ref, other_ref, d_hidden_ref, out_ref, sum_ref):
    def body(spot):
        d_rows = own_ref[spot, :] + wide(other_ref, spot)
        d_rows, d_gain = norm_back(wide(rows_ref, spot), gain_ref[0:1], d_rows)
        out_ref[spot, :] = (d_hidden_ref[spot, :] + d_rows).astype(jnp.bfloat16)
        return (d_gain,)

    (sum_ref[...],) = by_chunks(rows_ref.shape[0], body, 1, rows_ref.shape[1])


def on_chip(kernel, name, outs, *operands):
    space = pl.BlockSpec(memory_space=pltpu.VMEM)
    return pl.pallas_call(
        kernel,
        in_specs=[space] * len(operands),
        out_specs=[space] * len(outs),
        out_shape=[jax.ShapeDtypeStruct(shape, dtype) for shape, dtype in outs],
        compiler_params=pltpu.CompilerParams(vmem_limit_bytes=KERNEL_VMEM),
        name=name,
    )(*operands)


def whole_block(array):
    return pl.BlockSpec(array.shape, lambda j: (0,) * array.ndim)


def by_pairs(kernel, name, core, operands, pieces, blocks, outs, scratch):
    return pl.pallas_call(
        functools.partial(kernel, len(pieces[0])),
        grid=(len(pieces[0]),),
        in_specs=[pl.BlockSpec(memory_space=pltpu.SMEM)]
        + [whole_block(array) for array in (*operands, *pieces[0], *pieces[1])]
        + [spec for _, spec in blocks],
        out_specs=[spec for _, _, spec in outs],
        out_shape=[jax.ShapeDtypeStruct(shape, dtype) for shape, dtype, _ in outs],
        scratch_shapes=scratch,
        compiler_params=pltpu.CompilerParams(vmem_limit_bytes=KERNEL_VMEM),
        name=name,
    )(core, *operands, *pieces[0], *pieces[1], *[array for array, _ in blocks])


def attend(core, tables, rows, pieces):
    half, features = rows[0].shape
    length, count = 2 * half, len(pieces[0])
    lanes = ((count, length, 128), jnp.bfloat16, pl.BlockSpec((1, length, 128), lambda j: (j, 0, 0)))
    lse = ((count, 2, length), jnp.float32, pl.BlockSpec((1, 2, length), lambda j: (j, 0, 0)))
    mixed = ((length, count * 128), jnp.bfloat16, pl.BlockSpec((length, 128), lambda j: (0, j)))
    return by_pairs(
        attend_kernel,
        "attend",
        core,
        (*tables, *rows),
        pieces,
        (),
        (lanes, lanes, lanes, lse, mixed),
        [pltpu.VMEM((features, 384), jnp.bfloat16)],
    )


def attend_back(core, tables, rows, pieces, q, k, v, lse):
    half, features = rows[0].shape
    length, count = 2 * half, len(pieces[0])
    lanes = pl.BlockSpec((1, length, 128), lambda j: (j, 0, 0))
    lse_spec = pl.BlockSpec((1, 2, length), lambda j: (j, 0, 0))
    out = ((length, count * 384), jnp.bfloat16, pl.BlockSpec((length, 384), lambda j: (0, j)))
    return by_pairs(
        attend_back_kernel,
        "attend_back",
        core,
        (*tables, *rows),
        pieces,
        ((q, lanes), (k, lanes), (v, lanes), (lse, lse_spec)),
        (out,),
        [pltpu.VMEM((128, features), jnp.bfloat16)] + [pltpu.VMEM((length, 128), jnp.float32)] * 3,
    )[0]


def model_rows(kernel, name, left, pieces):
    owns, others = pieces
    length, width = left.shape[0], 2 * owns[0].shape[kernel is into_model_kernel]
    outs = (((length // 2, width), jnp.float32), ((length // 2, width), jnp.bfloat16))
    kernel = functools.partial(kernel, len(owns))
    own, other = on_chip(kernel, name, outs, left, *owns, *others)
    return own, flip_pairs(other, 1)


def flip_pairs(block, distance):
    size = lax.axis_size("dp")
    return lax.ppermute(block, "dp", [(i, i ^ distance) for i in range(size)])


def passed_on(block, step):
    size = lax.axis_size("tensor")
    return lax.ppermute(block, "tensor", [(i, (i + step) % size) for i in range(size)])


def spread(piece):
    pieces = [piece]
    for _ in range(lax.axis_size("tensor") - 1):
        pieces.append(passed_on(pieces[-1], 1))
    return pieces


def collected(pieces):
    total = pieces[-1]
    for piece in reversed(pieces[:-1]):
        total = piece + passed_on(total.astype(jnp.bfloat16), -1).astype(jnp.float32)
    return total


def summed_everywhere(value):
    for distance in (1, 2):
        value = value + flip_pairs(value, distance)
    size = lax.axis_size("tensor")
    for distance in (1, 2):
        value = value + lax.ppermute(value, "tensor", [(i, i ^ distance) for i in range(size)])
    return value


def after(values, token):
    return lax.optimization_barrier((values, token))[0]


def per_chip(
    inputs,
    out_cotangent,
    group_ids,
    group_weights,
    gains,
    qkv_weight,
    out_weight,
    up_weight,
    down_weight,
):
    micro, row_count, width = inputs.shape
    tensor = lax.axis_size("tensor")
    part = row_count // 2
    wide_half = width // 2
    length = tensor * row_count
    half = length // 2
    first = lax.axis_index("section") == 0
    place = lax.axis_index("dp")
    core = place % 2
    upper = place // 2 % 2
    core_zero = core == 0
    low_half = upper == 0

    def ordered(mine, other):
        return jnp.where(core_zero, mine, other), jnp.where(core_zero, other, mine)

    def own_first(values):
        return jnp.where(low_half, values, jnp.roll(values, wide_half, axis=-1))

    def both_rows(own):
        return own, flip_pairs(own, 1)

    def to_chip(block):
        split = block.reshape((micro, 2, part) + block.shape[2:])
        mine = lax.dynamic_index_in_dim(split, core, 1, keepdims=False)
        other = lax.dynamic_index_in_dim(split, 1 - core, 1, keepdims=False)
        return lax.all_to_all(
            jnp.concatenate(ordered(mine, flip_pairs(other, 1))), "tensor", 0, 0, tiled=True
        )

    def from_chip(block):
        spread_out = lax.all_to_all(block, "tensor", 0, 0, tiled=True)
        grouped = spread_out.reshape((2, micro, part) + block.shape[2:])
        mine = lax.dynamic_index_in_dim(grouped, core, 0, keepdims=False)
        other = lax.dynamic_index_in_dim(grouped, 1 - core, 0, keepdims=False)
        pair = ordered(mine, flip_pairs(other, 1))
        return jnp.stack(pair, axis=1).reshape((micro, row_count) + block.shape[2:])

    group_count = group_weights.shape[0]
    matches = group_ids[..., None] == jnp.arange(group_count, dtype=jnp.int32)
    row_scale = jnp.sum(jnp.where(matches, group_weights, 0.0), axis=-1)
    weighted = (out_cotangent.astype(jnp.float32) * row_scale[..., None]).astype(jnp.bfloat16)
    start = to_chip(own_first(jnp.where(first, inputs, weighted))).reshape(half, width)

    def columns(local):
        size = local.shape[-1] // 2
        mid = (0,) * (local.ndim - 2)
        piece = lax.dynamic_slice(
            local, (wide_half * upper, *mid, size * core), (wide_half, *local.shape[1:-1], size)
        )
        pieces = spread(piece.reshape(wide_half, -1))
        return pieces, [flip_pairs(piece, 2) for piece in pieces]

    def rows(local):
        size = local.shape[0] // 2
        pieces = spread(
            lax.dynamic_slice(local, (size * core, wide_half * upper), (size, wide_half))
        )
        return pieces, [flip_pairs(piece, 2) for piece in pieces]

    w_qkv = columns(qkv_weight[0])
    w_out = rows(out_weight[0])
    w_up = columns(up_weight[0])
    w_down = rows(down_weight[0])
    gain = own_first(gains[0])

    turns = jnp.arange(half, dtype=jnp.int32)
    turns = turns // part * row_count + turns % part
    positions = jnp.concatenate([turns + core * part, turns + (1 - core) * part])
    freqs = 10000.0 ** (-2.0 * jnp.arange(HEAD_DIM // 2, dtype=jnp.float32) / HEAD_DIM)
    angles = positions.astype(jnp.float32)[:, None] * freqs[None, :]
    cos_part, sin_part = jnp.cos(angles), jnp.sin(angles)
    tables = (
        jnp.concatenate([cos_part] * 4, axis=1),
        jnp.concatenate([-sin_part, sin_part] * 2, axis=1),
    )
    core_word = core.astype(jnp.int32).reshape(1)
    units = tensor * w_up[0][0].shape[1]
    row32, row16 = ((half, width), jnp.float32), ((half, width), jnp.bfloat16)
    unit16 = ((length, units), jnp.bfloat16)
    sum32 = ((1, width), jnp.float32)

    def forward(layer_input):
        attn_in = both_rows(on_chip(norm_in_kernel, "norm_in", (row16,), gain, layer_input)[0])
        *heads, mixed = attend(core_word, tables, attn_in, w_qkv)
        parts = model_rows(into_model_kernel, "attn_out", mixed, w_out)
        branch, hidden, mlp_in = on_chip(
            after_attention_kernel, "after_attn", (row32, row32, row16), gain, layer_input, *parts
        )
        mlp_in = both_rows(mlp_in)
        kernel = functools.partial(mlp_up_kernel, tensor)
        gelu_out, slope = on_chip(
            kernel, "mlp_up", (unit16, unit16), *mlp_in, *w_up[0], *w_up[1]
        )
        parts = model_rows(into_model_kernel, "mlp_down", gelu_out, w_down)
        mlp_branch, result = on_chip(
            after_mlp_kernel, "after_mlp", (row32, row16), gain, hidden, *parts
        )
        saved = (layer_input, heads, branch, hidden, slope, mlp_branch)
        return result, saved, (attn_in, mixed, mlp_in, gelu_out)

    def backward(grad, saved):
        layer_input, heads, branch, hidden, slope, mlp_branch = saved
        d_down, sum_three = on_chip(
            into_mlp_back_kernel, "into_mlp_back", (row16, sum32), gain, grad, mlp_branch
        )
        d_down = both_rows(d_down)
        kernel = functools.partial(mlp_up_back_kernel, tensor)
        d_up = on_chip(kernel, "mlp_up_back", (unit16,), *d_down, slope, *w_down[0], *w_down[1])[0]
        parts = model_rows(back_to_model_kernel, "mlp_back", d_up, w_up)
        d_hidden, d_attn, sum_one, sum_two = on_chip(
            into_attention_back_kernel,
            "into_attn_back",
            (row32, row16, sum32, sum32),
            gain,
            grad,
            *parts,
            hidden,
            branch,
        )
        d_attn = both_rows(d_attn)
        d_qkv = attend_back(core_word, tables, d_attn, w_out, *heads)
        parts = model_rows(back_to_model_kernel, "attn_back", d_qkv, w_qkv)
        d_input, sum_zero = on_chip(
            out_of_layer_kernel, "out_of_layer", (row16, sum32), gain, layer_input, *parts, d_hidden
        )
        sums = jnp.concatenate([sum_zero, sum_one, sum_two, sum_three])
        return d_input, (d_qkv, d_attn, d_up, d_down), sums

    low_zero, saved_zero, lefts_zero = forward(start)
    low_one, saved_one, lefts_one = forward(shifted(low_zero, "section", 1))
    grad_one, rights_one, gain_one = backward(start, saved_one)
    lows = after((low_zero, low_one), grad_one)
    outputs = from_chip(own_first(jnp.where(first, *lows)).reshape(tensor, part, width))
    grad_zero, rights_zero, gain_zero = backward(shifted(grad_one, "section", -1), saved_zero)
    grads = from_chip(own_first(jnp.where(first, grad_zero, grad_one)).reshape(tensor, part, width))

    def joined(pair):
        return lax.optimization_barrier(jnp.concatenate(pair, axis=0))

    def own_layer(zero, one):
        if isinstance(zero, tuple):
            zero, one = joined(zero), joined(one)
        return jnp.where(first, zero, one)

    attn_in, mixed, mlp_in, gelu_out = map(own_layer, lefts_zero, lefts_one)
    d_qkv, d_attn, d_up, d_down = map(own_layer, rights_zero, rights_one)

    def halves(total, axis):
        own = lax.slice_in_dim(total, 0, wide_half, axis=axis)
        other = lax.slice_in_dim(total, wide_half, width, axis=axis).astype(jnp.bfloat16)
        return own + flip_pairs(other, 2).astype(jnp.float32)

    def sum_columns(left, right):
        size = right.shape[1] // tensor
        pieces = [None] * tensor
        for j in reversed(range(tensor)):
            pieces[j] = halves(contract(left, right[:, j * size : (j + 1) * size]), 0)
        return collected(pieces)

    def sum_rows(left, right):
        size = left.shape[1] // tensor
        pieces = [None] * tensor
        for j in reversed(range(tensor)):
            pieces[j] = halves(contract(left[:, j * size : (j + 1) * size], right), 1)
        return collected(pieces)

    down_sum = sum_rows(gelu_out, d_down)
    up_sum = sum_columns(mlp_in, d_up)
    out_sum = sum_rows(mixed, d_attn)
    qkv_sum = sum_columns(attn_in, d_qkv)

    def by_columns(kept, count):
        size = kept.shape[1]
        kept = kept.reshape(2, wide_half // 2, size)
        mine = lax.dynamic_index_in_dim(kept, core, 0, keepdims=False)
        other = lax.dynamic_index_in_dim(kept, 1 - core, 0, keepdims=False)
        pair = ordered(mine, flip_pairs(other, 1))
        pair = [side.reshape(wide_half // 2, count, size // count) for side in pair]
        return jnp.concatenate(pair, axis=2)

    def by_rows(kept):
        sides = (kept[:, : wide_half // 2], kept[:, wide_half // 2 :])
        mine = jnp.where(core_zero, sides[0], sides[1])
        other = jnp.where(core_zero, sides[1], sides[0])
        return jnp.concatenate(ordered(mine, flip_pairs(other, 1)), axis=0)

    gain_total = summed_everywhere(own_first(jnp.where(first, gain_zero, gain_one)))
    size = width // (tensor * lax.axis_size("dp"))
    spot = (place * tensor + lax.axis_index("tensor")) * size
    gains_grad = lax.dynamic_slice_in_dim(gain_total, spot, size, axis=1)
    return (
        outputs[None],
        grads[None],
        gains_grad[None],
        by_columns(qkv_sum, 3)[None],
        by_rows(out_sum)[None],
        by_columns(up_sum, 1)[:, 0][None],
        by_rows(down_sum)[None],
    )


def takes_chips(sizes):
    return sizes["section"] == 2 and sizes["dp"] == 4 and sizes["tensor"] == 4


def solution(mesh):
    placed = (
        P("dp", "tensor", None),
        P("dp", "tensor", None),
        P("dp", "tensor"),
        P(),
        P("section", None, None),
        P("section", None, None, "tensor"),
        P("section", "tensor", None),
        P("section", None, "tensor"),
        P("section", "tensor", None),
    )
    body = per_chip if takes_chips(dict(mesh.shape)) else per_device
    return jax.shard_map(
        body,
        mesh=mesh,
        in_specs=placed,
        out_specs=(
            P("section", "dp", "tensor", None),
            P("section", "dp", "tensor", None),
            P("section", None, ("dp", "tensor")),
            P("section", "dp", None, "tensor"),
            P("section", "tensor", "dp"),
            P("section", "dp", "tensor"),
            P("section", "tensor", "dp"),
        ),
        check_vma=False,
    )
```

```python
import functools
import math

import jax
import jax.numpy as jnp
from jax import lax
from jax.experimental import pallas as pl
from jax.experimental.pallas import tpu as pltpu
from jax.sharding import PartitionSpec as P

HEAD_DIM = 64


NORM_EPSILON = 1e-06
TILE = 128
CHUNK = 32
KERNEL_VMEM = 40 << 20


def shifted(block, axis, distance):
    devices = range(lax.axis_size(axis))
    route = [(i - distance, i) for i in devices if i - distance in devices]
    return lax.ppermute(block, axis, route)


def norm_rows(vector, weight_gain):
    return (
        vector
        * lax.rsqrt(jnp.mean(vector * vector, axis=-1, keepdims=True) + NORM_EPSILON)
        * weight_gain
    )


def rotary_tables(seq_len, head_width):
    half_width = head_width // 2
    freqs = 10000.0 ** (-2.0 * jnp.arange(half_width, dtype=jnp.float32) / head_width)
    angles = jnp.arange(seq_len, dtype=jnp.float32)[:, None] * freqs[None, :]
    return (jnp.cos(angles), jnp.sin(angles))


def rotate(vector, cos_table, sin_table):
    first_half, second_half = jnp.split(vector, 2, axis=-1)
    cos_part = cos_table[:, None, :]
    sin_part = sin_table[:, None, :]
    return jnp.concatenate(
        [
            first_half * cos_part - second_half * sin_part,
            second_half * cos_part + first_half * sin_part,
        ],
        axis=-1,
    )


def contract(left_rows, right_rows):
    return lax.dot_general(
        left_rows, right_rows, (((0,), (0,)), ((), ())), preferred_element_type=jnp.float32
    )


def gather_rows(row_values, weight):

    def project(shard_rows, offset):
        return (shard_rows, jnp.dot(shard_rows, weight, preferred_element_type=jnp.float32))

    return project(lax.all_gather(row_values, "tensor", axis=0, tiled=True), jnp.int32(0))


def scatter_rows(row_values, weight, row_count):

    def partial_term(offset, span):
        return jnp.dot(row_values, weight, preferred_element_type=jnp.float32)

    return lax.psum_scatter(
        partial_term(jnp.int32(0), lax.axis_size("tensor") * row_count),
        "tensor",
        scatter_dimension=0,
        tiled=True,
    )


def gather_grads(row_values, weight):

    def project(shard_rows, offset):
        return (shard_rows, jnp.dot(shard_rows, weight.T, preferred_element_type=jnp.float32))

    return project(lax.all_gather(row_values, "tensor", axis=0, tiled=True), jnp.int32(0))


def scatter_grads(row_values, weight, row_count):

    def partial_term(offset, span):
        return jnp.dot(row_values, weight.T, preferred_element_type=jnp.float32)

    return lax.psum_scatter(
        partial_term(jnp.int32(0), lax.axis_size("tensor") * row_count),
        "tensor",
        scatter_dimension=0,
        tiled=True,
    )


def attention_probs(queries, key_rows):
    scores = jnp.einsum(
        "qhd,khd->hqk", queries, key_rows, preferred_element_type=jnp.float32
    ) * HEAD_DIM ** (-0.5)
    length = queries.shape[0]
    positions = jnp.arange(length, dtype=jnp.int32)
    causal = positions[:, None] >= positions[None, :]
    scores = jnp.where(causal[None], scores, -1e30)
    expos = jnp.exp(scores - jnp.max(scores, axis=-1, keepdims=True))
    return expos / jnp.sum(expos, axis=-1, keepdims=True)


def layer_forward(layer_input, weights):
    gains, w_qkv, w_out, w_up, w_down = weights
    row_count, model_width = layer_input.shape
    attn_in = norm_rows(layer_input, gains[0]).astype(jnp.bfloat16)
    gathered_a, qkv = gather_rows(attn_in, w_qkv.reshape(model_width, -1))
    length = qkv.shape[0]
    head_count = w_qkv.shape[2] // HEAD_DIM
    qkv = qkv.reshape(length, 3, head_count, HEAD_DIM)
    cos_table, sin_table = rotary_tables(length, HEAD_DIM)
    queries = rotate(qkv[:, 0], cos_table, sin_table).astype(jnp.bfloat16)
    key_rows = rotate(qkv[:, 1], cos_table, sin_table).astype(jnp.bfloat16)
    values = qkv[:, 2].astype(jnp.bfloat16)
    attn_probs = attention_probs(queries, key_rows).astype(jnp.bfloat16)
    mixed = jnp.einsum("hqk,khd->qhd", attn_probs, values, preferred_element_type=jnp.float32)
    mixed = mixed.reshape(length, -1).astype(jnp.bfloat16)
    attn_branch = scatter_rows(mixed, w_out, row_count)
    hidden = layer_input + norm_rows(attn_branch, gains[1])
    mlp_in = norm_rows(hidden, gains[2]).astype(jnp.bfloat16)
    gathered_c, up_act = gather_rows(mlp_in, w_up)
    gelu_out = jax.nn.gelu(up_act, approximate=True).astype(jnp.bfloat16)
    down_branch = scatter_rows(gelu_out, w_down, row_count)
    result = hidden + norm_rows(down_branch, gains[3])
    kept_values = (
        gathered_a,
        queries,
        key_rows,
        values,
        mixed,
        attn_branch,
        hidden,
        gathered_c,
        up_act,
        gelu_out,
        down_branch,
    )
    return (result, kept_values)


def layer_backward(layer_input, grad_result, kept_values, weights):
    gains, w_qkv, w_out, w_up, w_down = weights
    (
        gathered_a,
        queries,
        key_rows,
        values,
        mixed,
        attn_branch,
        hidden,
        gathered_c,
        up_act,
        gelu_out,
        down_branch,
    ) = kept_values
    row_count, model_width = layer_input.shape
    pullback = jax.vjp(norm_rows, down_branch, gains[3])[1]
    grad_down, gain_three = pullback(grad_result)
    gathered_dd, grad_gelu = gather_grads(grad_down.astype(jnp.bfloat16), w_down)
    down_total = contract(gelu_out, gathered_dd)
    pullback = jax.vjp(lambda vector: jax.nn.gelu(vector, approximate=True), up_act)[1]
    grad_up = pullback(grad_gelu)[0].astype(jnp.bfloat16)
    up_total = contract(gathered_c, grad_up)
    grad_mlp = scatter_grads(grad_up, w_up, row_count)
    pullback = jax.vjp(norm_rows, hidden, gains[2])[1]
    grad_norm_mlp, gain_two = pullback(grad_mlp)
    grad_hidden = grad_result + grad_norm_mlp
    pullback = jax.vjp(norm_rows, attn_branch, gains[1])[1]
    grad_attn, gain_one = pullback(grad_hidden)
    gathered_da, grad_mixed = gather_grads(grad_attn.astype(jnp.bfloat16), w_out)
    out_total = contract(mixed, gathered_da)
    length = grad_mixed.shape[0]
    head_count = w_qkv.shape[2] // HEAD_DIM
    grad_mixed = grad_mixed.astype(jnp.bfloat16).reshape(length, head_count, HEAD_DIM)
    attn_probs = attention_probs(queries, key_rows)
    probs_low = attn_probs.astype(jnp.bfloat16)
    grad_probs = jnp.einsum("qhd,khd->hqk", grad_mixed, values, preferred_element_type=jnp.float32)
    grad_values = jnp.einsum(
        "hqk,qhd->khd", probs_low, grad_mixed, preferred_element_type=jnp.float32
    )
    row_dots = jnp.sum(grad_probs * attn_probs, axis=-1, keepdims=True)
    grad_scores = (attn_probs * (grad_probs - row_dots)).astype(jnp.bfloat16)
    scale_value = HEAD_DIM ** (-0.5)
    grad_queries = (
        jnp.einsum("hqk,khd->qhd", grad_scores, key_rows, preferred_element_type=jnp.float32)
        * scale_value
    )
    grad_keys = (
        jnp.einsum("hqk,qhd->khd", grad_scores, queries, preferred_element_type=jnp.float32)
        * scale_value
    )
    cos_table, sin_table = rotary_tables(length, HEAD_DIM)
    pullback = jax.vjp(lambda vector: rotate(vector, cos_table, sin_table), grad_queries)[1]
    grad_q_raw = pullback(grad_queries)[0]
    grad_k_raw = pullback(grad_keys)[0]
    grad_qkv = (
        jnp.stack([grad_q_raw, grad_k_raw, grad_values], axis=1)
        .reshape(length, -1)
        .astype(jnp.bfloat16)
    )
    qkv_total = contract(gathered_a, grad_qkv).reshape(model_width, 3, -1)
    grad_attn_in = scatter_grads(grad_qkv, w_qkv.reshape(model_width, -1), row_count)
    pullback = jax.vjp(norm_rows, layer_input, gains[0])[1]
    grad_norm_in, gain_zero = pullback(grad_attn_in)
    grad_input = grad_hidden + grad_norm_in
    gain_total = jnp.stack([gain_zero, gain_one, gain_two, gain_three])
    return (grad_input, (gain_total, qkv_total, out_total, up_total, down_total))


def lagged(first_section, stacked):
    blank = jnp.zeros_like(stacked[:1])
    earlier = jnp.concatenate([blank, stacked[:-1]])
    later = jnp.concatenate([stacked[1:], blank])
    return jnp.where(first_section, earlier, later)


def per_device(
    inputs,
    out_cotangent,
    group_ids,
    group_weights,
    gains,
    qkv_weight,
    out_weight,
    up_weight,
    down_weight,
):
    weights = (gains[0], qkv_weight[0], out_weight[0], up_weight[0], down_weight[0])
    micro_count, row_count, model_width = inputs.shape
    first_section = lax.axis_index("section") == 0
    group_count = group_weights.shape[0]
    matches = group_ids[..., None] == jnp.arange(group_count, dtype=jnp.int32)
    row_scale = jnp.sum(jnp.where(matches, group_weights, 0.0), axis=-1)
    scaled = out_cotangent.astype(jnp.float32) * row_scale[..., None]
    padded = jnp.concatenate([inputs, jnp.zeros((1, row_count, model_width), jnp.bfloat16)])

    def forward_tick(received, fresh_input):
        layer_input = jnp.where(first_section, fresh_input, received)
        result, kept_values = layer_forward(layer_input.astype(jnp.float32), weights)
        result_low = result.astype(jnp.bfloat16)
        outgoing = shifted(result_low, "section", 1)
        stashed = ()
        return (outgoing, (layer_input, result_low, stashed))

    start_rows = jnp.zeros((row_count, model_width), jnp.bfloat16)
    _, (layer_inputs, layer_results, stashed) = lax.scan(forward_tick, start_rows, padded)
    layer_outputs = jnp.where(first_section, layer_results[:-1], layer_results[1:])[None]
    back_inputs = lagged(first_section, layer_inputs)
    back_stash = jax.tree.map(lambda stacked: lagged(first_section, stacked), stashed)
    grad_padded = jnp.concatenate([scaled, jnp.zeros((1, row_count, model_width), jnp.float32)])
    tick_index = jnp.arange(micro_count + 1, dtype=jnp.int32)
    tick_valid = jnp.where(first_section, tick_index >= 1, tick_index < micro_count).astype(
        jnp.float32
    )

    def backward_tick(carry, step_item):
        received, totals = carry
        layer_input, cotangent, valid_now, stash_now = step_item
        grad_now = jnp.where(first_section, received.astype(jnp.float32), cotangent)
        input_now = layer_input.astype(jnp.float32)
        kept_values = layer_forward(input_now, weights)[1]
        grad_input, layer_grads = layer_backward(input_now, grad_now, kept_values, weights)
        totals = jax.tree.map(lambda total, update: total + valid_now * update, totals, layer_grads)
        grad_low = grad_input.astype(jnp.bfloat16)
        outgoing = shifted(grad_low, "section", -1)
        return ((outgoing, totals), grad_low)

    start_totals = (
        jnp.zeros((4, model_width), jnp.float32),
        jnp.zeros(qkv_weight.shape[1:], jnp.float32),
        jnp.zeros(out_weight.shape[1:], jnp.float32),
        jnp.zeros(up_weight.shape[1:], jnp.float32),
        jnp.zeros(down_weight.shape[1:], jnp.float32),
    )
    (_, totals), grad_lows = lax.scan(
        backward_tick,
        (start_rows, start_totals),
        (back_inputs, grad_padded, tick_valid, back_stash),
    )
    input_grads = jnp.where(first_section, grad_lows[1:], grad_lows[:-1])[None]
    gain_total, qkv_total, out_total, up_total, down_total = totals
    gains_grad = lax.psum_scatter(gain_total, ("dp", "tensor"), scatter_dimension=1, tiled=True)
    qkv_grad, out_grad, up_grad, down_grad = (
        lax.psum_scatter(
            qkv_total.astype(jnp.bfloat16), "dp", scatter_dimension=0, tiled=True
        ).astype(jnp.float32),
        lax.psum_scatter(
            out_total.astype(jnp.bfloat16), "dp", scatter_dimension=1, tiled=True
        ).astype(jnp.float32),
        lax.psum_scatter(
            up_total.astype(jnp.bfloat16), "dp", scatter_dimension=0, tiled=True
        ).astype(jnp.float32),
        lax.psum_scatter(
            down_total.astype(jnp.bfloat16), "dp", scatter_dimension=1, tiled=True
        ).astype(jnp.float32),
    )
    return (
        layer_outputs,
        input_grads,
        gains_grad[None],
        qkv_grad[None],
        out_grad[None],
        up_grad[None],
        down_grad[None],
    )


def rotated(block, cos_rows, sin_rows):
    lane = lax.broadcasted_iota(jnp.int32, block.shape, 1)
    ahead = pltpu.roll(block, 96, 1)
    behind = pltpu.roll(block, 32, 1)
    swapped = jnp.where(lane % 64 < 32, ahead, behind)
    return block * cos_rows + swapped * sin_rows


def dot_nt(left, right):
    return lax.dot_general(
        left, right, (((1,), (1,)), ((), ())), preferred_element_type=jnp.float32
    )


def dot_nn(left, right):
    return jnp.dot(left, right, preferred_element_type=jnp.float32)


def side_by_side(refs):
    return jnp.concatenate([ref[...] for ref in refs], axis=1)


def stacked_up(refs):
    return jnp.concatenate([ref[...] for ref in refs], axis=0)


def edge_masks(core, rows):
    key = lax.broadcasted_iota(jnp.int32, (rows, 2 * rows), 0)
    query = lax.broadcasted_iota(jnp.int32, (rows, 2 * rows), 1)
    mine = query < rows
    place = jnp.where(mine, query + core * rows, query - rows + (1 - core) * rows)
    return (key + core * rows <= place, key + (1 - core) * rows <= place)


def both_sides(value, half, start, stop, axis=0):
    if axis == 0:
        return jnp.concatenate([value[start:stop], value[half + start : half + stop]], axis=0)
    return jnp.concatenate([value[:, start:stop], value[:, half + start : half + stop]], axis=1)


def hidden_scores(scores, masks, tile, step):
    seen = step * tile
    pieces = []
    for side in range(2):
        base = side * (seen + tile)
        if seen:
            pieces.append(scores[base : base + seen])
        pieces.append(jnp.where(masks[side], scores[base + seen : base + seen + tile], -1e30))
    return jnp.concatenate(pieces, axis=0)


def one_head(rows, head):
    lane = lax.broadcasted_iota(jnp.int32, rows.shape, 1)
    return jnp.where(lane // 64 == head, rows, jnp.zeros_like(rows))


def pick_piece(weight, owns, others, axis):
    for j, (own, other) in enumerate(zip(owns, others)):

        @pl.when(pl.program_id(0) == j)
        def _():
            size = own.shape[axis]
            if axis == 0:
                weight[:size] = own[...]
                weight[size:] = other[...]
            else:
                weight[:, :size] = own[...]
                weight[:, size:] = other[...]


def attend_kernel(pieces, core_ref, cos_ref, sin_ref, own_rows, other_rows, *refs):
    owns, others = refs[:pieces], refs[pieces : 2 * pieces]
    q_ref, k_ref, v_ref, lse_ref, mix_ref, weight = refs[2 * pieces :]
    half = own_rows.shape[0]
    tile = TILE
    pick_piece(weight, owns, others, 0)
    proj = dot_nn(stacked_up([own_rows, other_rows]), weight[...])
    cos_rows, sin_rows = cos_ref[...], sin_ref[...]
    q = (rotated(proj[:, :128], cos_rows, sin_rows) * HEAD_DIM ** (-0.5)).astype(jnp.bfloat16)
    k = rotated(proj[:, 128:256], cos_rows, sin_rows).astype(jnp.bfloat16)
    v32 = proj[:, 256:]
    q_ref[0] = q
    k_ref[0] = k
    v_ref[0] = v32.astype(jnp.bfloat16)
    v_flip = v32.T.astype(jnp.bfloat16)
    masks = edge_masks(core_ref[0], tile)

    def scored(step, head):
        stop = (step + 1) * tile
        q_head = one_head(both_sides(q, half, step * tile, stop), head)
        return hidden_scores(dot_nt(both_sides(k, half, 0, stop), q_head), masks, tile, step)

    units = [(step, head) for step in range(half // tile) for head in range(2)]
    ahead = scored(*units[0])
    outs = []
    for spot, (step, head) in enumerate(units):
        scores = ahead
        if spot + 1 < len(units):
            ahead = scored(*units[spot + 1])
        stop = (step + 1) * tile
        top = jnp.max(scores, axis=0, keepdims=True)
        expos = jnp.exp(scores - top)
        total = jnp.sum(expos, axis=0, keepdims=True)
        lse = top + jnp.log(total)
        lse_ref[0, head : head + 1, step * tile : stop] = lse[:, :tile]
        lse_ref[0, head : head + 1, half + step * tile : half + stop] = lse[:, tile:]
        v_cols = both_sides(v_flip, half, 0, stop, axis=1)
        out = dot_nn(v_cols[64 * head : 64 * head + 64], expos.astype(jnp.bfloat16))
        outs.append(out * (1.0 / total))
        if head == 1:
            mixed = jnp.concatenate(outs, axis=0).T.astype(jnp.bfloat16)
            outs = []
            mix_ref[step * tile : stop, :] = mixed[:tile]
            mix_ref[half + step * tile : half + stop, :] = mixed[tile:]


def attend_back_kernel(pieces, core_ref, cos_ref, sin_ref, own_rows, other_rows, *refs):
    owns, others = refs[:pieces], refs[pieces : 2 * pieces]
    q_ref, k_ref, v_ref, lse_ref, out_ref, weight, dq, dk, dv = refs[2 * pieces :]
    half = own_rows.shape[0]
    tile = TILE
    pick_piece(weight, owns, others, 1)
    d_mixed = dot_nt(stacked_up([own_rows, other_rows]), weight[...]).astype(jnp.bfloat16)
    q, k, v = q_ref[0], k_ref[0], v_ref[0]
    k_flip = k.astype(jnp.float32).T.astype(jnp.bfloat16)
    masks = edge_masks(core_ref[0], tile)
    steps = half // tile

    def scored(step, head):
        stop = (step + 1) * tile
        q_head = one_head(both_sides(q, half, step * tile, stop), head)
        g_head = one_head(both_sides(d_mixed, half, step * tile, stop), head)
        scores = hidden_scores(dot_nt(both_sides(k, half, 0, stop), q_head), masks, tile, step)
        return q_head, g_head, scores, dot_nt(both_sides(v, half, 0, stop), g_head)

    units = [(step, head) for step in reversed(range(steps)) for head in range(2)]
    ahead = scored(*units[0])
    dq_flips = []
    dk_sum = dv_sum = None
    for spot, (step, head) in enumerate(units):
        q_head, g_head, scores, d_probs = ahead
        if spot + 1 < len(units):
            ahead = scored(*units[spot + 1])
        stop = (step + 1) * tile
        lse = both_sides(lse_ref[0], half, step * tile, stop, axis=1)
        probs = jnp.exp(scores - lse[head : head + 1])
        dots = jnp.sum(probs * d_probs, axis=0, keepdims=True)
        d_scores = (probs * (d_probs - dots)).astype(jnp.bfloat16)
        dv_part = dot_nn(probs.astype(jnp.bfloat16), g_head)
        dk_part = dot_nn(d_scores, q_head)
        k_cols = both_sides(k_flip, half, 0, stop, axis=1)
        dq_flips.append(dot_nn(k_cols[64 * head : 64 * head + 64], d_scores))
        if head == 0:
            dv_sum, dk_sum = dv_part, dk_part
            continue
        dv_sum, dk_sum = dv_sum + dv_part, dk_sum + dk_part
        dq_rows = jnp.concatenate(dq_flips, axis=0).T * HEAD_DIM ** (-0.5)
        dq_flips = []
        dq[step * tile : stop] = dq_rows[:tile]
        dq[half + step * tile : half + stop] = dq_rows[tile:]
        for base, part in ((0, slice(0, stop)), (half, slice(stop, 2 * stop))):
            if step == steps - 1:
                dk[base : base + stop] = dk_sum[part]
                dv[base : base + stop] = dv_sum[part]
            else:
                dk[base : base + stop] += dk_sum[part]
                dv[base : base + stop] += dv_sum[part]
    cos_rows, sin_rows = cos_ref[...], -sin_ref[...]
    out_ref[:, :128] = rotated(dq[...], cos_rows, sin_rows).astype(jnp.bfloat16)
    out_ref[:, 128:256] = rotated(dk[...], cos_rows, sin_rows).astype(jnp.bfloat16)
    out_ref[:, 256:] = dv[...].astype(jnp.bfloat16)


def split_rows(total, own_ref, other_ref):
    half = own_ref.shape[0]
    own_ref[...] = total[:half]
    other_ref[...] = total[half:].astype(jnp.bfloat16)


def into_model_kernel(lefts, pieces, *refs):
    left, refs = side_by_side(refs[:lefts]), refs[lefts:]
    owns, others = refs[:pieces], refs[pieces : 2 * pieces]
    weight = jnp.concatenate([stacked_up(owns), stacked_up(others)], axis=1)
    split_rows(dot_nn(left, weight), *refs[2 * pieces :])


def back_to_model_kernel(lefts, pieces, *refs):
    left, refs = side_by_side(refs[:lefts]), refs[lefts:]
    owns, others = refs[:pieces], refs[pieces : 2 * pieces]
    weight = jnp.concatenate([side_by_side(owns), side_by_side(others)], axis=0)
    split_rows(dot_nt(left, weight), *refs[2 * pieces :])


def gelu_both(up_act):
    root = math.sqrt(2.0 / math.pi)
    square = up_act * up_act
    rise = 0.5 + 0.5 * jnp.tanh(up_act * (root + root * 0.044715 * square))
    value = up_act * rise
    slope = rise + value * (1.0 - rise) * (2.0 * root + 6.0 * root * 0.044715 * square)
    return value, slope


def mlp_up_kernel(pieces, own_rows, other_rows, *refs):
    owns, others = refs[:pieces], refs[pieces : 2 * pieces]
    gelu_ref, slope_ref = refs[2 * pieces :]
    half = own_rows.shape[0]
    size = owns[0].shape[1]
    step = half // 2
    units = [(j, i) for j in range(pieces) for i in range(4)]

    def product(j, i):
        rows = (own_rows, other_rows)[i // 2][i % 2 * step : (i % 2 + 1) * step]
        return dot_nn(rows, stacked_up([owns[j], others[j]]))

    ahead = product(*units[0])
    for spot, (j, i) in enumerate(units):
        up_act = ahead
        if spot + 1 < len(units):
            ahead = product(*units[spot + 1])
        value, slope = gelu_both(up_act)
        gelu_ref[i * step : (i + 1) * step, j * size : (j + 1) * size] = value.astype(jnp.bfloat16)
        slope_ref[i * step : (i + 1) * step, j * size : (j + 1) * size] = slope.astype(
            jnp.bfloat16
        )


def mlp_up_back_kernel(pieces, own_rows, other_rows, slope_ref, *refs):
    owns, others = refs[:pieces], refs[pieces : 2 * pieces]
    out_ref = refs[-1]
    size = owns[0].shape[0]
    rows = stacked_up([own_rows, other_rows])
    for j in range(pieces):
        cols = slice(j * size, (j + 1) * size)
        d_gelu = dot_nt(rows, side_by_side([owns[j], others[j]]))
        out_ref[:, cols] = (d_gelu * slope_ref[:, cols].astype(jnp.float32)).astype(jnp.bfloat16)


def inverse_size(rows):
    return lax.rsqrt(jnp.mean(rows * rows, axis=-1, keepdims=True) + NORM_EPSILON)


def norm_back(rows, gain, grad):
    scale = inverse_size(rows)
    weighted = grad * gain
    inner = jnp.mean(rows * weighted, axis=-1, keepdims=True)
    return scale * weighted - rows * (scale * scale * scale * inner), rows * scale * grad


def folded(rows):
    return jnp.sum(rows.reshape(rows.shape[0] // 8, 8, rows.shape[1]), axis=0)


def wide(ref, spot):
    return ref[spot, :].astype(jnp.float32)


def by_chunks(count, body, sums=0, width=0):
    def one(i, carry):
        more = body(pl.ds(pl.multiple_of(i * CHUNK, CHUNK), CHUNK))
        return tuple(old + folded(new) for old, new in zip(carry, more))

    start = tuple(jnp.zeros((8, width), jnp.float32) for _ in range(sums))
    totals = lax.fori_loop(0, count // CHUNK, one, start)
    return [jnp.sum(total, axis=0, keepdims=True) for total in totals]


def norm_in_kernel(gain_ref, rows_ref, out_ref):
    def body(spot):
        rows = wide(rows_ref, spot)
        out_ref[spot, :] = (rows * inverse_size(rows) * gain_ref[0:1]).astype(jnp.bfloat16)
        return ()

    by_chunks(rows_ref.shape[0], body)


def after_attention_kernel(
    gain_ref, rows_ref, own_ref, other_ref, branch_ref, hidden_ref, out_ref
):
    def body(spot):
        branch = own_ref[spot, :] + wide(other_ref, spot)
        hidden = wide(rows_ref, spot) + branch * inverse_size(branch) * gain_ref[1:2]
        branch_ref[spot, :] = branch
        hidden_ref[spot, :] = hidden
        out_ref[spot, :] = (hidden * inverse_size(hidden) * gain_ref[2:3]).astype(jnp.bfloat16)
        return ()

    by_chunks(rows_ref.shape[0], body)


def after_mlp_kernel(gain_ref, hidden_ref, own_ref, other_ref, branch_ref, out_ref):
    def body(spot):
        branch = own_ref[spot, :] + wide(other_ref, spot)
        branch_ref[spot, :] = branch
        result = hidden_ref[spot, :] + branch * inverse_size(branch) * gain_ref[3:4]
        out_ref[spot, :] = result.astype(jnp.bfloat16)
        return ()

    by_chunks(hidden_ref.shape[0], body)


def into_mlp_back_kernel(gain_ref, grad_ref, branch_ref, out_ref, sum_ref):
    def body(spot):
        d_rows, d_gain = norm_back(branch_ref[spot, :], gain_ref[3:4], wide(grad_ref, spot))
        out_ref[spot, :] = d_rows.astype(jnp.bfloat16)
        return (d_gain,)

    (sum_ref[...],) = by_chunks(grad_ref.shape[0], body, 1, grad_ref.shape[1])


def into_attention_back_kernel(
    gain_ref, grad_ref, own_ref, other_ref, hidden_ref, branch_ref, d_hidden_ref, out_ref, *sums
):
    def body(spot):
        d_rows = own_ref[spot, :] + wide(other_ref, spot)
        d_rows, d_gain = norm_back(hidden_ref[spot, :], gain_ref[2:3], d_rows)
        d_hidden = wide(grad_ref, spot) + d_rows
        d_hidden_ref[spot, :] = d_hidden
        d_rows, d_first = norm_back(branch_ref[spot, :], gain_ref[1:2], d_hidden)
        out_ref[spot, :] = d_rows.astype(jnp.bfloat16)
        return (d_first, d_gain)

    totals = by_chunks(grad_ref.shape[0], body, 2, grad_ref.shape[1])
    sums[0][...], sums[1][...] = totals


def out_of_layer_kernel(gain_ref, rows_ref, own_ref, other_ref, d_hidden_ref, out_ref, sum_ref):
    def body(spot):
        d_rows = own_ref[spot, :] + wide(other_ref, spot)
        d_rows, d_gain = norm_back(wide(rows_ref, spot), gain_ref[0:1], d_rows)
        out_ref[spot, :] = (d_hidden_ref[spot, :] + d_rows).astype(jnp.bfloat16)
        return (d_gain,)

    (sum_ref[...],) = by_chunks(rows_ref.shape[0], body, 1, rows_ref.shape[1])


def on_chip(kernel, name, outs, *operands):
    space = pl.BlockSpec(memory_space=pltpu.VMEM)
    return pl.pallas_call(
        kernel,
        in_specs=[space] * len(operands),
        out_specs=[space] * len(outs),
        out_shape=[jax.ShapeDtypeStruct(shape, dtype) for shape, dtype in outs],
        compiler_params=pltpu.CompilerParams(vmem_limit_bytes=KERNEL_VMEM),
        name=name,
    )(*operands)


def whole_block(array):
    return pl.BlockSpec(array.shape, lambda j: (0,) * array.ndim)


def by_pairs(kernel, name, core, operands, pieces, blocks, outs, scratch):
    return pl.pallas_call(
        functools.partial(kernel, len(pieces[0])),
        grid=(len(pieces[0]),),
        in_specs=[pl.BlockSpec(memory_space=pltpu.SMEM)]
        + [whole_block(array) for array in (*operands, *pieces[0], *pieces[1])]
        + [spec for _, spec in blocks],
        out_specs=[spec for _, _, spec in outs],
        out_shape=[jax.ShapeDtypeStruct(shape, dtype) for shape, dtype, _ in outs],
        scratch_shapes=scratch,
        compiler_params=pltpu.CompilerParams(vmem_limit_bytes=KERNEL_VMEM),
        name=name,
    )(core, *operands, *pieces[0], *pieces[1], *[array for array, _ in blocks])


def attend(core, tables, rows, pieces):
    half, features = rows[0].shape
    length, count = 2 * half, len(pieces[0])
    lanes = ((count, length, 128), jnp.bfloat16, pl.BlockSpec((1, length, 128), lambda j: (j, 0, 0)))
    lse = ((count, 2, length), jnp.float32, pl.BlockSpec((1, 2, length), lambda j: (j, 0, 0)))
    mixed = ((length, count * 128), jnp.bfloat16, pl.BlockSpec((length, 128), lambda j: (0, j)))
    return by_pairs(
        attend_kernel,
        "attend",
        core,
        (*tables, *rows),
        pieces,
        (),
        (lanes, lanes, lanes, lse, mixed),
        [pltpu.VMEM((features, 384), jnp.bfloat16)],
    )


def attend_back(core, tables, rows, pieces, base, q, k, v, lse):
    half, features = rows[0].shape
    length, count = 2 * half, len(pieces[0])
    lanes = pl.BlockSpec((1, length, 128), lambda j: (base + j, 0, 0))
    lse_spec = pl.BlockSpec((1, 2, length), lambda j: (base + j, 0, 0))
    out = ((length, count * 384), jnp.bfloat16, pl.BlockSpec((length, 384), lambda j: (0, j)))
    return by_pairs(
        attend_back_kernel,
        "attend_back",
        core,
        (*tables, *rows),
        pieces,
        ((q, lanes), (k, lanes), (v, lanes), (lse, lse_spec)),
        (out,),
        [pltpu.VMEM((128, features), jnp.bfloat16)] + [pltpu.VMEM((length, 128), jnp.float32)] * 3,
    )[0]


def model_rows(kernel, name, lefts, pieces):
    owns, others = pieces
    length, width = lefts[0].shape[0], 2 * owns[0].shape[kernel is into_model_kernel]
    outs = (((length // 2, width), jnp.float32), ((length // 2, width), jnp.bfloat16))
    kernel = functools.partial(kernel, len(lefts), len(owns))
    own, other = on_chip(kernel, name, outs, *lefts, *owns, *others)
    return own, flip_pairs(other, 1)


def flip_pairs(block, distance):
    size = lax.axis_size("dp")
    return lax.ppermute(block, "dp", [(i, i ^ distance) for i in range(size)])


def passed_on(block, step):
    size = lax.axis_size("tensor")
    return lax.ppermute(block, "tensor", [(i, (i + step) % size) for i in range(size)])


def summed_everywhere(value):
    for distance in (1, 2):
        value = value + flip_pairs(value, distance)
    size = lax.axis_size("tensor")
    for distance in (1, 2):
        value = value + lax.ppermute(value, "tensor", [(i, i ^ distance) for i in range(size)])
    return value


class Sequence:
    def __init__(self, token):
        self.token = token

    def step(self, *values):
        values, self.token = lax.optimization_barrier((values, self.token))
        return values[0] if len(values) == 1 else values


def per_chip(
    inputs,
    out_cotangent,
    group_ids,
    group_weights,
    gains,
    qkv_weight,
    out_weight,
    up_weight,
    down_weight,
):
    micro, row_count, width = inputs.shape
    tensor = lax.axis_size("tensor")
    part = row_count // 2
    wide_half = width // 2
    length = tensor * row_count
    half = length // 2
    first = lax.axis_index("section") == 0
    place = lax.axis_index("dp")
    core = place % 2
    upper = place // 2 % 2
    core_zero = core == 0
    low_half = upper == 0

    def ordered(mine, other):
        return jnp.where(core_zero, mine, other), jnp.where(core_zero, other, mine)

    def own_first(values):
        return jnp.where(low_half, values, jnp.roll(values, wide_half, axis=-1))

    def both_rows(own):
        return own, flip_pairs(own, 1)

    def to_chip(block):
        split = block.reshape((micro, 2, part) + block.shape[2:])
        mine = lax.dynamic_index_in_dim(split, core, 1, keepdims=False)
        other = lax.dynamic_index_in_dim(split, 1 - core, 1, keepdims=False)
        return lax.all_to_all(
            jnp.concatenate(ordered(mine, flip_pairs(other, 1))), "tensor", 0, 0, tiled=True
        )

    def from_chip(block):
        spread_out = lax.all_to_all(block, "tensor", 0, 0, tiled=True)
        grouped = spread_out.reshape((2, micro, part) + block.shape[2:])
        mine = lax.dynamic_index_in_dim(grouped, core, 0, keepdims=False)
        other = lax.dynamic_index_in_dim(grouped, 1 - core, 0, keepdims=False)
        pair = ordered(mine, flip_pairs(other, 1))
        return jnp.stack(pair, axis=1).reshape((micro, row_count) + block.shape[2:])

    def columns(local):
        size = local.shape[-1] // 2
        mid = (0,) * (local.ndim - 2)
        piece = lax.dynamic_slice(
            local, (wide_half * upper, *mid, size * core), (wide_half, *local.shape[1:-1], size)
        )
        return piece.reshape(wide_half, -1)

    def rows(local):
        size = local.shape[0] // 2
        return lax.dynamic_slice(local, (size * core, wide_half * upper), (size, wide_half))

    core_word = core.astype(jnp.int32).reshape(1)
    order = Sequence(core_word)
    pieces = {
        "qkv": [columns(qkv_weight[0])],
        "out": [rows(out_weight[0])],
        "up": [columns(up_weight[0])],
        "down": [rows(down_weight[0])],
    }
    flown = {name: [] for name in pieces}
    ringing = {}

    def flip(name):
        flown[name].append(flip_pairs(order.step(pieces[name][-1]), 2))

    def ring(name):
        ringing[name] = passed_on(order.step(pieces[name][-1]), 1)

    def caught(name):
        pieces[name].append(order.step(ringing.pop(name)))
        flip(name)

    def whole(name):
        flown[name] = list(order.step(*flown[name]))
        return pieces[name], flown[name]

    group_count = group_weights.shape[0]
    matches = group_ids[..., None] == jnp.arange(group_count, dtype=jnp.int32)
    row_scale = jnp.sum(jnp.where(matches, group_weights, 0.0), axis=-1)
    weighted = (out_cotangent.astype(jnp.float32) * row_scale[..., None]).astype(jnp.bfloat16)
    ring("qkv")
    flip("qkv")
    ring("out")
    flip("out")
    start = to_chip(own_first(jnp.where(first, inputs, weighted))).reshape(half, width)
    flip("up")
    caught("qkv")
    ring("qkv")
    caught("out")
    ring("out")
    flip("down")
    caught("out")
    ring("out")
    caught("qkv")
    ring("qkv")
    ring("up")
    caught("out")
    ring("down")
    start = order.step(start)
    caught("qkv")
    gain = own_first(gains[0])

    turns = jnp.arange(half, dtype=jnp.int32)
    turns = turns // part * row_count + turns % part
    positions = jnp.concatenate([turns + core * part, turns + (1 - core) * part])
    freqs = 10000.0 ** (-2.0 * jnp.arange(HEAD_DIM // 2, dtype=jnp.float32) / HEAD_DIM)
    angles = positions.astype(jnp.float32)[:, None] * freqs[None, :]
    cos_part, sin_part = jnp.cos(angles), jnp.sin(angles)
    tables = (
        jnp.concatenate([cos_part] * 4, axis=1),
        jnp.concatenate([-sin_part, sin_part] * 2, axis=1),
    )
    units = tensor * pieces["up"][0].shape[1]
    row32, row16 = ((half, width), jnp.float32), ((half, width), jnp.bfloat16)
    unit16 = ((length, units), jnp.bfloat16)
    sum32 = ((1, width), jnp.float32)

    def forward(layer_input, between=None):
        pause = between or (lambda: None)
        attn_in = both_rows(on_chip(norm_in_kernel, "norm_in", (row16,), gain, layer_input)[0])
        pause()
        *heads, mixed = attend(core_word, tables, order.step(*attn_in), weights["qkv"])
        mixed = order.step(mixed)
        pause()
        parts = model_rows(into_model_kernel, "attn_out", [mixed], weights["out"])
        branch, hidden, mlp_in = on_chip(
            after_attention_kernel, "after_attn", (row32, row32, row16), gain, layer_input, *parts
        )
        mlp_in = both_rows(order.step(mlp_in))
        pause()
        kernel = functools.partial(mlp_up_kernel, tensor)
        gelu_out, slope = on_chip(
            kernel, "mlp_up", (unit16, unit16), *mlp_in, *weights["up"][0], *weights["up"][1]
        )
        gelu_out = order.step(gelu_out)
        pause()
        parts = model_rows(into_model_kernel, "mlp_down", [gelu_out], weights["down"])
        mlp_branch, result = on_chip(
            after_mlp_kernel, "after_mlp", (row32, row16), gain, hidden, *parts
        )
        saved = (layer_input, heads, branch, hidden, slope, mlp_branch)
        return result, saved, (attn_in, mixed, mlp_in, gelu_out)

    def backward(grad, saved, between=None):
        pause = between or (lambda **new: None)
        layer_input, heads, branch, hidden, slope, mlp_branch = saved
        d_down, sum_three = on_chip(
            into_mlp_back_kernel, "into_mlp_back", (row16, sum32), gain, grad, mlp_branch
        )
        d_down = both_rows(d_down)
        kernel = functools.partial(mlp_up_back_kernel, tensor)
        d_up = on_chip(
            kernel, "mlp_up_back", (unit16,), *d_down, slope, *weights["down"][0], *weights["down"][1]
        )[0]
        pause(d_down=d_down)
        d_up = order.step(d_up)
        parts = model_rows(back_to_model_kernel, "mlp_back", [d_up], weights["up"])
        pause(d_up=d_up)
        d_hidden, d_attn, sum_one, sum_two = on_chip(
            into_attention_back_kernel,
            "into_attn_back",
            (row32, row16, sum32, sum32),
            gain,
            grad,
            *parts,
            hidden,
            branch,
        )
        d_attn = both_rows(order.step(d_attn))
        pause(d_attn=d_attn)
        d_qkv = []
        for base in range(0, tensor, 2):
            some = [side[base : base + 2] for side in weights["out"]]
            rows_now = order.step(*d_attn)
            d_qkv.append(attend_back(core_word, tables, rows_now, some, base, *heads))
            d_qkv[-1] = order.step(d_qkv[-1])
            pause(d_qkv=d_qkv[-1])
        parts = model_rows(back_to_model_kernel, "attn_back", d_qkv, weights["qkv"])
        d_input, sum_zero = on_chip(
            out_of_layer_kernel, "out_of_layer", (row16, sum32), gain, layer_input, *parts, d_hidden
        )
        sums = jnp.concatenate([sum_zero, sum_one, sum_two, sum_three])
        return order.step(d_input), (d_qkv, d_attn, d_up, d_down), sums

    weights = {}

    def arrivals():
        caught("up")
        ring("up")
        caught("down")
        ring("down")
        weights["qkv"] = whole("qkv")
        yield
        caught("up")
        ring("up")
        caught("down")
        ring("down")
        weights["out"] = whole("out")
        yield
        caught("up")
        caught("down")
        weights["up"] = whole("up")
        yield
        weights["down"] = whole("down")
        yield

    steps = arrivals()
    low_zero, saved_zero, lefts_zero = forward(start, lambda: next(steps))
    low_zero = order.step(low_zero)
    low_one, saved_one, lefts_one = forward(shifted(low_zero, "section", 1))
    grad_one, rights_one, gain_one = backward(start, saved_one)
    received = shifted(grad_one, "section", -1)

    def joined(pair):
        return lax.optimization_barrier(jnp.concatenate(pair, axis=0))

    def own_layer(zero, one):
        if isinstance(zero, tuple):
            zero, one = joined(zero), joined(one)
        return jnp.where(first, zero, one)

    lows = order.step(low_zero, low_one)
    outputs = from_chip(own_first(jnp.where(first, *lows)).reshape(tensor, part, width))
    lefts_zero, lefts_one = order.step(lefts_zero, lefts_one)
    attn_in, mixed, mlp_in, gelu_out = map(own_layer, lefts_zero, lefts_one)
    attn_in, mixed, mlp_in, gelu_out = order.step(attn_in, mixed, mlp_in, gelu_out)
    received = order.step(received)

    sums = {name: [None] * tensor for name in pieces}
    moving = {}

    def halves(name, j, total, axis):
        own = lax.slice_in_dim(total, 0, wide_half, axis=axis)
        other = lax.slice_in_dim(total, wide_half, width, axis=axis).astype(jnp.bfloat16)
        own, other = order.step(own, other)
        sums[name][j] = (own, flip_pairs(other, 2))

    def column_piece(name, j, left, right):
        halves(name, j, contract(*order.step(left, right)), 0)

    def row_piece(name, j, left, right):
        halves(name, j, contract(*order.step(left, right)), 1)

    def gathered(name, j):
        own, other = sums[name][j]
        total = own + order.step(other).astype(jnp.float32)
        if name in moving:
            total = total + order.step(moving.pop(name)).astype(jnp.float32)
        if j == 0:
            sums[name] = total
        else:
            moving[name] = passed_on(order.step(total.astype(jnp.bfloat16)), -1)

    def block(array, j, count=tensor):
        size = array.shape[1] // count
        return array[:, j * size : (j + 1) * size]

    new_one = {"d_qkv": list(rights_one[0]), "d_attn": rights_one[1], "d_up": rights_one[2]}
    new_one["d_down"] = rights_one[3]
    order_back = list(reversed(range(tensor)))

    def departures():
        new = yield
        d_down = own_layer(new["d_down"], new_one["d_down"])
        for j in order_back:
            row_piece("down", j, block(gelu_out, j), d_down)
        new = yield
        d_up = own_layer(new["d_up"], new_one["d_up"])
        for j in order_back:
            column_piece("up", j, mlp_in, block(d_up, j))
        new = yield
        d_attn = own_layer(new["d_attn"], new_one["d_attn"])
        gathered("down", 3)
        new = yield
        upper_pairs = []
        for half_pairs in range(2):
            d_qkv = own_layer(new["d_qkv"], new_one["d_qkv"][half_pairs])
            upper_pairs.append(d_qkv)
            if half_pairs == 0:
                gathered("down", 2)
                gathered("up", 3)
                new = yield
        gathered("down", 1)
        gathered("up", 2)
        for j in order_back:
            column_piece("qkv", j, attn_in, block(upper_pairs[j // 2], j % 2, 2))
        for j in order_back:
            row_piece("out", j, block(mixed, j), d_attn)
        yield

    leaving = departures()
    next(leaving)
    grad_zero, rights_zero, gain_zero = backward(
        received, saved_zero, lambda **new: leaving.send(new)
    )
    gathered("down", 0)
    gathered("up", 1)
    gathered("qkv", 3)
    gathered("up", 0)
    gathered("qkv", 2)
    gathered("out", 3)
    gathered("qkv", 1)
    gathered("out", 2)
    gathered("qkv", 0)
    gathered("out", 1)
    gathered("out", 0)
    down_sum, up_sum, out_sum, qkv_sum = (sums[name] for name in ("down", "up", "out", "qkv"))
    grads = from_chip(own_first(jnp.where(first, grad_zero, grad_one)).reshape(tensor, part, width))

    def by_columns(kept, count):
        size = kept.shape[1]
        kept = kept.reshape(2, wide_half // 2, size)
        mine = lax.dynamic_index_in_dim(kept, core, 0, keepdims=False)
        other = lax.dynamic_index_in_dim(kept, 1 - core, 0, keepdims=False)
        pair = ordered(mine, flip_pairs(other, 1))
        pair = [side.reshape(wide_half // 2, count, size // count) for side in pair]
        return jnp.concatenate(pair, axis=2)

    def by_rows(kept):
        sides = (kept[:, : wide_half // 2], kept[:, wide_half // 2 :])
        mine = jnp.where(core_zero, sides[0], sides[1])
        other = jnp.where(core_zero, sides[1], sides[0])
        return jnp.concatenate(ordered(mine, flip_pairs(other, 1)), axis=0)

    gain_total = summed_everywhere(own_first(jnp.where(first, gain_zero, gain_one)))
    size = width // (tensor * lax.axis_size("dp"))
    spot = (place * tensor + lax.axis_index("tensor")) * size
    gains_grad = lax.dynamic_slice_in_dim(gain_total, spot, size, axis=1)
    return (
        outputs[None],
        grads[None],
        gains_grad[None],
        by_columns(qkv_sum, 3)[None],
        by_rows(out_sum)[None],
        by_columns(up_sum, 1)[:, 0][None],
        by_rows(down_sum)[None],
    )


def takes_chips(sizes):
    return sizes["section"] == 2 and sizes["dp"] == 4 and sizes["tensor"] == 4


def solution(mesh):
    placed = (
        P("dp", "tensor", None),
        P("dp", "tensor", None),
        P("dp", "tensor"),
        P(),
        P("section", None, None),
        P("section", None, None, "tensor"),
        P("section", "tensor", None),
        P("section", None, "tensor"),
        P("section", "tensor", None),
    )
    body = per_chip if takes_chips(dict(mesh.shape)) else per_device
    return jax.shard_map(
        body,
        mesh=mesh,
        in_specs=placed,
        out_specs=(
            P("section", "dp", "tensor", None),
            P("section", "dp", "tensor", None),
            P("section", None, ("dp", "tensor")),
            P("section", "dp", None, "tensor"),
            P("section", "tensor", "dp"),
            P("section", "dp", "tensor"),
            P("section", "tensor", "dp"),
        ),
        check_vma=False,
    )
```

```python
import functools
import math

import jax
import jax.numpy as jnp
from jax import lax
from jax.experimental import pallas as pl
from jax.experimental.pallas import tpu as pltpu
from jax.sharding import PartitionSpec as P

HEAD_DIM = 64


NORM_EPSILON = 1e-06
TILE = 128
PAIR_WORK = 1024
QKV = slice(0, 384)
OUT = slice(384, 512)
CHUNK = 32
KERNEL_VMEM = 24 << 20
ROWS_VMEM = 8 << 20


def shifted(block, axis, distance):
    devices = range(lax.axis_size(axis))
    route = [(i - distance, i) for i in devices if i - distance in devices]
    return lax.ppermute(block, axis, route)


def norm_rows(vector, weight_gain):
    return (
        vector
        * lax.rsqrt(jnp.mean(vector * vector, axis=-1, keepdims=True) + NORM_EPSILON)
        * weight_gain
    )


def rotary_tables(seq_len, head_width):
    half_width = head_width // 2
    freqs = 10000.0 ** (-2.0 * jnp.arange(half_width, dtype=jnp.float32) / head_width)
    angles = jnp.arange(seq_len, dtype=jnp.float32)[:, None] * freqs[None, :]
    return (jnp.cos(angles), jnp.sin(angles))


def rotate(vector, cos_table, sin_table):
    first_half, second_half = jnp.split(vector, 2, axis=-1)
    cos_part = cos_table[:, None, :]
    sin_part = sin_table[:, None, :]
    return jnp.concatenate(
        [
            first_half * cos_part - second_half * sin_part,
            second_half * cos_part + first_half * sin_part,
        ],
        axis=-1,
    )


def contract(left_rows, right_rows):
    return lax.dot_general(
        left_rows, right_rows, (((0,), (0,)), ((), ())), preferred_element_type=jnp.float32
    )


def gather_rows(row_values, weight):

    def project(shard_rows, offset):
        return (shard_rows, jnp.dot(shard_rows, weight, preferred_element_type=jnp.float32))

    return project(lax.all_gather(row_values, "tensor", axis=0, tiled=True), jnp.int32(0))


def scatter_rows(row_values, weight, row_count):

    def partial_term(offset, span):
        return jnp.dot(row_values, weight, preferred_element_type=jnp.float32)

    return lax.psum_scatter(
        partial_term(jnp.int32(0), lax.axis_size("tensor") * row_count),
        "tensor",
        scatter_dimension=0,
        tiled=True,
    )


def gather_grads(row_values, weight):

    def project(shard_rows, offset):
        return (shard_rows, jnp.dot(shard_rows, weight.T, preferred_element_type=jnp.float32))

    return project(lax.all_gather(row_values, "tensor", axis=0, tiled=True), jnp.int32(0))


def scatter_grads(row_values, weight, row_count):

    def partial_term(offset, span):
        return jnp.dot(row_values, weight.T, preferred_element_type=jnp.float32)

    return lax.psum_scatter(
        partial_term(jnp.int32(0), lax.axis_size("tensor") * row_count),
        "tensor",
        scatter_dimension=0,
        tiled=True,
    )


def attention_probs(queries, key_rows):
    scores = jnp.einsum(
        "qhd,khd->hqk", queries, key_rows, preferred_element_type=jnp.float32
    ) * HEAD_DIM ** (-0.5)
    length = queries.shape[0]
    positions = jnp.arange(length, dtype=jnp.int32)
    causal = positions[:, None] >= positions[None, :]
    scores = jnp.where(causal[None], scores, -1e30)
    expos = jnp.exp(scores - jnp.max(scores, axis=-1, keepdims=True))
    return expos / jnp.sum(expos, axis=-1, keepdims=True)


def layer_forward(layer_input, weights):
    gains, w_qkv, w_out, w_up, w_down = weights
    row_count, model_width = layer_input.shape
    attn_in = norm_rows(layer_input, gains[0]).astype(jnp.bfloat16)
    gathered_a, qkv = gather_rows(attn_in, w_qkv.reshape(model_width, -1))
    length = qkv.shape[0]
    head_count = w_qkv.shape[2] // HEAD_DIM
    qkv = qkv.reshape(length, 3, head_count, HEAD_DIM)
    cos_table, sin_table = rotary_tables(length, HEAD_DIM)
    queries = rotate(qkv[:, 0], cos_table, sin_table).astype(jnp.bfloat16)
    key_rows = rotate(qkv[:, 1], cos_table, sin_table).astype(jnp.bfloat16)
    values = qkv[:, 2].astype(jnp.bfloat16)
    attn_probs = attention_probs(queries, key_rows).astype(jnp.bfloat16)
    mixed = jnp.einsum("hqk,khd->qhd", attn_probs, values, preferred_element_type=jnp.float32)
    mixed = mixed.reshape(length, -1).astype(jnp.bfloat16)
    attn_branch = scatter_rows(mixed, w_out, row_count)
    hidden = layer_input + norm_rows(attn_branch, gains[1])
    mlp_in = norm_rows(hidden, gains[2]).astype(jnp.bfloat16)
    gathered_c, up_act = gather_rows(mlp_in, w_up)
    gelu_out = jax.nn.gelu(up_act, approximate=True).astype(jnp.bfloat16)
    down_branch = scatter_rows(gelu_out, w_down, row_count)
    result = hidden + norm_rows(down_branch, gains[3])
    kept_values = (
        gathered_a,
        queries,
        key_rows,
        values,
        mixed,
        attn_branch,
        hidden,
        gathered_c,
        up_act,
        gelu_out,
        down_branch,
    )
    return (result, kept_values)


def layer_backward(layer_input, grad_result, kept_values, weights):
    gains, w_qkv, w_out, w_up, w_down = weights
    (
        gathered_a,
        queries,
        key_rows,
        values,
        mixed,
        attn_branch,
        hidden,
        gathered_c,
        up_act,
        gelu_out,
        down_branch,
    ) = kept_values
    row_count, model_width = layer_input.shape
    pullback = jax.vjp(norm_rows, down_branch, gains[3])[1]
    grad_down, gain_three = pullback(grad_result)
    gathered_dd, grad_gelu = gather_grads(grad_down.astype(jnp.bfloat16), w_down)
    down_total = contract(gelu_out, gathered_dd)
    pullback = jax.vjp(lambda vector: jax.nn.gelu(vector, approximate=True), up_act)[1]
    grad_up = pullback(grad_gelu)[0].astype(jnp.bfloat16)
    up_total = contract(gathered_c, grad_up)
    grad_mlp = scatter_grads(grad_up, w_up, row_count)
    pullback = jax.vjp(norm_rows, hidden, gains[2])[1]
    grad_norm_mlp, gain_two = pullback(grad_mlp)
    grad_hidden = grad_result + grad_norm_mlp
    pullback = jax.vjp(norm_rows, attn_branch, gains[1])[1]
    grad_attn, gain_one = pullback(grad_hidden)
    gathered_da, grad_mixed = gather_grads(grad_attn.astype(jnp.bfloat16), w_out)
    out_total = contract(mixed, gathered_da)
    length = grad_mixed.shape[0]
    head_count = w_qkv.shape[2] // HEAD_DIM
    grad_mixed = grad_mixed.astype(jnp.bfloat16).reshape(length, head_count, HEAD_DIM)
    attn_probs = attention_probs(queries, key_rows)
    probs_low = attn_probs.astype(jnp.bfloat16)
    grad_probs = jnp.einsum("qhd,khd->hqk", grad_mixed, values, preferred_element_type=jnp.float32)
    grad_values = jnp.einsum(
        "hqk,qhd->khd", probs_low, grad_mixed, preferred_element_type=jnp.float32
    )
    row_dots = jnp.sum(grad_probs * attn_probs, axis=-1, keepdims=True)
    grad_scores = (attn_probs * (grad_probs - row_dots)).astype(jnp.bfloat16)
    scale_value = HEAD_DIM ** (-0.5)
    grad_queries = (
        jnp.einsum("hqk,khd->qhd", grad_scores, key_rows, preferred_element_type=jnp.float32)
        * scale_value
    )
    grad_keys = (
        jnp.einsum("hqk,qhd->khd", grad_scores, queries, preferred_element_type=jnp.float32)
        * scale_value
    )
    cos_table, sin_table = rotary_tables(length, HEAD_DIM)
    pullback = jax.vjp(lambda vector: rotate(vector, cos_table, sin_table), grad_queries)[1]
    grad_q_raw = pullback(grad_queries)[0]
    grad_k_raw = pullback(grad_keys)[0]
    grad_qkv = (
        jnp.stack([grad_q_raw, grad_k_raw, grad_values], axis=1)
        .reshape(length, -1)
        .astype(jnp.bfloat16)
    )
    qkv_total = contract(gathered_a, grad_qkv).reshape(model_width, 3, -1)
    grad_attn_in = scatter_grads(grad_qkv, w_qkv.reshape(model_width, -1), row_count)
    pullback = jax.vjp(norm_rows, layer_input, gains[0])[1]
    grad_norm_in, gain_zero = pullback(grad_attn_in)
    grad_input = grad_hidden + grad_norm_in
    gain_total = jnp.stack([gain_zero, gain_one, gain_two, gain_three])
    return (grad_input, (gain_total, qkv_total, out_total, up_total, down_total))


def lagged(first_section, stacked):
    blank = jnp.zeros_like(stacked[:1])
    earlier = jnp.concatenate([blank, stacked[:-1]])
    later = jnp.concatenate([stacked[1:], blank])
    return jnp.where(first_section, earlier, later)


def per_device(
    inputs,
    out_cotangent,
    group_ids,
    group_weights,
    gains,
    qkv_weight,
    out_weight,
    up_weight,
    down_weight,
):
    weights = (gains[0], qkv_weight[0], out_weight[0], up_weight[0], down_weight[0])
    micro_count, row_count, model_width = inputs.shape
    first_section = lax.axis_index("section") == 0
    group_count = group_weights.shape[0]
    matches = group_ids[..., None] == jnp.arange(group_count, dtype=jnp.int32)
    row_scale = jnp.sum(jnp.where(matches, group_weights, 0.0), axis=-1)
    scaled = out_cotangent.astype(jnp.float32) * row_scale[..., None]
    padded = jnp.concatenate([inputs, jnp.zeros((1, row_count, model_width), jnp.bfloat16)])

    def forward_tick(received, fresh_input):
        layer_input = jnp.where(first_section, fresh_input, received)
        result, kept_values = layer_forward(layer_input.astype(jnp.float32), weights)
        result_low = result.astype(jnp.bfloat16)
        outgoing = shifted(result_low, "section", 1)
        stashed = ()
        return (outgoing, (layer_input, result_low, stashed))

    start_rows = jnp.zeros((row_count, model_width), jnp.bfloat16)
    _, (layer_inputs, layer_results, stashed) = lax.scan(forward_tick, start_rows, padded)
    layer_outputs = jnp.where(first_section, layer_results[:-1], layer_results[1:])[None]
    back_inputs = lagged(first_section, layer_inputs)
    back_stash = jax.tree.map(lambda stacked: lagged(first_section, stacked), stashed)
    grad_padded = jnp.concatenate([scaled, jnp.zeros((1, row_count, model_width), jnp.float32)])
    tick_index = jnp.arange(micro_count + 1, dtype=jnp.int32)
    tick_valid = jnp.where(first_section, tick_index >= 1, tick_index < micro_count).astype(
        jnp.float32
    )

    def backward_tick(carry, step_item):
        received, totals = carry
        layer_input, cotangent, valid_now, stash_now = step_item
        grad_now = jnp.where(first_section, received.astype(jnp.float32), cotangent)
        input_now = layer_input.astype(jnp.float32)
        kept_values = layer_forward(input_now, weights)[1]
        grad_input, layer_grads = layer_backward(input_now, grad_now, kept_values, weights)
        totals = jax.tree.map(lambda total, update: total + valid_now * update, totals, layer_grads)
        grad_low = grad_input.astype(jnp.bfloat16)
        outgoing = shifted(grad_low, "section", -1)
        return ((outgoing, totals), grad_low)

    start_totals = (
        jnp.zeros((4, model_width), jnp.float32),
        jnp.zeros(qkv_weight.shape[1:], jnp.float32),
        jnp.zeros(out_weight.shape[1:], jnp.float32),
        jnp.zeros(up_weight.shape[1:], jnp.float32),
        jnp.zeros(down_weight.shape[1:], jnp.float32),
    )
    (_, totals), grad_lows = lax.scan(
        backward_tick,
        (start_rows, start_totals),
        (back_inputs, grad_padded, tick_valid, back_stash),
    )
    input_grads = jnp.where(first_section, grad_lows[1:], grad_lows[:-1])[None]
    gain_total, qkv_total, out_total, up_total, down_total = totals
    gains_grad = lax.psum_scatter(gain_total, ("dp", "tensor"), scatter_dimension=1, tiled=True)
    qkv_grad, out_grad, up_grad, down_grad = (
        lax.psum_scatter(
            qkv_total.astype(jnp.bfloat16), "dp", scatter_dimension=0, tiled=True
        ).astype(jnp.float32),
        lax.psum_scatter(
            out_total.astype(jnp.bfloat16), "dp", scatter_dimension=1, tiled=True
        ).astype(jnp.float32),
        lax.psum_scatter(
            up_total.astype(jnp.bfloat16), "dp", scatter_dimension=0, tiled=True
        ).astype(jnp.float32),
        lax.psum_scatter(
            down_total.astype(jnp.bfloat16), "dp", scatter_dimension=1, tiled=True
        ).astype(jnp.float32),
    )
    return (
        layer_outputs,
        input_grads,
        gains_grad[None],
        qkv_grad[None],
        out_grad[None],
        up_grad[None],
        down_grad[None],
    )


def rotated(block, cos_rows, sin_rows):
    lane = lax.broadcasted_iota(jnp.int32, block.shape, 1)
    ahead = pltpu.roll(block, 96, 1)
    behind = pltpu.roll(block, 32, 1)
    swapped = jnp.where(lane % 64 < 32, ahead, behind)
    return block * cos_rows + swapped * sin_rows


def dot_nt(left, right):
    return lax.dot_general(
        left, right, (((1,), (1,)), ((), ())), preferred_element_type=jnp.float32
    )


def dot_nn(left, right):
    return jnp.dot(left, right, preferred_element_type=jnp.float32)


def model_weight(owns, others, cols):
    sides = [jnp.concatenate([ref[:, cols] for ref in refs], axis=1) for refs in (owns, others)]
    return jnp.concatenate(sides, axis=0)


def stacked_up(values):
    return jnp.concatenate(values, axis=0)


def edge_masks(core, rows):
    key = lax.broadcasted_iota(jnp.int32, (rows, 2 * rows), 0)
    query = lax.broadcasted_iota(jnp.int32, (rows, 2 * rows), 1)
    mine = query < rows
    place = jnp.where(mine, query + core * rows, query - rows + (1 - core) * rows)
    return (key + core * rows <= place, key + (1 - core) * rows <= place)


def both_sides(value, half, start, stop, axis=0):
    if axis == 0:
        return jnp.concatenate([value[start:stop], value[half + start : half + stop]], axis=0)
    return jnp.concatenate([value[:, start:stop], value[:, half + start : half + stop]], axis=1)


def hidden_scores(scores, masks, tile, step):
    seen = step * tile
    pieces = []
    for side in range(2):
        base = side * (seen + tile)
        if seen:
            pieces.append(scores[base : base + seen])
        pieces.append(jnp.where(masks[side], scores[base + seen : base + seen + tile], -1e30))
    return jnp.concatenate(pieces, axis=0)


def one_head(rows, head):
    lane = lax.broadcasted_iota(jnp.int32, rows.shape, 1)
    return jnp.where(lane // 64 == head, rows, jnp.zeros_like(rows))


def pick_piece(weight, owns, others, cols):
    for j, (own, other) in enumerate(zip(owns, others)):

        @pl.when(pl.program_id(0) == j)
        def _():
            size = own.shape[0]
            weight[:size] = own[:, cols]
            weight[size:] = other[:, cols]


def attend_kernel(pieces, core_ref, cos_ref, sin_ref, own_rows, other_rows, *refs):
    owns, others = refs[:pieces], refs[pieces : 2 * pieces]
    q_ref, k_ref, v_ref, lse_ref, mix_ref, weight = refs[2 * pieces :]
    half = own_rows.shape[0]
    tile = TILE
    pick_piece(weight, owns, others, QKV)
    proj = dot_nn(stacked_up([own_rows[...], other_rows[...]]), weight[...])
    cos_rows, sin_rows = cos_ref[...], sin_ref[...]
    q = (rotated(proj[:, :128], cos_rows, sin_rows) * HEAD_DIM ** (-0.5)).astype(jnp.bfloat16)
    k = rotated(proj[:, 128:256], cos_rows, sin_rows).astype(jnp.bfloat16)
    v32 = proj[:, 256:]
    q_ref[0] = q
    k_ref[0] = k
    v_ref[0] = v32.astype(jnp.bfloat16)
    v_flip = v32.T.astype(jnp.bfloat16)
    masks = edge_masks(core_ref[0], tile)

    def scored(step, head):
        stop = (step + 1) * tile
        q_head = one_head(both_sides(q, half, step * tile, stop), head)
        return hidden_scores(dot_nt(both_sides(k, half, 0, stop), q_head), masks, tile, step)

    units = [(step, head) for step in range(half // tile) for head in range(2)]
    ahead = scored(*units[0])
    outs = []
    for spot, (step, head) in enumerate(units):
        scores = ahead
        if spot + 1 < len(units):
            ahead = scored(*units[spot + 1])
        stop = (step + 1) * tile
        top = jnp.max(scores, axis=0, keepdims=True)
        expos = jnp.exp(scores - top)
        total = jnp.sum(expos, axis=0, keepdims=True)
        lse = top + jnp.log(total)
        lse_ref[0, head : head + 1, step * tile : stop] = lse[:, :tile]
        lse_ref[0, head : head + 1, half + step * tile : half + stop] = lse[:, tile:]
        v_cols = both_sides(v_flip, half, 0, stop, axis=1)
        out = dot_nn(v_cols[64 * head : 64 * head + 64], expos.astype(jnp.bfloat16))
        outs.append(out * (1.0 / total))
        if head == 1:
            mixed = jnp.concatenate(outs, axis=0).T.astype(jnp.bfloat16)
            outs = []
            mix_ref[step * tile : stop, :] = mixed[:tile]
            mix_ref[half + step * tile : half + stop, :] = mixed[tile:]


def attend_back_kernel(pieces, core_ref, cos_ref, sin_ref, own_rows, other_rows, *refs):
    owns, others = refs[:pieces], refs[pieces : 2 * pieces]
    q_ref, k_ref, v_ref, lse_ref, out_ref, weight, dq, dk, dv = refs[2 * pieces :]
    half = own_rows.shape[0]
    tile = TILE
    pick_piece(weight, owns, others, OUT)
    rows = stacked_up([own_rows[...], other_rows[...]])
    d_mixed = dot_nn(rows, weight[...]).astype(jnp.bfloat16)
    q, k, v = q_ref[0], k_ref[0], v_ref[0]
    k_flip = k.astype(jnp.float32).T.astype(jnp.bfloat16)
    masks = edge_masks(core_ref[0], tile)
    steps = half // tile

    def scored(step, head):
        stop = (step + 1) * tile
        q_head = one_head(both_sides(q, half, step * tile, stop), head)
        g_head = one_head(both_sides(d_mixed, half, step * tile, stop), head)
        scores = hidden_scores(dot_nt(both_sides(k, half, 0, stop), q_head), masks, tile, step)
        return q_head, g_head, scores, dot_nt(both_sides(v, half, 0, stop), g_head)

    units = [(step, head) for step in reversed(range(steps)) for head in range(2)]
    ahead = scored(*units[0])
    dq_flips = []
    dk_sum = dv_sum = None
    for spot, (step, head) in enumerate(units):
        q_head, g_head, scores, d_probs = ahead
        if spot + 1 < len(units):
            ahead = scored(*units[spot + 1])
        stop = (step + 1) * tile
        lse = both_sides(lse_ref[0], half, step * tile, stop, axis=1)
        probs = jnp.exp(scores - lse[head : head + 1])
        dots = jnp.sum(probs * d_probs, axis=0, keepdims=True)
        d_scores = (probs * (d_probs - dots)).astype(jnp.bfloat16)
        dv_part = dot_nn(probs.astype(jnp.bfloat16), g_head)
        dk_part = dot_nn(d_scores, q_head)
        k_cols = both_sides(k_flip, half, 0, stop, axis=1)
        dq_flips.append(dot_nn(k_cols[64 * head : 64 * head + 64], d_scores))
        if head == 0:
            dv_sum, dk_sum = dv_part, dk_part
            continue
        dv_sum, dk_sum = dv_sum + dv_part, dk_sum + dk_part
        dq_rows = jnp.concatenate(dq_flips, axis=0).T * HEAD_DIM ** (-0.5)
        dq_flips = []
        dq[step * tile : stop] = dq_rows[:tile]
        dq[half + step * tile : half + stop] = dq_rows[tile:]
        for base, part in ((0, slice(0, stop)), (half, slice(stop, 2 * stop))):
            if step == steps - 1:
                dk[base : base + stop] = dk_sum[part]
                dv[base : base + stop] = dv_sum[part]
            else:
                dk[base : base + stop] += dk_sum[part]
                dv[base : base + stop] += dv_sum[part]
    cos_rows, sin_rows = cos_ref[...], -sin_ref[...]
    out_ref[:, :128] = rotated(dq[...], cos_rows, sin_rows).astype(jnp.bfloat16)
    out_ref[:, 128:256] = rotated(dk[...], cos_rows, sin_rows).astype(jnp.bfloat16)
    out_ref[:, 256:] = dv[...].astype(jnp.bfloat16)


def split_rows(total, own_ref, other_ref):
    half = own_ref.shape[0]
    own_ref[...] = total[:half]
    other_ref[...] = total[half:].astype(jnp.bfloat16)


def to_model_kernel(lefts, pieces, cols, *refs):
    left, refs = jnp.concatenate([ref[...] for ref in refs[:lefts]], axis=1), refs[lefts:]
    weight = model_weight(refs[:pieces], refs[pieces : 2 * pieces], cols)
    split_rows(dot_nt(left, weight), *refs[2 * pieces :])


def gelu_both(up_act):
    root = math.sqrt(2.0 / math.pi)
    square = up_act * up_act
    rise = 0.5 + 0.5 * jnp.tanh(up_act * (root + root * 0.044715 * square))
    value = up_act * rise
    slope = rise + value * (1.0 - rise) * (2.0 * root + 6.0 * root * 0.044715 * square)
    return value, slope


def mlp_up_kernel(pieces, own_rows, other_rows, *refs):
    owns, others = refs[:pieces], refs[pieces : 2 * pieces]
    gelu_ref, slope_ref = refs[2 * pieces :]
    half = own_rows.shape[0]
    size = owns[0].shape[1] // 2
    step = half // 2
    units = [(j, i) for j in range(pieces) for i in range(4)]

    def product(j, i):
        rows = (own_rows, other_rows)[i // 2][i % 2 * step : (i % 2 + 1) * step]
        return dot_nn(rows, stacked_up([owns[j][:, :size], others[j][:, :size]]))

    ahead = product(*units[0])
    for spot, (j, i) in enumerate(units):
        up_act = ahead
        if spot + 1 < len(units):
            ahead = product(*units[spot + 1])
        value, slope = gelu_both(up_act)
        gelu_ref[i * step : (i + 1) * step, j * size : (j + 1) * size] = value.astype(jnp.bfloat16)
        slope_ref[i * step : (i + 1) * step, j * size : (j + 1) * size] = slope.astype(
            jnp.bfloat16
        )


def mlp_up_back_kernel(pieces, own_rows, other_rows, slope_ref, *refs):
    owns, others = refs[:pieces], refs[pieces : 2 * pieces]
    out_ref = refs[-1]
    size = owns[0].shape[1] // 2
    rows = stacked_up([own_rows[...], other_rows[...]])
    for j in range(pieces):
        cols = slice(j * size, (j + 1) * size)
        d_gelu = dot_nn(rows, stacked_up([owns[j][:, size:], others[j][:, size:]]))
        out_ref[:, cols] = (d_gelu * slope_ref[:, cols].astype(jnp.float32)).astype(jnp.bfloat16)


def inverse_size(rows):
    return lax.rsqrt(jnp.mean(rows * rows, axis=-1, keepdims=True) + NORM_EPSILON)


def norm_back(rows, gain, grad):
    scale = inverse_size(rows)
    weighted = grad * gain
    inner = jnp.mean(rows * weighted, axis=-1, keepdims=True)
    return scale * weighted - rows * (scale * scale * scale * inner), rows * scale * grad


def folded(rows):
    return jnp.sum(rows.reshape(rows.shape[0] // 8, 8, rows.shape[1]), axis=0)


def wide(ref, spot):
    return ref[spot, :].astype(jnp.float32)


def by_chunks(count, body, sums=0, width=0):
    def one(i, carry):
        more = body(pl.ds(pl.multiple_of(i * CHUNK, CHUNK), CHUNK))
        return tuple(old + folded(new) for old, new in zip(carry, more))

    start = tuple(jnp.zeros((8, width), jnp.float32) for _ in range(sums))
    totals = lax.fori_loop(0, count // CHUNK, one, start)
    return [jnp.sum(total, axis=0, keepdims=True) for total in totals]


def norm_in_kernel(gain_ref, rows_ref, out_ref):
    def body(spot):
        rows = wide(rows_ref, spot)
        out_ref[spot, :] = (rows * inverse_size(rows) * gain_ref[0:1]).astype(jnp.bfloat16)
        return ()

    by_chunks(rows_ref.shape[0], body)


def after_attention_kernel(
    gain_ref, rows_ref, own_ref, other_ref, branch_ref, hidden_ref, out_ref
):
    def body(spot):
        branch = own_ref[spot, :] + wide(other_ref, spot)
        hidden = wide(rows_ref, spot) + branch * inverse_size(branch) * gain_ref[1:2]
        branch_ref[spot, :] = branch
        hidden_ref[spot, :] = hidden
        out_ref[spot, :] = (hidden * inverse_size(hidden) * gain_ref[2:3]).astype(jnp.bfloat16)
        return ()

    by_chunks(rows_ref.shape[0], body)


def after_mlp_kernel(gain_ref, hidden_ref, own_ref, other_ref, branch_ref, out_ref):
    def body(spot):
        branch = own_ref[spot, :] + wide(other_ref, spot)
        branch_ref[spot, :] = branch
        result = hidden_ref[spot, :] + branch * inverse_size(branch) * gain_ref[3:4]
        out_ref[spot, :] = result.astype(jnp.bfloat16)
        return ()

    by_chunks(hidden_ref.shape[0], body)


def into_mlp_back_kernel(gain_ref, grad_ref, branch_ref, out_ref, sum_ref):
    def body(spot):
        d_rows, d_gain = norm_back(branch_ref[spot, :], gain_ref[3:4], wide(grad_ref, spot))
        out_ref[spot, :] = d_rows.astype(jnp.bfloat16)
        return (d_gain,)

    (sum_ref[...],) = by_chunks(grad_ref.shape[0], body, 1, grad_ref.shape[1])


def into_attention_back_kernel(
    gain_ref, grad_ref, own_ref, other_ref, hidden_ref, branch_ref, d_hidden_ref, out_ref, *sums
):
    def body(spot):
        d_rows = own_ref[spot, :] + wide(other_ref, spot)
        d_rows, d_gain = norm_back(hidden_ref[spot, :], gain_ref[2:3], d_rows)
        d_hidden = wide(grad_ref, spot) + d_rows
        d_hidden_ref[spot, :] = d_hidden
        d_rows, d_first = norm_back(branch_ref[spot, :], gain_ref[1:2], d_hidden)
        out_ref[spot, :] = d_rows.astype(jnp.bfloat16)
        return (d_first, d_gain)

    totals = by_chunks(grad_ref.shape[0], body, 2, grad_ref.shape[1])
    sums[0][...], sums[1][...] = totals


def out_of_layer_kernel(gain_ref, rows_ref, own_ref, other_ref, d_hidden_ref, out_ref, sum_ref):
    def body(spot):
        d_rows = own_ref[spot, :] + wide(other_ref, spot)
        d_rows, d_gain = norm_back(wide(rows_ref, spot), gain_ref[0:1], d_rows)
        out_ref[spot, :] = (d_hidden_ref[spot, :] + d_rows).astype(jnp.bfloat16)
        return (d_gain,)

    (sum_ref[...],) = by_chunks(rows_ref.shape[0], body, 1, rows_ref.shape[1])


def work(flops, arrays):
    size = sum(math.prod(array.shape) * jnp.dtype(array.dtype).itemsize for array in arrays)
    return pl.CostEstimate(flops=flops, bytes_accessed=size, transcendentals=0)


def on_chip(kernel, name, outs, *operands, limit=ROWS_VMEM, flops=0):
    shapes = [jax.ShapeDtypeStruct(shape, dtype) for shape, dtype in outs]
    space = pl.BlockSpec(memory_space=pltpu.VMEM)
    return pl.pallas_call(
        kernel,
        in_specs=[space] * len(operands),
        out_specs=[space] * len(outs),
        out_shape=shapes,
        compiler_params=pltpu.CompilerParams(vmem_limit_bytes=limit),
        cost_estimate=work(flops, (*operands, *shapes)),
        name=name,
    )(*operands)


def whole_block(array):
    return pl.BlockSpec(array.shape, lambda j: (0,) * array.ndim)


def by_pairs(kernel, name, core, operands, pieces, blocks, outs, scratch, flops):
    shapes = [jax.ShapeDtypeStruct(shape, dtype) for shape, dtype, _ in outs]
    return pl.pallas_call(
        functools.partial(kernel, len(pieces[0])),
        grid=(len(pieces[0]),),
        in_specs=[pl.BlockSpec(memory_space=pltpu.SMEM)]
        + [whole_block(array) for array in (*operands, *pieces[0], *pieces[1])]
        + [spec for _, spec in blocks],
        out_specs=[spec for _, _, spec in outs],
        out_shape=shapes,
        scratch_shapes=scratch,
        compiler_params=pltpu.CompilerParams(vmem_limit_bytes=KERNEL_VMEM),
        cost_estimate=work(flops, (*operands, *pieces[0], *pieces[1], *shapes)),
        name=name,
    )(core, *operands, *pieces[0], *pieces[1], *[array for array, _ in blocks])


def attend(core, tables, rows, pieces):
    half, features = rows[0].shape
    length, count = 2 * half, len(pieces[0])
    lanes = ((count, length, 128), jnp.bfloat16, pl.BlockSpec((1, length, 128), lambda j: (j, 0, 0)))
    lse = ((count, 2, length), jnp.float32, pl.BlockSpec((1, 2, length), lambda j: (j, 0, 0)))
    mixed = ((length, count * 128), jnp.bfloat16, pl.BlockSpec((length, 128), lambda j: (0, j)))
    return by_pairs(
        attend_kernel,
        "attend",
        core,
        (*tables, *rows),
        pieces,
        (),
        (lanes, lanes, lanes, lse, mixed),
        [pltpu.VMEM((features, 384), jnp.bfloat16)],
        count * length * (2 * features * 384 + 2 * PAIR_WORK * length),
    )


def attend_back(core, tables, rows, pieces, base, q, k, v, lse):
    half, features = rows[0].shape
    length, count = 2 * half, len(pieces[0])
    lanes = pl.BlockSpec((1, length, 128), lambda j: (base + j, 0, 0))
    lse_spec = pl.BlockSpec((1, 2, length), lambda j: (base + j, 0, 0))
    out = ((length, count * 384), jnp.bfloat16, pl.BlockSpec((length, 384), lambda j: (0, j)))
    return by_pairs(
        attend_back_kernel,
        "attend_back",
        core,
        (*tables, *rows),
        pieces,
        ((q, lanes), (k, lanes), (v, lanes), (lse, lse_spec)),
        (out,),
        [pltpu.VMEM((features, 128), jnp.bfloat16)] + [pltpu.VMEM((length, 128), jnp.float32)] * 3,
        count * length * (2 * features * 128 + 5 * PAIR_WORK * length),
    )[0]


def model_rows(name, lefts, pieces, cols):
    owns, others = pieces
    length, width = lefts[0].shape[0], 2 * owns[0].shape[0]
    outs = (((length // 2, width), jnp.float32), ((length // 2, width), jnp.bfloat16))
    kernel = functools.partial(to_model_kernel, len(lefts), len(owns), cols)
    hidden = sum(left.shape[1] for left in lefts)
    flops = 2 * length * width * hidden
    operands = (*lefts, *owns, *others)
    own, other = on_chip(kernel, name, outs, *operands, limit=KERNEL_VMEM, flops=flops)
    return own, flip_pairs(other, 1)


def flip_pairs(block, distance):
    size = lax.axis_size("dp")
    return lax.ppermute(block, "dp", [(i, i ^ distance) for i in range(size)])


def passed_on(block, step):
    size = lax.axis_size("tensor")
    return lax.ppermute(block, "tensor", [(i, (i + step) % size) for i in range(size)])


def summed_everywhere(value):
    for distance in (1, 2):
        value = value + flip_pairs(value, distance)
    size = lax.axis_size("tensor")
    for distance in (1, 2):
        value = value + lax.ppermute(value, "tensor", [(i, i ^ distance) for i in range(size)])
    return value


class Sequence:
    def __init__(self, token):
        self.token = token

    def step(self, *values):
        values, self.token = lax.optimization_barrier((values, self.token))
        return values[0] if len(values) == 1 else values


def per_chip(
    inputs,
    out_cotangent,
    group_ids,
    group_weights,
    gains,
    qkv_weight,
    out_weight,
    up_weight,
    down_weight,
):
    micro, row_count, width = inputs.shape
    tensor = lax.axis_size("tensor")
    part = row_count // 2
    wide_half = width // 2
    length = tensor * row_count
    half = length // 2
    first = lax.axis_index("section") == 0
    place = lax.axis_index("dp")
    core = place % 2
    upper = place // 2 % 2
    core_zero = core == 0
    low_half = upper == 0

    def ordered(mine, other):
        return jnp.where(core_zero, mine, other), jnp.where(core_zero, other, mine)

    def own_first(values):
        return jnp.where(low_half, values, jnp.roll(values, wide_half, axis=-1))

    def both_rows(own):
        return own, flip_pairs(own, 1)

    def to_chip(block):
        split = block.reshape((micro, 2, part) + block.shape[2:])
        mine = lax.dynamic_index_in_dim(split, core, 1, keepdims=False)
        other = lax.dynamic_index_in_dim(split, 1 - core, 1, keepdims=False)
        return lax.all_to_all(
            jnp.concatenate(ordered(mine, flip_pairs(other, 1))), "tensor", 0, 0, tiled=True
        )

    def from_chip(block):
        spread_out = lax.all_to_all(block, "tensor", 0, 0, tiled=True)
        grouped = spread_out.reshape((2, micro, part) + block.shape[2:])
        mine = lax.dynamic_index_in_dim(grouped, core, 0, keepdims=False)
        other = lax.dynamic_index_in_dim(grouped, 1 - core, 0, keepdims=False)
        pair = ordered(mine, flip_pairs(other, 1))
        return jnp.stack(pair, axis=1).reshape((micro, row_count) + block.shape[2:])

    def columns(local):
        size = local.shape[-1] // 2
        mid = (0,) * (local.ndim - 2)
        piece = lax.dynamic_slice(
            local,
            (wide_half * upper, *mid, size * core),
            (wide_half, *local.shape[1:-1], size),
        )
        return piece.reshape(wide_half, -1)

    def rows(local):
        size = local.shape[0] // 2
        return lax.dynamic_slice(local, (size * core, wide_half * upper), (size, wide_half)).T

    core_word = core.astype(jnp.int32).reshape(1)
    order = Sequence(core_word)
    pieces = {
        "attn": [jnp.concatenate([columns(qkv_weight[0]), rows(out_weight[0])], axis=1)],
        "mlp": [jnp.concatenate([columns(up_weight[0]), rows(down_weight[0])], axis=1)],
    }
    flown = {name: [] for name in pieces}
    ringing = {}

    def flip(name):
        flown[name].append(flip_pairs(order.step(pieces[name][-1]), 2))

    def flipped(name, j):
        flown[name][j] = order.step(flown[name][j])

    def ring(name):
        ringing[name] = passed_on(order.step(pieces[name][-1]), 1)

    def caught(name):
        pieces[name].append(order.step(ringing.pop(name)))

    group_count = group_weights.shape[0]
    matches = group_ids[..., None] == jnp.arange(group_count, dtype=jnp.int32)
    row_scale = jnp.sum(jnp.where(matches, group_weights, 0.0), axis=-1)
    weighted = (out_cotangent.astype(jnp.float32) * row_scale[..., None]).astype(jnp.bfloat16)
    start = to_chip(own_first(jnp.where(first, inputs, weighted))).reshape(half, width)
    flip("attn")
    ring("attn")
    caught("attn")
    flipped("attn", 0)
    ring("attn")
    flip("attn")
    flip("mlp")
    caught("attn")
    flipped("attn", 1)
    ring("attn")
    flip("attn")
    caught("attn")
    ring("mlp")
    flip("attn")
    flipped("mlp", 0)
    start = order.step(start)
    gain = own_first(gains[0])

    turns = jnp.arange(half, dtype=jnp.int32)
    turns = turns // part * row_count + turns % part
    positions = jnp.concatenate([turns + core * part, turns + (1 - core) * part])
    freqs = 10000.0 ** (-2.0 * jnp.arange(HEAD_DIM // 2, dtype=jnp.float32) / HEAD_DIM)
    angles = positions.astype(jnp.float32)[:, None] * freqs[None, :]
    cos_part, sin_part = jnp.cos(angles), jnp.sin(angles)
    tables = (
        jnp.concatenate([cos_part] * 4, axis=1),
        jnp.concatenate([-sin_part, sin_part] * 2, axis=1),
    )
    units = tensor * pieces["mlp"][0].shape[1] // 2
    row32, row16 = ((half, width), jnp.float32), ((half, width), jnp.bfloat16)
    unit16 = ((length, units), jnp.bfloat16)
    sum32 = ((1, width), jnp.float32)
    mlp_cost = {"limit": KERNEL_VMEM, "flops": 2 * length * width * units}
    ups, downs = slice(0, units // tensor), slice(units // tensor, None)
    weights = {name: (pieces[name], flown[name]) for name in pieces}

    def mlp_pieces():
        return (*weights["mlp"][0], *weights["mlp"][1])

    def forward(layer_input, between=None):
        pause = between or (lambda: None)
        attn_in = both_rows(on_chip(norm_in_kernel, "norm_in", (row16,), gain, layer_input)[0])
        pause()
        *heads, mixed = attend(core_word, tables, order.step(*attn_in), weights["attn"])
        mixed = order.step(mixed)
        pause()
        parts = model_rows("attn_out", [mixed], weights["attn"], OUT)
        branch, hidden, mlp_in = on_chip(
            after_attention_kernel, "after_attn", (row32, row32, row16), gain, layer_input, *parts
        )
        mlp_in = both_rows(order.step(mlp_in))
        pause()
        kernel = functools.partial(mlp_up_kernel, tensor)
        outs = (unit16, unit16)
        gelu_out, slope = on_chip(kernel, "mlp_up", outs, *mlp_in, *mlp_pieces(), **mlp_cost)
        gelu_out = order.step(gelu_out)
        pause()
        parts = model_rows("mlp_down", [gelu_out], weights["mlp"], downs)
        mlp_branch, result = on_chip(
            after_mlp_kernel, "after_mlp", (row32, row16), gain, hidden, *parts
        )
        saved = (layer_input, heads, branch, hidden, slope, mlp_branch)
        return result, saved, (attn_in, mixed, mlp_in, gelu_out)

    def backward(grad, saved, between=None):
        pause = between or (lambda **new: None)
        layer_input, heads, branch, hidden, slope, mlp_branch = saved
        d_down, sum_three = on_chip(
            into_mlp_back_kernel, "into_mlp_back", (row16, sum32), gain, grad, mlp_branch
        )
        d_down = both_rows(d_down)
        kernel = functools.partial(mlp_up_back_kernel, tensor)
        operands = (*d_down, slope, *mlp_pieces())
        (d_up,) = on_chip(kernel, "mlp_up_back", (unit16,), *operands, **mlp_cost)
        pause(d_down=d_down)
        d_up = order.step(d_up)
        parts = model_rows("mlp_back", [d_up], weights["mlp"], ups)
        pause(d_up=d_up)
        d_hidden, d_attn, sum_one, sum_two = on_chip(
            into_attention_back_kernel,
            "into_attn_back",
            (row32, row16, sum32, sum32),
            gain,
            grad,
            *parts,
            hidden,
            branch,
        )
        d_attn = both_rows(order.step(d_attn))
        pause(d_attn=d_attn)
        d_qkv = []
        for base in reversed(range(0, tensor, 2)):
            some = [side[base : base + 2] for side in weights["attn"]]
            rows_now = order.step(*d_attn)
            now = attend_back(core_word, tables, rows_now, some, base, *heads)
            d_qkv.insert(0, order.step(now))
            pause(d_qkv=d_qkv[0])
        parts = model_rows("attn_back", d_qkv, weights["attn"], QKV)
        d_input, sum_zero = on_chip(
            out_of_layer_kernel, "out_of_layer", (row16, sum32), gain, layer_input, *parts, d_hidden
        )
        sums = jnp.concatenate([sum_zero, sum_one, sum_two, sum_three])
        return order.step(d_input), (d_qkv, d_attn, d_up, d_down), sums

    def arrivals():
        flipped("attn", 2)
        caught("mlp")
        ring("mlp")
        flip("mlp")
        flipped("attn", 3)
        yield
        caught("mlp")
        ring("mlp")
        flip("mlp")
        yield
        flipped("mlp", 1)
        caught("mlp")
        flip("mlp")
        flipped("mlp", 2)
        flipped("mlp", 3)
        yield
        yield

    steps = arrivals()
    low_zero, saved_zero, lefts_zero = forward(start, lambda: next(steps))
    low_zero = order.step(low_zero)
    low_one, saved_one, lefts_one = forward(shifted(low_zero, "section", 1))
    grad_one, rights_one, gain_one = backward(start, saved_one)
    received = shifted(grad_one, "section", -1)

    def joined(pair):
        return lax.optimization_barrier(jnp.concatenate(pair, axis=0))

    def own_layer(zero, one):
        if isinstance(zero, tuple):
            zero, one = joined(zero), joined(one)
        return jnp.where(first, zero, one)

    lows = order.step(low_zero, low_one)
    outputs = from_chip(own_first(jnp.where(first, *lows)).reshape(tensor, part, width))
    lefts_zero, lefts_one = order.step(lefts_zero, lefts_one)
    attn_in, mixed, mlp_in, gelu_out = map(own_layer, lefts_zero, lefts_one)
    attn_in, mixed, mlp_in, gelu_out = order.step(attn_in, mixed, mlp_in, gelu_out)
    received = order.step(received)

    sums = {name: [None] * tensor for name in pieces}
    moving = {}

    def leave(name, j, *pairs):
        totals = [contract(*pair) for pair in order.step(*pairs)]
        own = jnp.concatenate([total[:wide_half] for total in totals], axis=1)
        other = jnp.concatenate(
            [total[wide_half:].astype(jnp.bfloat16) for total in totals], axis=1
        )
        own, other = order.step(own, other)
        sums[name][j] = (own, flip_pairs(other, 2))

    def gathered(name, j):
        own, other = sums[name][j]
        total = own + order.step(other).astype(jnp.float32)
        if name in moving:
            total = total + order.step(moving.pop(name)).astype(jnp.float32)
        if j == 0:
            sums[name] = total
        else:
            moving[name] = passed_on(order.step(total.astype(jnp.bfloat16)), -1)

    def block(array, j, count=tensor):
        size = array.shape[1] // count
        return array[:, j * size : (j + 1) * size]

    d_qkv_one, d_attn_one, d_up_one, d_down_one = rights_one

    def departures():
        new = yield
        d_down = own_layer(new["d_down"], d_down_one)
        new = yield
        d_up = own_layer(new["d_up"], d_up_one)

        def mlp_piece(j):
            leave("mlp", j, (mlp_in, block(d_up, j)), (d_down, block(gelu_out, j)))

        mlp_piece(3)
        mlp_piece(2)
        new = yield
        d_attn = own_layer(new["d_attn"], d_attn_one)
        gathered("mlp", 3)
        mlp_piece(1)
        new = yield
        high = own_layer(new["d_qkv"], d_qkv_one[1])
        gathered("mlp", 2)
        mlp_piece(0)
        new = yield
        low = own_layer(new["d_qkv"], d_qkv_one[0])
        gathered("mlp", 1)
        for j in reversed(range(tensor)):
            d_qkv = block((low, high)[j // 2], j % 2, 2)
            leave("attn", j, (attn_in, d_qkv), (d_attn, block(mixed, j)))
        yield

    leaving = departures()
    next(leaving)
    grad_zero, rights_zero, gain_zero = backward(
        received, saved_zero, lambda **new: leaving.send(new)
    )
    gathered("mlp", 0)
    gathered("attn", 3)
    gathered("attn", 2)
    gathered("attn", 1)
    gathered("attn", 0)
    grads = from_chip(own_first(jnp.where(first, grad_zero, grad_one)).reshape(tensor, part, width))

    def both_cores(kept):
        kept = kept.reshape(2, wide_half // 2, kept.shape[1])
        mine = lax.dynamic_index_in_dim(kept, core, 0, keepdims=False)
        other = lax.dynamic_index_in_dim(kept, 1 - core, 0, keepdims=False)
        return ordered(mine, flip_pairs(other, 1))

    pair = both_cores(sums["mlp"])
    up_grad = jnp.concatenate([side[:, ups] for side in pair], axis=1)
    down_grad = jnp.concatenate([side[:, downs].T for side in pair], axis=0)
    pair = both_cores(sums["attn"])
    qkv_grad = [side[:, QKV].reshape(wide_half // 2, 3, -1) for side in pair]
    qkv_grad = jnp.concatenate(qkv_grad, axis=2)
    out_grad = jnp.concatenate([side[:, OUT].T for side in pair], axis=0)

    gain_total = summed_everywhere(own_first(jnp.where(first, gain_zero, gain_one)))
    size = width // (tensor * lax.axis_size("dp"))
    spot = (place * tensor + lax.axis_index("tensor")) * size
    gains_grad = lax.dynamic_slice_in_dim(gain_total, spot, size, axis=1)
    return (
        outputs[None],
        grads[None],
        gains_grad[None],
        qkv_grad[None],
        out_grad[None],
        up_grad[None],
        down_grad[None],
    )


def takes_chips(sizes):
    return sizes["section"] == 2 and sizes["dp"] == 4 and sizes["tensor"] == 4


def solution(mesh):
    placed = (
        P("dp", "tensor", None),
        P("dp", "tensor", None),
        P("dp", "tensor"),
        P(),
        P("section", None, None),
        P("section", None, None, "tensor"),
        P("section", "tensor", None),
        P("section", None, "tensor"),
        P("section", "tensor", None),
    )
    body = per_chip if takes_chips(dict(mesh.shape)) else per_device
    return jax.shard_map(
        body,
        mesh=mesh,
        in_specs=placed,
        out_specs=(
            P("section", "dp", "tensor", None),
            P("section", "dp", "tensor", None),
            P("section", None, ("dp", "tensor")),
            P("section", "dp", None, "tensor"),
            P("section", "tensor", "dp"),
            P("section", "dp", "tensor"),
            P("section", "tensor", "dp"),
        ),
        check_vma=False,
    )
```

```python
import functools
import math

import jax
import jax.numpy as jnp
from jax import lax
from jax.experimental import pallas as pl
from jax.experimental.pallas import tpu as pltpu
from jax.sharding import PartitionSpec as P

HEAD_DIM = 64


NORM_EPSILON = 1e-06
TILE = 128
PAIR_WORK = 1024
QKV = slice(0, 384)
OUT = slice(384, 512)
CHUNK = 32
KERNEL_VMEM = 24 << 20
ROWS_VMEM = 8 << 20


def shifted(block, axis, distance):
    devices = range(lax.axis_size(axis))
    route = [(i - distance, i) for i in devices if i - distance in devices]
    return lax.ppermute(block, axis, route)


def norm_rows(vector, weight_gain):
    return (
        vector
        * lax.rsqrt(jnp.mean(vector * vector, axis=-1, keepdims=True) + NORM_EPSILON)
        * weight_gain
    )


def rotary_tables(seq_len, head_width):
    half_width = head_width // 2
    freqs = 10000.0 ** (-2.0 * jnp.arange(half_width, dtype=jnp.float32) / head_width)
    angles = jnp.arange(seq_len, dtype=jnp.float32)[:, None] * freqs[None, :]
    return (jnp.cos(angles), jnp.sin(angles))


def rotate(vector, cos_table, sin_table):
    first_half, second_half = jnp.split(vector, 2, axis=-1)
    cos_part = cos_table[:, None, :]
    sin_part = sin_table[:, None, :]
    return jnp.concatenate(
        [
            first_half * cos_part - second_half * sin_part,
            second_half * cos_part + first_half * sin_part,
        ],
        axis=-1,
    )


def contract(left_rows, right_rows):
    return lax.dot_general(
        left_rows, right_rows, (((0,), (0,)), ((), ())), preferred_element_type=jnp.float32
    )


def gather_rows(row_values, weight):

    def project(shard_rows, offset):
        return (shard_rows, jnp.dot(shard_rows, weight, preferred_element_type=jnp.float32))

    return project(lax.all_gather(row_values, "tensor", axis=0, tiled=True), jnp.int32(0))


def scatter_rows(row_values, weight, row_count):

    def partial_term(offset, span):
        return jnp.dot(row_values, weight, preferred_element_type=jnp.float32)

    return lax.psum_scatter(
        partial_term(jnp.int32(0), lax.axis_size("tensor") * row_count),
        "tensor",
        scatter_dimension=0,
        tiled=True,
    )


def gather_grads(row_values, weight):

    def project(shard_rows, offset):
        return (shard_rows, jnp.dot(shard_rows, weight.T, preferred_element_type=jnp.float32))

    return project(lax.all_gather(row_values, "tensor", axis=0, tiled=True), jnp.int32(0))


def scatter_grads(row_values, weight, row_count):

    def partial_term(offset, span):
        return jnp.dot(row_values, weight.T, preferred_element_type=jnp.float32)

    return lax.psum_scatter(
        partial_term(jnp.int32(0), lax.axis_size("tensor") * row_count),
        "tensor",
        scatter_dimension=0,
        tiled=True,
    )


def attention_probs(queries, key_rows):
    scores = jnp.einsum(
        "qhd,khd->hqk", queries, key_rows, preferred_element_type=jnp.float32
    ) * HEAD_DIM ** (-0.5)
    length = queries.shape[0]
    positions = jnp.arange(length, dtype=jnp.int32)
    causal = positions[:, None] >= positions[None, :]
    scores = jnp.where(causal[None], scores, -1e30)
    expos = jnp.exp(scores - jnp.max(scores, axis=-1, keepdims=True))
    return expos / jnp.sum(expos, axis=-1, keepdims=True)


def layer_forward(layer_input, weights):
    gains, w_qkv, w_out, w_up, w_down = weights
    row_count, model_width = layer_input.shape
    attn_in = norm_rows(layer_input, gains[0]).astype(jnp.bfloat16)
    gathered_a, qkv = gather_rows(attn_in, w_qkv.reshape(model_width, -1))
    length = qkv.shape[0]
    head_count = w_qkv.shape[2] // HEAD_DIM
    qkv = qkv.reshape(length, 3, head_count, HEAD_DIM)
    cos_table, sin_table = rotary_tables(length, HEAD_DIM)
    queries = rotate(qkv[:, 0], cos_table, sin_table).astype(jnp.bfloat16)
    key_rows = rotate(qkv[:, 1], cos_table, sin_table).astype(jnp.bfloat16)
    values = qkv[:, 2].astype(jnp.bfloat16)
    attn_probs = attention_probs(queries, key_rows).astype(jnp.bfloat16)
    mixed = jnp.einsum("hqk,khd->qhd", attn_probs, values, preferred_element_type=jnp.float32)
    mixed = mixed.reshape(length, -1).astype(jnp.bfloat16)
    attn_branch = scatter_rows(mixed, w_out, row_count)
    hidden = layer_input + norm_rows(attn_branch, gains[1])
    mlp_in = norm_rows(hidden, gains[2]).astype(jnp.bfloat16)
    gathered_c, up_act = gather_rows(mlp_in, w_up)
    gelu_out = jax.nn.gelu(up_act, approximate=True).astype(jnp.bfloat16)
    down_branch = scatter_rows(gelu_out, w_down, row_count)
    result = hidden + norm_rows(down_branch, gains[3])
    kept_values = (
        gathered_a,
        queries,
        key_rows,
        values,
        mixed,
        attn_branch,
        hidden,
        gathered_c,
        up_act,
        gelu_out,
        down_branch,
    )
    return (result, kept_values)


def layer_backward(layer_input, grad_result, kept_values, weights):
    gains, w_qkv, w_out, w_up, w_down = weights
    (
        gathered_a,
        queries,
        key_rows,
        values,
        mixed,
        attn_branch,
        hidden,
        gathered_c,
        up_act,
        gelu_out,
        down_branch,
    ) = kept_values
    row_count, model_width = layer_input.shape
    pullback = jax.vjp(norm_rows, down_branch, gains[3])[1]
    grad_down, gain_three = pullback(grad_result)
    gathered_dd, grad_gelu = gather_grads(grad_down.astype(jnp.bfloat16), w_down)
    down_total = contract(gelu_out, gathered_dd)
    pullback = jax.vjp(lambda vector: jax.nn.gelu(vector, approximate=True), up_act)[1]
    grad_up = pullback(grad_gelu)[0].astype(jnp.bfloat16)
    up_total = contract(gathered_c, grad_up)
    grad_mlp = scatter_grads(grad_up, w_up, row_count)
    pullback = jax.vjp(norm_rows, hidden, gains[2])[1]
    grad_norm_mlp, gain_two = pullback(grad_mlp)
    grad_hidden = grad_result + grad_norm_mlp
    pullback = jax.vjp(norm_rows, attn_branch, gains[1])[1]
    grad_attn, gain_one = pullback(grad_hidden)
    gathered_da, grad_mixed = gather_grads(grad_attn.astype(jnp.bfloat16), w_out)
    out_total = contract(mixed, gathered_da)
    length = grad_mixed.shape[0]
    head_count = w_qkv.shape[2] // HEAD_DIM
    grad_mixed = grad_mixed.astype(jnp.bfloat16).reshape(length, head_count, HEAD_DIM)
    attn_probs = attention_probs(queries, key_rows)
    probs_low = attn_probs.astype(jnp.bfloat16)
    grad_probs = jnp.einsum("qhd,khd->hqk", grad_mixed, values, preferred_element_type=jnp.float32)
    grad_values = jnp.einsum(
        "hqk,qhd->khd", probs_low, grad_mixed, preferred_element_type=jnp.float32
    )
    row_dots = jnp.sum(grad_probs * attn_probs, axis=-1, keepdims=True)
    grad_scores = (attn_probs * (grad_probs - row_dots)).astype(jnp.bfloat16)
    scale_value = HEAD_DIM ** (-0.5)
    grad_queries = (
        jnp.einsum("hqk,khd->qhd", grad_scores, key_rows, preferred_element_type=jnp.float32)
        * scale_value
    )
    grad_keys = (
        jnp.einsum("hqk,qhd->khd", grad_scores, queries, preferred_element_type=jnp.float32)
        * scale_value
    )
    cos_table, sin_table = rotary_tables(length, HEAD_DIM)
    pullback = jax.vjp(lambda vector: rotate(vector, cos_table, sin_table), grad_queries)[1]
    grad_q_raw = pullback(grad_queries)[0]
    grad_k_raw = pullback(grad_keys)[0]
    grad_qkv = (
        jnp.stack([grad_q_raw, grad_k_raw, grad_values], axis=1)
        .reshape(length, -1)
        .astype(jnp.bfloat16)
    )
    qkv_total = contract(gathered_a, grad_qkv).reshape(model_width, 3, -1)
    grad_attn_in = scatter_grads(grad_qkv, w_qkv.reshape(model_width, -1), row_count)
    pullback = jax.vjp(norm_rows, layer_input, gains[0])[1]
    grad_norm_in, gain_zero = pullback(grad_attn_in)
    grad_input = grad_hidden + grad_norm_in
    gain_total = jnp.stack([gain_zero, gain_one, gain_two, gain_three])
    return (grad_input, (gain_total, qkv_total, out_total, up_total, down_total))


def lagged(first_section, stacked):
    blank = jnp.zeros_like(stacked[:1])
    earlier = jnp.concatenate([blank, stacked[:-1]])
    later = jnp.concatenate([stacked[1:], blank])
    return jnp.where(first_section, earlier, later)


def per_device(
    inputs,
    out_cotangent,
    group_ids,
    group_weights,
    gains,
    qkv_weight,
    out_weight,
    up_weight,
    down_weight,
):
    weights = (gains[0], qkv_weight[0], out_weight[0], up_weight[0], down_weight[0])
    micro_count, row_count, model_width = inputs.shape
    first_section = lax.axis_index("section") == 0
    group_count = group_weights.shape[0]
    matches = group_ids[..., None] == jnp.arange(group_count, dtype=jnp.int32)
    row_scale = jnp.sum(jnp.where(matches, group_weights, 0.0), axis=-1)
    scaled = out_cotangent.astype(jnp.float32) * row_scale[..., None]
    padded = jnp.concatenate([inputs, jnp.zeros((1, row_count, model_width), jnp.bfloat16)])

    def forward_tick(received, fresh_input):
        layer_input = jnp.where(first_section, fresh_input, received)
        result, kept_values = layer_forward(layer_input.astype(jnp.float32), weights)
        result_low = result.astype(jnp.bfloat16)
        outgoing = shifted(result_low, "section", 1)
        stashed = ()
        return (outgoing, (layer_input, result_low, stashed))

    start_rows = jnp.zeros((row_count, model_width), jnp.bfloat16)
    _, (layer_inputs, layer_results, stashed) = lax.scan(forward_tick, start_rows, padded)
    layer_outputs = jnp.where(first_section, layer_results[:-1], layer_results[1:])[None]
    back_inputs = lagged(first_section, layer_inputs)
    back_stash = jax.tree.map(lambda stacked: lagged(first_section, stacked), stashed)
    grad_padded = jnp.concatenate([scaled, jnp.zeros((1, row_count, model_width), jnp.float32)])
    tick_index = jnp.arange(micro_count + 1, dtype=jnp.int32)
    tick_valid = jnp.where(first_section, tick_index >= 1, tick_index < micro_count).astype(
        jnp.float32
    )

    def backward_tick(carry, step_item):
        received, totals = carry
        layer_input, cotangent, valid_now, stash_now = step_item
        grad_now = jnp.where(first_section, received.astype(jnp.float32), cotangent)
        input_now = layer_input.astype(jnp.float32)
        kept_values = layer_forward(input_now, weights)[1]
        grad_input, layer_grads = layer_backward(input_now, grad_now, kept_values, weights)
        totals = jax.tree.map(lambda total, update: total + valid_now * update, totals, layer_grads)
        grad_low = grad_input.astype(jnp.bfloat16)
        outgoing = shifted(grad_low, "section", -1)
        return ((outgoing, totals), grad_low)

    start_totals = (
        jnp.zeros((4, model_width), jnp.float32),
        jnp.zeros(qkv_weight.shape[1:], jnp.float32),
        jnp.zeros(out_weight.shape[1:], jnp.float32),
        jnp.zeros(up_weight.shape[1:], jnp.float32),
        jnp.zeros(down_weight.shape[1:], jnp.float32),
    )
    (_, totals), grad_lows = lax.scan(
        backward_tick,
        (start_rows, start_totals),
        (back_inputs, grad_padded, tick_valid, back_stash),
    )
    input_grads = jnp.where(first_section, grad_lows[1:], grad_lows[:-1])[None]
    gain_total, qkv_total, out_total, up_total, down_total = totals
    gains_grad = lax.psum_scatter(gain_total, ("dp", "tensor"), scatter_dimension=1, tiled=True)
    qkv_grad, out_grad, up_grad, down_grad = (
        lax.psum_scatter(
            qkv_total.astype(jnp.bfloat16), "dp", scatter_dimension=0, tiled=True
        ).astype(jnp.float32),
        lax.psum_scatter(
            out_total.astype(jnp.bfloat16), "dp", scatter_dimension=1, tiled=True
        ).astype(jnp.float32),
        lax.psum_scatter(
            up_total.astype(jnp.bfloat16), "dp", scatter_dimension=0, tiled=True
        ).astype(jnp.float32),
        lax.psum_scatter(
            down_total.astype(jnp.bfloat16), "dp", scatter_dimension=1, tiled=True
        ).astype(jnp.float32),
    )
    return (
        layer_outputs,
        input_grads,
        gains_grad[None],
        qkv_grad[None],
        out_grad[None],
        up_grad[None],
        down_grad[None],
    )


def rotated(block, cos_rows, sin_rows):
    lane = lax.broadcasted_iota(jnp.int32, block.shape, 1)
    ahead = pltpu.roll(block, 96, 1)
    behind = pltpu.roll(block, 32, 1)
    swapped = jnp.where(lane % 64 < 32, ahead, behind)
    return block * cos_rows + swapped * sin_rows


def dot_nt(left, right):
    return lax.dot_general(
        left, right, (((1,), (1,)), ((), ())), preferred_element_type=jnp.float32
    )


def dot_nn(left, right):
    return jnp.dot(left, right, preferred_element_type=jnp.float32)


def columns_of(ref, cols):
    return ref[...] if ref.shape[1] == cols.stop - cols.start else ref[:, cols]


def model_weight(owns, others, cols):
    sides = [
        jnp.concatenate([columns_of(ref, cols) for ref in refs], axis=1) for refs in (owns, others)
    ]
    return jnp.concatenate(sides, axis=0)


def stacked_up(values):
    return jnp.concatenate(values, axis=0)


def edge_masks(core, rows):
    key = lax.broadcasted_iota(jnp.int32, (rows, 2 * rows), 0)
    query = lax.broadcasted_iota(jnp.int32, (rows, 2 * rows), 1)
    mine = query < rows
    place = jnp.where(mine, query + core * rows, query - rows + (1 - core) * rows)
    return (key + core * rows <= place, key + (1 - core) * rows <= place)


def both_sides(value, half, start, stop, axis=0):
    if axis == 0:
        return jnp.concatenate([value[start:stop], value[half + start : half + stop]], axis=0)
    return jnp.concatenate([value[:, start:stop], value[:, half + start : half + stop]], axis=1)


def hidden_scores(scores, masks, tile, step):
    seen = step * tile
    pieces = []
    for side in range(2):
        base = side * (seen + tile)
        if seen:
            pieces.append(scores[base : base + seen])
        pieces.append(jnp.where(masks[side], scores[base + seen : base + seen + tile], -1e30))
    return jnp.concatenate(pieces, axis=0)


def one_head(rows, head):
    lane = lax.broadcasted_iota(jnp.int32, rows.shape, 1)
    return jnp.where(lane // 64 == head, rows, jnp.zeros_like(rows))


def pick_piece(weight, owns, others, cols):
    for j, (own, other) in enumerate(zip(owns, others)):

        @pl.when(pl.program_id(0) == j)
        def _():
            size = own.shape[0]
            weight[:size] = own[:, cols]
            weight[size:] = other[:, cols]


def attend_kernel(pieces, core_ref, cos_ref, sin_ref, own_rows, other_rows, *refs):
    owns, others = refs[:pieces], refs[pieces : 2 * pieces]
    q_ref, k_ref, v_ref, lse_ref, mix_ref, weight = refs[2 * pieces :]
    half = own_rows.shape[0]
    tile = TILE
    pick_piece(weight, owns, others, QKV)
    proj = dot_nn(stacked_up([own_rows[...], other_rows[...]]), weight[...])
    cos_rows, sin_rows = cos_ref[...], sin_ref[...]
    q = (rotated(proj[:, :128], cos_rows, sin_rows) * HEAD_DIM ** (-0.5)).astype(jnp.bfloat16)
    k = rotated(proj[:, 128:256], cos_rows, sin_rows).astype(jnp.bfloat16)
    v32 = proj[:, 256:]
    q_ref[0] = q
    k_ref[0] = k
    v_ref[0] = v32.astype(jnp.bfloat16)
    v_flip = v32.T.astype(jnp.bfloat16)
    masks = edge_masks(core_ref[0], tile)

    def scored(step, head):
        stop = (step + 1) * tile
        q_head = one_head(both_sides(q, half, step * tile, stop), head)
        return hidden_scores(dot_nt(both_sides(k, half, 0, stop), q_head), masks, tile, step)

    units = [(step, head) for step in range(half // tile) for head in range(2)]
    ahead = scored(*units[0])
    outs = []
    for spot, (step, head) in enumerate(units):
        scores = ahead
        if spot + 1 < len(units):
            ahead = scored(*units[spot + 1])
        stop = (step + 1) * tile
        top = jnp.max(scores, axis=0, keepdims=True)
        expos = jnp.exp(scores - top)
        total = jnp.sum(expos, axis=0, keepdims=True)
        lse = top + jnp.log(total)
        lse_ref[0, head : head + 1, step * tile : stop] = lse[:, :tile]
        lse_ref[0, head : head + 1, half + step * tile : half + stop] = lse[:, tile:]
        v_cols = both_sides(v_flip, half, 0, stop, axis=1)
        out = dot_nn(v_cols[64 * head : 64 * head + 64], expos.astype(jnp.bfloat16))
        outs.append(out * (1.0 / total))
        if head == 1:
            mixed = jnp.concatenate(outs, axis=0).T.astype(jnp.bfloat16)
            outs = []
            mix_ref[step * tile : stop, :] = mixed[:tile]
            mix_ref[half + step * tile : half + stop, :] = mixed[tile:]


def attend_back_kernel(pieces, core_ref, cos_ref, sin_ref, own_rows, other_rows, *refs):
    owns, others = refs[:pieces], refs[pieces : 2 * pieces]
    q_ref, k_ref, v_ref, lse_ref, out_ref, weight, dq, dk, dv = refs[2 * pieces :]
    half = own_rows.shape[0]
    tile = TILE
    pick_piece(weight, owns, others, OUT)
    rows = stacked_up([own_rows[...], other_rows[...]])
    d_mixed = dot_nn(rows, weight[...]).astype(jnp.bfloat16)
    q, k, v = q_ref[0], k_ref[0], v_ref[0]
    k_flip = k.astype(jnp.float32).T.astype(jnp.bfloat16)
    masks = edge_masks(core_ref[0], tile)
    steps = half // tile

    def scored(step, head):
        stop = (step + 1) * tile
        q_head = one_head(both_sides(q, half, step * tile, stop), head)
        g_head = one_head(both_sides(d_mixed, half, step * tile, stop), head)
        scores = hidden_scores(dot_nt(both_sides(k, half, 0, stop), q_head), masks, tile, step)
        return q_head, g_head, scores, dot_nt(both_sides(v, half, 0, stop), g_head)

    units = [(step, head) for step in reversed(range(steps)) for head in range(2)]
    ahead = scored(*units[0])
    dq_flips = []
    dk_sum = dv_sum = None
    for spot, (step, head) in enumerate(units):
        q_head, g_head, scores, d_probs = ahead
        if spot + 1 < len(units):
            ahead = scored(*units[spot + 1])
        stop = (step + 1) * tile
        lse = both_sides(lse_ref[0], half, step * tile, stop, axis=1)
        probs = jnp.exp(scores - lse[head : head + 1])
        dots = jnp.sum(probs * d_probs, axis=0, keepdims=True)
        d_scores = (probs * (d_probs - dots)).astype(jnp.bfloat16)
        dv_part = dot_nn(probs.astype(jnp.bfloat16), g_head)
        dk_part = dot_nn(d_scores, q_head)
        k_cols = both_sides(k_flip, half, 0, stop, axis=1)
        dq_flips.append(dot_nn(k_cols[64 * head : 64 * head + 64], d_scores))
        if head == 0:
            dv_sum, dk_sum = dv_part, dk_part
            continue
        dv_sum, dk_sum = dv_sum + dv_part, dk_sum + dk_part
        dq_rows = jnp.concatenate(dq_flips, axis=0).T * HEAD_DIM ** (-0.5)
        dq_flips = []
        dq[step * tile : stop] = dq_rows[:tile]
        dq[half + step * tile : half + stop] = dq_rows[tile:]
        for base, part in ((0, slice(0, stop)), (half, slice(stop, 2 * stop))):
            if step == steps - 1:
                dk[base : base + stop] = dk_sum[part]
                dv[base : base + stop] = dv_sum[part]
            else:
                dk[base : base + stop] += dk_sum[part]
                dv[base : base + stop] += dv_sum[part]
    cos_rows, sin_rows = cos_ref[...], -sin_ref[...]
    out_ref[:, :128] = rotated(dq[...], cos_rows, sin_rows).astype(jnp.bfloat16)
    out_ref[:, 128:256] = rotated(dk[...], cos_rows, sin_rows).astype(jnp.bfloat16)
    out_ref[:, 256:] = dv[...].astype(jnp.bfloat16)


def split_rows(total, own_ref, other_ref):
    half = own_ref.shape[0]
    own_ref[...] = total[:half]
    other_ref[...] = total[half:].astype(jnp.bfloat16)


def to_model_kernel(lefts, pieces, cols, *refs):
    left, refs = jnp.concatenate([ref[...] for ref in refs[:lefts]], axis=1), refs[lefts:]
    weight = model_weight(refs[:pieces], refs[pieces : 2 * pieces], cols)
    split_rows(dot_nt(left, weight), *refs[2 * pieces :])


def gelu_both(up_act):
    root = math.sqrt(2.0 / math.pi)
    square = up_act * up_act
    rise = 0.5 + 0.5 * jnp.tanh(up_act * (root + root * 0.044715 * square))
    value = up_act * rise
    slope = rise + value * (1.0 - rise) * (2.0 * root + 6.0 * root * 0.044715 * square)
    return value, slope


def mlp_up_kernel(pieces, own_rows, other_rows, *refs):
    owns, others = refs[:pieces], refs[pieces : 2 * pieces]
    gelu_ref, slope_ref = refs[2 * pieces :]
    half = own_rows.shape[0]
    size = owns[0].shape[1] // 2
    cols = slice(0, size)
    step = half // 2
    units = [(j, i) for j in range(pieces) for i in range(4)]

    def product(j, i):
        rows = (own_rows, other_rows)[i // 2][i % 2 * step : (i % 2 + 1) * step]
        return dot_nn(rows, stacked_up([columns_of(owns[j], cols), columns_of(others[j], cols)]))

    ahead = product(*units[0])
    for spot, (j, i) in enumerate(units):
        up_act = ahead
        if spot + 1 < len(units):
            ahead = product(*units[spot + 1])
        value, slope = gelu_both(up_act)
        gelu_ref[i * step : (i + 1) * step, j * size : (j + 1) * size] = value.astype(jnp.bfloat16)
        slope_ref[i * step : (i + 1) * step, j * size : (j + 1) * size] = slope.astype(
            jnp.bfloat16
        )


def mlp_up_back_kernel(pieces, own_rows, other_rows, slope_ref, *refs):
    owns, others = refs[:pieces], refs[pieces : 2 * pieces]
    out_ref = refs[-1]
    size = owns[0].shape[1] // 2
    rows = stacked_up([own_rows[...], other_rows[...]])
    taken = slice(size, 2 * size)
    for j in range(pieces):
        cols = slice(j * size, (j + 1) * size)
        weight = stacked_up([columns_of(owns[j], taken), columns_of(others[j], taken)])
        d_gelu = dot_nn(rows, weight)
        out_ref[:, cols] = (d_gelu * slope_ref[:, cols].astype(jnp.float32)).astype(jnp.bfloat16)


def inverse_size(rows):
    return lax.rsqrt(jnp.mean(rows * rows, axis=-1, keepdims=True) + NORM_EPSILON)


def norm_back(rows, gain, grad):
    scale = inverse_size(rows)
    weighted = grad * gain
    inner = jnp.mean(rows * weighted, axis=-1, keepdims=True)
    return scale * weighted - rows * (scale * scale * scale * inner), rows * scale * grad


def folded(rows):
    return jnp.sum(rows.reshape(rows.shape[0] // 8, 8, rows.shape[1]), axis=0)


def wide(ref, spot):
    return ref[spot, :].astype(jnp.float32)


def by_chunks(count, body, sums=0, width=0):
    def one(i, carry):
        more = body(pl.ds(pl.multiple_of(i * CHUNK, CHUNK), CHUNK))
        return tuple(old + folded(new) for old, new in zip(carry, more))

    start = tuple(jnp.zeros((8, width), jnp.float32) for _ in range(sums))
    totals = lax.fori_loop(0, count // CHUNK, one, start)
    return [jnp.sum(total, axis=0, keepdims=True) for total in totals]


def norm_in_kernel(gain_ref, rows_ref, out_ref):
    def body(spot):
        rows = wide(rows_ref, spot)
        out_ref[spot, :] = (rows * inverse_size(rows) * gain_ref[0:1]).astype(jnp.bfloat16)
        return ()

    by_chunks(rows_ref.shape[0], body)


def after_attention_kernel(
    gain_ref, rows_ref, own_ref, other_ref, branch_ref, hidden_ref, out_ref
):
    def body(spot):
        branch = own_ref[spot, :] + wide(other_ref, spot)
        hidden = wide(rows_ref, spot) + branch * inverse_size(branch) * gain_ref[1:2]
        branch_ref[spot, :] = branch
        hidden_ref[spot, :] = hidden
        out_ref[spot, :] = (hidden * inverse_size(hidden) * gain_ref[2:3]).astype(jnp.bfloat16)
        return ()

    by_chunks(rows_ref.shape[0], body)


def after_mlp_kernel(gain_ref, hidden_ref, own_ref, other_ref, branch_ref, out_ref):
    def body(spot):
        branch = own_ref[spot, :] + wide(other_ref, spot)
        branch_ref[spot, :] = branch
        result = hidden_ref[spot, :] + branch * inverse_size(branch) * gain_ref[3:4]
        out_ref[spot, :] = result.astype(jnp.bfloat16)
        return ()

    by_chunks(hidden_ref.shape[0], body)


def into_mlp_back_kernel(gain_ref, grad_ref, branch_ref, out_ref, sum_ref):
    def body(spot):
        d_rows, d_gain = norm_back(branch_ref[spot, :], gain_ref[3:4], wide(grad_ref, spot))
        out_ref[spot, :] = d_rows.astype(jnp.bfloat16)
        return (d_gain,)

    (sum_ref[...],) = by_chunks(grad_ref.shape[0], body, 1, grad_ref.shape[1])


def into_attention_back_kernel(
    gain_ref, grad_ref, own_ref, other_ref, hidden_ref, branch_ref, d_hidden_ref, out_ref, *sums
):
    def body(spot):
        d_rows = own_ref[spot, :] + wide(other_ref, spot)
        d_rows, d_gain = norm_back(hidden_ref[spot, :], gain_ref[2:3], d_rows)
        d_hidden = wide(grad_ref, spot) + d_rows
        d_hidden_ref[spot, :] = d_hidden
        d_rows, d_first = norm_back(branch_ref[spot, :], gain_ref[1:2], d_hidden)
        out_ref[spot, :] = d_rows.astype(jnp.bfloat16)
        return (d_first, d_gain)

    totals = by_chunks(grad_ref.shape[0], body, 2, grad_ref.shape[1])
    sums[0][...], sums[1][...] = totals


def out_of_layer_kernel(gain_ref, rows_ref, own_ref, other_ref, d_hidden_ref, out_ref, sum_ref):
    def body(spot):
        d_rows = own_ref[spot, :] + wide(other_ref, spot)
        d_rows, d_gain = norm_back(wide(rows_ref, spot), gain_ref[0:1], d_rows)
        out_ref[spot, :] = (d_hidden_ref[spot, :] + d_rows).astype(jnp.bfloat16)
        return (d_gain,)

    (sum_ref[...],) = by_chunks(rows_ref.shape[0], body, 1, rows_ref.shape[1])


def work(flops, arrays):
    size = sum(math.prod(array.shape) * jnp.dtype(array.dtype).itemsize for array in arrays)
    return pl.CostEstimate(flops=flops, bytes_accessed=size, transcendentals=0)


def without(kernel, first, count):
    return lambda *refs: kernel(*refs[:first], *refs[first + count :])


def on_chip(kernel, name, outs, *operands, limit=ROWS_VMEM, flops=0, waits=()):
    shapes = [jax.ShapeDtypeStruct(shape, dtype) for shape, dtype in outs]
    space = pl.BlockSpec(memory_space=pltpu.VMEM)
    return pl.pallas_call(
        without(kernel, len(operands), len(waits)),
        in_specs=[space] * len(operands) + [pl.BlockSpec(memory_space=pl.ANY)] * len(waits),
        out_specs=[space] * len(outs),
        out_shape=shapes,
        compiler_params=pltpu.CompilerParams(vmem_limit_bytes=limit),
        cost_estimate=work(flops, (*operands, *shapes)),
        name=name,
    )(*operands, *waits)


def whole_block(array):
    return pl.BlockSpec(array.shape, lambda j: (0,) * array.ndim)


def by_pairs(kernel, name, core, operands, pieces, blocks, outs, scratch, flops, waits):
    shapes = [jax.ShapeDtypeStruct(shape, dtype) for shape, dtype, _ in outs]
    taken = 1 + len(operands) + 2 * len(pieces[0]) + len(blocks)
    return pl.pallas_call(
        without(functools.partial(kernel, len(pieces[0])), taken, len(waits)),
        grid=(len(pieces[0]),),
        in_specs=[pl.BlockSpec(memory_space=pltpu.SMEM)]
        + [whole_block(array) for array in (*operands, *pieces[0], *pieces[1])]
        + [spec for _, spec in blocks]
        + [pl.BlockSpec(memory_space=pl.ANY)] * len(waits),
        out_specs=[spec for _, _, spec in outs],
        out_shape=shapes,
        scratch_shapes=scratch,
        compiler_params=pltpu.CompilerParams(vmem_limit_bytes=KERNEL_VMEM),
        cost_estimate=work(flops, (*operands, *pieces[0], *pieces[1], *shapes)),
        name=name,
    )(core, *operands, *pieces[0], *pieces[1], *[array for array, _ in blocks], *waits)


def attend(core, tables, rows, pieces, waits):
    half, features = rows[0].shape
    length, count = 2 * half, len(pieces[0])
    lanes = ((count, length, 128), jnp.bfloat16, pl.BlockSpec((1, length, 128), lambda j: (j, 0, 0)))
    lse = ((count, 2, length), jnp.float32, pl.BlockSpec((1, 2, length), lambda j: (j, 0, 0)))
    mixed = ((length, count * 128), jnp.bfloat16, pl.BlockSpec((length, 128), lambda j: (0, j)))
    return by_pairs(
        attend_kernel,
        "attend",
        core,
        (*tables, *rows),
        pieces,
        (),
        (lanes, lanes, lanes, lse, mixed),
        [pltpu.VMEM((features, 384), jnp.bfloat16)],
        count * length * (2 * features * 384 + 2 * PAIR_WORK * length),
        waits,
    )


def attend_back(core, tables, rows, pieces, base, waits, q, k, v, lse):
    half, features = rows[0].shape
    length, count = 2 * half, len(pieces[0])
    lanes = pl.BlockSpec((1, length, 128), lambda j: (base + j, 0, 0))
    lse_spec = pl.BlockSpec((1, 2, length), lambda j: (base + j, 0, 0))
    out = ((length, count * 384), jnp.bfloat16, pl.BlockSpec((length, 384), lambda j: (0, j)))
    return by_pairs(
        attend_back_kernel,
        "attend_back",
        core,
        (*tables, *rows),
        pieces,
        ((q, lanes), (k, lanes), (v, lanes), (lse, lse_spec)),
        (out,),
        [pltpu.VMEM((features, 128), jnp.bfloat16)] + [pltpu.VMEM((length, 128), jnp.float32)] * 3,
        count * length * (2 * features * 128 + 5 * PAIR_WORK * length),
        waits,
    )[0]


def model_rows(name, lefts, pieces, cols, waits=()):
    owns, others = pieces
    length, width = lefts[0].shape[0], 2 * owns[0].shape[0]
    outs = (((length // 2, width), jnp.float32), ((length // 2, width), jnp.bfloat16))
    kernel = functools.partial(to_model_kernel, len(lefts), len(owns), cols)
    hidden = sum(left.shape[1] for left in lefts)
    flops = 2 * length * width * hidden
    operands = (*lefts, *owns, *others)
    more = {"limit": KERNEL_VMEM, "flops": flops, "waits": waits}
    own, other = on_chip(kernel, name, outs, *operands, **more)
    return own, flip_pairs(other, 1)


def flip_pairs(block, distance):
    size = lax.axis_size("dp")
    return lax.ppermute(block, "dp", [(i, i ^ distance) for i in range(size)])


def passed_on(block, step):
    size = lax.axis_size("tensor")
    return lax.ppermute(block, "tensor", [(i, (i + step) % size) for i in range(size)])


def pack_kernel(first_ref, second_ref, own_ref, other_ref):
    half, width = own_ref.shape[0], first_ref.shape[1]
    own_ref[:, :width] = first_ref[:half]
    own_ref[:, width:] = second_ref[:half]
    other_ref[:, :width] = first_ref[half:].astype(jnp.bfloat16)
    other_ref[:, width:] = second_ref[half:].astype(jnp.bfloat16)


def last_sum_kernel(core_ref, own_ref, other_ref, moved_ref, keep_ref, send_ref):
    rows = keep_ref.shape[0]

    def total(block):
        spot = pl.ds(pl.multiple_of(block * rows, rows), rows)
        return own_ref[spot, :] + wide(other_ref, spot) + wide(moved_ref, spot)

    keep_ref[...] = total(core_ref[0])
    send_ref[...] = total(1 - core_ref[0])


def joined_kernel(spots, core_ref, keep_ref, sent_ref, column_ref, row_ref):
    size = row_ref.shape[0] // 2
    for core in range(2):

        @pl.when(core_ref[0] == core)
        def _():
            for place, source in ((core, keep_ref), (1 - core, sent_ref)):
                for start, stop, to in spots:
                    step = stop - start
                    column_ref[:, to + place * step : to + (place + 1) * step] = source[:, start:stop]
                row_ref[place * size : (place + 1) * size] = source[:, spots[-1][1] :].T


def per_chip(
    inputs,
    out_cotangent,
    group_ids,
    group_weights,
    gains,
    qkv_weight,
    out_weight,
    up_weight,
    down_weight,
):
    micro, row_count, width = inputs.shape
    tensor = lax.axis_size("tensor")
    part = row_count // 2
    wide_half = width // 2
    length = tensor * row_count
    half = length // 2
    first = lax.axis_index("section") == 0
    place = lax.axis_index("dp")
    core = place % 2
    upper = place // 2 % 2
    core_zero = core == 0
    low_half = upper == 0

    def ordered(mine, other):
        return jnp.where(core_zero, mine, other), jnp.where(core_zero, other, mine)

    def own_first(values):
        return jnp.where(low_half, values, jnp.roll(values, wide_half, axis=-1))

    def both_rows(own):
        return own, flip_pairs(own, 1)

    def to_chip(block):
        split = block.reshape((micro, 2, part) + block.shape[2:])
        mine = lax.dynamic_index_in_dim(split, core, 1, keepdims=False)
        other = lax.dynamic_index_in_dim(split, 1 - core, 1, keepdims=False)
        return lax.all_to_all(
            jnp.concatenate(ordered(mine, flip_pairs(other, 1))), "tensor", 0, 0, tiled=True
        )

    def from_chip(block):
        spread_out = lax.all_to_all(block, "tensor", 0, 0, tiled=True)
        grouped = spread_out.reshape((2, micro, part) + block.shape[2:])
        mine = lax.dynamic_index_in_dim(grouped, core, 0, keepdims=False)
        other = lax.dynamic_index_in_dim(grouped, 1 - core, 0, keepdims=False)
        pair = ordered(mine, flip_pairs(other, 1))
        return jnp.stack(pair, axis=1).reshape((micro, row_count) + block.shape[2:])

    def columns(local):
        size = local.shape[-1] // 2
        mid = (0,) * (local.ndim - 2)
        piece = lax.dynamic_slice(
            local,
            (wide_half * upper, *mid, size * core),
            (wide_half, *local.shape[1:-1], size),
        )
        return piece.reshape(wide_half, -1)

    def rows(local):
        size = local.shape[0] // 2
        return lax.dynamic_slice(local, (size * core, wide_half * upper), (size, wide_half)).T

    core_word = core.astype(jnp.int32).reshape(1)
    attn_piece = jnp.concatenate([columns(qkv_weight[0]), rows(out_weight[0])], axis=1)
    mlp_piece = jnp.concatenate([columns(up_weight[0]), rows(down_weight[0])], axis=1)
    units = tensor * mlp_piece.shape[1] // 2
    ups, downs = slice(0, units // tensor), slice(units // tensor, 2 * units // tensor)

    def spread(piece):
        pieces = [piece]
        for _ in range(tensor - 1):
            pieces.append(passed_on(pieces[-1], 1))
        return pieces

    attn_own, mlp_own = spread(attn_piece), spread(mlp_piece)
    attn_other = [flip_pairs(piece, 2) for piece in attn_own]
    mlp_other = [flip_pairs(piece, 2) for piece in mlp_own[:-1]]
    up_last, down_last = (flip_pairs(mlp_own[-1][:, cols], 2) for cols in (ups, downs))
    w_attn = (attn_own, attn_other)
    w_up = (mlp_own, mlp_other + [up_last])
    w_down = (mlp_own, mlp_other + [down_last])

    group_count = group_weights.shape[0]
    matches = group_ids[..., None] == jnp.arange(group_count, dtype=jnp.int32)
    row_scale = jnp.sum(jnp.where(matches, group_weights, 0.0), axis=-1)
    weighted = (out_cotangent.astype(jnp.float32) * row_scale[..., None]).astype(jnp.bfloat16)
    start = to_chip(own_first(jnp.where(first, inputs, weighted))).reshape(half, width)
    gain = own_first(gains[0])

    turns = jnp.arange(half, dtype=jnp.int32)
    turns = turns // part * row_count + turns % part
    positions = jnp.concatenate([turns + core * part, turns + (1 - core) * part])
    freqs = 10000.0 ** (-2.0 * jnp.arange(HEAD_DIM // 2, dtype=jnp.float32) / HEAD_DIM)
    angles = positions.astype(jnp.float32)[:, None] * freqs[None, :]
    cos_part, sin_part = jnp.cos(angles), jnp.sin(angles)
    tables = (
        jnp.concatenate([cos_part] * 4, axis=1),
        jnp.concatenate([-sin_part, sin_part] * 2, axis=1),
    )
    row32, row16 = ((half, width), jnp.float32), ((half, width), jnp.bfloat16)
    unit16 = ((length, units), jnp.bfloat16)
    sum32 = ((1, width), jnp.float32)
    mlp_cost = {"limit": KERNEL_VMEM, "flops": 2 * length * width * units}

    def forward(layer_input, waits):
        attn_in = both_rows(
            on_chip(norm_in_kernel, "norm_in", (row16,), gain, layer_input, waits=waits[0])[0]
        )
        *heads, mixed = attend(core_word, tables, attn_in, w_attn, waits[1])
        parts = model_rows("attn_out", [mixed], w_attn, OUT, waits[2])
        operands = (gain, layer_input, *parts)
        branch, hidden, mlp_in = on_chip(
            after_attention_kernel, "after_attn", (row32, row32, row16), *operands, waits=waits[3]
        )
        mlp_in = both_rows(mlp_in)
        kernel = functools.partial(mlp_up_kernel, tensor)
        operands = (*mlp_in, *w_up[0], *w_up[1])
        gelu_out, slope = on_chip(kernel, "mlp_up", (unit16, unit16), *operands, **mlp_cost)
        parts = model_rows("mlp_down", [gelu_out], w_down, downs)
        mlp_branch, result = on_chip(
            after_mlp_kernel, "after_mlp", (row32, row16), gain, hidden, *parts
        )
        saved = (layer_input, heads, branch, hidden, slope, mlp_branch)
        return result, saved, (attn_in, mixed, mlp_in, gelu_out)

    def backward(grad, saved, hook, waits=()):
        layer_input, heads, branch, hidden, slope, mlp_branch = saved
        operands = (gain, grad, mlp_branch)
        d_down, sum_three = on_chip(
            into_mlp_back_kernel, "into_mlp_back", (row16, sum32), *operands, waits=waits
        )
        d_down = both_rows(d_down)
        kernel = functools.partial(mlp_up_back_kernel, tensor)
        operands = (*d_down, slope, *w_down[0], *w_down[1])
        (d_up,) = on_chip(kernel, "mlp_up_back", (unit16,), *operands, **mlp_cost)
        waits = hook(d_down, d_up)
        parts = model_rows("mlp_back", [d_up], w_up, ups)
        operands = (gain, grad, *parts, hidden, branch)
        outs = (row32, row16, sum32, sum32)
        d_hidden, d_attn, sum_one, sum_two = on_chip(
            into_attention_back_kernel, "into_attn_back", outs, *operands, waits=waits
        )
        d_attn = both_rows(d_attn)
        waits = hook(d_attn)
        d_qkv = []
        for base in reversed(range(0, tensor, 2)):
            some = [side[base : base + 2] for side in w_attn]
            now = attend_back(core_word, tables, d_attn, some, base, waits, *heads)
            d_qkv.insert(0, now)
            waits = hook(now)
        parts = model_rows("attn_back", d_qkv, w_attn, QKV, waits)
        operands = (gain, layer_input, *parts, d_hidden)
        d_input, sum_zero = on_chip(
            out_of_layer_kernel, "out_of_layer", (row16, sum32), *operands
        )
        sums = jnp.concatenate([sum_zero, sum_one, sum_two, sum_three])
        return d_input, (d_qkv, d_attn, d_up, d_down), sums

    low_zero, saved_zero, lefts_zero = forward(
        start,
        (
            (attn_own[3], mlp_other[0], attn_other[1]),
            (mlp_own[1],),
            (mlp_own[2], mlp_other[1]),
            (mlp_own[3], mlp_other[2]),
        ),
    )
    low_one, saved_one, lefts_one = forward(shifted(low_zero, "section", 1), ((),) * 4)
    grad_one, rights_one, gain_one = backward(start, saved_one, lambda *new: ())
    received = shifted(grad_one, "section", -1)

    def joined(pair):
        return lax.optimization_barrier(jnp.concatenate(pair, axis=0))

    def own_layer(zero, one):
        if isinstance(zero, tuple):
            zero, one = joined(zero), joined(one)
        return lax.optimization_barrier(jnp.where(first, zero, one))

    lefts_zero, lefts_one = lax.optimization_barrier((lefts_zero, lefts_one, grad_one))[:2]
    attn_in, mixed, mlp_in, gelu_out = lefts = list(map(own_layer, lefts_zero, lefts_one))
    lows = lax.optimization_barrier((low_zero, low_one, grad_one))[:2]
    outputs = from_chip(own_first(jnp.where(first, *lows)).reshape(tensor, part, width))

    def block(array, j, count=tensor):
        size = array.shape[1] // count
        return array[:, j * size : (j + 1) * size]

    def leave(*pairs):
        totals = [contract(*pair) for pair in pairs]
        size = sum(total.shape[1] for total in totals)
        outs = (((wide_half, size), jnp.float32), ((wide_half, size), jnp.bfloat16))
        own, other = on_chip(pack_kernel, "pack", outs, *totals)
        return own, flip_pairs(other, 2)

    def mlp_leaves(j):
        return leave((mlp_in, block(d_up, j)), (d_down, block(gelu_out, j)))

    def attn_leaves(j, d_qkv):
        return leave((attn_in, block(d_qkv, j % 2, 2)), (d_attn, block(mixed, j)))

    def moves_on(piece, moved=None):
        own, other = piece
        total = own + other.astype(jnp.float32)
        if moved is not None:
            total = total + moved.astype(jnp.float32)
        return passed_on(total.astype(jnp.bfloat16), -1)

    d_qkv_one, d_attn_one, d_up_one, d_down_one = rights_one
    mlp_sums, attn_sums = [None] * tensor, [None] * tensor
    mlp_moves, attn_moves = [None] * tensor, [None] * tensor
    hooks = iter(range(4))

    def hook(*new):
        nonlocal d_down, d_up, d_attn
        turn = next(hooks)
        if turn == 0:
            d_down, d_up = own_layer(new[0], d_down_one), own_layer(new[1], d_up_one)
            mlp_sums[3] = mlp_leaves(3)
            mlp_sums[2] = mlp_leaves(2)
            return (mlp_sums[3][1],)
        if turn == 1:
            d_attn = own_layer(new[0], d_attn_one)
            mlp_moves[3] = moves_on(mlp_sums[3])
            mlp_sums[1] = mlp_leaves(1)
            return (mlp_sums[2][1], mlp_moves[3])
        if turn == 2:
            mlp_moves[2] = moves_on(mlp_sums[2], mlp_moves[3])
            mlp_sums[0] = mlp_leaves(0)
            d_qkv = own_layer(new[0], d_qkv_one[1])
            attn_sums[3] = attn_leaves(3, d_qkv)
            attn_sums[2] = attn_leaves(2, d_qkv)
            return (mlp_sums[1][1], mlp_moves[2])
        mlp_moves[1] = moves_on(mlp_sums[1], mlp_moves[2])
        d_qkv = own_layer(new[0], d_qkv_one[0])
        attn_sums[1] = attn_leaves(1, d_qkv)
        attn_sums[0] = attn_leaves(0, d_qkv)
        return (mlp_sums[0][1], mlp_moves[1])

    d_down = d_up = d_attn = None
    grad_zero, rights_zero, gain_zero = backward(received, saved_zero, hook, tuple(lefts))
    attn_moves[3] = moves_on(attn_sums[3])
    attn_moves[2] = moves_on(attn_sums[2], attn_moves[3])
    attn_moves[1] = moves_on(attn_sums[1], attn_moves[2])
    grads = from_chip(own_first(jnp.where(first, grad_zero, grad_one)).reshape(tensor, part, width))

    def finished(name, piece, moved, spots, columns_out, rows_out):
        size = piece[0].shape[1]
        outs = (((wide_half // 2, size), jnp.float32),) * 2
        space = pl.BlockSpec(memory_space=pltpu.VMEM)

        def call(kernel, label, outs, *operands):
            return pl.pallas_call(
                kernel,
                in_specs=[pl.BlockSpec(memory_space=pltpu.SMEM)] + [space] * len(operands),
                out_specs=[space] * len(outs),
                out_shape=[jax.ShapeDtypeStruct(shape, dtype) for shape, dtype in outs],
                compiler_params=pltpu.CompilerParams(vmem_limit_bytes=ROWS_VMEM),
                name=label,
            )(core_word, *operands)

        keep, send = call(last_sum_kernel, name + "_sum", outs, *piece, moved)
        outs = (
            ((wide_half // 2, columns_out), jnp.float32),
            ((rows_out, wide_half // 2), jnp.float32),
        )
        kernel = functools.partial(joined_kernel, spots)
        return call(kernel, name + "_join", outs, keep, flip_pairs(send, 1))

    unit = units // tensor
    up_grad, down_grad = finished(
        "mlp", mlp_sums[0], mlp_moves[1], ((0, unit, 0),), 2 * unit, 2 * unit
    )
    spots = tuple((i * 128, (i + 1) * 128, i * 256) for i in range(3))
    qkv_grad, out_grad = finished("attn", attn_sums[0], attn_moves[1], spots, 768, 256)
    qkv_grad = qkv_grad.reshape(wide_half // 2, 3, -1)

    gain_total = own_first(jnp.where(first, gain_zero, gain_one))
    gains_grad = lax.psum_scatter(gain_total, ("dp", "tensor"), scatter_dimension=1, tiled=True)
    return (
        outputs[None],
        grads[None],
        gains_grad[None],
        qkv_grad[None],
        out_grad[None],
        up_grad[None],
        down_grad[None],
    )


def takes_chips(sizes):
    return sizes["section"] == 2 and sizes["dp"] == 4 and sizes["tensor"] == 4


def solution(mesh):
    placed = (
        P("dp", "tensor", None),
        P("dp", "tensor", None),
        P("dp", "tensor"),
        P(),
        P("section", None, None),
        P("section", None, None, "tensor"),
        P("section", "tensor", None),
        P("section", None, "tensor"),
        P("section", "tensor", None),
    )
    body = per_chip if takes_chips(dict(mesh.shape)) else per_device
    return jax.shard_map(
        body,
        mesh=mesh,
        in_specs=placed,
        out_specs=(
            P("section", "dp", "tensor", None),
            P("section", "dp", "tensor", None),
            P("section", None, ("dp", "tensor")),
            P("section", "dp", None, "tensor"),
            P("section", "tensor", "dp"),
            P("section", "dp", "tensor"),
            P("section", "tensor", "dp"),
        ),
        check_vma=False,
    )
```

```python
import functools
import math

import jax
import jax.numpy as jnp
from jax import lax
from jax.experimental import pallas as pl
from jax.experimental.pallas import tpu as pltpu
from jax.sharding import PartitionSpec as P

HEAD_DIM = 64


NORM_EPSILON = 1e-06
TILE = 128
PAIR_WORK = 1024
MODEL_HALF = 512
QKV = slice(0, 384)
OUT = slice(384, 512)
CHUNK = 32
KERNEL_VMEM = 20 << 20
ROWS_VMEM = 3 << 20


def shifted(block, axis, distance):
    devices = range(lax.axis_size(axis))
    route = [(i - distance, i) for i in devices if i - distance in devices]
    return lax.ppermute(block, axis, route)


def norm_rows(vector, weight_gain):
    return (
        vector
        * lax.rsqrt(jnp.mean(vector * vector, axis=-1, keepdims=True) + NORM_EPSILON)
        * weight_gain
    )


def rotary_tables(seq_len, head_width):
    half_width = head_width // 2
    freqs = 10000.0 ** (-2.0 * jnp.arange(half_width, dtype=jnp.float32) / head_width)
    angles = jnp.arange(seq_len, dtype=jnp.float32)[:, None] * freqs[None, :]
    return (jnp.cos(angles), jnp.sin(angles))


def rotate(vector, cos_table, sin_table):
    first_half, second_half = jnp.split(vector, 2, axis=-1)
    cos_part = cos_table[:, None, :]
    sin_part = sin_table[:, None, :]
    return jnp.concatenate(
        [
            first_half * cos_part - second_half * sin_part,
            second_half * cos_part + first_half * sin_part,
        ],
        axis=-1,
    )


def contract(left_rows, right_rows):
    return lax.dot_general(
        left_rows, right_rows, (((0,), (0,)), ((), ())), preferred_element_type=jnp.float32
    )


def gather_rows(row_values, weight):

    def project(shard_rows, offset):
        return (shard_rows, jnp.dot(shard_rows, weight, preferred_element_type=jnp.float32))

    return project(lax.all_gather(row_values, "tensor", axis=0, tiled=True), jnp.int32(0))


def scatter_rows(row_values, weight, row_count):

    def partial_term(offset, span):
        return jnp.dot(row_values, weight, preferred_element_type=jnp.float32)

    return lax.psum_scatter(
        partial_term(jnp.int32(0), lax.axis_size("tensor") * row_count),
        "tensor",
        scatter_dimension=0,
        tiled=True,
    )


def gather_grads(row_values, weight):

    def project(shard_rows, offset):
        return (shard_rows, jnp.dot(shard_rows, weight.T, preferred_element_type=jnp.float32))

    return project(lax.all_gather(row_values, "tensor", axis=0, tiled=True), jnp.int32(0))


def scatter_grads(row_values, weight, row_count):

    def partial_term(offset, span):
        return jnp.dot(row_values, weight.T, preferred_element_type=jnp.float32)

    return lax.psum_scatter(
        partial_term(jnp.int32(0), lax.axis_size("tensor") * row_count),
        "tensor",
        scatter_dimension=0,
        tiled=True,
    )


def attention_probs(queries, key_rows):
    scores = jnp.einsum(
        "qhd,khd->hqk", queries, key_rows, preferred_element_type=jnp.float32
    ) * HEAD_DIM ** (-0.5)
    length = queries.shape[0]
    positions = jnp.arange(length, dtype=jnp.int32)
    causal = positions[:, None] >= positions[None, :]
    scores = jnp.where(causal[None], scores, -1e30)
    expos = jnp.exp(scores - jnp.max(scores, axis=-1, keepdims=True))
    return expos / jnp.sum(expos, axis=-1, keepdims=True)


def layer_forward(layer_input, weights):
    gains, w_qkv, w_out, w_up, w_down = weights
    row_count, model_width = layer_input.shape
    attn_in = norm_rows(layer_input, gains[0]).astype(jnp.bfloat16)
    gathered_a, qkv = gather_rows(attn_in, w_qkv.reshape(model_width, -1))
    length = qkv.shape[0]
    head_count = w_qkv.shape[2] // HEAD_DIM
    qkv = qkv.reshape(length, 3, head_count, HEAD_DIM)
    cos_table, sin_table = rotary_tables(length, HEAD_DIM)
    queries = rotate(qkv[:, 0], cos_table, sin_table).astype(jnp.bfloat16)
    key_rows = rotate(qkv[:, 1], cos_table, sin_table).astype(jnp.bfloat16)
    values = qkv[:, 2].astype(jnp.bfloat16)
    attn_probs = attention_probs(queries, key_rows).astype(jnp.bfloat16)
    mixed = jnp.einsum("hqk,khd->qhd", attn_probs, values, preferred_element_type=jnp.float32)
    mixed = mixed.reshape(length, -1).astype(jnp.bfloat16)
    attn_branch = scatter_rows(mixed, w_out, row_count)
    hidden = layer_input + norm_rows(attn_branch, gains[1])
    mlp_in = norm_rows(hidden, gains[2]).astype(jnp.bfloat16)
    gathered_c, up_act = gather_rows(mlp_in, w_up)
    gelu_out = jax.nn.gelu(up_act, approximate=True).astype(jnp.bfloat16)
    down_branch = scatter_rows(gelu_out, w_down, row_count)
    result = hidden + norm_rows(down_branch, gains[3])
    kept_values = (
        gathered_a,
        queries,
        key_rows,
        values,
        mixed,
        attn_branch,
        hidden,
        gathered_c,
        up_act,
        gelu_out,
        down_branch,
    )
    return (result, kept_values)


def layer_backward(layer_input, grad_result, kept_values, weights):
    gains, w_qkv, w_out, w_up, w_down = weights
    (
        gathered_a,
        queries,
        key_rows,
        values,
        mixed,
        attn_branch,
        hidden,
        gathered_c,
        up_act,
        gelu_out,
        down_branch,
    ) = kept_values
    row_count, model_width = layer_input.shape
    pullback = jax.vjp(norm_rows, down_branch, gains[3])[1]
    grad_down, gain_three = pullback(grad_result)
    gathered_dd, grad_gelu = gather_grads(grad_down.astype(jnp.bfloat16), w_down)
    down_total = contract(gelu_out, gathered_dd)
    pullback = jax.vjp(lambda vector: jax.nn.gelu(vector, approximate=True), up_act)[1]
    grad_up = pullback(grad_gelu)[0].astype(jnp.bfloat16)
    up_total = contract(gathered_c, grad_up)
    grad_mlp = scatter_grads(grad_up, w_up, row_count)
    pullback = jax.vjp(norm_rows, hidden, gains[2])[1]
    grad_norm_mlp, gain_two = pullback(grad_mlp)
    grad_hidden = grad_result + grad_norm_mlp
    pullback = jax.vjp(norm_rows, attn_branch, gains[1])[1]
    grad_attn, gain_one = pullback(grad_hidden)
    gathered_da, grad_mixed = gather_grads(grad_attn.astype(jnp.bfloat16), w_out)
    out_total = contract(mixed, gathered_da)
    length = grad_mixed.shape[0]
    head_count = w_qkv.shape[2] // HEAD_DIM
    grad_mixed = grad_mixed.astype(jnp.bfloat16).reshape(length, head_count, HEAD_DIM)
    attn_probs = attention_probs(queries, key_rows)
    probs_low = attn_probs.astype(jnp.bfloat16)
    grad_probs = jnp.einsum("qhd,khd->hqk", grad_mixed, values, preferred_element_type=jnp.float32)
    grad_values = jnp.einsum(
        "hqk,qhd->khd", probs_low, grad_mixed, preferred_element_type=jnp.float32
    )
    row_dots = jnp.sum(grad_probs * attn_probs, axis=-1, keepdims=True)
    grad_scores = (attn_probs * (grad_probs - row_dots)).astype(jnp.bfloat16)
    scale_value = HEAD_DIM ** (-0.5)
    grad_queries = (
        jnp.einsum("hqk,khd->qhd", grad_scores, key_rows, preferred_element_type=jnp.float32)
        * scale_value
    )
    grad_keys = (
        jnp.einsum("hqk,qhd->khd", grad_scores, queries, preferred_element_type=jnp.float32)
        * scale_value
    )
    cos_table, sin_table = rotary_tables(length, HEAD_DIM)
    pullback = jax.vjp(lambda vector: rotate(vector, cos_table, sin_table), grad_queries)[1]
    grad_q_raw = pullback(grad_queries)[0]
    grad_k_raw = pullback(grad_keys)[0]
    grad_qkv = (
        jnp.stack([grad_q_raw, grad_k_raw, grad_values], axis=1)
        .reshape(length, -1)
        .astype(jnp.bfloat16)
    )
    qkv_total = contract(gathered_a, grad_qkv).reshape(model_width, 3, -1)
    grad_attn_in = scatter_grads(grad_qkv, w_qkv.reshape(model_width, -1), row_count)
    pullback = jax.vjp(norm_rows, layer_input, gains[0])[1]
    grad_norm_in, gain_zero = pullback(grad_attn_in)
    grad_input = grad_hidden + grad_norm_in
    gain_total = jnp.stack([gain_zero, gain_one, gain_two, gain_three])
    return (grad_input, (gain_total, qkv_total, out_total, up_total, down_total))


def lagged(first_section, stacked):
    blank = jnp.zeros_like(stacked[:1])
    earlier = jnp.concatenate([blank, stacked[:-1]])
    later = jnp.concatenate([stacked[1:], blank])
    return jnp.where(first_section, earlier, later)


def per_device(
    inputs,
    out_cotangent,
    group_ids,
    group_weights,
    gains,
    qkv_weight,
    out_weight,
    up_weight,
    down_weight,
):
    weights = (gains[0], qkv_weight[0], out_weight[0], up_weight[0], down_weight[0])
    micro_count, row_count, model_width = inputs.shape
    first_section = lax.axis_index("section") == 0
    group_count = group_weights.shape[0]
    matches = group_ids[..., None] == jnp.arange(group_count, dtype=jnp.int32)
    row_scale = jnp.sum(jnp.where(matches, group_weights, 0.0), axis=-1)
    scaled = out_cotangent.astype(jnp.float32) * row_scale[..., None]
    padded = jnp.concatenate([inputs, jnp.zeros((1, row_count, model_width), jnp.bfloat16)])

    def forward_tick(received, fresh_input):
        layer_input = jnp.where(first_section, fresh_input, received)
        result, kept_values = layer_forward(layer_input.astype(jnp.float32), weights)
        result_low = result.astype(jnp.bfloat16)
        outgoing = shifted(result_low, "section", 1)
        stashed = ()
        return (outgoing, (layer_input, result_low, stashed))

    start_rows = jnp.zeros((row_count, model_width), jnp.bfloat16)
    _, (layer_inputs, layer_results, stashed) = lax.scan(forward_tick, start_rows, padded)
    layer_outputs = jnp.where(first_section, layer_results[:-1], layer_results[1:])[None]
    back_inputs = lagged(first_section, layer_inputs)
    back_stash = jax.tree.map(lambda stacked: lagged(first_section, stacked), stashed)
    grad_padded = jnp.concatenate([scaled, jnp.zeros((1, row_count, model_width), jnp.float32)])
    tick_index = jnp.arange(micro_count + 1, dtype=jnp.int32)
    tick_valid = jnp.where(first_section, tick_index >= 1, tick_index < micro_count).astype(
        jnp.float32
    )

    def backward_tick(carry, step_item):
        received, totals = carry
        layer_input, cotangent, valid_now, stash_now = step_item
        grad_now = jnp.where(first_section, received.astype(jnp.float32), cotangent)
        input_now = layer_input.astype(jnp.float32)
        kept_values = layer_forward(input_now, weights)[1]
        grad_input, layer_grads = layer_backward(input_now, grad_now, kept_values, weights)
        totals = jax.tree.map(lambda total, update: total + valid_now * update, totals, layer_grads)
        grad_low = grad_input.astype(jnp.bfloat16)
        outgoing = shifted(grad_low, "section", -1)
        return ((outgoing, totals), grad_low)

    start_totals = (
        jnp.zeros((4, model_width), jnp.float32),
        jnp.zeros(qkv_weight.shape[1:], jnp.float32),
        jnp.zeros(out_weight.shape[1:], jnp.float32),
        jnp.zeros(up_weight.shape[1:], jnp.float32),
        jnp.zeros(down_weight.shape[1:], jnp.float32),
    )
    (_, totals), grad_lows = lax.scan(
        backward_tick,
        (start_rows, start_totals),
        (back_inputs, grad_padded, tick_valid, back_stash),
    )
    input_grads = jnp.where(first_section, grad_lows[1:], grad_lows[:-1])[None]
    gain_total, qkv_total, out_total, up_total, down_total = totals
    gains_grad = lax.psum_scatter(gain_total, ("dp", "tensor"), scatter_dimension=1, tiled=True)
    qkv_grad, out_grad, up_grad, down_grad = (
        lax.psum_scatter(
            qkv_total.astype(jnp.bfloat16), "dp", scatter_dimension=0, tiled=True
        ).astype(jnp.float32),
        lax.psum_scatter(
            out_total.astype(jnp.bfloat16), "dp", scatter_dimension=1, tiled=True
        ).astype(jnp.float32),
        lax.psum_scatter(
            up_total.astype(jnp.bfloat16), "dp", scatter_dimension=0, tiled=True
        ).astype(jnp.float32),
        lax.psum_scatter(
            down_total.astype(jnp.bfloat16), "dp", scatter_dimension=1, tiled=True
        ).astype(jnp.float32),
    )
    return (
        layer_outputs,
        input_grads,
        gains_grad[None],
        qkv_grad[None],
        out_grad[None],
        up_grad[None],
        down_grad[None],
    )


def rotated(block, cos_rows, sin_rows):
    lane = lax.broadcasted_iota(jnp.int32, block.shape, 1)
    ahead = pltpu.roll(block, 96, 1)
    behind = pltpu.roll(block, 32, 1)
    swapped = jnp.where(lane % 64 < 32, ahead, behind)
    return block * cos_rows + swapped * sin_rows


def dot_nt(left, right):
    return lax.dot_general(
        left, right, (((1,), (1,)), ((), ())), preferred_element_type=jnp.float32
    )


def dot_nn(left, right):
    return jnp.dot(left, right, preferred_element_type=jnp.float32)


def model_weight(owns, others, cols):
    sides = [jnp.concatenate([ref[:, cols] for ref in refs], axis=1) for refs in (owns, others)]
    return jnp.concatenate(sides, axis=0)


def stacked_up(values):
    return jnp.concatenate(values, axis=0)


def edge_masks(core, rows):
    key = lax.broadcasted_iota(jnp.int32, (rows, 2 * rows), 0)
    query = lax.broadcasted_iota(jnp.int32, (rows, 2 * rows), 1)
    mine = query < rows
    place = jnp.where(mine, query + core * rows, query - rows + (1 - core) * rows)
    return (key + core * rows <= place, key + (1 - core) * rows <= place)


def both_sides(value, half, start, stop, axis=0):
    if axis == 0:
        return jnp.concatenate([value[start:stop], value[half + start : half + stop]], axis=0)
    return jnp.concatenate([value[:, start:stop], value[:, half + start : half + stop]], axis=1)


def hidden_scores(scores, masks, tile, step):
    seen = step * tile
    pieces = []
    for side in range(2):
        base = side * (seen + tile)
        if seen:
            pieces.append(scores[base : base + seen])
        pieces.append(jnp.where(masks[side], scores[base + seen : base + seen + tile], -1e30))
    return jnp.concatenate(pieces, axis=0)


def one_head(rows, head):
    lane = lax.broadcasted_iota(jnp.int32, rows.shape, 1)
    return jnp.where(lane // 64 == head, rows, jnp.zeros_like(rows))


def pick_piece(weight, owns, others, cols):
    for j, (own, other) in enumerate(zip(owns, others)):

        @pl.when(pl.program_id(0) == j)
        def _():
            size = own.shape[0]
            weight[:size] = own[:, cols]
            weight[size:] = other[:, cols]


def attend_kernel(pieces, core_ref, cos_ref, sin_ref, own_rows, other_rows, *refs):
    owns, others = refs[:pieces], refs[pieces : 2 * pieces]
    q_ref, k_ref, v_ref, lse_ref, mix_ref, weight = refs[2 * pieces :]
    half = own_rows.shape[0]
    tile = TILE
    pick_piece(weight, owns, others, QKV)
    proj = dot_nn(stacked_up([own_rows[...], other_rows[...]]), weight[...])
    cos_rows, sin_rows = cos_ref[...], sin_ref[...]
    q = (rotated(proj[:, :128], cos_rows, sin_rows) * HEAD_DIM ** (-0.5)).astype(jnp.bfloat16)
    k = rotated(proj[:, 128:256], cos_rows, sin_rows).astype(jnp.bfloat16)
    v32 = proj[:, 256:]
    q_ref[0] = q
    k_ref[0] = k
    v_ref[0] = v32.astype(jnp.bfloat16)
    v_flip = v32.T.astype(jnp.bfloat16)
    masks = edge_masks(core_ref[0], tile)

    def scored(step, head):
        stop = (step + 1) * tile
        q_head = one_head(both_sides(q, half, step * tile, stop), head)
        return hidden_scores(dot_nt(both_sides(k, half, 0, stop), q_head), masks, tile, step)

    units = [(step, head) for step in range(half // tile) for head in range(2)]
    ahead = scored(*units[0])
    outs = []
    for spot, (step, head) in enumerate(units):
        scores = ahead
        if spot + 1 < len(units):
            ahead = scored(*units[spot + 1])
        stop = (step + 1) * tile
        top = jnp.max(scores, axis=0, keepdims=True)
        expos = jnp.exp(scores - top)
        total = jnp.sum(expos, axis=0, keepdims=True)
        lse = top + jnp.log(total)
        lse_ref[0, head : head + 1, step * tile : stop] = lse[:, :tile]
        lse_ref[0, head : head + 1, half + step * tile : half + stop] = lse[:, tile:]
        v_cols = both_sides(v_flip, half, 0, stop, axis=1)
        out = dot_nn(v_cols[64 * head : 64 * head + 64], expos.astype(jnp.bfloat16))
        outs.append(out * (1.0 / total))
        if head == 1:
            mixed = jnp.concatenate(outs, axis=0).T.astype(jnp.bfloat16)
            outs = []
            mix_ref[step * tile : stop, :] = mixed[:tile]
            mix_ref[half + step * tile : half + stop, :] = mixed[tile:]


def attend_back_kernel(pieces, core_ref, cos_ref, sin_ref, own_rows, other_rows, *refs):
    owns, others = refs[:pieces], refs[pieces : 2 * pieces]
    q_ref, k_ref, v_ref, lse_ref, out_ref, weight, dq, dk, dv = refs[2 * pieces :]
    half = own_rows.shape[0]
    tile = TILE
    pick_piece(weight, owns, others, OUT)
    rows = stacked_up([own_rows[...], other_rows[...]])
    d_mixed = dot_nn(rows, weight[...]).astype(jnp.bfloat16)
    q, k, v = q_ref[0], k_ref[0], v_ref[0]
    k_flip = k.astype(jnp.float32).T.astype(jnp.bfloat16)
    masks = edge_masks(core_ref[0], tile)
    steps = half // tile

    def scored(step, head):
        stop = (step + 1) * tile
        q_head = one_head(both_sides(q, half, step * tile, stop), head)
        g_head = one_head(both_sides(d_mixed, half, step * tile, stop), head)
        scores = hidden_scores(dot_nt(both_sides(k, half, 0, stop), q_head), masks, tile, step)
        return q_head, g_head, scores, dot_nt(both_sides(v, half, 0, stop), g_head)

    units = [(step, head) for step in reversed(range(steps)) for head in range(2)]
    ahead = scored(*units[0])
    dq_flips = []
    dk_sum = dv_sum = None
    for spot, (step, head) in enumerate(units):
        q_head, g_head, scores, d_probs = ahead
        if spot + 1 < len(units):
            ahead = scored(*units[spot + 1])
        stop = (step + 1) * tile
        lse = both_sides(lse_ref[0], half, step * tile, stop, axis=1)
        probs = jnp.exp(scores - lse[head : head + 1])
        dots = jnp.sum(probs * d_probs, axis=0, keepdims=True)
        d_scores = (probs * (d_probs - dots)).astype(jnp.bfloat16)
        dv_part = dot_nn(probs.astype(jnp.bfloat16), g_head)
        dk_part = dot_nn(d_scores, q_head)
        k_cols = both_sides(k_flip, half, 0, stop, axis=1)
        dq_flips.append(dot_nn(k_cols[64 * head : 64 * head + 64], d_scores))
        if head == 0:
            dv_sum, dk_sum = dv_part, dk_part
            continue
        dv_sum, dk_sum = dv_sum + dv_part, dk_sum + dk_part
        dq_rows = jnp.concatenate(dq_flips, axis=0).T * HEAD_DIM ** (-0.5)
        dq_flips = []
        dq[step * tile : stop] = dq_rows[:tile]
        dq[half + step * tile : half + stop] = dq_rows[tile:]
        for base, part in ((0, slice(0, stop)), (half, slice(stop, 2 * stop))):
            if step == steps - 1:
                dk[base : base + stop] = dk_sum[part]
                dv[base : base + stop] = dv_sum[part]
            else:
                dk[base : base + stop] += dk_sum[part]
                dv[base : base + stop] += dv_sum[part]
    cos_rows, sin_rows = cos_ref[...], -sin_ref[...]
    out_ref[:, :128] = rotated(dq[...], cos_rows, sin_rows).astype(jnp.bfloat16)
    out_ref[:, 128:256] = rotated(dk[...], cos_rows, sin_rows).astype(jnp.bfloat16)
    out_ref[:, 256:] = dv[...].astype(jnp.bfloat16)


def split_rows(total, own_ref, other_ref):
    half = own_ref.shape[0]
    own_ref[...] = total[:half]
    other_ref[...] = total[half:].astype(jnp.bfloat16)


def to_model_kernel(lefts, pieces, cols, *refs):
    left, refs = jnp.concatenate([ref[...] for ref in refs[:lefts]], axis=1), refs[lefts:]
    weight = model_weight(refs[:pieces], refs[pieces : 2 * pieces], cols)
    split_rows(dot_nt(left, weight), *refs[2 * pieces :])


def mlp_down_kernel(pieces, left_ref, *refs):
    sides = [stacked_up([ref[...] for ref in side]) for side in (refs[:pieces], refs[pieces:-2])]
    split_rows(dot_nn(left_ref[...], jnp.concatenate(sides, axis=1)), *refs[-2:])


def gelu_both(up_act):
    root = math.sqrt(2.0 / math.pi)
    square = up_act * up_act
    rise = 0.5 + 0.5 * jnp.tanh(up_act * (root + root * 0.044715 * square))
    value = up_act * rise
    slope = rise + value * (1.0 - rise) * (2.0 * root + 6.0 * root * 0.044715 * square)
    return value, slope


def mlp_up_kernel(pieces, own_rows, other_rows, *refs):
    owns, others = refs[:pieces], refs[pieces : 2 * pieces]
    gelu_ref, slope_ref = refs[2 * pieces :]
    half = own_rows.shape[0]
    size = owns[0].shape[1]
    step = half // 2
    units = [(j, i) for j in range(pieces) for i in range(4)]

    def product(j, i):
        rows = (own_rows, other_rows)[i // 2][i % 2 * step : (i % 2 + 1) * step]
        return dot_nn(rows, stacked_up([owns[j][...], others[j][...]]))

    ahead = product(*units[0])
    for spot, (j, i) in enumerate(units):
        up_act = ahead
        if spot + 1 < len(units):
            ahead = product(*units[spot + 1])
        value, slope = gelu_both(up_act)
        gelu_ref[i * step : (i + 1) * step, j * size : (j + 1) * size] = value.astype(jnp.bfloat16)
        slope_ref[i * step : (i + 1) * step, j * size : (j + 1) * size] = slope.astype(
            jnp.bfloat16
        )


def mlp_up_back_kernel(pieces, own_rows, other_rows, slope_ref, *refs):
    owns, others = refs[:pieces], refs[pieces : 2 * pieces]
    out_ref = refs[-1]
    size = owns[0].shape[0]
    rows = stacked_up([own_rows[...], other_rows[...]])
    for j in range(pieces):
        cols = slice(j * size, (j + 1) * size)
        weight = jnp.concatenate([owns[j][...], others[j][...]], axis=1)
        d_gelu = dot_nt(rows, weight)
        out_ref[:, cols] = (d_gelu * slope_ref[:, cols].astype(jnp.float32)).astype(jnp.bfloat16)


def inverse_size(rows):
    return lax.rsqrt(jnp.mean(rows * rows, axis=-1, keepdims=True) + NORM_EPSILON)


def norm_back(rows, gain, grad):
    scale = inverse_size(rows)
    weighted = grad * gain
    inner = jnp.mean(rows * weighted, axis=-1, keepdims=True)
    return scale * weighted - rows * (scale * scale * scale * inner), rows * scale * grad


def folded(rows):
    return jnp.sum(rows.reshape(rows.shape[0] // 8, 8, rows.shape[1]), axis=0)


def wide(ref, spot):
    return ref[spot, :].astype(jnp.float32)


def by_chunks(count, body, sums=0, width=0):
    def one(i, carry):
        more = body(pl.ds(pl.multiple_of(i * CHUNK, CHUNK), CHUNK))
        return tuple(old + folded(new) for old, new in zip(carry, more))

    start = tuple(jnp.zeros((8, width), jnp.float32) for _ in range(sums))
    totals = lax.fori_loop(0, count // CHUNK, one, start)
    return [jnp.sum(total, axis=0, keepdims=True) for total in totals]


def norm_in_kernel(gain_ref, rows_ref, out_ref):
    def body(spot):
        rows = wide(rows_ref, spot)
        out_ref[spot, :] = (rows * inverse_size(rows) * gain_ref[0:1]).astype(jnp.bfloat16)
        return ()

    by_chunks(rows_ref.shape[0], body)


def after_attention_kernel(
    gain_ref, rows_ref, own_ref, other_ref, branch_ref, hidden_ref, out_ref
):
    def body(spot):
        branch = own_ref[spot, :] + wide(other_ref, spot)
        hidden = wide(rows_ref, spot) + branch * inverse_size(branch) * gain_ref[1:2]
        branch_ref[spot, :] = branch
        hidden_ref[spot, :] = hidden
        out_ref[spot, :] = (hidden * inverse_size(hidden) * gain_ref[2:3]).astype(jnp.bfloat16)
        return ()

    by_chunks(rows_ref.shape[0], body)


def after_mlp_kernel(gain_ref, hidden_ref, own_ref, other_ref, branch_ref, out_ref):
    def body(spot):
        branch = own_ref[spot, :] + wide(other_ref, spot)
        branch_ref[spot, :] = branch
        result = hidden_ref[spot, :] + branch * inverse_size(branch) * gain_ref[3:4]
        out_ref[spot, :] = result.astype(jnp.bfloat16)
        return ()

    by_chunks(hidden_ref.shape[0], body)


def into_mlp_back_kernel(gain_ref, grad_ref, branch_ref, out_ref, sum_ref):
    def body(spot):
        d_rows, d_gain = norm_back(branch_ref[spot, :], gain_ref[3:4], wide(grad_ref, spot))
        out_ref[spot, :] = d_rows.astype(jnp.bfloat16)
        return (d_gain,)

    (sum_ref[...],) = by_chunks(grad_ref.shape[0], body, 1, grad_ref.shape[1])


def into_attention_back_kernel(
    gain_ref, grad_ref, own_ref, other_ref, hidden_ref, branch_ref, d_hidden_ref, out_ref, *sums
):
    def body(spot):
        d_rows = own_ref[spot, :] + wide(other_ref, spot)
        d_rows, d_gain = norm_back(hidden_ref[spot, :], gain_ref[2:3], d_rows)
        d_hidden = wide(grad_ref, spot) + d_rows
        d_hidden_ref[spot, :] = d_hidden
        d_rows, d_first = norm_back(branch_ref[spot, :], gain_ref[1:2], d_hidden)
        out_ref[spot, :] = d_rows.astype(jnp.bfloat16)
        return (d_first, d_gain)

    totals = by_chunks(grad_ref.shape[0], body, 2, grad_ref.shape[1])
    sums[0][...], sums[1][...] = totals


def out_of_layer_kernel(gain_ref, rows_ref, own_ref, other_ref, d_hidden_ref, out_ref, sum_ref):
    def body(spot):
        d_rows = own_ref[spot, :] + wide(other_ref, spot)
        d_rows, d_gain = norm_back(wide(rows_ref, spot), gain_ref[0:1], d_rows)
        out_ref[spot, :] = (d_hidden_ref[spot, :] + d_rows).astype(jnp.bfloat16)
        return (d_gain,)

    (sum_ref[...],) = by_chunks(rows_ref.shape[0], body, 1, rows_ref.shape[1])


def work(flops, arrays):
    size = sum(math.prod(array.shape) * jnp.dtype(array.dtype).itemsize for array in arrays)
    return pl.CostEstimate(flops=flops, bytes_accessed=size, transcendentals=0)


def without(kernel, first, count):
    return lambda *refs: kernel(*refs[:first], *refs[first + count :])


def on_chip(kernel, name, outs, *operands, limit=ROWS_VMEM, flops=0, waits=()):
    shapes = [jax.ShapeDtypeStruct(shape, dtype) for shape, dtype in outs]
    space = pl.BlockSpec(memory_space=pltpu.VMEM)
    return pl.pallas_call(
        without(kernel, len(operands), len(waits)),
        in_specs=[space] * len(operands) + [pl.BlockSpec(memory_space=pl.ANY)] * len(waits),
        out_specs=[space] * len(outs),
        out_shape=shapes,
        compiler_params=pltpu.CompilerParams(vmem_limit_bytes=limit),
        cost_estimate=work(flops, (*operands, *shapes)),
        name=name,
    )(*operands, *waits)


def whole_block(array):
    return pl.BlockSpec(array.shape, lambda j: (0,) * array.ndim)


def by_pairs(kernel, name, core, operands, pieces, blocks, outs, scratch, flops, waits):
    shapes = [jax.ShapeDtypeStruct(shape, dtype) for shape, dtype, _ in outs]
    taken = 1 + len(operands) + 2 * len(pieces[0]) + len(blocks)
    return pl.pallas_call(
        without(functools.partial(kernel, len(pieces[0])), taken, len(waits)),
        grid=(len(pieces[0]),),
        in_specs=[pl.BlockSpec(memory_space=pltpu.SMEM)]
        + [whole_block(array) for array in (*operands, *pieces[0], *pieces[1])]
        + [spec for _, spec in blocks]
        + [pl.BlockSpec(memory_space=pl.ANY)] * len(waits),
        out_specs=[spec for _, _, spec in outs],
        out_shape=shapes,
        scratch_shapes=scratch,
        compiler_params=pltpu.CompilerParams(vmem_limit_bytes=KERNEL_VMEM),
        cost_estimate=work(flops, (*operands, *pieces[0], *pieces[1], *shapes)),
        name=name,
    )(core, *operands, *pieces[0], *pieces[1], *[array for array, _ in blocks], *waits)


def attend(core, tables, rows, pieces, waits):
    half, features = rows[0].shape
    length, count = 2 * half, len(pieces[0])
    lanes = ((count, length, 128), jnp.bfloat16, pl.BlockSpec((1, length, 128), lambda j: (j, 0, 0)))
    lse = ((count, 2, length), jnp.float32, pl.BlockSpec((1, 2, length), lambda j: (j, 0, 0)))
    mixed = ((length, count * 128), jnp.bfloat16, pl.BlockSpec((length, 128), lambda j: (0, j)))
    return by_pairs(
        attend_kernel,
        "attend",
        core,
        (*tables, *rows),
        pieces,
        (),
        (lanes, lanes, lanes, lse, mixed),
        [pltpu.VMEM((features, 384), jnp.bfloat16)],
        count * length * (2 * features * 384 + 2 * PAIR_WORK * length),
        waits,
    )


def attend_back(core, tables, rows, pieces, base, waits, q, k, v, lse):
    half, features = rows[0].shape
    length, count = 2 * half, len(pieces[0])
    lanes = pl.BlockSpec((1, length, 128), lambda j: (base + j, 0, 0))
    lse_spec = pl.BlockSpec((1, 2, length), lambda j: (base + j, 0, 0))
    out = ((length, count * 384), jnp.bfloat16, pl.BlockSpec((length, 384), lambda j: (0, j)))
    return by_pairs(
        attend_back_kernel,
        "attend_back",
        core,
        (*tables, *rows),
        pieces,
        ((q, lanes), (k, lanes), (v, lanes), (lse, lse_spec)),
        (out,),
        [pltpu.VMEM((features, 128), jnp.bfloat16)] + [pltpu.VMEM((length, 128), jnp.float32)] * 3,
        count * length * (2 * features * 128 + 5 * PAIR_WORK * length),
        waits,
    )[0]


def exchanged(parts):
    return parts[0], flip_pairs(parts[1], 1)


def model_rows(kernel, name, lefts, pieces, waits=()):
    length, width = lefts[0].shape[0], 2 * MODEL_HALF
    outs = (((length // 2, width), jnp.float32), ((length // 2, width), jnp.bfloat16))
    hidden = sum(left.shape[1] for left in lefts)
    more = {"limit": KERNEL_VMEM, "flops": 2 * length * width * hidden, "waits": waits}
    return exchanged(on_chip(kernel, name, outs, *lefts, *pieces[0], *pieces[1], **more))


def flip_pairs(block, distance):
    size = lax.axis_size("dp")
    return lax.ppermute(block, "dp", [(i, i ^ distance) for i in range(size)])


def passed_on(block, step):
    size = lax.axis_size("tensor")
    return lax.ppermute(block, "tensor", [(i, (i + step) % size) for i in range(size)])


def pack_kernel(first_ref, second_ref, own_ref, other_ref):
    half = first_ref.shape[0] // 2
    own_ref[:half] = first_ref[:half]
    own_ref[half:] = second_ref[:, :half]
    other_ref[:half] = first_ref[half:].astype(jnp.bfloat16)
    other_ref[half:] = second_ref[:, half:].astype(jnp.bfloat16)


def pack_wide_kernel(first_ref, second_ref, own_ref, other_ref):
    half, width = own_ref.shape[0], first_ref.shape[1]
    own_ref[:, :width] = first_ref[:half]
    own_ref[:, width:] = second_ref[:half]
    other_ref[:, :width] = first_ref[half:].astype(jnp.bfloat16)
    other_ref[:, width:] = second_ref[half:].astype(jnp.bfloat16)


def gate_kernel(up_ref, down_ref, up_out, down_out):
    up_out[...] = up_ref[...]
    down_out[...] = down_ref[...]


def mlp_sum_kernel(core_ref, own_ref, other_ref, moved_ref, up_keep, down_keep, up_send, down_send):
    half = own_ref.shape[0] // 2
    size = up_keep.shape[0]

    def total(rows, cols):
        more = other_ref[rows, cols].astype(jnp.float32) + moved_ref[rows, cols].astype(jnp.float32)
        return own_ref[rows, cols] + more

    for core in range(2):

        @pl.when(core_ref[0] == core)
        def _():
            for place, up, down in ((core, up_keep, down_keep), (1 - core, up_send, down_send)):
                spot = slice(place * size, (place + 1) * size)
                up[...] = total(spot, slice(None))
                down[...] = total(slice(half, None), spot)


def mlp_join_kernel(core_ref, up_keep, down_keep, up_sent, down_sent, up_out, down_out):
    size = up_keep.shape[1]
    for core in range(2):

        @pl.when(core_ref[0] == core)
        def _():
            places = ((core, up_keep, down_keep), (1 - core, up_sent, down_sent))
            for place, up, down in places:
                spot = slice(place * size, (place + 1) * size)
                up_out[:, spot] = up[...]
                down_out[spot] = down[...]


def pick_kernel(core_ref, rows_ref, keep_ref, send_ref):
    count = keep_ref.shape[0]
    keep_ref[...] = rows_ref[pl.ds(core_ref[0] * count, count)]
    send_ref[...] = rows_ref[pl.ds((1 - core_ref[0]) * count, count)]


def in_order_kernel(core_ref, keep_ref, sent_ref, out_ref):
    out_ref[:, pl.ds(core_ref[0], 1)] = keep_ref[...][:, None]
    out_ref[:, pl.ds(1 - core_ref[0], 1)] = sent_ref[...][:, None]


def with_core(kernel, name, core, outs, *operands, waits=()):
    space = pl.BlockSpec(memory_space=pltpu.VMEM)
    return pl.pallas_call(
        without(kernel, 1 + len(operands), len(waits)),
        in_specs=[pl.BlockSpec(memory_space=pltpu.SMEM)]
        + [space] * len(operands)
        + [pl.BlockSpec(memory_space=pl.ANY)] * len(waits),
        out_specs=[space] * len(outs),
        out_shape=[jax.ShapeDtypeStruct(shape, dtype) for shape, dtype in outs],
        compiler_params=pltpu.CompilerParams(vmem_limit_bytes=ROWS_VMEM),
        name=name,
    )(core, *operands, *waits)


def last_sum_kernel(core_ref, own_ref, other_ref, moved_ref, keep_ref, send_ref):
    rows = keep_ref.shape[0]

    def total(block):
        spot = pl.ds(pl.multiple_of(block * rows, rows), rows)
        return own_ref[spot, :] + wide(other_ref, spot) + wide(moved_ref, spot)

    keep_ref[...] = total(core_ref[0])
    send_ref[...] = total(1 - core_ref[0])


def joined_kernel(spots, core_ref, keep_ref, sent_ref, column_ref, row_ref):
    size = row_ref.shape[0] // 2
    for core in range(2):

        @pl.when(core_ref[0] == core)
        def _():
            for place, source in ((core, keep_ref), (1 - core, sent_ref)):
                for start, stop, to in spots:
                    step = stop - start
                    column_ref[:, to + place * step : to + (place + 1) * step] = source[:, start:stop]
                row_ref[place * size : (place + 1) * size] = source[:, spots[-1][1] :].T


def per_chip(
    inputs,
    out_cotangent,
    group_ids,
    group_weights,
    gains,
    qkv_weight,
    out_weight,
    up_weight,
    down_weight,
):
    micro, row_count, width = inputs.shape
    tensor = lax.axis_size("tensor")
    part = row_count // 2
    wide_half = width // 2
    length = tensor * row_count
    half = length // 2
    first = lax.axis_index("section") == 0
    place = lax.axis_index("dp")
    core = place % 2
    upper = place // 2 % 2
    core_zero = core == 0
    low_half = upper == 0

    def ordered(mine, other):
        return jnp.where(core_zero, mine, other), jnp.where(core_zero, other, mine)

    def own_first(values):
        return jnp.where(low_half, values, jnp.roll(values, wide_half, axis=-1))

    def both_rows(own):
        return own, flip_pairs(own, 1)

    def to_chip(block):
        split = block.reshape((micro, 2, part) + block.shape[2:])
        mine = lax.dynamic_index_in_dim(split, core, 1, keepdims=False)
        other = lax.dynamic_index_in_dim(split, 1 - core, 1, keepdims=False)
        return lax.all_to_all(
            jnp.concatenate(ordered(mine, flip_pairs(other, 1))), "tensor", 0, 0, tiled=True
        )

    def from_chip(block, waits=()):
        spread_out = lax.all_to_all(block, "tensor", 0, 0, tiled=True)
        piece = ((micro, part, width), jnp.bfloat16)
        keep, send = with_core(
            pick_kernel, "pick", core_word, (piece, piece), spread_out, waits=waits
        )
        outs = (((micro, 2, part, width), jnp.bfloat16),)
        (rows,) = with_core(
            in_order_kernel, "in_order", core_word, outs, keep, flip_pairs(send, 1)
        )
        return rows.reshape(micro, row_count, width)

    def columns(local):
        size = local.shape[-1] // 2
        mid = (0,) * (local.ndim - 2)
        piece = lax.dynamic_slice(
            local,
            (wide_half * upper, *mid, size * core),
            (wide_half, *local.shape[1:-1], size),
        )
        return piece.reshape(wide_half, -1)

    def rows(local):
        size = local.shape[0] // 2
        return lax.dynamic_slice(local, (size * core, wide_half * upper), (size, wide_half))

    core_word = core.astype(jnp.int32).reshape(1)
    attn_piece = jnp.concatenate([columns(qkv_weight[0]), rows(out_weight[0]).T], axis=1)

    def spread(piece):
        pieces = [piece]
        for _ in range(tensor - 1):
            pieces.append(passed_on(pieces[-1], 1))
        return pieces

    attn_own = spread(attn_piece)
    attn_other = [flip_pairs(piece, 2) for piece in attn_own]
    up_piece, down_piece = columns(up_weight[0]), rows(down_weight[0])
    outs = tuple((piece.shape, piece.dtype) for piece in (up_piece, down_piece))
    up_piece, down_piece = on_chip(
        gate_kernel, "gate", outs, up_piece, down_piece, waits=(attn_own[2],)
    )
    up_own, down_own = spread(up_piece), spread(down_piece)
    up_other = [flip_pairs(piece, 2) for piece in up_own]
    down_other = [flip_pairs(piece, 2) for piece in down_own]
    w_attn, w_up, w_down = (attn_own, attn_other), (up_own, up_other), (down_own, down_other)
    unit = up_piece.shape[1]
    units = tensor * unit

    group_count = group_weights.shape[0]
    matches = group_ids[..., None] == jnp.arange(group_count, dtype=jnp.int32)
    row_scale = jnp.sum(jnp.where(matches, group_weights, 0.0), axis=-1)
    weighted = (out_cotangent.astype(jnp.float32) * row_scale[..., None]).astype(jnp.bfloat16)
    start = to_chip(own_first(jnp.where(first, inputs, weighted))).reshape(half, width)
    gain = own_first(gains[0])

    turns = jnp.arange(half, dtype=jnp.int32)
    turns = turns // part * row_count + turns % part
    positions = jnp.concatenate([turns + core * part, turns + (1 - core) * part])
    freqs = 10000.0 ** (-2.0 * jnp.arange(HEAD_DIM // 2, dtype=jnp.float32) / HEAD_DIM)
    angles = positions.astype(jnp.float32)[:, None] * freqs[None, :]
    cos_part, sin_part = jnp.cos(angles), jnp.sin(angles)
    tables = (
        jnp.concatenate([cos_part] * 4, axis=1),
        jnp.concatenate([-sin_part, sin_part] * 2, axis=1),
    )
    row32, row16 = ((half, width), jnp.float32), ((half, width), jnp.bfloat16)
    unit16 = ((length, units), jnp.bfloat16)
    sum32 = ((1, width), jnp.float32)
    mlp_cost = {"limit": KERNEL_VMEM, "flops": 2 * length * width * units}
    every = slice(None)

    def model_kernel(cols, lefts=1):
        return functools.partial(to_model_kernel, lefts, tensor, cols)

    down_kernel = functools.partial(mlp_down_kernel, tensor)

    def forward(layer_input, waits):
        attn_in = both_rows(
            on_chip(norm_in_kernel, "norm_in", (row16,), gain, layer_input, waits=waits[0])[0]
        )
        *heads, mixed = attend(core_word, tables, attn_in, w_attn, waits[1])
        parts = model_rows(model_kernel(OUT), "attn_out", [mixed], w_attn, waits[2])
        operands = (gain, layer_input, *parts)
        branch, hidden, mlp_in = on_chip(
            after_attention_kernel, "after_attn", (row32, row32, row16), *operands, waits=waits[3]
        )
        mlp_in = both_rows(mlp_in)
        kernel = functools.partial(mlp_up_kernel, tensor)
        operands = (*mlp_in, *w_up[0], *w_up[1])
        gelu_out, slope = on_chip(kernel, "mlp_up", (unit16, unit16), *operands, **mlp_cost)
        parts = model_rows(down_kernel, "mlp_down", [gelu_out], w_down)
        mlp_branch, result = on_chip(
            after_mlp_kernel, "after_mlp", (row32, row16), gain, hidden, *parts
        )
        saved = (layer_input, heads, branch, hidden, slope, mlp_branch)
        return result, saved, (attn_in, mixed, mlp_in, gelu_out)

    def backward(grad, saved, hook, waits=()):
        layer_input, heads, branch, hidden, slope, mlp_branch = saved
        operands = (gain, grad, mlp_branch)
        d_down, sum_three = on_chip(
            into_mlp_back_kernel, "into_mlp_back", (row16, sum32), *operands, waits=waits
        )
        d_down = both_rows(d_down)
        kernel = functools.partial(mlp_up_back_kernel, tensor)
        operands = (*d_down, slope, *w_down[0], *w_down[1])
        (d_up,) = on_chip(kernel, "mlp_up_back", (unit16,), *operands, **mlp_cost)
        waits = hook(d_down, d_up)
        parts = model_rows(model_kernel(every), "mlp_back", [d_up], w_up, waits)
        waits = hook()
        operands = (gain, grad, *parts, hidden, branch)
        outs = (row32, row16, sum32, sum32)
        d_hidden, d_attn, sum_one, sum_two = on_chip(
            into_attention_back_kernel, "into_attn_back", outs, *operands, waits=waits
        )
        d_attn = both_rows(d_attn)
        waits = hook(d_attn)
        d_qkv = []
        for base in reversed(range(0, tensor, 2)):
            some = [side[base : base + 2] for side in w_attn]
            now = attend_back(core_word, tables, d_attn, some, base, waits, *heads)
            d_qkv.insert(0, now)
            waits = hook(now)
        parts = model_rows(model_kernel(QKV, 2), "attn_back", d_qkv, w_attn, waits)
        operands = (gain, layer_input, *parts, d_hidden)
        d_input, sum_zero = on_chip(
            out_of_layer_kernel, "out_of_layer", (row16, sum32), *operands
        )
        sums = jnp.concatenate([sum_zero, sum_one, sum_two, sum_three])
        return d_input, (d_qkv, d_attn, d_up, d_down), sums

    low_zero, saved_zero, lefts_zero = forward(
        start,
        (
            (attn_other[1],),
            (up_own[1], down_own[1], up_other[0]),
            (up_own[2], down_other[0]),
            (down_own[2], up_other[1], down_other[1], up_own[3]),
        ),
    )
    low_one, saved_one, lefts_one = forward(shifted(low_zero, "section", 1), ((),) * 4)
    grad_one, rights_one, gain_one = backward(start, saved_one, lambda *new: ())
    received = shifted(grad_one, "section", -1)

    def joined(pair):
        return lax.optimization_barrier(jnp.concatenate(pair, axis=0))

    def own_layer(zero, one):
        if isinstance(zero, tuple):
            zero, one = joined(zero), joined(one)
        return jnp.where(first, zero, one)

    lefts_zero, lefts_one = lax.optimization_barrier((lefts_zero, lefts_one, grad_one))[:2]
    attn_in, mixed, mlp_in, gelu_out = lefts = list(map(own_layer, lefts_zero, lefts_one))
    lows = lax.optimization_barrier((low_zero, low_one, grad_one))[:2]
    lows = own_first(jnp.where(first, *lows)).reshape(tensor, part, width)

    def block(array, j, count=tensor):
        size = array.shape[1] // count
        return array[:, j * size : (j + 1) * size]

    def leave(kernel, shape, *pairs):
        totals = [contract(*pair) for pair in pairs]
        own, other = on_chip(kernel, "pack", ((shape, jnp.float32), (shape, jnp.bfloat16)), *totals)
        return own, flip_pairs(other, 2)

    def mlp_leaves(j):
        shape = (wide_half + unit, unit)
        return leave(pack_kernel, shape, (mlp_in, block(d_up, j)), (block(gelu_out, j), d_down))

    def attn_leaves(j, d_qkv):
        shape = (wide_half, 512)
        pairs = ((attn_in, block(d_qkv, j % 2, 2)), (d_attn, block(mixed, j)))
        return leave(pack_wide_kernel, shape, *pairs)

    def moves_on(piece, moved=None):
        own, other = piece
        total = own + other.astype(jnp.float32)
        if moved is not None:
            total = total + moved.astype(jnp.float32)
        return passed_on(total.astype(jnp.bfloat16), -1)

    d_qkv_one, d_attn_one, d_up_one, d_down_one = rights_one
    mlp_sums, attn_sums = [None] * tensor, [None] * tensor
    mlp_moves, attn_moves = [None] * tensor, [None] * tensor
    hooks = iter(range(5))

    def hook(*new):
        nonlocal d_down, d_up, d_attn
        turn = next(hooks)
        if turn == 0:
            d_down, d_up = own_layer(new[0], d_down_one), own_layer(new[1], d_up_one)
            mlp_sums[3] = mlp_leaves(3)
            mlp_sums[2] = mlp_leaves(2)
            return (mlp_sums[3][0], mlp_sums[2][0])
        if turn == 1:
            return (mlp_sums[3][1],)
        if turn == 2:
            d_attn = own_layer(new[0], d_attn_one)
            mlp_moves[3] = moves_on(mlp_sums[3])
            mlp_sums[1] = mlp_leaves(1)
            return (mlp_sums[2][1], mlp_moves[3])
        if turn == 3:
            mlp_moves[2] = moves_on(mlp_sums[2], mlp_moves[3])
            mlp_sums[0] = mlp_leaves(0)
            d_qkv = own_layer(new[0], d_qkv_one[1])
            attn_sums[3] = attn_leaves(3, d_qkv)
            attn_sums[2] = attn_leaves(2, d_qkv)
            return (mlp_sums[1][1], mlp_moves[2])
        mlp_moves[1] = moves_on(mlp_sums[1], mlp_moves[2])
        d_qkv = own_layer(new[0], d_qkv_one[0])
        attn_sums[1] = attn_leaves(1, d_qkv)
        attn_sums[0] = attn_leaves(0, d_qkv)
        return (mlp_sums[0][1], mlp_moves[1])

    d_down = d_up = d_attn = None
    grad_zero, rights_zero, gain_zero = backward(received, saved_zero, hook, tuple(lefts))
    attn_moves[3] = moves_on(attn_sums[3])
    attn_moves[2] = moves_on(attn_sums[2], attn_moves[3])
    attn_moves[1] = moves_on(attn_sums[1], attn_moves[2])
    outputs = from_chip(lows, (attn_sums[3][0],))
    grads = from_chip(own_first(jnp.where(first, grad_zero, grad_one)).reshape(tensor, part, width))

    block32 = ((wide_half // 2, unit), jnp.float32)
    down32 = ((unit, wide_half // 2), jnp.float32)
    up_keep, down_keep, up_send, down_send = with_core(
        mlp_sum_kernel,
        "mlp_sum",
        core_word,
        (block32, down32, block32, down32),
        *mlp_sums[0],
        mlp_moves[1],
    )
    outs = (
        ((wide_half // 2, 2 * unit), jnp.float32),
        ((2 * unit, wide_half // 2), jnp.float32),
    )
    sent = flip_pairs(up_send, 1), flip_pairs(down_send, 1)
    up_grad, down_grad = with_core(
        mlp_join_kernel, "mlp_join", core_word, outs, up_keep, down_keep, *sent
    )
    outs = (((wide_half // 2, 512), jnp.float32),) * 2
    keep, send = with_core(
        last_sum_kernel, "attn_sum", core_word, outs, *attn_sums[0], attn_moves[1]
    )
    spots = tuple((i * 128, (i + 1) * 128, i * 256) for i in range(3))
    outs = (((wide_half // 2, 768), jnp.float32), ((256, wide_half // 2), jnp.float32))
    kernel = functools.partial(joined_kernel, spots)
    qkv_grad, out_grad = with_core(
        kernel, "attn_join", core_word, outs, keep, flip_pairs(send, 1)
    )
    qkv_grad = qkv_grad.reshape(wide_half // 2, 3, -1)

    gain_total = own_first(jnp.where(first, gain_zero, gain_one))
    count = tensor * lax.axis_size("dp")
    gain_parts = gain_total.reshape(4, count, width // count).swapaxes(0, 1)
    gain_parts = lax.all_to_all(gain_parts, ("dp", "tensor"), 0, 0, tiled=True)
    gains_grad = jnp.sum(gain_parts, axis=0)
    return (
        outputs[None],
        grads[None],
        gains_grad[None],
        qkv_grad[None],
        out_grad[None],
        up_grad[None],
        down_grad[None],
    )


def takes_chips(sizes):
    return sizes["section"] == 2 and sizes["dp"] == 4 and sizes["tensor"] == 4


def solution(mesh):
    placed = (
        P("dp", "tensor", None),
        P("dp", "tensor", None),
        P("dp", "tensor"),
        P(),
        P("section", None, None),
        P("section", None, None, "tensor"),
        P("section", "tensor", None),
        P("section", None, "tensor"),
        P("section", "tensor", None),
    )
    body = per_chip if takes_chips(dict(mesh.shape)) else per_device
    return jax.shard_map(
        body,
        mesh=mesh,
        in_specs=placed,
        out_specs=(
            P("section", "dp", "tensor", None),
            P("section", "dp", "tensor", None),
            P("section", None, ("dp", "tensor")),
            P("section", "dp", None, "tensor"),
            P("section", "tensor", "dp"),
            P("section", "dp", "tensor"),
            P("section", "tensor", "dp"),
        ),
        check_vma=False,
    )
```

```python
import functools
import math

import jax
import jax.numpy as jnp
from jax import lax
from jax.experimental import pallas as pl
from jax.experimental.pallas import tpu as pltpu
from jax.sharding import PartitionSpec as P

HEAD_DIM = 64


NORM_EPSILON = 1e-06
TILE = 128
PAIR_WORK = 1024
MODEL_HALF = 512
QKV = slice(0, 384)
OUT = slice(384, 512)
CHUNK = 32
KERNEL_VMEM = 20 << 20
ROWS_VMEM = 3 << 20


def shifted(block, axis, distance):
    devices = range(lax.axis_size(axis))
    route = [(i - distance, i) for i in devices if i - distance in devices]
    return lax.ppermute(block, axis, route)


def norm_rows(vector, weight_gain):
    return (
        vector
        * lax.rsqrt(jnp.mean(vector * vector, axis=-1, keepdims=True) + NORM_EPSILON)
        * weight_gain
    )


def rotary_tables(seq_len, head_width):
    half_width = head_width // 2
    freqs = 10000.0 ** (-2.0 * jnp.arange(half_width, dtype=jnp.float32) / head_width)
    angles = jnp.arange(seq_len, dtype=jnp.float32)[:, None] * freqs[None, :]
    return (jnp.cos(angles), jnp.sin(angles))


def rotate(vector, cos_table, sin_table):
    first_half, second_half = jnp.split(vector, 2, axis=-1)
    cos_part = cos_table[:, None, :]
    sin_part = sin_table[:, None, :]
    return jnp.concatenate(
        [
            first_half * cos_part - second_half * sin_part,
            second_half * cos_part + first_half * sin_part,
        ],
        axis=-1,
    )


def contract(left_rows, right_rows):
    return lax.dot_general(
        left_rows, right_rows, (((0,), (0,)), ((), ())), preferred_element_type=jnp.float32
    )


def gather_rows(row_values, weight):

    def project(shard_rows, offset):
        return (shard_rows, jnp.dot(shard_rows, weight, preferred_element_type=jnp.float32))

    return project(lax.all_gather(row_values, "tensor", axis=0, tiled=True), jnp.int32(0))


def scatter_rows(row_values, weight, row_count):

    def partial_term(offset, span):
        return jnp.dot(row_values, weight, preferred_element_type=jnp.float32)

    return lax.psum_scatter(
        partial_term(jnp.int32(0), lax.axis_size("tensor") * row_count),
        "tensor",
        scatter_dimension=0,
        tiled=True,
    )


def gather_grads(row_values, weight):

    def project(shard_rows, offset):
        return (shard_rows, jnp.dot(shard_rows, weight.T, preferred_element_type=jnp.float32))

    return project(lax.all_gather(row_values, "tensor", axis=0, tiled=True), jnp.int32(0))


def scatter_grads(row_values, weight, row_count):

    def partial_term(offset, span):
        return jnp.dot(row_values, weight.T, preferred_element_type=jnp.float32)

    return lax.psum_scatter(
        partial_term(jnp.int32(0), lax.axis_size("tensor") * row_count),
        "tensor",
        scatter_dimension=0,
        tiled=True,
    )


def attention_probs(queries, key_rows):
    scores = jnp.einsum(
        "qhd,khd->hqk", queries, key_rows, preferred_element_type=jnp.float32
    ) * HEAD_DIM ** (-0.5)
    length = queries.shape[0]
    positions = jnp.arange(length, dtype=jnp.int32)
    causal = positions[:, None] >= positions[None, :]
    scores = jnp.where(causal[None], scores, -1e30)
    expos = jnp.exp(scores - jnp.max(scores, axis=-1, keepdims=True))
    return expos / jnp.sum(expos, axis=-1, keepdims=True)


def layer_forward(layer_input, weights):
    gains, w_qkv, w_out, w_up, w_down = weights
    row_count, model_width = layer_input.shape
    attn_in = norm_rows(layer_input, gains[0]).astype(jnp.bfloat16)
    gathered_a, qkv = gather_rows(attn_in, w_qkv.reshape(model_width, -1))
    length = qkv.shape[0]
    head_count = w_qkv.shape[2] // HEAD_DIM
    qkv = qkv.reshape(length, 3, head_count, HEAD_DIM)
    cos_table, sin_table = rotary_tables(length, HEAD_DIM)
    queries = rotate(qkv[:, 0], cos_table, sin_table).astype(jnp.bfloat16)
    key_rows = rotate(qkv[:, 1], cos_table, sin_table).astype(jnp.bfloat16)
    values = qkv[:, 2].astype(jnp.bfloat16)
    attn_probs = attention_probs(queries, key_rows).astype(jnp.bfloat16)
    mixed = jnp.einsum("hqk,khd->qhd", attn_probs, values, preferred_element_type=jnp.float32)
    mixed = mixed.reshape(length, -1).astype(jnp.bfloat16)
    attn_branch = scatter_rows(mixed, w_out, row_count)
    hidden = layer_input + norm_rows(attn_branch, gains[1])
    mlp_in = norm_rows(hidden, gains[2]).astype(jnp.bfloat16)
    gathered_c, up_act = gather_rows(mlp_in, w_up)
    gelu_out = jax.nn.gelu(up_act, approximate=True).astype(jnp.bfloat16)
    down_branch = scatter_rows(gelu_out, w_down, row_count)
    result = hidden + norm_rows(down_branch, gains[3])
    kept_values = (
        gathered_a,
        queries,
        key_rows,
        values,
        mixed,
        attn_branch,
        hidden,
        gathered_c,
        up_act,
        gelu_out,
        down_branch,
    )
    return (result, kept_values)


def layer_backward(layer_input, grad_result, kept_values, weights):
    gains, w_qkv, w_out, w_up, w_down = weights
    (
        gathered_a,
        queries,
        key_rows,
        values,
        mixed,
        attn_branch,
        hidden,
        gathered_c,
        up_act,
        gelu_out,
        down_branch,
    ) = kept_values
    row_count, model_width = layer_input.shape
    pullback = jax.vjp(norm_rows, down_branch, gains[3])[1]
    grad_down, gain_three = pullback(grad_result)
    gathered_dd, grad_gelu = gather_grads(grad_down.astype(jnp.bfloat16), w_down)
    down_total = contract(gelu_out, gathered_dd)
    pullback = jax.vjp(lambda vector: jax.nn.gelu(vector, approximate=True), up_act)[1]
    grad_up = pullback(grad_gelu)[0].astype(jnp.bfloat16)
    up_total = contract(gathered_c, grad_up)
    grad_mlp = scatter_grads(grad_up, w_up, row_count)
    pullback = jax.vjp(norm_rows, hidden, gains[2])[1]
    grad_norm_mlp, gain_two = pullback(grad_mlp)
    grad_hidden = grad_result + grad_norm_mlp
    pullback = jax.vjp(norm_rows, attn_branch, gains[1])[1]
    grad_attn, gain_one = pullback(grad_hidden)
    gathered_da, grad_mixed = gather_grads(grad_attn.astype(jnp.bfloat16), w_out)
    out_total = contract(mixed, gathered_da)
    length = grad_mixed.shape[0]
    head_count = w_qkv.shape[2] // HEAD_DIM
    grad_mixed = grad_mixed.astype(jnp.bfloat16).reshape(length, head_count, HEAD_DIM)
    attn_probs = attention_probs(queries, key_rows)
    probs_low = attn_probs.astype(jnp.bfloat16)
    grad_probs = jnp.einsum("qhd,khd->hqk", grad_mixed, values, preferred_element_type=jnp.float32)
    grad_values = jnp.einsum(
        "hqk,qhd->khd", probs_low, grad_mixed, preferred_element_type=jnp.float32
    )
    row_dots = jnp.sum(grad_probs * attn_probs, axis=-1, keepdims=True)
    grad_scores = (attn_probs * (grad_probs - row_dots)).astype(jnp.bfloat16)
    scale_value = HEAD_DIM ** (-0.5)
    grad_queries = (
        jnp.einsum("hqk,khd->qhd", grad_scores, key_rows, preferred_element_type=jnp.float32)
        * scale_value
    )
    grad_keys = (
        jnp.einsum("hqk,qhd->khd", grad_scores, queries, preferred_element_type=jnp.float32)
        * scale_value
    )
    cos_table, sin_table = rotary_tables(length, HEAD_DIM)
    pullback = jax.vjp(lambda vector: rotate(vector, cos_table, sin_table), grad_queries)[1]
    grad_q_raw = pullback(grad_queries)[0]
    grad_k_raw = pullback(grad_keys)[0]
    grad_qkv = (
        jnp.stack([grad_q_raw, grad_k_raw, grad_values], axis=1)
        .reshape(length, -1)
        .astype(jnp.bfloat16)
    )
    qkv_total = contract(gathered_a, grad_qkv).reshape(model_width, 3, -1)
    grad_attn_in = scatter_grads(grad_qkv, w_qkv.reshape(model_width, -1), row_count)
    pullback = jax.vjp(norm_rows, layer_input, gains[0])[1]
    grad_norm_in, gain_zero = pullback(grad_attn_in)
    grad_input = grad_hidden + grad_norm_in
    gain_total = jnp.stack([gain_zero, gain_one, gain_two, gain_three])
    return (grad_input, (gain_total, qkv_total, out_total, up_total, down_total))


def lagged(first_section, stacked):
    blank = jnp.zeros_like(stacked[:1])
    earlier = jnp.concatenate([blank, stacked[:-1]])
    later = jnp.concatenate([stacked[1:], blank])
    return jnp.where(first_section, earlier, later)


def per_device(
    inputs,
    out_cotangent,
    group_ids,
    group_weights,
    gains,
    qkv_weight,
    out_weight,
    up_weight,
    down_weight,
):
    weights = (gains[0], qkv_weight[0], out_weight[0], up_weight[0], down_weight[0])
    micro_count, row_count, model_width = inputs.shape
    first_section = lax.axis_index("section") == 0
    group_count = group_weights.shape[0]
    matches = group_ids[..., None] == jnp.arange(group_count, dtype=jnp.int32)
    row_scale = jnp.sum(jnp.where(matches, group_weights, 0.0), axis=-1)
    scaled = out_cotangent.astype(jnp.float32) * row_scale[..., None]
    padded = jnp.concatenate([inputs, jnp.zeros((1, row_count, model_width), jnp.bfloat16)])

    def forward_tick(received, fresh_input):
        layer_input = jnp.where(first_section, fresh_input, received)
        result, kept_values = layer_forward(layer_input.astype(jnp.float32), weights)
        result_low = result.astype(jnp.bfloat16)
        outgoing = shifted(result_low, "section", 1)
        stashed = ()
        return (outgoing, (layer_input, result_low, stashed))

    start_rows = jnp.zeros((row_count, model_width), jnp.bfloat16)
    _, (layer_inputs, layer_results, stashed) = lax.scan(forward_tick, start_rows, padded)
    layer_outputs = jnp.where(first_section, layer_results[:-1], layer_results[1:])[None]
    back_inputs = lagged(first_section, layer_inputs)
    back_stash = jax.tree.map(lambda stacked: lagged(first_section, stacked), stashed)
    grad_padded = jnp.concatenate([scaled, jnp.zeros((1, row_count, model_width), jnp.float32)])
    tick_index = jnp.arange(micro_count + 1, dtype=jnp.int32)
    tick_valid = jnp.where(first_section, tick_index >= 1, tick_index < micro_count).astype(
        jnp.float32
    )

    def backward_tick(carry, step_item):
        received, totals = carry
        layer_input, cotangent, valid_now, stash_now = step_item
        grad_now = jnp.where(first_section, received.astype(jnp.float32), cotangent)
        input_now = layer_input.astype(jnp.float32)
        kept_values = layer_forward(input_now, weights)[1]
        grad_input, layer_grads = layer_backward(input_now, grad_now, kept_values, weights)
        totals = jax.tree.map(lambda total, update: total + valid_now * update, totals, layer_grads)
        grad_low = grad_input.astype(jnp.bfloat16)
        outgoing = shifted(grad_low, "section", -1)
        return ((outgoing, totals), grad_low)

    start_totals = (
        jnp.zeros((4, model_width), jnp.float32),
        jnp.zeros(qkv_weight.shape[1:], jnp.float32),
        jnp.zeros(out_weight.shape[1:], jnp.float32),
        jnp.zeros(up_weight.shape[1:], jnp.float32),
        jnp.zeros(down_weight.shape[1:], jnp.float32),
    )
    (_, totals), grad_lows = lax.scan(
        backward_tick,
        (start_rows, start_totals),
        (back_inputs, grad_padded, tick_valid, back_stash),
    )
    input_grads = jnp.where(first_section, grad_lows[1:], grad_lows[:-1])[None]
    gain_total, qkv_total, out_total, up_total, down_total = totals
    gains_grad = lax.psum_scatter(gain_total, ("dp", "tensor"), scatter_dimension=1, tiled=True)
    qkv_grad, out_grad, up_grad, down_grad = (
        lax.psum_scatter(
            qkv_total.astype(jnp.bfloat16), "dp", scatter_dimension=0, tiled=True
        ).astype(jnp.float32),
        lax.psum_scatter(
            out_total.astype(jnp.bfloat16), "dp", scatter_dimension=1, tiled=True
        ).astype(jnp.float32),
        lax.psum_scatter(
            up_total.astype(jnp.bfloat16), "dp", scatter_dimension=0, tiled=True
        ).astype(jnp.float32),
        lax.psum_scatter(
            down_total.astype(jnp.bfloat16), "dp", scatter_dimension=1, tiled=True
        ).astype(jnp.float32),
    )
    return (
        layer_outputs,
        input_grads,
        gains_grad[None],
        qkv_grad[None],
        out_grad[None],
        up_grad[None],
        down_grad[None],
    )


def rotated(block, cos_rows, sin_rows):
    lane = lax.broadcasted_iota(jnp.int32, block.shape, 1)
    ahead = pltpu.roll(block, 96, 1)
    behind = pltpu.roll(block, 32, 1)
    swapped = jnp.where(lane % 64 < 32, ahead, behind)
    return block * cos_rows + swapped * sin_rows


def dot_nt(left, right):
    return lax.dot_general(
        left, right, (((1,), (1,)), ((), ())), preferred_element_type=jnp.float32
    )


def dot_nn(left, right):
    return jnp.dot(left, right, preferred_element_type=jnp.float32)


def model_weight(owns, others, cols):
    sides = [jnp.concatenate([ref[:, cols] for ref in refs], axis=1) for refs in (owns, others)]
    return jnp.concatenate(sides, axis=0)


def stacked_up(values):
    return jnp.concatenate(values, axis=0)


def edge_masks(core, rows):
    key = lax.broadcasted_iota(jnp.int32, (rows, 2 * rows), 0)
    query = lax.broadcasted_iota(jnp.int32, (rows, 2 * rows), 1)
    mine = query < rows
    place = jnp.where(mine, query + core * rows, query - rows + (1 - core) * rows)
    return (key + core * rows <= place, key + (1 - core) * rows <= place)


def both_sides(value, half, start, stop, axis=0):
    if axis == 0:
        return jnp.concatenate([value[start:stop], value[half + start : half + stop]], axis=0)
    return jnp.concatenate([value[:, start:stop], value[:, half + start : half + stop]], axis=1)


def hidden_scores(scores, masks, tile, step):
    seen = step * tile
    pieces = []
    for side in range(2):
        base = side * (seen + tile)
        if seen:
            pieces.append(scores[base : base + seen])
        pieces.append(jnp.where(masks[side], scores[base + seen : base + seen + tile], -1e30))
    return jnp.concatenate(pieces, axis=0)


def one_head(rows, head):
    lane = lax.broadcasted_iota(jnp.int32, rows.shape, 1)
    return jnp.where(lane // 64 == head, rows, jnp.zeros_like(rows))


def pick_piece(weight, owns, others, cols):
    for j, (own, other) in enumerate(zip(owns, others)):

        @pl.when(pl.program_id(0) == j)
        def _():
            size = own.shape[0]
            weight[:size] = own[:, cols]
            weight[size:] = other[:, cols]


def attend_kernel(pieces, core_ref, cos_ref, sin_ref, own_rows, other_rows, *refs):
    owns, others = refs[:pieces], refs[pieces : 2 * pieces]
    q_ref, k_ref, v_ref, lse_ref, mix_ref, weight = refs[2 * pieces :]
    half = own_rows.shape[0]
    tile = TILE
    pick_piece(weight, owns, others, QKV)
    proj = dot_nn(stacked_up([own_rows[...], other_rows[...]]), weight[...])
    cos_rows, sin_rows = cos_ref[...], sin_ref[...]
    q = (rotated(proj[:, :128], cos_rows, sin_rows) * HEAD_DIM ** (-0.5)).astype(jnp.bfloat16)
    k = rotated(proj[:, 128:256], cos_rows, sin_rows).astype(jnp.bfloat16)
    v32 = proj[:, 256:]
    q_ref[0] = q
    k_ref[0] = k
    v_ref[0] = v32.astype(jnp.bfloat16)
    v_flip = v32.T.astype(jnp.bfloat16)
    masks = edge_masks(core_ref[0], tile)

    def scored(step, head):
        stop = (step + 1) * tile
        q_head = one_head(both_sides(q, half, step * tile, stop), head)
        return hidden_scores(dot_nt(both_sides(k, half, 0, stop), q_head), masks, tile, step)

    units = [(step, head) for step in range(half // tile) for head in range(2)]
    ahead = scored(*units[0])
    outs = []
    for spot, (step, head) in enumerate(units):
        scores = ahead
        if spot + 1 < len(units):
            ahead = scored(*units[spot + 1])
        stop = (step + 1) * tile
        top = jnp.max(scores, axis=0, keepdims=True)
        expos = jnp.exp(scores - top)
        total = jnp.sum(expos, axis=0, keepdims=True)
        lse = top + jnp.log(total)
        lse_ref[0, head : head + 1, step * tile : stop] = lse[:, :tile]
        lse_ref[0, head : head + 1, half + step * tile : half + stop] = lse[:, tile:]
        v_cols = both_sides(v_flip, half, 0, stop, axis=1)
        out = dot_nn(v_cols[64 * head : 64 * head + 64], expos.astype(jnp.bfloat16))
        outs.append(out * (1.0 / total))
        if head == 1:
            mixed = jnp.concatenate(outs, axis=0).T.astype(jnp.bfloat16)
            outs = []
            mix_ref[step * tile : stop, :] = mixed[:tile]
            mix_ref[half + step * tile : half + stop, :] = mixed[tile:]


def attend_back_kernel(pieces, core_ref, cos_ref, sin_ref, own_rows, other_rows, *refs):
    owns, others = refs[:pieces], refs[pieces : 2 * pieces]
    q_ref, k_ref, v_ref, lse_ref, out_ref, weight, dq, dk, dv = refs[2 * pieces :]
    half = own_rows.shape[0]
    tile = TILE
    pick_piece(weight, owns, others, OUT)
    rows = stacked_up([own_rows[...], other_rows[...]])
    d_mixed = dot_nn(rows, weight[...]).astype(jnp.bfloat16)
    q, k, v = q_ref[0], k_ref[0], v_ref[0]
    k_flip = k.astype(jnp.float32).T.astype(jnp.bfloat16)
    masks = edge_masks(core_ref[0], tile)
    steps = half // tile

    def scored(step, head):
        stop = (step + 1) * tile
        q_head = one_head(both_sides(q, half, step * tile, stop), head)
        g_head = one_head(both_sides(d_mixed, half, step * tile, stop), head)
        scores = hidden_scores(dot_nt(both_sides(k, half, 0, stop), q_head), masks, tile, step)
        return q_head, g_head, scores, dot_nt(both_sides(v, half, 0, stop), g_head)

    units = [(step, head) for step in reversed(range(steps)) for head in range(2)]
    ahead = scored(*units[0])
    dq_flips = []
    dk_sum = dv_sum = None
    for spot, (step, head) in enumerate(units):
        q_head, g_head, scores, d_probs = ahead
        if spot + 1 < len(units):
            ahead = scored(*units[spot + 1])
        stop = (step + 1) * tile
        lse = both_sides(lse_ref[0], half, step * tile, stop, axis=1)
        probs = jnp.exp(scores - lse[head : head + 1])
        dots = jnp.sum(probs * d_probs, axis=0, keepdims=True)
        d_scores = (probs * (d_probs - dots)).astype(jnp.bfloat16)
        dv_part = dot_nn(probs.astype(jnp.bfloat16), g_head)
        dk_part = dot_nn(d_scores, q_head)
        k_cols = both_sides(k_flip, half, 0, stop, axis=1)
        dq_flips.append(dot_nn(k_cols[64 * head : 64 * head + 64], d_scores))
        if head == 0:
            dv_sum, dk_sum = dv_part, dk_part
            continue
        dv_sum, dk_sum = dv_sum + dv_part, dk_sum + dk_part
        dq_rows = jnp.concatenate(dq_flips, axis=0).T * HEAD_DIM ** (-0.5)
        dq_flips = []
        dq[step * tile : stop] = dq_rows[:tile]
        dq[half + step * tile : half + stop] = dq_rows[tile:]
        for base, part in ((0, slice(0, stop)), (half, slice(stop, 2 * stop))):
            if step == steps - 1:
                dk[base : base + stop] = dk_sum[part]
                dv[base : base + stop] = dv_sum[part]
            else:
                dk[base : base + stop] += dk_sum[part]
                dv[base : base + stop] += dv_sum[part]
    cos_rows, sin_rows = cos_ref[...], -sin_ref[...]
    out_ref[:, :128] = rotated(dq[...], cos_rows, sin_rows).astype(jnp.bfloat16)
    out_ref[:, 128:256] = rotated(dk[...], cos_rows, sin_rows).astype(jnp.bfloat16)
    out_ref[:, 256:] = dv[...].astype(jnp.bfloat16)


def split_rows(total, own_ref, other_ref):
    half = own_ref.shape[0]
    own_ref[...] = total[:half]
    other_ref[...] = total[half:].astype(jnp.bfloat16)


def to_model_kernel(lefts, pieces, cols, *refs):
    left, refs = jnp.concatenate([ref[...] for ref in refs[:lefts]], axis=1), refs[lefts:]
    weight = model_weight(refs[:pieces], refs[pieces : 2 * pieces], cols)
    split_rows(dot_nt(left, weight), *refs[2 * pieces :])


def mlp_down_kernel(pieces, left_ref, *refs):
    sides = [stacked_up([ref[...] for ref in side]) for side in (refs[:pieces], refs[pieces:-2])]
    split_rows(dot_nn(left_ref[...], jnp.concatenate(sides, axis=1)), *refs[-2:])


def gelu_both(up_act):
    root = math.sqrt(2.0 / math.pi)
    square = up_act * up_act
    rise = 0.5 + 0.5 * jnp.tanh(up_act * (root + root * 0.044715 * square))
    value = up_act * rise
    slope = rise + value * (1.0 - rise) * (2.0 * root + 6.0 * root * 0.044715 * square)
    return value, slope


def mlp_up_kernel(pieces, own_rows, other_rows, *refs):
    owns, others = refs[:pieces], refs[pieces : 2 * pieces]
    gelu_ref, slope_ref = refs[2 * pieces :]
    half = own_rows.shape[0]
    size = owns[0].shape[1]
    step = half // 2
    units = [(j, i) for j in range(pieces) for i in range(4)]

    def product(j, i):
        rows = (own_rows, other_rows)[i // 2][i % 2 * step : (i % 2 + 1) * step]
        return dot_nn(rows, stacked_up([owns[j][...], others[j][...]]))

    ahead = product(*units[0])
    for spot, (j, i) in enumerate(units):
        up_act = ahead
        if spot + 1 < len(units):
            ahead = product(*units[spot + 1])
        value, slope = gelu_both(up_act)
        gelu_ref[i * step : (i + 1) * step, j * size : (j + 1) * size] = value.astype(jnp.bfloat16)
        slope_ref[i * step : (i + 1) * step, j * size : (j + 1) * size] = slope.astype(
            jnp.bfloat16
        )


def mlp_up_back_kernel(pieces, own_rows, other_rows, slope_ref, *refs):
    owns, others = refs[:pieces], refs[pieces : 2 * pieces]
    out_ref = refs[-1]
    size = owns[0].shape[0]
    rows = stacked_up([own_rows[...], other_rows[...]])
    for j in range(pieces):
        cols = slice(j * size, (j + 1) * size)
        weight = jnp.concatenate([owns[j][...], others[j][...]], axis=1)
        d_gelu = dot_nt(rows, weight)
        out_ref[:, cols] = (d_gelu * slope_ref[:, cols].astype(jnp.float32)).astype(jnp.bfloat16)


def inverse_size(rows):
    return lax.rsqrt(jnp.mean(rows * rows, axis=-1, keepdims=True) + NORM_EPSILON)


def norm_back(rows, gain, grad):
    scale = inverse_size(rows)
    weighted = grad * gain
    inner = jnp.mean(rows * weighted, axis=-1, keepdims=True)
    return scale * weighted - rows * (scale * scale * scale * inner), rows * scale * grad


def folded(rows):
    return jnp.sum(rows.reshape(rows.shape[0] // 8, 8, rows.shape[1]), axis=0)


def wide(ref, spot):
    return ref[spot, :].astype(jnp.float32)


def by_chunks(count, body, sums=0, width=0):
    def one(i, carry):
        more = body(pl.ds(pl.multiple_of(i * CHUNK, CHUNK), CHUNK))
        return tuple(old + folded(new) for old, new in zip(carry, more))

    start = tuple(jnp.zeros((8, width), jnp.float32) for _ in range(sums))
    totals = lax.fori_loop(0, count // CHUNK, one, start)
    return [jnp.sum(total, axis=0, keepdims=True) for total in totals]


def norm_in_kernel(gain_ref, rows_ref, out_ref):
    def body(spot):
        rows = wide(rows_ref, spot)
        out_ref[spot, :] = (rows * inverse_size(rows) * gain_ref[0:1]).astype(jnp.bfloat16)
        return ()

    by_chunks(rows_ref.shape[0], body)


def after_attention_kernel(
    gain_ref, rows_ref, own_ref, other_ref, branch_ref, hidden_ref, out_ref
):
    def body(spot):
        branch = own_ref[spot, :] + wide(other_ref, spot)
        hidden = wide(rows_ref, spot) + branch * inverse_size(branch) * gain_ref[1:2]
        branch_ref[spot, :] = branch
        hidden_ref[spot, :] = hidden
        out_ref[spot, :] = (hidden * inverse_size(hidden) * gain_ref[2:3]).astype(jnp.bfloat16)
        return ()

    by_chunks(rows_ref.shape[0], body)


def after_mlp_kernel(gain_ref, hidden_ref, own_ref, other_ref, branch_ref, out_ref):
    def body(spot):
        branch = own_ref[spot, :] + wide(other_ref, spot)
        branch_ref[spot, :] = branch
        result = hidden_ref[spot, :] + branch * inverse_size(branch) * gain_ref[3:4]
        out_ref[spot, :] = result.astype(jnp.bfloat16)
        return ()

    by_chunks(hidden_ref.shape[0], body)


def into_mlp_back_kernel(gain_ref, grad_ref, branch_ref, out_ref, sum_ref):
    def body(spot):
        d_rows, d_gain = norm_back(branch_ref[spot, :], gain_ref[3:4], wide(grad_ref, spot))
        out_ref[spot, :] = d_rows.astype(jnp.bfloat16)
        return (d_gain,)

    (sum_ref[...],) = by_chunks(grad_ref.shape[0], body, 1, grad_ref.shape[1])


def into_attention_back_kernel(
    gain_ref, grad_ref, own_ref, other_ref, hidden_ref, branch_ref, d_hidden_ref, out_ref, *sums
):
    def body(spot):
        d_rows = own_ref[spot, :] + wide(other_ref, spot)
        d_rows, d_gain = norm_back(hidden_ref[spot, :], gain_ref[2:3], d_rows)
        d_hidden = wide(grad_ref, spot) + d_rows
        d_hidden_ref[spot, :] = d_hidden
        d_rows, d_first = norm_back(branch_ref[spot, :], gain_ref[1:2], d_hidden)
        out_ref[spot, :] = d_rows.astype(jnp.bfloat16)
        return (d_first, d_gain)

    totals = by_chunks(grad_ref.shape[0], body, 2, grad_ref.shape[1])
    sums[0][...], sums[1][...] = totals


def out_of_layer_kernel(gain_ref, rows_ref, own_ref, other_ref, d_hidden_ref, out_ref, sum_ref):
    def body(spot):
        d_rows = own_ref[spot, :] + wide(other_ref, spot)
        d_rows, d_gain = norm_back(wide(rows_ref, spot), gain_ref[0:1], d_rows)
        out_ref[spot, :] = (d_hidden_ref[spot, :] + d_rows).astype(jnp.bfloat16)
        return (d_gain,)

    (sum_ref[...],) = by_chunks(rows_ref.shape[0], body, 1, rows_ref.shape[1])


def work(flops, arrays):
    size = sum(math.prod(array.shape) * jnp.dtype(array.dtype).itemsize for array in arrays)
    return pl.CostEstimate(flops=flops, bytes_accessed=size, transcendentals=0)


def without(kernel, first, count):
    return lambda *refs: kernel(*refs[:first], *refs[first + count :])


def on_chip(kernel, name, outs, *operands, limit=ROWS_VMEM, flops=0, waits=()):
    shapes = [jax.ShapeDtypeStruct(shape, dtype) for shape, dtype in outs]
    space = pl.BlockSpec(memory_space=pltpu.VMEM)
    return pl.pallas_call(
        without(kernel, len(operands), len(waits)),
        in_specs=[space] * len(operands) + [pl.BlockSpec(memory_space=pl.ANY)] * len(waits),
        out_specs=[space] * len(outs),
        out_shape=shapes,
        compiler_params=pltpu.CompilerParams(vmem_limit_bytes=limit),
        cost_estimate=work(flops, (*operands, *shapes)),
        name=name,
    )(*operands, *waits)


def whole_block(array):
    return pl.BlockSpec(array.shape, lambda j: (0,) * array.ndim)


def by_pairs(kernel, name, core, operands, pieces, blocks, outs, scratch, flops, waits):
    shapes = [jax.ShapeDtypeStruct(shape, dtype) for shape, dtype, _ in outs]
    taken = 1 + len(operands) + 2 * len(pieces[0]) + len(blocks)
    return pl.pallas_call(
        without(functools.partial(kernel, len(pieces[0])), taken, len(waits)),
        grid=(len(pieces[0]),),
        in_specs=[pl.BlockSpec(memory_space=pltpu.SMEM)]
        + [whole_block(array) for array in (*operands, *pieces[0], *pieces[1])]
        + [spec for _, spec in blocks]
        + [pl.BlockSpec(memory_space=pl.ANY)] * len(waits),
        out_specs=[spec for _, _, spec in outs],
        out_shape=shapes,
        scratch_shapes=scratch,
        compiler_params=pltpu.CompilerParams(vmem_limit_bytes=KERNEL_VMEM),
        cost_estimate=work(flops, (*operands, *pieces[0], *pieces[1], *shapes)),
        name=name,
    )(core, *operands, *pieces[0], *pieces[1], *[array for array, _ in blocks], *waits)


def attend(core, tables, rows, pieces, waits):
    half, features = rows[0].shape
    length, count = 2 * half, len(pieces[0])
    lanes = ((count, length, 128), jnp.bfloat16, pl.BlockSpec((1, length, 128), lambda j: (j, 0, 0)))
    lse = ((count, 2, length), jnp.float32, pl.BlockSpec((1, 2, length), lambda j: (j, 0, 0)))
    mixed = ((length, count * 128), jnp.bfloat16, pl.BlockSpec((length, 128), lambda j: (0, j)))
    return by_pairs(
        attend_kernel,
        "attend",
        core,
        (*tables, *rows),
        pieces,
        (),
        (lanes, lanes, lanes, lse, mixed),
        [pltpu.VMEM((features, 384), jnp.bfloat16)],
        count * length * (2 * features * 384 + 2 * PAIR_WORK * length),
        waits,
    )


def attend_back(core, tables, rows, pieces, base, waits, q, k, v, lse):
    half, features = rows[0].shape
    length, count = 2 * half, len(pieces[0])
    lanes = pl.BlockSpec((1, length, 128), lambda j: (base + j, 0, 0))
    lse_spec = pl.BlockSpec((1, 2, length), lambda j: (base + j, 0, 0))
    out = ((length, count * 384), jnp.bfloat16, pl.BlockSpec((length, 384), lambda j: (0, j)))
    return by_pairs(
        attend_back_kernel,
        "attend_back",
        core,
        (*tables, *rows),
        pieces,
        ((q, lanes), (k, lanes), (v, lanes), (lse, lse_spec)),
        (out,),
        [pltpu.VMEM((features, 128), jnp.bfloat16)] + [pltpu.VMEM((length, 128), jnp.float32)] * 3,
        count * length * (2 * features * 128 + 5 * PAIR_WORK * length),
        waits,
    )[0]


def exchanged(parts):
    return parts[0], flip_pairs(parts[1], 1)


def model_rows(kernel, name, lefts, pieces, waits=()):
    length, width = lefts[0].shape[0], 2 * MODEL_HALF
    outs = (((length // 2, width), jnp.float32), ((length // 2, width), jnp.bfloat16))
    hidden = sum(left.shape[1] for left in lefts)
    more = {"limit": KERNEL_VMEM, "flops": 2 * length * width * hidden, "waits": waits}
    return exchanged(on_chip(kernel, name, outs, *lefts, *pieces[0], *pieces[1], **more))


def flip_pairs(block, distance):
    size = lax.axis_size("dp")
    return lax.ppermute(block, "dp", [(i, i ^ distance) for i in range(size)])


def passed_on(block, step):
    size = lax.axis_size("tensor")
    return lax.ppermute(block, "tensor", [(i, (i + step) % size) for i in range(size)])


def dot_tn(left, right):
    return lax.dot_general(
        left, right, (((0,), (0,)), ((), ())), preferred_element_type=jnp.float32
    )


def fetch(first_ref, zeros, ones, buffers, sems):
    for section, sources in enumerate((zeros, ones)):

        @pl.when(first_ref[0] == section)
        def _():
            copies = [
                pltpu.make_async_copy(source, buffer, sems.at[i])
                for i, (source, buffer) in enumerate(zip(sources, buffers))
            ]
            for copy in copies:
                copy.start()
            for copy in copies:
                copy.wait()


def mlp_grads_kernel(base, section_ref, *refs):
    (own_one, other_one, own_two, other_two), (rows, d_up, gelu, d_down, sems) = refs[12:16], refs[16:]
    half, size = own_one.shape[0] // 2, own_one.shape[1]
    cols = pl.ds(base * size, 2 * size)

    def parts(own_rows, other_rows, d_up_ref, gelu_ref, own_grad, other_grad):
        whole = (d_up_ref.at[:, cols], gelu_ref.at[:, cols])
        return (own_rows, other_rows, *whole, own_grad, other_grad)

    count = refs[0].shape[0]
    buffers = (
        rows.at[pl.ds(0, count)],
        rows.at[pl.ds(count, count)],
        d_up,
        gelu,
        d_down.at[pl.ds(0, count)],
        d_down.at[pl.ds(count, count)],
    )
    fetch(section_ref, parts(*refs[:6]), parts(*refs[6:12]), buffers, sems)
    for j, own, other in ((1, own_two, other_two), (0, own_one, other_one)):
        cols = slice(j * size, (j + 1) * size)
        up = dot_tn(rows[...], d_up[:, cols])
        own[:half] = up[:half]
        other[:half] = up[half:].astype(jnp.bfloat16)
        down = dot_tn(gelu[:, cols], d_down[...])
        own[half:] = down[:, :half]
        other[half:] = down[:, half:].astype(jnp.bfloat16)


def attn_grads_kernel(base, section_ref, *refs):
    (own_one, other_one, own_two, other_two), (rows, d_qkv, mixed, d_attn, sems) = refs[12:16], refs[16:]
    half, size = own_one.shape[0], d_qkv.shape[1] // 2
    count = refs[0].shape[0]
    cols = pl.ds(base * 128, 256)

    def parts(own_rows, other_rows, d_qkv_ref, mixed_ref, own_grad, other_grad):
        return (own_rows, other_rows, d_qkv_ref, mixed_ref.at[:, cols], own_grad, other_grad)

    buffers = (
        rows.at[pl.ds(0, count)],
        rows.at[pl.ds(count, count)],
        d_qkv,
        mixed,
        d_attn.at[pl.ds(0, count)],
        d_attn.at[pl.ds(count, count)],
    )
    fetch(section_ref, parts(*refs[:6]), parts(*refs[6:12]), buffers, sems)
    for j, own, other in ((1, own_two, other_two), (0, own_one, other_one)):
        qkv = dot_tn(rows[...], d_qkv[:, j * size : (j + 1) * size])
        out = dot_tn(d_attn[...], mixed[:, j * 128 : (j + 1) * 128])
        own[:, :size] = qkv[:half]
        own[:, size:] = out[:half]
        other[:, :size] = qkv[half:].astype(jnp.bfloat16)
        other[:, size:] = out[half:].astype(jnp.bfloat16)


def weight_grads(kernel, name, base, section, zeros, ones, shape, columns, waits=()):
    length = 2 * zeros[0].shape[0]
    width = zeros[0].shape[1]
    every = pl.BlockSpec(memory_space=pl.ANY)
    space = pl.BlockSpec(memory_space=pltpu.VMEM)
    arrays = (*zeros, *ones)
    first, second, third, fourth = pl.pallas_call(
        without(functools.partial(kernel, base), 1 + len(arrays), len(waits)),
        in_specs=[pl.BlockSpec(memory_space=pltpu.SMEM)] + [every] * (len(arrays) + len(waits)),
        out_specs=[space] * 4,
        out_shape=[
            jax.ShapeDtypeStruct(shape, jnp.float32),
            jax.ShapeDtypeStruct(shape, jnp.bfloat16),
        ]
        * 2,
        scratch_shapes=[
            pltpu.VMEM((length, width), jnp.bfloat16),
            pltpu.VMEM((length, columns[0]), jnp.bfloat16),
            pltpu.VMEM((length, columns[1]), jnp.bfloat16),
            pltpu.VMEM((length, width), jnp.bfloat16),
            pltpu.SemaphoreType.DMA((6,)),
        ],
        compiler_params=pltpu.CompilerParams(vmem_limit_bytes=KERNEL_VMEM),
        name=name,
    )(section, *arrays, *waits)
    return [(first, flip_pairs(second, 2)), (third, flip_pairs(fourth, 2))]


def gate_kernel(up_ref, down_ref, up_out, down_out):
    up_out[...] = up_ref[...]
    down_out[...] = down_ref[...]


def mlp_sum_kernel(core_ref, own_ref, other_ref, moved_ref, up_keep, down_keep, up_send, down_send):
    half = own_ref.shape[0] // 2
    size = up_keep.shape[0]

    def total(rows, cols):
        more = other_ref[rows, cols].astype(jnp.float32) + moved_ref[rows, cols].astype(jnp.float32)
        return own_ref[rows, cols] + more

    for core in range(2):

        @pl.when(core_ref[0] == core)
        def _():
            for place, up, down in ((core, up_keep, down_keep), (1 - core, up_send, down_send)):
                spot = slice(place * size, (place + 1) * size)
                up[...] = total(spot, slice(None))
                down[...] = total(slice(half, None), spot)


def mlp_join_kernel(core_ref, up_keep, down_keep, up_sent, down_sent, up_out, down_out):
    size = up_keep.shape[1]
    for core in range(2):

        @pl.when(core_ref[0] == core)
        def _():
            places = ((core, up_keep, down_keep), (1 - core, up_sent, down_sent))
            for place, up, down in places:
                spot = slice(place * size, (place + 1) * size)
                up_out[:, spot] = up[...]
                down_out[spot] = down[...]


def pick_kernel(core_ref, rows_ref, keep_ref, send_ref):
    count = keep_ref.shape[0]
    keep_ref[...] = rows_ref[pl.ds(core_ref[0] * count, count)]
    send_ref[...] = rows_ref[pl.ds((1 - core_ref[0]) * count, count)]


def in_order_kernel(core_ref, keep_ref, sent_ref, out_ref):
    out_ref[:, pl.ds(core_ref[0], 1)] = keep_ref[...][:, None]
    out_ref[:, pl.ds(1 - core_ref[0], 1)] = sent_ref[...][:, None]


def with_core(kernel, name, core, outs, *operands, waits=()):
    space = pl.BlockSpec(memory_space=pltpu.VMEM)
    return pl.pallas_call(
        without(kernel, 1 + len(operands), len(waits)),
        in_specs=[pl.BlockSpec(memory_space=pltpu.SMEM)]
        + [space] * len(operands)
        + [pl.BlockSpec(memory_space=pl.ANY)] * len(waits),
        out_specs=[space] * len(outs),
        out_shape=[jax.ShapeDtypeStruct(shape, dtype) for shape, dtype in outs],
        compiler_params=pltpu.CompilerParams(vmem_limit_bytes=ROWS_VMEM),
        name=name,
    )(core, *operands, *waits)


def last_sum_kernel(core_ref, own_ref, other_ref, moved_ref, keep_ref, send_ref):
    rows = keep_ref.shape[0]

    def total(block):
        spot = pl.ds(pl.multiple_of(block * rows, rows), rows)
        return own_ref[spot, :] + wide(other_ref, spot) + wide(moved_ref, spot)

    keep_ref[...] = total(core_ref[0])
    send_ref[...] = total(1 - core_ref[0])


def joined_kernel(spots, core_ref, keep_ref, sent_ref, column_ref, row_ref):
    size = row_ref.shape[0] // 2
    for core in range(2):

        @pl.when(core_ref[0] == core)
        def _():
            for place, source in ((core, keep_ref), (1 - core, sent_ref)):
                for start, stop, to in spots:
                    step = stop - start
                    column_ref[:, to + place * step : to + (place + 1) * step] = source[:, start:stop]
                row_ref[place * size : (place + 1) * size] = source[:, spots[-1][1] :].T


def per_chip(
    inputs,
    out_cotangent,
    group_ids,
    group_weights,
    gains,
    qkv_weight,
    out_weight,
    up_weight,
    down_weight,
):
    micro, row_count, width = inputs.shape
    tensor = lax.axis_size("tensor")
    part = row_count // 2
    wide_half = width // 2
    length = tensor * row_count
    half = length // 2
    first = lax.axis_index("section") == 0
    place = lax.axis_index("dp")
    core = place % 2
    upper = place // 2 % 2
    core_zero = core == 0
    low_half = upper == 0

    def ordered(mine, other):
        return jnp.where(core_zero, mine, other), jnp.where(core_zero, other, mine)

    def own_first(values):
        return jnp.where(low_half, values, jnp.roll(values, wide_half, axis=-1))

    def both_rows(own):
        return own, flip_pairs(own, 1)

    def to_chip(block):
        split = block.reshape((micro, 2, part) + block.shape[2:])
        mine = lax.dynamic_index_in_dim(split, core, 1, keepdims=False)
        other = lax.dynamic_index_in_dim(split, 1 - core, 1, keepdims=False)
        return lax.all_to_all(
            jnp.concatenate(ordered(mine, flip_pairs(other, 1))), "tensor", 0, 0, tiled=True
        )

    def from_chip(spread_out, waits=()):
        piece = ((micro, part, width), jnp.bfloat16)
        keep, send = with_core(
            pick_kernel, "pick", core_word, (piece, piece), spread_out, waits=waits
        )
        outs = (((micro, 2, part, width), jnp.bfloat16),)
        (rows,) = with_core(
            in_order_kernel, "in_order", core_word, outs, keep, flip_pairs(send, 1)
        )
        return rows.reshape(micro, row_count, width)

    def columns(local):
        size = local.shape[-1] // 2
        mid = (0,) * (local.ndim - 2)
        piece = lax.dynamic_slice(
            local,
            (wide_half * upper, *mid, size * core),
            (wide_half, *local.shape[1:-1], size),
        )
        return piece.reshape(wide_half, -1)

    def rows(local):
        size = local.shape[0] // 2
        return lax.dynamic_slice(local, (size * core, wide_half * upper), (size, wide_half))

    core_word = core.astype(jnp.int32).reshape(1)
    attn_piece = jnp.concatenate([columns(qkv_weight[0]), rows(out_weight[0]).T], axis=1)

    def spread(piece):
        pieces = [piece]
        for _ in range(tensor - 1):
            pieces.append(passed_on(pieces[-1], 1))
        return pieces

    attn_own = spread(attn_piece)
    attn_other = [flip_pairs(piece, 2) for piece in attn_own]
    up_piece, down_piece = columns(up_weight[0]), rows(down_weight[0])
    outs = tuple((piece.shape, piece.dtype) for piece in (up_piece, down_piece))
    up_piece, down_piece = on_chip(
        gate_kernel, "gate", outs, up_piece, down_piece, waits=(attn_own[2],)
    )
    up_own, down_own = spread(up_piece), spread(down_piece)
    up_other = [flip_pairs(piece, 2) for piece in up_own]
    down_other = [flip_pairs(piece, 2) for piece in down_own]
    w_attn, w_up, w_down = (attn_own, attn_other), (up_own, up_other), (down_own, down_other)
    unit = up_piece.shape[1]
    units = tensor * unit

    group_count = group_weights.shape[0]
    matches = group_ids[..., None] == jnp.arange(group_count, dtype=jnp.int32)
    row_scale = jnp.sum(jnp.where(matches, group_weights, 0.0), axis=-1)
    weighted = (out_cotangent.astype(jnp.float32) * row_scale[..., None]).astype(jnp.bfloat16)
    start = to_chip(own_first(jnp.where(first, inputs, weighted))).reshape(half, width)
    gain = own_first(gains[0])

    turns = jnp.arange(half, dtype=jnp.int32)
    turns = turns // part * row_count + turns % part
    positions = jnp.concatenate([turns + core * part, turns + (1 - core) * part])
    freqs = 10000.0 ** (-2.0 * jnp.arange(HEAD_DIM // 2, dtype=jnp.float32) / HEAD_DIM)
    angles = positions.astype(jnp.float32)[:, None] * freqs[None, :]
    cos_part, sin_part = jnp.cos(angles), jnp.sin(angles)
    tables = (
        jnp.concatenate([cos_part] * 4, axis=1),
        jnp.concatenate([-sin_part, sin_part] * 2, axis=1),
    )
    row32, row16 = ((half, width), jnp.float32), ((half, width), jnp.bfloat16)
    unit16 = ((length, units), jnp.bfloat16)
    sum32 = ((1, width), jnp.float32)
    mlp_cost = {"limit": KERNEL_VMEM, "flops": 2 * length * width * units}
    every = slice(None)

    def model_kernel(cols, lefts=1):
        return functools.partial(to_model_kernel, lefts, tensor, cols)

    down_kernel = functools.partial(mlp_down_kernel, tensor)

    def forward(layer_input, waits):
        attn_in = both_rows(
            on_chip(norm_in_kernel, "norm_in", (row16,), gain, layer_input, waits=waits[0])[0]
        )
        *heads, mixed = attend(core_word, tables, attn_in, w_attn, waits[1])
        parts = model_rows(model_kernel(OUT), "attn_out", [mixed], w_attn, waits[2])
        operands = (gain, layer_input, *parts)
        branch, hidden, mlp_in = on_chip(
            after_attention_kernel, "after_attn", (row32, row32, row16), *operands, waits=waits[3]
        )
        mlp_in = both_rows(mlp_in)
        kernel = functools.partial(mlp_up_kernel, tensor)
        operands = (*mlp_in, *w_up[0], *w_up[1])
        gelu_out, slope = on_chip(kernel, "mlp_up", (unit16, unit16), *operands, **mlp_cost)
        parts = model_rows(down_kernel, "mlp_down", [gelu_out], w_down)
        mlp_branch, result = on_chip(
            after_mlp_kernel, "after_mlp", (row32, row16), gain, hidden, *parts
        )
        saved = (layer_input, heads, branch, hidden, slope, mlp_branch)
        return result, saved, (attn_in, mixed, mlp_in, gelu_out)

    def backward(grad, saved, hook, late=()):
        layer_input, heads, branch, hidden, slope, mlp_branch = saved
        operands = (gain, grad, mlp_branch)
        d_down, sum_three = on_chip(
            into_mlp_back_kernel, "into_mlp_back", (row16, sum32), *operands
        )
        d_down = both_rows(d_down)
        kernel = functools.partial(mlp_up_back_kernel, tensor)
        operands = (*d_down, slope, *w_down[0], *w_down[1])
        (d_up,) = on_chip(kernel, "mlp_up_back", (unit16,), *operands, **mlp_cost, waits=late)
        waits = hook(d_down, d_up)
        parts = model_rows(model_kernel(every), "mlp_back", [d_up], w_up, waits)
        waits = hook()
        operands = (gain, grad, *parts, hidden, branch)
        outs = (row32, row16, sum32, sum32)
        d_hidden, d_attn, sum_one, sum_two = on_chip(
            into_attention_back_kernel, "into_attn_back", outs, *operands, waits=waits
        )
        d_attn = both_rows(d_attn)
        waits = hook(d_attn)
        d_qkv = []
        for base in reversed(range(0, tensor, 2)):
            some = [side[base : base + 2] for side in w_attn]
            now = attend_back(core_word, tables, d_attn, some, base, waits, *heads)
            d_qkv.insert(0, now)
            waits = hook(now)
        parts = model_rows(model_kernel(QKV, 2), "attn_back", d_qkv, w_attn, waits)
        operands = (gain, layer_input, *parts, d_hidden)
        d_input, sum_zero = on_chip(
            out_of_layer_kernel, "out_of_layer", (row16, sum32), *operands, waits=hook()
        )
        sums = jnp.concatenate([sum_zero, sum_one, sum_two, sum_three])
        return d_input, (d_qkv, d_attn, d_up, d_down), sums

    low_zero, saved_zero, lefts_zero = forward(
        start,
        (
            (up_piece,),
            (up_own[1], down_own[1]),
            (up_own[2], down_own[2], up_other[0], down_other[0]),
            (up_own[3], down_own[3], up_other[1], down_other[1]),
        ),
    )
    low_one, saved_one, lefts_one = forward(shifted(low_zero, "section", 1), ((),) * 4)
    grad_one, rights_one, gain_one = backward(start, saved_one, lambda *new: ())
    received = shifted(grad_one, "section", -1)

    lows = lax.optimization_barrier((low_zero, low_one, grad_one))[:2]
    lows = own_first(jnp.where(first, *lows)).reshape(tensor, part, width)
    lows = lax.all_to_all(lows, "tensor", 0, 0, tiled=True)

    section_word = lax.axis_index("section").astype(jnp.int32).reshape(1)

    def mlp_leaves(base):
        zeros = (*lefts_zero[2], d_up, lefts_zero[3], *d_down)
        ones = (*lefts_one[2], rights_one[2], lefts_one[3], *rights_one[3])
        mlp_sums[base : base + 2] = weight_grads(
            mlp_grads_kernel,
            "mlp_grads",
            base,
            section_word,
            zeros,
            ones,
            (wide_half + unit, unit),
            (2 * unit, 2 * unit),
        )

    def attn_leaves(base, d_qkv):
        zeros = (*lefts_zero[0], d_qkv, lefts_zero[1], *d_attn)
        ones = (*lefts_one[0], rights_one[0][base // 2], lefts_one[1], *rights_one[1])
        attn_sums[base : base + 2] = weight_grads(
            attn_grads_kernel,
            "attn_grads",
            base,
            section_word,
            zeros,
            ones,
            (wide_half, 512),
            (768, 256),
        )

    def moves_on(piece, moved=None):
        own, other = piece
        total = own + other.astype(jnp.float32)
        if moved is not None:
            total = total + moved.astype(jnp.float32)
        return passed_on(total.astype(jnp.bfloat16), -1)

    mlp_sums, attn_sums = [None] * tensor, [None] * tensor
    mlp_moves, attn_moves = [None] * tensor, [None] * tensor
    hooks = iter(range(6))

    def hook(*new):
        nonlocal d_down, d_up, d_attn
        turn = next(hooks)
        if turn == 0:
            d_down, d_up = new
            mlp_leaves(2)
            return (mlp_sums[3][0],)
        if turn == 1:
            mlp_leaves(0)
            return (mlp_sums[1][0],)
        if turn == 2:
            (d_attn,) = new
            return (mlp_sums[3][1],)
        if turn == 3:
            mlp_moves[3] = moves_on(mlp_sums[3])
            attn_leaves(2, new[0])
            return (mlp_sums[2][1], mlp_moves[3], attn_sums[3][0])
        if turn == 4:
            mlp_moves[2] = moves_on(mlp_sums[2], mlp_moves[3])
            attn_leaves(0, new[0])
            return (mlp_sums[1][1], mlp_moves[2], attn_sums[1][0])
        mlp_moves[1] = moves_on(mlp_sums[1], mlp_moves[2])
        return (mlp_sums[0][1], mlp_moves[1])

    d_down = d_up = d_attn = None
    grad_zero, rights_zero, gain_zero = backward(received, saved_zero, hook, (lows,))
    attn_moves[3] = moves_on(attn_sums[3])
    attn_moves[2] = moves_on(attn_sums[2], attn_moves[3])
    attn_moves[1] = moves_on(attn_sums[1], attn_moves[2])
    outputs = from_chip(lows, (grad_zero,))
    grads = own_first(jnp.where(first, grad_zero, grad_one)).reshape(tensor, part, width)
    grads = from_chip(lax.all_to_all(grads, "tensor", 0, 0, tiled=True))

    block32 = ((wide_half // 2, unit), jnp.float32)
    down32 = ((unit, wide_half // 2), jnp.float32)
    up_keep, down_keep, up_send, down_send = with_core(
        mlp_sum_kernel,
        "mlp_sum",
        core_word,
        (block32, down32, block32, down32),
        *mlp_sums[0],
        mlp_moves[1],
    )
    outs = (
        ((wide_half // 2, 2 * unit), jnp.float32),
        ((2 * unit, wide_half // 2), jnp.float32),
    )
    sent = flip_pairs(up_send, 1), flip_pairs(down_send, 1)
    up_grad, down_grad = with_core(
        mlp_join_kernel, "mlp_join", core_word, outs, up_keep, down_keep, *sent
    )
    outs = (((wide_half // 2, 512), jnp.float32),) * 2
    keep, send = with_core(
        last_sum_kernel, "attn_sum", core_word, outs, *attn_sums[0], attn_moves[1]
    )
    spots = tuple((i * 128, (i + 1) * 128, i * 256) for i in range(3))
    outs = (((wide_half // 2, 768), jnp.float32), ((256, wide_half // 2), jnp.float32))
    kernel = functools.partial(joined_kernel, spots)
    qkv_grad, out_grad = with_core(
        kernel, "attn_join", core_word, outs, keep, flip_pairs(send, 1)
    )
    qkv_grad = qkv_grad.reshape(wide_half // 2, 3, -1)

    gain_total = own_first(jnp.where(first, gain_zero, gain_one))
    count = tensor * lax.axis_size("dp")
    gain_parts = gain_total.reshape(4, count, width // count).swapaxes(0, 1)
    gain_parts = lax.all_to_all(gain_parts, ("dp", "tensor"), 0, 0, tiled=True)
    gains_grad = jnp.sum(gain_parts, axis=0)
    return (
        outputs[None],
        grads[None],
        gains_grad[None],
        qkv_grad[None],
        out_grad[None],
        up_grad[None],
        down_grad[None],
    )


def takes_chips(sizes):
    return sizes["section"] == 2 and sizes["dp"] == 4 and sizes["tensor"] == 4


def solution(mesh):
    placed = (
        P("dp", "tensor", None),
        P("dp", "tensor", None),
        P("dp", "tensor"),
        P(),
        P("section", None, None),
        P("section", None, None, "tensor"),
        P("section", "tensor", None),
        P("section", None, "tensor"),
        P("section", "tensor", None),
    )
    body = per_chip if takes_chips(dict(mesh.shape)) else per_device
    return jax.shard_map(
        body,
        mesh=mesh,
        in_specs=placed,
        out_specs=(
            P("section", "dp", "tensor", None),
            P("section", "dp", "tensor", None),
            P("section", None, ("dp", "tensor")),
            P("section", "dp", None, "tensor"),
            P("section", "tensor", "dp"),
            P("section", "dp", "tensor"),
            P("section", "tensor", "dp"),
        ),
        check_vma=False,
    )
```

```python
import functools
import math

import jax
import jax.numpy as jnp
from jax import lax
from jax.experimental import pallas as pl
from jax.experimental.pallas import tpu as pltpu
from jax.sharding import PartitionSpec as P

HEAD_DIM = 64


NORM_EPSILON = 1e-06
TILE = 128
PAIR_WORK = 1024
MODEL_HALF = 512
QKV = slice(0, 384)
OUT = slice(384, 512)
CHUNK = 32
KERNEL_VMEM = 20 << 20
ROWS_VMEM = 3 << 20


def shifted(block, axis, distance):
    devices = range(lax.axis_size(axis))
    route = [(i - distance, i) for i in devices if i - distance in devices]
    return lax.ppermute(block, axis, route)


def norm_rows(vector, weight_gain):
    return (
        vector
        * lax.rsqrt(jnp.mean(vector * vector, axis=-1, keepdims=True) + NORM_EPSILON)
        * weight_gain
    )


def rotary_tables(seq_len, head_width):
    half_width = head_width // 2
    freqs = 10000.0 ** (-2.0 * jnp.arange(half_width, dtype=jnp.float32) / head_width)
    angles = jnp.arange(seq_len, dtype=jnp.float32)[:, None] * freqs[None, :]
    return (jnp.cos(angles), jnp.sin(angles))


def rotate(vector, cos_table, sin_table):
    first_half, second_half = jnp.split(vector, 2, axis=-1)
    cos_part = cos_table[:, None, :]
    sin_part = sin_table[:, None, :]
    return jnp.concatenate(
        [
            first_half * cos_part - second_half * sin_part,
            second_half * cos_part + first_half * sin_part,
        ],
        axis=-1,
    )


def contract(left_rows, right_rows):
    return lax.dot_general(
        left_rows, right_rows, (((0,), (0,)), ((), ())), preferred_element_type=jnp.float32
    )


def gather_rows(row_values, weight):

    def project(shard_rows, offset):
        return (shard_rows, jnp.dot(shard_rows, weight, preferred_element_type=jnp.float32))

    return project(lax.all_gather(row_values, "tensor", axis=0, tiled=True), jnp.int32(0))


def scatter_rows(row_values, weight, row_count):

    def partial_term(offset, span):
        return jnp.dot(row_values, weight, preferred_element_type=jnp.float32)

    return lax.psum_scatter(
        partial_term(jnp.int32(0), lax.axis_size("tensor") * row_count),
        "tensor",
        scatter_dimension=0,
        tiled=True,
    )


def gather_grads(row_values, weight):

    def project(shard_rows, offset):
        return (shard_rows, jnp.dot(shard_rows, weight.T, preferred_element_type=jnp.float32))

    return project(lax.all_gather(row_values, "tensor", axis=0, tiled=True), jnp.int32(0))


def scatter_grads(row_values, weight, row_count):

    def partial_term(offset, span):
        return jnp.dot(row_values, weight.T, preferred_element_type=jnp.float32)

    return lax.psum_scatter(
        partial_term(jnp.int32(0), lax.axis_size("tensor") * row_count),
        "tensor",
        scatter_dimension=0,
        tiled=True,
    )


def attention_probs(queries, key_rows):
    scores = jnp.einsum(
        "qhd,khd->hqk", queries, key_rows, preferred_element_type=jnp.float32
    ) * HEAD_DIM ** (-0.5)
    length = queries.shape[0]
    positions = jnp.arange(length, dtype=jnp.int32)
    causal = positions[:, None] >= positions[None, :]
    scores = jnp.where(causal[None], scores, -1e30)
    expos = jnp.exp(scores - jnp.max(scores, axis=-1, keepdims=True))
    return expos / jnp.sum(expos, axis=-1, keepdims=True)


def layer_forward(layer_input, weights):
    gains, w_qkv, w_out, w_up, w_down = weights
    row_count, model_width = layer_input.shape
    attn_in = norm_rows(layer_input, gains[0]).astype(jnp.bfloat16)
    gathered_a, qkv = gather_rows(attn_in, w_qkv.reshape(model_width, -1))
    length = qkv.shape[0]
    head_count = w_qkv.shape[2] // HEAD_DIM
    qkv = qkv.reshape(length, 3, head_count, HEAD_DIM)
    cos_table, sin_table = rotary_tables(length, HEAD_DIM)
    queries = rotate(qkv[:, 0], cos_table, sin_table).astype(jnp.bfloat16)
    key_rows = rotate(qkv[:, 1], cos_table, sin_table).astype(jnp.bfloat16)
    values = qkv[:, 2].astype(jnp.bfloat16)
    attn_probs = attention_probs(queries, key_rows).astype(jnp.bfloat16)
    mixed = jnp.einsum("hqk,khd->qhd", attn_probs, values, preferred_element_type=jnp.float32)
    mixed = mixed.reshape(length, -1).astype(jnp.bfloat16)
    attn_branch = scatter_rows(mixed, w_out, row_count)
    hidden = layer_input + norm_rows(attn_branch, gains[1])
    mlp_in = norm_rows(hidden, gains[2]).astype(jnp.bfloat16)
    gathered_c, up_act = gather_rows(mlp_in, w_up)
    gelu_out = jax.nn.gelu(up_act, approximate=True).astype(jnp.bfloat16)
    down_branch = scatter_rows(gelu_out, w_down, row_count)
    result = hidden + norm_rows(down_branch, gains[3])
    kept_values = (
        gathered_a,
        queries,
        key_rows,
        values,
        mixed,
        attn_branch,
        hidden,
        gathered_c,
        up_act,
        gelu_out,
        down_branch,
    )
    return (result, kept_values)


def layer_backward(layer_input, grad_result, kept_values, weights):
    gains, w_qkv, w_out, w_up, w_down = weights
    (
        gathered_a,
        queries,
        key_rows,
        values,
        mixed,
        attn_branch,
        hidden,
        gathered_c,
        up_act,
        gelu_out,
        down_branch,
    ) = kept_values
    row_count, model_width = layer_input.shape
    pullback = jax.vjp(norm_rows, down_branch, gains[3])[1]
    grad_down, gain_three = pullback(grad_result)
    gathered_dd, grad_gelu = gather_grads(grad_down.astype(jnp.bfloat16), w_down)
    down_total = contract(gelu_out, gathered_dd)
    pullback = jax.vjp(lambda vector: jax.nn.gelu(vector, approximate=True), up_act)[1]
    grad_up = pullback(grad_gelu)[0].astype(jnp.bfloat16)
    up_total = contract(gathered_c, grad_up)
    grad_mlp = scatter_grads(grad_up, w_up, row_count)
    pullback = jax.vjp(norm_rows, hidden, gains[2])[1]
    grad_norm_mlp, gain_two = pullback(grad_mlp)
    grad_hidden = grad_result + grad_norm_mlp
    pullback = jax.vjp(norm_rows, attn_branch, gains[1])[1]
    grad_attn, gain_one = pullback(grad_hidden)
    gathered_da, grad_mixed = gather_grads(grad_attn.astype(jnp.bfloat16), w_out)
    out_total = contract(mixed, gathered_da)
    length = grad_mixed.shape[0]
    head_count = w_qkv.shape[2] // HEAD_DIM
    grad_mixed = grad_mixed.astype(jnp.bfloat16).reshape(length, head_count, HEAD_DIM)
    attn_probs = attention_probs(queries, key_rows)
    probs_low = attn_probs.astype(jnp.bfloat16)
    grad_probs = jnp.einsum("qhd,khd->hqk", grad_mixed, values, preferred_element_type=jnp.float32)
    grad_values = jnp.einsum(
        "hqk,qhd->khd", probs_low, grad_mixed, preferred_element_type=jnp.float32
    )
    row_dots = jnp.sum(grad_probs * attn_probs, axis=-1, keepdims=True)
    grad_scores = (attn_probs * (grad_probs - row_dots)).astype(jnp.bfloat16)
    scale_value = HEAD_DIM ** (-0.5)
    grad_queries = (
        jnp.einsum("hqk,khd->qhd", grad_scores, key_rows, preferred_element_type=jnp.float32)
        * scale_value
    )
    grad_keys = (
        jnp.einsum("hqk,qhd->khd", grad_scores, queries, preferred_element_type=jnp.float32)
        * scale_value
    )
    cos_table, sin_table = rotary_tables(length, HEAD_DIM)
    pullback = jax.vjp(lambda vector: rotate(vector, cos_table, sin_table), grad_queries)[1]
    grad_q_raw = pullback(grad_queries)[0]
    grad_k_raw = pullback(grad_keys)[0]
    grad_qkv = (
        jnp.stack([grad_q_raw, grad_k_raw, grad_values], axis=1)
        .reshape(length, -1)
        .astype(jnp.bfloat16)
    )
    qkv_total = contract(gathered_a, grad_qkv).reshape(model_width, 3, -1)
    grad_attn_in = scatter_grads(grad_qkv, w_qkv.reshape(model_width, -1), row_count)
    pullback = jax.vjp(norm_rows, layer_input, gains[0])[1]
    grad_norm_in, gain_zero = pullback(grad_attn_in)
    grad_input = grad_hidden + grad_norm_in
    gain_total = jnp.stack([gain_zero, gain_one, gain_two, gain_three])
    return (grad_input, (gain_total, qkv_total, out_total, up_total, down_total))


def lagged(first_section, stacked):
    blank = jnp.zeros_like(stacked[:1])
    earlier = jnp.concatenate([blank, stacked[:-1]])
    later = jnp.concatenate([stacked[1:], blank])
    return jnp.where(first_section, earlier, later)


def per_device(
    inputs,
    out_cotangent,
    group_ids,
    group_weights,
    gains,
    qkv_weight,
    out_weight,
    up_weight,
    down_weight,
):
    weights = (gains[0], qkv_weight[0], out_weight[0], up_weight[0], down_weight[0])
    micro_count, row_count, model_width = inputs.shape
    first_section = lax.axis_index("section") == 0
    group_count = group_weights.shape[0]
    matches = group_ids[..., None] == jnp.arange(group_count, dtype=jnp.int32)
    row_scale = jnp.sum(jnp.where(matches, group_weights, 0.0), axis=-1)
    scaled = out_cotangent.astype(jnp.float32) * row_scale[..., None]
    padded = jnp.concatenate([inputs, jnp.zeros((1, row_count, model_width), jnp.bfloat16)])

    def forward_tick(received, fresh_input):
        layer_input = jnp.where(first_section, fresh_input, received)
        result, kept_values = layer_forward(layer_input.astype(jnp.float32), weights)
        result_low = result.astype(jnp.bfloat16)
        outgoing = shifted(result_low, "section", 1)
        stashed = ()
        return (outgoing, (layer_input, result_low, stashed))

    start_rows = jnp.zeros((row_count, model_width), jnp.bfloat16)
    _, (layer_inputs, layer_results, stashed) = lax.scan(forward_tick, start_rows, padded)
    layer_outputs = jnp.where(first_section, layer_results[:-1], layer_results[1:])[None]
    back_inputs = lagged(first_section, layer_inputs)
    back_stash = jax.tree.map(lambda stacked: lagged(first_section, stacked), stashed)
    grad_padded = jnp.concatenate([scaled, jnp.zeros((1, row_count, model_width), jnp.float32)])
    tick_index = jnp.arange(micro_count + 1, dtype=jnp.int32)
    tick_valid = jnp.where(first_section, tick_index >= 1, tick_index < micro_count).astype(
        jnp.float32
    )

    def backward_tick(carry, step_item):
        received, totals = carry
        layer_input, cotangent, valid_now, stash_now = step_item
        grad_now = jnp.where(first_section, received.astype(jnp.float32), cotangent)
        input_now = layer_input.astype(jnp.float32)
        kept_values = layer_forward(input_now, weights)[1]
        grad_input, layer_grads = layer_backward(input_now, grad_now, kept_values, weights)
        totals = jax.tree.map(lambda total, update: total + valid_now * update, totals, layer_grads)
        grad_low = grad_input.astype(jnp.bfloat16)
        outgoing = shifted(grad_low, "section", -1)
        return ((outgoing, totals), grad_low)

    start_totals = (
        jnp.zeros((4, model_width), jnp.float32),
        jnp.zeros(qkv_weight.shape[1:], jnp.float32),
        jnp.zeros(out_weight.shape[1:], jnp.float32),
        jnp.zeros(up_weight.shape[1:], jnp.float32),
        jnp.zeros(down_weight.shape[1:], jnp.float32),
    )
    (_, totals), grad_lows = lax.scan(
        backward_tick,
        (start_rows, start_totals),
        (back_inputs, grad_padded, tick_valid, back_stash),
    )
    input_grads = jnp.where(first_section, grad_lows[1:], grad_lows[:-1])[None]
    gain_total, qkv_total, out_total, up_total, down_total = totals
    gains_grad = lax.psum_scatter(gain_total, ("dp", "tensor"), scatter_dimension=1, tiled=True)
    qkv_grad, out_grad, up_grad, down_grad = (
        lax.psum_scatter(
            qkv_total.astype(jnp.bfloat16), "dp", scatter_dimension=0, tiled=True
        ).astype(jnp.float32),
        lax.psum_scatter(
            out_total.astype(jnp.bfloat16), "dp", scatter_dimension=1, tiled=True
        ).astype(jnp.float32),
        lax.psum_scatter(
            up_total.astype(jnp.bfloat16), "dp", scatter_dimension=0, tiled=True
        ).astype(jnp.float32),
        lax.psum_scatter(
            down_total.astype(jnp.bfloat16), "dp", scatter_dimension=1, tiled=True
        ).astype(jnp.float32),
    )
    return (
        layer_outputs,
        input_grads,
        gains_grad[None],
        qkv_grad[None],
        out_grad[None],
        up_grad[None],
        down_grad[None],
    )


def rotated(block, cos_rows, sin_rows):
    lane = lax.broadcasted_iota(jnp.int32, block.shape, 1)
    ahead = pltpu.roll(block, 96, 1)
    behind = pltpu.roll(block, 32, 1)
    swapped = jnp.where(lane % 64 < 32, ahead, behind)
    return block * cos_rows + swapped * sin_rows


def dot_nt(left, right):
    return lax.dot_general(
        left, right, (((1,), (1,)), ((), ())), preferred_element_type=jnp.float32
    )


def dot_nn(left, right):
    return jnp.dot(left, right, preferred_element_type=jnp.float32)


def model_weight(owns, others, cols):
    sides = [jnp.concatenate([ref[:, cols] for ref in refs], axis=1) for refs in (owns, others)]
    return jnp.concatenate(sides, axis=0)


def stacked_up(values):
    return jnp.concatenate(values, axis=0)


def edge_masks(core, rows):
    key = lax.broadcasted_iota(jnp.int32, (rows, 2 * rows), 0)
    query = lax.broadcasted_iota(jnp.int32, (rows, 2 * rows), 1)
    mine = query < rows
    place = jnp.where(mine, query + core * rows, query - rows + (1 - core) * rows)
    return (key + core * rows <= place, key + (1 - core) * rows <= place)


def both_sides(value, half, start, stop, axis=0):
    if axis == 0:
        return jnp.concatenate([value[start:stop], value[half + start : half + stop]], axis=0)
    return jnp.concatenate([value[:, start:stop], value[:, half + start : half + stop]], axis=1)


def hidden_scores(scores, masks, tile, step):
    seen = step * tile
    pieces = []
    for side in range(2):
        base = side * (seen + tile)
        if seen:
            pieces.append(scores[base : base + seen])
        pieces.append(jnp.where(masks[side], scores[base + seen : base + seen + tile], -1e30))
    return jnp.concatenate(pieces, axis=0)


def one_head(rows, head):
    lane = lax.broadcasted_iota(jnp.int32, rows.shape, 1)
    return jnp.where(lane // 64 == head, rows, jnp.zeros_like(rows))


def pick_piece(weight, owns, others, cols):
    for j, (own, other) in enumerate(zip(owns, others)):

        @pl.when(pl.program_id(0) == j)
        def _():
            size = own.shape[0]
            weight[:size] = own[:, cols]
            weight[size:] = other[:, cols]


def attend_kernel(pieces, core_ref, cos_ref, sin_ref, own_rows, other_rows, *refs):
    owns, others = refs[:pieces], refs[pieces : 2 * pieces]
    q_ref, k_ref, v_ref, lse_ref, mix_ref, weight = refs[2 * pieces :]
    half = own_rows.shape[0]
    tile = TILE
    pick_piece(weight, owns, others, QKV)
    proj = dot_nn(stacked_up([own_rows[...], other_rows[...]]), weight[...])
    cos_rows, sin_rows = cos_ref[...], sin_ref[...]
    q = (rotated(proj[:, :128], cos_rows, sin_rows) * HEAD_DIM ** (-0.5)).astype(jnp.bfloat16)
    k = rotated(proj[:, 128:256], cos_rows, sin_rows).astype(jnp.bfloat16)
    v32 = proj[:, 256:]
    q_ref[0] = q
    k_ref[0] = k
    v_ref[0] = v32.astype(jnp.bfloat16)
    v_flip = v32.T.astype(jnp.bfloat16)
    masks = edge_masks(core_ref[0], tile)

    def scored(step, head):
        stop = (step + 1) * tile
        q_head = one_head(both_sides(q, half, step * tile, stop), head)
        return hidden_scores(dot_nt(both_sides(k, half, 0, stop), q_head), masks, tile, step)

    units = [(step, head) for step in range(half // tile) for head in range(2)]
    ahead = scored(*units[0])
    outs = []
    for spot, (step, head) in enumerate(units):
        scores = ahead
        if spot + 1 < len(units):
            ahead = scored(*units[spot + 1])
        stop = (step + 1) * tile
        top = jnp.max(scores, axis=0, keepdims=True)
        expos = jnp.exp(scores - top)
        total = jnp.sum(expos, axis=0, keepdims=True)
        lse = top + jnp.log(total)
        lse_ref[0, head : head + 1, step * tile : stop] = lse[:, :tile]
        lse_ref[0, head : head + 1, half + step * tile : half + stop] = lse[:, tile:]
        v_cols = both_sides(v_flip, half, 0, stop, axis=1)
        out = dot_nn(v_cols[64 * head : 64 * head + 64], expos.astype(jnp.bfloat16))
        outs.append(out * (1.0 / total))
        if head == 1:
            mixed = jnp.concatenate(outs, axis=0).T.astype(jnp.bfloat16)
            outs = []
            mix_ref[step * tile : stop, :] = mixed[:tile]
            mix_ref[half + step * tile : half + stop, :] = mixed[tile:]


def attend_back_kernel(pieces, core_ref, cos_ref, sin_ref, own_rows, other_rows, *refs):
    owns, others = refs[:pieces], refs[pieces : 2 * pieces]
    q_ref, k_ref, v_ref, lse_ref, out_ref, weight, dq, dk, dv = refs[2 * pieces :]
    half = own_rows.shape[0]
    tile = TILE
    pick_piece(weight, owns, others, OUT)
    rows = stacked_up([own_rows[...], other_rows[...]])
    d_mixed = dot_nn(rows, weight[...]).astype(jnp.bfloat16)
    q, k, v = q_ref[0], k_ref[0], v_ref[0]
    k_flip = k.astype(jnp.float32).T.astype(jnp.bfloat16)
    masks = edge_masks(core_ref[0], tile)
    steps = half // tile

    def scored(step, head):
        stop = (step + 1) * tile
        q_head = one_head(both_sides(q, half, step * tile, stop), head)
        g_head = one_head(both_sides(d_mixed, half, step * tile, stop), head)
        scores = hidden_scores(dot_nt(both_sides(k, half, 0, stop), q_head), masks, tile, step)
        return q_head, g_head, scores, dot_nt(both_sides(v, half, 0, stop), g_head)

    units = [(step, head) for step in reversed(range(steps)) for head in range(2)]
    ahead = scored(*units[0])
    dq_flips = []
    dk_sum = dv_sum = None
    for spot, (step, head) in enumerate(units):
        q_head, g_head, scores, d_probs = ahead
        if spot + 1 < len(units):
            ahead = scored(*units[spot + 1])
        stop = (step + 1) * tile
        lse = both_sides(lse_ref[0], half, step * tile, stop, axis=1)
        probs = jnp.exp(scores - lse[head : head + 1])
        dots = jnp.sum(probs * d_probs, axis=0, keepdims=True)
        d_scores = (probs * (d_probs - dots)).astype(jnp.bfloat16)
        dv_part = dot_nn(probs.astype(jnp.bfloat16), g_head)
        dk_part = dot_nn(d_scores, q_head)
        k_cols = both_sides(k_flip, half, 0, stop, axis=1)
        dq_flips.append(dot_nn(k_cols[64 * head : 64 * head + 64], d_scores))
        if head == 0:
            dv_sum, dk_sum = dv_part, dk_part
            continue
        dv_sum, dk_sum = dv_sum + dv_part, dk_sum + dk_part
        dq_rows = jnp.concatenate(dq_flips, axis=0).T * HEAD_DIM ** (-0.5)
        dq_flips = []
        dq[step * tile : stop] = dq_rows[:tile]
        dq[half + step * tile : half + stop] = dq_rows[tile:]
        for base, part in ((0, slice(0, stop)), (half, slice(stop, 2 * stop))):
            if step == steps - 1:
                dk[base : base + stop] = dk_sum[part]
                dv[base : base + stop] = dv_sum[part]
            else:
                dk[base : base + stop] += dk_sum[part]
                dv[base : base + stop] += dv_sum[part]
    cos_rows, sin_rows = cos_ref[...], -sin_ref[...]
    out_ref[:, :128] = rotated(dq[...], cos_rows, sin_rows).astype(jnp.bfloat16)
    out_ref[:, 128:256] = rotated(dk[...], cos_rows, sin_rows).astype(jnp.bfloat16)
    out_ref[:, 256:] = dv[...].astype(jnp.bfloat16)


def split_rows(total, own_ref, other_ref):
    half = own_ref.shape[0]
    own_ref[...] = total[:half]
    other_ref[...] = total[half:].astype(jnp.bfloat16)


def to_model_kernel(lefts, pieces, cols, *refs):
    left, refs = jnp.concatenate([ref[...] for ref in refs[:lefts]], axis=1), refs[lefts:]
    weight = model_weight(refs[:pieces], refs[pieces : 2 * pieces], cols)
    split_rows(dot_nt(left, weight), *refs[2 * pieces :])


def mlp_down_kernel(pieces, left_ref, *refs):
    sides = [stacked_up([ref[...] for ref in side]) for side in (refs[:pieces], refs[pieces:-2])]
    split_rows(dot_nn(left_ref[...], jnp.concatenate(sides, axis=1)), *refs[-2:])


def gelu_both(up_act):
    root = math.sqrt(2.0 / math.pi)
    square = up_act * up_act
    rise = 0.5 + 0.5 * jnp.tanh(up_act * (root + root * 0.044715 * square))
    value = up_act * rise
    slope = rise + value * (1.0 - rise) * (2.0 * root + 6.0 * root * 0.044715 * square)
    return value, slope


def mlp_up_kernel(pieces, own_rows, other_rows, *refs):
    owns, others = refs[:pieces], refs[pieces : 2 * pieces]
    gelu_ref, slope_ref = refs[2 * pieces :]
    half = own_rows.shape[0]
    size = owns[0].shape[1]
    step = half // 2
    units = [(j, i) for j in range(pieces) for i in range(4)]

    def product(j, i):
        rows = (own_rows, other_rows)[i // 2][i % 2 * step : (i % 2 + 1) * step]
        return dot_nn(rows, stacked_up([owns[j][...], others[j][...]]))

    ahead = product(*units[0])
    for spot, (j, i) in enumerate(units):
        up_act = ahead
        if spot + 1 < len(units):
            ahead = product(*units[spot + 1])
        value, slope = gelu_both(up_act)
        gelu_ref[i * step : (i + 1) * step, j * size : (j + 1) * size] = value.astype(jnp.bfloat16)
        slope_ref[i * step : (i + 1) * step, j * size : (j + 1) * size] = slope.astype(
            jnp.bfloat16
        )


def mlp_up_back_kernel(pieces, own_rows, other_rows, slope_ref, *refs):
    owns, others = refs[:pieces], refs[pieces : 2 * pieces]
    out_ref, weight, slope, sems = refs[2 * pieces :]
    half = own_rows.shape[1] // 2
    size = owns[0].shape[0]
    order = list(reversed(range(pieces)))
    copies = []
    for j in order:
        sources = (owns[j], others[j], slope_ref.at[:, pl.ds(j * size, size)])
        targets = (
            weight.at[j, :, pl.ds(0, half)],
            weight.at[j, :, pl.ds(half, half)],
            slope.at[:, pl.ds(j * size, size)],
        )
        copies.append(
            [
                pltpu.make_async_copy(source, target, sems.at[j, i])
                for i, (source, target) in enumerate(zip(sources, targets))
            ]
        )
        for copy in copies[-1]:
            copy.start()
    rows = stacked_up([own_rows[...], other_rows[...]])
    for j, arriving in zip(order, copies):
        cols = slice(j * size, (j + 1) * size)
        for copy in arriving:
            copy.wait()
        d_gelu = dot_nt(rows, weight[j])
        out_ref[:, cols] = (d_gelu * slope[:, cols].astype(jnp.float32)).astype(jnp.bfloat16)


def inverse_size(rows):
    return lax.rsqrt(jnp.mean(rows * rows, axis=-1, keepdims=True) + NORM_EPSILON)


def norm_back(rows, gain, grad):
    scale = inverse_size(rows)
    weighted = grad * gain
    inner = jnp.mean(rows * weighted, axis=-1, keepdims=True)
    return scale * weighted - rows * (scale * scale * scale * inner), rows * scale * grad


def folded(rows):
    return jnp.sum(rows.reshape(rows.shape[0] // 8, 8, rows.shape[1]), axis=0)


def wide(ref, spot):
    return ref[spot, :].astype(jnp.float32)


def by_chunks(count, body, sums=0, width=0):
    def one(i, carry):
        more = body(pl.ds(pl.multiple_of(i * CHUNK, CHUNK), CHUNK))
        return tuple(old + folded(new) for old, new in zip(carry, more))

    start = tuple(jnp.zeros((8, width), jnp.float32) for _ in range(sums))
    totals = lax.fori_loop(0, count // CHUNK, one, start)
    return [jnp.sum(total, axis=0, keepdims=True) for total in totals]


def norm_in_kernel(gain_ref, rows_ref, out_ref):
    def body(spot):
        rows = wide(rows_ref, spot)
        out_ref[spot, :] = (rows * inverse_size(rows) * gain_ref[0:1]).astype(jnp.bfloat16)
        return ()

    by_chunks(rows_ref.shape[0], body)


def after_attention_kernel(
    gain_ref, rows_ref, own_ref, other_ref, branch_ref, hidden_ref, out_ref
):
    def body(spot):
        branch = own_ref[spot, :] + wide(other_ref, spot)
        hidden = wide(rows_ref, spot) + branch * inverse_size(branch) * gain_ref[1:2]
        branch_ref[spot, :] = branch
        hidden_ref[spot, :] = hidden
        out_ref[spot, :] = (hidden * inverse_size(hidden) * gain_ref[2:3]).astype(jnp.bfloat16)
        return ()

    by_chunks(rows_ref.shape[0], body)


def after_mlp_kernel(gain_ref, hidden_ref, own_ref, other_ref, branch_ref, out_ref):
    def body(spot):
        branch = own_ref[spot, :] + wide(other_ref, spot)
        branch_ref[spot, :] = branch
        result = hidden_ref[spot, :] + branch * inverse_size(branch) * gain_ref[3:4]
        out_ref[spot, :] = result.astype(jnp.bfloat16)
        return ()

    by_chunks(hidden_ref.shape[0], body)


def into_mlp_back_kernel(gain_ref, grad_ref, branch_ref, out_ref, sum_ref):
    def body(spot):
        d_rows, d_gain = norm_back(branch_ref[spot, :], gain_ref[3:4], wide(grad_ref, spot))
        out_ref[spot, :] = d_rows.astype(jnp.bfloat16)
        return (d_gain,)

    (sum_ref[...],) = by_chunks(grad_ref.shape[0], body, 1, grad_ref.shape[1])


def into_attention_back_kernel(
    gain_ref, grad_ref, own_ref, other_ref, hidden_ref, branch_ref, d_hidden_ref, out_ref, *sums
):
    def body(spot):
        d_rows = own_ref[spot, :] + wide(other_ref, spot)
        d_rows, d_gain = norm_back(hidden_ref[spot, :], gain_ref[2:3], d_rows)
        d_hidden = wide(grad_ref, spot) + d_rows
        d_hidden_ref[spot, :] = d_hidden
        d_rows, d_first = norm_back(branch_ref[spot, :], gain_ref[1:2], d_hidden)
        out_ref[spot, :] = d_rows.astype(jnp.bfloat16)
        return (d_first, d_gain)

    totals = by_chunks(grad_ref.shape[0], body, 2, grad_ref.shape[1])
    sums[0][...], sums[1][...] = totals


def out_of_layer_kernel(gain_ref, rows_ref, own_ref, other_ref, d_hidden_ref, out_ref, sum_ref):
    def body(spot):
        d_rows = own_ref[spot, :] + wide(other_ref, spot)
        d_rows, d_gain = norm_back(wide(rows_ref, spot), gain_ref[0:1], d_rows)
        out_ref[spot, :] = (d_hidden_ref[spot, :] + d_rows).astype(jnp.bfloat16)
        return (d_gain,)

    (sum_ref[...],) = by_chunks(rows_ref.shape[0], body, 1, rows_ref.shape[1])


def work(flops, arrays):
    size = sum(math.prod(array.shape) * jnp.dtype(array.dtype).itemsize for array in arrays)
    return pl.CostEstimate(flops=flops, bytes_accessed=size, transcendentals=0)


def without(kernel, first, count):
    return lambda *refs: kernel(*refs[:first], *refs[first + count :])


def on_chip(kernel, name, outs, *operands, limit=ROWS_VMEM, flops=0, waits=()):
    shapes = [jax.ShapeDtypeStruct(shape, dtype) for shape, dtype in outs]
    space = pl.BlockSpec(memory_space=pltpu.VMEM)
    return pl.pallas_call(
        without(kernel, len(operands), len(waits)),
        in_specs=[space] * len(operands) + [pl.BlockSpec(memory_space=pl.ANY)] * len(waits),
        out_specs=[space] * len(outs),
        out_shape=shapes,
        compiler_params=pltpu.CompilerParams(vmem_limit_bytes=limit),
        cost_estimate=work(flops, (*operands, *shapes)),
        name=name,
    )(*operands, *waits)


def whole_block(array):
    return pl.BlockSpec(array.shape, lambda j: (0,) * array.ndim)


def by_pairs(kernel, name, core, operands, pieces, blocks, outs, scratch, flops, waits):
    shapes = [jax.ShapeDtypeStruct(shape, dtype) for shape, dtype, _ in outs]
    taken = 1 + len(operands) + 2 * len(pieces[0]) + len(blocks)
    return pl.pallas_call(
        without(functools.partial(kernel, len(pieces[0])), taken, len(waits)),
        grid=(len(pieces[0]),),
        in_specs=[pl.BlockSpec(memory_space=pltpu.SMEM)]
        + [whole_block(array) for array in (*operands, *pieces[0], *pieces[1])]
        + [spec for _, spec in blocks]
        + [pl.BlockSpec(memory_space=pl.ANY)] * len(waits),
        out_specs=[spec for _, _, spec in outs],
        out_shape=shapes,
        scratch_shapes=scratch,
        compiler_params=pltpu.CompilerParams(vmem_limit_bytes=KERNEL_VMEM),
        cost_estimate=work(flops, (*operands, *pieces[0], *pieces[1], *shapes)),
        name=name,
    )(core, *operands, *pieces[0], *pieces[1], *[array for array, _ in blocks], *waits)


def mlp_up_back(rows, slope, pieces, waits):
    length, units = slope.shape
    unit, half = pieces[0][0].shape
    count = len(pieces[0])
    every, space = pl.BlockSpec(memory_space=pl.ANY), pl.BlockSpec(memory_space=pltpu.VMEM)
    return pl.pallas_call(
        without(functools.partial(mlp_up_back_kernel, count), 3 + 2 * count, len(waits)),
        in_specs=[space] * 2 + [every] * (1 + 2 * count + len(waits)),
        out_specs=space,
        out_shape=jax.ShapeDtypeStruct((length, units), jnp.bfloat16),
        scratch_shapes=[
            pltpu.VMEM((count, unit, 2 * half), jnp.bfloat16),
            pltpu.VMEM((length, units), jnp.bfloat16),
            pltpu.SemaphoreType.DMA((count, 3)),
        ],
        compiler_params=pltpu.CompilerParams(vmem_limit_bytes=KERNEL_VMEM),
        name="mlp_up_back",
    )(*rows, slope, *pieces[0], *pieces[1], *waits)


def attend(core, tables, rows, pieces, waits):
    half, features = rows[0].shape
    length, count = 2 * half, len(pieces[0])
    lanes = ((count, length, 128), jnp.bfloat16, pl.BlockSpec((1, length, 128), lambda j: (j, 0, 0)))
    lse = ((count, 2, length), jnp.float32, pl.BlockSpec((1, 2, length), lambda j: (j, 0, 0)))
    mixed = ((length, count * 128), jnp.bfloat16, pl.BlockSpec((length, 128), lambda j: (0, j)))
    return by_pairs(
        attend_kernel,
        "attend",
        core,
        (*tables, *rows),
        pieces,
        (),
        (lanes, lanes, lanes, lse, mixed),
        [pltpu.VMEM((features, 384), jnp.bfloat16)],
        count * length * (2 * features * 384 + 2 * PAIR_WORK * length),
        waits,
    )


def attend_back(core, tables, rows, pieces, base, waits, q, k, v, lse):
    half, features = rows[0].shape
    length, count = 2 * half, len(pieces[0])
    lanes = pl.BlockSpec((1, length, 128), lambda j: (base + j, 0, 0))
    lse_spec = pl.BlockSpec((1, 2, length), lambda j: (base + j, 0, 0))
    out = ((length, count * 384), jnp.bfloat16, pl.BlockSpec((length, 384), lambda j: (0, j)))
    return by_pairs(
        attend_back_kernel,
        "attend_back",
        core,
        (*tables, *rows),
        pieces,
        ((q, lanes), (k, lanes), (v, lanes), (lse, lse_spec)),
        (out,),
        [pltpu.VMEM((features, 128), jnp.bfloat16)] + [pltpu.VMEM((length, 128), jnp.float32)] * 3,
        count * length * (2 * features * 128 + 5 * PAIR_WORK * length),
        waits,
    )[0]


def exchanged(parts):
    return parts[0], flip_pairs(parts[1], 1)


def model_rows(kernel, name, lefts, pieces, waits=()):
    length, width = lefts[0].shape[0], 2 * MODEL_HALF
    outs = (((length // 2, width), jnp.float32), ((length // 2, width), jnp.bfloat16))
    hidden = sum(left.shape[1] for left in lefts)
    more = {"limit": KERNEL_VMEM, "flops": 2 * length * width * hidden, "waits": waits}
    return exchanged(on_chip(kernel, name, outs, *lefts, *pieces[0], *pieces[1], **more))


def flip_pairs(block, distance):
    size = lax.axis_size("dp")
    return lax.ppermute(block, "dp", [(i, i ^ distance) for i in range(size)])


def passed_on(block, step):
    size = lax.axis_size("tensor")
    return lax.ppermute(block, "tensor", [(i, (i + step) % size) for i in range(size)])


def dot_tn(left, right):
    return lax.dot_general(
        left, right, (((0,), (0,)), ((), ())), preferred_element_type=jnp.float32
    )


def fetch(first_ref, zeros, ones, buffers, sems):
    for section, sources in enumerate((zeros, ones)):

        @pl.when(first_ref[0] == section)
        def _():
            for i, (source, buffer) in enumerate(zip(sources, buffers)):
                pltpu.make_async_copy(source, buffer, sems.at[i]).start()

    def arrived(*places):
        for i in places:
            pltpu.make_async_copy(zeros[i], buffers[i], sems.at[i]).wait()

    return arrived


def mlp_grads_kernel(base, section_ref, *refs):
    (own_one, other_one, own_two, other_two), (rows, d_up, gelu, d_down, sems) = refs[12:16], refs[16:]
    half, size = own_one.shape[0] // 2, own_one.shape[1]
    cols = pl.ds(base * size, 2 * size)

    def parts(own_rows, other_rows, d_up_ref, gelu_ref, own_grad, other_grad):
        whole = (d_up_ref.at[:, cols], gelu_ref.at[:, cols])
        return (own_rows, other_rows, *whole, own_grad, other_grad)

    count = refs[0].shape[0]
    buffers = (
        rows.at[pl.ds(0, count)],
        rows.at[pl.ds(count, count)],
        d_up,
        gelu,
        d_down.at[pl.ds(0, count)],
        d_down.at[pl.ds(count, count)],
    )
    arrived = fetch(section_ref, parts(*refs[:6]), parts(*refs[6:12]), buffers, sems)
    for j, own, other in ((1, own_two, other_two), (0, own_one, other_one)):
        cols = slice(j * size, (j + 1) * size)
        if j == 1:
            arrived(0, 1, 2)
        up = dot_tn(rows[...], d_up[:, cols])
        own[:half] = up[:half]
        other[:half] = up[half:].astype(jnp.bfloat16)
        if j == 1:
            arrived(3, 4, 5)
        down = dot_tn(gelu[:, cols], d_down[...])
        own[half:] = down[:, :half]
        other[half:] = down[:, half:].astype(jnp.bfloat16)


def attn_grads_kernel(base, section_ref, *refs):
    (own_one, other_one, own_two, other_two), (rows, d_qkv, mixed, d_attn, sems) = refs[12:16], refs[16:]
    half, size = own_one.shape[0], d_qkv.shape[1] // 2
    count = refs[0].shape[0]
    cols = pl.ds(base * 128, 256)

    def parts(own_rows, other_rows, d_qkv_ref, mixed_ref, own_grad, other_grad):
        return (own_rows, other_rows, d_qkv_ref, mixed_ref.at[:, cols], own_grad, other_grad)

    buffers = (
        rows.at[pl.ds(0, count)],
        rows.at[pl.ds(count, count)],
        d_qkv,
        mixed,
        d_attn.at[pl.ds(0, count)],
        d_attn.at[pl.ds(count, count)],
    )
    arrived = fetch(section_ref, parts(*refs[:6]), parts(*refs[6:12]), buffers, sems)
    for j, own, other in ((1, own_two, other_two), (0, own_one, other_one)):
        if j == 1:
            arrived(0, 1, 2)
        qkv = dot_tn(rows[...], d_qkv[:, j * size : (j + 1) * size])
        if j == 1:
            arrived(3, 4, 5)
        out = dot_tn(d_attn[...], mixed[:, j * 128 : (j + 1) * 128])
        own[:, :size] = qkv[:half]
        own[:, size:] = out[:half]
        other[:, :size] = qkv[half:].astype(jnp.bfloat16)
        other[:, size:] = out[half:].astype(jnp.bfloat16)


def weight_grads(kernel, name, base, section, zeros, ones, shape, columns, waits=()):
    length = 2 * zeros[0].shape[0]
    width = zeros[0].shape[1]
    every = pl.BlockSpec(memory_space=pl.ANY)
    space = pl.BlockSpec(memory_space=pltpu.VMEM)
    arrays = (*zeros, *ones)
    first, second, third, fourth = pl.pallas_call(
        without(functools.partial(kernel, base), 1 + len(arrays), len(waits)),
        in_specs=[pl.BlockSpec(memory_space=pltpu.SMEM)] + [every] * (len(arrays) + len(waits)),
        out_specs=[space] * 4,
        out_shape=[
            jax.ShapeDtypeStruct(shape, jnp.float32),
            jax.ShapeDtypeStruct(shape, jnp.bfloat16),
        ]
        * 2,
        scratch_shapes=[
            pltpu.VMEM((length, width), jnp.bfloat16),
            pltpu.VMEM((length, columns[0]), jnp.bfloat16),
            pltpu.VMEM((length, columns[1]), jnp.bfloat16),
            pltpu.VMEM((length, width), jnp.bfloat16),
            pltpu.SemaphoreType.DMA((6,)),
        ],
        compiler_params=pltpu.CompilerParams(vmem_limit_bytes=KERNEL_VMEM),
        name=name,
    )(section, *arrays, *waits)
    return [(first, flip_pairs(second, 2)), (third, flip_pairs(fourth, 2))]


def moved_kernel(own_ref, other_ref, *refs):
    out_ref = refs[-1]

    def body(i, carry):
        spot = pl.ds(pl.multiple_of(i * CHUNK, CHUNK), CHUNK)
        total = own_ref[spot, :]
        for ref in (other_ref, *refs[:-1]):
            total = total + wide(ref, spot)
        out_ref[spot, :] = total.astype(jnp.bfloat16)
        return carry

    lax.fori_loop(0, own_ref.shape[0] // CHUNK, body, 0)


def gate_kernel(up_ref, down_ref, up_out, down_out):
    up_out[...] = up_ref[...]
    down_out[...] = down_ref[...]


def mlp_sum_kernel(core_ref, own_ref, other_ref, moved_ref, up_keep, down_keep, up_send, down_send):
    half = own_ref.shape[0] // 2
    size = up_keep.shape[0]

    def total(rows, cols):
        more = other_ref[rows, cols].astype(jnp.float32) + moved_ref[rows, cols].astype(jnp.float32)
        return own_ref[rows, cols] + more

    for core in range(2):

        @pl.when(core_ref[0] == core)
        def _():
            for place, up, down in ((core, up_keep, down_keep), (1 - core, up_send, down_send)):
                spot = slice(place * size, (place + 1) * size)
                up[...] = total(spot, slice(None))
                down[...] = total(slice(half, None), spot)


def mlp_join_kernel(core_ref, up_keep, down_keep, up_sent, down_sent, up_out, down_out):
    size = up_keep.shape[1]
    for core in range(2):

        @pl.when(core_ref[0] == core)
        def _():
            places = ((core, up_keep, down_keep), (1 - core, up_sent, down_sent))
            for place, up, down in places:
                spot = slice(place * size, (place + 1) * size)
                up_out[:, spot] = up[...]
                down_out[spot] = down[...]


def pick_kernel(core_ref, rows_ref, keep_ref, send_ref):
    count = keep_ref.shape[0]
    keep_ref[...] = rows_ref[pl.ds(core_ref[0] * count, count)]
    send_ref[...] = rows_ref[pl.ds((1 - core_ref[0]) * count, count)]


def in_order_kernel(core_ref, keep_ref, sent_ref, out_ref):
    out_ref[:, pl.ds(core_ref[0], 1)] = keep_ref[...][:, None]
    out_ref[:, pl.ds(1 - core_ref[0], 1)] = sent_ref[...][:, None]


def with_core(kernel, name, core, outs, *operands, waits=()):
    space = pl.BlockSpec(memory_space=pltpu.VMEM)
    return pl.pallas_call(
        without(kernel, 1 + len(operands), len(waits)),
        in_specs=[pl.BlockSpec(memory_space=pltpu.SMEM)]
        + [space] * len(operands)
        + [pl.BlockSpec(memory_space=pl.ANY)] * len(waits),
        out_specs=[space] * len(outs),
        out_shape=[jax.ShapeDtypeStruct(shape, dtype) for shape, dtype in outs],
        compiler_params=pltpu.CompilerParams(vmem_limit_bytes=ROWS_VMEM),
        name=name,
    )(core, *operands, *waits)


def last_sum_kernel(core_ref, own_ref, other_ref, moved_ref, keep_ref, send_ref):
    rows = keep_ref.shape[0]

    def total(block):
        spot = pl.ds(pl.multiple_of(block * rows, rows), rows)
        return own_ref[spot, :] + wide(other_ref, spot) + wide(moved_ref, spot)

    keep_ref[...] = total(core_ref[0])
    send_ref[...] = total(1 - core_ref[0])


def joined_kernel(spots, core_ref, keep_ref, sent_ref, column_ref, row_ref):
    size = row_ref.shape[0] // 2
    for core in range(2):

        @pl.when(core_ref[0] == core)
        def _():
            for place, source in ((core, keep_ref), (1 - core, sent_ref)):
                for start, stop, to in spots:
                    step = stop - start
                    column_ref[:, to + place * step : to + (place + 1) * step] = source[:, start:stop]
                row_ref[place * size : (place + 1) * size] = source[:, spots[-1][1] :].T


def per_chip(
    inputs,
    out_cotangent,
    group_ids,
    group_weights,
    gains,
    qkv_weight,
    out_weight,
    up_weight,
    down_weight,
):
    micro, row_count, width = inputs.shape
    tensor = lax.axis_size("tensor")
    part = row_count // 2
    wide_half = width // 2
    length = tensor * row_count
    half = length // 2
    first = lax.axis_index("section") == 0
    place = lax.axis_index("dp")
    core = place % 2
    upper = place // 2 % 2
    core_zero = core == 0
    low_half = upper == 0

    def ordered(mine, other):
        return jnp.where(core_zero, mine, other), jnp.where(core_zero, other, mine)

    def own_first(values):
        return jnp.where(low_half, values, jnp.roll(values, wide_half, axis=-1))

    def both_rows(own):
        return own, flip_pairs(own, 1)

    def to_chip(block):
        split = block.reshape((micro, 2, part) + block.shape[2:])
        mine = lax.dynamic_index_in_dim(split, core, 1, keepdims=False)
        other = lax.dynamic_index_in_dim(split, 1 - core, 1, keepdims=False)
        return lax.all_to_all(
            jnp.concatenate(ordered(mine, flip_pairs(other, 1))), "tensor", 0, 0, tiled=True
        )

    def from_chip(spread_out, waits=()):
        piece = ((micro, part, width), jnp.bfloat16)
        keep, send = with_core(
            pick_kernel, "pick", core_word, (piece, piece), spread_out, waits=waits
        )
        outs = (((micro, 2, part, width), jnp.bfloat16),)
        (rows,) = with_core(
            in_order_kernel, "in_order", core_word, outs, keep, flip_pairs(send, 1)
        )
        return rows.reshape(micro, row_count, width)

    def columns(local):
        size = local.shape[-1] // 2
        mid = (0,) * (local.ndim - 2)
        piece = lax.dynamic_slice(
            local,
            (wide_half * upper, *mid, size * core),
            (wide_half, *local.shape[1:-1], size),
        )
        return piece.reshape(wide_half, -1)

    def rows(local):
        size = local.shape[0] // 2
        return lax.dynamic_slice(local, (size * core, wide_half * upper), (size, wide_half))

    core_word = core.astype(jnp.int32).reshape(1)
    attn_piece = jnp.concatenate([columns(qkv_weight[0]), rows(out_weight[0]).T], axis=1)

    def spread(piece):
        pieces = [piece]
        for _ in range(tensor - 1):
            pieces.append(passed_on(pieces[-1], 1))
        return pieces

    attn_own = spread(attn_piece)
    attn_other = [flip_pairs(piece, 2) for piece in attn_own]
    up_piece, down_piece = columns(up_weight[0]), rows(down_weight[0])
    up_other, down_other = [flip_pairs(up_piece, 2)], [flip_pairs(down_piece, 2)]
    outs = tuple((piece.shape, piece.dtype) for piece in (up_piece, down_piece))
    up_piece, down_piece = on_chip(
        gate_kernel, "gate", outs, up_piece, down_piece, waits=(attn_own[2], attn_other[0])
    )
    up_own, down_own = spread(up_piece), spread(down_piece)
    up_other += [flip_pairs(piece, 2) for piece in up_own[1:]]
    down_other += [flip_pairs(piece, 2) for piece in down_own[1:]]
    w_attn, w_up, w_down = (attn_own, attn_other), (up_own, up_other), (down_own, down_other)
    unit = up_piece.shape[1]
    units = tensor * unit

    group_count = group_weights.shape[0]
    matches = group_ids[..., None] == jnp.arange(group_count, dtype=jnp.int32)
    row_scale = jnp.sum(jnp.where(matches, group_weights, 0.0), axis=-1)
    weighted = (out_cotangent.astype(jnp.float32) * row_scale[..., None]).astype(jnp.bfloat16)
    start = to_chip(own_first(jnp.where(first, inputs, weighted))).reshape(half, width)
    gain = own_first(gains[0])

    turns = jnp.arange(half, dtype=jnp.int32)
    turns = turns // part * row_count + turns % part
    positions = jnp.concatenate([turns + core * part, turns + (1 - core) * part])
    freqs = 10000.0 ** (-2.0 * jnp.arange(HEAD_DIM // 2, dtype=jnp.float32) / HEAD_DIM)
    angles = positions.astype(jnp.float32)[:, None] * freqs[None, :]
    cos_part, sin_part = jnp.cos(angles), jnp.sin(angles)
    tables = (
        jnp.concatenate([cos_part] * 4, axis=1),
        jnp.concatenate([-sin_part, sin_part] * 2, axis=1),
    )
    row32, row16 = ((half, width), jnp.float32), ((half, width), jnp.bfloat16)
    unit16 = ((length, units), jnp.bfloat16)
    sum32 = ((1, width), jnp.float32)
    mlp_cost = {"limit": KERNEL_VMEM, "flops": 2 * length * width * units}
    every = slice(None)

    def model_kernel(cols, lefts=1):
        return functools.partial(to_model_kernel, lefts, tensor, cols)

    down_kernel = functools.partial(mlp_down_kernel, tensor)

    def forward(layer_input, waits):
        attn_in = both_rows(
            on_chip(norm_in_kernel, "norm_in", (row16,), gain, layer_input, waits=waits[0])[0]
        )
        *heads, mixed = attend(core_word, tables, attn_in, w_attn, waits[1])
        parts = model_rows(model_kernel(OUT), "attn_out", [mixed], w_attn, waits[2])
        operands = (gain, layer_input, *parts)
        branch, hidden, mlp_in = on_chip(
            after_attention_kernel, "after_attn", (row32, row32, row16), *operands, waits=waits[3]
        )
        mlp_in = both_rows(mlp_in)
        kernel = functools.partial(mlp_up_kernel, tensor)
        operands = (*mlp_in, *w_up[0], *w_up[1])
        gelu_out, slope = on_chip(kernel, "mlp_up", (unit16, unit16), *operands, **mlp_cost)
        parts = model_rows(down_kernel, "mlp_down", [gelu_out], w_down)
        mlp_branch, result = on_chip(
            after_mlp_kernel, "after_mlp", (row32, row16), gain, hidden, *parts
        )
        saved = (layer_input, heads, branch, hidden, slope, mlp_branch)
        return result, saved, (attn_in, mixed, mlp_in, gelu_out)

    def backward(grad, saved, hook, late=()):
        layer_input, heads, branch, hidden, slope, mlp_branch = saved
        operands = (gain, grad, mlp_branch)
        d_down, sum_three = on_chip(
            into_mlp_back_kernel, "into_mlp_back", (row16, sum32), *operands
        )
        d_down = both_rows(d_down)
        d_up = mlp_up_back(d_down, slope, w_down, late)
        waits = hook(d_down, d_up)
        parts = model_rows(model_kernel(every), "mlp_back", [d_up], w_up, waits)
        waits = hook()
        operands = (gain, grad, *parts, hidden, branch)
        outs = (row32, row16, sum32, sum32)
        d_hidden, d_attn, sum_one, sum_two = on_chip(
            into_attention_back_kernel, "into_attn_back", outs, *operands, waits=waits
        )
        d_attn = both_rows(d_attn)
        waits = hook(d_attn)
        d_qkv = []
        for base in reversed(range(0, tensor, 2)):
            some = [side[base : base + 2] for side in w_attn]
            now = attend_back(core_word, tables, d_attn, some, base, waits, *heads)
            d_qkv.insert(0, now)
            waits = hook(now)
        parts = model_rows(model_kernel(QKV, 2), "attn_back", d_qkv, w_attn, waits)
        operands = (gain, layer_input, *parts, d_hidden)
        d_input, sum_zero = on_chip(
            out_of_layer_kernel, "out_of_layer", (row16, sum32), *operands, waits=hook()
        )
        sums = jnp.concatenate([sum_zero, sum_one, sum_two, sum_three])
        return d_input, (d_qkv, d_attn, d_up, d_down), sums

    low_zero, saved_zero, lefts_zero = forward(
        start,
        (
            (up_piece, up_other[0], down_other[0]),
            (up_own[1], down_own[1]),
            (up_own[2], down_own[2], up_other[1], down_other[1]),
            (up_own[3], down_own[3], up_other[2], down_other[2]),
        ),
    )
    low_one, saved_one, lefts_one = forward(shifted(low_zero, "section", 1), ((),) * 4)
    grad_one, rights_one, gain_one = backward(start, saved_one, lambda *new: ())
    received = shifted(grad_one, "section", -1)

    lows = lax.optimization_barrier((low_zero, low_one, grad_one))[:2]
    lows = own_first(jnp.where(first, *lows)).reshape(tensor, part, width)
    lows = lax.all_to_all(lows, "tensor", 0, 0, tiled=True)

    section_word = lax.axis_index("section").astype(jnp.int32).reshape(1)

    def mlp_leaves(base):
        zeros = (*lefts_zero[2], d_up, lefts_zero[3], *d_down)
        ones = (*lefts_one[2], rights_one[2], lefts_one[3], *rights_one[3])
        mlp_sums[base : base + 2] = weight_grads(
            mlp_grads_kernel,
            "mlp_grads",
            base,
            section_word,
            zeros,
            ones,
            (wide_half + unit, unit),
            (2 * unit, 2 * unit),
        )

    def attn_leaves(base, d_qkv):
        zeros = (*lefts_zero[0], d_qkv, lefts_zero[1], *d_attn)
        ones = (*lefts_one[0], rights_one[0][base // 2], lefts_one[1], *rights_one[1])
        attn_sums[base : base + 2] = weight_grads(
            attn_grads_kernel,
            "attn_grads",
            base,
            section_word,
            zeros,
            ones,
            (wide_half, 512),
            (768, 256),
        )

    def moves_on(piece, *moved, waits=()):
        outs = ((piece[1].shape, jnp.bfloat16),)
        (total,) = on_chip(moved_kernel, "moved", outs, *piece, *moved, waits=waits)
        return passed_on(total, -1)

    mlp_sums, attn_sums = [None] * tensor, [None] * tensor
    mlp_moves, attn_moves = [None] * tensor, [None] * tensor
    hooks = iter(range(6))

    def hook(*new):
        nonlocal d_down, d_up, d_attn
        turn = next(hooks)
        if turn == 0:
            d_down, d_up = new
            mlp_leaves(2)
            return (mlp_sums[3][0],)
        if turn == 1:
            mlp_leaves(0)
            return (mlp_sums[1][0],)
        if turn == 2:
            (d_attn,) = new
            mlp_moves[3] = moves_on(mlp_sums[3], waits=d_attn[:1])
            return (mlp_sums[3][1],)
        if turn == 3:
            mlp_moves[2] = moves_on(mlp_sums[2], mlp_moves[3], waits=new)
            attn_leaves(2, new[0])
            return (mlp_sums[2][1], mlp_moves[3], attn_sums[3][0])
        if turn == 4:
            mlp_moves[1] = moves_on(mlp_sums[1], mlp_moves[2], waits=new)
            attn_leaves(0, new[0])
            return (mlp_sums[1][1], mlp_moves[2], attn_sums[1][0])
        return (mlp_sums[0][1], attn_sums[3][1], attn_sums[2][1])

    d_down = d_up = d_attn = None
    grad_zero, rights_zero, gain_zero = backward(received, saved_zero, hook, (lows,))
    attn_moves[3] = moves_on(attn_sums[3])
    attn_moves[2] = moves_on(attn_sums[2], attn_moves[3])
    attn_moves[1] = moves_on(attn_sums[1], attn_moves[2])
    gain_total = own_first(jnp.where(first, gain_zero, gain_one))
    count = tensor * lax.axis_size("dp")
    gain_parts = gain_total.reshape(4, count, width // count).swapaxes(0, 1)
    gain_parts = lax.all_to_all(gain_parts, ("dp", "tensor"), 0, 0, tiled=True)
    gains_grad = jnp.sum(gain_parts, axis=0)
    outputs = from_chip(lows, (grad_zero, attn_sums[1][1]))
    grads = own_first(jnp.where(first, grad_zero, grad_one)).reshape(tensor, part, width)
    grads = from_chip(lax.all_to_all(grads, "tensor", 0, 0, tiled=True), attn_sums[0][1:])

    block32 = ((wide_half // 2, unit), jnp.float32)
    down32 = ((unit, wide_half // 2), jnp.float32)
    up_keep, down_keep, up_send, down_send = with_core(
        mlp_sum_kernel,
        "mlp_sum",
        core_word,
        (block32, down32, block32, down32),
        *mlp_sums[0],
        mlp_moves[1],
    )
    outs = (
        ((wide_half // 2, 2 * unit), jnp.float32),
        ((2 * unit, wide_half // 2), jnp.float32),
    )
    sent = flip_pairs(up_send, 1), flip_pairs(down_send, 1)
    up_grad, down_grad = with_core(
        mlp_join_kernel, "mlp_join", core_word, outs, up_keep, down_keep, *sent
    )
    outs = (((wide_half // 2, 512), jnp.float32),) * 2
    keep, send = with_core(
        last_sum_kernel,
        "attn_sum",
        core_word,
        outs,
        *attn_sums[0],
        attn_moves[1],
        waits=(outputs, grads, gain_parts, up_grad),
    )
    spots = tuple((i * 128, (i + 1) * 128, i * 256) for i in range(3))
    outs = (((wide_half // 2, 768), jnp.float32), ((256, wide_half // 2), jnp.float32))
    kernel = functools.partial(joined_kernel, spots)
    qkv_grad, out_grad = with_core(
        kernel, "attn_join", core_word, outs, keep, flip_pairs(send, 1)
    )
    qkv_grad = qkv_grad.reshape(wide_half // 2, 3, -1)

    return (
        outputs[None],
        grads[None],
        gains_grad[None],
        qkv_grad[None],
        out_grad[None],
        up_grad[None],
        down_grad[None],
    )


def takes_chips(sizes):
    return sizes["section"] == 2 and sizes["dp"] == 4 and sizes["tensor"] == 4


def solution(mesh):
    placed = (
        P("dp", "tensor", None),
        P("dp", "tensor", None),
        P("dp", "tensor"),
        P(),
        P("section", None, None),
        P("section", None, None, "tensor"),
        P("section", "tensor", None),
        P("section", None, "tensor"),
        P("section", "tensor", None),
    )
    body = per_chip if takes_chips(dict(mesh.shape)) else per_device
    return jax.shard_map(
        body,
        mesh=mesh,
        in_specs=placed,
        out_specs=(
            P("section", "dp", "tensor", None),
            P("section", "dp", "tensor", None),
            P("section", None, ("dp", "tensor")),
            P("section", "dp", None, "tensor"),
            P("section", "tensor", "dp"),
            P("section", "dp", "tensor"),
            P("section", "tensor", "dp"),
        ),
        check_vma=False,
    )
```

```python
import functools
import math

import jax
import jax.numpy as jnp
from jax import lax
from jax.experimental import pallas as pl
from jax.experimental.pallas import tpu as pltpu
from jax.sharding import PartitionSpec as P

HEAD_DIM = 64


NORM_EPSILON = 1e-06
TILE = 128
PAIR_WORK = 1024
MODEL_HALF = 512
QKV = slice(0, 384)
OUT = slice(384, 512)
CHUNK = 32
KERNEL_VMEM = 20 << 20
ROWS_VMEM = 3 << 20


def shifted(block, axis, distance):
    devices = range(lax.axis_size(axis))
    route = [(i - distance, i) for i in devices if i - distance in devices]
    return lax.ppermute(block, axis, route)


def norm_rows(vector, weight_gain):
    return (
        vector
        * lax.rsqrt(jnp.mean(vector * vector, axis=-1, keepdims=True) + NORM_EPSILON)
        * weight_gain
    )


def rotary_tables(seq_len, head_width):
    half_width = head_width // 2
    freqs = 10000.0 ** (-2.0 * jnp.arange(half_width, dtype=jnp.float32) / head_width)
    angles = jnp.arange(seq_len, dtype=jnp.float32)[:, None] * freqs[None, :]
    return (jnp.cos(angles), jnp.sin(angles))


def rotate(vector, cos_table, sin_table):
    first_half, second_half = jnp.split(vector, 2, axis=-1)
    cos_part = cos_table[:, None, :]
    sin_part = sin_table[:, None, :]
    return jnp.concatenate(
        [
            first_half * cos_part - second_half * sin_part,
            second_half * cos_part + first_half * sin_part,
        ],
        axis=-1,
    )


def contract(left_rows, right_rows):
    return lax.dot_general(
        left_rows, right_rows, (((0,), (0,)), ((), ())), preferred_element_type=jnp.float32
    )


def gather_rows(row_values, weight):

    def project(shard_rows, offset):
        return (shard_rows, jnp.dot(shard_rows, weight, preferred_element_type=jnp.float32))

    return project(lax.all_gather(row_values, "tensor", axis=0, tiled=True), jnp.int32(0))


def scatter_rows(row_values, weight, row_count):

    def partial_term(offset, span):
        return jnp.dot(row_values, weight, preferred_element_type=jnp.float32)

    return lax.psum_scatter(
        partial_term(jnp.int32(0), lax.axis_size("tensor") * row_count),
        "tensor",
        scatter_dimension=0,
        tiled=True,
    )


def gather_grads(row_values, weight):

    def project(shard_rows, offset):
        return (shard_rows, jnp.dot(shard_rows, weight.T, preferred_element_type=jnp.float32))

    return project(lax.all_gather(row_values, "tensor", axis=0, tiled=True), jnp.int32(0))


def scatter_grads(row_values, weight, row_count):

    def partial_term(offset, span):
        return jnp.dot(row_values, weight.T, preferred_element_type=jnp.float32)

    return lax.psum_scatter(
        partial_term(jnp.int32(0), lax.axis_size("tensor") * row_count),
        "tensor",
        scatter_dimension=0,
        tiled=True,
    )


def attention_probs(queries, key_rows):
    scores = jnp.einsum(
        "qhd,khd->hqk", queries, key_rows, preferred_element_type=jnp.float32
    ) * HEAD_DIM ** (-0.5)
    length = queries.shape[0]
    positions = jnp.arange(length, dtype=jnp.int32)
    causal = positions[:, None] >= positions[None, :]
    scores = jnp.where(causal[None], scores, -1e30)
    expos = jnp.exp(scores - jnp.max(scores, axis=-1, keepdims=True))
    return expos / jnp.sum(expos, axis=-1, keepdims=True)


def layer_forward(layer_input, weights):
    gains, w_qkv, w_out, w_up, w_down = weights
    row_count, model_width = layer_input.shape
    attn_in = norm_rows(layer_input, gains[0]).astype(jnp.bfloat16)
    gathered_a, qkv = gather_rows(attn_in, w_qkv.reshape(model_width, -1))
    length = qkv.shape[0]
    head_count = w_qkv.shape[2] // HEAD_DIM
    qkv = qkv.reshape(length, 3, head_count, HEAD_DIM)
    cos_table, sin_table = rotary_tables(length, HEAD_DIM)
    queries = rotate(qkv[:, 0], cos_table, sin_table).astype(jnp.bfloat16)
    key_rows = rotate(qkv[:, 1], cos_table, sin_table).astype(jnp.bfloat16)
    values = qkv[:, 2].astype(jnp.bfloat16)
    attn_probs = attention_probs(queries, key_rows).astype(jnp.bfloat16)
    mixed = jnp.einsum("hqk,khd->qhd", attn_probs, values, preferred_element_type=jnp.float32)
    mixed = mixed.reshape(length, -1).astype(jnp.bfloat16)
    attn_branch = scatter_rows(mixed, w_out, row_count)
    hidden = layer_input + norm_rows(attn_branch, gains[1])
    mlp_in = norm_rows(hidden, gains[2]).astype(jnp.bfloat16)
    gathered_c, up_act = gather_rows(mlp_in, w_up)
    gelu_out = jax.nn.gelu(up_act, approximate=True).astype(jnp.bfloat16)
    down_branch = scatter_rows(gelu_out, w_down, row_count)
    result = hidden + norm_rows(down_branch, gains[3])
    kept_values = (
        gathered_a,
        queries,
        key_rows,
        values,
        mixed,
        attn_branch,
        hidden,
        gathered_c,
        up_act,
        gelu_out,
        down_branch,
    )
    return (result, kept_values)


def layer_backward(layer_input, grad_result, kept_values, weights):
    gains, w_qkv, w_out, w_up, w_down = weights
    (
        gathered_a,
        queries,
        key_rows,
        values,
        mixed,
        attn_branch,
        hidden,
        gathered_c,
        up_act,
        gelu_out,
        down_branch,
    ) = kept_values
    row_count, model_width = layer_input.shape
    pullback = jax.vjp(norm_rows, down_branch, gains[3])[1]
    grad_down, gain_three = pullback(grad_result)
    gathered_dd, grad_gelu = gather_grads(grad_down.astype(jnp.bfloat16), w_down)
    down_total = contract(gelu_out, gathered_dd)
    pullback = jax.vjp(lambda vector: jax.nn.gelu(vector, approximate=True), up_act)[1]
    grad_up = pullback(grad_gelu)[0].astype(jnp.bfloat16)
    up_total = contract(gathered_c, grad_up)
    grad_mlp = scatter_grads(grad_up, w_up, row_count)
    pullback = jax.vjp(norm_rows, hidden, gains[2])[1]
    grad_norm_mlp, gain_two = pullback(grad_mlp)
    grad_hidden = grad_result + grad_norm_mlp
    pullback = jax.vjp(norm_rows, attn_branch, gains[1])[1]
    grad_attn, gain_one = pullback(grad_hidden)
    gathered_da, grad_mixed = gather_grads(grad_attn.astype(jnp.bfloat16), w_out)
    out_total = contract(mixed, gathered_da)
    length = grad_mixed.shape[0]
    head_count = w_qkv.shape[2] // HEAD_DIM
    grad_mixed = grad_mixed.astype(jnp.bfloat16).reshape(length, head_count, HEAD_DIM)
    attn_probs = attention_probs(queries, key_rows)
    probs_low = attn_probs.astype(jnp.bfloat16)
    grad_probs = jnp.einsum("qhd,khd->hqk", grad_mixed, values, preferred_element_type=jnp.float32)
    grad_values = jnp.einsum(
        "hqk,qhd->khd", probs_low, grad_mixed, preferred_element_type=jnp.float32
    )
    row_dots = jnp.sum(grad_probs * attn_probs, axis=-1, keepdims=True)
    grad_scores = (attn_probs * (grad_probs - row_dots)).astype(jnp.bfloat16)
    scale_value = HEAD_DIM ** (-0.5)
    grad_queries = (
        jnp.einsum("hqk,khd->qhd", grad_scores, key_rows, preferred_element_type=jnp.float32)
        * scale_value
    )
    grad_keys = (
        jnp.einsum("hqk,qhd->khd", grad_scores, queries, preferred_element_type=jnp.float32)
        * scale_value
    )
    cos_table, sin_table = rotary_tables(length, HEAD_DIM)
    pullback = jax.vjp(lambda vector: rotate(vector, cos_table, sin_table), grad_queries)[1]
    grad_q_raw = pullback(grad_queries)[0]
    grad_k_raw = pullback(grad_keys)[0]
    grad_qkv = (
        jnp.stack([grad_q_raw, grad_k_raw, grad_values], axis=1)
        .reshape(length, -1)
        .astype(jnp.bfloat16)
    )
    qkv_total = contract(gathered_a, grad_qkv).reshape(model_width, 3, -1)
    grad_attn_in = scatter_grads(grad_qkv, w_qkv.reshape(model_width, -1), row_count)
    pullback = jax.vjp(norm_rows, layer_input, gains[0])[1]
    grad_norm_in, gain_zero = pullback(grad_attn_in)
    grad_input = grad_hidden + grad_norm_in
    gain_total = jnp.stack([gain_zero, gain_one, gain_two, gain_three])
    return (grad_input, (gain_total, qkv_total, out_total, up_total, down_total))


def lagged(first_section, stacked):
    blank = jnp.zeros_like(stacked[:1])
    earlier = jnp.concatenate([blank, stacked[:-1]])
    later = jnp.concatenate([stacked[1:], blank])
    return jnp.where(first_section, earlier, later)


def per_device(
    inputs,
    out_cotangent,
    group_ids,
    group_weights,
    gains,
    qkv_weight,
    out_weight,
    up_weight,
    down_weight,
):
    weights = (gains[0], qkv_weight[0], out_weight[0], up_weight[0], down_weight[0])
    micro_count, row_count, model_width = inputs.shape
    first_section = lax.axis_index("section") == 0
    group_count = group_weights.shape[0]
    matches = group_ids[..., None] == jnp.arange(group_count, dtype=jnp.int32)
    row_scale = jnp.sum(jnp.where(matches, group_weights, 0.0), axis=-1)
    scaled = out_cotangent.astype(jnp.float32) * row_scale[..., None]
    padded = jnp.concatenate([inputs, jnp.zeros((1, row_count, model_width), jnp.bfloat16)])

    def forward_tick(received, fresh_input):
        layer_input = jnp.where(first_section, fresh_input, received)
        result, kept_values = layer_forward(layer_input.astype(jnp.float32), weights)
        result_low = result.astype(jnp.bfloat16)
        outgoing = shifted(result_low, "section", 1)
        stashed = ()
        return (outgoing, (layer_input, result_low, stashed))

    start_rows = jnp.zeros((row_count, model_width), jnp.bfloat16)
    _, (layer_inputs, layer_results, stashed) = lax.scan(forward_tick, start_rows, padded)
    layer_outputs = jnp.where(first_section, layer_results[:-1], layer_results[1:])[None]
    back_inputs = lagged(first_section, layer_inputs)
    back_stash = jax.tree.map(lambda stacked: lagged(first_section, stacked), stashed)
    grad_padded = jnp.concatenate([scaled, jnp.zeros((1, row_count, model_width), jnp.float32)])
    tick_index = jnp.arange(micro_count + 1, dtype=jnp.int32)
    tick_valid = jnp.where(first_section, tick_index >= 1, tick_index < micro_count).astype(
        jnp.float32
    )

    def backward_tick(carry, step_item):
        received, totals = carry
        layer_input, cotangent, valid_now, stash_now = step_item
        grad_now = jnp.where(first_section, received.astype(jnp.float32), cotangent)
        input_now = layer_input.astype(jnp.float32)
        kept_values = layer_forward(input_now, weights)[1]
        grad_input, layer_grads = layer_backward(input_now, grad_now, kept_values, weights)
        totals = jax.tree.map(lambda total, update: total + valid_now * update, totals, layer_grads)
        grad_low = grad_input.astype(jnp.bfloat16)
        outgoing = shifted(grad_low, "section", -1)
        return ((outgoing, totals), grad_low)

    start_totals = (
        jnp.zeros((4, model_width), jnp.float32),
        jnp.zeros(qkv_weight.shape[1:], jnp.float32),
        jnp.zeros(out_weight.shape[1:], jnp.float32),
        jnp.zeros(up_weight.shape[1:], jnp.float32),
        jnp.zeros(down_weight.shape[1:], jnp.float32),
    )
    (_, totals), grad_lows = lax.scan(
        backward_tick,
        (start_rows, start_totals),
        (back_inputs, grad_padded, tick_valid, back_stash),
    )
    input_grads = jnp.where(first_section, grad_lows[1:], grad_lows[:-1])[None]
    gain_total, qkv_total, out_total, up_total, down_total = totals
    gains_grad = lax.psum_scatter(gain_total, ("dp", "tensor"), scatter_dimension=1, tiled=True)
    qkv_grad, out_grad, up_grad, down_grad = (
        lax.psum_scatter(
            qkv_total.astype(jnp.bfloat16), "dp", scatter_dimension=0, tiled=True
        ).astype(jnp.float32),
        lax.psum_scatter(
            out_total.astype(jnp.bfloat16), "dp", scatter_dimension=1, tiled=True
        ).astype(jnp.float32),
        lax.psum_scatter(
            up_total.astype(jnp.bfloat16), "dp", scatter_dimension=0, tiled=True
        ).astype(jnp.float32),
        lax.psum_scatter(
            down_total.astype(jnp.bfloat16), "dp", scatter_dimension=1, tiled=True
        ).astype(jnp.float32),
    )
    return (
        layer_outputs,
        input_grads,
        gains_grad[None],
        qkv_grad[None],
        out_grad[None],
        up_grad[None],
        down_grad[None],
    )


def rotated(block, cos_rows, sin_rows):
    lane = lax.broadcasted_iota(jnp.int32, block.shape, 1)
    ahead = pltpu.roll(block, 96, 1)
    behind = pltpu.roll(block, 32, 1)
    swapped = jnp.where(lane % 64 < 32, ahead, behind)
    return block * cos_rows + swapped * sin_rows


def dot_nt(left, right):
    return lax.dot_general(
        left, right, (((1,), (1,)), ((), ())), preferred_element_type=jnp.float32
    )


def dot_nn(left, right):
    return jnp.dot(left, right, preferred_element_type=jnp.float32)


def model_weight(owns, others, cols):
    sides = [jnp.concatenate([ref[:, cols] for ref in refs], axis=1) for refs in (owns, others)]
    return jnp.concatenate(sides, axis=0)


def stacked_up(values):
    return jnp.concatenate(values, axis=0)


def edge_masks(core, rows):
    key = lax.broadcasted_iota(jnp.int32, (rows, 2 * rows), 0)
    query = lax.broadcasted_iota(jnp.int32, (rows, 2 * rows), 1)
    mine = query < rows
    place = jnp.where(mine, query + core * rows, query - rows + (1 - core) * rows)
    return (key + core * rows <= place, key + (1 - core) * rows <= place)


def both_sides(value, half, start, stop, axis=0):
    if axis == 0:
        return jnp.concatenate([value[start:stop], value[half + start : half + stop]], axis=0)
    return jnp.concatenate([value[:, start:stop], value[:, half + start : half + stop]], axis=1)


def hidden_scores(scores, masks, tile, step):
    seen = step * tile
    pieces = []
    for side in range(2):
        base = side * (seen + tile)
        if seen:
            pieces.append(scores[base : base + seen])
        pieces.append(jnp.where(masks[side], scores[base + seen : base + seen + tile], -1e30))
    return jnp.concatenate(pieces, axis=0)


def one_head(rows, head):
    lane = lax.broadcasted_iota(jnp.int32, rows.shape, 1)
    return jnp.where(lane // 64 == head, rows, jnp.zeros_like(rows))


def pick_piece(weight, owns, others, cols):
    for j, (own, other) in enumerate(zip(owns, others)):

        @pl.when(pl.program_id(0) == j)
        def _():
            size = own.shape[0]
            weight[:size] = own[:, cols]
            weight[size:] = other[:, cols]


def attend_kernel(pieces, core_ref, cos_ref, sin_ref, own_rows, other_rows, *refs):
    owns, others = refs[:pieces], refs[pieces : 2 * pieces]
    q_ref, k_ref, v_ref, lse_ref, mix_ref, weight = refs[2 * pieces :]
    half = own_rows.shape[0]
    tile = TILE
    pick_piece(weight, owns, others, QKV)
    proj = dot_nn(stacked_up([own_rows[...], other_rows[...]]), weight[...])
    cos_rows, sin_rows = cos_ref[...], sin_ref[...]
    q = (rotated(proj[:, :128], cos_rows, sin_rows) * HEAD_DIM ** (-0.5)).astype(jnp.bfloat16)
    k = rotated(proj[:, 128:256], cos_rows, sin_rows).astype(jnp.bfloat16)
    v32 = proj[:, 256:]
    q_ref[0] = q
    k_ref[0] = k
    v_ref[0] = v32.astype(jnp.bfloat16)
    v_flip = v32.T.astype(jnp.bfloat16)
    masks = edge_masks(core_ref[0], tile)

    def scored(step, head):
        stop = (step + 1) * tile
        q_head = one_head(both_sides(q, half, step * tile, stop), head)
        return hidden_scores(dot_nt(both_sides(k, half, 0, stop), q_head), masks, tile, step)

    units = [(step, head) for step in range(half // tile) for head in range(2)]
    ahead = scored(*units[0])
    outs = []
    for spot, (step, head) in enumerate(units):
        scores = ahead
        if spot + 1 < len(units):
            ahead = scored(*units[spot + 1])
        stop = (step + 1) * tile
        top = jnp.max(scores, axis=0, keepdims=True)
        expos = jnp.exp(scores - top)
        total = jnp.sum(expos, axis=0, keepdims=True)
        lse = top + jnp.log(total)
        lse_ref[0, head : head + 1, step * tile : stop] = lse[:, :tile]
        lse_ref[0, head : head + 1, half + step * tile : half + stop] = lse[:, tile:]
        v_cols = both_sides(v_flip, half, 0, stop, axis=1)
        out = dot_nn(v_cols[64 * head : 64 * head + 64], expos.astype(jnp.bfloat16))
        outs.append(out * (1.0 / total))
        if head == 1:
            mixed = jnp.concatenate(outs, axis=0).T.astype(jnp.bfloat16)
            outs = []
            mix_ref[step * tile : stop, :] = mixed[:tile]
            mix_ref[half + step * tile : half + stop, :] = mixed[tile:]


def attend_back_kernel(pieces, core_ref, cos_ref, sin_ref, own_rows, other_rows, *refs):
    owns, others = refs[:pieces], refs[pieces : 2 * pieces]
    q_ref, k_ref, v_ref, lse_ref, out_ref, weight, dq, dk, dv = refs[2 * pieces :]
    half = own_rows.shape[0]
    tile = TILE
    pick_piece(weight, owns, others, OUT)
    rows = stacked_up([own_rows[...], other_rows[...]])
    d_mixed = dot_nn(rows, weight[...]).astype(jnp.bfloat16)
    q, k, v = q_ref[0], k_ref[0], v_ref[0]
    k_flip = k.astype(jnp.float32).T.astype(jnp.bfloat16)
    masks = edge_masks(core_ref[0], tile)
    steps = half // tile

    def scored(step, head):
        stop = (step + 1) * tile
        q_head = one_head(both_sides(q, half, step * tile, stop), head)
        g_head = one_head(both_sides(d_mixed, half, step * tile, stop), head)
        scores = hidden_scores(dot_nt(both_sides(k, half, 0, stop), q_head), masks, tile, step)
        return q_head, g_head, scores, dot_nt(both_sides(v, half, 0, stop), g_head)

    units = [(step, head) for step in reversed(range(steps)) for head in range(2)]
    ahead = scored(*units[0])
    dq_flips = []
    dk_sum = dv_sum = None
    for spot, (step, head) in enumerate(units):
        q_head, g_head, scores, d_probs = ahead
        if spot + 1 < len(units):
            ahead = scored(*units[spot + 1])
        stop = (step + 1) * tile
        lse = both_sides(lse_ref[0], half, step * tile, stop, axis=1)
        probs = jnp.exp(scores - lse[head : head + 1])
        dots = jnp.sum(probs * d_probs, axis=0, keepdims=True)
        d_scores = (probs * (d_probs - dots)).astype(jnp.bfloat16)
        dv_part = dot_nn(probs.astype(jnp.bfloat16), g_head)
        dk_part = dot_nn(d_scores, q_head)
        k_cols = both_sides(k_flip, half, 0, stop, axis=1)
        dq_flips.append(dot_nn(k_cols[64 * head : 64 * head + 64], d_scores))
        if head == 0:
            dv_sum, dk_sum = dv_part, dk_part
            continue
        dv_sum, dk_sum = dv_sum + dv_part, dk_sum + dk_part
        dq_rows = jnp.concatenate(dq_flips, axis=0).T * HEAD_DIM ** (-0.5)
        dq_flips = []
        dq[step * tile : stop] = dq_rows[:tile]
        dq[half + step * tile : half + stop] = dq_rows[tile:]
        for base, part in ((0, slice(0, stop)), (half, slice(stop, 2 * stop))):
            if step == steps - 1:
                dk[base : base + stop] = dk_sum[part]
                dv[base : base + stop] = dv_sum[part]
            else:
                dk[base : base + stop] += dk_sum[part]
                dv[base : base + stop] += dv_sum[part]
    cos_rows, sin_rows = cos_ref[...], -sin_ref[...]
    out_ref[:, :128] = rotated(dq[...], cos_rows, sin_rows).astype(jnp.bfloat16)
    out_ref[:, 128:256] = rotated(dk[...], cos_rows, sin_rows).astype(jnp.bfloat16)
    out_ref[:, 256:] = dv[...].astype(jnp.bfloat16)


def split_rows(total, own_ref, other_ref):
    half = own_ref.shape[0]
    own_ref[...] = total[:half]
    other_ref[...] = total[half:].astype(jnp.bfloat16)


def to_model_kernel(lefts, pieces, cols, *refs):
    left, refs = jnp.concatenate([ref[...] for ref in refs[:lefts]], axis=1), refs[lefts:]
    weight = model_weight(refs[:pieces], refs[pieces : 2 * pieces], cols)
    split_rows(dot_nt(left, weight), *refs[2 * pieces :])


def mlp_down_kernel(pieces, left_ref, *refs):
    sides = [stacked_up([ref[...] for ref in side]) for side in (refs[:pieces], refs[pieces:-2])]
    split_rows(dot_nn(left_ref[...], jnp.concatenate(sides, axis=1)), *refs[-2:])


def gelu_both(up_act):
    root = math.sqrt(2.0 / math.pi)
    square = up_act * up_act
    rise = 0.5 + 0.5 * jnp.tanh(up_act * (root + root * 0.044715 * square))
    value = up_act * rise
    slope = rise + value * (1.0 - rise) * (2.0 * root + 6.0 * root * 0.044715 * square)
    return value, slope


def mlp_up_kernel(pieces, own_rows, other_rows, *refs):
    owns, others = refs[:pieces], refs[pieces : 2 * pieces]
    gelu_ref, slope_ref = refs[2 * pieces :]
    half = own_rows.shape[0]
    size = owns[0].shape[1]
    step = half // 2
    units = [(j, i) for j in range(pieces) for i in range(4)]

    def product(j, i):
        rows = (own_rows, other_rows)[i // 2][i % 2 * step : (i % 2 + 1) * step]
        return dot_nn(rows, stacked_up([owns[j][...], others[j][...]]))

    ahead = product(*units[0])
    for spot, (j, i) in enumerate(units):
        up_act = ahead
        if spot + 1 < len(units):
            ahead = product(*units[spot + 1])
        value, slope = gelu_both(up_act)
        gelu_ref[i * step : (i + 1) * step, j * size : (j + 1) * size] = value.astype(jnp.bfloat16)
        slope_ref[i * step : (i + 1) * step, j * size : (j + 1) * size] = slope.astype(
            jnp.bfloat16
        )


def mlp_up_back_kernel(pieces, own_rows, other_rows, slope_ref, *refs):
    owns, others = refs[:pieces], refs[pieces : 2 * pieces]
    out_ref, weight, slope, sems = refs[2 * pieces :]
    half = own_rows.shape[1] // 2
    size = owns[0].shape[0]
    order = list(reversed(range(pieces)))
    copies = []
    for j in order:
        sources = (owns[j], others[j], slope_ref.at[:, pl.ds(j * size, size)])
        targets = (
            weight.at[j, :, pl.ds(0, half)],
            weight.at[j, :, pl.ds(half, half)],
            slope.at[:, pl.ds(j * size, size)],
        )
        copies.append(
            [
                pltpu.make_async_copy(source, target, sems.at[j, i])
                for i, (source, target) in enumerate(zip(sources, targets))
            ]
        )
        for copy in copies[-1]:
            copy.start()
    rows = stacked_up([own_rows[...], other_rows[...]])
    for j, arriving in zip(order, copies):
        cols = slice(j * size, (j + 1) * size)
        for copy in arriving:
            copy.wait()
        d_gelu = dot_nt(rows, weight[j])
        out_ref[:, cols] = (d_gelu * slope[:, cols].astype(jnp.float32)).astype(jnp.bfloat16)


def inverse_size(rows):
    return lax.rsqrt(jnp.mean(rows * rows, axis=-1, keepdims=True) + NORM_EPSILON)


def norm_back(rows, gain, grad):
    scale = inverse_size(rows)
    weighted = grad * gain
    inner = jnp.mean(rows * weighted, axis=-1, keepdims=True)
    return scale * weighted - rows * (scale * scale * scale * inner), rows * scale * grad


def folded(rows):
    return jnp.sum(rows.reshape(rows.shape[0] // 8, 8, rows.shape[1]), axis=0)


def wide(ref, spot):
    return ref[spot, :].astype(jnp.float32)


def by_chunks(count, body, sums=0, width=0):
    def one(i, carry):
        more = body(pl.ds(pl.multiple_of(i * CHUNK, CHUNK), CHUNK))
        return tuple(old + folded(new) for old, new in zip(carry, more))

    start = tuple(jnp.zeros((8, width), jnp.float32) for _ in range(sums))
    totals = lax.fori_loop(0, count // CHUNK, one, start)
    return [jnp.sum(total, axis=0, keepdims=True) for total in totals]


def norm_in_kernel(gain_ref, rows_ref, out_ref):
    def body(spot):
        rows = wide(rows_ref, spot)
        out_ref[spot, :] = (rows * inverse_size(rows) * gain_ref[0:1]).astype(jnp.bfloat16)
        return ()

    by_chunks(rows_ref.shape[0], body)


def after_attention_kernel(
    gain_ref, rows_ref, own_ref, other_ref, branch_ref, hidden_ref, out_ref
):
    def body(spot):
        branch = own_ref[spot, :] + wide(other_ref, spot)
        hidden = wide(rows_ref, spot) + branch * inverse_size(branch) * gain_ref[1:2]
        branch_ref[spot, :] = branch
        hidden_ref[spot, :] = hidden
        out_ref[spot, :] = (hidden * inverse_size(hidden) * gain_ref[2:3]).astype(jnp.bfloat16)
        return ()

    by_chunks(rows_ref.shape[0], body)


def after_mlp_kernel(gain_ref, hidden_ref, own_ref, other_ref, branch_ref, out_ref):
    def body(spot):
        branch = own_ref[spot, :] + wide(other_ref, spot)
        branch_ref[spot, :] = branch
        result = hidden_ref[spot, :] + branch * inverse_size(branch) * gain_ref[3:4]
        out_ref[spot, :] = result.astype(jnp.bfloat16)
        return ()

    by_chunks(hidden_ref.shape[0], body)


def into_mlp_back_kernel(gain_ref, grad_ref, branch_ref, out_ref, sum_ref):
    def body(spot):
        d_rows, d_gain = norm_back(branch_ref[spot, :], gain_ref[3:4], wide(grad_ref, spot))
        out_ref[spot, :] = d_rows.astype(jnp.bfloat16)
        return (d_gain,)

    (sum_ref[...],) = by_chunks(grad_ref.shape[0], body, 1, grad_ref.shape[1])


def into_attention_back_kernel(
    gain_ref, grad_ref, own_ref, other_ref, hidden_ref, branch_ref, d_hidden_ref, out_ref, *sums
):
    def body(spot):
        d_rows = own_ref[spot, :] + wide(other_ref, spot)
        d_rows, d_gain = norm_back(hidden_ref[spot, :], gain_ref[2:3], d_rows)
        d_hidden = wide(grad_ref, spot) + d_rows
        d_hidden_ref[spot, :] = d_hidden
        d_rows, d_first = norm_back(branch_ref[spot, :], gain_ref[1:2], d_hidden)
        out_ref[spot, :] = d_rows.astype(jnp.bfloat16)
        return (d_first, d_gain)

    totals = by_chunks(grad_ref.shape[0], body, 2, grad_ref.shape[1])
    sums[0][...], sums[1][...] = totals


def out_of_layer_kernel(gain_ref, rows_ref, own_ref, other_ref, d_hidden_ref, out_ref, sum_ref):
    def body(spot):
        d_rows = own_ref[spot, :] + wide(other_ref, spot)
        d_rows, d_gain = norm_back(wide(rows_ref, spot), gain_ref[0:1], d_rows)
        out_ref[spot, :] = (d_hidden_ref[spot, :] + d_rows).astype(jnp.bfloat16)
        return (d_gain,)

    (sum_ref[...],) = by_chunks(rows_ref.shape[0], body, 1, rows_ref.shape[1])


def work(flops, arrays):
    size = sum(math.prod(array.shape) * jnp.dtype(array.dtype).itemsize for array in arrays)
    return pl.CostEstimate(flops=flops, bytes_accessed=size, transcendentals=0)


def without(kernel, first, count):
    return lambda *refs: kernel(*refs[:first], *refs[first + count :])


def on_chip(kernel, name, outs, *operands, limit=ROWS_VMEM, flops=0, waits=()):
    shapes = [jax.ShapeDtypeStruct(shape, dtype) for shape, dtype in outs]
    space = pl.BlockSpec(memory_space=pltpu.VMEM)
    return pl.pallas_call(
        without(kernel, len(operands), len(waits)),
        in_specs=[space] * len(operands) + [pl.BlockSpec(memory_space=pl.ANY)] * len(waits),
        out_specs=[space] * len(outs),
        out_shape=shapes,
        compiler_params=pltpu.CompilerParams(vmem_limit_bytes=limit),
        cost_estimate=work(flops, (*operands, *shapes)),
        name=name,
    )(*operands, *waits)


def whole_block(array):
    return pl.BlockSpec(array.shape, lambda j: (0,) * array.ndim)


def by_pairs(kernel, name, core, operands, pieces, blocks, outs, scratch, flops, waits):
    shapes = [jax.ShapeDtypeStruct(shape, dtype) for shape, dtype, _ in outs]
    taken = 1 + len(operands) + 2 * len(pieces[0]) + len(blocks)
    return pl.pallas_call(
        without(functools.partial(kernel, len(pieces[0])), taken, len(waits)),
        grid=(len(pieces[0]),),
        in_specs=[pl.BlockSpec(memory_space=pltpu.SMEM)]
        + [whole_block(array) for array in (*operands, *pieces[0], *pieces[1])]
        + [spec for _, spec in blocks]
        + [pl.BlockSpec(memory_space=pl.ANY)] * len(waits),
        out_specs=[spec for _, _, spec in outs],
        out_shape=shapes,
        scratch_shapes=scratch,
        compiler_params=pltpu.CompilerParams(vmem_limit_bytes=KERNEL_VMEM),
        cost_estimate=work(flops, (*operands, *pieces[0], *pieces[1], *shapes)),
        name=name,
    )(core, *operands, *pieces[0], *pieces[1], *[array for array, _ in blocks], *waits)


def mlp_up_back(rows, slope, pieces, waits):
    length, units = slope.shape
    unit, half = pieces[0][0].shape
    count = len(pieces[0])
    every, space = pl.BlockSpec(memory_space=pl.ANY), pl.BlockSpec(memory_space=pltpu.VMEM)
    far = pl.BlockSpec(memory_space=pltpu.HBM)
    return pl.pallas_call(
        without(functools.partial(mlp_up_back_kernel, count), 3 + 2 * count, len(waits)),
        in_specs=[space] * 2 + [far] * (1 + 2 * count) + [every] * len(waits),
        out_specs=space,
        out_shape=jax.ShapeDtypeStruct((length, units), jnp.bfloat16),
        scratch_shapes=[
            pltpu.VMEM((count, unit, 2 * half), jnp.bfloat16),
            pltpu.VMEM((length, units), jnp.bfloat16),
            pltpu.SemaphoreType.DMA((count, 3)),
        ],
        compiler_params=pltpu.CompilerParams(vmem_limit_bytes=KERNEL_VMEM),
        name="mlp_up_back",
    )(*rows, slope, *pieces[0], *pieces[1], *waits)


def attend(core, tables, rows, pieces, waits):
    half, features = rows[0].shape
    length, count = 2 * half, len(pieces[0])
    lanes = ((count, length, 128), jnp.bfloat16, pl.BlockSpec((1, length, 128), lambda j: (j, 0, 0)))
    lse = ((count, 2, length), jnp.float32, pl.BlockSpec((1, 2, length), lambda j: (j, 0, 0)))
    mixed = ((length, count * 128), jnp.bfloat16, pl.BlockSpec((length, 128), lambda j: (0, j)))
    return by_pairs(
        attend_kernel,
        "attend",
        core,
        (*tables, *rows),
        pieces,
        (),
        (lanes, lanes, lanes, lse, mixed),
        [pltpu.VMEM((features, 384), jnp.bfloat16)],
        count * length * (2 * features * 384 + 2 * PAIR_WORK * length),
        waits,
    )


def attend_back(core, tables, rows, pieces, base, waits, q, k, v, lse):
    half, features = rows[0].shape
    length, count = 2 * half, len(pieces[0])
    lanes = pl.BlockSpec((1, length, 128), lambda j: (base + j, 0, 0))
    lse_spec = pl.BlockSpec((1, 2, length), lambda j: (base + j, 0, 0))
    out = ((length, count * 384), jnp.bfloat16, pl.BlockSpec((length, 384), lambda j: (0, j)))
    return by_pairs(
        attend_back_kernel,
        "attend_back",
        core,
        (*tables, *rows),
        pieces,
        ((q, lanes), (k, lanes), (v, lanes), (lse, lse_spec)),
        (out,),
        [pltpu.VMEM((features, 128), jnp.bfloat16)] + [pltpu.VMEM((length, 128), jnp.float32)] * 3,
        count * length * (2 * features * 128 + 5 * PAIR_WORK * length),
        waits,
    )[0]


def exchanged(parts):
    return parts[0], flip_pairs(parts[1], 1)


def model_rows(kernel, name, lefts, pieces, waits=()):
    length, width = lefts[0].shape[0], 2 * MODEL_HALF
    outs = (((length // 2, width), jnp.float32), ((length // 2, width), jnp.bfloat16))
    hidden = sum(left.shape[1] for left in lefts)
    more = {"limit": KERNEL_VMEM, "flops": 2 * length * width * hidden, "waits": waits}
    return exchanged(on_chip(kernel, name, outs, *lefts, *pieces[0], *pieces[1], **more))


def flip_pairs(block, distance):
    size = lax.axis_size("dp")
    return lax.ppermute(block, "dp", [(i, i ^ distance) for i in range(size)])


def passed_on(block, step):
    size = lax.axis_size("tensor")
    return lax.ppermute(block, "tensor", [(i, (i + step) % size) for i in range(size)])


def dot_tn(left, right):
    return lax.dot_general(
        left, right, (((0,), (0,)), ((), ())), preferred_element_type=jnp.float32
    )


def fetch(first_ref, zeros, ones, buffers, sems):
    for section, sources in enumerate((zeros, ones)):

        @pl.when(first_ref[0] == section)
        def _():
            for i, (source, buffer) in enumerate(zip(sources, buffers)):
                pltpu.make_async_copy(source, buffer, sems.at[i]).start()

    def arrived(*places):
        for i in places:
            pltpu.make_async_copy(zeros[i], buffers[i], sems.at[i]).wait()

    return arrived


def mlp_grads_kernel(base, section_ref, *refs):
    (own_one, other_one, own_two, other_two), (rows, d_up, gelu, d_down, sems) = refs[12:16], refs[16:]
    half, size = own_one.shape[0] // 2, own_one.shape[1]
    cols = pl.ds(base * size, 2 * size)

    def parts(own_rows, other_rows, d_up_ref, gelu_ref, own_grad, other_grad):
        whole = (d_up_ref.at[:, cols], gelu_ref.at[:, cols])
        return (own_rows, other_rows, *whole, own_grad, other_grad)

    count = refs[0].shape[0]
    buffers = (
        rows.at[pl.ds(0, count)],
        rows.at[pl.ds(count, count)],
        d_up,
        gelu,
        d_down.at[pl.ds(0, count)],
        d_down.at[pl.ds(count, count)],
    )
    arrived = fetch(section_ref, parts(*refs[:6]), parts(*refs[6:12]), buffers, sems)
    for j, own, other in ((1, own_two, other_two), (0, own_one, other_one)):
        cols = slice(j * size, (j + 1) * size)
        if j == 1:
            arrived(0, 1, 2)
        up = dot_tn(rows[...], d_up[:, cols])
        own[:half] = up[:half]
        other[:half] = up[half:].astype(jnp.bfloat16)
        if j == 1:
            arrived(3, 4, 5)
        down = dot_tn(gelu[:, cols], d_down[...])
        own[half:] = down[:, :half]
        other[half:] = down[:, half:].astype(jnp.bfloat16)


def attn_grads_kernel(base, section_ref, *refs):
    (own_one, other_one, own_two, other_two), (rows, d_qkv, mixed, d_attn, sems) = refs[12:16], refs[16:]
    half, size = own_one.shape[0], d_qkv.shape[1] // 2
    count = refs[0].shape[0]
    cols = pl.ds(base * 128, 256)

    def parts(own_rows, other_rows, d_qkv_ref, mixed_ref, own_grad, other_grad):
        return (own_rows, other_rows, d_qkv_ref, mixed_ref.at[:, cols], own_grad, other_grad)

    buffers = (
        rows.at[pl.ds(0, count)],
        rows.at[pl.ds(count, count)],
        d_qkv,
        mixed,
        d_attn.at[pl.ds(0, count)],
        d_attn.at[pl.ds(count, count)],
    )
    arrived = fetch(section_ref, parts(*refs[:6]), parts(*refs[6:12]), buffers, sems)
    for j, own, other in ((1, own_two, other_two), (0, own_one, other_one)):
        if j == 1:
            arrived(0, 1, 2)
        qkv = dot_tn(rows[...], d_qkv[:, j * size : (j + 1) * size])
        if j == 1:
            arrived(3, 4, 5)
        out = dot_tn(d_attn[...], mixed[:, j * 128 : (j + 1) * 128])
        own[:, :size] = qkv[:half]
        own[:, size:] = out[:half]
        other[:, :size] = qkv[half:].astype(jnp.bfloat16)
        other[:, size:] = out[half:].astype(jnp.bfloat16)


def weight_grads(kernel, name, base, section, zeros, ones, shape, columns, waits=()):
    length = 2 * zeros[0].shape[0]
    width = zeros[0].shape[1]
    every = pl.BlockSpec(memory_space=pl.ANY)
    space = pl.BlockSpec(memory_space=pltpu.VMEM)
    arrays = (*zeros, *ones)
    first, second, third, fourth = pl.pallas_call(
        without(functools.partial(kernel, base), 1 + len(arrays), len(waits)),
        in_specs=[pl.BlockSpec(memory_space=pltpu.SMEM)] + [every] * (len(arrays) + len(waits)),
        out_specs=[space] * 4,
        out_shape=[
            jax.ShapeDtypeStruct(shape, jnp.float32),
            jax.ShapeDtypeStruct(shape, jnp.bfloat16),
        ]
        * 2,
        scratch_shapes=[
            pltpu.VMEM((length, width), jnp.bfloat16),
            pltpu.VMEM((length, columns[0]), jnp.bfloat16),
            pltpu.VMEM((length, columns[1]), jnp.bfloat16),
            pltpu.VMEM((length, width), jnp.bfloat16),
            pltpu.SemaphoreType.DMA((6,)),
        ],
        compiler_params=pltpu.CompilerParams(vmem_limit_bytes=KERNEL_VMEM),
        name=name,
    )(section, *arrays, *waits)
    return [(first, flip_pairs(second, 2)), (third, flip_pairs(fourth, 2))]


def moved_kernel(own_ref, other_ref, *refs):
    out_ref = refs[-1]

    def body(i, carry):
        spot = pl.ds(pl.multiple_of(i * CHUNK, CHUNK), CHUNK)
        total = own_ref[spot, :]
        for ref in (other_ref, *refs[:-1]):
            total = total + wide(ref, spot)
        out_ref[spot, :] = total.astype(jnp.bfloat16)
        return carry

    lax.fori_loop(0, own_ref.shape[0] // CHUNK, body, 0)


def gate_kernel(up_ref, down_ref, up_out, down_out):
    up_out[...] = up_ref[...]
    down_out[...] = down_ref[...]


def mlp_sum_kernel(core_ref, own_ref, other_ref, moved_ref, up_keep, down_keep, up_send, down_send):
    half = own_ref.shape[0] // 2
    size = up_keep.shape[0]

    def total(rows, cols):
        more = other_ref[rows, cols].astype(jnp.float32) + moved_ref[rows, cols].astype(jnp.float32)
        return own_ref[rows, cols] + more

    for core in range(2):

        @pl.when(core_ref[0] == core)
        def _():
            for place, up, down in ((core, up_keep, down_keep), (1 - core, up_send, down_send)):
                spot = slice(place * size, (place + 1) * size)
                up[...] = total(spot, slice(None))
                down[...] = total(slice(half, None), spot)


def mlp_join_kernel(core_ref, up_keep, down_keep, up_sent, down_sent, up_out, down_out):
    size = up_keep.shape[1]
    for core in range(2):

        @pl.when(core_ref[0] == core)
        def _():
            places = ((core, up_keep, down_keep), (1 - core, up_sent, down_sent))
            for place, up, down in places:
                spot = slice(place * size, (place + 1) * size)
                up_out[:, spot] = up[...]
                down_out[spot] = down[...]


def pick_kernel(core_ref, rows_ref, keep_ref, send_ref):
    count = keep_ref.shape[0]
    keep_ref[...] = rows_ref[pl.ds(core_ref[0] * count, count)]
    send_ref[...] = rows_ref[pl.ds((1 - core_ref[0]) * count, count)]


def both_kernel(core_ref, keep_ref, sent_ref, out_ref):
    count = keep_ref.shape[0]
    out_ref[pl.ds(core_ref[0] * count, count)] = keep_ref[...]
    out_ref[pl.ds((1 - core_ref[0]) * count, count)] = sent_ref[...]


def in_order_kernel(core_ref, keep_ref, sent_ref, out_ref):
    out_ref[:, pl.ds(core_ref[0], 1)] = keep_ref[...][:, None]
    out_ref[:, pl.ds(1 - core_ref[0], 1)] = sent_ref[...][:, None]


def with_core(kernel, name, core, outs, *operands, waits=()):
    space = pl.BlockSpec(memory_space=pltpu.VMEM)
    return pl.pallas_call(
        without(kernel, 1 + len(operands), len(waits)),
        in_specs=[pl.BlockSpec(memory_space=pltpu.SMEM)]
        + [space] * len(operands)
        + [pl.BlockSpec(memory_space=pl.ANY)] * len(waits),
        out_specs=[space] * len(outs),
        out_shape=[jax.ShapeDtypeStruct(shape, dtype) for shape, dtype in outs],
        compiler_params=pltpu.CompilerParams(vmem_limit_bytes=ROWS_VMEM),
        name=name,
    )(core, *operands, *waits)


def last_sum_kernel(core_ref, own_ref, other_ref, moved_ref, keep_ref, send_ref):
    rows = keep_ref.shape[0]

    def total(block):
        spot = pl.ds(pl.multiple_of(block * rows, rows), rows)
        return own_ref[spot, :] + wide(other_ref, spot) + wide(moved_ref, spot)

    keep_ref[...] = total(core_ref[0])
    send_ref[...] = total(1 - core_ref[0])


def joined_kernel(spots, core_ref, keep_ref, sent_ref, column_ref, row_ref):
    size = row_ref.shape[0] // 2
    for core in range(2):

        @pl.when(core_ref[0] == core)
        def _():
            for place, source in ((core, keep_ref), (1 - core, sent_ref)):
                for start, stop, to in spots:
                    step = stop - start
                    column_ref[:, to + place * step : to + (place + 1) * step] = source[:, start:stop]
                row_ref[place * size : (place + 1) * size] = source[:, spots[-1][1] :].T


def per_chip(
    inputs,
    out_cotangent,
    group_ids,
    group_weights,
    gains,
    qkv_weight,
    out_weight,
    up_weight,
    down_weight,
):
    micro, row_count, width = inputs.shape
    tensor = lax.axis_size("tensor")
    part = row_count // 2
    wide_half = width // 2
    length = tensor * row_count
    half = length // 2
    first = lax.axis_index("section") == 0
    place = lax.axis_index("dp")
    core = place % 2
    upper = place // 2 % 2
    core_zero = core == 0
    low_half = upper == 0

    def ordered(mine, other):
        return jnp.where(core_zero, mine, other), jnp.where(core_zero, other, mine)

    def own_first(values):
        return jnp.where(low_half, values, jnp.roll(values, wide_half, axis=-1))

    def both_rows(own):
        return own, flip_pairs(own, 1)

    def to_chip(block):
        split = block.reshape((micro, 2, part) + block.shape[2:])
        mine = lax.dynamic_index_in_dim(split, core, 1, keepdims=False)
        other = lax.dynamic_index_in_dim(split, 1 - core, 1, keepdims=False)
        outs = (((2 * micro, part, width), jnp.bfloat16),)
        (rows,) = with_core(
            both_kernel, "both", core_word, outs, mine, flip_pairs(other, 1), waits=(attn_piece,)
        )
        return lax.all_to_all(rows, "tensor", 0, 0, tiled=True)

    def from_chip(spread_out, waits=()):
        piece = ((micro, part, width), jnp.bfloat16)
        keep, send = with_core(
            pick_kernel, "pick", core_word, (piece, piece), spread_out, waits=waits
        )
        outs = (((micro, 2, part, width), jnp.bfloat16),)
        (rows,) = with_core(
            in_order_kernel, "in_order", core_word, outs, keep, flip_pairs(send, 1)
        )
        return rows.reshape(micro, row_count, width)

    def columns(local):
        size = local.shape[-1] // 2
        mid = (0,) * (local.ndim - 2)
        piece = lax.dynamic_slice(
            local,
            (wide_half * upper, *mid, size * core),
            (wide_half, *local.shape[1:-1], size),
        )
        return piece.reshape(wide_half, -1)

    def rows(local):
        size = local.shape[0] // 2
        return lax.dynamic_slice(local, (size * core, wide_half * upper), (size, wide_half))

    core_word = core.astype(jnp.int32).reshape(1)
    attn_piece = jnp.concatenate([columns(qkv_weight[0]), rows(out_weight[0]).T], axis=1)

    def spread(piece):
        pieces = [piece]
        for _ in range(tensor - 1):
            pieces.append(passed_on(pieces[-1], 1))
        return pieces

    attn_own = spread(attn_piece)
    attn_other = [flip_pairs(piece, 2) for piece in attn_own]
    up_piece, down_piece = columns(up_weight[0]), rows(down_weight[0])
    up_other, down_other = [flip_pairs(up_piece, 2)], [flip_pairs(down_piece, 2)]
    outs = tuple((piece.shape, piece.dtype) for piece in (up_piece, down_piece))
    up_piece, down_piece = on_chip(
        gate_kernel, "gate", outs, up_piece, down_piece, waits=(attn_own[2], attn_other[0])
    )
    up_own, down_own = spread(up_piece), spread(down_piece)
    up_other += [flip_pairs(piece, 2) for piece in up_own[1:]]
    down_other += [flip_pairs(piece, 2) for piece in down_own[1:]]
    w_attn, w_up, w_down = (attn_own, attn_other), (up_own, up_other), (down_own, down_other)
    unit = up_piece.shape[1]
    units = tensor * unit

    group_count = group_weights.shape[0]
    matches = group_ids[..., None] == jnp.arange(group_count, dtype=jnp.int32)
    row_scale = jnp.sum(jnp.where(matches, group_weights, 0.0), axis=-1)
    weighted = (out_cotangent.astype(jnp.float32) * row_scale[..., None]).astype(jnp.bfloat16)
    start = to_chip(own_first(jnp.where(first, inputs, weighted))).reshape(half, width)
    gain = own_first(gains[0])

    turns = jnp.arange(half, dtype=jnp.int32)
    turns = turns // part * row_count + turns % part
    positions = jnp.concatenate([turns + core * part, turns + (1 - core) * part])
    freqs = 10000.0 ** (-2.0 * jnp.arange(HEAD_DIM // 2, dtype=jnp.float32) / HEAD_DIM)
    angles = positions.astype(jnp.float32)[:, None] * freqs[None, :]
    cos_part, sin_part = jnp.cos(angles), jnp.sin(angles)
    tables = (
        jnp.concatenate([cos_part] * 4, axis=1),
        jnp.concatenate([-sin_part, sin_part] * 2, axis=1),
    )
    row32, row16 = ((half, width), jnp.float32), ((half, width), jnp.bfloat16)
    unit16 = ((length, units), jnp.bfloat16)
    sum32 = ((1, width), jnp.float32)
    mlp_cost = {"limit": KERNEL_VMEM, "flops": 2 * length * width * units}
    every = slice(None)

    def model_kernel(cols, lefts=1):
        return functools.partial(to_model_kernel, lefts, tensor, cols)

    down_kernel = functools.partial(mlp_down_kernel, tensor)

    def forward(layer_input, waits):
        attn_in = both_rows(
            on_chip(norm_in_kernel, "norm_in", (row16,), gain, layer_input, waits=waits[0])[0]
        )
        *heads, mixed = attend(core_word, tables, attn_in, w_attn, waits[1])
        parts = model_rows(model_kernel(OUT), "attn_out", [mixed], w_attn, waits[2])
        operands = (gain, layer_input, *parts)
        branch, hidden, mlp_in = on_chip(
            after_attention_kernel, "after_attn", (row32, row32, row16), *operands, waits=waits[3]
        )
        mlp_in = both_rows(mlp_in)
        kernel = functools.partial(mlp_up_kernel, tensor)
        operands = (*mlp_in, *w_up[0], *w_up[1])
        gelu_out, slope = on_chip(kernel, "mlp_up", (unit16, unit16), *operands, **mlp_cost)
        parts = model_rows(down_kernel, "mlp_down", [gelu_out], w_down)
        mlp_branch, result = on_chip(
            after_mlp_kernel, "after_mlp", (row32, row16), gain, hidden, *parts
        )
        saved = (layer_input, heads, branch, hidden, slope, mlp_branch)
        return result, saved, (attn_in, mixed, mlp_in, gelu_out)

    def backward(grad, saved, hook, late=()):
        layer_input, heads, branch, hidden, slope, mlp_branch = saved
        operands = (gain, grad, mlp_branch)
        d_down, sum_three = on_chip(
            into_mlp_back_kernel, "into_mlp_back", (row16, sum32), *operands
        )
        d_down = both_rows(d_down)
        d_up = mlp_up_back(d_down, slope, w_down, late)
        waits = hook(d_down, d_up)
        parts = model_rows(model_kernel(every), "mlp_back", [d_up], w_up, waits)
        waits = hook()
        operands = (gain, grad, *parts, hidden, branch)
        outs = (row32, row16, sum32, sum32)
        d_hidden, d_attn, sum_one, sum_two = on_chip(
            into_attention_back_kernel, "into_attn_back", outs, *operands, waits=waits
        )
        d_attn = both_rows(d_attn)
        waits = hook(d_attn)
        d_qkv = []
        for base in reversed(range(0, tensor, 2)):
            some = [side[base : base + 2] for side in w_attn]
            now = attend_back(core_word, tables, d_attn, some, base, waits, *heads)
            d_qkv.insert(0, now)
            waits = hook(now)
        parts = model_rows(model_kernel(QKV, 2), "attn_back", d_qkv, w_attn, waits)
        operands = (gain, layer_input, *parts, d_hidden)
        d_input, sum_zero = on_chip(
            out_of_layer_kernel, "out_of_layer", (row16, sum32), *operands, waits=hook()
        )
        sums = jnp.concatenate([sum_zero, sum_one, sum_two, sum_three])
        return d_input, (d_qkv, d_attn, d_up, d_down), sums

    low_zero, saved_zero, lefts_zero = forward(
        start,
        (
            (up_piece, up_other[0], down_other[0]),
            (up_own[1], down_own[1]),
            (up_own[2], down_own[2], up_other[1], down_other[1]),
            (up_own[3], down_own[3], up_other[2], down_other[2]),
        ),
    )
    low_one, saved_one, lefts_one = forward(shifted(low_zero, "section", 1), ((),) * 4)
    grad_one, rights_one, gain_one = backward(start, saved_one, lambda *new: ())
    received = shifted(grad_one, "section", -1)

    lows = lax.optimization_barrier((low_zero, low_one, grad_one))[:2]
    lows = own_first(jnp.where(first, *lows)).reshape(tensor, part, width)
    lows = lax.all_to_all(lows, "tensor", 0, 0, tiled=True)

    section_word = lax.axis_index("section").astype(jnp.int32).reshape(1)

    def mlp_leaves(base):
        zeros = (*lefts_zero[2], d_up, lefts_zero[3], *d_down)
        ones = (*lefts_one[2], rights_one[2], lefts_one[3], *rights_one[3])
        mlp_sums[base : base + 2] = weight_grads(
            mlp_grads_kernel,
            "mlp_grads",
            base,
            section_word,
            zeros,
            ones,
            (wide_half + unit, unit),
            (2 * unit, 2 * unit),
        )

    def attn_leaves(base, d_qkv):
        zeros = (*lefts_zero[0], d_qkv, lefts_zero[1], *d_attn)
        ones = (*lefts_one[0], rights_one[0][base // 2], lefts_one[1], *rights_one[1])
        attn_sums[base : base + 2] = weight_grads(
            attn_grads_kernel,
            "attn_grads",
            base,
            section_word,
            zeros,
            ones,
            (wide_half, 512),
            (768, 256),
        )

    def moves_on(piece, *moved, waits=()):
        outs = ((piece[1].shape, jnp.bfloat16),)
        (total,) = on_chip(moved_kernel, "moved", outs, *piece, *moved, waits=waits)
        return passed_on(total, -1)

    mlp_sums, attn_sums = [None] * tensor, [None] * tensor
    mlp_moves, attn_moves = [None] * tensor, [None] * tensor
    hooks = iter(range(6))

    def hook(*new):
        nonlocal d_down, d_up, d_attn
        turn = next(hooks)
        if turn == 0:
            d_down, d_up = new
            mlp_leaves(2)
            return (mlp_sums[3][0],)
        if turn == 1:
            mlp_leaves(0)
            return (mlp_sums[1][0],)
        if turn == 2:
            (d_attn,) = new
            mlp_moves[3] = moves_on(mlp_sums[3], waits=d_attn[:1])
            return (mlp_sums[3][1],)
        if turn == 3:
            mlp_moves[2] = moves_on(mlp_sums[2], mlp_moves[3], waits=new)
            attn_leaves(2, new[0])
            return (mlp_sums[2][1], mlp_moves[3], attn_sums[3][0])
        if turn == 4:
            mlp_moves[1] = moves_on(mlp_sums[1], mlp_moves[2], waits=new)
            attn_leaves(0, new[0])
            return (mlp_sums[1][1], mlp_moves[2], attn_sums[1][0])
        return (mlp_sums[0][1], attn_sums[3][1], attn_sums[2][1], mlp_moves[1])

    d_down = d_up = d_attn = None
    grad_zero, rights_zero, gain_zero = backward(received, saved_zero, hook, (lows,))
    gain_total = own_first(jnp.where(first, gain_zero, gain_one))
    count = tensor * lax.axis_size("dp")
    gain_parts = gain_total.reshape(4, count, width // count).swapaxes(0, 1)
    gain_parts = lax.all_to_all(gain_parts, ("dp", "tensor"), 0, 0, tiled=True)
    gains_grad = jnp.sum(gain_parts, axis=0)
    attn_moves[3] = moves_on(attn_sums[3])
    attn_moves[2] = moves_on(attn_sums[2], attn_moves[3])
    attn_moves[1] = moves_on(attn_sums[1], attn_moves[2], waits=(gains_grad,))
    outputs = from_chip(lows, (grad_zero, attn_sums[1][1]))
    grads = own_first(jnp.where(first, grad_zero, grad_one)).reshape(tensor, part, width)
    grads = from_chip(lax.all_to_all(grads, "tensor", 0, 0, tiled=True), attn_sums[0][1:])

    block32 = ((wide_half // 2, unit), jnp.float32)
    down32 = ((unit, wide_half // 2), jnp.float32)
    up_keep, down_keep, up_send, down_send = with_core(
        mlp_sum_kernel,
        "mlp_sum",
        core_word,
        (block32, down32, block32, down32),
        *mlp_sums[0],
        mlp_moves[1],
    )
    outs = (
        ((wide_half // 2, 2 * unit), jnp.float32),
        ((2 * unit, wide_half // 2), jnp.float32),
    )
    sent = flip_pairs(up_send, 1), flip_pairs(down_send, 1)
    up_grad, down_grad = with_core(
        mlp_join_kernel, "mlp_join", core_word, outs, up_keep, down_keep, *sent
    )
    outs = (((wide_half // 2, 512), jnp.float32),) * 2
    keep, send = with_core(
        last_sum_kernel,
        "attn_sum",
        core_word,
        outs,
        *attn_sums[0],
        attn_moves[1],
        waits=(outputs, grads, gains_grad, up_grad),
    )
    spots = tuple((i * 128, (i + 1) * 128, i * 256) for i in range(3))
    outs = (((wide_half // 2, 768), jnp.float32), ((256, wide_half // 2), jnp.float32))
    kernel = functools.partial(joined_kernel, spots)
    qkv_grad, out_grad = with_core(
        kernel, "attn_join", core_word, outs, keep, flip_pairs(send, 1)
    )
    qkv_grad = qkv_grad.reshape(wide_half // 2, 3, -1)

    return (
        outputs[None],
        grads[None],
        gains_grad[None],
        qkv_grad[None],
        out_grad[None],
        up_grad[None],
        down_grad[None],
    )


def takes_chips(sizes):
    return sizes["section"] == 2 and sizes["dp"] == 4 and sizes["tensor"] == 4


def solution(mesh):
    placed = (
        P("dp", "tensor", None),
        P("dp", "tensor", None),
        P("dp", "tensor"),
        P(),
        P("section", None, None),
        P("section", None, None, "tensor"),
        P("section", "tensor", None),
        P("section", None, "tensor"),
        P("section", "tensor", None),
    )
    body = per_chip if takes_chips(dict(mesh.shape)) else per_device
    return jax.shard_map(
        body,
        mesh=mesh,
        in_specs=placed,
        out_specs=(
            P("section", "dp", "tensor", None),
            P("section", "dp", "tensor", None),
            P("section", None, ("dp", "tensor")),
            P("section", "dp", None, "tensor"),
            P("section", "tensor", "dp"),
            P("section", "dp", "tensor"),
            P("section", "tensor", "dp"),
        ),
        check_vma=False,
    )
```

```python
import functools
import math

import jax
import jax.numpy as jnp
from jax import lax
from jax.experimental import pallas as pl
from jax.experimental.pallas import tpu as pltpu
from jax.sharding import PartitionSpec as P

HEAD_DIM = 64


NORM_EPSILON = 1e-06
TILE = 128
PAIR_WORK = 1024
MODEL_HALF = 512
QKV = slice(0, 384)
OUT = slice(384, 512)
CHUNK = 32
KERNEL_VMEM = 20 << 20
ROWS_VMEM = 3 << 20


def shifted(block, axis, distance):
    devices = range(lax.axis_size(axis))
    route = [(i - distance, i) for i in devices if i - distance in devices]
    return lax.ppermute(block, axis, route)


def norm_rows(vector, weight_gain):
    return (
        vector
        * lax.rsqrt(jnp.mean(vector * vector, axis=-1, keepdims=True) + NORM_EPSILON)
        * weight_gain
    )


def rotary_tables(seq_len, head_width):
    half_width = head_width // 2
    freqs = 10000.0 ** (-2.0 * jnp.arange(half_width, dtype=jnp.float32) / head_width)
    angles = jnp.arange(seq_len, dtype=jnp.float32)[:, None] * freqs[None, :]
    return (jnp.cos(angles), jnp.sin(angles))


def rotate(vector, cos_table, sin_table):
    first_half, second_half = jnp.split(vector, 2, axis=-1)
    cos_part = cos_table[:, None, :]
    sin_part = sin_table[:, None, :]
    return jnp.concatenate(
        [
            first_half * cos_part - second_half * sin_part,
            second_half * cos_part + first_half * sin_part,
        ],
        axis=-1,
    )


def contract(left_rows, right_rows):
    return lax.dot_general(
        left_rows, right_rows, (((0,), (0,)), ((), ())), preferred_element_type=jnp.float32
    )


def gather_rows(row_values, weight):

    def project(shard_rows, offset):
        return (shard_rows, jnp.dot(shard_rows, weight, preferred_element_type=jnp.float32))

    return project(lax.all_gather(row_values, "tensor", axis=0, tiled=True), jnp.int32(0))


def scatter_rows(row_values, weight, row_count):

    def partial_term(offset, span):
        return jnp.dot(row_values, weight, preferred_element_type=jnp.float32)

    return lax.psum_scatter(
        partial_term(jnp.int32(0), lax.axis_size("tensor") * row_count),
        "tensor",
        scatter_dimension=0,
        tiled=True,
    )


def gather_grads(row_values, weight):

    def project(shard_rows, offset):
        return (shard_rows, jnp.dot(shard_rows, weight.T, preferred_element_type=jnp.float32))

    return project(lax.all_gather(row_values, "tensor", axis=0, tiled=True), jnp.int32(0))


def scatter_grads(row_values, weight, row_count):

    def partial_term(offset, span):
        return jnp.dot(row_values, weight.T, preferred_element_type=jnp.float32)

    return lax.psum_scatter(
        partial_term(jnp.int32(0), lax.axis_size("tensor") * row_count),
        "tensor",
        scatter_dimension=0,
        tiled=True,
    )


def attention_probs(queries, key_rows):
    scores = jnp.einsum(
        "qhd,khd->hqk", queries, key_rows, preferred_element_type=jnp.float32
    ) * HEAD_DIM ** (-0.5)
    length = queries.shape[0]
    positions = jnp.arange(length, dtype=jnp.int32)
    causal = positions[:, None] >= positions[None, :]
    scores = jnp.where(causal[None], scores, -1e30)
    expos = jnp.exp(scores - jnp.max(scores, axis=-1, keepdims=True))
    return expos / jnp.sum(expos, axis=-1, keepdims=True)


def layer_forward(layer_input, weights):
    gains, w_qkv, w_out, w_up, w_down = weights
    row_count, model_width = layer_input.shape
    attn_in = norm_rows(layer_input, gains[0]).astype(jnp.bfloat16)
    gathered_a, qkv = gather_rows(attn_in, w_qkv.reshape(model_width, -1))
    length = qkv.shape[0]
    head_count = w_qkv.shape[2] // HEAD_DIM
    qkv = qkv.reshape(length, 3, head_count, HEAD_DIM)
    cos_table, sin_table = rotary_tables(length, HEAD_DIM)
    queries = rotate(qkv[:, 0], cos_table, sin_table).astype(jnp.bfloat16)
    key_rows = rotate(qkv[:, 1], cos_table, sin_table).astype(jnp.bfloat16)
    values = qkv[:, 2].astype(jnp.bfloat16)
    attn_probs = attention_probs(queries, key_rows).astype(jnp.bfloat16)
    mixed = jnp.einsum("hqk,khd->qhd", attn_probs, values, preferred_element_type=jnp.float32)
    mixed = mixed.reshape(length, -1).astype(jnp.bfloat16)
    attn_branch = scatter_rows(mixed, w_out, row_count)
    hidden = layer_input + norm_rows(attn_branch, gains[1])
    mlp_in = norm_rows(hidden, gains[2]).astype(jnp.bfloat16)
    gathered_c, up_act = gather_rows(mlp_in, w_up)
    gelu_out = jax.nn.gelu(up_act, approximate=True).astype(jnp.bfloat16)
    down_branch = scatter_rows(gelu_out, w_down, row_count)
    result = hidden + norm_rows(down_branch, gains[3])
    kept_values = (
        gathered_a,
        queries,
        key_rows,
        values,
        mixed,
        attn_branch,
        hidden,
        gathered_c,
        up_act,
        gelu_out,
        down_branch,
    )
    return (result, kept_values)


def layer_backward(layer_input, grad_result, kept_values, weights):
    gains, w_qkv, w_out, w_up, w_down = weights
    (
        gathered_a,
        queries,
        key_rows,
        values,
        mixed,
        attn_branch,
        hidden,
        gathered_c,
        up_act,
        gelu_out,
        down_branch,
    ) = kept_values
    row_count, model_width = layer_input.shape
    pullback = jax.vjp(norm_rows, down_branch, gains[3])[1]
    grad_down, gain_three = pullback(grad_result)
    gathered_dd, grad_gelu = gather_grads(grad_down.astype(jnp.bfloat16), w_down)
    down_total = contract(gelu_out, gathered_dd)
    pullback = jax.vjp(lambda vector: jax.nn.gelu(vector, approximate=True), up_act)[1]
    grad_up = pullback(grad_gelu)[0].astype(jnp.bfloat16)
    up_total = contract(gathered_c, grad_up)
    grad_mlp = scatter_grads(grad_up, w_up, row_count)
    pullback = jax.vjp(norm_rows, hidden, gains[2])[1]
    grad_norm_mlp, gain_two = pullback(grad_mlp)
    grad_hidden = grad_result + grad_norm_mlp
    pullback = jax.vjp(norm_rows, attn_branch, gains[1])[1]
    grad_attn, gain_one = pullback(grad_hidden)
    gathered_da, grad_mixed = gather_grads(grad_attn.astype(jnp.bfloat16), w_out)
    out_total = contract(mixed, gathered_da)
    length = grad_mixed.shape[0]
    head_count = w_qkv.shape[2] // HEAD_DIM
    grad_mixed = grad_mixed.astype(jnp.bfloat16).reshape(length, head_count, HEAD_DIM)
    attn_probs = attention_probs(queries, key_rows)
    probs_low = attn_probs.astype(jnp.bfloat16)
    grad_probs = jnp.einsum("qhd,khd->hqk", grad_mixed, values, preferred_element_type=jnp.float32)
    grad_values = jnp.einsum(
        "hqk,qhd->khd", probs_low, grad_mixed, preferred_element_type=jnp.float32
    )
    row_dots = jnp.sum(grad_probs * attn_probs, axis=-1, keepdims=True)
    grad_scores = (attn_probs * (grad_probs - row_dots)).astype(jnp.bfloat16)
    scale_value = HEAD_DIM ** (-0.5)
    grad_queries = (
        jnp.einsum("hqk,khd->qhd", grad_scores, key_rows, preferred_element_type=jnp.float32)
        * scale_value
    )
    grad_keys = (
        jnp.einsum("hqk,qhd->khd", grad_scores, queries, preferred_element_type=jnp.float32)
        * scale_value
    )
    cos_table, sin_table = rotary_tables(length, HEAD_DIM)
    pullback = jax.vjp(lambda vector: rotate(vector, cos_table, sin_table), grad_queries)[1]
    grad_q_raw = pullback(grad_queries)[0]
    grad_k_raw = pullback(grad_keys)[0]
    grad_qkv = (
        jnp.stack([grad_q_raw, grad_k_raw, grad_values], axis=1)
        .reshape(length, -1)
        .astype(jnp.bfloat16)
    )
    qkv_total = contract(gathered_a, grad_qkv).reshape(model_width, 3, -1)
    grad_attn_in = scatter_grads(grad_qkv, w_qkv.reshape(model_width, -1), row_count)
    pullback = jax.vjp(norm_rows, layer_input, gains[0])[1]
    grad_norm_in, gain_zero = pullback(grad_attn_in)
    grad_input = grad_hidden + grad_norm_in
    gain_total = jnp.stack([gain_zero, gain_one, gain_two, gain_three])
    return (grad_input, (gain_total, qkv_total, out_total, up_total, down_total))


def lagged(first_section, stacked):
    blank = jnp.zeros_like(stacked[:1])
    earlier = jnp.concatenate([blank, stacked[:-1]])
    later = jnp.concatenate([stacked[1:], blank])
    return jnp.where(first_section, earlier, later)


def per_device(
    inputs,
    out_cotangent,
    group_ids,
    group_weights,
    gains,
    qkv_weight,
    out_weight,
    up_weight,
    down_weight,
):
    weights = (gains[0], qkv_weight[0], out_weight[0], up_weight[0], down_weight[0])
    micro_count, row_count, model_width = inputs.shape
    first_section = lax.axis_index("section") == 0
    group_count = group_weights.shape[0]
    matches = group_ids[..., None] == jnp.arange(group_count, dtype=jnp.int32)
    row_scale = jnp.sum(jnp.where(matches, group_weights, 0.0), axis=-1)
    scaled = out_cotangent.astype(jnp.float32) * row_scale[..., None]
    padded = jnp.concatenate([inputs, jnp.zeros((1, row_count, model_width), jnp.bfloat16)])

    def forward_tick(received, fresh_input):
        layer_input = jnp.where(first_section, fresh_input, received)
        result, kept_values = layer_forward(layer_input.astype(jnp.float32), weights)
        result_low = result.astype(jnp.bfloat16)
        outgoing = shifted(result_low, "section", 1)
        stashed = ()
        return (outgoing, (layer_input, result_low, stashed))

    start_rows = jnp.zeros((row_count, model_width), jnp.bfloat16)
    _, (layer_inputs, layer_results, stashed) = lax.scan(forward_tick, start_rows, padded)
    layer_outputs = jnp.where(first_section, layer_results[:-1], layer_results[1:])[None]
    back_inputs = lagged(first_section, layer_inputs)
    back_stash = jax.tree.map(lambda stacked: lagged(first_section, stacked), stashed)
    grad_padded = jnp.concatenate([scaled, jnp.zeros((1, row_count, model_width), jnp.float32)])
    tick_index = jnp.arange(micro_count + 1, dtype=jnp.int32)
    tick_valid = jnp.where(first_section, tick_index >= 1, tick_index < micro_count).astype(
        jnp.float32
    )

    def backward_tick(carry, step_item):
        received, totals = carry
        layer_input, cotangent, valid_now, stash_now = step_item
        grad_now = jnp.where(first_section, received.astype(jnp.float32), cotangent)
        input_now = layer_input.astype(jnp.float32)
        kept_values = layer_forward(input_now, weights)[1]
        grad_input, layer_grads = layer_backward(input_now, grad_now, kept_values, weights)
        totals = jax.tree.map(lambda total, update: total + valid_now * update, totals, layer_grads)
        grad_low = grad_input.astype(jnp.bfloat16)
        outgoing = shifted(grad_low, "section", -1)
        return ((outgoing, totals), grad_low)

    start_totals = (
        jnp.zeros((4, model_width), jnp.float32),
        jnp.zeros(qkv_weight.shape[1:], jnp.float32),
        jnp.zeros(out_weight.shape[1:], jnp.float32),
        jnp.zeros(up_weight.shape[1:], jnp.float32),
        jnp.zeros(down_weight.shape[1:], jnp.float32),
    )
    (_, totals), grad_lows = lax.scan(
        backward_tick,
        (start_rows, start_totals),
        (back_inputs, grad_padded, tick_valid, back_stash),
    )
    input_grads = jnp.where(first_section, grad_lows[1:], grad_lows[:-1])[None]
    gain_total, qkv_total, out_total, up_total, down_total = totals
    gains_grad = lax.psum_scatter(gain_total, ("dp", "tensor"), scatter_dimension=1, tiled=True)
    qkv_grad, out_grad, up_grad, down_grad = (
        lax.psum_scatter(
            qkv_total.astype(jnp.bfloat16), "dp", scatter_dimension=0, tiled=True
        ).astype(jnp.float32),
        lax.psum_scatter(
            out_total.astype(jnp.bfloat16), "dp", scatter_dimension=1, tiled=True
        ).astype(jnp.float32),
        lax.psum_scatter(
            up_total.astype(jnp.bfloat16), "dp", scatter_dimension=0, tiled=True
        ).astype(jnp.float32),
        lax.psum_scatter(
            down_total.astype(jnp.bfloat16), "dp", scatter_dimension=1, tiled=True
        ).astype(jnp.float32),
    )
    return (
        layer_outputs,
        input_grads,
        gains_grad[None],
        qkv_grad[None],
        out_grad[None],
        up_grad[None],
        down_grad[None],
    )


def rotated(block, cos_rows, sin_rows):
    lane = lax.broadcasted_iota(jnp.int32, block.shape, 1)
    ahead = pltpu.roll(block, 96, 1)
    behind = pltpu.roll(block, 32, 1)
    swapped = jnp.where(lane % 64 < 32, ahead, behind)
    return block * cos_rows + swapped * sin_rows


def dot_nt(left, right):
    return lax.dot_general(
        left, right, (((1,), (1,)), ((), ())), preferred_element_type=jnp.float32
    )


def dot_nn(left, right):
    return jnp.dot(left, right, preferred_element_type=jnp.float32)


def model_weight(owns, others, cols):
    sides = [jnp.concatenate([ref[:, cols] for ref in refs], axis=1) for refs in (owns, others)]
    return jnp.concatenate(sides, axis=0)


def stacked_up(values):
    return jnp.concatenate(values, axis=0)


def edge_masks(core, rows):
    key = lax.broadcasted_iota(jnp.int32, (rows, 2 * rows), 0)
    query = lax.broadcasted_iota(jnp.int32, (rows, 2 * rows), 1)
    mine = query < rows
    place = jnp.where(mine, query + core * rows, query - rows + (1 - core) * rows)
    return (key + core * rows <= place, key + (1 - core) * rows <= place)


def both_sides(value, half, start, stop, axis=0):
    if axis == 0:
        return jnp.concatenate([value[start:stop], value[half + start : half + stop]], axis=0)
    return jnp.concatenate([value[:, start:stop], value[:, half + start : half + stop]], axis=1)


def hidden_scores(scores, masks, tile, step):
    seen = step * tile
    pieces = []
    for side in range(2):
        base = side * (seen + tile)
        if seen:
            pieces.append(scores[base : base + seen])
        pieces.append(jnp.where(masks[side], scores[base + seen : base + seen + tile], -1e30))
    return jnp.concatenate(pieces, axis=0)


def one_head(rows, head):
    lane = lax.broadcasted_iota(jnp.int32, rows.shape, 1)
    return jnp.where(lane // 64 == head, rows, jnp.zeros_like(rows))


def pick_piece(weight, owns, others, cols):
    for j, (own, other) in enumerate(zip(owns, others)):

        @pl.when(pl.program_id(0) == j)
        def _():
            size = own.shape[0]
            weight[:size] = own[:, cols]
            weight[size:] = other[:, cols]


def attend_kernel(pieces, core_ref, cos_ref, sin_ref, own_rows, other_rows, *refs):
    owns, others = refs[:pieces], refs[pieces : 2 * pieces]
    q_ref, k_ref, v_ref, lse_ref, mix_ref, weight = refs[2 * pieces :]
    half = own_rows.shape[0]
    tile = TILE
    pick_piece(weight, owns, others, QKV)
    proj = dot_nn(stacked_up([own_rows[...], other_rows[...]]), weight[...])
    cos_rows, sin_rows = cos_ref[...], sin_ref[...]
    q = (rotated(proj[:, :128], cos_rows, sin_rows) * HEAD_DIM ** (-0.5)).astype(jnp.bfloat16)
    k = rotated(proj[:, 128:256], cos_rows, sin_rows).astype(jnp.bfloat16)
    v32 = proj[:, 256:]
    q_ref[0] = q
    k_ref[0] = k
    v_ref[0] = v32.astype(jnp.bfloat16)
    v_flip = v32.T.astype(jnp.bfloat16)
    masks = edge_masks(core_ref[0], tile)

    def scored(step, head):
        stop = (step + 1) * tile
        q_head = one_head(both_sides(q, half, step * tile, stop), head)
        return hidden_scores(dot_nt(both_sides(k, half, 0, stop), q_head), masks, tile, step)

    units = [(step, head) for step in range(half // tile) for head in range(2)]
    ahead = scored(*units[0])
    outs = []
    for spot, (step, head) in enumerate(units):
        scores = ahead
        if spot + 1 < len(units):
            ahead = scored(*units[spot + 1])
        stop = (step + 1) * tile
        top = jnp.max(scores, axis=0, keepdims=True)
        expos = jnp.exp(scores - top)
        total = jnp.sum(expos, axis=0, keepdims=True)
        lse = top + jnp.log(total)
        lse_ref[0, head : head + 1, step * tile : stop] = lse[:, :tile]
        lse_ref[0, head : head + 1, half + step * tile : half + stop] = lse[:, tile:]
        v_cols = both_sides(v_flip, half, 0, stop, axis=1)
        out = dot_nn(v_cols[64 * head : 64 * head + 64], expos.astype(jnp.bfloat16))
        outs.append(out * (1.0 / total))
        if head == 1:
            mixed = jnp.concatenate(outs, axis=0).T.astype(jnp.bfloat16)
            outs = []
            mix_ref[step * tile : stop, :] = mixed[:tile]
            mix_ref[half + step * tile : half + stop, :] = mixed[tile:]


def attend_back_kernel(pieces, core_ref, cos_ref, sin_ref, own_rows, other_rows, *refs):
    owns, others = refs[:pieces], refs[pieces : 2 * pieces]
    q_ref, k_ref, v_ref, lse_ref, out_ref, weight, dq, dk, dv = refs[2 * pieces :]
    half = own_rows.shape[0]
    tile = TILE
    pick_piece(weight, owns, others, OUT)
    rows = stacked_up([own_rows[...], other_rows[...]])
    d_mixed = dot_nn(rows, weight[...]).astype(jnp.bfloat16)
    q, k, v = q_ref[0], k_ref[0], v_ref[0]
    k_flip = k.astype(jnp.float32).T.astype(jnp.bfloat16)
    masks = edge_masks(core_ref[0], tile)
    steps = half // tile

    def scored(step, head):
        stop = (step + 1) * tile
        q_head = one_head(both_sides(q, half, step * tile, stop), head)
        g_head = one_head(both_sides(d_mixed, half, step * tile, stop), head)
        scores = hidden_scores(dot_nt(both_sides(k, half, 0, stop), q_head), masks, tile, step)
        return q_head, g_head, scores, dot_nt(both_sides(v, half, 0, stop), g_head)

    units = [(step, head) for step in reversed(range(steps)) for head in range(2)]
    ahead = scored(*units[0])
    dq_flips = []
    dk_sum = dv_sum = None
    for spot, (step, head) in enumerate(units):
        q_head, g_head, scores, d_probs = ahead
        if spot + 1 < len(units):
            ahead = scored(*units[spot + 1])
        stop = (step + 1) * tile
        lse = both_sides(lse_ref[0], half, step * tile, stop, axis=1)
        probs = jnp.exp(scores - lse[head : head + 1])
        dots = jnp.sum(probs * d_probs, axis=0, keepdims=True)
        d_scores = (probs * (d_probs - dots)).astype(jnp.bfloat16)
        dv_part = dot_nn(probs.astype(jnp.bfloat16), g_head)
        dk_part = dot_nn(d_scores, q_head)
        k_cols = both_sides(k_flip, half, 0, stop, axis=1)
        dq_flips.append(dot_nn(k_cols[64 * head : 64 * head + 64], d_scores))
        if head == 0:
            dv_sum, dk_sum = dv_part, dk_part
            continue
        dv_sum, dk_sum = dv_sum + dv_part, dk_sum + dk_part
        dq_rows = jnp.concatenate(dq_flips, axis=0).T * HEAD_DIM ** (-0.5)
        dq_flips = []
        dq[step * tile : stop] = dq_rows[:tile]
        dq[half + step * tile : half + stop] = dq_rows[tile:]
        for base, part in ((0, slice(0, stop)), (half, slice(stop, 2 * stop))):
            if step == steps - 1:
                dk[base : base + stop] = dk_sum[part]
                dv[base : base + stop] = dv_sum[part]
            else:
                dk[base : base + stop] += dk_sum[part]
                dv[base : base + stop] += dv_sum[part]
    cos_rows, sin_rows = cos_ref[...], -sin_ref[...]
    out_ref[:, :128] = rotated(dq[...], cos_rows, sin_rows).astype(jnp.bfloat16)
    out_ref[:, 128:256] = rotated(dk[...], cos_rows, sin_rows).astype(jnp.bfloat16)
    out_ref[:, 256:] = dv[...].astype(jnp.bfloat16)


def split_rows(total, own_ref, other_ref):
    half = own_ref.shape[0]
    own_ref[...] = total[:half]
    other_ref[...] = total[half:].astype(jnp.bfloat16)


def to_model_kernel(lefts, pieces, cols, *refs):
    left, refs = jnp.concatenate([ref[...] for ref in refs[:lefts]], axis=1), refs[lefts:]
    weight = model_weight(refs[:pieces], refs[pieces : 2 * pieces], cols)
    split_rows(dot_nt(left, weight), *refs[2 * pieces :])


def mlp_down_kernel(pieces, left_ref, *refs):
    sides = [stacked_up([ref[...] for ref in side]) for side in (refs[:pieces], refs[pieces:-2])]
    split_rows(dot_nn(left_ref[...], jnp.concatenate(sides, axis=1)), *refs[-2:])


def gelu_both(up_act):
    root = math.sqrt(2.0 / math.pi)
    square = up_act * up_act
    rise = 0.5 + 0.5 * jnp.tanh(up_act * (root + root * 0.044715 * square))
    value = up_act * rise
    slope = rise + value * (1.0 - rise) * (2.0 * root + 6.0 * root * 0.044715 * square)
    return value, slope


def mlp_up_kernel(pieces, own_rows, other_rows, *refs):
    owns, others = refs[:pieces], refs[pieces : 2 * pieces]
    gelu_ref, slope_ref = refs[2 * pieces :]
    half = own_rows.shape[0]
    size = owns[0].shape[1]
    step = half // 2
    units = [(j, i) for j in range(pieces) for i in range(4)]

    def product(j, i):
        rows = (own_rows, other_rows)[i // 2][i % 2 * step : (i % 2 + 1) * step]
        return dot_nn(rows, stacked_up([owns[j][...], others[j][...]]))

    ahead = product(*units[0])
    for spot, (j, i) in enumerate(units):
        up_act = ahead
        if spot + 1 < len(units):
            ahead = product(*units[spot + 1])
        value, slope = gelu_both(up_act)
        gelu_ref[i * step : (i + 1) * step, j * size : (j + 1) * size] = value.astype(jnp.bfloat16)
        slope_ref[i * step : (i + 1) * step, j * size : (j + 1) * size] = slope.astype(
            jnp.bfloat16
        )


def mlp_up_back_kernel(pieces, own_rows, other_rows, slope_ref, *refs):
    owns, others = refs[:pieces], refs[pieces : 2 * pieces]
    out_ref, weight, slope, sems = refs[2 * pieces :]
    half = own_rows.shape[1] // 2
    size = owns[0].shape[0]
    order = list(reversed(range(pieces)))
    copies = []
    for j in order:
        sources = (owns[j], others[j], slope_ref.at[:, pl.ds(j * size, size)])
        targets = (
            weight.at[j, :, pl.ds(0, half)],
            weight.at[j, :, pl.ds(half, half)],
            slope.at[:, pl.ds(j * size, size)],
        )
        copies.append(
            [
                pltpu.make_async_copy(source, target, sems.at[j, i])
                for i, (source, target) in enumerate(zip(sources, targets))
            ]
        )
        for copy in copies[-1]:
            copy.start()
    rows = stacked_up([own_rows[...], other_rows[...]])
    for j, arriving in zip(order, copies):
        cols = slice(j * size, (j + 1) * size)
        for copy in arriving:
            copy.wait()
        d_gelu = dot_nt(rows, weight[j])
        out_ref[:, cols] = (d_gelu * slope[:, cols].astype(jnp.float32)).astype(jnp.bfloat16)


def inverse_size(rows):
    return lax.rsqrt(jnp.mean(rows * rows, axis=-1, keepdims=True) + NORM_EPSILON)


def norm_back(rows, gain, grad):
    scale = inverse_size(rows)
    weighted = grad * gain
    inner = jnp.mean(rows * weighted, axis=-1, keepdims=True)
    return scale * weighted - rows * (scale * scale * scale * inner), rows * scale * grad


def folded(rows):
    return jnp.sum(rows.reshape(rows.shape[0] // 8, 8, rows.shape[1]), axis=0)


def wide(ref, spot):
    return ref[spot, :].astype(jnp.float32)


def by_chunks(count, body, sums=0, width=0):
    def one(i, carry):
        more = body(pl.ds(pl.multiple_of(i * CHUNK, CHUNK), CHUNK))
        return tuple(old + folded(new) for old, new in zip(carry, more))

    start = tuple(jnp.zeros((8, width), jnp.float32) for _ in range(sums))
    totals = lax.fori_loop(0, count // CHUNK, one, start)
    return [jnp.sum(total, axis=0, keepdims=True) for total in totals]


def norm_in_kernel(gain_ref, rows_ref, out_ref):
    def body(spot):
        rows = wide(rows_ref, spot)
        out_ref[spot, :] = (rows * inverse_size(rows) * gain_ref[0:1]).astype(jnp.bfloat16)
        return ()

    by_chunks(rows_ref.shape[0], body)


def after_attention_kernel(
    gain_ref, rows_ref, own_ref, other_ref, branch_ref, hidden_ref, out_ref
):
    def body(spot):
        branch = own_ref[spot, :] + wide(other_ref, spot)
        hidden = wide(rows_ref, spot) + branch * inverse_size(branch) * gain_ref[1:2]
        branch_ref[spot, :] = branch
        hidden_ref[spot, :] = hidden
        out_ref[spot, :] = (hidden * inverse_size(hidden) * gain_ref[2:3]).astype(jnp.bfloat16)
        return ()

    by_chunks(rows_ref.shape[0], body)


def after_mlp_kernel(gain_ref, hidden_ref, own_ref, other_ref, branch_ref, out_ref):
    def body(spot):
        branch = own_ref[spot, :] + wide(other_ref, spot)
        branch_ref[spot, :] = branch
        result = hidden_ref[spot, :] + branch * inverse_size(branch) * gain_ref[3:4]
        out_ref[spot, :] = result.astype(jnp.bfloat16)
        return ()

    by_chunks(hidden_ref.shape[0], body)


def into_mlp_back_kernel(gain_ref, grad_ref, branch_ref, out_ref, sum_ref):
    def body(spot):
        d_rows, d_gain = norm_back(branch_ref[spot, :], gain_ref[3:4], wide(grad_ref, spot))
        out_ref[spot, :] = d_rows.astype(jnp.bfloat16)
        return (d_gain,)

    (sum_ref[...],) = by_chunks(grad_ref.shape[0], body, 1, grad_ref.shape[1])


def into_attention_back_kernel(
    gain_ref, grad_ref, own_ref, other_ref, hidden_ref, branch_ref, d_hidden_ref, out_ref, *sums
):
    def body(spot):
        d_rows = own_ref[spot, :] + wide(other_ref, spot)
        d_rows, d_gain = norm_back(hidden_ref[spot, :], gain_ref[2:3], d_rows)
        d_hidden = wide(grad_ref, spot) + d_rows
        d_hidden_ref[spot, :] = d_hidden
        d_rows, d_first = norm_back(branch_ref[spot, :], gain_ref[1:2], d_hidden)
        out_ref[spot, :] = d_rows.astype(jnp.bfloat16)
        return (d_first, d_gain)

    totals = by_chunks(grad_ref.shape[0], body, 2, grad_ref.shape[1])
    sums[0][...], sums[1][...] = totals


def out_of_layer_kernel(gain_ref, rows_ref, own_ref, other_ref, d_hidden_ref, out_ref, sum_ref):
    def body(spot):
        d_rows = own_ref[spot, :] + wide(other_ref, spot)
        d_rows, d_gain = norm_back(wide(rows_ref, spot), gain_ref[0:1], d_rows)
        out_ref[spot, :] = (d_hidden_ref[spot, :] + d_rows).astype(jnp.bfloat16)
        return (d_gain,)

    (sum_ref[...],) = by_chunks(rows_ref.shape[0], body, 1, rows_ref.shape[1])


def work(flops, arrays):
    size = sum(math.prod(array.shape) * jnp.dtype(array.dtype).itemsize for array in arrays)
    return pl.CostEstimate(flops=flops, bytes_accessed=size, transcendentals=0)


def far(array):
    return pltpu.with_memory_space_constraint(array, pltpu.HBM)


def without(kernel, first, count):
    return lambda *refs: kernel(*refs[:first], *refs[first + count :])


def on_chip(kernel, name, outs, *operands, limit=ROWS_VMEM, flops=0, waits=()):
    shapes = [jax.ShapeDtypeStruct(shape, dtype) for shape, dtype in outs]
    space = pl.BlockSpec(memory_space=pltpu.VMEM)
    return pl.pallas_call(
        without(kernel, len(operands), len(waits)),
        in_specs=[space] * len(operands) + [pl.BlockSpec(memory_space=pl.ANY)] * len(waits),
        out_specs=[space] * len(outs),
        out_shape=shapes,
        compiler_params=pltpu.CompilerParams(vmem_limit_bytes=limit),
        cost_estimate=work(flops, (*operands, *shapes)),
        name=name,
    )(*operands, *map(far, waits))


def whole_block(array):
    return pl.BlockSpec(array.shape, lambda j: (0,) * array.ndim)


def by_pairs(kernel, name, core, operands, pieces, blocks, outs, scratch, flops, waits):
    shapes = [jax.ShapeDtypeStruct(shape, dtype) for shape, dtype, _ in outs]
    taken = 1 + len(operands) + 2 * len(pieces[0]) + len(blocks)
    return pl.pallas_call(
        without(functools.partial(kernel, len(pieces[0])), taken, len(waits)),
        grid=(len(pieces[0]),),
        in_specs=[pl.BlockSpec(memory_space=pltpu.SMEM)]
        + [whole_block(array) for array in (*operands, *pieces[0], *pieces[1])]
        + [spec for _, spec in blocks]
        + [pl.BlockSpec(memory_space=pl.ANY)] * len(waits),
        out_specs=[spec for _, _, spec in outs],
        out_shape=shapes,
        scratch_shapes=scratch,
        compiler_params=pltpu.CompilerParams(vmem_limit_bytes=KERNEL_VMEM),
        cost_estimate=work(flops, (*operands, *pieces[0], *pieces[1], *shapes)),
        name=name,
    )(core, *operands, *pieces[0], *pieces[1], *[array for array, _ in blocks], *map(far, waits))


def mlp_up_back(rows, slope, pieces, waits):
    length, units = slope.shape
    unit, half = pieces[0][0].shape
    count = len(pieces[0])
    every, space = pl.BlockSpec(memory_space=pl.ANY), pl.BlockSpec(memory_space=pltpu.VMEM)
    return pl.pallas_call(
        without(functools.partial(mlp_up_back_kernel, count), 3 + 2 * count, len(waits)),
        in_specs=[space] * 2 + [every] * (1 + 2 * count + len(waits)),
        out_specs=space,
        out_shape=jax.ShapeDtypeStruct((length, units), jnp.bfloat16),
        scratch_shapes=[
            pltpu.VMEM((count, unit, 2 * half), jnp.bfloat16),
            pltpu.VMEM((length, units), jnp.bfloat16),
            pltpu.SemaphoreType.DMA((count, 3)),
        ],
        compiler_params=pltpu.CompilerParams(vmem_limit_bytes=KERNEL_VMEM),
        name="mlp_up_back",
    )(*rows, *map(far, (slope, *pieces[0], *pieces[1], *waits)))


def attend(core, tables, rows, pieces, waits):
    half, features = rows[0].shape
    length, count = 2 * half, len(pieces[0])
    lanes = ((count, length, 128), jnp.bfloat16, pl.BlockSpec((1, length, 128), lambda j: (j, 0, 0)))
    lse = ((count, 2, length), jnp.float32, pl.BlockSpec((1, 2, length), lambda j: (j, 0, 0)))
    mixed = ((length, count * 128), jnp.bfloat16, pl.BlockSpec((length, 128), lambda j: (0, j)))
    return by_pairs(
        attend_kernel,
        "attend",
        core,
        (*tables, *rows),
        pieces,
        (),
        (lanes, lanes, lanes, lse, mixed),
        [pltpu.VMEM((features, 384), jnp.bfloat16)],
        count * length * (2 * features * 384 + 2 * PAIR_WORK * length),
        waits,
    )


def attend_back(core, tables, rows, pieces, base, waits, q, k, v, lse):
    half, features = rows[0].shape
    length, count = 2 * half, len(pieces[0])
    lanes = pl.BlockSpec((1, length, 128), lambda j: (base + j, 0, 0))
    lse_spec = pl.BlockSpec((1, 2, length), lambda j: (base + j, 0, 0))
    out = ((length, count * 384), jnp.bfloat16, pl.BlockSpec((length, 384), lambda j: (0, j)))
    return by_pairs(
        attend_back_kernel,
        "attend_back",
        core,
        (*tables, *rows),
        pieces,
        ((q, lanes), (k, lanes), (v, lanes), (lse, lse_spec)),
        (out,),
        [pltpu.VMEM((features, 128), jnp.bfloat16)] + [pltpu.VMEM((length, 128), jnp.float32)] * 3,
        count * length * (2 * features * 128 + 5 * PAIR_WORK * length),
        waits,
    )[0]


def exchanged(parts):
    return parts[0], flip_pairs(parts[1], 1)


def model_rows(kernel, name, lefts, pieces, waits=()):
    length, width = lefts[0].shape[0], 2 * MODEL_HALF
    outs = (((length // 2, width), jnp.float32), ((length // 2, width), jnp.bfloat16))
    hidden = sum(left.shape[1] for left in lefts)
    more = {"limit": KERNEL_VMEM, "flops": 2 * length * width * hidden, "waits": waits}
    return exchanged(on_chip(kernel, name, outs, *lefts, *pieces[0], *pieces[1], **more))


def flip_pairs(block, distance):
    size = lax.axis_size("dp")
    return lax.ppermute(block, "dp", [(i, i ^ distance) for i in range(size)])


def passed_on(block, step):
    size = lax.axis_size("tensor")
    return lax.ppermute(block, "tensor", [(i, (i + step) % size) for i in range(size)])


def dot_tn(left, right):
    return lax.dot_general(
        left, right, (((0,), (0,)), ((), ())), preferred_element_type=jnp.float32
    )


def fetch(first_ref, zeros, ones, buffers, sems):
    for section, sources in enumerate((zeros, ones)):

        @pl.when(first_ref[0] == section)
        def _():
            for i, (source, buffer) in enumerate(zip(sources, buffers)):
                pltpu.make_async_copy(source, buffer, sems.at[i]).start()

    def arrived(*places):
        for i in places:
            pltpu.make_async_copy(zeros[i], buffers[i], sems.at[i]).wait()

    return arrived


def mlp_grads_kernel(base, section_ref, *refs):
    (own_one, other_one, own_two, other_two), (rows, d_up, gelu, d_down, sems) = refs[12:16], refs[16:]
    half, size = own_one.shape[0] // 2, own_one.shape[1]
    cols = pl.ds(base * size, 2 * size)

    def parts(own_rows, other_rows, d_up_ref, gelu_ref, own_grad, other_grad):
        whole = (d_up_ref.at[:, cols], gelu_ref.at[:, cols])
        return (own_rows, other_rows, *whole, own_grad, other_grad)

    count = refs[0].shape[0]
    buffers = (
        rows.at[pl.ds(0, count)],
        rows.at[pl.ds(count, count)],
        d_up,
        gelu,
        d_down.at[pl.ds(0, count)],
        d_down.at[pl.ds(count, count)],
    )
    arrived = fetch(section_ref, parts(*refs[:6]), parts(*refs[6:12]), buffers, sems)
    for j, own, other in ((1, own_two, other_two), (0, own_one, other_one)):
        cols = slice(j * size, (j + 1) * size)
        if j == 1:
            arrived(0, 1, 2)
        up = dot_tn(rows[...], d_up[:, cols])
        own[:half] = up[:half]
        other[:half] = up[half:].astype(jnp.bfloat16)
        if j == 1:
            arrived(3, 4, 5)
        down = dot_tn(gelu[:, cols], d_down[...])
        own[half:] = down[:, :half]
        other[half:] = down[:, half:].astype(jnp.bfloat16)


def attn_grads_kernel(base, section_ref, *refs):
    (own_one, other_one, own_two, other_two), (rows, d_qkv, mixed, d_attn, sems) = refs[12:16], refs[16:]
    half, size = own_one.shape[0], d_qkv.shape[1] // 2
    count = refs[0].shape[0]
    cols = pl.ds(base * 128, 256)

    def parts(own_rows, other_rows, d_qkv_ref, mixed_ref, own_grad, other_grad):
        return (own_rows, other_rows, d_qkv_ref, mixed_ref.at[:, cols], own_grad, other_grad)

    buffers = (
        rows.at[pl.ds(0, count)],
        rows.at[pl.ds(count, count)],
        d_qkv,
        mixed,
        d_attn.at[pl.ds(0, count)],
        d_attn.at[pl.ds(count, count)],
    )
    arrived = fetch(section_ref, parts(*refs[:6]), parts(*refs[6:12]), buffers, sems)
    for j, own, other in ((1, own_two, other_two), (0, own_one, other_one)):
        if j == 1:
            arrived(0, 1, 2)
        qkv = dot_tn(rows[...], d_qkv[:, j * size : (j + 1) * size])
        if j == 1:
            arrived(3, 4, 5)
        out = dot_tn(d_attn[...], mixed[:, j * 128 : (j + 1) * 128])
        own[:, :size] = qkv[:half]
        own[:, size:] = out[:half]
        other[:, :size] = qkv[half:].astype(jnp.bfloat16)
        other[:, size:] = out[half:].astype(jnp.bfloat16)


def weight_grads(kernel, name, base, section, zeros, ones, shape, columns, waits=()):
    length = 2 * zeros[0].shape[0]
    width = zeros[0].shape[1]
    every = pl.BlockSpec(memory_space=pl.ANY)
    space = pl.BlockSpec(memory_space=pltpu.VMEM)
    arrays = (*zeros, *ones)
    first, second, third, fourth = pl.pallas_call(
        without(functools.partial(kernel, base), 1 + len(arrays), len(waits)),
        in_specs=[pl.BlockSpec(memory_space=pltpu.SMEM)] + [every] * (len(arrays) + len(waits)),
        out_specs=[space] * 4,
        out_shape=[
            jax.ShapeDtypeStruct(shape, jnp.float32),
            jax.ShapeDtypeStruct(shape, jnp.bfloat16),
        ]
        * 2,
        scratch_shapes=[
            pltpu.VMEM((length, width), jnp.bfloat16),
            pltpu.VMEM((length, columns[0]), jnp.bfloat16),
            pltpu.VMEM((length, columns[1]), jnp.bfloat16),
            pltpu.VMEM((length, width), jnp.bfloat16),
            pltpu.SemaphoreType.DMA((6,)),
        ],
        compiler_params=pltpu.CompilerParams(vmem_limit_bytes=KERNEL_VMEM),
        name=name,
    )(section, *map(far, (*arrays, *waits)))
    return [(first, flip_pairs(second, 2)), (third, flip_pairs(fourth, 2))]


def moved_kernel(own_ref, other_ref, *refs):
    out_ref = refs[-1]

    def body(i, carry):
        spot = pl.ds(pl.multiple_of(i * CHUNK, CHUNK), CHUNK)
        total = own_ref[spot, :]
        for ref in (other_ref, *refs[:-1]):
            total = total + wide(ref, spot)
        out_ref[spot, :] = total.astype(jnp.bfloat16)
        return carry

    lax.fori_loop(0, own_ref.shape[0] // CHUNK, body, 0)


def gate_kernel(piece_ref, out_ref):
    out_ref[...] = piece_ref[...]


def mlp_sum_kernel(core_ref, own_ref, other_ref, moved_ref, up_keep, down_keep, up_send, down_send):
    half = own_ref.shape[0] // 2
    size = up_keep.shape[0]

    def total(rows, cols):
        more = other_ref[rows, cols].astype(jnp.float32) + moved_ref[rows, cols].astype(jnp.float32)
        return own_ref[rows, cols] + more

    for core in range(2):

        @pl.when(core_ref[0] == core)
        def _():
            for place, up, down in ((core, up_keep, down_keep), (1 - core, up_send, down_send)):
                spot = slice(place * size, (place + 1) * size)
                up[...] = total(spot, slice(None))
                down[...] = total(slice(half, None), spot)


def mlp_join_kernel(core_ref, up_keep, down_keep, up_sent, down_sent, up_out, down_out):
    size = up_keep.shape[1]
    for core in range(2):

        @pl.when(core_ref[0] == core)
        def _():
            places = ((core, up_keep, down_keep), (1 - core, up_sent, down_sent))
            for place, up, down in places:
                spot = slice(place * size, (place + 1) * size)
                up_out[:, spot] = up[...]
                down_out[spot] = down[...]


def pick_kernel(core_ref, rows_ref, keep_ref, send_ref):
    count = keep_ref.shape[0]
    keep_ref[...] = rows_ref[pl.ds(core_ref[0] * count, count)]
    send_ref[...] = rows_ref[pl.ds((1 - core_ref[0]) * count, count)]


def both_kernel(core_ref, keep_ref, sent_ref, out_ref):
    count = keep_ref.shape[0]
    out_ref[pl.ds(core_ref[0] * count, count)] = keep_ref[...]
    out_ref[pl.ds((1 - core_ref[0]) * count, count)] = sent_ref[...]


def in_order_kernel(core_ref, keep_ref, sent_ref, out_ref):
    out_ref[:, pl.ds(core_ref[0], 1)] = keep_ref[...][:, None]
    out_ref[:, pl.ds(1 - core_ref[0], 1)] = sent_ref[...][:, None]


def with_core(kernel, name, core, outs, *operands, waits=()):
    space = pl.BlockSpec(memory_space=pltpu.VMEM)
    return pl.pallas_call(
        without(kernel, 1 + len(operands), len(waits)),
        in_specs=[pl.BlockSpec(memory_space=pltpu.SMEM)]
        + [space] * len(operands)
        + [pl.BlockSpec(memory_space=pl.ANY)] * len(waits),
        out_specs=[space] * len(outs),
        out_shape=[jax.ShapeDtypeStruct(shape, dtype) for shape, dtype in outs],
        compiler_params=pltpu.CompilerParams(vmem_limit_bytes=ROWS_VMEM),
        name=name,
    )(core, *operands, *map(far, waits))


def last_sum_kernel(core_ref, own_ref, other_ref, moved_ref, keep_ref, send_ref):
    rows = keep_ref.shape[0]

    def total(block):
        spot = pl.ds(pl.multiple_of(block * rows, rows), rows)
        return own_ref[spot, :] + wide(other_ref, spot) + wide(moved_ref, spot)

    keep_ref[...] = total(core_ref[0])
    send_ref[...] = total(1 - core_ref[0])


def joined_kernel(spots, core_ref, keep_ref, sent_ref, column_ref, row_ref):
    size = row_ref.shape[0] // 2
    for core in range(2):

        @pl.when(core_ref[0] == core)
        def _():
            for place, source in ((core, keep_ref), (1 - core, sent_ref)):
                for start, stop, to in spots:
                    step = stop - start
                    column_ref[:, to + place * step : to + (place + 1) * step] = source[:, start:stop]
                row_ref[place * size : (place + 1) * size] = source[:, spots[-1][1] :].T


def per_chip(
    inputs,
    out_cotangent,
    group_ids,
    group_weights,
    gains,
    qkv_weight,
    out_weight,
    up_weight,
    down_weight,
):
    micro, row_count, width = inputs.shape
    tensor = lax.axis_size("tensor")
    part = row_count // 2
    wide_half = width // 2
    length = tensor * row_count
    half = length // 2
    first = lax.axis_index("section") == 0
    place = lax.axis_index("dp")
    core = place % 2
    upper = place // 2 % 2
    core_zero = core == 0
    low_half = upper == 0

    def ordered(mine, other):
        return jnp.where(core_zero, mine, other), jnp.where(core_zero, other, mine)

    def own_first(values):
        return jnp.where(low_half, values, jnp.roll(values, wide_half, axis=-1))

    def both_rows(own):
        return own, flip_pairs(own, 1)

    def to_chip(block):
        split = block.reshape((micro, 2, part) + block.shape[2:])
        mine = lax.dynamic_index_in_dim(split, core, 1, keepdims=False)
        other = lax.dynamic_index_in_dim(split, 1 - core, 1, keepdims=False)
        outs = (((2 * micro, part, width), jnp.bfloat16),)
        (rows,) = with_core(
            both_kernel, "both", core_word, outs, mine, flip_pairs(other, 1), waits=(attn_piece,)
        )
        return lax.all_to_all(rows, "tensor", 0, 0, tiled=True)

    def from_chip(spread_out, waits=()):
        piece = ((micro, part, width), jnp.bfloat16)
        keep, send = with_core(
            pick_kernel, "pick", core_word, (piece, piece), spread_out, waits=waits
        )
        outs = (((micro, 2, part, width), jnp.bfloat16),)
        (rows,) = with_core(
            in_order_kernel, "in_order", core_word, outs, keep, flip_pairs(send, 1)
        )
        return rows.reshape(micro, row_count, width)

    def columns(local):
        size = local.shape[-1] // 2
        mid = (0,) * (local.ndim - 2)
        piece = lax.dynamic_slice(
            local,
            (wide_half * upper, *mid, size * core),
            (wide_half, *local.shape[1:-1], size),
        )
        return piece.reshape(wide_half, -1)

    def rows(local):
        size = local.shape[0] // 2
        return lax.dynamic_slice(local, (size * core, wide_half * upper), (size, wide_half))

    core_word = core.astype(jnp.int32).reshape(1)
    attn_piece = jnp.concatenate([columns(qkv_weight[0]), rows(out_weight[0]).T], axis=1)

    def spread(piece):
        pieces = [piece]
        for _ in range(tensor - 1):
            pieces.append(passed_on(pieces[-1], 1))
        return pieces

    attn_own = spread(attn_piece)
    attn_other = [flip_pairs(piece, 2) for piece in attn_own]
    up_piece, down_piece = columns(up_weight[0]), rows(down_weight[0])
    up_other, down_other = [flip_pairs(up_piece, 2)], [flip_pairs(down_piece, 2)]
    (up_piece,) = on_chip(
        gate_kernel,
        "gate",
        ((up_piece.shape, up_piece.dtype),),
        up_piece,
        waits=(attn_own[2], attn_other[0]),
    )
    (down_piece,) = on_chip(
        gate_kernel,
        "gate",
        ((down_piece.shape, down_piece.dtype),),
        down_piece,
        waits=(attn_own[3],),
    )
    up_own, down_own = spread(up_piece), spread(down_piece)
    up_other += [flip_pairs(piece, 2) for piece in up_own[1:]]
    down_other += [flip_pairs(piece, 2) for piece in down_own[1:]]
    w_attn, w_up, w_down = (attn_own, attn_other), (up_own, up_other), (down_own, down_other)
    unit = up_piece.shape[1]
    units = tensor * unit

    group_count = group_weights.shape[0]
    matches = group_ids[..., None] == jnp.arange(group_count, dtype=jnp.int32)
    row_scale = jnp.sum(jnp.where(matches, group_weights, 0.0), axis=-1)
    weighted = (out_cotangent.astype(jnp.float32) * row_scale[..., None]).astype(jnp.bfloat16)
    start = to_chip(own_first(jnp.where(first, inputs, weighted))).reshape(half, width)
    gain = own_first(gains[0])

    turns = jnp.arange(half, dtype=jnp.int32)
    turns = turns // part * row_count + turns % part
    positions = jnp.concatenate([turns + core * part, turns + (1 - core) * part])
    freqs = 10000.0 ** (-2.0 * jnp.arange(HEAD_DIM // 2, dtype=jnp.float32) / HEAD_DIM)
    angles = positions.astype(jnp.float32)[:, None] * freqs[None, :]
    cos_part, sin_part = jnp.cos(angles), jnp.sin(angles)
    tables = (
        jnp.concatenate([cos_part] * 4, axis=1),
        jnp.concatenate([-sin_part, sin_part] * 2, axis=1),
    )
    row32, row16 = ((half, width), jnp.float32), ((half, width), jnp.bfloat16)
    unit16 = ((length, units), jnp.bfloat16)
    sum32 = ((1, width), jnp.float32)
    mlp_cost = {"limit": KERNEL_VMEM, "flops": 2 * length * width * units}
    every = slice(None)

    def model_kernel(cols, lefts=1):
        return functools.partial(to_model_kernel, lefts, tensor, cols)

    down_kernel = functools.partial(mlp_down_kernel, tensor)

    def forward(layer_input, waits):
        attn_in = both_rows(
            on_chip(norm_in_kernel, "norm_in", (row16,), gain, layer_input, waits=waits[0])[0]
        )
        *heads, mixed = attend(core_word, tables, attn_in, w_attn, waits[1])
        parts = model_rows(model_kernel(OUT), "attn_out", [mixed], w_attn, waits[2])
        operands = (gain, layer_input, *parts)
        branch, hidden, mlp_in = on_chip(
            after_attention_kernel, "after_attn", (row32, row32, row16), *operands, waits=waits[3]
        )
        mlp_in = both_rows(mlp_in)
        kernel = functools.partial(mlp_up_kernel, tensor)
        operands = (*mlp_in, *w_up[0], *w_up[1])
        gelu_out, slope = on_chip(kernel, "mlp_up", (unit16, unit16), *operands, **mlp_cost)
        parts = model_rows(down_kernel, "mlp_down", [gelu_out], w_down)
        mlp_branch, result = on_chip(
            after_mlp_kernel, "after_mlp", (row32, row16), gain, hidden, *parts
        )
        saved = (layer_input, heads, branch, hidden, slope, mlp_branch)
        return result, saved, (attn_in, mixed, mlp_in, gelu_out)

    def backward(grad, saved, hook, late=()):
        layer_input, heads, branch, hidden, slope, mlp_branch = saved
        operands = (gain, grad, mlp_branch)
        d_down, sum_three = on_chip(
            into_mlp_back_kernel, "into_mlp_back", (row16, sum32), *operands
        )
        d_down = both_rows(d_down)
        d_up = mlp_up_back(d_down, slope, w_down, late)
        waits = hook(d_down, d_up)
        parts = model_rows(model_kernel(every), "mlp_back", [d_up], w_up, waits)
        waits = hook()
        operands = (gain, grad, *parts, hidden, branch)
        outs = (row32, row16, sum32, sum32)
        d_hidden, d_attn, sum_one, sum_two = on_chip(
            into_attention_back_kernel, "into_attn_back", outs, *operands, waits=waits
        )
        d_attn = both_rows(d_attn)
        waits = hook(d_attn)
        d_qkv = []
        for base in reversed(range(0, tensor, 2)):
            some = [side[base : base + 2] for side in w_attn]
            now = attend_back(core_word, tables, d_attn, some, base, waits, *heads)
            d_qkv.insert(0, now)
            waits = hook(now)
        parts = model_rows(model_kernel(QKV, 2), "attn_back", d_qkv, w_attn, waits)
        operands = (gain, layer_input, *parts, d_hidden)
        d_input, sum_zero = on_chip(
            out_of_layer_kernel, "out_of_layer", (row16, sum32), *operands, waits=hook()
        )
        sums = jnp.concatenate([sum_zero, sum_one, sum_two, sum_three])
        return d_input, (d_qkv, d_attn, d_up, d_down), sums

    low_zero, saved_zero, lefts_zero = forward(
        start,
        (
            (up_piece, up_other[0], down_other[0]),
            (up_own[1], down_own[1]),
            (up_own[2], down_own[2], up_other[1]),
            (up_own[3], down_own[3], down_other[1], up_other[2]),
        ),
    )
    low_one, saved_one, lefts_one = forward(shifted(low_zero, "section", 1), ((),) * 4)
    grad_one, rights_one, gain_one = backward(start, saved_one, lambda *new: ())
    received = shifted(grad_one, "section", -1)

    lows = lax.optimization_barrier((low_zero, low_one, grad_one))[:2]
    lows = own_first(jnp.where(first, *lows)).reshape(tensor, part, width)
    lows = lax.all_to_all(lows, "tensor", 0, 0, tiled=True)

    section_word = lax.axis_index("section").astype(jnp.int32).reshape(1)

    def mlp_leaves(base):
        zeros = (*lefts_zero[2], d_up, lefts_zero[3], *d_down)
        ones = (*lefts_one[2], rights_one[2], lefts_one[3], *rights_one[3])
        mlp_sums[base : base + 2] = weight_grads(
            mlp_grads_kernel,
            "mlp_grads",
            base,
            section_word,
            zeros,
            ones,
            (wide_half + unit, unit),
            (2 * unit, 2 * unit),
        )

    def attn_leaves(base, d_qkv, waits):
        zeros = (*lefts_zero[0], d_qkv, lefts_zero[1], *d_attn)
        ones = (*lefts_one[0], rights_one[0][base // 2], lefts_one[1], *rights_one[1])
        attn_sums[base : base + 2] = weight_grads(
            attn_grads_kernel,
            "attn_grads",
            base,
            section_word,
            zeros,
            ones,
            (wide_half, 512),
            (768, 256),
            waits,
        )

    def moves_on(piece, *moved, waits=()):
        outs = ((piece[1].shape, jnp.bfloat16),)
        (total,) = on_chip(moved_kernel, "moved", outs, *piece, *moved, waits=waits)
        return total, passed_on(total, -1)

    mlp_sums, attn_sums = [None] * tensor, [None] * tensor
    mlp_moves, attn_moves = [None] * tensor, [None] * tensor
    hooks = iter(range(6))

    def hook(*new):
        nonlocal d_down, d_up, d_attn
        turn = next(hooks)
        if turn == 0:
            d_down, d_up = new
            mlp_leaves(2)
            return (mlp_sums[3][0],)
        if turn == 1:
            mlp_leaves(0)
            return (mlp_sums[1][0],)
        if turn == 2:
            (d_attn,) = new
            _, mlp_moves[3] = moves_on(mlp_sums[3], waits=d_attn[:1])
            return (mlp_sums[3][1],)
        if turn == 3:
            total, mlp_moves[2] = moves_on(mlp_sums[2], mlp_moves[3], waits=new)
            attn_leaves(2, new[0], (total,))
            return (mlp_sums[2][1], mlp_moves[3], attn_sums[3][0])
        if turn == 4:
            total, mlp_moves[1] = moves_on(mlp_sums[1], mlp_moves[2], waits=new)
            attn_leaves(0, new[0], (total,))
            return (attn_sums[1][0],)
        total, attn_moves[3] = moves_on(attn_sums[3])
        return (mlp_sums[0][1], total, mlp_moves[1])

    d_down = d_up = d_attn = None
    grad_zero, rights_zero, gain_zero = backward(received, saved_zero, hook, (lows,))
    _, attn_moves[2] = moves_on(attn_sums[2], attn_moves[3])
    last, attn_moves[1] = moves_on(attn_sums[1], attn_moves[2], waits=attn_sums[0][1:])
    gain_zero, gain_one = lax.optimization_barrier((gain_zero, gain_one))
    gain_total = own_first(jnp.where(first, gain_zero, gain_one))
    count = tensor * lax.axis_size("dp")
    gain_parts = gain_total.reshape(4, count, width // count).swapaxes(0, 1)
    (gain_parts,) = on_chip(
        gate_kernel, "gate", ((gain_parts.shape, gain_parts.dtype),), gain_parts, waits=(last,)
    )
    gain_parts = lax.all_to_all(gain_parts, ("dp", "tensor"), 0, 0, tiled=True)
    gains_grad = jnp.sum(gain_parts, axis=0)
    outputs = from_chip(lows, (last,))
    grads = own_first(jnp.where(first, grad_zero, grad_one)).reshape(tensor, part, width)
    grads = from_chip(lax.all_to_all(grads, "tensor", 0, 0, tiled=True), (last,))

    block32 = ((wide_half // 2, unit), jnp.float32)
    down32 = ((unit, wide_half // 2), jnp.float32)
    up_keep, down_keep, up_send, down_send = with_core(
        mlp_sum_kernel,
        "mlp_sum",
        core_word,
        (block32, down32, block32, down32),
        *mlp_sums[0],
        mlp_moves[1],
        waits=(last,),
    )
    outs = (
        ((wide_half // 2, 2 * unit), jnp.float32),
        ((2 * unit, wide_half // 2), jnp.float32),
    )
    sent = flip_pairs(up_send, 1), flip_pairs(down_send, 1)
    up_grad, down_grad = with_core(
        mlp_join_kernel, "mlp_join", core_word, outs, up_keep, down_keep, *sent
    )
    outs = (((wide_half // 2, 512), jnp.float32),) * 2
    keep, send = with_core(
        last_sum_kernel,
        "attn_sum",
        core_word,
        outs,
        *attn_sums[0],
        attn_moves[1],
        waits=(outputs, grads, gains_grad, up_grad),
    )
    spots = tuple((i * 128, (i + 1) * 128, i * 256) for i in range(3))
    outs = (((wide_half // 2, 768), jnp.float32), ((256, wide_half // 2), jnp.float32))
    kernel = functools.partial(joined_kernel, spots)
    qkv_grad, out_grad = with_core(
        kernel, "attn_join", core_word, outs, keep, flip_pairs(send, 1)
    )
    qkv_grad = qkv_grad.reshape(wide_half // 2, 3, -1)

    return (
        outputs[None],
        grads[None],
        gains_grad[None],
        qkv_grad[None],
        out_grad[None],
        up_grad[None],
        down_grad[None],
    )


def takes_chips(sizes):
    return sizes["section"] == 2 and sizes["dp"] == 4 and sizes["tensor"] == 4


def solution(mesh):
    placed = (
        P("dp", "tensor", None),
        P("dp", "tensor", None),
        P("dp", "tensor"),
        P(),
        P("section", None, None),
        P("section", None, None, "tensor"),
        P("section", "tensor", None),
        P("section", None, "tensor"),
        P("section", "tensor", None),
    )
    body = per_chip if takes_chips(dict(mesh.shape)) else per_device
    return jax.shard_map(
        body,
        mesh=mesh,
        in_specs=placed,
        out_specs=(
            P("section", "dp", "tensor", None),
            P("section", "dp", "tensor", None),
            P("section", None, ("dp", "tensor")),
            P("section", "dp", None, "tensor"),
            P("section", "tensor", "dp"),
            P("section", "dp", "tensor"),
            P("section", "tensor", "dp"),
        ),
        check_vma=False,
    )
```

```python
import functools
import math

import jax
import jax.numpy as jnp
from jax import lax
from jax.experimental import pallas as pl
from jax.experimental.pallas import tpu as pltpu
from jax.sharding import PartitionSpec as P

HEAD_DIM = 64


NORM_EPSILON = 1e-06
TILE = 128
PAIR_WORK = 1024
MODEL_HALF = 512
QKV = slice(0, 384)
OUT = slice(384, 512)
CHUNK = 32
KERNEL_VMEM = 20 << 20
ROWS_VMEM = 3 << 20


def shifted(block, axis, distance):
    devices = range(lax.axis_size(axis))
    route = [(i - distance, i) for i in devices if i - distance in devices]
    return lax.ppermute(block, axis, route)


def norm_rows(vector, weight_gain):
    return (
        vector
        * lax.rsqrt(jnp.mean(vector * vector, axis=-1, keepdims=True) + NORM_EPSILON)
        * weight_gain
    )


def rotary_tables(seq_len, head_width):
    half_width = head_width // 2
    freqs = 10000.0 ** (-2.0 * jnp.arange(half_width, dtype=jnp.float32) / head_width)
    angles = jnp.arange(seq_len, dtype=jnp.float32)[:, None] * freqs[None, :]
    return (jnp.cos(angles), jnp.sin(angles))


def rotate(vector, cos_table, sin_table):
    first_half, second_half = jnp.split(vector, 2, axis=-1)
    cos_part = cos_table[:, None, :]
    sin_part = sin_table[:, None, :]
    return jnp.concatenate(
        [
            first_half * cos_part - second_half * sin_part,
            second_half * cos_part + first_half * sin_part,
        ],
        axis=-1,
    )


def contract(left_rows, right_rows):
    return lax.dot_general(
        left_rows, right_rows, (((0,), (0,)), ((), ())), preferred_element_type=jnp.float32
    )


def gather_rows(row_values, weight):

    def project(shard_rows, offset):
        return (shard_rows, jnp.dot(shard_rows, weight, preferred_element_type=jnp.float32))

    return project(lax.all_gather(row_values, "tensor", axis=0, tiled=True), jnp.int32(0))


def scatter_rows(row_values, weight, row_count):

    def partial_term(offset, span):
        return jnp.dot(row_values, weight, preferred_element_type=jnp.float32)

    return lax.psum_scatter(
        partial_term(jnp.int32(0), lax.axis_size("tensor") * row_count),
        "tensor",
        scatter_dimension=0,
        tiled=True,
    )


def gather_grads(row_values, weight):

    def project(shard_rows, offset):
        return (shard_rows, jnp.dot(shard_rows, weight.T, preferred_element_type=jnp.float32))

    return project(lax.all_gather(row_values, "tensor", axis=0, tiled=True), jnp.int32(0))


def scatter_grads(row_values, weight, row_count):

    def partial_term(offset, span):
        return jnp.dot(row_values, weight.T, preferred_element_type=jnp.float32)

    return lax.psum_scatter(
        partial_term(jnp.int32(0), lax.axis_size("tensor") * row_count),
        "tensor",
        scatter_dimension=0,
        tiled=True,
    )


def attention_probs(queries, key_rows):
    scores = jnp.einsum(
        "qhd,khd->hqk", queries, key_rows, preferred_element_type=jnp.float32
    ) * HEAD_DIM ** (-0.5)
    length = queries.shape[0]
    positions = jnp.arange(length, dtype=jnp.int32)
    causal = positions[:, None] >= positions[None, :]
    scores = jnp.where(causal[None], scores, -1e30)
    expos = jnp.exp(scores - jnp.max(scores, axis=-1, keepdims=True))
    return expos / jnp.sum(expos, axis=-1, keepdims=True)


def layer_forward(layer_input, weights):
    gains, w_qkv, w_out, w_up, w_down = weights
    row_count, model_width = layer_input.shape
    attn_in = norm_rows(layer_input, gains[0]).astype(jnp.bfloat16)
    gathered_a, qkv = gather_rows(attn_in, w_qkv.reshape(model_width, -1))
    length = qkv.shape[0]
    head_count = w_qkv.shape[2] // HEAD_DIM
    qkv = qkv.reshape(length, 3, head_count, HEAD_DIM)
    cos_table, sin_table = rotary_tables(length, HEAD_DIM)
    queries = rotate(qkv[:, 0], cos_table, sin_table).astype(jnp.bfloat16)
    key_rows = rotate(qkv[:, 1], cos_table, sin_table).astype(jnp.bfloat16)
    values = qkv[:, 2].astype(jnp.bfloat16)
    attn_probs = attention_probs(queries, key_rows).astype(jnp.bfloat16)
    mixed = jnp.einsum("hqk,khd->qhd", attn_probs, values, preferred_element_type=jnp.float32)
    mixed = mixed.reshape(length, -1).astype(jnp.bfloat16)
    attn_branch = scatter_rows(mixed, w_out, row_count)
    hidden = layer_input + norm_rows(attn_branch, gains[1])
    mlp_in = norm_rows(hidden, gains[2]).astype(jnp.bfloat16)
    gathered_c, up_act = gather_rows(mlp_in, w_up)
    gelu_out = jax.nn.gelu(up_act, approximate=True).astype(jnp.bfloat16)
    down_branch = scatter_rows(gelu_out, w_down, row_count)
    result = hidden + norm_rows(down_branch, gains[3])
    kept_values = (
        gathered_a,
        queries,
        key_rows,
        values,
        mixed,
        attn_branch,
        hidden,
        gathered_c,
        up_act,
        gelu_out,
        down_branch,
    )
    return (result, kept_values)


def layer_backward(layer_input, grad_result, kept_values, weights):
    gains, w_qkv, w_out, w_up, w_down = weights
    (
        gathered_a,
        queries,
        key_rows,
        values,
        mixed,
        attn_branch,
        hidden,
        gathered_c,
        up_act,
        gelu_out,
        down_branch,
    ) = kept_values
    row_count, model_width = layer_input.shape
    pullback = jax.vjp(norm_rows, down_branch, gains[3])[1]
    grad_down, gain_three = pullback(grad_result)
    gathered_dd, grad_gelu = gather_grads(grad_down.astype(jnp.bfloat16), w_down)
    down_total = contract(gelu_out, gathered_dd)
    pullback = jax.vjp(lambda vector: jax.nn.gelu(vector, approximate=True), up_act)[1]
    grad_up = pullback(grad_gelu)[0].astype(jnp.bfloat16)
    up_total = contract(gathered_c, grad_up)
    grad_mlp = scatter_grads(grad_up, w_up, row_count)
    pullback = jax.vjp(norm_rows, hidden, gains[2])[1]
    grad_norm_mlp, gain_two = pullback(grad_mlp)
    grad_hidden = grad_result + grad_norm_mlp
    pullback = jax.vjp(norm_rows, attn_branch, gains[1])[1]
    grad_attn, gain_one = pullback(grad_hidden)
    gathered_da, grad_mixed = gather_grads(grad_attn.astype(jnp.bfloat16), w_out)
    out_total = contract(mixed, gathered_da)
    length = grad_mixed.shape[0]
    head_count = w_qkv.shape[2] // HEAD_DIM
    grad_mixed = grad_mixed.astype(jnp.bfloat16).reshape(length, head_count, HEAD_DIM)
    attn_probs = attention_probs(queries, key_rows)
    probs_low = attn_probs.astype(jnp.bfloat16)
    grad_probs = jnp.einsum("qhd,khd->hqk", grad_mixed, values, preferred_element_type=jnp.float32)
    grad_values = jnp.einsum(
        "hqk,qhd->khd", probs_low, grad_mixed, preferred_element_type=jnp.float32
    )
    row_dots = jnp.sum(grad_probs * attn_probs, axis=-1, keepdims=True)
    grad_scores = (attn_probs * (grad_probs - row_dots)).astype(jnp.bfloat16)
    scale_value = HEAD_DIM ** (-0.5)
    grad_queries = (
        jnp.einsum("hqk,khd->qhd", grad_scores, key_rows, preferred_element_type=jnp.float32)
        * scale_value
    )
    grad_keys = (
        jnp.einsum("hqk,qhd->khd", grad_scores, queries, preferred_element_type=jnp.float32)
        * scale_value
    )
    cos_table, sin_table = rotary_tables(length, HEAD_DIM)
    pullback = jax.vjp(lambda vector: rotate(vector, cos_table, sin_table), grad_queries)[1]
    grad_q_raw = pullback(grad_queries)[0]
    grad_k_raw = pullback(grad_keys)[0]
    grad_qkv = (
        jnp.stack([grad_q_raw, grad_k_raw, grad_values], axis=1)
        .reshape(length, -1)
        .astype(jnp.bfloat16)
    )
    qkv_total = contract(gathered_a, grad_qkv).reshape(model_width, 3, -1)
    grad_attn_in = scatter_grads(grad_qkv, w_qkv.reshape(model_width, -1), row_count)
    pullback = jax.vjp(norm_rows, layer_input, gains[0])[1]
    grad_norm_in, gain_zero = pullback(grad_attn_in)
    grad_input = grad_hidden + grad_norm_in
    gain_total = jnp.stack([gain_zero, gain_one, gain_two, gain_three])
    return (grad_input, (gain_total, qkv_total, out_total, up_total, down_total))


def lagged(first_section, stacked):
    blank = jnp.zeros_like(stacked[:1])
    earlier = jnp.concatenate([blank, stacked[:-1]])
    later = jnp.concatenate([stacked[1:], blank])
    return jnp.where(first_section, earlier, later)


def per_device(
    inputs,
    out_cotangent,
    group_ids,
    group_weights,
    gains,
    qkv_weight,
    out_weight,
    up_weight,
    down_weight,
):
    weights = (gains[0], qkv_weight[0], out_weight[0], up_weight[0], down_weight[0])
    micro_count, row_count, model_width = inputs.shape
    first_section = lax.axis_index("section") == 0
    group_count = group_weights.shape[0]
    matches = group_ids[..., None] == jnp.arange(group_count, dtype=jnp.int32)
    row_scale = jnp.sum(jnp.where(matches, group_weights, 0.0), axis=-1)
    scaled = out_cotangent.astype(jnp.float32) * row_scale[..., None]
    padded = jnp.concatenate([inputs, jnp.zeros((1, row_count, model_width), jnp.bfloat16)])

    def forward_tick(received, fresh_input):
        layer_input = jnp.where(first_section, fresh_input, received)
        result, kept_values = layer_forward(layer_input.astype(jnp.float32), weights)
        result_low = result.astype(jnp.bfloat16)
        outgoing = shifted(result_low, "section", 1)
        stashed = ()
        return (outgoing, (layer_input, result_low, stashed))

    start_rows = jnp.zeros((row_count, model_width), jnp.bfloat16)
    _, (layer_inputs, layer_results, stashed) = lax.scan(forward_tick, start_rows, padded)
    layer_outputs = jnp.where(first_section, layer_results[:-1], layer_results[1:])[None]
    back_inputs = lagged(first_section, layer_inputs)
    back_stash = jax.tree.map(lambda stacked: lagged(first_section, stacked), stashed)
    grad_padded = jnp.concatenate([scaled, jnp.zeros((1, row_count, model_width), jnp.float32)])
    tick_index = jnp.arange(micro_count + 1, dtype=jnp.int32)
    tick_valid = jnp.where(first_section, tick_index >= 1, tick_index < micro_count).astype(
        jnp.float32
    )

    def backward_tick(carry, step_item):
        received, totals = carry
        layer_input, cotangent, valid_now, stash_now = step_item
        grad_now = jnp.where(first_section, received.astype(jnp.float32), cotangent)
        input_now = layer_input.astype(jnp.float32)
        kept_values = layer_forward(input_now, weights)[1]
        grad_input, layer_grads = layer_backward(input_now, grad_now, kept_values, weights)
        totals = jax.tree.map(lambda total, update: total + valid_now * update, totals, layer_grads)
        grad_low = grad_input.astype(jnp.bfloat16)
        outgoing = shifted(grad_low, "section", -1)
        return ((outgoing, totals), grad_low)

    start_totals = (
        jnp.zeros((4, model_width), jnp.float32),
        jnp.zeros(qkv_weight.shape[1:], jnp.float32),
        jnp.zeros(out_weight.shape[1:], jnp.float32),
        jnp.zeros(up_weight.shape[1:], jnp.float32),
        jnp.zeros(down_weight.shape[1:], jnp.float32),
    )
    (_, totals), grad_lows = lax.scan(
        backward_tick,
        (start_rows, start_totals),
        (back_inputs, grad_padded, tick_valid, back_stash),
    )
    input_grads = jnp.where(first_section, grad_lows[1:], grad_lows[:-1])[None]
    gain_total, qkv_total, out_total, up_total, down_total = totals
    gains_grad = lax.psum_scatter(gain_total, ("dp", "tensor"), scatter_dimension=1, tiled=True)
    qkv_grad, out_grad, up_grad, down_grad = (
        lax.psum_scatter(
            qkv_total.astype(jnp.bfloat16), "dp", scatter_dimension=0, tiled=True
        ).astype(jnp.float32),
        lax.psum_scatter(
            out_total.astype(jnp.bfloat16), "dp", scatter_dimension=1, tiled=True
        ).astype(jnp.float32),
        lax.psum_scatter(
            up_total.astype(jnp.bfloat16), "dp", scatter_dimension=0, tiled=True
        ).astype(jnp.float32),
        lax.psum_scatter(
            down_total.astype(jnp.bfloat16), "dp", scatter_dimension=1, tiled=True
        ).astype(jnp.float32),
    )
    return (
        layer_outputs,
        input_grads,
        gains_grad[None],
        qkv_grad[None],
        out_grad[None],
        up_grad[None],
        down_grad[None],
    )


def rotated(block, cos_rows, sin_rows):
    lane = lax.broadcasted_iota(jnp.int32, block.shape, 1)
    ahead = pltpu.roll(block, 96, 1)
    behind = pltpu.roll(block, 32, 1)
    swapped = jnp.where(lane % 64 < 32, ahead, behind)
    return block * cos_rows + swapped * sin_rows


def dot_nt(left, right):
    return lax.dot_general(
        left, right, (((1,), (1,)), ((), ())), preferred_element_type=jnp.float32
    )


def dot_nn(left, right):
    return jnp.dot(left, right, preferred_element_type=jnp.float32)


def model_weight(owns, others, cols):
    sides = [jnp.concatenate([ref[:, cols] for ref in refs], axis=1) for refs in (owns, others)]
    return jnp.concatenate(sides, axis=0)


def stacked_up(values):
    return jnp.concatenate(values, axis=0)


def edge_masks(core, rows):
    key = lax.broadcasted_iota(jnp.int32, (rows, 2 * rows), 0)
    query = lax.broadcasted_iota(jnp.int32, (rows, 2 * rows), 1)
    mine = query < rows
    place = jnp.where(mine, query + core * rows, query - rows + (1 - core) * rows)
    return (key + core * rows <= place, key + (1 - core) * rows <= place)


def both_sides(value, half, start, stop, axis=0):
    if axis == 0:
        return jnp.concatenate([value[start:stop], value[half + start : half + stop]], axis=0)
    return jnp.concatenate([value[:, start:stop], value[:, half + start : half + stop]], axis=1)


def hidden_scores(scores, masks, tile, step):
    seen = step * tile
    pieces = []
    for side in range(2):
        base = side * (seen + tile)
        if seen:
            pieces.append(scores[base : base + seen])
        pieces.append(jnp.where(masks[side], scores[base + seen : base + seen + tile], -1e30))
    return jnp.concatenate(pieces, axis=0)


def one_head(rows, head):
    lane = lax.broadcasted_iota(jnp.int32, rows.shape, 1)
    return jnp.where(lane // 64 == head, rows, jnp.zeros_like(rows))


def pick_piece(weight, owns, others, cols):
    for j, (own, other) in enumerate(zip(owns, others)):

        @pl.when(pl.program_id(0) == j)
        def _():
            size = own.shape[0]
            weight[:size] = own[:, cols]
            weight[size:] = other[:, cols]


def attend_kernel(pieces, core_ref, cos_ref, sin_ref, own_rows, other_rows, *refs):
    owns, others = refs[:pieces], refs[pieces : 2 * pieces]
    q_ref, k_ref, v_ref, lse_ref, mix_ref, weight = refs[2 * pieces :]
    half = own_rows.shape[0]
    tile = TILE
    pick_piece(weight, owns, others, QKV)
    proj = dot_nn(stacked_up([own_rows[...], other_rows[...]]), weight[...])
    cos_rows, sin_rows = cos_ref[...], sin_ref[...]
    q = (rotated(proj[:, :128], cos_rows, sin_rows) * HEAD_DIM ** (-0.5)).astype(jnp.bfloat16)
    k = rotated(proj[:, 128:256], cos_rows, sin_rows).astype(jnp.bfloat16)
    v32 = proj[:, 256:]
    q_ref[0] = q
    k_ref[0] = k
    v_ref[0] = v32.astype(jnp.bfloat16)
    v_flip = v32.T.astype(jnp.bfloat16)
    masks = edge_masks(core_ref[0], tile)

    def scored(step, head):
        stop = (step + 1) * tile
        q_head = one_head(both_sides(q, half, step * tile, stop), head)
        return hidden_scores(dot_nt(both_sides(k, half, 0, stop), q_head), masks, tile, step)

    units = [(step, head) for step in range(half // tile) for head in range(2)]
    ahead = scored(*units[0])
    outs = []
    for spot, (step, head) in enumerate(units):
        scores = ahead
        if spot + 1 < len(units):
            ahead = scored(*units[spot + 1])
        stop = (step + 1) * tile
        top = jnp.max(scores, axis=0, keepdims=True)
        expos = jnp.exp(scores - top)
        total = jnp.sum(expos, axis=0, keepdims=True)
        lse = top + jnp.log(total)
        lse_ref[0, head : head + 1, step * tile : stop] = lse[:, :tile]
        lse_ref[0, head : head + 1, half + step * tile : half + stop] = lse[:, tile:]
        v_cols = both_sides(v_flip, half, 0, stop, axis=1)
        out = dot_nn(v_cols[64 * head : 64 * head + 64], expos.astype(jnp.bfloat16))
        outs.append(out * (1.0 / total))
        if head == 1:
            mixed = jnp.concatenate(outs, axis=0).T.astype(jnp.bfloat16)
            outs = []
            mix_ref[step * tile : stop, :] = mixed[:tile]
            mix_ref[half + step * tile : half + stop, :] = mixed[tile:]


def attend_back_kernel(pieces, core_ref, cos_ref, sin_ref, own_rows, other_rows, *refs):
    owns, others = refs[:pieces], refs[pieces : 2 * pieces]
    q_ref, k_ref, v_ref, lse_ref, out_ref, weight, dq, dk, dv = refs[2 * pieces :]
    half = own_rows.shape[0]
    tile = TILE
    pick_piece(weight, owns, others, OUT)
    rows = stacked_up([own_rows[...], other_rows[...]])
    d_mixed = dot_nn(rows, weight[...]).astype(jnp.bfloat16)
    q, k, v = q_ref[0], k_ref[0], v_ref[0]
    k_flip = k.astype(jnp.float32).T.astype(jnp.bfloat16)
    masks = edge_masks(core_ref[0], tile)
    steps = half // tile

    def scored(step, head):
        stop = (step + 1) * tile
        q_head = one_head(both_sides(q, half, step * tile, stop), head)
        g_head = one_head(both_sides(d_mixed, half, step * tile, stop), head)
        scores = hidden_scores(dot_nt(both_sides(k, half, 0, stop), q_head), masks, tile, step)
        return q_head, g_head, scores, dot_nt(both_sides(v, half, 0, stop), g_head)

    units = [(step, head) for step in reversed(range(steps)) for head in range(2)]
    ahead = scored(*units[0])
    dq_flips = []
    dk_sum = dv_sum = None
    for spot, (step, head) in enumerate(units):
        q_head, g_head, scores, d_probs = ahead
        if spot + 1 < len(units):
            ahead = scored(*units[spot + 1])
        stop = (step + 1) * tile
        lse = both_sides(lse_ref[0], half, step * tile, stop, axis=1)
        probs = jnp.exp(scores - lse[head : head + 1])
        dots = jnp.sum(probs * d_probs, axis=0, keepdims=True)
        d_scores = (probs * (d_probs - dots)).astype(jnp.bfloat16)
        dv_part = dot_nn(probs.astype(jnp.bfloat16), g_head)
        dk_part = dot_nn(d_scores, q_head)
        k_cols = both_sides(k_flip, half, 0, stop, axis=1)
        dq_flips.append(dot_nn(k_cols[64 * head : 64 * head + 64], d_scores))
        if head == 0:
            dv_sum, dk_sum = dv_part, dk_part
            continue
        dv_sum, dk_sum = dv_sum + dv_part, dk_sum + dk_part
        dq_rows = jnp.concatenate(dq_flips, axis=0).T * HEAD_DIM ** (-0.5)
        dq_flips = []
        dq[step * tile : stop] = dq_rows[:tile]
        dq[half + step * tile : half + stop] = dq_rows[tile:]
        for base, part in ((0, slice(0, stop)), (half, slice(stop, 2 * stop))):
            if step == steps - 1:
                dk[base : base + stop] = dk_sum[part]
                dv[base : base + stop] = dv_sum[part]
            else:
                dk[base : base + stop] += dk_sum[part]
                dv[base : base + stop] += dv_sum[part]
    cos_rows, sin_rows = cos_ref[...], -sin_ref[...]
    out_ref[:, :128] = rotated(dq[...], cos_rows, sin_rows).astype(jnp.bfloat16)
    out_ref[:, 128:256] = rotated(dk[...], cos_rows, sin_rows).astype(jnp.bfloat16)
    out_ref[:, 256:] = dv[...].astype(jnp.bfloat16)


def split_rows(total, own_ref, other_ref):
    half = own_ref.shape[0]
    own_ref[...] = total[:half]
    other_ref[...] = total[half:].astype(jnp.bfloat16)


def to_model_kernel(lefts, pieces, cols, *refs):
    left, refs = jnp.concatenate([ref[...] for ref in refs[:lefts]], axis=1), refs[lefts:]
    weight = model_weight(refs[:pieces], refs[pieces : 2 * pieces], cols)
    split_rows(dot_nt(left, weight), *refs[2 * pieces :])


def mlp_down_kernel(pieces, left_ref, *refs):
    sides = [stacked_up([ref[...] for ref in side]) for side in (refs[:pieces], refs[pieces:-2])]
    split_rows(dot_nn(left_ref[...], jnp.concatenate(sides, axis=1)), *refs[-2:])


def gelu_both(up_act):
    root = math.sqrt(2.0 / math.pi)
    square = up_act * up_act
    rise = 0.5 + 0.5 * jnp.tanh(up_act * (root + root * 0.044715 * square))
    value = up_act * rise
    slope = rise + value * (1.0 - rise) * (2.0 * root + 6.0 * root * 0.044715 * square)
    return value, slope


def mlp_up_kernel(pieces, own_rows, other_rows, *refs):
    owns, others = refs[:pieces], refs[pieces : 2 * pieces]
    gelu_ref, slope_ref = refs[2 * pieces :]
    half = own_rows.shape[0]
    size = owns[0].shape[1]
    step = half // 2
    units = [(j, i) for j in range(pieces) for i in range(4)]

    def product(j, i):
        rows = (own_rows, other_rows)[i // 2][i % 2 * step : (i % 2 + 1) * step]
        return dot_nn(rows, stacked_up([owns[j][...], others[j][...]]))

    ahead = product(*units[0])
    for spot, (j, i) in enumerate(units):
        up_act = ahead
        if spot + 1 < len(units):
            ahead = product(*units[spot + 1])
        value, slope = gelu_both(up_act)
        gelu_ref[i * step : (i + 1) * step, j * size : (j + 1) * size] = value.astype(jnp.bfloat16)
        slope_ref[i * step : (i + 1) * step, j * size : (j + 1) * size] = slope.astype(
            jnp.bfloat16
        )


def mlp_up_back_kernel(pieces, own_rows, other_rows, slope_ref, *refs):
    owns, others = refs[:pieces], refs[pieces : 2 * pieces]
    out_ref, weight, slope, sems = refs[2 * pieces :]
    half = own_rows.shape[1] // 2
    size = owns[0].shape[0]
    order = list(reversed(range(pieces)))
    copies = []
    for j in order:
        sources = (owns[j], others[j], slope_ref.at[:, pl.ds(j * size, size)])
        targets = (
            weight.at[j, :, pl.ds(0, half)],
            weight.at[j, :, pl.ds(half, half)],
            slope.at[:, pl.ds(j * size, size)],
        )
        copies.append(
            [
                pltpu.make_async_copy(source, target, sems.at[j, i])
                for i, (source, target) in enumerate(zip(sources, targets))
            ]
        )
        for copy in copies[-1]:
            copy.start()
    rows = stacked_up([own_rows[...], other_rows[...]])
    for j, arriving in zip(order, copies):
        cols = slice(j * size, (j + 1) * size)
        for copy in arriving:
            copy.wait()
        d_gelu = dot_nt(rows, weight[j])
        out_ref[:, cols] = (d_gelu * slope[:, cols].astype(jnp.float32)).astype(jnp.bfloat16)


def inverse_size(rows):
    return lax.rsqrt(jnp.mean(rows * rows, axis=-1, keepdims=True) + NORM_EPSILON)


def norm_back(rows, gain, grad):
    scale = inverse_size(rows)
    weighted = grad * gain
    inner = jnp.mean(rows * weighted, axis=-1, keepdims=True)
    return scale * weighted - rows * (scale * scale * scale * inner), rows * scale * grad


def folded(rows):
    return jnp.sum(rows.reshape(rows.shape[0] // 8, 8, rows.shape[1]), axis=0)


def wide(ref, spot):
    return ref[spot, :].astype(jnp.float32)


def by_chunks(count, body, sums=0, width=0):
    def one(i, carry):
        more = body(pl.ds(pl.multiple_of(i * CHUNK, CHUNK), CHUNK))
        return tuple(old + folded(new) for old, new in zip(carry, more))

    start = tuple(jnp.zeros((8, width), jnp.float32) for _ in range(sums))
    totals = lax.fori_loop(0, count // CHUNK, one, start)
    return [jnp.sum(total, axis=0, keepdims=True) for total in totals]


def norm_in_kernel(gain_ref, rows_ref, out_ref):
    def body(spot):
        rows = wide(rows_ref, spot)
        out_ref[spot, :] = (rows * inverse_size(rows) * gain_ref[0:1]).astype(jnp.bfloat16)
        return ()

    by_chunks(rows_ref.shape[0], body)


def after_attention_kernel(
    gain_ref, rows_ref, own_ref, other_ref, branch_ref, hidden_ref, out_ref
):
    def body(spot):
        branch = own_ref[spot, :] + wide(other_ref, spot)
        hidden = wide(rows_ref, spot) + branch * inverse_size(branch) * gain_ref[1:2]
        branch_ref[spot, :] = branch
        hidden_ref[spot, :] = hidden
        out_ref[spot, :] = (hidden * inverse_size(hidden) * gain_ref[2:3]).astype(jnp.bfloat16)
        return ()

    by_chunks(rows_ref.shape[0], body)


def after_mlp_kernel(gain_ref, hidden_ref, own_ref, other_ref, branch_ref, out_ref):
    def body(spot):
        branch = own_ref[spot, :] + wide(other_ref, spot)
        branch_ref[spot, :] = branch
        result = hidden_ref[spot, :] + branch * inverse_size(branch) * gain_ref[3:4]
        out_ref[spot, :] = result.astype(jnp.bfloat16)
        return ()

    by_chunks(hidden_ref.shape[0], body)


def into_mlp_back_kernel(gain_ref, grad_ref, branch_ref, out_ref, sum_ref):
    def body(spot):
        d_rows, d_gain = norm_back(branch_ref[spot, :], gain_ref[3:4], wide(grad_ref, spot))
        out_ref[spot, :] = d_rows.astype(jnp.bfloat16)
        return (d_gain,)

    (sum_ref[...],) = by_chunks(grad_ref.shape[0], body, 1, grad_ref.shape[1])


def into_attention_back_kernel(
    gain_ref, grad_ref, own_ref, other_ref, hidden_ref, branch_ref, d_hidden_ref, out_ref, *sums
):
    def body(spot):
        d_rows = own_ref[spot, :] + wide(other_ref, spot)
        d_rows, d_gain = norm_back(hidden_ref[spot, :], gain_ref[2:3], d_rows)
        d_hidden = wide(grad_ref, spot) + d_rows
        d_hidden_ref[spot, :] = d_hidden
        d_rows, d_first = norm_back(branch_ref[spot, :], gain_ref[1:2], d_hidden)
        out_ref[spot, :] = d_rows.astype(jnp.bfloat16)
        return (d_first, d_gain)

    totals = by_chunks(grad_ref.shape[0], body, 2, grad_ref.shape[1])
    sums[0][...], sums[1][...] = totals


def out_of_layer_kernel(gain_ref, rows_ref, own_ref, other_ref, d_hidden_ref, out_ref, sum_ref):
    def body(spot):
        d_rows = own_ref[spot, :] + wide(other_ref, spot)
        d_rows, d_gain = norm_back(wide(rows_ref, spot), gain_ref[0:1], d_rows)
        out_ref[spot, :] = (d_hidden_ref[spot, :] + d_rows).astype(jnp.bfloat16)
        return (d_gain,)

    (sum_ref[...],) = by_chunks(rows_ref.shape[0], body, 1, rows_ref.shape[1])


def work(flops, arrays):
    size = sum(math.prod(array.shape) * jnp.dtype(array.dtype).itemsize for array in arrays)
    return pl.CostEstimate(flops=flops, bytes_accessed=size, transcendentals=0)


def far(array):
    return pltpu.with_memory_space_constraint(array, pltpu.HBM)


def without(kernel, first, count):
    return lambda *refs: kernel(*refs[:first], *refs[first + count :])


def on_chip(kernel, name, outs, *operands, limit=ROWS_VMEM, flops=0, waits=()):
    shapes = [jax.ShapeDtypeStruct(shape, dtype) for shape, dtype in outs]
    space = pl.BlockSpec(memory_space=pltpu.VMEM)
    return pl.pallas_call(
        without(kernel, len(operands), len(waits)),
        in_specs=[space] * len(operands) + [pl.BlockSpec(memory_space=pl.ANY)] * len(waits),
        out_specs=[space] * len(outs),
        out_shape=shapes,
        compiler_params=pltpu.CompilerParams(vmem_limit_bytes=limit),
        cost_estimate=work(flops, (*operands, *shapes)),
        name=name,
    )(*operands, *map(far, waits))


def whole_block(array):
    return pl.BlockSpec(array.shape, lambda j: (0,) * array.ndim)


def by_pairs(kernel, name, core, operands, pieces, blocks, outs, scratch, flops, waits):
    shapes = [jax.ShapeDtypeStruct(shape, dtype) for shape, dtype, _ in outs]
    taken = 1 + len(operands) + 2 * len(pieces[0]) + len(blocks)
    return pl.pallas_call(
        without(functools.partial(kernel, len(pieces[0])), taken, len(waits)),
        grid=(len(pieces[0]),),
        in_specs=[pl.BlockSpec(memory_space=pltpu.SMEM)]
        + [whole_block(array) for array in (*operands, *pieces[0], *pieces[1])]
        + [spec for _, spec in blocks]
        + [pl.BlockSpec(memory_space=pl.ANY)] * len(waits),
        out_specs=[spec for _, _, spec in outs],
        out_shape=shapes,
        scratch_shapes=scratch,
        compiler_params=pltpu.CompilerParams(vmem_limit_bytes=KERNEL_VMEM),
        cost_estimate=work(flops, (*operands, *pieces[0], *pieces[1], *shapes)),
        name=name,
    )(core, *operands, *pieces[0], *pieces[1], *[array for array, _ in blocks], *map(far, waits))


def mlp_up_back(rows, slope, pieces, waits):
    length, units = slope.shape
    unit, half = pieces[0][0].shape
    count = len(pieces[0])
    every, space = pl.BlockSpec(memory_space=pl.ANY), pl.BlockSpec(memory_space=pltpu.VMEM)
    return pl.pallas_call(
        without(functools.partial(mlp_up_back_kernel, count), 3 + 2 * count, len(waits)),
        in_specs=[space] * 2 + [every] * (1 + 2 * count + len(waits)),
        out_specs=space,
        out_shape=jax.ShapeDtypeStruct((length, units), jnp.bfloat16),
        scratch_shapes=[
            pltpu.VMEM((count, unit, 2 * half), jnp.bfloat16),
            pltpu.VMEM((length, units), jnp.bfloat16),
            pltpu.SemaphoreType.DMA((count, 3)),
        ],
        compiler_params=pltpu.CompilerParams(vmem_limit_bytes=KERNEL_VMEM),
        name="mlp_up_back",
    )(*rows, *map(far, (slope, *pieces[0], *pieces[1], *waits)))


def attend(core, tables, rows, pieces, waits):
    half, features = rows[0].shape
    length, count = 2 * half, len(pieces[0])
    lanes = ((count, length, 128), jnp.bfloat16, pl.BlockSpec((1, length, 128), lambda j: (j, 0, 0)))
    lse = ((count, 2, length), jnp.float32, pl.BlockSpec((1, 2, length), lambda j: (j, 0, 0)))
    mixed = ((length, count * 128), jnp.bfloat16, pl.BlockSpec((length, 128), lambda j: (0, j)))
    return by_pairs(
        attend_kernel,
        "attend",
        core,
        (*tables, *rows),
        pieces,
        (),
        (lanes, lanes, lanes, lse, mixed),
        [pltpu.VMEM((features, 384), jnp.bfloat16)],
        count * length * (2 * features * 384 + 2 * PAIR_WORK * length),
        waits,
    )


def attend_back(core, tables, rows, pieces, base, waits, q, k, v, lse):
    half, features = rows[0].shape
    length, count = 2 * half, len(pieces[0])
    lanes = pl.BlockSpec((1, length, 128), lambda j: (base + j, 0, 0))
    lse_spec = pl.BlockSpec((1, 2, length), lambda j: (base + j, 0, 0))
    out = ((length, count * 384), jnp.bfloat16, pl.BlockSpec((length, 384), lambda j: (0, j)))
    return by_pairs(
        attend_back_kernel,
        "attend_back",
        core,
        (*tables, *rows),
        pieces,
        ((q, lanes), (k, lanes), (v, lanes), (lse, lse_spec)),
        (out,),
        [pltpu.VMEM((features, 128), jnp.bfloat16)] + [pltpu.VMEM((length, 128), jnp.float32)] * 3,
        count * length * (2 * features * 128 + 5 * PAIR_WORK * length),
        waits,
    )[0]


def exchanged(parts):
    return parts[0], flip_pairs(parts[1], 1)


def model_rows(kernel, name, lefts, pieces, waits=()):
    length, width = lefts[0].shape[0], 2 * MODEL_HALF
    outs = (((length // 2, width), jnp.float32), ((length // 2, width), jnp.bfloat16))
    hidden = sum(left.shape[1] for left in lefts)
    more = {"limit": KERNEL_VMEM, "flops": 2 * length * width * hidden, "waits": waits}
    return exchanged(on_chip(kernel, name, outs, *lefts, *pieces[0], *pieces[1], **more))


def flip_pairs(block, distance):
    size = lax.axis_size("dp")
    return lax.ppermute(block, "dp", [(i, i ^ distance) for i in range(size)])


def passed_on(block, step):
    size = lax.axis_size("tensor")
    return lax.ppermute(block, "tensor", [(i, (i + step) % size) for i in range(size)])


def dot_tn(left, right):
    return lax.dot_general(
        left, right, (((0,), (0,)), ((), ())), preferred_element_type=jnp.float32
    )


def fetch(first_ref, zeros, ones, buffers, sems):
    for section, sources in enumerate((zeros, ones)):

        @pl.when(first_ref[0] == section)
        def _():
            for i, (source, buffer) in enumerate(zip(sources, buffers)):
                pltpu.make_async_copy(source, buffer, sems.at[i]).start()

    def arrived(*places):
        for i in places:
            pltpu.make_async_copy(zeros[i], buffers[i], sems.at[i]).wait()

    return arrived


def mlp_grads_kernel(base, section_ref, *refs):
    (own_one, other_one, own_two, other_two), (rows, d_up, gelu, d_down, sems) = refs[12:16], refs[16:]
    half, size = own_one.shape[0] // 2, own_one.shape[1]
    cols = pl.ds(base * size, 2 * size)

    def parts(own_rows, other_rows, d_up_ref, gelu_ref, own_grad, other_grad):
        whole = (d_up_ref.at[:, cols], gelu_ref.at[:, cols])
        return (own_rows, other_rows, *whole, own_grad, other_grad)

    count = refs[0].shape[0]
    buffers = (
        rows.at[pl.ds(0, count)],
        rows.at[pl.ds(count, count)],
        d_up,
        gelu,
        d_down.at[pl.ds(0, count)],
        d_down.at[pl.ds(count, count)],
    )
    arrived = fetch(section_ref, parts(*refs[:6]), parts(*refs[6:12]), buffers, sems)
    for j, own, other in ((1, own_two, other_two), (0, own_one, other_one)):
        cols = slice(j * size, (j + 1) * size)
        if j == 1:
            arrived(0, 1, 2)
        up = dot_tn(rows[...], d_up[:, cols])
        own[:half] = up[:half]
        other[:half] = up[half:].astype(jnp.bfloat16)
        if j == 1:
            arrived(3, 4, 5)
        down = dot_tn(gelu[:, cols], d_down[...])
        own[half:] = down[:, :half]
        other[half:] = down[:, half:].astype(jnp.bfloat16)


def attn_grads_kernel(base, section_ref, *refs):
    (own_one, other_one, own_two, other_two), (rows, d_qkv, mixed, d_attn, sems) = refs[12:16], refs[16:]
    half, size = own_one.shape[0], d_qkv.shape[1] // 2
    count = refs[0].shape[0]
    cols = pl.ds(base * 128, 256)

    def parts(own_rows, other_rows, d_qkv_ref, mixed_ref, own_grad, other_grad):
        return (own_rows, other_rows, d_qkv_ref, mixed_ref.at[:, cols], own_grad, other_grad)

    buffers = (
        rows.at[pl.ds(0, count)],
        rows.at[pl.ds(count, count)],
        d_qkv,
        mixed,
        d_attn.at[pl.ds(0, count)],
        d_attn.at[pl.ds(count, count)],
    )
    arrived = fetch(section_ref, parts(*refs[:6]), parts(*refs[6:12]), buffers, sems)
    for j, own, other in ((1, own_two, other_two), (0, own_one, other_one)):
        if j == 1:
            arrived(0, 1, 2)
        qkv = dot_tn(rows[...], d_qkv[:, j * size : (j + 1) * size])
        if j == 1:
            arrived(3, 4, 5)
        out = dot_tn(d_attn[...], mixed[:, j * 128 : (j + 1) * 128])
        own[:, :size] = qkv[:half]
        own[:, size:] = out[:half]
        other[:, :size] = qkv[half:].astype(jnp.bfloat16)
        other[:, size:] = out[half:].astype(jnp.bfloat16)


def weight_grads(kernel, name, base, section, zeros, ones, shape, columns, waits=()):
    length = 2 * zeros[0].shape[0]
    width = zeros[0].shape[1]
    every = pl.BlockSpec(memory_space=pl.ANY)
    space = pl.BlockSpec(memory_space=pltpu.VMEM)
    arrays = (*zeros, *ones)
    first, second, third, fourth = pl.pallas_call(
        without(functools.partial(kernel, base), 1 + len(arrays), len(waits)),
        in_specs=[pl.BlockSpec(memory_space=pltpu.SMEM)] + [every] * (len(arrays) + len(waits)),
        out_specs=[space] * 4,
        out_shape=[
            jax.ShapeDtypeStruct(shape, jnp.float32),
            jax.ShapeDtypeStruct(shape, jnp.bfloat16),
        ]
        * 2,
        scratch_shapes=[
            pltpu.VMEM((length, width), jnp.bfloat16),
            pltpu.VMEM((length, columns[0]), jnp.bfloat16),
            pltpu.VMEM((length, columns[1]), jnp.bfloat16),
            pltpu.VMEM((length, width), jnp.bfloat16),
            pltpu.SemaphoreType.DMA((6,)),
        ],
        compiler_params=pltpu.CompilerParams(vmem_limit_bytes=KERNEL_VMEM),
        name=name,
    )(section, *map(far, (*arrays, *waits)))
    return [(first, flip_pairs(second, 2)), (third, flip_pairs(fourth, 2))]


def moved_kernel(own_ref, other_ref, *refs):
    out_ref = refs[-1]

    def body(i, carry):
        spot = pl.ds(pl.multiple_of(i * CHUNK, CHUNK), CHUNK)
        total = own_ref[spot, :]
        for ref in (other_ref, *refs[:-1]):
            total = total + wide(ref, spot)
        out_ref[spot, :] = total.astype(jnp.bfloat16)
        return carry

    lax.fori_loop(0, own_ref.shape[0] // CHUNK, body, 0)


def gate_kernel(piece_ref, out_ref):
    out_ref[...] = piece_ref[...]


def mlp_sum_kernel(core_ref, own_ref, other_ref, moved_ref, up_keep, down_keep, up_send, down_send):
    half = own_ref.shape[0] // 2
    size = up_keep.shape[0]

    def total(rows, cols):
        more = other_ref[rows, cols].astype(jnp.float32) + moved_ref[rows, cols].astype(jnp.float32)
        return own_ref[rows, cols] + more

    for core in range(2):

        @pl.when(core_ref[0] == core)
        def _():
            for place, up, down in ((core, up_keep, down_keep), (1 - core, up_send, down_send)):
                spot = slice(place * size, (place + 1) * size)
                up[...] = total(spot, slice(None))
                down[...] = total(slice(half, None), spot)


def mlp_join_kernel(core_ref, up_keep, down_keep, up_sent, down_sent, up_out, down_out):
    size = up_keep.shape[1]
    for core in range(2):

        @pl.when(core_ref[0] == core)
        def _():
            places = ((core, up_keep, down_keep), (1 - core, up_sent, down_sent))
            for place, up, down in places:
                spot = slice(place * size, (place + 1) * size)
                up_out[:, spot] = up[...]
                down_out[spot] = down[...]


def pick_kernel(core_ref, rows_ref, keep_ref, send_ref):
    count = keep_ref.shape[0]
    keep_ref[...] = rows_ref[pl.ds(core_ref[0] * count, count)]
    send_ref[...] = rows_ref[pl.ds((1 - core_ref[0]) * count, count)]


def turned_kernel(place_ref, keep_ref, sent_ref, *outs):
    count = keep_ref.shape[0]
    for step, out in enumerate(outs):
        goal = lax.rem(place_ref[1] + step, len(outs))
        for k in range(len(outs)):
            for here in range(2):

                @pl.when(jnp.logical_and(goal == k, (place_ref[0] == k // count) == (here == 0)))
                def _():
                    out[...] = (keep_ref, sent_ref)[here][k % count]


def placed_kernel(place_ref, *refs):
    blocks, out_ref = refs[:-1], refs[-1]
    for step, block in enumerate(blocks):
        source = lax.rem(place_ref[1] + len(blocks) - step, len(blocks))
        out_ref[pl.ds(source, 1)] = block[...][None]


def in_order_kernel(core_ref, keep_ref, sent_ref, out_ref):
    out_ref[:, pl.ds(core_ref[0], 1)] = keep_ref[...][:, None]
    out_ref[:, pl.ds(1 - core_ref[0], 1)] = sent_ref[...][:, None]


def with_core(kernel, name, core, outs, *operands, waits=()):
    space = pl.BlockSpec(memory_space=pltpu.VMEM)
    return pl.pallas_call(
        without(kernel, 1 + len(operands), len(waits)),
        in_specs=[pl.BlockSpec(memory_space=pltpu.SMEM)]
        + [space] * len(operands)
        + [pl.BlockSpec(memory_space=pl.ANY)] * len(waits),
        out_specs=[space] * len(outs),
        out_shape=[jax.ShapeDtypeStruct(shape, dtype) for shape, dtype in outs],
        compiler_params=pltpu.CompilerParams(vmem_limit_bytes=ROWS_VMEM),
        name=name,
    )(core, *operands, *map(far, waits))


def last_sum_kernel(core_ref, own_ref, other_ref, moved_ref, keep_ref, send_ref):
    rows = keep_ref.shape[0]

    def total(block):
        spot = pl.ds(pl.multiple_of(block * rows, rows), rows)
        return own_ref[spot, :] + wide(other_ref, spot) + wide(moved_ref, spot)

    keep_ref[...] = total(core_ref[0])
    send_ref[...] = total(1 - core_ref[0])


def joined_kernel(spots, core_ref, keep_ref, sent_ref, column_ref, row_ref):
    size = row_ref.shape[0] // 2
    for core in range(2):

        @pl.when(core_ref[0] == core)
        def _():
            for place, source in ((core, keep_ref), (1 - core, sent_ref)):
                for start, stop, to in spots:
                    step = stop - start
                    column_ref[:, to + place * step : to + (place + 1) * step] = source[:, start:stop]
                row_ref[place * size : (place + 1) * size] = source[:, spots[-1][1] :].T


def per_chip(
    inputs,
    out_cotangent,
    group_ids,
    group_weights,
    gains,
    qkv_weight,
    out_weight,
    up_weight,
    down_weight,
):
    micro, row_count, width = inputs.shape
    tensor = lax.axis_size("tensor")
    part = row_count // 2
    wide_half = width // 2
    length = tensor * row_count
    half = length // 2
    first = lax.axis_index("section") == 0
    place = lax.axis_index("dp")
    core = place % 2
    upper = place // 2 % 2
    core_zero = core == 0
    low_half = upper == 0

    def ordered(mine, other):
        return jnp.where(core_zero, mine, other), jnp.where(core_zero, other, mine)

    def own_first(values):
        return jnp.where(low_half, values, jnp.roll(values, wide_half, axis=-1))

    def both_rows(own):
        return own, flip_pairs(own, 1)

    def turned(block, waits=()):
        split = block.reshape(micro, 2, part, width)
        mine = lax.dynamic_index_in_dim(split, core, 1, keepdims=False)
        other = lax.dynamic_index_in_dim(split, 1 - core, 1, keepdims=False)
        outs = (((part, width), jnp.bfloat16),) * tensor
        return with_core(
            turned_kernel, "turned", place_word, outs, mine, flip_pairs(other, 1), waits=waits
        )

    def along(block, step, section=None):
        pairs = [(i, (i + step) % tensor) for i in range(tensor)]
        if section is None:
            return lax.ppermute(block, "tensor", pairs)
        pairs = [(section * tensor + i, section * tensor + k) for i, k in pairs]
        return lax.ppermute(block, ("section", "tensor"), pairs)

    def on_chips(blocks, section=None):
        moved = [along(block, step, section) if step else block for step, block in enumerate(blocks)]
        outs = (((tensor, part, width), jnp.bfloat16),)
        (rows,) = with_core(placed_kernel, "placed", place_word, outs, *moved)
        return rows.reshape(half, width)

    def from_chip(spread_out, waits=()):
        piece = ((micro, part, width), jnp.bfloat16)
        keep, send = with_core(
            pick_kernel, "pick", core_word, (piece, piece), spread_out, waits=waits
        )
        outs = (((micro, 2, part, width), jnp.bfloat16),)
        (rows,) = with_core(
            in_order_kernel, "in_order", core_word, outs, keep, flip_pairs(send, 1)
        )
        return rows.reshape(micro, row_count, width)

    def columns(local):
        size = local.shape[-1] // 2
        mid = (0,) * (local.ndim - 2)
        piece = lax.dynamic_slice(
            local,
            (wide_half * upper, *mid, size * core),
            (wide_half, *local.shape[1:-1], size),
        )
        return piece.reshape(wide_half, -1)

    def rows(local):
        size = local.shape[0] // 2
        return lax.dynamic_slice(local, (size * core, wide_half * upper), (size, wide_half))

    core_word = core.astype(jnp.int32).reshape(1)
    place_word = jnp.stack([core, lax.axis_index("tensor")]).astype(jnp.int32)
    attn_piece = jnp.concatenate([columns(qkv_weight[0]), rows(out_weight[0]).T], axis=1)

    def spread(piece):
        pieces = [piece]
        for _ in range(tensor - 1):
            pieces.append(passed_on(pieces[-1], 1))
        return pieces

    attn_own = spread(attn_piece)
    attn_other = [flip_pairs(piece, 2) for piece in attn_own]
    up_piece, down_piece = columns(up_weight[0]), rows(down_weight[0])
    up_other, down_other = [flip_pairs(up_piece, 2)], [flip_pairs(down_piece, 2)]
    gates = []
    for piece in (up_piece, down_piece):
        outs = ((piece.shape, piece.dtype),)
        gates += on_chip(gate_kernel, "gate", outs, piece, waits=(attn_own[2], attn_other[0]))
    up_piece, down_piece = gates
    up_own, down_own = spread(up_piece), spread(down_piece)
    up_other += [flip_pairs(piece, 2) for piece in up_own[1:]]
    down_other += [flip_pairs(piece, 2) for piece in down_own[1:]]
    w_attn, w_up, w_down = (attn_own, attn_other), (up_own, up_other), (down_own, down_other)
    unit = up_piece.shape[1]
    units = tensor * unit

    start = shifted(on_chips(turned(own_first(inputs), (attn_piece,)), 1), "section", -1)
    group_count = group_weights.shape[0]
    matches = group_ids[..., None] == jnp.arange(group_count, dtype=jnp.int32)
    row_scale = jnp.sum(jnp.where(matches, group_weights, 0.0), axis=-1)
    weighted = (out_cotangent.astype(jnp.float32) * row_scale[..., None]).astype(jnp.bfloat16)
    gain = own_first(gains[0])

    turns = jnp.arange(half, dtype=jnp.int32)
    turns = turns // part * row_count + turns % part
    positions = jnp.concatenate([turns + core * part, turns + (1 - core) * part])
    freqs = 10000.0 ** (-2.0 * jnp.arange(HEAD_DIM // 2, dtype=jnp.float32) / HEAD_DIM)
    angles = positions.astype(jnp.float32)[:, None] * freqs[None, :]
    cos_part, sin_part = jnp.cos(angles), jnp.sin(angles)
    tables = (
        jnp.concatenate([cos_part] * 4, axis=1),
        jnp.concatenate([-sin_part, sin_part] * 2, axis=1),
    )
    row32, row16 = ((half, width), jnp.float32), ((half, width), jnp.bfloat16)
    unit16 = ((length, units), jnp.bfloat16)
    sum32 = ((1, width), jnp.float32)
    mlp_cost = {"limit": KERNEL_VMEM, "flops": 2 * length * width * units}
    every = slice(None)

    def model_kernel(cols, lefts=1):
        return functools.partial(to_model_kernel, lefts, tensor, cols)

    down_kernel = functools.partial(mlp_down_kernel, tensor)

    def forward(layer_input, waits):
        attn_in = both_rows(
            on_chip(norm_in_kernel, "norm_in", (row16,), gain, layer_input, waits=waits[0])[0]
        )
        *heads, mixed = attend(core_word, tables, attn_in, w_attn, waits[1])
        parts = model_rows(model_kernel(OUT), "attn_out", [mixed], w_attn, waits[2])
        operands = (gain, layer_input, *parts)
        branch, hidden, mlp_in = on_chip(
            after_attention_kernel, "after_attn", (row32, row32, row16), *operands, waits=waits[3]
        )
        mlp_in = both_rows(mlp_in)
        kernel = functools.partial(mlp_up_kernel, tensor)
        operands = (*mlp_in, *w_up[0], *w_up[1])
        gelu_out, slope = on_chip(kernel, "mlp_up", (unit16, unit16), *operands, **mlp_cost)
        parts = model_rows(down_kernel, "mlp_down", [gelu_out], w_down)
        mlp_branch, result = on_chip(
            after_mlp_kernel, "after_mlp", (row32, row16), gain, hidden, *parts
        )
        saved = (layer_input, heads, branch, hidden, slope, mlp_branch)
        return result, saved, (attn_in, mixed, mlp_in, gelu_out)

    def backward(grad, saved, hook, late=()):
        layer_input, heads, branch, hidden, slope, mlp_branch = saved
        operands = (gain, grad, mlp_branch)
        d_down, sum_three = on_chip(
            into_mlp_back_kernel, "into_mlp_back", (row16, sum32), *operands
        )
        d_down = both_rows(d_down)
        d_up = mlp_up_back(d_down, slope, w_down, late)
        waits = hook(d_down, d_up)
        parts = model_rows(model_kernel(every), "mlp_back", [d_up], w_up, waits)
        waits = hook()
        operands = (gain, grad, *parts, hidden, branch)
        outs = (row32, row16, sum32, sum32)
        d_hidden, d_attn, sum_one, sum_two = on_chip(
            into_attention_back_kernel, "into_attn_back", outs, *operands, waits=waits
        )
        d_attn = both_rows(d_attn)
        waits = hook(d_attn)
        d_qkv = []
        for base in reversed(range(0, tensor, 2)):
            some = [side[base : base + 2] for side in w_attn]
            now = attend_back(core_word, tables, d_attn, some, base, waits, *heads)
            d_qkv.insert(0, now)
            waits = hook(now)
        parts = model_rows(model_kernel(QKV, 2), "attn_back", d_qkv, w_attn, waits)
        operands = (gain, layer_input, *parts, d_hidden)
        d_input, sum_zero = on_chip(
            out_of_layer_kernel, "out_of_layer", (row16, sum32), *operands, waits=hook()
        )
        sums = jnp.concatenate([sum_zero, sum_one, sum_two, sum_three])
        return d_input, (d_qkv, d_attn, d_up, d_down), sums

    low_zero, saved_zero, lefts_zero = forward(
        start,
        (
            (up_piece, up_other[0], down_other[0]),
            (up_own[1], down_own[1]),
            (up_own[2], down_own[2], up_other[1], down_other[1]),
            (up_own[3], down_own[3], up_other[2], down_other[2]),
        ),
    )
    goals = on_chips(turned(own_first(weighted), (low_zero,)))
    low_one, saved_one, lefts_one = forward(
        shifted(low_zero, "section", 1), ((goals,), (), (), ())
    )
    grad_one, rights_one, gain_one = backward(goals, saved_one, lambda *new: ())
    received = shifted(grad_one, "section", -1)

    lows = lax.optimization_barrier((low_zero, low_one, grad_one))[:2]
    lows = own_first(jnp.where(first, *lows)).reshape(tensor, part, width)
    lows = lax.all_to_all(lows, "tensor", 0, 0, tiled=True)

    section_word = lax.axis_index("section").astype(jnp.int32).reshape(1)

    def mlp_leaves(base):
        zeros = (*lefts_zero[2], d_up, lefts_zero[3], *d_down)
        ones = (*lefts_one[2], rights_one[2], lefts_one[3], *rights_one[3])
        mlp_sums[base : base + 2] = weight_grads(
            mlp_grads_kernel,
            "mlp_grads",
            base,
            section_word,
            zeros,
            ones,
            (wide_half + unit, unit),
            (2 * unit, 2 * unit),
        )

    def attn_leaves(base, d_qkv, waits):
        zeros = (*lefts_zero[0], d_qkv, lefts_zero[1], *d_attn)
        ones = (*lefts_one[0], rights_one[0][base // 2], lefts_one[1], *rights_one[1])
        attn_sums[base : base + 2] = weight_grads(
            attn_grads_kernel,
            "attn_grads",
            base,
            section_word,
            zeros,
            ones,
            (wide_half, 512),
            (768, 256),
            waits,
        )

    def moves_on(piece, *moved, waits=()):
        outs = ((piece[1].shape, jnp.bfloat16),)
        (total,) = on_chip(moved_kernel, "moved", outs, *piece, *moved, waits=waits)
        return total, passed_on(total, -1)

    mlp_sums, attn_sums = [None] * tensor, [None] * tensor
    mlp_moves, attn_moves = [None] * tensor, [None] * tensor
    hooks = iter(range(6))

    def hook(*new):
        nonlocal d_down, d_up, d_attn
        turn = next(hooks)
        if turn == 0:
            d_down, d_up = new
            mlp_leaves(2)
            return (mlp_sums[3][0],)
        if turn == 1:
            mlp_leaves(0)
            return (mlp_sums[1][0],)
        if turn == 2:
            (d_attn,) = new
            _, mlp_moves[3] = moves_on(mlp_sums[3], waits=d_attn[:1])
            return (mlp_sums[3][1],)
        if turn == 3:
            total, mlp_moves[2] = moves_on(mlp_sums[2], mlp_moves[3], waits=new)
            attn_leaves(2, new[0], (total,))
            return (mlp_sums[2][1], mlp_moves[3], attn_sums[3][0])
        if turn == 4:
            total, mlp_moves[1] = moves_on(mlp_sums[1], mlp_moves[2], waits=new)
            attn_leaves(0, new[0], (total,))
            return (attn_sums[1][0],)
        total, attn_moves[3] = moves_on(attn_sums[3])
        return (mlp_sums[0][1], total, mlp_moves[1])

    d_down = d_up = d_attn = None
    grad_zero, rights_zero, gain_zero = backward(received, saved_zero, hook, (lows,))
    gain_total = own_first(jnp.where(first, gain_zero, gain_one))
    count = tensor * lax.axis_size("dp")
    gain_parts = gain_total.reshape(4, count, width // count).swapaxes(0, 1)
    outputs = from_chip(lows, (grad_zero,))
    grads = own_first(jnp.where(first, grad_zero, grad_one)).reshape(tensor, part, width)
    grads = from_chip(lax.all_to_all(grads, "tensor", 0, 0, tiled=True))

    block32 = ((wide_half // 2, unit), jnp.float32)
    down32 = ((unit, wide_half // 2), jnp.float32)
    up_keep, down_keep, up_send, down_send = with_core(
        mlp_sum_kernel,
        "mlp_sum",
        core_word,
        (block32, down32, block32, down32),
        *mlp_sums[0],
        mlp_moves[1],
    )
    outs = (
        ((wide_half // 2, 2 * unit), jnp.float32),
        ((2 * unit, wide_half // 2), jnp.float32),
    )
    sent = flip_pairs(up_send, 1), flip_pairs(down_send, 1)
    up_grad, down_grad = with_core(
        mlp_join_kernel, "mlp_join", core_word, outs, up_keep, down_keep, *sent
    )
    waits = (outputs, attn_sums[1][1])
    total, attn_moves[2] = moves_on(attn_sums[2], attn_moves[3], waits=waits)
    outs = ((gain_parts.shape, gain_parts.dtype),)
    (gain_parts,) = on_chip(gate_kernel, "gate", outs, gain_parts, waits=(total,))
    gain_parts = lax.all_to_all(gain_parts, ("dp", "tensor"), 0, 0, tiled=True)
    gains_grad = jnp.sum(gain_parts, axis=0)
    waits = (up_grad, gains_grad, attn_sums[0][1])
    last, attn_moves[1] = moves_on(attn_sums[1], attn_moves[2], waits=waits)
    outs = (((wide_half // 2, 512), jnp.float32),) * 2
    keep, send = with_core(
        last_sum_kernel,
        "attn_sum",
        core_word,
        outs,
        *attn_sums[0],
        attn_moves[1],
        waits=(grads,),
    )
    spots = tuple((i * 128, (i + 1) * 128, i * 256) for i in range(3))
    outs = (((wide_half // 2, 768), jnp.float32), ((256, wide_half // 2), jnp.float32))
    kernel = functools.partial(joined_kernel, spots)
    qkv_grad, out_grad = with_core(
        kernel, "attn_join", core_word, outs, keep, flip_pairs(send, 1)
    )
    qkv_grad = qkv_grad.reshape(wide_half // 2, 3, -1)

    return (
        outputs[None],
        grads[None],
        gains_grad[None],
        qkv_grad[None],
        out_grad[None],
        up_grad[None],
        down_grad[None],
    )


def takes_chips(sizes):
    return sizes["section"] == 2 and sizes["dp"] == 4 and sizes["tensor"] == 4


def solution(mesh):
    placed = (
        P("dp", "tensor", None),
        P("dp", "tensor", None),
        P("dp", "tensor"),
        P(),
        P("section", None, None),
        P("section", None, None, "tensor"),
        P("section", "tensor", None),
        P("section", None, "tensor"),
        P("section", "tensor", None),
    )
    body = per_chip if takes_chips(dict(mesh.shape)) else per_device
    return jax.shard_map(
        body,
        mesh=mesh,
        in_specs=placed,
        out_specs=(
            P("section", "dp", "tensor", None),
            P("section", "dp", "tensor", None),
            P("section", None, ("dp", "tensor")),
            P("section", "dp", None, "tensor"),
            P("section", "tensor", "dp"),
            P("section", "dp", "tensor"),
            P("section", "tensor", "dp"),
        ),
        check_vma=False,
    )
```

```python
import functools
import math

import jax
import jax.numpy as jnp
from jax import lax
from jax.experimental import pallas as pl
from jax.experimental.pallas import tpu as pltpu
from jax.sharding import PartitionSpec as P

HEAD_DIM = 64


NORM_EPSILON = 1e-06
TILE = 128
PAIR_WORK = 1024
MODEL_HALF = 512
QKV = slice(0, 384)
OUT = slice(384, 512)
CHUNK = 32
KERNEL_VMEM = 20 << 20
ROWS_VMEM = 3 << 20


def shifted(block, axis, distance):
    devices = range(lax.axis_size(axis))
    route = [(i - distance, i) for i in devices if i - distance in devices]
    return lax.ppermute(block, axis, route)


def norm_rows(vector, weight_gain):
    return (
        vector
        * lax.rsqrt(jnp.mean(vector * vector, axis=-1, keepdims=True) + NORM_EPSILON)
        * weight_gain
    )


def rotary_tables(seq_len, head_width):
    half_width = head_width // 2
    freqs = 10000.0 ** (-2.0 * jnp.arange(half_width, dtype=jnp.float32) / head_width)
    angles = jnp.arange(seq_len, dtype=jnp.float32)[:, None] * freqs[None, :]
    return (jnp.cos(angles), jnp.sin(angles))


def rotate(vector, cos_table, sin_table):
    first_half, second_half = jnp.split(vector, 2, axis=-1)
    cos_part = cos_table[:, None, :]
    sin_part = sin_table[:, None, :]
    return jnp.concatenate(
        [
            first_half * cos_part - second_half * sin_part,
            second_half * cos_part + first_half * sin_part,
        ],
        axis=-1,
    )


def contract(left_rows, right_rows):
    return lax.dot_general(
        left_rows, right_rows, (((0,), (0,)), ((), ())), preferred_element_type=jnp.float32
    )


def gather_rows(row_values, weight):

    def project(shard_rows, offset):
        return (shard_rows, jnp.dot(shard_rows, weight, preferred_element_type=jnp.float32))

    return project(lax.all_gather(row_values, "tensor", axis=0, tiled=True), jnp.int32(0))


def scatter_rows(row_values, weight, row_count):

    def partial_term(offset, span):
        return jnp.dot(row_values, weight, preferred_element_type=jnp.float32)

    return lax.psum_scatter(
        partial_term(jnp.int32(0), lax.axis_size("tensor") * row_count),
        "tensor",
        scatter_dimension=0,
        tiled=True,
    )


def gather_grads(row_values, weight):

    def project(shard_rows, offset):
        return (shard_rows, jnp.dot(shard_rows, weight.T, preferred_element_type=jnp.float32))

    return project(lax.all_gather(row_values, "tensor", axis=0, tiled=True), jnp.int32(0))


def scatter_grads(row_values, weight, row_count):

    def partial_term(offset, span):
        return jnp.dot(row_values, weight.T, preferred_element_type=jnp.float32)

    return lax.psum_scatter(
        partial_term(jnp.int32(0), lax.axis_size("tensor") * row_count),
        "tensor",
        scatter_dimension=0,
        tiled=True,
    )


def attention_probs(queries, key_rows):
    scores = jnp.einsum(
        "qhd,khd->hqk", queries, key_rows, preferred_element_type=jnp.float32
    ) * HEAD_DIM ** (-0.5)
    length = queries.shape[0]
    positions = jnp.arange(length, dtype=jnp.int32)
    causal = positions[:, None] >= positions[None, :]
    scores = jnp.where(causal[None], scores, -1e30)
    expos = jnp.exp(scores - jnp.max(scores, axis=-1, keepdims=True))
    return expos / jnp.sum(expos, axis=-1, keepdims=True)


def layer_forward(layer_input, weights):
    gains, w_qkv, w_out, w_up, w_down = weights
    row_count, model_width = layer_input.shape
    attn_in = norm_rows(layer_input, gains[0]).astype(jnp.bfloat16)
    gathered_a, qkv = gather_rows(attn_in, w_qkv.reshape(model_width, -1))
    length = qkv.shape[0]
    head_count = w_qkv.shape[2] // HEAD_DIM
    qkv = qkv.reshape(length, 3, head_count, HEAD_DIM)
    cos_table, sin_table = rotary_tables(length, HEAD_DIM)
    queries = rotate(qkv[:, 0], cos_table, sin_table).astype(jnp.bfloat16)
    key_rows = rotate(qkv[:, 1], cos_table, sin_table).astype(jnp.bfloat16)
    values = qkv[:, 2].astype(jnp.bfloat16)
    attn_probs = attention_probs(queries, key_rows).astype(jnp.bfloat16)
    mixed = jnp.einsum("hqk,khd->qhd", attn_probs, values, preferred_element_type=jnp.float32)
    mixed = mixed.reshape(length, -1).astype(jnp.bfloat16)
    attn_branch = scatter_rows(mixed, w_out, row_count)
    hidden = layer_input + norm_rows(attn_branch, gains[1])
    mlp_in = norm_rows(hidden, gains[2]).astype(jnp.bfloat16)
    gathered_c, up_act = gather_rows(mlp_in, w_up)
    gelu_out = jax.nn.gelu(up_act, approximate=True).astype(jnp.bfloat16)
    down_branch = scatter_rows(gelu_out, w_down, row_count)
    result = hidden + norm_rows(down_branch, gains[3])
    kept_values = (
        gathered_a,
        queries,
        key_rows,
        values,
        mixed,
        attn_branch,
        hidden,
        gathered_c,
        up_act,
        gelu_out,
        down_branch,
    )
    return (result, kept_values)


def layer_backward(layer_input, grad_result, kept_values, weights):
    gains, w_qkv, w_out, w_up, w_down = weights
    (
        gathered_a,
        queries,
        key_rows,
        values,
        mixed,
        attn_branch,
        hidden,
        gathered_c,
        up_act,
        gelu_out,
        down_branch,
    ) = kept_values
    row_count, model_width = layer_input.shape
    pullback = jax.vjp(norm_rows, down_branch, gains[3])[1]
    grad_down, gain_three = pullback(grad_result)
    gathered_dd, grad_gelu = gather_grads(grad_down.astype(jnp.bfloat16), w_down)
    down_total = contract(gelu_out, gathered_dd)
    pullback = jax.vjp(lambda vector: jax.nn.gelu(vector, approximate=True), up_act)[1]
    grad_up = pullback(grad_gelu)[0].astype(jnp.bfloat16)
    up_total = contract(gathered_c, grad_up)
    grad_mlp = scatter_grads(grad_up, w_up, row_count)
    pullback = jax.vjp(norm_rows, hidden, gains[2])[1]
    grad_norm_mlp, gain_two = pullback(grad_mlp)
    grad_hidden = grad_result + grad_norm_mlp
    pullback = jax.vjp(norm_rows, attn_branch, gains[1])[1]
    grad_attn, gain_one = pullback(grad_hidden)
    gathered_da, grad_mixed = gather_grads(grad_attn.astype(jnp.bfloat16), w_out)
    out_total = contract(mixed, gathered_da)
    length = grad_mixed.shape[0]
    head_count = w_qkv.shape[2] // HEAD_DIM
    grad_mixed = grad_mixed.astype(jnp.bfloat16).reshape(length, head_count, HEAD_DIM)
    attn_probs = attention_probs(queries, key_rows)
    probs_low = attn_probs.astype(jnp.bfloat16)
    grad_probs = jnp.einsum("qhd,khd->hqk", grad_mixed, values, preferred_element_type=jnp.float32)
    grad_values = jnp.einsum(
        "hqk,qhd->khd", probs_low, grad_mixed, preferred_element_type=jnp.float32
    )
    row_dots = jnp.sum(grad_probs * attn_probs, axis=-1, keepdims=True)
    grad_scores = (attn_probs * (grad_probs - row_dots)).astype(jnp.bfloat16)
    scale_value = HEAD_DIM ** (-0.5)
    grad_queries = (
        jnp.einsum("hqk,khd->qhd", grad_scores, key_rows, preferred_element_type=jnp.float32)
        * scale_value
    )
    grad_keys = (
        jnp.einsum("hqk,qhd->khd", grad_scores, queries, preferred_element_type=jnp.float32)
        * scale_value
    )
    cos_table, sin_table = rotary_tables(length, HEAD_DIM)
    pullback = jax.vjp(lambda vector: rotate(vector, cos_table, sin_table), grad_queries)[1]
    grad_q_raw = pullback(grad_queries)[0]
    grad_k_raw = pullback(grad_keys)[0]
    grad_qkv = (
        jnp.stack([grad_q_raw, grad_k_raw, grad_values], axis=1)
        .reshape(length, -1)
        .astype(jnp.bfloat16)
    )
    qkv_total = contract(gathered_a, grad_qkv).reshape(model_width, 3, -1)
    grad_attn_in = scatter_grads(grad_qkv, w_qkv.reshape(model_width, -1), row_count)
    pullback = jax.vjp(norm_rows, layer_input, gains[0])[1]
    grad_norm_in, gain_zero = pullback(grad_attn_in)
    grad_input = grad_hidden + grad_norm_in
    gain_total = jnp.stack([gain_zero, gain_one, gain_two, gain_three])
    return (grad_input, (gain_total, qkv_total, out_total, up_total, down_total))


def lagged(first_section, stacked):
    blank = jnp.zeros_like(stacked[:1])
    earlier = jnp.concatenate([blank, stacked[:-1]])
    later = jnp.concatenate([stacked[1:], blank])
    return jnp.where(first_section, earlier, later)


def per_device(
    inputs,
    out_cotangent,
    group_ids,
    group_weights,
    gains,
    qkv_weight,
    out_weight,
    up_weight,
    down_weight,
):
    weights = (gains[0], qkv_weight[0], out_weight[0], up_weight[0], down_weight[0])
    micro_count, row_count, model_width = inputs.shape
    first_section = lax.axis_index("section") == 0
    group_count = group_weights.shape[0]
    matches = group_ids[..., None] == jnp.arange(group_count, dtype=jnp.int32)
    row_scale = jnp.sum(jnp.where(matches, group_weights, 0.0), axis=-1)
    scaled = out_cotangent.astype(jnp.float32) * row_scale[..., None]
    padded = jnp.concatenate([inputs, jnp.zeros((1, row_count, model_width), jnp.bfloat16)])

    def forward_tick(received, fresh_input):
        layer_input = jnp.where(first_section, fresh_input, received)
        result, kept_values = layer_forward(layer_input.astype(jnp.float32), weights)
        result_low = result.astype(jnp.bfloat16)
        outgoing = shifted(result_low, "section", 1)
        stashed = ()
        return (outgoing, (layer_input, result_low, stashed))

    start_rows = jnp.zeros((row_count, model_width), jnp.bfloat16)
    _, (layer_inputs, layer_results, stashed) = lax.scan(forward_tick, start_rows, padded)
    layer_outputs = jnp.where(first_section, layer_results[:-1], layer_results[1:])[None]
    back_inputs = lagged(first_section, layer_inputs)
    back_stash = jax.tree.map(lambda stacked: lagged(first_section, stacked), stashed)
    grad_padded = jnp.concatenate([scaled, jnp.zeros((1, row_count, model_width), jnp.float32)])
    tick_index = jnp.arange(micro_count + 1, dtype=jnp.int32)
    tick_valid = jnp.where(first_section, tick_index >= 1, tick_index < micro_count).astype(
        jnp.float32
    )

    def backward_tick(carry, step_item):
        received, totals = carry
        layer_input, cotangent, valid_now, stash_now = step_item
        grad_now = jnp.where(first_section, received.astype(jnp.float32), cotangent)
        input_now = layer_input.astype(jnp.float32)
        kept_values = layer_forward(input_now, weights)[1]
        grad_input, layer_grads = layer_backward(input_now, grad_now, kept_values, weights)
        totals = jax.tree.map(lambda total, update: total + valid_now * update, totals, layer_grads)
        grad_low = grad_input.astype(jnp.bfloat16)
        outgoing = shifted(grad_low, "section", -1)
        return ((outgoing, totals), grad_low)

    start_totals = (
        jnp.zeros((4, model_width), jnp.float32),
        jnp.zeros(qkv_weight.shape[1:], jnp.float32),
        jnp.zeros(out_weight.shape[1:], jnp.float32),
        jnp.zeros(up_weight.shape[1:], jnp.float32),
        jnp.zeros(down_weight.shape[1:], jnp.float32),
    )
    (_, totals), grad_lows = lax.scan(
        backward_tick,
        (start_rows, start_totals),
        (back_inputs, grad_padded, tick_valid, back_stash),
    )
    input_grads = jnp.where(first_section, grad_lows[1:], grad_lows[:-1])[None]
    gain_total, qkv_total, out_total, up_total, down_total = totals
    gains_grad = lax.psum_scatter(gain_total, ("dp", "tensor"), scatter_dimension=1, tiled=True)
    qkv_grad, out_grad, up_grad, down_grad = (
        lax.psum_scatter(
            qkv_total.astype(jnp.bfloat16), "dp", scatter_dimension=0, tiled=True
        ).astype(jnp.float32),
        lax.psum_scatter(
            out_total.astype(jnp.bfloat16), "dp", scatter_dimension=1, tiled=True
        ).astype(jnp.float32),
        lax.psum_scatter(
            up_total.astype(jnp.bfloat16), "dp", scatter_dimension=0, tiled=True
        ).astype(jnp.float32),
        lax.psum_scatter(
            down_total.astype(jnp.bfloat16), "dp", scatter_dimension=1, tiled=True
        ).astype(jnp.float32),
    )
    return (
        layer_outputs,
        input_grads,
        gains_grad[None],
        qkv_grad[None],
        out_grad[None],
        up_grad[None],
        down_grad[None],
    )


def rotated(block, cos_rows, sin_rows):
    lane = lax.broadcasted_iota(jnp.int32, block.shape, 1)
    ahead = pltpu.roll(block, 96, 1)
    behind = pltpu.roll(block, 32, 1)
    swapped = jnp.where(lane % 64 < 32, ahead, behind)
    return block * cos_rows + swapped * sin_rows


def dot_nt(left, right):
    return lax.dot_general(
        left, right, (((1,), (1,)), ((), ())), preferred_element_type=jnp.float32
    )


def dot_nn(left, right):
    return jnp.dot(left, right, preferred_element_type=jnp.float32)


def model_weight(owns, others, cols):
    sides = [jnp.concatenate([ref[:, cols] for ref in refs], axis=1) for refs in (owns, others)]
    return jnp.concatenate(sides, axis=0)


def stacked_up(values):
    return jnp.concatenate(values, axis=0)


def edge_masks(core, rows):
    key = lax.broadcasted_iota(jnp.int32, (rows, 2 * rows), 0)
    query = lax.broadcasted_iota(jnp.int32, (rows, 2 * rows), 1)
    mine = query < rows
    place = jnp.where(mine, query + core * rows, query - rows + (1 - core) * rows)
    return (key + core * rows <= place, key + (1 - core) * rows <= place)


def both_sides(value, half, start, stop, axis=0):
    if axis == 0:
        return jnp.concatenate([value[start:stop], value[half + start : half + stop]], axis=0)
    return jnp.concatenate([value[:, start:stop], value[:, half + start : half + stop]], axis=1)


def hidden_scores(scores, masks, tile, step):
    seen = step * tile
    pieces = []
    for side in range(2):
        base = side * (seen + tile)
        if seen:
            pieces.append(scores[base : base + seen])
        pieces.append(jnp.where(masks[side], scores[base + seen : base + seen + tile], -1e30))
    return jnp.concatenate(pieces, axis=0)


def one_head(rows, head):
    lane = lax.broadcasted_iota(jnp.int32, rows.shape, 1)
    return jnp.where(lane // 64 == head, rows, jnp.zeros_like(rows))


def pick_piece(weight, owns, others, cols):
    for j, (own, other) in enumerate(zip(owns, others)):

        @pl.when(pl.program_id(0) == j)
        def _():
            size = own.shape[0]
            weight[:size] = own[:, cols]
            weight[size:] = other[:, cols]


def attend_kernel(pieces, core_ref, cos_ref, sin_ref, own_rows, other_rows, *refs):
    owns, others = refs[:pieces], refs[pieces : 2 * pieces]
    q_ref, k_ref, v_ref, lse_ref, mix_ref, weight = refs[2 * pieces :]
    half = own_rows.shape[0]
    tile = TILE
    pick_piece(weight, owns, others, QKV)
    proj = dot_nn(stacked_up([own_rows[...], other_rows[...]]), weight[...])
    cos_rows, sin_rows = cos_ref[...], sin_ref[...]
    q = (rotated(proj[:, :128], cos_rows, sin_rows) * HEAD_DIM ** (-0.5)).astype(jnp.bfloat16)
    k = rotated(proj[:, 128:256], cos_rows, sin_rows).astype(jnp.bfloat16)
    v32 = proj[:, 256:]
    q_ref[0] = q
    k_ref[0] = k
    v_ref[0] = v32.astype(jnp.bfloat16)
    v_flip = v32.T.astype(jnp.bfloat16)
    masks = edge_masks(core_ref[0], tile)

    def scored(step, head):
        stop = (step + 1) * tile
        q_head = one_head(both_sides(q, half, step * tile, stop), head)
        return hidden_scores(dot_nt(both_sides(k, half, 0, stop), q_head), masks, tile, step)

    units = [(step, head) for step in range(half // tile) for head in range(2)]
    ahead = scored(*units[0])
    outs = []
    for spot, (step, head) in enumerate(units):
        scores = ahead
        if spot + 1 < len(units):
            ahead = scored(*units[spot + 1])
        stop = (step + 1) * tile
        top = jnp.max(scores, axis=0, keepdims=True)
        expos = jnp.exp(scores - top)
        total = jnp.sum(expos, axis=0, keepdims=True)
        lse = top + jnp.log(total)
        lse_ref[0, head : head + 1, step * tile : stop] = lse[:, :tile]
        lse_ref[0, head : head + 1, half + step * tile : half + stop] = lse[:, tile:]
        v_cols = both_sides(v_flip, half, 0, stop, axis=1)
        out = dot_nn(v_cols[64 * head : 64 * head + 64], expos.astype(jnp.bfloat16))
        outs.append(out * (1.0 / total))
        if head == 1:
            mixed = jnp.concatenate(outs, axis=0).T.astype(jnp.bfloat16)
            outs = []
            mix_ref[step * tile : stop, :] = mixed[:tile]
            mix_ref[half + step * tile : half + stop, :] = mixed[tile:]


def attend_back_kernel(pieces, core_ref, cos_ref, sin_ref, own_rows, other_rows, *refs):
    owns, others = refs[:pieces], refs[pieces : 2 * pieces]
    q_ref, k_ref, v_ref, lse_ref, out_ref, weight, dq, dk, dv = refs[2 * pieces :]
    half = own_rows.shape[0]
    tile = TILE
    pick_piece(weight, owns, others, OUT)
    rows = stacked_up([own_rows[...], other_rows[...]])
    d_mixed = dot_nn(rows, weight[...]).astype(jnp.bfloat16)
    q, k, v = q_ref[0], k_ref[0], v_ref[0]
    k_flip = k.astype(jnp.float32).T.astype(jnp.bfloat16)
    masks = edge_masks(core_ref[0], tile)
    steps = half // tile

    def scored(step, head):
        stop = (step + 1) * tile
        q_head = one_head(both_sides(q, half, step * tile, stop), head)
        g_head = one_head(both_sides(d_mixed, half, step * tile, stop), head)
        scores = hidden_scores(dot_nt(both_sides(k, half, 0, stop), q_head), masks, tile, step)
        return q_head, g_head, scores, dot_nt(both_sides(v, half, 0, stop), g_head)

    units = [(step, head) for step in reversed(range(steps)) for head in range(2)]
    ahead = scored(*units[0])
    dq_flips = []
    dk_sum = dv_sum = None
    for spot, (step, head) in enumerate(units):
        q_head, g_head, scores, d_probs = ahead
        if spot + 1 < len(units):
            ahead = scored(*units[spot + 1])
        stop = (step + 1) * tile
        lse = both_sides(lse_ref[0], half, step * tile, stop, axis=1)
        probs = jnp.exp(scores - lse[head : head + 1])
        dots = jnp.sum(probs * d_probs, axis=0, keepdims=True)
        d_scores = (probs * (d_probs - dots)).astype(jnp.bfloat16)
        dv_part = dot_nn(probs.astype(jnp.bfloat16), g_head)
        dk_part = dot_nn(d_scores, q_head)
        k_cols = both_sides(k_flip, half, 0, stop, axis=1)
        dq_flips.append(dot_nn(k_cols[64 * head : 64 * head + 64], d_scores))
        if head == 0:
            dv_sum, dk_sum = dv_part, dk_part
            continue
        dv_sum, dk_sum = dv_sum + dv_part, dk_sum + dk_part
        dq_rows = jnp.concatenate(dq_flips, axis=0).T * HEAD_DIM ** (-0.5)
        dq_flips = []
        dq[step * tile : stop] = dq_rows[:tile]
        dq[half + step * tile : half + stop] = dq_rows[tile:]
        for base, part in ((0, slice(0, stop)), (half, slice(stop, 2 * stop))):
            if step == steps - 1:
                dk[base : base + stop] = dk_sum[part]
                dv[base : base + stop] = dv_sum[part]
            else:
                dk[base : base + stop] += dk_sum[part]
                dv[base : base + stop] += dv_sum[part]
    cos_rows, sin_rows = cos_ref[...], -sin_ref[...]
    out_ref[:, :128] = rotated(dq[...], cos_rows, sin_rows).astype(jnp.bfloat16)
    out_ref[:, 128:256] = rotated(dk[...], cos_rows, sin_rows).astype(jnp.bfloat16)
    out_ref[:, 256:] = dv[...].astype(jnp.bfloat16)


def split_rows(total, own_ref, other_ref):
    half = own_ref.shape[0]
    own_ref[...] = total[:half]
    other_ref[...] = total[half:].astype(jnp.bfloat16)


def to_model_kernel(lefts, pieces, cols, *refs):
    left, refs = jnp.concatenate([ref[...] for ref in refs[:lefts]], axis=1), refs[lefts:]
    weight = model_weight(refs[:pieces], refs[pieces : 2 * pieces], cols)
    split_rows(dot_nt(left, weight), *refs[2 * pieces :])


def mlp_down_kernel(pieces, left_ref, *refs):
    sides = [stacked_up([ref[...] for ref in side]) for side in (refs[:pieces], refs[pieces:-2])]
    split_rows(dot_nn(left_ref[...], jnp.concatenate(sides, axis=1)), *refs[-2:])


def gelu_both(up_act):
    root = math.sqrt(2.0 / math.pi)
    square = up_act * up_act
    rise = 0.5 + 0.5 * jnp.tanh(up_act * (root + root * 0.044715 * square))
    value = up_act * rise
    slope = rise + value * (1.0 - rise) * (2.0 * root + 6.0 * root * 0.044715 * square)
    return value, slope


def mlp_up_kernel(pieces, own_rows, other_rows, *refs):
    owns, others = refs[:pieces], refs[pieces : 2 * pieces]
    gelu_ref, slope_ref = refs[2 * pieces :]
    half = own_rows.shape[0]
    size = owns[0].shape[1]
    step = half // 2
    units = [(j, i) for j in range(pieces) for i in range(4)]

    def product(j, i):
        rows = (own_rows, other_rows)[i // 2][i % 2 * step : (i % 2 + 1) * step]
        return dot_nn(rows, stacked_up([owns[j][...], others[j][...]]))

    ahead = product(*units[0])
    for spot, (j, i) in enumerate(units):
        up_act = ahead
        if spot + 1 < len(units):
            ahead = product(*units[spot + 1])
        value, slope = gelu_both(up_act)
        gelu_ref[i * step : (i + 1) * step, j * size : (j + 1) * size] = value.astype(jnp.bfloat16)
        slope_ref[i * step : (i + 1) * step, j * size : (j + 1) * size] = slope.astype(
            jnp.bfloat16
        )


def mlp_up_back_kernel(pieces, own_rows, other_rows, slope_ref, *refs):
    owns, others = refs[:pieces], refs[pieces : 2 * pieces]
    out_ref, weight, slope, sems = refs[2 * pieces :]
    half = own_rows.shape[1] // 2
    size = owns[0].shape[0]
    order = list(reversed(range(pieces)))
    copies = []
    for j in order:
        sources = (owns[j], others[j], slope_ref.at[:, pl.ds(j * size, size)])
        targets = (
            weight.at[j, :, pl.ds(0, half)],
            weight.at[j, :, pl.ds(half, half)],
            slope.at[:, pl.ds(j * size, size)],
        )
        copies.append(
            [
                pltpu.make_async_copy(source, target, sems.at[j, i])
                for i, (source, target) in enumerate(zip(sources, targets))
            ]
        )
        for copy in copies[-1]:
            copy.start()
    rows = stacked_up([own_rows[...], other_rows[...]])
    for j, arriving in zip(order, copies):
        cols = slice(j * size, (j + 1) * size)
        for copy in arriving:
            copy.wait()
        d_gelu = dot_nt(rows, weight[j])
        out_ref[:, cols] = (d_gelu * slope[:, cols].astype(jnp.float32)).astype(jnp.bfloat16)


def inverse_size(rows):
    return lax.rsqrt(jnp.mean(rows * rows, axis=-1, keepdims=True) + NORM_EPSILON)


def norm_back(rows, gain, grad):
    scale = inverse_size(rows)
    weighted = grad * gain
    inner = jnp.mean(rows * weighted, axis=-1, keepdims=True)
    return scale * weighted - rows * (scale * scale * scale * inner), rows * scale * grad


def folded(rows):
    return jnp.sum(rows.reshape(rows.shape[0] // 8, 8, rows.shape[1]), axis=0)


def wide(ref, spot):
    return ref[spot, :].astype(jnp.float32)


def by_chunks(count, body, sums=0, width=0):
    def one(i, carry):
        more = body(pl.ds(pl.multiple_of(i * CHUNK, CHUNK), CHUNK))
        return tuple(old + folded(new) for old, new in zip(carry, more))

    start = tuple(jnp.zeros((8, width), jnp.float32) for _ in range(sums))
    totals = lax.fori_loop(0, count // CHUNK, one, start)
    return [jnp.sum(total, axis=0, keepdims=True) for total in totals]


def norm_in_kernel(gain_ref, rows_ref, out_ref):
    def body(spot):
        rows = wide(rows_ref, spot)
        out_ref[spot, :] = (rows * inverse_size(rows) * gain_ref[0:1]).astype(jnp.bfloat16)
        return ()

    by_chunks(rows_ref.shape[0], body)


def after_attention_kernel(
    gain_ref, rows_ref, own_ref, other_ref, branch_ref, hidden_ref, out_ref
):
    def body(spot):
        branch = own_ref[spot, :] + wide(other_ref, spot)
        hidden = wide(rows_ref, spot) + branch * inverse_size(branch) * gain_ref[1:2]
        branch_ref[spot, :] = branch
        hidden_ref[spot, :] = hidden
        out_ref[spot, :] = (hidden * inverse_size(hidden) * gain_ref[2:3]).astype(jnp.bfloat16)
        return ()

    by_chunks(rows_ref.shape[0], body)


def after_mlp_kernel(gain_ref, hidden_ref, own_ref, other_ref, branch_ref, out_ref):
    def body(spot):
        branch = own_ref[spot, :] + wide(other_ref, spot)
        branch_ref[spot, :] = branch
        result = hidden_ref[spot, :] + branch * inverse_size(branch) * gain_ref[3:4]
        out_ref[spot, :] = result.astype(jnp.bfloat16)
        return ()

    by_chunks(hidden_ref.shape[0], body)


def into_mlp_back_kernel(gain_ref, grad_ref, branch_ref, out_ref, sum_ref):
    def body(spot):
        d_rows, d_gain = norm_back(branch_ref[spot, :], gain_ref[3:4], wide(grad_ref, spot))
        out_ref[spot, :] = d_rows.astype(jnp.bfloat16)
        return (d_gain,)

    (sum_ref[...],) = by_chunks(grad_ref.shape[0], body, 1, grad_ref.shape[1])


def into_attention_back_kernel(
    gain_ref, grad_ref, own_ref, other_ref, hidden_ref, branch_ref, d_hidden_ref, out_ref, *sums
):
    def body(spot):
        d_rows = own_ref[spot, :] + wide(other_ref, spot)
        d_rows, d_gain = norm_back(hidden_ref[spot, :], gain_ref[2:3], d_rows)
        d_hidden = wide(grad_ref, spot) + d_rows
        d_hidden_ref[spot, :] = d_hidden
        d_rows, d_first = norm_back(branch_ref[spot, :], gain_ref[1:2], d_hidden)
        out_ref[spot, :] = d_rows.astype(jnp.bfloat16)
        return (d_first, d_gain)

    totals = by_chunks(grad_ref.shape[0], body, 2, grad_ref.shape[1])
    sums[0][...], sums[1][...] = totals


def out_of_layer_kernel(gain_ref, rows_ref, own_ref, other_ref, d_hidden_ref, out_ref, sum_ref):
    def body(spot):
        d_rows = own_ref[spot, :] + wide(other_ref, spot)
        d_rows, d_gain = norm_back(wide(rows_ref, spot), gain_ref[0:1], d_rows)
        out_ref[spot, :] = (d_hidden_ref[spot, :] + d_rows).astype(jnp.bfloat16)
        return (d_gain,)

    (sum_ref[...],) = by_chunks(rows_ref.shape[0], body, 1, rows_ref.shape[1])


def work(flops, arrays):
    size = sum(math.prod(array.shape) * jnp.dtype(array.dtype).itemsize for array in arrays)
    return pl.CostEstimate(flops=flops, bytes_accessed=size, transcendentals=0)


def far(array):
    return pltpu.with_memory_space_constraint(array, pltpu.HBM)


def without(kernel, first, count):
    return lambda *refs: kernel(*refs[:first], *refs[first + count :])


def on_chip(kernel, name, outs, *operands, limit=ROWS_VMEM, flops=0, waits=()):
    shapes = [jax.ShapeDtypeStruct(shape, dtype) for shape, dtype in outs]
    space = pl.BlockSpec(memory_space=pltpu.VMEM)
    return pl.pallas_call(
        without(kernel, len(operands), len(waits)),
        in_specs=[space] * len(operands) + [pl.BlockSpec(memory_space=pl.ANY)] * len(waits),
        out_specs=[space] * len(outs),
        out_shape=shapes,
        compiler_params=pltpu.CompilerParams(vmem_limit_bytes=limit),
        cost_estimate=work(flops, (*operands, *shapes)),
        name=name,
    )(*operands, *map(far, waits))


def whole_block(array):
    return pl.BlockSpec(array.shape, lambda j: (0,) * array.ndim)


def by_pairs(kernel, name, core, operands, pieces, blocks, outs, scratch, flops, waits):
    shapes = [jax.ShapeDtypeStruct(shape, dtype) for shape, dtype, _ in outs]
    taken = 1 + len(operands) + 2 * len(pieces[0]) + len(blocks)
    return pl.pallas_call(
        without(functools.partial(kernel, len(pieces[0])), taken, len(waits)),
        grid=(len(pieces[0]),),
        in_specs=[pl.BlockSpec(memory_space=pltpu.SMEM)]
        + [whole_block(array) for array in (*operands, *pieces[0], *pieces[1])]
        + [spec for _, spec in blocks]
        + [pl.BlockSpec(memory_space=pl.ANY)] * len(waits),
        out_specs=[spec for _, _, spec in outs],
        out_shape=shapes,
        scratch_shapes=scratch,
        compiler_params=pltpu.CompilerParams(vmem_limit_bytes=KERNEL_VMEM),
        cost_estimate=work(flops, (*operands, *pieces[0], *pieces[1], *shapes)),
        name=name,
    )(core, *operands, *pieces[0], *pieces[1], *[array for array, _ in blocks], *map(far, waits))


def mlp_up_back(rows, slope, pieces, waits):
    length, units = slope.shape
    unit, half = pieces[0][0].shape
    count = len(pieces[0])
    every, space = pl.BlockSpec(memory_space=pl.ANY), pl.BlockSpec(memory_space=pltpu.VMEM)
    return pl.pallas_call(
        without(functools.partial(mlp_up_back_kernel, count), 3 + 2 * count, len(waits)),
        in_specs=[space] * 2 + [every] * (1 + 2 * count + len(waits)),
        out_specs=space,
        out_shape=jax.ShapeDtypeStruct((length, units), jnp.bfloat16),
        scratch_shapes=[
            pltpu.VMEM((count, unit, 2 * half), jnp.bfloat16),
            pltpu.VMEM((length, units), jnp.bfloat16),
            pltpu.SemaphoreType.DMA((count, 3)),
        ],
        compiler_params=pltpu.CompilerParams(vmem_limit_bytes=KERNEL_VMEM),
        name="mlp_up_back",
    )(*rows, *map(far, (slope, *pieces[0], *pieces[1], *waits)))


def attend(core, tables, rows, pieces, waits):
    half, features = rows[0].shape
    length, count = 2 * half, len(pieces[0])
    lanes = ((count, length, 128), jnp.bfloat16, pl.BlockSpec((1, length, 128), lambda j: (j, 0, 0)))
    lse = ((count, 2, length), jnp.float32, pl.BlockSpec((1, 2, length), lambda j: (j, 0, 0)))
    mixed = ((length, count * 128), jnp.bfloat16, pl.BlockSpec((length, 128), lambda j: (0, j)))
    return by_pairs(
        attend_kernel,
        "attend",
        core,
        (*tables, *rows),
        pieces,
        (),
        (lanes, lanes, lanes, lse, mixed),
        [pltpu.VMEM((features, 384), jnp.bfloat16)],
        count * length * (2 * features * 384 + 2 * PAIR_WORK * length),
        waits,
    )


def attend_back(core, tables, rows, pieces, base, waits, q, k, v, lse):
    half, features = rows[0].shape
    length, count = 2 * half, len(pieces[0])
    lanes = pl.BlockSpec((1, length, 128), lambda j: (base + j, 0, 0))
    lse_spec = pl.BlockSpec((1, 2, length), lambda j: (base + j, 0, 0))
    out = ((length, count * 384), jnp.bfloat16, pl.BlockSpec((length, 384), lambda j: (0, j)))
    return by_pairs(
        attend_back_kernel,
        "attend_back",
        core,
        (*tables, *rows),
        pieces,
        ((q, lanes), (k, lanes), (v, lanes), (lse, lse_spec)),
        (out,),
        [pltpu.VMEM((features, 128), jnp.bfloat16)] + [pltpu.VMEM((length, 128), jnp.float32)] * 3,
        count * length * (2 * features * 128 + 5 * PAIR_WORK * length),
        waits,
    )[0]


def exchanged(parts):
    return parts[0], flip_pairs(parts[1], 1)


def model_rows(kernel, name, lefts, pieces, waits=()):
    length, width = lefts[0].shape[0], 2 * MODEL_HALF
    outs = (((length // 2, width), jnp.float32), ((length // 2, width), jnp.bfloat16))
    hidden = sum(left.shape[1] for left in lefts)
    more = {"limit": KERNEL_VMEM, "flops": 2 * length * width * hidden, "waits": waits}
    return exchanged(on_chip(kernel, name, outs, *lefts, *pieces[0], *pieces[1], **more))


def flip_pairs(block, distance):
    size = lax.axis_size("dp")
    return lax.ppermute(block, "dp", [(i, i ^ distance) for i in range(size)])


def passed_on(block, step):
    size = lax.axis_size("tensor")
    return lax.ppermute(block, "tensor", [(i, (i + step) % size) for i in range(size)])


def dot_tn(left, right):
    return lax.dot_general(
        left, right, (((0,), (0,)), ((), ())), preferred_element_type=jnp.float32
    )


def fetch(first_ref, zeros, ones, buffers, sems):
    for section, sources in enumerate((zeros, ones)):

        @pl.when(first_ref[0] == section)
        def _():
            for i, (source, buffer) in enumerate(zip(sources, buffers)):
                pltpu.make_async_copy(source, buffer, sems.at[i]).start()

    def arrived(*places):
        for i in places:
            pltpu.make_async_copy(zeros[i], buffers[i], sems.at[i]).wait()

    return arrived


def mlp_grads_kernel(base, section_ref, *refs):
    (own_one, other_one, own_two, other_two), (rows, d_up, gelu, d_down, sems) = refs[12:16], refs[16:]
    half, size = own_one.shape[0] // 2, own_one.shape[1]
    cols = pl.ds(base * size, 2 * size)

    def parts(own_rows, other_rows, d_up_ref, gelu_ref, own_grad, other_grad):
        whole = (d_up_ref.at[:, cols], gelu_ref.at[:, cols])
        return (own_rows, other_rows, *whole, own_grad, other_grad)

    count = refs[0].shape[0]
    buffers = (
        rows.at[pl.ds(0, count)],
        rows.at[pl.ds(count, count)],
        d_up,
        gelu,
        d_down.at[pl.ds(0, count)],
        d_down.at[pl.ds(count, count)],
    )
    arrived = fetch(section_ref, parts(*refs[:6]), parts(*refs[6:12]), buffers, sems)
    for j, own, other in ((1, own_two, other_two), (0, own_one, other_one)):
        cols = slice(j * size, (j + 1) * size)
        if j == 1:
            arrived(0, 1, 2)
        up = dot_tn(rows[...], d_up[:, cols])
        own[:half] = up[:half]
        other[:half] = up[half:].astype(jnp.bfloat16)
        if j == 1:
            arrived(3, 4, 5)
        down = dot_tn(gelu[:, cols], d_down[...])
        own[half:] = down[:, :half]
        other[half:] = down[:, half:].astype(jnp.bfloat16)


def attn_grads_kernel(base, section_ref, *refs):
    (own_one, other_one, own_two, other_two), (rows, d_qkv, mixed, d_attn, sems) = refs[12:16], refs[16:]
    half, size = own_one.shape[0], d_qkv.shape[1] // 2
    count = refs[0].shape[0]
    cols = pl.ds(base * 128, 256)

    def parts(own_rows, other_rows, d_qkv_ref, mixed_ref, own_grad, other_grad):
        return (own_rows, other_rows, d_qkv_ref, mixed_ref.at[:, cols], own_grad, other_grad)

    buffers = (
        rows.at[pl.ds(0, count)],
        rows.at[pl.ds(count, count)],
        d_qkv,
        mixed,
        d_attn.at[pl.ds(0, count)],
        d_attn.at[pl.ds(count, count)],
    )
    arrived = fetch(section_ref, parts(*refs[:6]), parts(*refs[6:12]), buffers, sems)
    for j, own, other in ((1, own_two, other_two), (0, own_one, other_one)):
        if j == 1:
            arrived(0, 1, 2)
        qkv = dot_tn(rows[...], d_qkv[:, j * size : (j + 1) * size])
        if j == 1:
            arrived(3, 4, 5)
        out = dot_tn(d_attn[...], mixed[:, j * 128 : (j + 1) * 128])
        own[:, :size] = qkv[:half]
        own[:, size:] = out[:half]
        other[:, :size] = qkv[half:].astype(jnp.bfloat16)
        other[:, size:] = out[half:].astype(jnp.bfloat16)


def weight_grads(kernel, name, base, section, zeros, ones, shape, columns, waits=()):
    length = 2 * zeros[0].shape[0]
    width = zeros[0].shape[1]
    every = pl.BlockSpec(memory_space=pl.ANY)
    space = pl.BlockSpec(memory_space=pltpu.VMEM)
    arrays = (*zeros, *ones)
    first, second, third, fourth = pl.pallas_call(
        without(functools.partial(kernel, base), 1 + len(arrays), len(waits)),
        in_specs=[pl.BlockSpec(memory_space=pltpu.SMEM)] + [every] * (len(arrays) + len(waits)),
        out_specs=[space] * 4,
        out_shape=[
            jax.ShapeDtypeStruct(shape, jnp.float32),
            jax.ShapeDtypeStruct(shape, jnp.bfloat16),
        ]
        * 2,
        scratch_shapes=[
            pltpu.VMEM((length, width), jnp.bfloat16),
            pltpu.VMEM((length, columns[0]), jnp.bfloat16),
            pltpu.VMEM((length, columns[1]), jnp.bfloat16),
            pltpu.VMEM((length, width), jnp.bfloat16),
            pltpu.SemaphoreType.DMA((6,)),
        ],
        compiler_params=pltpu.CompilerParams(vmem_limit_bytes=KERNEL_VMEM),
        name=name,
    )(section, *map(far, (*arrays, *waits)))
    return [(first, flip_pairs(second, 2)), (third, flip_pairs(fourth, 2))]


def moved_kernel(own_ref, other_ref, *refs):
    out_ref = refs[-1]

    def body(i, carry):
        spot = pl.ds(pl.multiple_of(i * CHUNK, CHUNK), CHUNK)
        total = own_ref[spot, :]
        for ref in (other_ref, *refs[:-1]):
            total = total + wide(ref, spot)
        out_ref[spot, :] = total.astype(jnp.bfloat16)
        return carry

    lax.fori_loop(0, own_ref.shape[0] // CHUNK, body, 0)


def gates_kernel(up_ref, down_ref, up_out, down_out):
    up_out[...] = up_ref[...]
    down_out[...] = down_ref[...]


def gate_kernel(piece_ref, out_ref):
    out_ref[...] = piece_ref[...]


def mlp_sum_kernel(core_ref, own_ref, other_ref, moved_ref, up_keep, down_keep, up_send, down_send):
    half = own_ref.shape[0] // 2
    size = up_keep.shape[0]

    def total(rows, cols):
        more = other_ref[rows, cols].astype(jnp.float32) + moved_ref[rows, cols].astype(jnp.float32)
        return own_ref[rows, cols] + more

    for core in range(2):

        @pl.when(core_ref[0] == core)
        def _():
            for place, up, down in ((core, up_keep, down_keep), (1 - core, up_send, down_send)):
                spot = slice(place * size, (place + 1) * size)
                up[...] = total(spot, slice(None))
                down[...] = total(slice(half, None), spot)


def mlp_join_kernel(core_ref, up_keep, down_keep, up_sent, down_sent, up_out, down_out):
    size = up_keep.shape[1]
    for core in range(2):

        @pl.when(core_ref[0] == core)
        def _():
            places = ((core, up_keep, down_keep), (1 - core, up_sent, down_sent))
            for place, up, down in places:
                spot = slice(place * size, (place + 1) * size)
                up_out[:, spot] = up[...]
                down_out[spot] = down[...]


def pick_kernel(core_ref, rows_ref, keep_ref, send_ref):
    count = keep_ref.shape[0]
    keep_ref[...] = rows_ref[pl.ds(core_ref[0] * count, count)]
    send_ref[...] = rows_ref[pl.ds((1 - core_ref[0]) * count, count)]


def in_order_kernel(core_ref, keep_ref, sent_ref, out_ref):
    out_ref[:, pl.ds(core_ref[0], 1)] = keep_ref[...][:, None]
    out_ref[:, pl.ds(1 - core_ref[0], 1)] = sent_ref[...][:, None]


def with_core(kernel, name, core, outs, *operands, waits=()):
    space = pl.BlockSpec(memory_space=pltpu.VMEM)
    return pl.pallas_call(
        without(kernel, 1 + len(operands), len(waits)),
        in_specs=[pl.BlockSpec(memory_space=pltpu.SMEM)]
        + [space] * len(operands)
        + [pl.BlockSpec(memory_space=pl.ANY)] * len(waits),
        out_specs=[space] * len(outs),
        out_shape=[jax.ShapeDtypeStruct(shape, dtype) for shape, dtype in outs],
        compiler_params=pltpu.CompilerParams(vmem_limit_bytes=ROWS_VMEM),
        name=name,
    )(core, *operands, *map(far, waits))


def last_sum_kernel(core_ref, own_ref, other_ref, moved_ref, keep_ref, send_ref):
    rows = keep_ref.shape[0]

    def total(block):
        spot = pl.ds(pl.multiple_of(block * rows, rows), rows)
        return own_ref[spot, :] + wide(other_ref, spot) + wide(moved_ref, spot)

    keep_ref[...] = total(core_ref[0])
    send_ref[...] = total(1 - core_ref[0])


def joined_kernel(spots, core_ref, keep_ref, sent_ref, column_ref, row_ref):
    size = row_ref.shape[0] // 2
    for core in range(2):

        @pl.when(core_ref[0] == core)
        def _():
            for place, source in ((core, keep_ref), (1 - core, sent_ref)):
                for start, stop, to in spots:
                    step = stop - start
                    column_ref[:, to + place * step : to + (place + 1) * step] = source[:, start:stop]
                row_ref[place * size : (place + 1) * size] = source[:, spots[-1][1] :].T


def per_chip(
    inputs,
    out_cotangent,
    group_ids,
    group_weights,
    gains,
    qkv_weight,
    out_weight,
    up_weight,
    down_weight,
):
    micro, row_count, width = inputs.shape
    tensor = lax.axis_size("tensor")
    part = row_count // 2
    wide_half = width // 2
    length = tensor * row_count
    half = length // 2
    first = lax.axis_index("section") == 0
    place = lax.axis_index("dp")
    core = place % 2
    upper = place // 2 % 2
    core_zero = core == 0
    low_half = upper == 0

    def ordered(mine, other):
        return jnp.where(core_zero, mine, other), jnp.where(core_zero, other, mine)

    def own_first(values):
        return jnp.where(low_half, values, jnp.roll(values, wide_half, axis=-1))

    def both_rows(own):
        return own, flip_pairs(own, 1)

    def to_chip(block):
        split = block.reshape((micro, 2, part) + block.shape[2:])
        mine = lax.dynamic_index_in_dim(split, core, 1, keepdims=False)
        other = lax.dynamic_index_in_dim(split, 1 - core, 1, keepdims=False)
        return lax.all_to_all(
            jnp.concatenate(ordered(mine, flip_pairs(other, 1))), "tensor", 0, 0, tiled=True
        )

    def from_chip(spread_out, waits=()):
        piece = ((micro, part, width), jnp.bfloat16)
        keep, send = with_core(
            pick_kernel, "pick", core_word, (piece, piece), spread_out, waits=waits
        )
        outs = (((micro, 2, part, width), jnp.bfloat16),)
        (rows,) = with_core(
            in_order_kernel, "in_order", core_word, outs, keep, flip_pairs(send, 1)
        )
        return rows.reshape(micro, row_count, width)

    def columns(local):
        size = local.shape[-1] // 2
        mid = (0,) * (local.ndim - 2)
        piece = lax.dynamic_slice(
            local,
            (wide_half * upper, *mid, size * core),
            (wide_half, *local.shape[1:-1], size),
        )
        return piece.reshape(wide_half, -1)

    def rows(local):
        size = local.shape[0] // 2
        return lax.dynamic_slice(local, (size * core, wide_half * upper), (size, wide_half))

    core_word = core.astype(jnp.int32).reshape(1)
    attn_piece = jnp.concatenate([columns(qkv_weight[0]), rows(out_weight[0]).T], axis=1)

    def spread(piece):
        pieces = [piece]
        for _ in range(tensor - 1):
            pieces.append(passed_on(pieces[-1], 1))
        return pieces

    attn_own = spread(attn_piece)
    attn_other = [flip_pairs(piece, 2) for piece in attn_own]
    up_piece, down_piece = columns(up_weight[0]), rows(down_weight[0])
    up_other, down_other = [flip_pairs(up_piece, 2)], [flip_pairs(down_piece, 2)]
    outs = tuple((piece.shape, piece.dtype) for piece in (up_piece, down_piece))
    up_piece, down_piece = on_chip(
        gates_kernel, "gate", outs, up_piece, down_piece, waits=(attn_own[2], attn_other[0])
    )
    up_own, down_own = spread(up_piece), spread(down_piece)
    up_other += [flip_pairs(piece, 2) for piece in up_own[1:]]
    down_other += [flip_pairs(piece, 2) for piece in down_own[1:]]
    w_attn, w_up, w_down = (attn_own, attn_other), (up_own, up_other), (down_own, down_other)
    unit = up_piece.shape[1]
    units = tensor * unit

    group_count = group_weights.shape[0]
    matches = group_ids[..., None] == jnp.arange(group_count, dtype=jnp.int32)
    row_scale = jnp.sum(jnp.where(matches, group_weights, 0.0), axis=-1)
    weighted = (out_cotangent.astype(jnp.float32) * row_scale[..., None]).astype(jnp.bfloat16)
    start = to_chip(own_first(jnp.where(first, inputs, weighted))).reshape(half, width)
    gain = own_first(gains[0])

    turns = jnp.arange(half, dtype=jnp.int32)
    turns = turns // part * row_count + turns % part
    positions = jnp.concatenate([turns + core * part, turns + (1 - core) * part])
    freqs = 10000.0 ** (-2.0 * jnp.arange(HEAD_DIM // 2, dtype=jnp.float32) / HEAD_DIM)
    angles = positions.astype(jnp.float32)[:, None] * freqs[None, :]
    cos_part, sin_part = jnp.cos(angles), jnp.sin(angles)
    tables = (
        jnp.concatenate([cos_part] * 4, axis=1),
        jnp.concatenate([-sin_part, sin_part] * 2, axis=1),
    )
    row32, row16 = ((half, width), jnp.float32), ((half, width), jnp.bfloat16)
    unit16 = ((length, units), jnp.bfloat16)
    sum32 = ((1, width), jnp.float32)
    mlp_cost = {"limit": KERNEL_VMEM, "flops": 2 * length * width * units}
    every = slice(None)

    def model_kernel(cols, lefts=1):
        return functools.partial(to_model_kernel, lefts, tensor, cols)

    down_kernel = functools.partial(mlp_down_kernel, tensor)

    def forward(layer_input, waits):
        attn_in = both_rows(
            on_chip(norm_in_kernel, "norm_in", (row16,), gain, layer_input, waits=waits[0])[0]
        )
        *heads, mixed = attend(core_word, tables, attn_in, w_attn, waits[1])
        parts = model_rows(model_kernel(OUT), "attn_out", [mixed], w_attn, waits[2])
        operands = (gain, layer_input, *parts)
        branch, hidden, mlp_in = on_chip(
            after_attention_kernel, "after_attn", (row32, row32, row16), *operands, waits=waits[3]
        )
        mlp_in = both_rows(mlp_in)
        kernel = functools.partial(mlp_up_kernel, tensor)
        operands = (*mlp_in, *w_up[0], *w_up[1])
        gelu_out, slope = on_chip(kernel, "mlp_up", (unit16, unit16), *operands, **mlp_cost)
        parts = model_rows(down_kernel, "mlp_down", [gelu_out], w_down)
        mlp_branch, result = on_chip(
            after_mlp_kernel, "after_mlp", (row32, row16), gain, hidden, *parts
        )
        saved = (layer_input, heads, branch, hidden, slope, mlp_branch)
        return result, saved, (attn_in, mixed, mlp_in, gelu_out)

    def backward(grad, saved, hook, late=()):
        layer_input, heads, branch, hidden, slope, mlp_branch = saved
        operands = (gain, grad, mlp_branch)
        d_down, sum_three = on_chip(
            into_mlp_back_kernel, "into_mlp_back", (row16, sum32), *operands
        )
        d_down = both_rows(d_down)
        d_up = mlp_up_back(d_down, slope, w_down, late)
        waits = hook(d_down, d_up)
        parts = model_rows(model_kernel(every), "mlp_back", [d_up], w_up, waits)
        waits = hook()
        operands = (gain, grad, *parts, hidden, branch)
        outs = (row32, row16, sum32, sum32)
        d_hidden, d_attn, sum_one, sum_two = on_chip(
            into_attention_back_kernel, "into_attn_back", outs, *operands, waits=waits
        )
        d_attn = both_rows(d_attn)
        waits = hook(d_attn)
        d_qkv = []
        for base in reversed(range(0, tensor, 2)):
            some = [side[base : base + 2] for side in w_attn]
            now = attend_back(core_word, tables, d_attn, some, base, waits, *heads)
            d_qkv.insert(0, now)
            waits = hook(now)
        parts = model_rows(model_kernel(QKV, 2), "attn_back", d_qkv, w_attn, waits)
        operands = (gain, layer_input, *parts, d_hidden)
        d_input, sum_zero = on_chip(
            out_of_layer_kernel, "out_of_layer", (row16, sum32), *operands, waits=hook()
        )
        sums = jnp.concatenate([sum_zero, sum_one, sum_two, sum_three])
        return d_input, (d_qkv, d_attn, d_up, d_down), sums

    low_zero, saved_zero, lefts_zero = forward(
        start,
        (
            (up_piece, up_other[0], down_other[0]),
            (up_own[1], down_own[1]),
            (up_own[2], down_own[2], up_other[1], down_other[1]),
            (up_own[3], down_own[3], up_other[2], down_other[2]),
        ),
    )
    low_one, saved_one, lefts_one = forward(shifted(low_zero, "section", 1), ((),) * 4)
    grad_one, rights_one, gain_one = backward(start, saved_one, lambda *new: ())
    received = shifted(grad_one, "section", -1)

    lows = lax.optimization_barrier((low_zero, low_one, grad_one))[:2]
    lows = own_first(jnp.where(first, *lows)).reshape(tensor, part, width)
    lows = lax.all_to_all(lows, "tensor", 0, 0, tiled=True)

    section_word = lax.axis_index("section").astype(jnp.int32).reshape(1)

    def mlp_leaves(base, waits=()):
        zeros = (*lefts_zero[2], d_up, lefts_zero[3], *d_down)
        ones = (*lefts_one[2], rights_one[2], lefts_one[3], *rights_one[3])
        mlp_sums[base : base + 2] = weight_grads(
            mlp_grads_kernel,
            "mlp_grads",
            base,
            section_word,
            zeros,
            ones,
            (wide_half + unit, unit),
            (2 * unit, 2 * unit),
            waits,
        )

    def attn_leaves(base, d_qkv, waits):
        zeros = (*lefts_zero[0], d_qkv, lefts_zero[1], *d_attn)
        ones = (*lefts_one[0], rights_one[0][base // 2], lefts_one[1], *rights_one[1])
        attn_sums[base : base + 2] = weight_grads(
            attn_grads_kernel,
            "attn_grads",
            base,
            section_word,
            zeros,
            ones,
            (wide_half, 512),
            (768, 256),
            waits,
        )

    def moves_on(piece, *moved, waits=()):
        outs = ((piece[1].shape, jnp.bfloat16),)
        (total,) = on_chip(moved_kernel, "moved", outs, *piece, *moved, waits=waits)
        return total, passed_on(total, -1)

    mlp_sums, attn_sums = [None] * tensor, [None] * tensor
    mlp_moves, attn_moves = [None] * tensor, [None] * tensor
    hooks = iter(range(6))

    def hook(*new):
        nonlocal d_down, d_up, d_attn
        turn = next(hooks)
        if turn == 0:
            d_down, d_up = new
            mlp_leaves(2)
            return (mlp_sums[3][0],)
        if turn == 1:
            return ()
        if turn == 2:
            (d_attn,) = new
            total, mlp_moves[3] = moves_on(mlp_sums[3], waits=d_attn[:1])
            mlp_leaves(0, (total,))
            return (mlp_sums[1][0],)
        if turn == 3:
            total, mlp_moves[2] = moves_on(mlp_sums[2], mlp_moves[3], waits=new)
            attn_leaves(2, new[0], (total,))
            return (mlp_sums[2][1], mlp_moves[3], attn_sums[3][0])
        if turn == 4:
            total, mlp_moves[1] = moves_on(mlp_sums[1], mlp_moves[2], waits=new)
            attn_leaves(0, new[0], (total,))
            return (attn_sums[1][0],)
        total, attn_moves[3] = moves_on(attn_sums[3])
        return (mlp_sums[0][1], total, mlp_moves[1])

    d_down = d_up = d_attn = None
    grad_zero, rights_zero, gain_zero = backward(received, saved_zero, hook, (lows,))
    outputs = from_chip(lows, (grad_zero,))
    grads = own_first(jnp.where(first, grad_zero, grad_one)).reshape(tensor, part, width)
    grads = lax.all_to_all(grads, "tensor", 0, 0, tiled=True)

    block32 = ((wide_half // 2, unit), jnp.float32)
    down32 = ((unit, wide_half // 2), jnp.float32)
    up_keep, down_keep, up_send, down_send = with_core(
        mlp_sum_kernel,
        "mlp_sum",
        core_word,
        (block32, down32, block32, down32),
        *mlp_sums[0],
        mlp_moves[1],
    )
    outs = (
        ((wide_half // 2, 2 * unit), jnp.float32),
        ((2 * unit, wide_half // 2), jnp.float32),
    )
    sent = flip_pairs(up_send, 1), flip_pairs(down_send, 1)
    up_grad, down_grad = with_core(
        mlp_join_kernel, "mlp_join", core_word, outs, up_keep, down_keep, *sent
    )
    waits = (outputs, attn_sums[1][1])
    _, attn_moves[2] = moves_on(attn_sums[2], attn_moves[3], waits=waits)
    waits = (up_grad, grads, attn_sums[0][1])
    last, attn_moves[1] = moves_on(attn_sums[1], attn_moves[2], waits=waits)
    grads = from_chip(grads, (last,))
    gain_total = own_first(jnp.where(first, gain_zero, gain_one))
    count = tensor * lax.axis_size("dp")
    gain_parts = gain_total.reshape(4, count, width // count).swapaxes(0, 1)
    outs = ((gain_parts.shape, gain_parts.dtype),)
    (gain_parts,) = on_chip(gate_kernel, "gate", outs, gain_parts, waits=(last,))
    gain_parts = lax.all_to_all(gain_parts, ("dp", "tensor"), 0, 0, tiled=True)
    gains_grad = jnp.sum(gain_parts, axis=0)
    outs = (((wide_half // 2, 512), jnp.float32),) * 2
    keep, send = with_core(
        last_sum_kernel,
        "attn_sum",
        core_word,
        outs,
        *attn_sums[0],
        attn_moves[1],
        waits=(grads, gains_grad),
    )
    spots = tuple((i * 128, (i + 1) * 128, i * 256) for i in range(3))
    outs = (((wide_half // 2, 768), jnp.float32), ((256, wide_half // 2), jnp.float32))
    kernel = functools.partial(joined_kernel, spots)
    qkv_grad, out_grad = with_core(
        kernel, "attn_join", core_word, outs, keep, flip_pairs(send, 1)
    )
    qkv_grad = qkv_grad.reshape(wide_half // 2, 3, -1)

    return (
        outputs[None],
        grads[None],
        gains_grad[None],
        qkv_grad[None],
        out_grad[None],
        up_grad[None],
        down_grad[None],
    )


def takes_chips(sizes):
    return sizes["section"] == 2 and sizes["dp"] == 4 and sizes["tensor"] == 4


def solution(mesh):
    placed = (
        P("dp", "tensor", None),
        P("dp", "tensor", None),
        P("dp", "tensor"),
        P(),
        P("section", None, None),
        P("section", None, None, "tensor"),
        P("section", "tensor", None),
        P("section", None, "tensor"),
        P("section", "tensor", None),
    )
    body = per_chip if takes_chips(dict(mesh.shape)) else per_device
    return jax.shard_map(
        body,
        mesh=mesh,
        in_specs=placed,
        out_specs=(
            P("section", "dp", "tensor", None),
            P("section", "dp", "tensor", None),
            P("section", None, ("dp", "tensor")),
            P("section", "dp", None, "tensor"),
            P("section", "tensor", "dp"),
            P("section", "dp", "tensor"),
            P("section", "tensor", "dp"),
        ),
        check_vma=False,
    )
```

```python
import functools
import math

import jax
import jax.numpy as jnp
from jax import lax
from jax.experimental import pallas as pl
from jax.experimental.pallas import tpu as pltpu
from jax.sharding import PartitionSpec as P

HEAD_DIM = 64


NORM_EPSILON = 1e-06
TILE = 128
PAIR_WORK = 1024
MODEL_HALF = 512
QKV = slice(0, 384)
OUT = slice(384, 512)
CHUNK = 32
KERNEL_VMEM = 20 << 20
ROWS_VMEM = 3 << 20


def shifted(block, axis, distance):
    devices = range(lax.axis_size(axis))
    route = [(i - distance, i) for i in devices if i - distance in devices]
    return lax.ppermute(block, axis, route)


def norm_rows(vector, weight_gain):
    return (
        vector
        * lax.rsqrt(jnp.mean(vector * vector, axis=-1, keepdims=True) + NORM_EPSILON)
        * weight_gain
    )


def rotary_tables(seq_len, head_width):
    half_width = head_width // 2
    freqs = 10000.0 ** (-2.0 * jnp.arange(half_width, dtype=jnp.float32) / head_width)
    angles = jnp.arange(seq_len, dtype=jnp.float32)[:, None] * freqs[None, :]
    return (jnp.cos(angles), jnp.sin(angles))


def rotate(vector, cos_table, sin_table):
    first_half, second_half = jnp.split(vector, 2, axis=-1)
    cos_part = cos_table[:, None, :]
    sin_part = sin_table[:, None, :]
    return jnp.concatenate(
        [
            first_half * cos_part - second_half * sin_part,
            second_half * cos_part + first_half * sin_part,
        ],
        axis=-1,
    )


def contract(left_rows, right_rows):
    return lax.dot_general(
        left_rows, right_rows, (((0,), (0,)), ((), ())), preferred_element_type=jnp.float32
    )


def gather_rows(row_values, weight):

    def project(shard_rows, offset):
        return (shard_rows, jnp.dot(shard_rows, weight, preferred_element_type=jnp.float32))

    return project(lax.all_gather(row_values, "tensor", axis=0, tiled=True), jnp.int32(0))


def scatter_rows(row_values, weight, row_count):

    def partial_term(offset, span):
        return jnp.dot(row_values, weight, preferred_element_type=jnp.float32)

    return lax.psum_scatter(
        partial_term(jnp.int32(0), lax.axis_size("tensor") * row_count),
        "tensor",
        scatter_dimension=0,
        tiled=True,
    )


def gather_grads(row_values, weight):

    def project(shard_rows, offset):
        return (shard_rows, jnp.dot(shard_rows, weight.T, preferred_element_type=jnp.float32))

    return project(lax.all_gather(row_values, "tensor", axis=0, tiled=True), jnp.int32(0))


def scatter_grads(row_values, weight, row_count):

    def partial_term(offset, span):
        return jnp.dot(row_values, weight.T, preferred_element_type=jnp.float32)

    return lax.psum_scatter(
        partial_term(jnp.int32(0), lax.axis_size("tensor") * row_count),
        "tensor",
        scatter_dimension=0,
        tiled=True,
    )


def attention_probs(queries, key_rows):
    scores = jnp.einsum(
        "qhd,khd->hqk", queries, key_rows, preferred_element_type=jnp.float32
    ) * HEAD_DIM ** (-0.5)
    length = queries.shape[0]
    positions = jnp.arange(length, dtype=jnp.int32)
    causal = positions[:, None] >= positions[None, :]
    scores = jnp.where(causal[None], scores, -1e30)
    expos = jnp.exp(scores - jnp.max(scores, axis=-1, keepdims=True))
    return expos / jnp.sum(expos, axis=-1, keepdims=True)


def layer_forward(layer_input, weights):
    gains, w_qkv, w_out, w_up, w_down = weights
    row_count, model_width = layer_input.shape
    attn_in = norm_rows(layer_input, gains[0]).astype(jnp.bfloat16)
    gathered_a, qkv = gather_rows(attn_in, w_qkv.reshape(model_width, -1))
    length = qkv.shape[0]
    head_count = w_qkv.shape[2] // HEAD_DIM
    qkv = qkv.reshape(length, 3, head_count, HEAD_DIM)
    cos_table, sin_table = rotary_tables(length, HEAD_DIM)
    queries = rotate(qkv[:, 0], cos_table, sin_table).astype(jnp.bfloat16)
    key_rows = rotate(qkv[:, 1], cos_table, sin_table).astype(jnp.bfloat16)
    values = qkv[:, 2].astype(jnp.bfloat16)
    attn_probs = attention_probs(queries, key_rows).astype(jnp.bfloat16)
    mixed = jnp.einsum("hqk,khd->qhd", attn_probs, values, preferred_element_type=jnp.float32)
    mixed = mixed.reshape(length, -1).astype(jnp.bfloat16)
    attn_branch = scatter_rows(mixed, w_out, row_count)
    hidden = layer_input + norm_rows(attn_branch, gains[1])
    mlp_in = norm_rows(hidden, gains[2]).astype(jnp.bfloat16)
    gathered_c, up_act = gather_rows(mlp_in, w_up)
    gelu_out = jax.nn.gelu(up_act, approximate=True).astype(jnp.bfloat16)
    down_branch = scatter_rows(gelu_out, w_down, row_count)
    result = hidden + norm_rows(down_branch, gains[3])
    kept_values = (
        gathered_a,
        queries,
        key_rows,
        values,
        mixed,
        attn_branch,
        hidden,
        gathered_c,
        up_act,
        gelu_out,
        down_branch,
    )
    return (result, kept_values)


def layer_backward(layer_input, grad_result, kept_values, weights):
    gains, w_qkv, w_out, w_up, w_down = weights
    (
        gathered_a,
        queries,
        key_rows,
        values,
        mixed,
        attn_branch,
        hidden,
        gathered_c,
        up_act,
        gelu_out,
        down_branch,
    ) = kept_values
    row_count, model_width = layer_input.shape
    pullback = jax.vjp(norm_rows, down_branch, gains[3])[1]
    grad_down, gain_three = pullback(grad_result)
    gathered_dd, grad_gelu = gather_grads(grad_down.astype(jnp.bfloat16), w_down)
    down_total = contract(gelu_out, gathered_dd)
    pullback = jax.vjp(lambda vector: jax.nn.gelu(vector, approximate=True), up_act)[1]
    grad_up = pullback(grad_gelu)[0].astype(jnp.bfloat16)
    up_total = contract(gathered_c, grad_up)
    grad_mlp = scatter_grads(grad_up, w_up, row_count)
    pullback = jax.vjp(norm_rows, hidden, gains[2])[1]
    grad_norm_mlp, gain_two = pullback(grad_mlp)
    grad_hidden = grad_result + grad_norm_mlp
    pullback = jax.vjp(norm_rows, attn_branch, gains[1])[1]
    grad_attn, gain_one = pullback(grad_hidden)
    gathered_da, grad_mixed = gather_grads(grad_attn.astype(jnp.bfloat16), w_out)
    out_total = contract(mixed, gathered_da)
    length = grad_mixed.shape[0]
    head_count = w_qkv.shape[2] // HEAD_DIM
    grad_mixed = grad_mixed.astype(jnp.bfloat16).reshape(length, head_count, HEAD_DIM)
    attn_probs = attention_probs(queries, key_rows)
    probs_low = attn_probs.astype(jnp.bfloat16)
    grad_probs = jnp.einsum("qhd,khd->hqk", grad_mixed, values, preferred_element_type=jnp.float32)
    grad_values = jnp.einsum(
        "hqk,qhd->khd", probs_low, grad_mixed, preferred_element_type=jnp.float32
    )
    row_dots = jnp.sum(grad_probs * attn_probs, axis=-1, keepdims=True)
    grad_scores = (attn_probs * (grad_probs - row_dots)).astype(jnp.bfloat16)
    scale_value = HEAD_DIM ** (-0.5)
    grad_queries = (
        jnp.einsum("hqk,khd->qhd", grad_scores, key_rows, preferred_element_type=jnp.float32)
        * scale_value
    )
    grad_keys = (
        jnp.einsum("hqk,qhd->khd", grad_scores, queries, preferred_element_type=jnp.float32)
        * scale_value
    )
    cos_table, sin_table = rotary_tables(length, HEAD_DIM)
    pullback = jax.vjp(lambda vector: rotate(vector, cos_table, sin_table), grad_queries)[1]
    grad_q_raw = pullback(grad_queries)[0]
    grad_k_raw = pullback(grad_keys)[0]
    grad_qkv = (
        jnp.stack([grad_q_raw, grad_k_raw, grad_values], axis=1)
        .reshape(length, -1)
        .astype(jnp.bfloat16)
    )
    qkv_total = contract(gathered_a, grad_qkv).reshape(model_width, 3, -1)
    grad_attn_in = scatter_grads(grad_qkv, w_qkv.reshape(model_width, -1), row_count)
    pullback = jax.vjp(norm_rows, layer_input, gains[0])[1]
    grad_norm_in, gain_zero = pullback(grad_attn_in)
    grad_input = grad_hidden + grad_norm_in
    gain_total = jnp.stack([gain_zero, gain_one, gain_two, gain_three])
    return (grad_input, (gain_total, qkv_total, out_total, up_total, down_total))


def lagged(first_section, stacked):
    blank = jnp.zeros_like(stacked[:1])
    earlier = jnp.concatenate([blank, stacked[:-1]])
    later = jnp.concatenate([stacked[1:], blank])
    return jnp.where(first_section, earlier, later)


def per_device(
    inputs,
    out_cotangent,
    group_ids,
    group_weights,
    gains,
    qkv_weight,
    out_weight,
    up_weight,
    down_weight,
):
    weights = (gains[0], qkv_weight[0], out_weight[0], up_weight[0], down_weight[0])
    micro_count, row_count, model_width = inputs.shape
    first_section = lax.axis_index("section") == 0
    group_count = group_weights.shape[0]
    matches = group_ids[..., None] == jnp.arange(group_count, dtype=jnp.int32)
    row_scale = jnp.sum(jnp.where(matches, group_weights, 0.0), axis=-1)
    scaled = out_cotangent.astype(jnp.float32) * row_scale[..., None]
    padded = jnp.concatenate([inputs, jnp.zeros((1, row_count, model_width), jnp.bfloat16)])

    def forward_tick(received, fresh_input):
        layer_input = jnp.where(first_section, fresh_input, received)
        result, kept_values = layer_forward(layer_input.astype(jnp.float32), weights)
        result_low = result.astype(jnp.bfloat16)
        outgoing = shifted(result_low, "section", 1)
        stashed = ()
        return (outgoing, (layer_input, result_low, stashed))

    start_rows = jnp.zeros((row_count, model_width), jnp.bfloat16)
    _, (layer_inputs, layer_results, stashed) = lax.scan(forward_tick, start_rows, padded)
    layer_outputs = jnp.where(first_section, layer_results[:-1], layer_results[1:])[None]
    back_inputs = lagged(first_section, layer_inputs)
    back_stash = jax.tree.map(lambda stacked: lagged(first_section, stacked), stashed)
    grad_padded = jnp.concatenate([scaled, jnp.zeros((1, row_count, model_width), jnp.float32)])
    tick_index = jnp.arange(micro_count + 1, dtype=jnp.int32)
    tick_valid = jnp.where(first_section, tick_index >= 1, tick_index < micro_count).astype(
        jnp.float32
    )

    def backward_tick(carry, step_item):
        received, totals = carry
        layer_input, cotangent, valid_now, stash_now = step_item
        grad_now = jnp.where(first_section, received.astype(jnp.float32), cotangent)
        input_now = layer_input.astype(jnp.float32)
        kept_values = layer_forward(input_now, weights)[1]
        grad_input, layer_grads = layer_backward(input_now, grad_now, kept_values, weights)
        totals = jax.tree.map(lambda total, update: total + valid_now * update, totals, layer_grads)
        grad_low = grad_input.astype(jnp.bfloat16)
        outgoing = shifted(grad_low, "section", -1)
        return ((outgoing, totals), grad_low)

    start_totals = (
        jnp.zeros((4, model_width), jnp.float32),
        jnp.zeros(qkv_weight.shape[1:], jnp.float32),
        jnp.zeros(out_weight.shape[1:], jnp.float32),
        jnp.zeros(up_weight.shape[1:], jnp.float32),
        jnp.zeros(down_weight.shape[1:], jnp.float32),
    )
    (_, totals), grad_lows = lax.scan(
        backward_tick,
        (start_rows, start_totals),
        (back_inputs, grad_padded, tick_valid, back_stash),
    )
    input_grads = jnp.where(first_section, grad_lows[1:], grad_lows[:-1])[None]
    gain_total, qkv_total, out_total, up_total, down_total = totals
    gains_grad = lax.psum_scatter(gain_total, ("dp", "tensor"), scatter_dimension=1, tiled=True)
    qkv_grad, out_grad, up_grad, down_grad = (
        lax.psum_scatter(
            qkv_total.astype(jnp.bfloat16), "dp", scatter_dimension=0, tiled=True
        ).astype(jnp.float32),
        lax.psum_scatter(
            out_total.astype(jnp.bfloat16), "dp", scatter_dimension=1, tiled=True
        ).astype(jnp.float32),
        lax.psum_scatter(
            up_total.astype(jnp.bfloat16), "dp", scatter_dimension=0, tiled=True
        ).astype(jnp.float32),
        lax.psum_scatter(
            down_total.astype(jnp.bfloat16), "dp", scatter_dimension=1, tiled=True
        ).astype(jnp.float32),
    )
    return (
        layer_outputs,
        input_grads,
        gains_grad[None],
        qkv_grad[None],
        out_grad[None],
        up_grad[None],
        down_grad[None],
    )


def rotated(block, cos_rows, sin_rows):
    lane = lax.broadcasted_iota(jnp.int32, block.shape, 1)
    ahead = pltpu.roll(block, 96, 1)
    behind = pltpu.roll(block, 32, 1)
    swapped = jnp.where(lane % 64 < 32, ahead, behind)
    return block * cos_rows + swapped * sin_rows


def dot_nt(left, right):
    return lax.dot_general(
        left, right, (((1,), (1,)), ((), ())), preferred_element_type=jnp.float32
    )


def dot_nn(left, right):
    return jnp.dot(left, right, preferred_element_type=jnp.float32)


def model_weight(owns, others, cols):
    sides = [jnp.concatenate([ref[:, cols] for ref in refs], axis=1) for refs in (owns, others)]
    return jnp.concatenate(sides, axis=0)


def stacked_up(values):
    return jnp.concatenate(values, axis=0)


def edge_masks(core, rows):
    key = lax.broadcasted_iota(jnp.int32, (rows, 2 * rows), 0)
    query = lax.broadcasted_iota(jnp.int32, (rows, 2 * rows), 1)
    mine = query < rows
    place = jnp.where(mine, query + core * rows, query - rows + (1 - core) * rows)
    return (key + core * rows <= place, key + (1 - core) * rows <= place)


def both_sides(value, half, start, stop, axis=0):
    if axis == 0:
        return jnp.concatenate([value[start:stop], value[half + start : half + stop]], axis=0)
    return jnp.concatenate([value[:, start:stop], value[:, half + start : half + stop]], axis=1)


def hidden_scores(scores, masks, tile, step):
    seen = step * tile
    pieces = []
    for side in range(2):
        base = side * (seen + tile)
        if seen:
            pieces.append(scores[base : base + seen])
        pieces.append(jnp.where(masks[side], scores[base + seen : base + seen + tile], -1e30))
    return jnp.concatenate(pieces, axis=0)


def one_head(rows, head):
    lane = lax.broadcasted_iota(jnp.int32, rows.shape, 1)
    return jnp.where(lane // 64 == head, rows, jnp.zeros_like(rows))


def pick_piece(weight, owns, others, cols):
    for j, (own, other) in enumerate(zip(owns, others)):

        @pl.when(pl.program_id(0) == j)
        def _():
            size = own.shape[0]
            weight[:size] = own[:, cols]
            weight[size:] = other[:, cols]


def attend_kernel(pieces, core_ref, cos_ref, sin_ref, own_rows, other_rows, *refs):
    owns, others = refs[:pieces], refs[pieces : 2 * pieces]
    q_ref, k_ref, v_ref, lse_ref, mix_ref, weight = refs[2 * pieces :]
    half = own_rows.shape[0]
    tile = TILE
    pick_piece(weight, owns, others, QKV)
    proj = dot_nn(stacked_up([own_rows[...], other_rows[...]]), weight[...])
    cos_rows, sin_rows = cos_ref[...], sin_ref[...]
    q = (rotated(proj[:, :128], cos_rows, sin_rows) * HEAD_DIM ** (-0.5)).astype(jnp.bfloat16)
    k = rotated(proj[:, 128:256], cos_rows, sin_rows).astype(jnp.bfloat16)
    v32 = proj[:, 256:]
    q_ref[0] = q
    k_ref[0] = k
    v_ref[0] = v32.astype(jnp.bfloat16)
    v_flip = v32.T.astype(jnp.bfloat16)
    masks = edge_masks(core_ref[0], tile)

    def scored(step, head):
        stop = (step + 1) * tile
        q_head = one_head(both_sides(q, half, step * tile, stop), head)
        return hidden_scores(dot_nt(both_sides(k, half, 0, stop), q_head), masks, tile, step)

    units = [(step, head) for step in range(half // tile) for head in range(2)]
    ahead = scored(*units[0])
    outs = []
    for spot, (step, head) in enumerate(units):
        scores = ahead
        if spot + 1 < len(units):
            ahead = scored(*units[spot + 1])
        stop = (step + 1) * tile
        top = jnp.max(scores, axis=0, keepdims=True)
        expos = jnp.exp(scores - top)
        total = jnp.sum(expos, axis=0, keepdims=True)
        lse = top + jnp.log(total)
        lse_ref[0, head : head + 1, step * tile : stop] = lse[:, :tile]
        lse_ref[0, head : head + 1, half + step * tile : half + stop] = lse[:, tile:]
        v_cols = both_sides(v_flip, half, 0, stop, axis=1)
        out = dot_nn(v_cols[64 * head : 64 * head + 64], expos.astype(jnp.bfloat16))
        outs.append(out * (1.0 / total))
        if head == 1:
            mixed = jnp.concatenate(outs, axis=0).T.astype(jnp.bfloat16)
            outs = []
            mix_ref[step * tile : stop, :] = mixed[:tile]
            mix_ref[half + step * tile : half + stop, :] = mixed[tile:]


def attend_back_kernel(pieces, core_ref, cos_ref, sin_ref, own_rows, other_rows, *refs):
    owns, others = refs[:pieces], refs[pieces : 2 * pieces]
    q_ref, k_ref, v_ref, lse_ref, out_ref, weight, dq, dk, dv = refs[2 * pieces :]
    half = own_rows.shape[0]
    tile = TILE
    pick_piece(weight, owns, others, OUT)
    rows = stacked_up([own_rows[...], other_rows[...]])
    d_mixed = dot_nn(rows, weight[...]).astype(jnp.bfloat16)
    q, k, v = q_ref[0], k_ref[0], v_ref[0]
    k_flip = k.astype(jnp.float32).T.astype(jnp.bfloat16)
    masks = edge_masks(core_ref[0], tile)
    steps = half // tile

    def scored(step, head):
        stop = (step + 1) * tile
        q_head = one_head(both_sides(q, half, step * tile, stop), head)
        g_head = one_head(both_sides(d_mixed, half, step * tile, stop), head)
        scores = hidden_scores(dot_nt(both_sides(k, half, 0, stop), q_head), masks, tile, step)
        return q_head, g_head, scores, dot_nt(both_sides(v, half, 0, stop), g_head)

    units = [(step, head) for step in reversed(range(steps)) for head in range(2)]
    ahead = scored(*units[0])
    dq_flips = []
    dk_sum = dv_sum = None
    for spot, (step, head) in enumerate(units):
        q_head, g_head, scores, d_probs = ahead
        if spot + 1 < len(units):
            ahead = scored(*units[spot + 1])
        stop = (step + 1) * tile
        lse = both_sides(lse_ref[0], half, step * tile, stop, axis=1)
        probs = jnp.exp(scores - lse[head : head + 1])
        dots = jnp.sum(probs * d_probs, axis=0, keepdims=True)
        d_scores = (probs * (d_probs - dots)).astype(jnp.bfloat16)
        dv_part = dot_nn(probs.astype(jnp.bfloat16), g_head)
        dk_part = dot_nn(d_scores, q_head)
        k_cols = both_sides(k_flip, half, 0, stop, axis=1)
        dq_flips.append(dot_nn(k_cols[64 * head : 64 * head + 64], d_scores))
        if head == 0:
            dv_sum, dk_sum = dv_part, dk_part
            continue
        dv_sum, dk_sum = dv_sum + dv_part, dk_sum + dk_part
        dq_rows = jnp.concatenate(dq_flips, axis=0).T * HEAD_DIM ** (-0.5)
        dq_flips = []
        dq[step * tile : stop] = dq_rows[:tile]
        dq[half + step * tile : half + stop] = dq_rows[tile:]
        for base, part in ((0, slice(0, stop)), (half, slice(stop, 2 * stop))):
            if step == steps - 1:
                dk[base : base + stop] = dk_sum[part]
                dv[base : base + stop] = dv_sum[part]
            else:
                dk[base : base + stop] += dk_sum[part]
                dv[base : base + stop] += dv_sum[part]
    cos_rows, sin_rows = cos_ref[...], -sin_ref[...]
    out_ref[:, :128] = rotated(dq[...], cos_rows, sin_rows).astype(jnp.bfloat16)
    out_ref[:, 128:256] = rotated(dk[...], cos_rows, sin_rows).astype(jnp.bfloat16)
    out_ref[:, 256:] = dv[...].astype(jnp.bfloat16)


def split_rows(total, own_ref, other_ref):
    half = own_ref.shape[0]
    own_ref[...] = total[:half]
    other_ref[...] = total[half:].astype(jnp.bfloat16)


def to_model_kernel(lefts, pieces, cols, *refs):
    left, refs = jnp.concatenate([ref[...] for ref in refs[:lefts]], axis=1), refs[lefts:]
    weight = model_weight(refs[:pieces], refs[pieces : 2 * pieces], cols)
    split_rows(dot_nt(left, weight), *refs[2 * pieces :])


def mlp_down_kernel(pieces, left_ref, *refs):
    sides = [stacked_up([ref[...] for ref in side]) for side in (refs[:pieces], refs[pieces:-2])]
    split_rows(dot_nn(left_ref[...], jnp.concatenate(sides, axis=1)), *refs[-2:])


def gelu_both(up_act):
    root = math.sqrt(2.0 / math.pi)
    square = up_act * up_act
    rise = 0.5 + 0.5 * jnp.tanh(up_act * (root + root * 0.044715 * square))
    value = up_act * rise
    slope = rise + value * (1.0 - rise) * (2.0 * root + 6.0 * root * 0.044715 * square)
    return value, slope


def mlp_up_kernel(pieces, own_rows, other_rows, *refs):
    owns, others = refs[:pieces], refs[pieces : 2 * pieces]
    gelu_ref, slope_ref = refs[2 * pieces :]
    half = own_rows.shape[0]
    size = owns[0].shape[1]
    step = half // 2
    units = [(j, i) for j in range(pieces) for i in range(4)]

    def product(j, i):
        rows = (own_rows, other_rows)[i // 2][i % 2 * step : (i % 2 + 1) * step]
        return dot_nn(rows, stacked_up([owns[j][...], others[j][...]]))

    ahead = product(*units[0])
    for spot, (j, i) in enumerate(units):
        up_act = ahead
        if spot + 1 < len(units):
            ahead = product(*units[spot + 1])
        value, slope = gelu_both(up_act)
        gelu_ref[i * step : (i + 1) * step, j * size : (j + 1) * size] = value.astype(jnp.bfloat16)
        slope_ref[i * step : (i + 1) * step, j * size : (j + 1) * size] = slope.astype(
            jnp.bfloat16
        )


def mlp_up_back_kernel(pieces, own_rows, other_rows, slope_ref, *refs):
    owns, others = refs[:pieces], refs[pieces : 2 * pieces]
    out_ref, weight, slope, sems = refs[2 * pieces :]
    half = own_rows.shape[1] // 2
    size = owns[0].shape[0]
    order = list(reversed(range(pieces)))
    copies = []
    for j in order:
        sources = (owns[j], others[j], slope_ref.at[:, pl.ds(j * size, size)])
        targets = (
            weight.at[j, :, pl.ds(0, half)],
            weight.at[j, :, pl.ds(half, half)],
            slope.at[:, pl.ds(j * size, size)],
        )
        copies.append(
            [
                pltpu.make_async_copy(source, target, sems.at[j, i])
                for i, (source, target) in enumerate(zip(sources, targets))
            ]
        )
        for copy in copies[-1]:
            copy.start()
    rows = stacked_up([own_rows[...], other_rows[...]])
    for j, arriving in zip(order, copies):
        cols = slice(j * size, (j + 1) * size)
        for copy in arriving:
            copy.wait()
        d_gelu = dot_nt(rows, weight[j])
        out_ref[:, cols] = (d_gelu * slope[:, cols].astype(jnp.float32)).astype(jnp.bfloat16)


def inverse_size(rows):
    return lax.rsqrt(jnp.mean(rows * rows, axis=-1, keepdims=True) + NORM_EPSILON)


def norm_back(rows, gain, grad):
    scale = inverse_size(rows)
    weighted = grad * gain
    inner = jnp.mean(rows * weighted, axis=-1, keepdims=True)
    return scale * weighted - rows * (scale * scale * scale * inner), rows * scale * grad


def folded(rows):
    return jnp.sum(rows.reshape(rows.shape[0] // 8, 8, rows.shape[1]), axis=0)


def wide(ref, spot):
    return ref[spot, :].astype(jnp.float32)


def by_chunks(count, body, sums=0, width=0):
    def one(i, carry):
        more = body(pl.ds(pl.multiple_of(i * CHUNK, CHUNK), CHUNK))
        return tuple(old + folded(new) for old, new in zip(carry, more))

    start = tuple(jnp.zeros((8, width), jnp.float32) for _ in range(sums))
    totals = lax.fori_loop(0, count // CHUNK, one, start)
    return [jnp.sum(total, axis=0, keepdims=True) for total in totals]


def norm_in_kernel(gain_ref, rows_ref, out_ref):
    def body(spot):
        rows = wide(rows_ref, spot)
        out_ref[spot, :] = (rows * inverse_size(rows) * gain_ref[0:1]).astype(jnp.bfloat16)
        return ()

    by_chunks(rows_ref.shape[0], body)


def after_attention_kernel(
    gain_ref, rows_ref, own_ref, other_ref, branch_ref, hidden_ref, out_ref
):
    def body(spot):
        branch = own_ref[spot, :] + wide(other_ref, spot)
        hidden = wide(rows_ref, spot) + branch * inverse_size(branch) * gain_ref[1:2]
        branch_ref[spot, :] = branch
        hidden_ref[spot, :] = hidden
        out_ref[spot, :] = (hidden * inverse_size(hidden) * gain_ref[2:3]).astype(jnp.bfloat16)
        return ()

    by_chunks(rows_ref.shape[0], body)


def after_mlp_kernel(gain_ref, hidden_ref, own_ref, other_ref, branch_ref, out_ref):
    def body(spot):
        branch = own_ref[spot, :] + wide(other_ref, spot)
        branch_ref[spot, :] = branch
        result = hidden_ref[spot, :] + branch * inverse_size(branch) * gain_ref[3:4]
        out_ref[spot, :] = result.astype(jnp.bfloat16)
        return ()

    by_chunks(hidden_ref.shape[0], body)


def into_mlp_back_kernel(gain_ref, grad_ref, branch_ref, out_ref, sum_ref):
    def body(spot):
        d_rows, d_gain = norm_back(branch_ref[spot, :], gain_ref[3:4], wide(grad_ref, spot))
        out_ref[spot, :] = d_rows.astype(jnp.bfloat16)
        return (d_gain,)

    (sum_ref[...],) = by_chunks(grad_ref.shape[0], body, 1, grad_ref.shape[1])


def into_attention_back_kernel(
    gain_ref, grad_ref, own_ref, other_ref, hidden_ref, branch_ref, d_hidden_ref, out_ref, *sums
):
    def body(spot):
        d_rows = own_ref[spot, :] + wide(other_ref, spot)
        d_rows, d_gain = norm_back(hidden_ref[spot, :], gain_ref[2:3], d_rows)
        d_hidden = wide(grad_ref, spot) + d_rows
        d_hidden_ref[spot, :] = d_hidden
        d_rows, d_first = norm_back(branch_ref[spot, :], gain_ref[1:2], d_hidden)
        out_ref[spot, :] = d_rows.astype(jnp.bfloat16)
        return (d_first, d_gain)

    totals = by_chunks(grad_ref.shape[0], body, 2, grad_ref.shape[1])
    sums[0][...], sums[1][...] = totals


def out_of_layer_kernel(gain_ref, rows_ref, own_ref, other_ref, d_hidden_ref, out_ref, sum_ref):
    def body(spot):
        d_rows = own_ref[spot, :] + wide(other_ref, spot)
        d_rows, d_gain = norm_back(wide(rows_ref, spot), gain_ref[0:1], d_rows)
        out_ref[spot, :] = (d_hidden_ref[spot, :] + d_rows).astype(jnp.bfloat16)
        return (d_gain,)

    (sum_ref[...],) = by_chunks(rows_ref.shape[0], body, 1, rows_ref.shape[1])


def work(flops, arrays):
    size = sum(math.prod(array.shape) * jnp.dtype(array.dtype).itemsize for array in arrays)
    return pl.CostEstimate(flops=flops, bytes_accessed=size, transcendentals=0)


def far(array):
    return pltpu.with_memory_space_constraint(array, pltpu.HBM)


def without(kernel, first, count):
    return lambda *refs: kernel(*refs[:first], *refs[first + count :])


def on_chip(kernel, name, outs, *operands, limit=ROWS_VMEM, flops=0, waits=()):
    shapes = [jax.ShapeDtypeStruct(shape, dtype) for shape, dtype in outs]
    space = pl.BlockSpec(memory_space=pltpu.VMEM)
    return pl.pallas_call(
        without(kernel, len(operands), len(waits)),
        in_specs=[space] * len(operands) + [pl.BlockSpec(memory_space=pl.ANY)] * len(waits),
        out_specs=[space] * len(outs),
        out_shape=shapes,
        compiler_params=pltpu.CompilerParams(vmem_limit_bytes=limit),
        cost_estimate=work(flops, (*operands, *shapes)),
        name=name,
    )(*operands, *map(far, waits))


def whole_block(array):
    return pl.BlockSpec(array.shape, lambda j: (0,) * array.ndim)


def by_pairs(kernel, name, core, operands, pieces, blocks, outs, scratch, flops, waits):
    shapes = [jax.ShapeDtypeStruct(shape, dtype) for shape, dtype, _ in outs]
    taken = 1 + len(operands) + 2 * len(pieces[0]) + len(blocks)
    return pl.pallas_call(
        without(functools.partial(kernel, len(pieces[0])), taken, len(waits)),
        grid=(len(pieces[0]),),
        in_specs=[pl.BlockSpec(memory_space=pltpu.SMEM)]
        + [whole_block(array) for array in (*operands, *pieces[0], *pieces[1])]
        + [spec for _, spec in blocks]
        + [pl.BlockSpec(memory_space=pl.ANY)] * len(waits),
        out_specs=[spec for _, _, spec in outs],
        out_shape=shapes,
        scratch_shapes=scratch,
        compiler_params=pltpu.CompilerParams(vmem_limit_bytes=KERNEL_VMEM),
        cost_estimate=work(flops, (*operands, *pieces[0], *pieces[1], *shapes)),
        name=name,
    )(core, *operands, *pieces[0], *pieces[1], *[array for array, _ in blocks], *map(far, waits))


def mlp_up_back(rows, slope, pieces, waits):
    length, units = slope.shape
    unit, half = pieces[0][0].shape
    count = len(pieces[0])
    every, space = pl.BlockSpec(memory_space=pl.ANY), pl.BlockSpec(memory_space=pltpu.VMEM)
    return pl.pallas_call(
        without(functools.partial(mlp_up_back_kernel, count), 3 + 2 * count, len(waits)),
        in_specs=[space] * 2 + [every] * (1 + 2 * count + len(waits)),
        out_specs=space,
        out_shape=jax.ShapeDtypeStruct((length, units), jnp.bfloat16),
        scratch_shapes=[
            pltpu.VMEM((count, unit, 2 * half), jnp.bfloat16),
            pltpu.VMEM((length, units), jnp.bfloat16),
            pltpu.SemaphoreType.DMA((count, 3)),
        ],
        compiler_params=pltpu.CompilerParams(vmem_limit_bytes=KERNEL_VMEM),
        name="mlp_up_back",
    )(*rows, *map(far, (slope, *pieces[0], *pieces[1], *waits)))


def attend(core, tables, rows, pieces, waits):
    half, features = rows[0].shape
    length, count = 2 * half, len(pieces[0])
    lanes = ((count, length, 128), jnp.bfloat16, pl.BlockSpec((1, length, 128), lambda j: (j, 0, 0)))
    lse = ((count, 2, length), jnp.float32, pl.BlockSpec((1, 2, length), lambda j: (j, 0, 0)))
    mixed = ((length, count * 128), jnp.bfloat16, pl.BlockSpec((length, 128), lambda j: (0, j)))
    return by_pairs(
        attend_kernel,
        "attend",
        core,
        (*tables, *rows),
        pieces,
        (),
        (lanes, lanes, lanes, lse, mixed),
        [pltpu.VMEM((features, 384), jnp.bfloat16)],
        count * length * (2 * features * 384 + 2 * PAIR_WORK * length),
        waits,
    )


def attend_back(core, tables, rows, pieces, base, waits, q, k, v, lse):
    half, features = rows[0].shape
    length, count = 2 * half, len(pieces[0])
    lanes = pl.BlockSpec((1, length, 128), lambda j: (base + j, 0, 0))
    lse_spec = pl.BlockSpec((1, 2, length), lambda j: (base + j, 0, 0))
    out = ((length, count * 384), jnp.bfloat16, pl.BlockSpec((length, 384), lambda j: (0, j)))
    return by_pairs(
        attend_back_kernel,
        "attend_back",
        core,
        (*tables, *rows),
        pieces,
        ((q, lanes), (k, lanes), (v, lanes), (lse, lse_spec)),
        (out,),
        [pltpu.VMEM((features, 128), jnp.bfloat16)] + [pltpu.VMEM((length, 128), jnp.float32)] * 3,
        count * length * (2 * features * 128 + 5 * PAIR_WORK * length),
        waits,
    )[0]


def exchanged(parts):
    return parts[0], flip_pairs(parts[1], 1)


def model_rows(kernel, name, lefts, pieces, waits=()):
    length, width = lefts[0].shape[0], 2 * MODEL_HALF
    outs = (((length // 2, width), jnp.float32), ((length // 2, width), jnp.bfloat16))
    hidden = sum(left.shape[1] for left in lefts)
    more = {"limit": KERNEL_VMEM, "flops": 2 * length * width * hidden, "waits": waits}
    return exchanged(on_chip(kernel, name, outs, *lefts, *pieces[0], *pieces[1], **more))


def flip_pairs(block, distance):
    size = lax.axis_size("dp")
    return lax.ppermute(block, "dp", [(i, i ^ distance) for i in range(size)])


def passed_on(block, step):
    size = lax.axis_size("tensor")
    return lax.ppermute(block, "tensor", [(i, (i + step) % size) for i in range(size)])


def dot_tn(left, right):
    return lax.dot_general(
        left, right, (((0,), (0,)), ((), ())), preferred_element_type=jnp.float32
    )


def fetch(first_ref, zeros, ones, buffers, sems):
    for section, sources in enumerate((zeros, ones)):

        @pl.when(first_ref[0] == section)
        def _():
            for i, (source, buffer) in enumerate(zip(sources, buffers)):
                pltpu.make_async_copy(source, buffer, sems.at[i]).start()

    def arrived(*places):
        for i in places:
            pltpu.make_async_copy(zeros[i], buffers[i], sems.at[i]).wait()

    return arrived


def mlp_grads_kernel(base, section_ref, *refs):
    (own_one, other_one, own_two, other_two), (rows, d_up, gelu, d_down, sems) = refs[12:16], refs[16:]
    half, size = own_one.shape[0] // 2, own_one.shape[1]
    cols = pl.ds(base * size, 2 * size)

    def parts(own_rows, other_rows, d_up_ref, gelu_ref, own_grad, other_grad):
        whole = (d_up_ref.at[:, cols], gelu_ref.at[:, cols])
        return (own_rows, other_rows, *whole, own_grad, other_grad)

    count = refs[0].shape[0]
    buffers = (
        rows.at[pl.ds(0, count)],
        rows.at[pl.ds(count, count)],
        d_up,
        gelu,
        d_down.at[pl.ds(0, count)],
        d_down.at[pl.ds(count, count)],
    )
    arrived = fetch(section_ref, parts(*refs[:6]), parts(*refs[6:12]), buffers, sems)
    for j, own, other in ((1, own_two, other_two), (0, own_one, other_one)):
        cols = slice(j * size, (j + 1) * size)
        if j == 1:
            arrived(0, 1, 2)
        up = dot_tn(rows[...], d_up[:, cols])
        own[:half] = up[:half]
        other[:half] = up[half:].astype(jnp.bfloat16)
        if j == 1:
            arrived(3, 4, 5)
        down = dot_tn(gelu[:, cols], d_down[...])
        own[half:] = down[:, :half]
        other[half:] = down[:, half:].astype(jnp.bfloat16)


def attn_grads_kernel(base, section_ref, *refs):
    (own_one, other_one, own_two, other_two), (rows, d_qkv, mixed, d_attn, sems) = refs[12:16], refs[16:]
    half, size = own_one.shape[0], d_qkv.shape[1] // 2
    count = refs[0].shape[0]
    cols = pl.ds(base * 128, 256)

    def parts(own_rows, other_rows, d_qkv_ref, mixed_ref, own_grad, other_grad):
        return (own_rows, other_rows, d_qkv_ref, mixed_ref.at[:, cols], own_grad, other_grad)

    buffers = (
        rows.at[pl.ds(0, count)],
        rows.at[pl.ds(count, count)],
        d_qkv,
        mixed,
        d_attn.at[pl.ds(0, count)],
        d_attn.at[pl.ds(count, count)],
    )
    arrived = fetch(section_ref, parts(*refs[:6]), parts(*refs[6:12]), buffers, sems)
    for j, own, other in ((1, own_two, other_two), (0, own_one, other_one)):
        if j == 1:
            arrived(0, 1, 2)
        qkv = dot_tn(rows[...], d_qkv[:, j * size : (j + 1) * size])
        if j == 1:
            arrived(3, 4, 5)
        out = dot_tn(d_attn[...], mixed[:, j * 128 : (j + 1) * 128])
        own[:, :size] = qkv[:half]
        own[:, size:] = out[:half]
        other[:, :size] = qkv[half:].astype(jnp.bfloat16)
        other[:, size:] = out[half:].astype(jnp.bfloat16)


def weight_grads(kernel, name, base, section, zeros, ones, shape, columns, waits=()):
    length = 2 * zeros[0].shape[0]
    width = zeros[0].shape[1]
    every = pl.BlockSpec(memory_space=pl.ANY)
    space = pl.BlockSpec(memory_space=pltpu.VMEM)
    arrays = (*zeros, *ones)
    first, second, third, fourth = pl.pallas_call(
        without(functools.partial(kernel, base), 1 + len(arrays), len(waits)),
        in_specs=[pl.BlockSpec(memory_space=pltpu.SMEM)] + [every] * (len(arrays) + len(waits)),
        out_specs=[space] * 4,
        out_shape=[
            jax.ShapeDtypeStruct(shape, jnp.float32),
            jax.ShapeDtypeStruct(shape, jnp.bfloat16),
        ]
        * 2,
        scratch_shapes=[
            pltpu.VMEM((length, width), jnp.bfloat16),
            pltpu.VMEM((length, columns[0]), jnp.bfloat16),
            pltpu.VMEM((length, columns[1]), jnp.bfloat16),
            pltpu.VMEM((length, width), jnp.bfloat16),
            pltpu.SemaphoreType.DMA((6,)),
        ],
        compiler_params=pltpu.CompilerParams(vmem_limit_bytes=KERNEL_VMEM),
        name=name,
    )(section, *map(far, (*arrays, *waits)))
    return [(first, flip_pairs(second, 2)), (third, flip_pairs(fourth, 2))]


def moved_kernel(own_ref, other_ref, *refs):
    out_ref = refs[-1]

    def body(i, carry):
        spot = pl.ds(pl.multiple_of(i * CHUNK, CHUNK), CHUNK)
        total = own_ref[spot, :]
        for ref in (other_ref, *refs[:-1]):
            total = total + wide(ref, spot)
        out_ref[spot, :] = total.astype(jnp.bfloat16)
        return carry

    lax.fori_loop(0, own_ref.shape[0] // CHUNK, body, 0)


def gates_kernel(up_ref, down_ref, up_out, down_out):
    up_out[...] = up_ref[...]
    down_out[...] = down_ref[...]


def gate_kernel(piece_ref, out_ref):
    out_ref[...] = piece_ref[...]


def mlp_sum_kernel(core_ref, own_ref, other_ref, moved_ref, up_keep, down_keep, up_send, down_send):
    half = own_ref.shape[0] // 2
    size = up_keep.shape[0]

    def total(rows, cols):
        more = other_ref[rows, cols].astype(jnp.float32) + moved_ref[rows, cols].astype(jnp.float32)
        return own_ref[rows, cols] + more

    for core in range(2):

        @pl.when(core_ref[0] == core)
        def _():
            for place, up, down in ((core, up_keep, down_keep), (1 - core, up_send, down_send)):
                spot = slice(place * size, (place + 1) * size)
                up[...] = total(spot, slice(None))
                down[...] = total(slice(half, None), spot)


def mlp_join_kernel(core_ref, up_keep, down_keep, up_sent, down_sent, up_out, down_out):
    size = up_keep.shape[1]
    for core in range(2):

        @pl.when(core_ref[0] == core)
        def _():
            places = ((core, up_keep, down_keep), (1 - core, up_sent, down_sent))
            for place, up, down in places:
                spot = slice(place * size, (place + 1) * size)
                up_out[:, spot] = up[...]
                down_out[spot] = down[...]


def pick_kernel(core_ref, rows_ref, keep_ref, send_ref):
    count = keep_ref.shape[0]
    keep_ref[...] = rows_ref[pl.ds(core_ref[0] * count, count)]
    send_ref[...] = rows_ref[pl.ds((1 - core_ref[0]) * count, count)]


def in_order_kernel(core_ref, keep_ref, sent_ref, out_ref):
    out_ref[:, pl.ds(core_ref[0], 1)] = keep_ref[...][:, None]
    out_ref[:, pl.ds(1 - core_ref[0], 1)] = sent_ref[...][:, None]


def with_core(kernel, name, core, outs, *operands, waits=()):
    space = pl.BlockSpec(memory_space=pltpu.VMEM)
    return pl.pallas_call(
        without(kernel, 1 + len(operands), len(waits)),
        in_specs=[pl.BlockSpec(memory_space=pltpu.SMEM)]
        + [space] * len(operands)
        + [pl.BlockSpec(memory_space=pl.ANY)] * len(waits),
        out_specs=[space] * len(outs),
        out_shape=[jax.ShapeDtypeStruct(shape, dtype) for shape, dtype in outs],
        compiler_params=pltpu.CompilerParams(vmem_limit_bytes=ROWS_VMEM),
        name=name,
    )(core, *operands, *map(far, waits))


def last_sum_kernel(core_ref, own_ref, other_ref, moved_ref, keep_ref, send_ref):
    rows = keep_ref.shape[0]

    def total(block):
        spot = pl.ds(pl.multiple_of(block * rows, rows), rows)
        return own_ref[spot, :] + wide(other_ref, spot) + wide(moved_ref, spot)

    keep_ref[...] = total(core_ref[0])
    send_ref[...] = total(1 - core_ref[0])


def joined_kernel(spots, core_ref, keep_ref, sent_ref, column_ref, row_ref):
    size = row_ref.shape[0] // 2
    for core in range(2):

        @pl.when(core_ref[0] == core)
        def _():
            for place, source in ((core, keep_ref), (1 - core, sent_ref)):
                for start, stop, to in spots:
                    step = stop - start
                    column_ref[:, to + place * step : to + (place + 1) * step] = source[:, start:stop]
                row_ref[place * size : (place + 1) * size] = source[:, spots[-1][1] :].T


def per_chip(
    inputs,
    out_cotangent,
    group_ids,
    group_weights,
    gains,
    qkv_weight,
    out_weight,
    up_weight,
    down_weight,
):
    micro, row_count, width = inputs.shape
    tensor = lax.axis_size("tensor")
    part = row_count // 2
    wide_half = width // 2
    length = tensor * row_count
    half = length // 2
    first = lax.axis_index("section") == 0
    place = lax.axis_index("dp")
    core = place % 2
    upper = place // 2 % 2
    core_zero = core == 0
    low_half = upper == 0

    def ordered(mine, other):
        return jnp.where(core_zero, mine, other), jnp.where(core_zero, other, mine)

    def own_first(values):
        return jnp.where(low_half, values, jnp.roll(values, wide_half, axis=-1))

    def both_rows(own):
        return own, flip_pairs(own, 1)

    def to_chip(block):
        split = block.reshape((micro, 2, part) + block.shape[2:])
        mine = lax.dynamic_index_in_dim(split, core, 1, keepdims=False)
        other = lax.dynamic_index_in_dim(split, 1 - core, 1, keepdims=False)
        return lax.all_to_all(
            jnp.concatenate(ordered(mine, flip_pairs(other, 1))), "tensor", 0, 0, tiled=True
        )

    def from_chip(spread_out, waits=()):
        piece = ((micro, part, width), jnp.bfloat16)
        keep, send = with_core(
            pick_kernel, "pick", core_word, (piece, piece), spread_out, waits=waits
        )
        outs = (((micro, 2, part, width), jnp.bfloat16),)
        (rows,) = with_core(
            in_order_kernel, "in_order", core_word, outs, keep, flip_pairs(send, 1)
        )
        return rows.reshape(micro, row_count, width)

    def columns(local):
        size = local.shape[-1] // 2
        mid = (0,) * (local.ndim - 2)
        piece = lax.dynamic_slice(
            local,
            (wide_half * upper, *mid, size * core),
            (wide_half, *local.shape[1:-1], size),
        )
        return piece.reshape(wide_half, -1)

    def rows(local):
        size = local.shape[0] // 2
        return lax.dynamic_slice(local, (size * core, wide_half * upper), (size, wide_half))

    core_word = core.astype(jnp.int32).reshape(1)
    attn_piece = jnp.concatenate([columns(qkv_weight[0]), rows(out_weight[0]).T], axis=1)

    def spread(piece):
        pieces = [piece]
        for _ in range(tensor - 1):
            pieces.append(passed_on(pieces[-1], 1))
        return pieces

    attn_own = spread(attn_piece)
    attn_other = [flip_pairs(piece, 2) for piece in attn_own]
    up_piece, down_piece = columns(up_weight[0]), rows(down_weight[0])
    up_other, down_other = [flip_pairs(up_piece, 2)], [flip_pairs(down_piece, 2)]
    outs = tuple((piece.shape, piece.dtype) for piece in (up_piece, down_piece))
    up_piece, down_piece = on_chip(
        gates_kernel, "gate", outs, up_piece, down_piece, waits=(attn_own[2], attn_other[0])
    )
    up_own, down_own = spread(up_piece), spread(down_piece)
    up_other += [flip_pairs(piece, 2) for piece in up_own[1:]]
    down_other += [flip_pairs(piece, 2) for piece in down_own[1:]]
    w_attn, w_up, w_down = (attn_own, attn_other), (up_own, up_other), (down_own, down_other)
    unit = up_piece.shape[1]
    units = tensor * unit

    group_count = group_weights.shape[0]
    matches = group_ids[..., None] == jnp.arange(group_count, dtype=jnp.int32)
    row_scale = jnp.sum(jnp.where(matches, group_weights, 0.0), axis=-1)
    weighted = (out_cotangent.astype(jnp.float32) * row_scale[..., None]).astype(jnp.bfloat16)
    start = to_chip(own_first(jnp.where(first, inputs, weighted))).reshape(half, width)
    gain = own_first(gains[0])

    turns = jnp.arange(half, dtype=jnp.int32)
    turns = turns // part * row_count + turns % part
    positions = jnp.concatenate([turns + core * part, turns + (1 - core) * part])
    freqs = 10000.0 ** (-2.0 * jnp.arange(HEAD_DIM // 2, dtype=jnp.float32) / HEAD_DIM)
    angles = positions.astype(jnp.float32)[:, None] * freqs[None, :]
    cos_part, sin_part = jnp.cos(angles), jnp.sin(angles)
    tables = (
        jnp.concatenate([cos_part] * 4, axis=1),
        jnp.concatenate([-sin_part, sin_part] * 2, axis=1),
    )
    row32, row16 = ((half, width), jnp.float32), ((half, width), jnp.bfloat16)
    unit16 = ((length, units), jnp.bfloat16)
    sum32 = ((1, width), jnp.float32)
    mlp_cost = {"limit": KERNEL_VMEM, "flops": 2 * length * width * units}
    every = slice(None)

    def model_kernel(cols, lefts=1):
        return functools.partial(to_model_kernel, lefts, tensor, cols)

    down_kernel = functools.partial(mlp_down_kernel, tensor)

    def forward(layer_input, waits):
        attn_in = both_rows(
            on_chip(norm_in_kernel, "norm_in", (row16,), gain, layer_input, waits=waits[0])[0]
        )
        *heads, mixed = attend(core_word, tables, attn_in, w_attn, waits[1])
        parts = model_rows(model_kernel(OUT), "attn_out", [mixed], w_attn, waits[2])
        operands = (gain, layer_input, *parts)
        branch, hidden, mlp_in = on_chip(
            after_attention_kernel, "after_attn", (row32, row32, row16), *operands, waits=waits[3]
        )
        mlp_in = both_rows(mlp_in)
        kernel = functools.partial(mlp_up_kernel, tensor)
        operands = (*mlp_in, *w_up[0], *w_up[1])
        gelu_out, slope = on_chip(kernel, "mlp_up", (unit16, unit16), *operands, **mlp_cost)
        parts = model_rows(down_kernel, "mlp_down", [gelu_out], w_down)
        mlp_branch, result = on_chip(
            after_mlp_kernel, "after_mlp", (row32, row16), gain, hidden, *parts
        )
        saved = (layer_input, heads, branch, hidden, slope, mlp_branch)
        return result, saved, (attn_in, mixed, mlp_in, gelu_out)

    def backward(grad, saved, hook, late=()):
        layer_input, heads, branch, hidden, slope, mlp_branch = saved
        operands = (gain, grad, mlp_branch)
        d_down, sum_three = on_chip(
            into_mlp_back_kernel, "into_mlp_back", (row16, sum32), *operands
        )
        d_down = both_rows(d_down)
        d_up = mlp_up_back(d_down, slope, w_down, late)
        waits = hook(d_down, d_up)
        parts = model_rows(model_kernel(every), "mlp_back", [d_up], w_up, waits)
        waits = hook()
        operands = (gain, grad, *parts, hidden, branch)
        outs = (row32, row16, sum32, sum32)
        d_hidden, d_attn, sum_one, sum_two = on_chip(
            into_attention_back_kernel, "into_attn_back", outs, *operands, waits=waits
        )
        d_attn = both_rows(d_attn)
        waits = hook(d_attn)
        d_qkv = []
        for base in reversed(range(0, tensor, 2)):
            some = [side[base : base + 2] for side in w_attn]
            now = attend_back(core_word, tables, d_attn, some, base, waits, *heads)
            d_qkv.insert(0, now)
            waits = hook(now)
        parts = model_rows(model_kernel(QKV, 2), "attn_back", d_qkv, w_attn, waits)
        operands = (gain, layer_input, *parts, d_hidden)
        d_input, sum_zero = on_chip(
            out_of_layer_kernel, "out_of_layer", (row16, sum32), *operands, waits=hook()
        )
        sums = jnp.concatenate([sum_zero, sum_one, sum_two, sum_three])
        return d_input, (d_qkv, d_attn, d_up, d_down), sums

    low_zero, saved_zero, lefts_zero = forward(
        start,
        (
            (up_piece, up_other[0], down_other[0]),
            (up_own[1], down_own[1]),
            (up_own[2], down_own[2], up_other[1], down_other[1]),
            (up_own[3], down_own[3], up_other[2], down_other[2]),
        ),
    )
    low_one, saved_one, lefts_one = forward(shifted(low_zero, "section", 1), ((),) * 4)
    grad_one, rights_one, gain_one = backward(start, saved_one, lambda *new: ())
    received = shifted(grad_one, "section", -1)

    lows = lax.optimization_barrier((low_zero, low_one, grad_one))[:2]
    lows = own_first(jnp.where(first, *lows)).reshape(tensor, part, width)
    lows = lax.all_to_all(lows, "tensor", 0, 0, tiled=True)

    section_word = lax.axis_index("section").astype(jnp.int32).reshape(1)

    def mlp_leaves(base, waits=()):
        zeros = (*lefts_zero[2], d_up, lefts_zero[3], *d_down)
        ones = (*lefts_one[2], rights_one[2], lefts_one[3], *rights_one[3])
        mlp_sums[base : base + 2] = weight_grads(
            mlp_grads_kernel,
            "mlp_grads",
            base,
            section_word,
            zeros,
            ones,
            (wide_half + unit, unit),
            (2 * unit, 2 * unit),
            waits,
        )

    def attn_leaves(base, d_qkv, waits):
        zeros = (*lefts_zero[0], d_qkv, lefts_zero[1], *d_attn)
        ones = (*lefts_one[0], rights_one[0][base // 2], lefts_one[1], *rights_one[1])
        attn_sums[base : base + 2] = weight_grads(
            attn_grads_kernel,
            "attn_grads",
            base,
            section_word,
            zeros,
            ones,
            (wide_half, 512),
            (768, 256),
            waits,
        )

    def moves_on(piece, *moved, waits=()):
        outs = ((piece[1].shape, jnp.bfloat16),)
        (total,) = on_chip(moved_kernel, "moved", outs, *piece, *moved, waits=waits)
        return total, passed_on(total, -1)

    mlp_sums, attn_sums = [None] * tensor, [None] * tensor
    mlp_moves, attn_moves = [None] * tensor, [None] * tensor
    hooks = iter(range(6))

    def hook(*new):
        nonlocal d_down, d_up, d_attn, outputs
        turn = next(hooks)
        if turn == 0:
            d_down, d_up = new
            mlp_leaves(2)
            return (mlp_sums[3][0],)
        if turn == 1:
            return ()
        if turn == 2:
            (d_attn,) = new
            outputs = from_chip(lows, d_attn[:1])
            total, mlp_moves[3] = moves_on(mlp_sums[3], waits=(outputs,))
            mlp_leaves(0, (total,))
            return (mlp_sums[1][0],)
        if turn == 3:
            total, mlp_moves[2] = moves_on(mlp_sums[2], mlp_moves[3], waits=new)
            attn_leaves(2, new[0], (total,))
            return (mlp_sums[2][1], mlp_moves[3], attn_sums[3][0])
        if turn == 4:
            total, mlp_moves[1] = moves_on(mlp_sums[1], mlp_moves[2], waits=new)
            attn_leaves(0, new[0], (total,))
            total, attn_moves[3] = moves_on(attn_sums[3], waits=attn_sums[1][:1])
            return (total, mlp_moves[1], mlp_sums[0][1])
        return attn_sums[2][1:]

    d_down = d_up = d_attn = outputs = None
    grad_zero, rights_zero, gain_zero = backward(received, saved_zero, hook, (lows,))
    grads = own_first(jnp.where(first, grad_zero, grad_one)).reshape(tensor, part, width)
    grads = lax.all_to_all(grads, "tensor", 0, 0, tiled=True)

    block32 = ((wide_half // 2, unit), jnp.float32)
    down32 = ((unit, wide_half // 2), jnp.float32)
    up_keep, down_keep, up_send, down_send = with_core(
        mlp_sum_kernel,
        "mlp_sum",
        core_word,
        (block32, down32, block32, down32),
        *mlp_sums[0],
        mlp_moves[1],
    )
    outs = (
        ((wide_half // 2, 2 * unit), jnp.float32),
        ((2 * unit, wide_half // 2), jnp.float32),
    )
    sent = flip_pairs(up_send, 1), flip_pairs(down_send, 1)
    up_grad, down_grad = with_core(
        mlp_join_kernel, "mlp_join", core_word, outs, up_keep, down_keep, *sent
    )
    total, attn_moves[2] = moves_on(attn_sums[2], attn_moves[3], waits=(grad_zero, attn_sums[1][1]))
    waits = (up_grad, attn_sums[0][1], grads)
    last, attn_moves[1] = moves_on(attn_sums[1], attn_moves[2], waits=waits)
    grads = from_chip(grads, (last,))
    gain_total = own_first(jnp.where(first, gain_zero, gain_one))
    count = tensor * lax.axis_size("dp")
    gain_parts = gain_total.reshape(4, count, width // count).swapaxes(0, 1)
    outs = ((gain_parts.shape, gain_parts.dtype),)
    (gain_parts,) = on_chip(gate_kernel, "gate", outs, gain_parts, waits=(last,))
    gain_parts = lax.all_to_all(gain_parts, ("dp", "tensor"), 0, 0, tiled=True)
    gains_grad = jnp.sum(gain_parts, axis=0)
    outs = (((wide_half // 2, 512), jnp.float32),) * 2
    keep, send = with_core(
        last_sum_kernel,
        "attn_sum",
        core_word,
        outs,
        *attn_sums[0],
        attn_moves[1],
        waits=(grads, outputs, gains_grad),
    )
    spots = tuple((i * 128, (i + 1) * 128, i * 256) for i in range(3))
    outs = (((wide_half // 2, 768), jnp.float32), ((256, wide_half // 2), jnp.float32))
    kernel = functools.partial(joined_kernel, spots)
    qkv_grad, out_grad = with_core(
        kernel, "attn_join", core_word, outs, keep, flip_pairs(send, 1)
    )
    qkv_grad = qkv_grad.reshape(wide_half // 2, 3, -1)

    return (
        outputs[None],
        grads[None],
        gains_grad[None],
        qkv_grad[None],
        out_grad[None],
        up_grad[None],
        down_grad[None],
    )


def takes_chips(sizes):
    return sizes["section"] == 2 and sizes["dp"] == 4 and sizes["tensor"] == 4


def solution(mesh):
    placed = (
        P("dp", "tensor", None),
        P("dp", "tensor", None),
        P("dp", "tensor"),
        P(),
        P("section", None, None),
        P("section", None, None, "tensor"),
        P("section", "tensor", None),
        P("section", None, "tensor"),
        P("section", "tensor", None),
    )
    body = per_chip if takes_chips(dict(mesh.shape)) else per_device
    return jax.shard_map(
        body,
        mesh=mesh,
        in_specs=placed,
        out_specs=(
            P("section", "dp", "tensor", None),
            P("section", "dp", "tensor", None),
            P("section", None, ("dp", "tensor")),
            P("section", "dp", None, "tensor"),
            P("section", "tensor", "dp"),
            P("section", "dp", "tensor"),
            P("section", "tensor", "dp"),
        ),
        check_vma=False,
    )
```

```python
import functools
import math

import jax
import jax.numpy as jnp
from jax import lax
from jax.experimental import pallas as pl
from jax.experimental.pallas import tpu as pltpu
from jax.sharding import PartitionSpec as P

HEAD_DIM = 64


NORM_EPSILON = 1e-06
TILE = 128
PAIR_WORK = 1024
MODEL_HALF = 512
QKV = slice(0, 384)
OUT = slice(384, 512)
CHUNK = 32
KERNEL_VMEM = 20 << 20
ROWS_VMEM = 3 << 20


def shifted(block, axis, distance):
    devices = range(lax.axis_size(axis))
    route = [(i - distance, i) for i in devices if i - distance in devices]
    return lax.ppermute(block, axis, route)


def norm_rows(vector, weight_gain):
    return (
        vector
        * lax.rsqrt(jnp.mean(vector * vector, axis=-1, keepdims=True) + NORM_EPSILON)
        * weight_gain
    )


def rotary_tables(seq_len, head_width):
    half_width = head_width // 2
    freqs = 10000.0 ** (-2.0 * jnp.arange(half_width, dtype=jnp.float32) / head_width)
    angles = jnp.arange(seq_len, dtype=jnp.float32)[:, None] * freqs[None, :]
    return (jnp.cos(angles), jnp.sin(angles))


def rotate(vector, cos_table, sin_table):
    first_half, second_half = jnp.split(vector, 2, axis=-1)
    cos_part = cos_table[:, None, :]
    sin_part = sin_table[:, None, :]
    return jnp.concatenate(
        [
            first_half * cos_part - second_half * sin_part,
            second_half * cos_part + first_half * sin_part,
        ],
        axis=-1,
    )


def contract(left_rows, right_rows):
    return lax.dot_general(
        left_rows, right_rows, (((0,), (0,)), ((), ())), preferred_element_type=jnp.float32
    )


def gather_rows(row_values, weight):

    def project(shard_rows, offset):
        return (shard_rows, jnp.dot(shard_rows, weight, preferred_element_type=jnp.float32))

    return project(lax.all_gather(row_values, "tensor", axis=0, tiled=True), jnp.int32(0))


def scatter_rows(row_values, weight, row_count):

    def partial_term(offset, span):
        return jnp.dot(row_values, weight, preferred_element_type=jnp.float32)

    return lax.psum_scatter(
        partial_term(jnp.int32(0), lax.axis_size("tensor") * row_count),
        "tensor",
        scatter_dimension=0,
        tiled=True,
    )


def gather_grads(row_values, weight):

    def project(shard_rows, offset):
        return (shard_rows, jnp.dot(shard_rows, weight.T, preferred_element_type=jnp.float32))

    return project(lax.all_gather(row_values, "tensor", axis=0, tiled=True), jnp.int32(0))


def scatter_grads(row_values, weight, row_count):

    def partial_term(offset, span):
        return jnp.dot(row_values, weight.T, preferred_element_type=jnp.float32)

    return lax.psum_scatter(
        partial_term(jnp.int32(0), lax.axis_size("tensor") * row_count),
        "tensor",
        scatter_dimension=0,
        tiled=True,
    )


def attention_probs(queries, key_rows):
    scores = jnp.einsum(
        "qhd,khd->hqk", queries, key_rows, preferred_element_type=jnp.float32
    ) * HEAD_DIM ** (-0.5)
    length = queries.shape[0]
    positions = jnp.arange(length, dtype=jnp.int32)
    causal = positions[:, None] >= positions[None, :]
    scores = jnp.where(causal[None], scores, -1e30)
    expos = jnp.exp(scores - jnp.max(scores, axis=-1, keepdims=True))
    return expos / jnp.sum(expos, axis=-1, keepdims=True)


def layer_forward(layer_input, weights):
    gains, w_qkv, w_out, w_up, w_down = weights
    row_count, model_width = layer_input.shape
    attn_in = norm_rows(layer_input, gains[0]).astype(jnp.bfloat16)
    gathered_a, qkv = gather_rows(attn_in, w_qkv.reshape(model_width, -1))
    length = qkv.shape[0]
    head_count = w_qkv.shape[2] // HEAD_DIM
    qkv = qkv.reshape(length, 3, head_count, HEAD_DIM)
    cos_table, sin_table = rotary_tables(length, HEAD_DIM)
    queries = rotate(qkv[:, 0], cos_table, sin_table).astype(jnp.bfloat16)
    key_rows = rotate(qkv[:, 1], cos_table, sin_table).astype(jnp.bfloat16)
    values = qkv[:, 2].astype(jnp.bfloat16)
    attn_probs = attention_probs(queries, key_rows).astype(jnp.bfloat16)
    mixed = jnp.einsum("hqk,khd->qhd", attn_probs, values, preferred_element_type=jnp.float32)
    mixed = mixed.reshape(length, -1).astype(jnp.bfloat16)
    attn_branch = scatter_rows(mixed, w_out, row_count)
    hidden = layer_input + norm_rows(attn_branch, gains[1])
    mlp_in = norm_rows(hidden, gains[2]).astype(jnp.bfloat16)
    gathered_c, up_act = gather_rows(mlp_in, w_up)
    gelu_out = jax.nn.gelu(up_act, approximate=True).astype(jnp.bfloat16)
    down_branch = scatter_rows(gelu_out, w_down, row_count)
    result = hidden + norm_rows(down_branch, gains[3])
    kept_values = (
        gathered_a,
        queries,
        key_rows,
        values,
        mixed,
        attn_branch,
        hidden,
        gathered_c,
        up_act,
        gelu_out,
        down_branch,
    )
    return (result, kept_values)


def layer_backward(layer_input, grad_result, kept_values, weights):
    gains, w_qkv, w_out, w_up, w_down = weights
    (
        gathered_a,
        queries,
        key_rows,
        values,
        mixed,
        attn_branch,
        hidden,
        gathered_c,
        up_act,
        gelu_out,
        down_branch,
    ) = kept_values
    row_count, model_width = layer_input.shape
    pullback = jax.vjp(norm_rows, down_branch, gains[3])[1]
    grad_down, gain_three = pullback(grad_result)
    gathered_dd, grad_gelu = gather_grads(grad_down.astype(jnp.bfloat16), w_down)
    down_total = contract(gelu_out, gathered_dd)
    pullback = jax.vjp(lambda vector: jax.nn.gelu(vector, approximate=True), up_act)[1]
    grad_up = pullback(grad_gelu)[0].astype(jnp.bfloat16)
    up_total = contract(gathered_c, grad_up)
    grad_mlp = scatter_grads(grad_up, w_up, row_count)
    pullback = jax.vjp(norm_rows, hidden, gains[2])[1]
    grad_norm_mlp, gain_two = pullback(grad_mlp)
    grad_hidden = grad_result + grad_norm_mlp
    pullback = jax.vjp(norm_rows, attn_branch, gains[1])[1]
    grad_attn, gain_one = pullback(grad_hidden)
    gathered_da, grad_mixed = gather_grads(grad_attn.astype(jnp.bfloat16), w_out)
    out_total = contract(mixed, gathered_da)
    length = grad_mixed.shape[0]
    head_count = w_qkv.shape[2] // HEAD_DIM
    grad_mixed = grad_mixed.astype(jnp.bfloat16).reshape(length, head_count, HEAD_DIM)
    attn_probs = attention_probs(queries, key_rows)
    probs_low = attn_probs.astype(jnp.bfloat16)
    grad_probs = jnp.einsum("qhd,khd->hqk", grad_mixed, values, preferred_element_type=jnp.float32)
    grad_values = jnp.einsum(
        "hqk,qhd->khd", probs_low, grad_mixed, preferred_element_type=jnp.float32
    )
    row_dots = jnp.sum(grad_probs * attn_probs, axis=-1, keepdims=True)
    grad_scores = (attn_probs * (grad_probs - row_dots)).astype(jnp.bfloat16)
    scale_value = HEAD_DIM ** (-0.5)
    grad_queries = (
        jnp.einsum("hqk,khd->qhd", grad_scores, key_rows, preferred_element_type=jnp.float32)
        * scale_value
    )
    grad_keys = (
        jnp.einsum("hqk,qhd->khd", grad_scores, queries, preferred_element_type=jnp.float32)
        * scale_value
    )
    cos_table, sin_table = rotary_tables(length, HEAD_DIM)
    pullback = jax.vjp(lambda vector: rotate(vector, cos_table, sin_table), grad_queries)[1]
    grad_q_raw = pullback(grad_queries)[0]
    grad_k_raw = pullback(grad_keys)[0]
    grad_qkv = (
        jnp.stack([grad_q_raw, grad_k_raw, grad_values], axis=1)
        .reshape(length, -1)
        .astype(jnp.bfloat16)
    )
    qkv_total = contract(gathered_a, grad_qkv).reshape(model_width, 3, -1)
    grad_attn_in = scatter_grads(grad_qkv, w_qkv.reshape(model_width, -1), row_count)
    pullback = jax.vjp(norm_rows, layer_input, gains[0])[1]
    grad_norm_in, gain_zero = pullback(grad_attn_in)
    grad_input = grad_hidden + grad_norm_in
    gain_total = jnp.stack([gain_zero, gain_one, gain_two, gain_three])
    return (grad_input, (gain_total, qkv_total, out_total, up_total, down_total))


def lagged(first_section, stacked):
    blank = jnp.zeros_like(stacked[:1])
    earlier = jnp.concatenate([blank, stacked[:-1]])
    later = jnp.concatenate([stacked[1:], blank])
    return jnp.where(first_section, earlier, later)


def per_device(
    inputs,
    out_cotangent,
    group_ids,
    group_weights,
    gains,
    qkv_weight,
    out_weight,
    up_weight,
    down_weight,
):
    weights = (gains[0], qkv_weight[0], out_weight[0], up_weight[0], down_weight[0])
    micro_count, row_count, model_width = inputs.shape
    first_section = lax.axis_index("section") == 0
    group_count = group_weights.shape[0]
    matches = group_ids[..., None] == jnp.arange(group_count, dtype=jnp.int32)
    row_scale = jnp.sum(jnp.where(matches, group_weights, 0.0), axis=-1)
    scaled = out_cotangent.astype(jnp.float32) * row_scale[..., None]
    padded = jnp.concatenate([inputs, jnp.zeros((1, row_count, model_width), jnp.bfloat16)])

    def forward_tick(received, fresh_input):
        layer_input = jnp.where(first_section, fresh_input, received)
        result, kept_values = layer_forward(layer_input.astype(jnp.float32), weights)
        result_low = result.astype(jnp.bfloat16)
        outgoing = shifted(result_low, "section", 1)
        stashed = ()
        return (outgoing, (layer_input, result_low, stashed))

    start_rows = jnp.zeros((row_count, model_width), jnp.bfloat16)
    _, (layer_inputs, layer_results, stashed) = lax.scan(forward_tick, start_rows, padded)
    layer_outputs = jnp.where(first_section, layer_results[:-1], layer_results[1:])[None]
    back_inputs = lagged(first_section, layer_inputs)
    back_stash = jax.tree.map(lambda stacked: lagged(first_section, stacked), stashed)
    grad_padded = jnp.concatenate([scaled, jnp.zeros((1, row_count, model_width), jnp.float32)])
    tick_index = jnp.arange(micro_count + 1, dtype=jnp.int32)
    tick_valid = jnp.where(first_section, tick_index >= 1, tick_index < micro_count).astype(
        jnp.float32
    )

    def backward_tick(carry, step_item):
        received, totals = carry
        layer_input, cotangent, valid_now, stash_now = step_item
        grad_now = jnp.where(first_section, received.astype(jnp.float32), cotangent)
        input_now = layer_input.astype(jnp.float32)
        kept_values = layer_forward(input_now, weights)[1]
        grad_input, layer_grads = layer_backward(input_now, grad_now, kept_values, weights)
        totals = jax.tree.map(lambda total, update: total + valid_now * update, totals, layer_grads)
        grad_low = grad_input.astype(jnp.bfloat16)
        outgoing = shifted(grad_low, "section", -1)
        return ((outgoing, totals), grad_low)

    start_totals = (
        jnp.zeros((4, model_width), jnp.float32),
        jnp.zeros(qkv_weight.shape[1:], jnp.float32),
        jnp.zeros(out_weight.shape[1:], jnp.float32),
        jnp.zeros(up_weight.shape[1:], jnp.float32),
        jnp.zeros(down_weight.shape[1:], jnp.float32),
    )
    (_, totals), grad_lows = lax.scan(
        backward_tick,
        (start_rows, start_totals),
        (back_inputs, grad_padded, tick_valid, back_stash),
    )
    input_grads = jnp.where(first_section, grad_lows[1:], grad_lows[:-1])[None]
    gain_total, qkv_total, out_total, up_total, down_total = totals
    gains_grad = lax.psum_scatter(gain_total, ("dp", "tensor"), scatter_dimension=1, tiled=True)
    qkv_grad, out_grad, up_grad, down_grad = (
        lax.psum_scatter(
            qkv_total.astype(jnp.bfloat16), "dp", scatter_dimension=0, tiled=True
        ).astype(jnp.float32),
        lax.psum_scatter(
            out_total.astype(jnp.bfloat16), "dp", scatter_dimension=1, tiled=True
        ).astype(jnp.float32),
        lax.psum_scatter(
            up_total.astype(jnp.bfloat16), "dp", scatter_dimension=0, tiled=True
        ).astype(jnp.float32),
        lax.psum_scatter(
            down_total.astype(jnp.bfloat16), "dp", scatter_dimension=1, tiled=True
        ).astype(jnp.float32),
    )
    return (
        layer_outputs,
        input_grads,
        gains_grad[None],
        qkv_grad[None],
        out_grad[None],
        up_grad[None],
        down_grad[None],
    )


def rotated(block, cos_rows, sin_rows):
    lane = lax.broadcasted_iota(jnp.int32, block.shape, 1)
    ahead = pltpu.roll(block, 96, 1)
    behind = pltpu.roll(block, 32, 1)
    swapped = jnp.where(lane % 64 < 32, ahead, behind)
    return block * cos_rows + swapped * sin_rows


def dot_nt(left, right):
    return lax.dot_general(
        left, right, (((1,), (1,)), ((), ())), preferred_element_type=jnp.float32
    )


def dot_nn(left, right):
    return jnp.dot(left, right, preferred_element_type=jnp.float32)


def model_weight(owns, others, cols):
    sides = [jnp.concatenate([ref[:, cols] for ref in refs], axis=1) for refs in (owns, others)]
    return jnp.concatenate(sides, axis=0)


def stacked_up(values):
    return jnp.concatenate(values, axis=0)


def edge_masks(core, rows):
    key = lax.broadcasted_iota(jnp.int32, (rows, 2 * rows), 0)
    query = lax.broadcasted_iota(jnp.int32, (rows, 2 * rows), 1)
    mine = query < rows
    place = jnp.where(mine, query + core * rows, query - rows + (1 - core) * rows)
    return (key + core * rows <= place, key + (1 - core) * rows <= place)


def both_sides(value, half, start, stop, axis=0):
    if axis == 0:
        return jnp.concatenate([value[start:stop], value[half + start : half + stop]], axis=0)
    return jnp.concatenate([value[:, start:stop], value[:, half + start : half + stop]], axis=1)


def hidden_scores(scores, masks, tile, step):
    seen = step * tile
    pieces = []
    for side in range(2):
        base = side * (seen + tile)
        if seen:
            pieces.append(scores[base : base + seen])
        pieces.append(jnp.where(masks[side], scores[base + seen : base + seen + tile], -1e30))
    return jnp.concatenate(pieces, axis=0)


def one_head(rows, head):
    lane = lax.broadcasted_iota(jnp.int32, rows.shape, 1)
    return jnp.where(lane // 64 == head, rows, jnp.zeros_like(rows))


def pick_piece(weight, owns, others, cols):
    for j, (own, other) in enumerate(zip(owns, others)):

        @pl.when(pl.program_id(0) == j)
        def _():
            size = own.shape[0]
            weight[:size] = own[:, cols]
            weight[size:] = other[:, cols]


def attend_kernel(pieces, core_ref, cos_ref, sin_ref, own_rows, other_rows, *refs):
    owns, others = refs[:pieces], refs[pieces : 2 * pieces]
    q_ref, k_ref, v_ref, lse_ref, mix_ref, weight = refs[2 * pieces :]
    half = own_rows.shape[0]
    tile = TILE
    pick_piece(weight, owns, others, QKV)
    proj = dot_nn(stacked_up([own_rows[...], other_rows[...]]), weight[...])
    cos_rows, sin_rows = cos_ref[...], sin_ref[...]
    q = (rotated(proj[:, :128], cos_rows, sin_rows) * HEAD_DIM ** (-0.5)).astype(jnp.bfloat16)
    k = rotated(proj[:, 128:256], cos_rows, sin_rows).astype(jnp.bfloat16)
    v32 = proj[:, 256:]
    q_ref[0] = q
    k_ref[0] = k
    v_ref[0] = v32.astype(jnp.bfloat16)
    v_flip = v32.T.astype(jnp.bfloat16)
    masks = edge_masks(core_ref[0], tile)

    def scored(step, head):
        stop = (step + 1) * tile
        q_head = one_head(both_sides(q, half, step * tile, stop), head)
        return hidden_scores(dot_nt(both_sides(k, half, 0, stop), q_head), masks, tile, step)

    units = [(step, head) for step in range(half // tile) for head in range(2)]
    ahead = scored(*units[0])
    outs = []
    for spot, (step, head) in enumerate(units):
        scores = ahead
        if spot + 1 < len(units):
            ahead = scored(*units[spot + 1])
        stop = (step + 1) * tile
        top = jnp.max(scores, axis=0, keepdims=True)
        expos = jnp.exp(scores - top)
        total = jnp.sum(expos, axis=0, keepdims=True)
        lse = top + jnp.log(total)
        lse_ref[0, head : head + 1, step * tile : stop] = lse[:, :tile]
        lse_ref[0, head : head + 1, half + step * tile : half + stop] = lse[:, tile:]
        v_cols = both_sides(v_flip, half, 0, stop, axis=1)
        out = dot_nn(v_cols[64 * head : 64 * head + 64], expos.astype(jnp.bfloat16))
        outs.append(out * (1.0 / total))
        if head == 1:
            mixed = jnp.concatenate(outs, axis=0).T.astype(jnp.bfloat16)
            outs = []
            mix_ref[step * tile : stop, :] = mixed[:tile]
            mix_ref[half + step * tile : half + stop, :] = mixed[tile:]


def attend_back_kernel(pieces, core_ref, cos_ref, sin_ref, own_rows, other_rows, *refs):
    owns, others = refs[:pieces], refs[pieces : 2 * pieces]
    q_ref, k_ref, v_ref, lse_ref, out_ref, weight, dq, dk, dv = refs[2 * pieces :]
    half = own_rows.shape[0]
    tile = TILE
    pick_piece(weight, owns, others, OUT)
    rows = stacked_up([own_rows[...], other_rows[...]])
    d_mixed = dot_nn(rows, weight[...]).astype(jnp.bfloat16)
    q, k, v = q_ref[0], k_ref[0], v_ref[0]
    k_flip = k.astype(jnp.float32).T.astype(jnp.bfloat16)
    masks = edge_masks(core_ref[0], tile)
    steps = half // tile

    def scored(step, head):
        stop = (step + 1) * tile
        q_head = one_head(both_sides(q, half, step * tile, stop), head)
        g_head = one_head(both_sides(d_mixed, half, step * tile, stop), head)
        scores = hidden_scores(dot_nt(both_sides(k, half, 0, stop), q_head), masks, tile, step)
        return q_head, g_head, scores, dot_nt(both_sides(v, half, 0, stop), g_head)

    units = [(step, head) for step in reversed(range(steps)) for head in range(2)]
    ahead = scored(*units[0])
    dq_flips = []
    dk_sum = dv_sum = None
    for spot, (step, head) in enumerate(units):
        q_head, g_head, scores, d_probs = ahead
        if spot + 1 < len(units):
            ahead = scored(*units[spot + 1])
        stop = (step + 1) * tile
        lse = both_sides(lse_ref[0], half, step * tile, stop, axis=1)
        probs = jnp.exp(scores - lse[head : head + 1])
        dots = jnp.sum(probs * d_probs, axis=0, keepdims=True)
        d_scores = (probs * (d_probs - dots)).astype(jnp.bfloat16)
        dv_part = dot_nn(probs.astype(jnp.bfloat16), g_head)
        dk_part = dot_nn(d_scores, q_head)
        k_cols = both_sides(k_flip, half, 0, stop, axis=1)
        dq_flips.append(dot_nn(k_cols[64 * head : 64 * head + 64], d_scores))
        if head == 0:
            dv_sum, dk_sum = dv_part, dk_part
            continue
        dv_sum, dk_sum = dv_sum + dv_part, dk_sum + dk_part
        dq_rows = jnp.concatenate(dq_flips, axis=0).T * HEAD_DIM ** (-0.5)
        dq_flips = []
        dq[step * tile : stop] = dq_rows[:tile]
        dq[half + step * tile : half + stop] = dq_rows[tile:]
        for base, part in ((0, slice(0, stop)), (half, slice(stop, 2 * stop))):
            if step == steps - 1:
                dk[base : base + stop] = dk_sum[part]
                dv[base : base + stop] = dv_sum[part]
            else:
                dk[base : base + stop] += dk_sum[part]
                dv[base : base + stop] += dv_sum[part]
    cos_rows, sin_rows = cos_ref[...], -sin_ref[...]
    out_ref[:, :128] = rotated(dq[...], cos_rows, sin_rows).astype(jnp.bfloat16)
    out_ref[:, 128:256] = rotated(dk[...], cos_rows, sin_rows).astype(jnp.bfloat16)
    out_ref[:, 256:] = dv[...].astype(jnp.bfloat16)


def split_rows(total, own_ref, other_ref):
    half = own_ref.shape[0]
    own_ref[...] = total[:half]
    other_ref[...] = total[half:].astype(jnp.bfloat16)


def to_model_kernel(lefts, pieces, cols, *refs):
    left, refs = jnp.concatenate([ref[...] for ref in refs[:lefts]], axis=1), refs[lefts:]
    weight = model_weight(refs[:pieces], refs[pieces : 2 * pieces], cols)
    split_rows(dot_nt(left, weight), *refs[2 * pieces :])


def mlp_down_kernel(pieces, left_ref, *refs):
    sides = [stacked_up([ref[...] for ref in side]) for side in (refs[:pieces], refs[pieces:-2])]
    split_rows(dot_nn(left_ref[...], jnp.concatenate(sides, axis=1)), *refs[-2:])


def gelu_both(up_act):
    root = math.sqrt(2.0 / math.pi)
    square = up_act * up_act
    rise = 0.5 + 0.5 * jnp.tanh(up_act * (root + root * 0.044715 * square))
    value = up_act * rise
    slope = rise + value * (1.0 - rise) * (2.0 * root + 6.0 * root * 0.044715 * square)
    return value, slope


def mlp_up_kernel(pieces, own_rows, other_rows, *refs):
    owns, others = refs[:pieces], refs[pieces : 2 * pieces]
    gelu_ref, slope_ref = refs[2 * pieces :]
    half = own_rows.shape[0]
    size = owns[0].shape[1]
    step = half // 2
    units = [(j, i) for j in range(pieces) for i in range(4)]

    def product(j, i):
        rows = (own_rows, other_rows)[i // 2][i % 2 * step : (i % 2 + 1) * step]
        return dot_nn(rows, stacked_up([owns[j][...], others[j][...]]))

    ahead = product(*units[0])
    for spot, (j, i) in enumerate(units):
        up_act = ahead
        if spot + 1 < len(units):
            ahead = product(*units[spot + 1])
        value, slope = gelu_both(up_act)
        gelu_ref[i * step : (i + 1) * step, j * size : (j + 1) * size] = value.astype(jnp.bfloat16)
        slope_ref[i * step : (i + 1) * step, j * size : (j + 1) * size] = slope.astype(
            jnp.bfloat16
        )


def mlp_up_back_kernel(pieces, own_rows, other_rows, slope_ref, *refs):
    owns, others = refs[:pieces], refs[pieces : 2 * pieces]
    out_ref, weight, slope, sems = refs[2 * pieces :]
    half = own_rows.shape[1] // 2
    size = owns[0].shape[0]
    order = list(reversed(range(pieces)))
    copies = []
    for j in order:
        sources = (owns[j], others[j], slope_ref.at[:, pl.ds(j * size, size)])
        targets = (
            weight.at[j, :, pl.ds(0, half)],
            weight.at[j, :, pl.ds(half, half)],
            slope.at[:, pl.ds(j * size, size)],
        )
        copies.append(
            [
                pltpu.make_async_copy(source, target, sems.at[j, i])
                for i, (source, target) in enumerate(zip(sources, targets))
            ]
        )
        for copy in copies[-1]:
            copy.start()
    rows = stacked_up([own_rows[...], other_rows[...]])
    for j, arriving in zip(order, copies):
        cols = slice(j * size, (j + 1) * size)
        for copy in arriving:
            copy.wait()
        d_gelu = dot_nt(rows, weight[j])
        out_ref[:, cols] = (d_gelu * slope[:, cols].astype(jnp.float32)).astype(jnp.bfloat16)


def inverse_size(rows):
    return lax.rsqrt(jnp.mean(rows * rows, axis=-1, keepdims=True) + NORM_EPSILON)


def norm_back(rows, gain, grad):
    scale = inverse_size(rows)
    weighted = grad * gain
    inner = jnp.mean(rows * weighted, axis=-1, keepdims=True)
    return scale * weighted - rows * (scale * scale * scale * inner), rows * scale * grad


def folded(rows):
    return jnp.sum(rows.reshape(rows.shape[0] // 8, 8, rows.shape[1]), axis=0)


def wide(ref, spot):
    return ref[spot, :].astype(jnp.float32)


def by_chunks(count, body, sums=0, width=0):
    def one(i, carry):
        more = body(pl.ds(pl.multiple_of(i * CHUNK, CHUNK), CHUNK))
        return tuple(old + folded(new) for old, new in zip(carry, more))

    start = tuple(jnp.zeros((8, width), jnp.float32) for _ in range(sums))
    totals = lax.fori_loop(0, count // CHUNK, one, start)
    return [jnp.sum(total, axis=0, keepdims=True) for total in totals]


def norm_in_kernel(gain_ref, rows_ref, out_ref):
    def body(spot):
        rows = wide(rows_ref, spot)
        out_ref[spot, :] = (rows * inverse_size(rows) * gain_ref[0:1]).astype(jnp.bfloat16)
        return ()

    by_chunks(rows_ref.shape[0], body)


def after_attention_kernel(
    gain_ref, rows_ref, own_ref, other_ref, branch_ref, hidden_ref, out_ref
):
    def body(spot):
        branch = own_ref[spot, :] + wide(other_ref, spot)
        hidden = wide(rows_ref, spot) + branch * inverse_size(branch) * gain_ref[1:2]
        branch_ref[spot, :] = branch
        hidden_ref[spot, :] = hidden
        out_ref[spot, :] = (hidden * inverse_size(hidden) * gain_ref[2:3]).astype(jnp.bfloat16)
        return ()

    by_chunks(rows_ref.shape[0], body)


def after_mlp_kernel(gain_ref, hidden_ref, own_ref, other_ref, branch_ref, out_ref):
    def body(spot):
        branch = own_ref[spot, :] + wide(other_ref, spot)
        branch_ref[spot, :] = branch
        result = hidden_ref[spot, :] + branch * inverse_size(branch) * gain_ref[3:4]
        out_ref[spot, :] = result.astype(jnp.bfloat16)
        return ()

    by_chunks(hidden_ref.shape[0], body)


def into_mlp_back_kernel(gain_ref, grad_ref, branch_ref, out_ref, sum_ref):
    def body(spot):
        d_rows, d_gain = norm_back(branch_ref[spot, :], gain_ref[3:4], wide(grad_ref, spot))
        out_ref[spot, :] = d_rows.astype(jnp.bfloat16)
        return (d_gain,)

    (sum_ref[...],) = by_chunks(grad_ref.shape[0], body, 1, grad_ref.shape[1])


def into_attention_back_kernel(
    gain_ref, grad_ref, own_ref, other_ref, hidden_ref, branch_ref, d_hidden_ref, out_ref, *sums
):
    def body(spot):
        d_rows = own_ref[spot, :] + wide(other_ref, spot)
        d_rows, d_gain = norm_back(hidden_ref[spot, :], gain_ref[2:3], d_rows)
        d_hidden = wide(grad_ref, spot) + d_rows
        d_hidden_ref[spot, :] = d_hidden
        d_rows, d_first = norm_back(branch_ref[spot, :], gain_ref[1:2], d_hidden)
        out_ref[spot, :] = d_rows.astype(jnp.bfloat16)
        return (d_first, d_gain)

    totals = by_chunks(grad_ref.shape[0], body, 2, grad_ref.shape[1])
    sums[0][...], sums[1][...] = totals


def out_of_layer_kernel(gain_ref, rows_ref, own_ref, other_ref, d_hidden_ref, out_ref, sum_ref):
    def body(spot):
        d_rows = own_ref[spot, :] + wide(other_ref, spot)
        d_rows, d_gain = norm_back(wide(rows_ref, spot), gain_ref[0:1], d_rows)
        out_ref[spot, :] = (d_hidden_ref[spot, :] + d_rows).astype(jnp.bfloat16)
        return (d_gain,)

    (sum_ref[...],) = by_chunks(rows_ref.shape[0], body, 1, rows_ref.shape[1])


def work(flops, arrays):
    size = sum(math.prod(array.shape) * jnp.dtype(array.dtype).itemsize for array in arrays)
    return pl.CostEstimate(flops=flops, bytes_accessed=size, transcendentals=0)


def far(array):
    return pltpu.with_memory_space_constraint(array, pltpu.HBM)


def without(kernel, first, count):
    return lambda *refs: kernel(*refs[:first], *refs[first + count :])


def on_chip(kernel, name, outs, *operands, limit=ROWS_VMEM, flops=0, waits=()):
    shapes = [jax.ShapeDtypeStruct(shape, dtype) for shape, dtype in outs]
    space = pl.BlockSpec(memory_space=pltpu.VMEM)
    return pl.pallas_call(
        without(kernel, len(operands), len(waits)),
        in_specs=[space] * len(operands) + [pl.BlockSpec(memory_space=pl.ANY)] * len(waits),
        out_specs=[space] * len(outs),
        out_shape=shapes,
        compiler_params=pltpu.CompilerParams(vmem_limit_bytes=limit),
        cost_estimate=work(flops, (*operands, *shapes)),
        name=name,
    )(*operands, *map(far, waits))


def whole_block(array):
    return pl.BlockSpec(array.shape, lambda j: (0,) * array.ndim)


def by_pairs(kernel, name, core, operands, pieces, blocks, outs, scratch, flops, waits):
    shapes = [jax.ShapeDtypeStruct(shape, dtype) for shape, dtype, _ in outs]
    taken = 1 + len(operands) + 2 * len(pieces[0]) + len(blocks)
    return pl.pallas_call(
        without(functools.partial(kernel, len(pieces[0])), taken, len(waits)),
        grid=(len(pieces[0]),),
        in_specs=[pl.BlockSpec(memory_space=pltpu.SMEM)]
        + [whole_block(array) for array in (*operands, *pieces[0], *pieces[1])]
        + [spec for _, spec in blocks]
        + [pl.BlockSpec(memory_space=pl.ANY)] * len(waits),
        out_specs=[spec for _, _, spec in outs],
        out_shape=shapes,
        scratch_shapes=scratch,
        compiler_params=pltpu.CompilerParams(vmem_limit_bytes=KERNEL_VMEM),
        cost_estimate=work(flops, (*operands, *pieces[0], *pieces[1], *shapes)),
        name=name,
    )(core, *operands, *pieces[0], *pieces[1], *[array for array, _ in blocks], *map(far, waits))


def mlp_up_back(rows, slope, pieces, waits):
    length, units = slope.shape
    unit, half = pieces[0][0].shape
    count = len(pieces[0])
    every, space = pl.BlockSpec(memory_space=pl.ANY), pl.BlockSpec(memory_space=pltpu.VMEM)
    return pl.pallas_call(
        without(functools.partial(mlp_up_back_kernel, count), 3 + 2 * count, len(waits)),
        in_specs=[space] * 2 + [every] * (1 + 2 * count + len(waits)),
        out_specs=space,
        out_shape=jax.ShapeDtypeStruct((length, units), jnp.bfloat16),
        scratch_shapes=[
            pltpu.VMEM((count, unit, 2 * half), jnp.bfloat16),
            pltpu.VMEM((length, units), jnp.bfloat16),
            pltpu.SemaphoreType.DMA((count, 3)),
        ],
        compiler_params=pltpu.CompilerParams(vmem_limit_bytes=KERNEL_VMEM),
        name="mlp_up_back",
    )(*rows, *map(far, (slope, *pieces[0], *pieces[1], *waits)))


def attend(core, tables, rows, pieces, waits):
    half, features = rows[0].shape
    length, count = 2 * half, len(pieces[0])
    lanes = ((count, length, 128), jnp.bfloat16, pl.BlockSpec((1, length, 128), lambda j: (j, 0, 0)))
    lse = ((count, 2, length), jnp.float32, pl.BlockSpec((1, 2, length), lambda j: (j, 0, 0)))
    mixed = ((length, count * 128), jnp.bfloat16, pl.BlockSpec((length, 128), lambda j: (0, j)))
    return by_pairs(
        attend_kernel,
        "attend",
        core,
        (*tables, *rows),
        pieces,
        (),
        (lanes, lanes, lanes, lse, mixed),
        [pltpu.VMEM((features, 384), jnp.bfloat16)],
        count * length * (2 * features * 384 + 2 * PAIR_WORK * length),
        waits,
    )


def attend_back(core, tables, rows, pieces, base, waits, q, k, v, lse):
    half, features = rows[0].shape
    length, count = 2 * half, len(pieces[0])
    lanes = pl.BlockSpec((1, length, 128), lambda j: (base + j, 0, 0))
    lse_spec = pl.BlockSpec((1, 2, length), lambda j: (base + j, 0, 0))
    out = ((length, count * 384), jnp.bfloat16, pl.BlockSpec((length, 384), lambda j: (0, j)))
    return by_pairs(
        attend_back_kernel,
        "attend_back",
        core,
        (*tables, *rows),
        pieces,
        ((q, lanes), (k, lanes), (v, lanes), (lse, lse_spec)),
        (out,),
        [pltpu.VMEM((features, 128), jnp.bfloat16)] + [pltpu.VMEM((length, 128), jnp.float32)] * 3,
        count * length * (2 * features * 128 + 5 * PAIR_WORK * length),
        waits,
    )[0]


def exchanged(parts):
    return parts[0], flip_pairs(parts[1], 1)


def model_rows(kernel, name, lefts, pieces, waits=()):
    length, width = lefts[0].shape[0], 2 * MODEL_HALF
    outs = (((length // 2, width), jnp.float32), ((length // 2, width), jnp.bfloat16))
    hidden = sum(left.shape[1] for left in lefts)
    more = {"limit": KERNEL_VMEM, "flops": 2 * length * width * hidden, "waits": waits}
    return exchanged(on_chip(kernel, name, outs, *lefts, *pieces[0], *pieces[1], **more))


def flip_pairs(block, distance):
    size = lax.axis_size("dp")
    return lax.ppermute(block, "dp", [(i, i ^ distance) for i in range(size)])


def passed_on(block, step):
    size = lax.axis_size("tensor")
    return lax.ppermute(block, "tensor", [(i, (i + step) % size) for i in range(size)])


def dot_tn(left, right):
    return lax.dot_general(
        left, right, (((0,), (0,)), ((), ())), preferred_element_type=jnp.float32
    )


def fetch(first_ref, zeros, ones, buffers, sems):
    for section, sources in enumerate((zeros, ones)):

        @pl.when(first_ref[0] == section)
        def _():
            for i, (source, buffer) in enumerate(zip(sources, buffers)):
                pltpu.make_async_copy(source, buffer, sems.at[i]).start()

    def arrived(*places):
        for i in places:
            pltpu.make_async_copy(zeros[i], buffers[i], sems.at[i]).wait()

    return arrived


def mlp_grads_kernel(base, section_ref, *refs):
    (own_one, other_one, own_two, other_two), (rows, d_up, gelu, d_down, sems) = refs[12:16], refs[16:]
    half, size = own_one.shape[0] // 2, own_one.shape[1]
    cols = pl.ds(base * size, 2 * size)

    def parts(own_rows, other_rows, d_up_ref, gelu_ref, own_grad, other_grad):
        whole = (d_up_ref.at[:, cols], gelu_ref.at[:, cols])
        return (own_rows, other_rows, *whole, own_grad, other_grad)

    count = refs[0].shape[0]
    buffers = (
        rows.at[pl.ds(0, count)],
        rows.at[pl.ds(count, count)],
        d_up,
        gelu,
        d_down.at[pl.ds(0, count)],
        d_down.at[pl.ds(count, count)],
    )
    arrived = fetch(section_ref, parts(*refs[:6]), parts(*refs[6:12]), buffers, sems)
    for j, own, other in ((1, own_two, other_two), (0, own_one, other_one)):
        cols = slice(j * size, (j + 1) * size)
        if j == 1:
            arrived(0, 1, 2)
        up = dot_tn(rows[...], d_up[:, cols])
        own[:half] = up[:half]
        other[:half] = up[half:].astype(jnp.bfloat16)
        if j == 1:
            arrived(3, 4, 5)
        down = dot_tn(gelu[:, cols], d_down[...])
        own[half:] = down[:, :half]
        other[half:] = down[:, half:].astype(jnp.bfloat16)


def attn_grads_kernel(base, section_ref, *refs):
    (own_one, other_one, own_two, other_two), (rows, d_qkv, mixed, d_attn, sems) = refs[12:16], refs[16:]
    half, size = own_one.shape[0], d_qkv.shape[1] // 2
    count = refs[0].shape[0]
    cols = pl.ds(base * 128, 256)

    def parts(own_rows, other_rows, d_qkv_ref, mixed_ref, own_grad, other_grad):
        return (own_rows, other_rows, d_qkv_ref, mixed_ref.at[:, cols], own_grad, other_grad)

    buffers = (
        rows.at[pl.ds(0, count)],
        rows.at[pl.ds(count, count)],
        d_qkv,
        mixed,
        d_attn.at[pl.ds(0, count)],
        d_attn.at[pl.ds(count, count)],
    )
    arrived = fetch(section_ref, parts(*refs[:6]), parts(*refs[6:12]), buffers, sems)
    for j, own, other in ((1, own_two, other_two), (0, own_one, other_one)):
        if j == 1:
            arrived(0, 1, 2)
        qkv = dot_tn(rows[...], d_qkv[:, j * size : (j + 1) * size])
        if j == 1:
            arrived(3, 4, 5)
        out = dot_tn(d_attn[...], mixed[:, j * 128 : (j + 1) * 128])
        own[:, :size] = qkv[:half]
        own[:, size:] = out[:half]
        other[:, :size] = qkv[half:].astype(jnp.bfloat16)
        other[:, size:] = out[half:].astype(jnp.bfloat16)


def weight_grads(kernel, name, base, section, zeros, ones, shape, columns, waits=()):
    length = 2 * zeros[0].shape[0]
    width = zeros[0].shape[1]
    every = pl.BlockSpec(memory_space=pl.ANY)
    space = pl.BlockSpec(memory_space=pltpu.VMEM)
    arrays = (*zeros, *ones)
    first, second, third, fourth = pl.pallas_call(
        without(functools.partial(kernel, base), 1 + len(arrays), len(waits)),
        in_specs=[pl.BlockSpec(memory_space=pltpu.SMEM)] + [every] * (len(arrays) + len(waits)),
        out_specs=[space] * 4,
        out_shape=[
            jax.ShapeDtypeStruct(shape, jnp.float32),
            jax.ShapeDtypeStruct(shape, jnp.bfloat16),
        ]
        * 2,
        scratch_shapes=[
            pltpu.VMEM((length, width), jnp.bfloat16),
            pltpu.VMEM((length, columns[0]), jnp.bfloat16),
            pltpu.VMEM((length, columns[1]), jnp.bfloat16),
            pltpu.VMEM((length, width), jnp.bfloat16),
            pltpu.SemaphoreType.DMA((6,)),
        ],
        compiler_params=pltpu.CompilerParams(vmem_limit_bytes=KERNEL_VMEM),
        name=name,
    )(section, *map(far, (*arrays, *waits)))
    return [(first, flip_pairs(second, 2)), (third, flip_pairs(fourth, 2))]


def moved_kernel(own_ref, other_ref, *refs):
    out_ref = refs[-1]

    def body(i, carry):
        spot = pl.ds(pl.multiple_of(i * CHUNK, CHUNK), CHUNK)
        total = own_ref[spot, :]
        for ref in (other_ref, *refs[:-1]):
            total = total + wide(ref, spot)
        out_ref[spot, :] = total.astype(jnp.bfloat16)
        return carry

    lax.fori_loop(0, own_ref.shape[0] // CHUNK, body, 0)


def gates_kernel(up_ref, down_ref, up_out, down_out):
    up_out[...] = up_ref[...]
    down_out[...] = down_ref[...]


def gate_kernel(piece_ref, out_ref):
    out_ref[...] = piece_ref[...]


def mlp_sum_kernel(core_ref, own_ref, other_ref, moved_ref, up_keep, down_keep, up_send, down_send):
    half = own_ref.shape[0] // 2
    size = up_keep.shape[0]

    def total(rows, cols):
        more = other_ref[rows, cols].astype(jnp.float32) + moved_ref[rows, cols].astype(jnp.float32)
        return own_ref[rows, cols] + more

    for core in range(2):

        @pl.when(core_ref[0] == core)
        def _():
            for place, up, down in ((core, up_keep, down_keep), (1 - core, up_send, down_send)):
                spot = slice(place * size, (place + 1) * size)
                up[...] = total(spot, slice(None))
                down[...] = total(slice(half, None), spot)


def mlp_join_kernel(core_ref, up_keep, down_keep, up_sent, down_sent, up_out, down_out):
    size = up_keep.shape[1]
    for core in range(2):

        @pl.when(core_ref[0] == core)
        def _():
            places = ((core, up_keep, down_keep), (1 - core, up_sent, down_sent))
            for place, up, down in places:
                spot = slice(place * size, (place + 1) * size)
                up_out[:, spot] = up[...]
                down_out[spot] = down[...]


def chosen_kernel(place_ref, zero_ref, one_ref, out_ref):
    half = out_ref.shape[1] // 2
    for section, rows_ref in enumerate((zero_ref, one_ref)):
        for upper in range(2):

            @pl.when(jnp.logical_and(place_ref[0] == section, place_ref[1] == upper))
            def _():
                for side in range(2):
                    place = (side + upper) % 2 * half
                    out_ref[:, place : place + half] = rows_ref[:, side * half : (side + 1) * half]


def pick_kernel(core_ref, rows_ref, keep_ref, send_ref):
    count = keep_ref.shape[0]
    keep_ref[...] = rows_ref[pl.ds(core_ref[0] * count, count)]
    send_ref[...] = rows_ref[pl.ds((1 - core_ref[0]) * count, count)]


def in_order_kernel(core_ref, keep_ref, sent_ref, out_ref):
    out_ref[:, pl.ds(core_ref[0], 1)] = keep_ref[...][:, None]
    out_ref[:, pl.ds(1 - core_ref[0], 1)] = sent_ref[...][:, None]


def with_core(kernel, name, core, outs, *operands, waits=()):
    space = pl.BlockSpec(memory_space=pltpu.VMEM)
    return pl.pallas_call(
        without(kernel, 1 + len(operands), len(waits)),
        in_specs=[pl.BlockSpec(memory_space=pltpu.SMEM)]
        + [space] * len(operands)
        + [pl.BlockSpec(memory_space=pl.ANY)] * len(waits),
        out_specs=[space] * len(outs),
        out_shape=[jax.ShapeDtypeStruct(shape, dtype) for shape, dtype in outs],
        compiler_params=pltpu.CompilerParams(vmem_limit_bytes=ROWS_VMEM),
        name=name,
    )(core, *operands, *map(far, waits))


def last_sum_kernel(core_ref, own_ref, other_ref, moved_ref, keep_ref, send_ref):
    rows = keep_ref.shape[0]

    def total(block):
        spot = pl.ds(pl.multiple_of(block * rows, rows), rows)
        return own_ref[spot, :] + wide(other_ref, spot) + wide(moved_ref, spot)

    keep_ref[...] = total(core_ref[0])
    send_ref[...] = total(1 - core_ref[0])


def joined_kernel(spots, core_ref, keep_ref, sent_ref, column_ref, row_ref):
    size = row_ref.shape[0] // 2
    for core in range(2):

        @pl.when(core_ref[0] == core)
        def _():
            for place, source in ((core, keep_ref), (1 - core, sent_ref)):
                for start, stop, to in spots:
                    step = stop - start
                    column_ref[:, to + place * step : to + (place + 1) * step] = source[:, start:stop]
                row_ref[place * size : (place + 1) * size] = source[:, spots[-1][1] :].T


def per_chip(
    inputs,
    out_cotangent,
    group_ids,
    group_weights,
    gains,
    qkv_weight,
    out_weight,
    up_weight,
    down_weight,
):
    micro, row_count, width = inputs.shape
    tensor = lax.axis_size("tensor")
    part = row_count // 2
    wide_half = width // 2
    length = tensor * row_count
    half = length // 2
    first = lax.axis_index("section") == 0
    place = lax.axis_index("dp")
    core = place % 2
    upper = place // 2 % 2
    core_zero = core == 0
    low_half = upper == 0

    def ordered(mine, other):
        return jnp.where(core_zero, mine, other), jnp.where(core_zero, other, mine)

    def own_first(values):
        return jnp.where(low_half, values, jnp.roll(values, wide_half, axis=-1))

    def both_rows(own):
        return own, flip_pairs(own, 1)

    def to_chip(block):
        split = block.reshape((micro, 2, part) + block.shape[2:])
        mine = lax.dynamic_index_in_dim(split, core, 1, keepdims=False)
        other = lax.dynamic_index_in_dim(split, 1 - core, 1, keepdims=False)
        return lax.all_to_all(
            jnp.concatenate(ordered(mine, flip_pairs(other, 1))), "tensor", 0, 0, tiled=True
        )

    def from_chip(spread_out, waits=()):
        piece = ((micro, part, width), jnp.bfloat16)
        keep, send = with_core(
            pick_kernel, "pick", core_word, (piece, piece), spread_out, waits=waits
        )
        outs = (((micro, 2, part, width), jnp.bfloat16),)
        (rows,) = with_core(
            in_order_kernel, "in_order", core_word, outs, keep, flip_pairs(send, 1)
        )
        return rows.reshape(micro, row_count, width)

    def columns(local):
        size = local.shape[-1] // 2
        mid = (0,) * (local.ndim - 2)
        piece = lax.dynamic_slice(
            local,
            (wide_half * upper, *mid, size * core),
            (wide_half, *local.shape[1:-1], size),
        )
        return piece.reshape(wide_half, -1)

    def rows(local):
        size = local.shape[0] // 2
        return lax.dynamic_slice(local, (size * core, wide_half * upper), (size, wide_half))

    core_word = core.astype(jnp.int32).reshape(1)
    attn_piece = jnp.concatenate([columns(qkv_weight[0]), rows(out_weight[0]).T], axis=1)

    def spread(piece):
        pieces = [piece]
        for _ in range(tensor - 1):
            pieces.append(passed_on(pieces[-1], 1))
        return pieces

    up_piece, down_piece = columns(up_weight[0]), rows(down_weight[0])
    up_other, down_other = [flip_pairs(up_piece, 2)], [flip_pairs(down_piece, 2)]
    attn_own = [attn_piece, passed_on(attn_piece, 1)]
    attn_first = flip_pairs(attn_piece, 2)
    outs = ((attn_piece.shape, attn_piece.dtype),)
    attn_own[1] = on_chip(gate_kernel, "gate", outs, attn_own[1], waits=(attn_first, up_other[0]))[0]
    attn_own += spread(attn_own[1])[1:-1]
    attn_other = [attn_first] + [flip_pairs(piece, 2) for piece in attn_own[1:]]
    outs = tuple((piece.shape, piece.dtype) for piece in (up_piece, down_piece))
    up_piece, down_piece = on_chip(
        gates_kernel, "gate", outs, up_piece, down_piece, waits=(attn_own[2], attn_other[0], down_other[0])
    )
    up_own, down_own = spread(up_piece), spread(down_piece)
    up_other += [flip_pairs(piece, 2) for piece in up_own[1:]]
    down_other += [flip_pairs(piece, 2) for piece in down_own[1:]]
    w_attn, w_up, w_down = (attn_own, attn_other), (up_own, up_other), (down_own, down_other)
    unit = up_piece.shape[1]
    units = tensor * unit

    group_count = group_weights.shape[0]
    matches = group_ids[..., None] == jnp.arange(group_count, dtype=jnp.int32)
    row_scale = jnp.sum(jnp.where(matches, group_weights, 0.0), axis=-1)
    weighted = (out_cotangent.astype(jnp.float32) * row_scale[..., None]).astype(jnp.bfloat16)
    start = to_chip(own_first(jnp.where(first, inputs, weighted))).reshape(half, width)
    gain = own_first(gains[0])

    turns = jnp.arange(half, dtype=jnp.int32)
    turns = turns // part * row_count + turns % part
    positions = jnp.concatenate([turns + core * part, turns + (1 - core) * part])
    freqs = 10000.0 ** (-2.0 * jnp.arange(HEAD_DIM // 2, dtype=jnp.float32) / HEAD_DIM)
    angles = positions.astype(jnp.float32)[:, None] * freqs[None, :]
    cos_part, sin_part = jnp.cos(angles), jnp.sin(angles)
    tables = (
        jnp.concatenate([cos_part] * 4, axis=1),
        jnp.concatenate([-sin_part, sin_part] * 2, axis=1),
    )
    row32, row16 = ((half, width), jnp.float32), ((half, width), jnp.bfloat16)
    unit16 = ((length, units), jnp.bfloat16)
    sum32 = ((1, width), jnp.float32)
    mlp_cost = {"limit": KERNEL_VMEM, "flops": 2 * length * width * units}
    every = slice(None)

    def model_kernel(cols, lefts=1):
        return functools.partial(to_model_kernel, lefts, tensor, cols)

    down_kernel = functools.partial(mlp_down_kernel, tensor)

    def forward(layer_input, waits):
        attn_in = both_rows(
            on_chip(norm_in_kernel, "norm_in", (row16,), gain, layer_input, waits=waits[0])[0]
        )
        *heads, mixed = attend(core_word, tables, attn_in, w_attn, waits[1])
        parts = model_rows(model_kernel(OUT), "attn_out", [mixed], w_attn, waits[2])
        operands = (gain, layer_input, *parts)
        branch, hidden, mlp_in = on_chip(
            after_attention_kernel, "after_attn", (row32, row32, row16), *operands, waits=waits[3]
        )
        mlp_in = both_rows(mlp_in)
        kernel = functools.partial(mlp_up_kernel, tensor)
        operands = (*mlp_in, *w_up[0], *w_up[1])
        gelu_out, slope = on_chip(kernel, "mlp_up", (unit16, unit16), *operands, **mlp_cost)
        parts = model_rows(down_kernel, "mlp_down", [gelu_out], w_down)
        mlp_branch, result = on_chip(
            after_mlp_kernel, "after_mlp", (row32, row16), gain, hidden, *parts
        )
        saved = (layer_input, heads, branch, hidden, slope, mlp_branch)
        return result, saved, (attn_in, mixed, mlp_in, gelu_out)

    def backward(grad, saved, hook, late=()):
        layer_input, heads, branch, hidden, slope, mlp_branch = saved
        operands = (gain, grad, mlp_branch)
        d_down, sum_three = on_chip(
            into_mlp_back_kernel, "into_mlp_back", (row16, sum32), *operands
        )
        d_down = both_rows(d_down)
        d_up = mlp_up_back(d_down, slope, w_down, late)
        waits = hook(d_down, d_up)
        parts = model_rows(model_kernel(every), "mlp_back", [d_up], w_up, waits)
        waits = hook()
        operands = (gain, grad, *parts, hidden, branch)
        outs = (row32, row16, sum32, sum32)
        d_hidden, d_attn, sum_one, sum_two = on_chip(
            into_attention_back_kernel, "into_attn_back", outs, *operands, waits=waits
        )
        d_attn = both_rows(d_attn)
        waits = hook(d_attn)
        d_qkv = []
        for base in reversed(range(0, tensor, 2)):
            some = [side[base : base + 2] for side in w_attn]
            now = attend_back(core_word, tables, d_attn, some, base, waits, *heads)
            d_qkv.insert(0, now)
            waits = hook(now)
        parts = model_rows(model_kernel(QKV, 2), "attn_back", d_qkv, w_attn, waits)
        operands = (gain, layer_input, *parts, d_hidden)
        d_input, sum_zero = on_chip(
            out_of_layer_kernel, "out_of_layer", (row16, sum32), *operands, waits=hook()
        )
        sums = jnp.concatenate([sum_zero, sum_one, sum_two, sum_three])
        return d_input, (d_qkv, d_attn, d_up, d_down), sums

    low_zero, saved_zero, lefts_zero = forward(
        start,
        (
            (up_piece, up_other[0], down_other[0]),
            (up_own[1], down_own[1]),
            (up_own[2], down_own[2], up_other[1], down_other[1]),
            (up_own[3], down_own[3], up_other[2], down_other[2]),
        ),
    )
    low_one, saved_one, lefts_one = forward(shifted(low_zero, "section", 1), ((),) * 4)
    grad_one, rights_one, gain_one = backward(start, saved_one, lambda *new: ())
    received = shifted(grad_one, "section", -1)

    lows = lax.optimization_barrier((low_zero, low_one, grad_one))[:2]
    lows = own_first(jnp.where(first, *lows)).reshape(tensor, part, width)
    lows = lax.all_to_all(lows, "tensor", 0, 0, tiled=True)

    section_word = lax.axis_index("section").astype(jnp.int32).reshape(1)

    def mlp_leaves(base, waits=()):
        zeros = (*lefts_zero[2], d_up, lefts_zero[3], *d_down)
        ones = (*lefts_one[2], rights_one[2], lefts_one[3], *rights_one[3])
        mlp_sums[base : base + 2] = weight_grads(
            mlp_grads_kernel,
            "mlp_grads",
            base,
            section_word,
            zeros,
            ones,
            (wide_half + unit, unit),
            (2 * unit, 2 * unit),
            waits,
        )

    def attn_leaves(base, d_qkv, waits):
        zeros = (*lefts_zero[0], d_qkv, lefts_zero[1], *d_attn)
        ones = (*lefts_one[0], rights_one[0][base // 2], lefts_one[1], *rights_one[1])
        attn_sums[base : base + 2] = weight_grads(
            attn_grads_kernel,
            "attn_grads",
            base,
            section_word,
            zeros,
            ones,
            (wide_half, 512),
            (768, 256),
            waits,
        )

    def moves_on(piece, *moved, waits=()):
        outs = ((piece[1].shape, jnp.bfloat16),)
        (total,) = on_chip(moved_kernel, "moved", outs, *piece, *moved, waits=waits)
        return total, passed_on(total, -1)

    mlp_sums, attn_sums = [None] * tensor, [None] * tensor
    mlp_moves, attn_moves = [None] * tensor, [None] * tensor
    hooks = iter(range(6))

    def hook(*new):
        nonlocal d_down, d_up, d_attn, outputs
        turn = next(hooks)
        if turn == 0:
            d_down, d_up = new
            mlp_leaves(2)
            return (mlp_sums[3][0],)
        if turn == 1:
            return ()
        if turn == 2:
            (d_attn,) = new
            outputs = from_chip(lows, d_attn[:1])
            total, mlp_moves[3] = moves_on(mlp_sums[3], waits=(outputs,))
            mlp_leaves(0, (total,))
            return (mlp_sums[1][0],)
        if turn == 3:
            total, mlp_moves[2] = moves_on(mlp_sums[2], mlp_moves[3], waits=new)
            attn_leaves(2, new[0], (total,))
            return (mlp_sums[2][1], mlp_moves[3], attn_sums[3][0])
        if turn == 4:
            total, mlp_moves[1] = moves_on(mlp_sums[1], mlp_moves[2], waits=new)
            attn_leaves(0, new[0], (total,))
            total, attn_moves[3] = moves_on(attn_sums[3], waits=attn_sums[1][:1])
            return (total, mlp_moves[1], mlp_sums[0][1])
        return attn_sums[2][1:]

    d_down = d_up = d_attn = outputs = None
    grad_zero, rights_zero, gain_zero = backward(received, saved_zero, hook, (lows,))
    place_word = jnp.stack([lax.axis_index("section"), upper]).astype(jnp.int32)
    (grads,) = with_core(
        chosen_kernel,
        "chosen",
        place_word,
        (row16,),
        grad_zero,
        grad_one,
        waits=(attn_moves[3], attn_sums[1][1]),
    )
    grads = lax.all_to_all(grads.reshape(tensor, part, width), "tensor", 0, 0, tiled=True)

    block32 = ((wide_half // 2, unit), jnp.float32)
    down32 = ((unit, wide_half // 2), jnp.float32)
    up_keep, down_keep, up_send, down_send = with_core(
        mlp_sum_kernel,
        "mlp_sum",
        core_word,
        (block32, down32, block32, down32),
        *mlp_sums[0],
        mlp_moves[1],
        waits=(grad_zero,),
    )
    outs = (
        ((wide_half // 2, 2 * unit), jnp.float32),
        ((2 * unit, wide_half // 2), jnp.float32),
    )
    sent = flip_pairs(up_send, 1), flip_pairs(down_send, 1)
    up_grad, down_grad = with_core(
        mlp_join_kernel, "mlp_join", core_word, outs, up_keep, down_keep, *sent
    )
    total, attn_moves[2] = moves_on(attn_sums[2], attn_moves[3], waits=(grad_zero,))
    waits = (up_grad, attn_sums[0][1], grads)
    last, attn_moves[1] = moves_on(attn_sums[1], attn_moves[2], waits=waits)
    grads = from_chip(grads, (last,))
    gain_total = own_first(jnp.where(first, gain_zero, gain_one))
    count = tensor * lax.axis_size("dp")
    gain_parts = gain_total.reshape(4, count, width // count).swapaxes(0, 1)
    outs = ((gain_parts.shape, gain_parts.dtype),)
    (gain_parts,) = on_chip(gate_kernel, "gate", outs, gain_parts, waits=(last,))
    gain_parts = lax.all_to_all(gain_parts, ("dp", "tensor"), 0, 0, tiled=True)
    gains_grad = jnp.sum(gain_parts, axis=0)
    outs = (((wide_half // 2, 512), jnp.float32),) * 2
    keep, send = with_core(
        last_sum_kernel,
        "attn_sum",
        core_word,
        outs,
        *attn_sums[0],
        attn_moves[1],
        waits=(grads, outputs, gains_grad),
    )
    spots = tuple((i * 128, (i + 1) * 128, i * 256) for i in range(3))
    outs = (((wide_half // 2, 768), jnp.float32), ((256, wide_half // 2), jnp.float32))
    kernel = functools.partial(joined_kernel, spots)
    qkv_grad, out_grad = with_core(
        kernel, "attn_join", core_word, outs, keep, flip_pairs(send, 1)
    )
    qkv_grad = qkv_grad.reshape(wide_half // 2, 3, -1)

    return (
        outputs[None],
        grads[None],
        gains_grad[None],
        qkv_grad[None],
        out_grad[None],
        up_grad[None],
        down_grad[None],
    )


def takes_chips(sizes):
    return sizes["section"] == 2 and sizes["dp"] == 4 and sizes["tensor"] == 4


def solution(mesh):
    placed = (
        P("dp", "tensor", None),
        P("dp", "tensor", None),
        P("dp", "tensor"),
        P(),
        P("section", None, None),
        P("section", None, None, "tensor"),
        P("section", "tensor", None),
        P("section", None, "tensor"),
        P("section", "tensor", None),
    )
    body = per_chip if takes_chips(dict(mesh.shape)) else per_device
    return jax.shard_map(
        body,
        mesh=mesh,
        in_specs=placed,
        out_specs=(
            P("section", "dp", "tensor", None),
            P("section", "dp", "tensor", None),
            P("section", None, ("dp", "tensor")),
            P("section", "dp", None, "tensor"),
            P("section", "tensor", "dp"),
            P("section", "dp", "tensor"),
            P("section", "tensor", "dp"),
        ),
        check_vma=False,
    )
```

```python
import functools
import math

import jax
import jax.numpy as jnp
from jax import lax
from jax.experimental import pallas as pl
from jax.experimental.pallas import tpu as pltpu
from jax.sharding import PartitionSpec as P

HEAD_DIM = 64


NORM_EPSILON = 1e-06
TILE = 128
PAIR_WORK = 1024
MODEL_HALF = 512
QKV = slice(0, 384)
OUT = slice(384, 512)
CHUNK = 32
KERNEL_VMEM = 20 << 20
ROWS_VMEM = 3 << 20


def shifted(block, axis, distance):
    devices = range(lax.axis_size(axis))
    route = [(i - distance, i) for i in devices if i - distance in devices]
    return lax.ppermute(block, axis, route)


def norm_rows(vector, weight_gain):
    return (
        vector
        * lax.rsqrt(jnp.mean(vector * vector, axis=-1, keepdims=True) + NORM_EPSILON)
        * weight_gain
    )


def rotary_tables(seq_len, head_width):
    half_width = head_width // 2
    freqs = 10000.0 ** (-2.0 * jnp.arange(half_width, dtype=jnp.float32) / head_width)
    angles = jnp.arange(seq_len, dtype=jnp.float32)[:, None] * freqs[None, :]
    return (jnp.cos(angles), jnp.sin(angles))


def rotate(vector, cos_table, sin_table):
    first_half, second_half = jnp.split(vector, 2, axis=-1)
    cos_part = cos_table[:, None, :]
    sin_part = sin_table[:, None, :]
    return jnp.concatenate(
        [
            first_half * cos_part - second_half * sin_part,
            second_half * cos_part + first_half * sin_part,
        ],
        axis=-1,
    )


def contract(left_rows, right_rows):
    return lax.dot_general(
        left_rows, right_rows, (((0,), (0,)), ((), ())), preferred_element_type=jnp.float32
    )


def gather_rows(row_values, weight):

    def project(shard_rows, offset):
        return (shard_rows, jnp.dot(shard_rows, weight, preferred_element_type=jnp.float32))

    return project(lax.all_gather(row_values, "tensor", axis=0, tiled=True), jnp.int32(0))


def scatter_rows(row_values, weight, row_count):

    def partial_term(offset, span):
        return jnp.dot(row_values, weight, preferred_element_type=jnp.float32)

    return lax.psum_scatter(
        partial_term(jnp.int32(0), lax.axis_size("tensor") * row_count),
        "tensor",
        scatter_dimension=0,
        tiled=True,
    )


def gather_grads(row_values, weight):

    def project(shard_rows, offset):
        return (shard_rows, jnp.dot(shard_rows, weight.T, preferred_element_type=jnp.float32))

    return project(lax.all_gather(row_values, "tensor", axis=0, tiled=True), jnp.int32(0))


def scatter_grads(row_values, weight, row_count):

    def partial_term(offset, span):
        return jnp.dot(row_values, weight.T, preferred_element_type=jnp.float32)

    return lax.psum_scatter(
        partial_term(jnp.int32(0), lax.axis_size("tensor") * row_count),
        "tensor",
        scatter_dimension=0,
        tiled=True,
    )


def attention_probs(queries, key_rows):
    scores = jnp.einsum(
        "qhd,khd->hqk", queries, key_rows, preferred_element_type=jnp.float32
    ) * HEAD_DIM ** (-0.5)
    length = queries.shape[0]
    positions = jnp.arange(length, dtype=jnp.int32)
    causal = positions[:, None] >= positions[None, :]
    scores = jnp.where(causal[None], scores, -1e30)
    expos = jnp.exp(scores - jnp.max(scores, axis=-1, keepdims=True))
    return expos / jnp.sum(expos, axis=-1, keepdims=True)


def layer_forward(layer_input, weights):
    gains, w_qkv, w_out, w_up, w_down = weights
    row_count, model_width = layer_input.shape
    attn_in = norm_rows(layer_input, gains[0]).astype(jnp.bfloat16)
    gathered_a, qkv = gather_rows(attn_in, w_qkv.reshape(model_width, -1))
    length = qkv.shape[0]
    head_count = w_qkv.shape[2] // HEAD_DIM
    qkv = qkv.reshape(length, 3, head_count, HEAD_DIM)
    cos_table, sin_table = rotary_tables(length, HEAD_DIM)
    queries = rotate(qkv[:, 0], cos_table, sin_table).astype(jnp.bfloat16)
    key_rows = rotate(qkv[:, 1], cos_table, sin_table).astype(jnp.bfloat16)
    values = qkv[:, 2].astype(jnp.bfloat16)
    attn_probs = attention_probs(queries, key_rows).astype(jnp.bfloat16)
    mixed = jnp.einsum("hqk,khd->qhd", attn_probs, values, preferred_element_type=jnp.float32)
    mixed = mixed.reshape(length, -1).astype(jnp.bfloat16)
    attn_branch = scatter_rows(mixed, w_out, row_count)
    hidden = layer_input + norm_rows(attn_branch, gains[1])
    mlp_in = norm_rows(hidden, gains[2]).astype(jnp.bfloat16)
    gathered_c, up_act = gather_rows(mlp_in, w_up)
    gelu_out = jax.nn.gelu(up_act, approximate=True).astype(jnp.bfloat16)
    down_branch = scatter_rows(gelu_out, w_down, row_count)
    result = hidden + norm_rows(down_branch, gains[3])
    kept_values = (
        gathered_a,
        queries,
        key_rows,
        values,
        mixed,
        attn_branch,
        hidden,
        gathered_c,
        up_act,
        gelu_out,
        down_branch,
    )
    return (result, kept_values)


def layer_backward(layer_input, grad_result, kept_values, weights):
    gains, w_qkv, w_out, w_up, w_down = weights
    (
        gathered_a,
        queries,
        key_rows,
        values,
        mixed,
        attn_branch,
        hidden,
        gathered_c,
        up_act,
        gelu_out,
        down_branch,
    ) = kept_values
    row_count, model_width = layer_input.shape
    pullback = jax.vjp(norm_rows, down_branch, gains[3])[1]
    grad_down, gain_three = pullback(grad_result)
    gathered_dd, grad_gelu = gather_grads(grad_down.astype(jnp.bfloat16), w_down)
    down_total = contract(gelu_out, gathered_dd)
    pullback = jax.vjp(lambda vector: jax.nn.gelu(vector, approximate=True), up_act)[1]
    grad_up = pullback(grad_gelu)[0].astype(jnp.bfloat16)
    up_total = contract(gathered_c, grad_up)
    grad_mlp = scatter_grads(grad_up, w_up, row_count)
    pullback = jax.vjp(norm_rows, hidden, gains[2])[1]
    grad_norm_mlp, gain_two = pullback(grad_mlp)
    grad_hidden = grad_result + grad_norm_mlp
    pullback = jax.vjp(norm_rows, attn_branch, gains[1])[1]
    grad_attn, gain_one = pullback(grad_hidden)
    gathered_da, grad_mixed = gather_grads(grad_attn.astype(jnp.bfloat16), w_out)
    out_total = contract(mixed, gathered_da)
    length = grad_mixed.shape[0]
    head_count = w_qkv.shape[2] // HEAD_DIM
    grad_mixed = grad_mixed.astype(jnp.bfloat16).reshape(length, head_count, HEAD_DIM)
    attn_probs = attention_probs(queries, key_rows)
    probs_low = attn_probs.astype(jnp.bfloat16)
    grad_probs = jnp.einsum("qhd,khd->hqk", grad_mixed, values, preferred_element_type=jnp.float32)
    grad_values = jnp.einsum(
        "hqk,qhd->khd", probs_low, grad_mixed, preferred_element_type=jnp.float32
    )
    row_dots = jnp.sum(grad_probs * attn_probs, axis=-1, keepdims=True)
    grad_scores = (attn_probs * (grad_probs - row_dots)).astype(jnp.bfloat16)
    scale_value = HEAD_DIM ** (-0.5)
    grad_queries = (
        jnp.einsum("hqk,khd->qhd", grad_scores, key_rows, preferred_element_type=jnp.float32)
        * scale_value
    )
    grad_keys = (
        jnp.einsum("hqk,qhd->khd", grad_scores, queries, preferred_element_type=jnp.float32)
        * scale_value
    )
    cos_table, sin_table = rotary_tables(length, HEAD_DIM)
    pullback = jax.vjp(lambda vector: rotate(vector, cos_table, sin_table), grad_queries)[1]
    grad_q_raw = pullback(grad_queries)[0]
    grad_k_raw = pullback(grad_keys)[0]
    grad_qkv = (
        jnp.stack([grad_q_raw, grad_k_raw, grad_values], axis=1)
        .reshape(length, -1)
        .astype(jnp.bfloat16)
    )
    qkv_total = contract(gathered_a, grad_qkv).reshape(model_width, 3, -1)
    grad_attn_in = scatter_grads(grad_qkv, w_qkv.reshape(model_width, -1), row_count)
    pullback = jax.vjp(norm_rows, layer_input, gains[0])[1]
    grad_norm_in, gain_zero = pullback(grad_attn_in)
    grad_input = grad_hidden + grad_norm_in
    gain_total = jnp.stack([gain_zero, gain_one, gain_two, gain_three])
    return (grad_input, (gain_total, qkv_total, out_total, up_total, down_total))


def lagged(first_section, stacked):
    blank = jnp.zeros_like(stacked[:1])
    earlier = jnp.concatenate([blank, stacked[:-1]])
    later = jnp.concatenate([stacked[1:], blank])
    return jnp.where(first_section, earlier, later)


def per_device(
    inputs,
    out_cotangent,
    group_ids,
    group_weights,
    gains,
    qkv_weight,
    out_weight,
    up_weight,
    down_weight,
):
    weights = (gains[0], qkv_weight[0], out_weight[0], up_weight[0], down_weight[0])
    micro_count, row_count, model_width = inputs.shape
    first_section = lax.axis_index("section") == 0
    group_count = group_weights.shape[0]
    matches = group_ids[..., None] == jnp.arange(group_count, dtype=jnp.int32)
    row_scale = jnp.sum(jnp.where(matches, group_weights, 0.0), axis=-1)
    scaled = out_cotangent.astype(jnp.float32) * row_scale[..., None]
    padded = jnp.concatenate([inputs, jnp.zeros((1, row_count, model_width), jnp.bfloat16)])

    def forward_tick(received, fresh_input):
        layer_input = jnp.where(first_section, fresh_input, received)
        result, kept_values = layer_forward(layer_input.astype(jnp.float32), weights)
        result_low = result.astype(jnp.bfloat16)
        outgoing = shifted(result_low, "section", 1)
        stashed = ()
        return (outgoing, (layer_input, result_low, stashed))

    start_rows = jnp.zeros((row_count, model_width), jnp.bfloat16)
    _, (layer_inputs, layer_results, stashed) = lax.scan(forward_tick, start_rows, padded)
    layer_outputs = jnp.where(first_section, layer_results[:-1], layer_results[1:])[None]
    back_inputs = lagged(first_section, layer_inputs)
    back_stash = jax.tree.map(lambda stacked: lagged(first_section, stacked), stashed)
    grad_padded = jnp.concatenate([scaled, jnp.zeros((1, row_count, model_width), jnp.float32)])
    tick_index = jnp.arange(micro_count + 1, dtype=jnp.int32)
    tick_valid = jnp.where(first_section, tick_index >= 1, tick_index < micro_count).astype(
        jnp.float32
    )

    def backward_tick(carry, step_item):
        received, totals = carry
        layer_input, cotangent, valid_now, stash_now = step_item
        grad_now = jnp.where(first_section, received.astype(jnp.float32), cotangent)
        input_now = layer_input.astype(jnp.float32)
        kept_values = layer_forward(input_now, weights)[1]
        grad_input, layer_grads = layer_backward(input_now, grad_now, kept_values, weights)
        totals = jax.tree.map(lambda total, update: total + valid_now * update, totals, layer_grads)
        grad_low = grad_input.astype(jnp.bfloat16)
        outgoing = shifted(grad_low, "section", -1)
        return ((outgoing, totals), grad_low)

    start_totals = (
        jnp.zeros((4, model_width), jnp.float32),
        jnp.zeros(qkv_weight.shape[1:], jnp.float32),
        jnp.zeros(out_weight.shape[1:], jnp.float32),
        jnp.zeros(up_weight.shape[1:], jnp.float32),
        jnp.zeros(down_weight.shape[1:], jnp.float32),
    )
    (_, totals), grad_lows = lax.scan(
        backward_tick,
        (start_rows, start_totals),
        (back_inputs, grad_padded, tick_valid, back_stash),
    )
    input_grads = jnp.where(first_section, grad_lows[1:], grad_lows[:-1])[None]
    gain_total, qkv_total, out_total, up_total, down_total = totals
    gains_grad = lax.psum_scatter(gain_total, ("dp", "tensor"), scatter_dimension=1, tiled=True)
    qkv_grad, out_grad, up_grad, down_grad = (
        lax.psum_scatter(
            qkv_total.astype(jnp.bfloat16), "dp", scatter_dimension=0, tiled=True
        ).astype(jnp.float32),
        lax.psum_scatter(
            out_total.astype(jnp.bfloat16), "dp", scatter_dimension=1, tiled=True
        ).astype(jnp.float32),
        lax.psum_scatter(
            up_total.astype(jnp.bfloat16), "dp", scatter_dimension=0, tiled=True
        ).astype(jnp.float32),
        lax.psum_scatter(
            down_total.astype(jnp.bfloat16), "dp", scatter_dimension=1, tiled=True
        ).astype(jnp.float32),
    )
    return (
        layer_outputs,
        input_grads,
        gains_grad[None],
        qkv_grad[None],
        out_grad[None],
        up_grad[None],
        down_grad[None],
    )


def rotated(block, cos_rows, sin_rows):
    lane = lax.broadcasted_iota(jnp.int32, block.shape, 1)
    ahead = pltpu.roll(block, 96, 1)
    behind = pltpu.roll(block, 32, 1)
    swapped = jnp.where(lane % 64 < 32, ahead, behind)
    return block * cos_rows + swapped * sin_rows


def dot_nt(left, right):
    return lax.dot_general(
        left, right, (((1,), (1,)), ((), ())), preferred_element_type=jnp.float32
    )


def dot_nn(left, right):
    return jnp.dot(left, right, preferred_element_type=jnp.float32)


def model_weight(owns, others, cols):
    sides = [jnp.concatenate([ref[:, cols] for ref in refs], axis=1) for refs in (owns, others)]
    return jnp.concatenate(sides, axis=0)


def stacked_up(values):
    return jnp.concatenate(values, axis=0)


def edge_masks(core, rows):
    key = lax.broadcasted_iota(jnp.int32, (rows, 2 * rows), 0)
    query = lax.broadcasted_iota(jnp.int32, (rows, 2 * rows), 1)
    mine = query < rows
    place = jnp.where(mine, query + core * rows, query - rows + (1 - core) * rows)
    return (key + core * rows <= place, key + (1 - core) * rows <= place)


def both_sides(value, half, start, stop, axis=0):
    if axis == 0:
        return jnp.concatenate([value[start:stop], value[half + start : half + stop]], axis=0)
    return jnp.concatenate([value[:, start:stop], value[:, half + start : half + stop]], axis=1)


def hidden_scores(scores, masks, tile, step):
    seen = step * tile
    pieces = []
    for side in range(2):
        base = side * (seen + tile)
        if seen:
            pieces.append(scores[base : base + seen])
        pieces.append(jnp.where(masks[side], scores[base + seen : base + seen + tile], -1e30))
    return jnp.concatenate(pieces, axis=0)


def one_head(rows, head):
    lane = lax.broadcasted_iota(jnp.int32, rows.shape, 1)
    return jnp.where(lane // 64 == head, rows, jnp.zeros_like(rows))


def pick_piece(weight, owns, others, cols):
    for j, (own, other) in enumerate(zip(owns, others)):

        @pl.when(pl.program_id(0) == j)
        def _():
            size = own.shape[0]
            weight[:size] = own[:, cols]
            weight[size:] = other[:, cols]


def attend_kernel(pieces, core_ref, cos_ref, sin_ref, own_rows, other_rows, *refs):
    owns, others = refs[:pieces], refs[pieces : 2 * pieces]
    q_ref, k_ref, v_ref, lse_ref, mix_ref, weight = refs[2 * pieces :]
    half = own_rows.shape[0]
    tile = TILE
    pick_piece(weight, owns, others, QKV)
    proj = dot_nn(stacked_up([own_rows[...], other_rows[...]]), weight[...])
    cos_rows, sin_rows = cos_ref[...], sin_ref[...]
    q = (rotated(proj[:, :128], cos_rows, sin_rows) * HEAD_DIM ** (-0.5)).astype(jnp.bfloat16)
    k = rotated(proj[:, 128:256], cos_rows, sin_rows).astype(jnp.bfloat16)
    v32 = proj[:, 256:]
    q_ref[0] = q
    k_ref[0] = k
    v_ref[0] = v32.astype(jnp.bfloat16)
    v_flip = v32.T.astype(jnp.bfloat16)
    masks = edge_masks(core_ref[0], tile)

    def scored(step, head):
        stop = (step + 1) * tile
        q_head = one_head(both_sides(q, half, step * tile, stop), head)
        return hidden_scores(dot_nt(both_sides(k, half, 0, stop), q_head), masks, tile, step)

    units = [(step, head) for step in range(half // tile) for head in range(2)]
    ahead = scored(*units[0])
    outs = []
    for spot, (step, head) in enumerate(units):
        scores = ahead
        if spot + 1 < len(units):
            ahead = scored(*units[spot + 1])
        stop = (step + 1) * tile
        top = jnp.max(scores, axis=0, keepdims=True)
        expos = jnp.exp(scores - top)
        total = jnp.sum(expos, axis=0, keepdims=True)
        lse = top + jnp.log(total)
        lse_ref[0, head : head + 1, step * tile : stop] = lse[:, :tile]
        lse_ref[0, head : head + 1, half + step * tile : half + stop] = lse[:, tile:]
        v_cols = both_sides(v_flip, half, 0, stop, axis=1)
        out = dot_nn(v_cols[64 * head : 64 * head + 64], expos.astype(jnp.bfloat16))
        outs.append(out * (1.0 / total))
        if head == 1:
            mixed = jnp.concatenate(outs, axis=0).T.astype(jnp.bfloat16)
            outs = []
            mix_ref[step * tile : stop, :] = mixed[:tile]
            mix_ref[half + step * tile : half + stop, :] = mixed[tile:]


def attend_back_kernel(pieces, core_ref, cos_ref, sin_ref, own_rows, other_rows, *refs):
    owns, others = refs[:pieces], refs[pieces : 2 * pieces]
    q_ref, k_ref, v_ref, lse_ref, out_ref, weight, dq, dk, dv = refs[2 * pieces :]
    half = own_rows.shape[0]
    tile = TILE
    pick_piece(weight, owns, others, OUT)
    rows = stacked_up([own_rows[...], other_rows[...]])
    d_mixed = dot_nn(rows, weight[...]).astype(jnp.bfloat16)
    q, k, v = q_ref[0], k_ref[0], v_ref[0]
    k_flip = k.astype(jnp.float32).T.astype(jnp.bfloat16)
    masks = edge_masks(core_ref[0], tile)
    steps = half // tile

    def scored(step, head):
        stop = (step + 1) * tile
        q_head = one_head(both_sides(q, half, step * tile, stop), head)
        g_head = one_head(both_sides(d_mixed, half, step * tile, stop), head)
        scores = hidden_scores(dot_nt(both_sides(k, half, 0, stop), q_head), masks, tile, step)
        return q_head, g_head, scores, dot_nt(both_sides(v, half, 0, stop), g_head)

    units = [(step, head) for step in reversed(range(steps)) for head in range(2)]
    ahead = scored(*units[0])
    dq_flips = []
    dk_sum = dv_sum = None
    for spot, (step, head) in enumerate(units):
        q_head, g_head, scores, d_probs = ahead
        if spot + 1 < len(units):
            ahead = scored(*units[spot + 1])
        stop = (step + 1) * tile
        lse = both_sides(lse_ref[0], half, step * tile, stop, axis=1)
        probs = jnp.exp(scores - lse[head : head + 1])
        dots = jnp.sum(probs * d_probs, axis=0, keepdims=True)
        d_scores = (probs * (d_probs - dots)).astype(jnp.bfloat16)
        dv_part = dot_nn(probs.astype(jnp.bfloat16), g_head)
        dk_part = dot_nn(d_scores, q_head)
        k_cols = both_sides(k_flip, half, 0, stop, axis=1)
        dq_flips.append(dot_nn(k_cols[64 * head : 64 * head + 64], d_scores))
        if head == 0:
            dv_sum, dk_sum = dv_part, dk_part
            continue
        dv_sum, dk_sum = dv_sum + dv_part, dk_sum + dk_part
        dq_rows = jnp.concatenate(dq_flips, axis=0).T * HEAD_DIM ** (-0.5)
        dq_flips = []
        dq[step * tile : stop] = dq_rows[:tile]
        dq[half + step * tile : half + stop] = dq_rows[tile:]
        for base, part in ((0, slice(0, stop)), (half, slice(stop, 2 * stop))):
            if step == steps - 1:
                dk[base : base + stop] = dk_sum[part]
                dv[base : base + stop] = dv_sum[part]
            else:
                dk[base : base + stop] += dk_sum[part]
                dv[base : base + stop] += dv_sum[part]
    cos_rows, sin_rows = cos_ref[...], -sin_ref[...]
    out_ref[:, :128] = rotated(dq[...], cos_rows, sin_rows).astype(jnp.bfloat16)
    out_ref[:, 128:256] = rotated(dk[...], cos_rows, sin_rows).astype(jnp.bfloat16)
    out_ref[:, 256:] = dv[...].astype(jnp.bfloat16)


def split_rows(total, own_ref, other_ref):
    half = own_ref.shape[0]
    own_ref[...] = total[:half]
    other_ref[...] = total[half:].astype(jnp.bfloat16)


def to_model_kernel(lefts, pieces, cols, *refs):
    left, refs = jnp.concatenate([ref[...] for ref in refs[:lefts]], axis=1), refs[lefts:]
    weight = model_weight(refs[:pieces], refs[pieces : 2 * pieces], cols)
    split_rows(dot_nt(left, weight), *refs[2 * pieces :])


def mlp_down_kernel(pieces, left_ref, *refs):
    sides = [stacked_up([ref[...] for ref in side]) for side in (refs[:pieces], refs[pieces:-2])]
    split_rows(dot_nn(left_ref[...], jnp.concatenate(sides, axis=1)), *refs[-2:])


def gelu_both(up_act):
    root = math.sqrt(2.0 / math.pi)
    square = up_act * up_act
    rise = 0.5 + 0.5 * jnp.tanh(up_act * (root + root * 0.044715 * square))
    value = up_act * rise
    slope = rise + value * (1.0 - rise) * (2.0 * root + 6.0 * root * 0.044715 * square)
    return value, slope


def mlp_up_kernel(pieces, own_rows, other_rows, *refs):
    owns, others = refs[:pieces], refs[pieces : 2 * pieces]
    gelu_ref, slope_ref = refs[2 * pieces :]
    half = own_rows.shape[0]
    size = owns[0].shape[1]
    step = half // 2
    units = [(j, i) for j in range(pieces) for i in range(4)]

    def product(j, i):
        rows = (own_rows, other_rows)[i // 2][i % 2 * step : (i % 2 + 1) * step]
        return dot_nn(rows, stacked_up([owns[j][...], others[j][...]]))

    ahead = product(*units[0])
    for spot, (j, i) in enumerate(units):
        up_act = ahead
        if spot + 1 < len(units):
            ahead = product(*units[spot + 1])
        value, slope = gelu_both(up_act)
        gelu_ref[i * step : (i + 1) * step, j * size : (j + 1) * size] = value.astype(jnp.bfloat16)
        slope_ref[i * step : (i + 1) * step, j * size : (j + 1) * size] = slope.astype(
            jnp.bfloat16
        )


def mlp_up_back_kernel(pieces, own_rows, other_rows, slope_ref, *refs):
    owns, others = refs[:pieces], refs[pieces : 2 * pieces]
    out_ref, weight, slope, sems = refs[2 * pieces :]
    half = own_rows.shape[1] // 2
    size = owns[0].shape[0]
    order = list(reversed(range(pieces)))
    copies = []
    for j in order:
        sources = (owns[j], others[j], slope_ref.at[:, pl.ds(j * size, size)])
        targets = (
            weight.at[j, :, pl.ds(0, half)],
            weight.at[j, :, pl.ds(half, half)],
            slope.at[:, pl.ds(j * size, size)],
        )
        copies.append(
            [
                pltpu.make_async_copy(source, target, sems.at[j, i])
                for i, (source, target) in enumerate(zip(sources, targets))
            ]
        )
        for copy in copies[-1]:
            copy.start()
    rows = stacked_up([own_rows[...], other_rows[...]])
    for j, arriving in zip(order, copies):
        cols = slice(j * size, (j + 1) * size)
        for copy in arriving:
            copy.wait()
        d_gelu = dot_nt(rows, weight[j])
        out_ref[:, cols] = (d_gelu * slope[:, cols].astype(jnp.float32)).astype(jnp.bfloat16)


def inverse_size(rows):
    return lax.rsqrt(jnp.mean(rows * rows, axis=-1, keepdims=True) + NORM_EPSILON)


def norm_back(rows, gain, grad):
    scale = inverse_size(rows)
    weighted = grad * gain
    inner = jnp.mean(rows * weighted, axis=-1, keepdims=True)
    return scale * weighted - rows * (scale * scale * scale * inner), rows * scale * grad


def folded(rows):
    return jnp.sum(rows.reshape(rows.shape[0] // 8, 8, rows.shape[1]), axis=0)


def wide(ref, spot):
    return ref[spot, :].astype(jnp.float32)


def by_chunks(count, body, sums=0, width=0):
    def one(i, carry):
        more = body(pl.ds(pl.multiple_of(i * CHUNK, CHUNK), CHUNK))
        return tuple(old + folded(new) for old, new in zip(carry, more))

    start = tuple(jnp.zeros((8, width), jnp.float32) for _ in range(sums))
    totals = lax.fori_loop(0, count // CHUNK, one, start)
    return [jnp.sum(total, axis=0, keepdims=True) for total in totals]


def norm_in_kernel(gain_ref, rows_ref, out_ref):
    def body(spot):
        rows = wide(rows_ref, spot)
        out_ref[spot, :] = (rows * inverse_size(rows) * gain_ref[0:1]).astype(jnp.bfloat16)
        return ()

    by_chunks(rows_ref.shape[0], body)


def after_attention_kernel(
    gain_ref, rows_ref, own_ref, other_ref, branch_ref, hidden_ref, out_ref
):
    def body(spot):
        branch = own_ref[spot, :] + wide(other_ref, spot)
        hidden = wide(rows_ref, spot) + branch * inverse_size(branch) * gain_ref[1:2]
        branch_ref[spot, :] = branch
        hidden_ref[spot, :] = hidden
        out_ref[spot, :] = (hidden * inverse_size(hidden) * gain_ref[2:3]).astype(jnp.bfloat16)
        return ()

    by_chunks(rows_ref.shape[0], body)


def after_mlp_kernel(gain_ref, hidden_ref, own_ref, other_ref, branch_ref, out_ref):
    def body(spot):
        branch = own_ref[spot, :] + wide(other_ref, spot)
        branch_ref[spot, :] = branch
        result = hidden_ref[spot, :] + branch * inverse_size(branch) * gain_ref[3:4]
        out_ref[spot, :] = result.astype(jnp.bfloat16)
        return ()

    by_chunks(hidden_ref.shape[0], body)


def into_mlp_back_kernel(gain_ref, grad_ref, branch_ref, out_ref, sum_ref):
    def body(spot):
        d_rows, d_gain = norm_back(branch_ref[spot, :], gain_ref[3:4], wide(grad_ref, spot))
        out_ref[spot, :] = d_rows.astype(jnp.bfloat16)
        return (d_gain,)

    (sum_ref[...],) = by_chunks(grad_ref.shape[0], body, 1, grad_ref.shape[1])


def into_attention_back_kernel(
    gain_ref, grad_ref, own_ref, other_ref, hidden_ref, branch_ref, d_hidden_ref, out_ref, *sums
):
    def body(spot):
        d_rows = own_ref[spot, :] + wide(other_ref, spot)
        d_rows, d_gain = norm_back(hidden_ref[spot, :], gain_ref[2:3], d_rows)
        d_hidden = wide(grad_ref, spot) + d_rows
        d_hidden_ref[spot, :] = d_hidden
        d_rows, d_first = norm_back(branch_ref[spot, :], gain_ref[1:2], d_hidden)
        out_ref[spot, :] = d_rows.astype(jnp.bfloat16)
        return (d_first, d_gain)

    totals = by_chunks(grad_ref.shape[0], body, 2, grad_ref.shape[1])
    sums[0][...], sums[1][...] = totals


def out_of_layer_kernel(gain_ref, rows_ref, own_ref, other_ref, d_hidden_ref, out_ref, sum_ref):
    def body(spot):
        d_rows = own_ref[spot, :] + wide(other_ref, spot)
        d_rows, d_gain = norm_back(wide(rows_ref, spot), gain_ref[0:1], d_rows)
        out_ref[spot, :] = (d_hidden_ref[spot, :] + d_rows).astype(jnp.bfloat16)
        return (d_gain,)

    (sum_ref[...],) = by_chunks(rows_ref.shape[0], body, 1, rows_ref.shape[1])


def work(flops, arrays):
    size = sum(math.prod(array.shape) * jnp.dtype(array.dtype).itemsize for array in arrays)
    return pl.CostEstimate(flops=flops, bytes_accessed=size, transcendentals=0)


def far(array):
    return pltpu.with_memory_space_constraint(array, pltpu.HBM)


def without(kernel, first, count):
    return lambda *refs: kernel(*refs[:first], *refs[first + count :])


def on_chip(kernel, name, outs, *operands, limit=ROWS_VMEM, flops=0, waits=()):
    shapes = [jax.ShapeDtypeStruct(shape, dtype) for shape, dtype in outs]
    space = pl.BlockSpec(memory_space=pltpu.VMEM)
    return pl.pallas_call(
        without(kernel, len(operands), len(waits)),
        in_specs=[space] * len(operands) + [pl.BlockSpec(memory_space=pl.ANY)] * len(waits),
        out_specs=[space] * len(outs),
        out_shape=shapes,
        compiler_params=pltpu.CompilerParams(vmem_limit_bytes=limit),
        cost_estimate=work(flops, (*operands, *shapes)),
        name=name,
    )(*operands, *map(far, waits))


def whole_block(array):
    return pl.BlockSpec(array.shape, lambda j: (0,) * array.ndim)


def by_pairs(kernel, name, core, operands, pieces, blocks, outs, scratch, flops, waits):
    shapes = [jax.ShapeDtypeStruct(shape, dtype) for shape, dtype, _ in outs]
    taken = 1 + len(operands) + 2 * len(pieces[0]) + len(blocks)
    return pl.pallas_call(
        without(functools.partial(kernel, len(pieces[0])), taken, len(waits)),
        grid=(len(pieces[0]),),
        in_specs=[pl.BlockSpec(memory_space=pltpu.SMEM)]
        + [whole_block(array) for array in (*operands, *pieces[0], *pieces[1])]
        + [spec for _, spec in blocks]
        + [pl.BlockSpec(memory_space=pl.ANY)] * len(waits),
        out_specs=[spec for _, _, spec in outs],
        out_shape=shapes,
        scratch_shapes=scratch,
        compiler_params=pltpu.CompilerParams(vmem_limit_bytes=KERNEL_VMEM),
        cost_estimate=work(flops, (*operands, *pieces[0], *pieces[1], *shapes)),
        name=name,
    )(core, *operands, *pieces[0], *pieces[1], *[array for array, _ in blocks], *map(far, waits))


def mlp_up_back(rows, slope, pieces, waits):
    length, units = slope.shape
    unit, half = pieces[0][0].shape
    count = len(pieces[0])
    every, space = pl.BlockSpec(memory_space=pl.ANY), pl.BlockSpec(memory_space=pltpu.VMEM)
    return pl.pallas_call(
        without(functools.partial(mlp_up_back_kernel, count), 3 + 2 * count, len(waits)),
        in_specs=[space] * 2 + [every] * (1 + 2 * count + len(waits)),
        out_specs=space,
        out_shape=jax.ShapeDtypeStruct((length, units), jnp.bfloat16),
        scratch_shapes=[
            pltpu.VMEM((count, unit, 2 * half), jnp.bfloat16),
            pltpu.VMEM((length, units), jnp.bfloat16),
            pltpu.SemaphoreType.DMA((count, 3)),
        ],
        compiler_params=pltpu.CompilerParams(vmem_limit_bytes=KERNEL_VMEM),
        name="mlp_up_back",
    )(*rows, *map(far, (slope, *pieces[0], *pieces[1], *waits)))


def attend(core, tables, rows, pieces, waits):
    half, features = rows[0].shape
    length, count = 2 * half, len(pieces[0])
    lanes = ((count, length, 128), jnp.bfloat16, pl.BlockSpec((1, length, 128), lambda j: (j, 0, 0)))
    lse = ((count, 2, length), jnp.float32, pl.BlockSpec((1, 2, length), lambda j: (j, 0, 0)))
    mixed = ((length, count * 128), jnp.bfloat16, pl.BlockSpec((length, 128), lambda j: (0, j)))
    return by_pairs(
        attend_kernel,
        "attend",
        core,
        (*tables, *rows),
        pieces,
        (),
        (lanes, lanes, lanes, lse, mixed),
        [pltpu.VMEM((features, 384), jnp.bfloat16)],
        count * length * (2 * features * 384 + 2 * PAIR_WORK * length),
        waits,
    )


def attend_back(core, tables, rows, pieces, base, waits, q, k, v, lse):
    half, features = rows[0].shape
    length, count = 2 * half, len(pieces[0])
    lanes = pl.BlockSpec((1, length, 128), lambda j: (base + j, 0, 0))
    lse_spec = pl.BlockSpec((1, 2, length), lambda j: (base + j, 0, 0))
    out = ((length, count * 384), jnp.bfloat16, pl.BlockSpec((length, 384), lambda j: (0, j)))
    return by_pairs(
        attend_back_kernel,
        "attend_back",
        core,
        (*tables, *rows),
        pieces,
        ((q, lanes), (k, lanes), (v, lanes), (lse, lse_spec)),
        (out,),
        [pltpu.VMEM((features, 128), jnp.bfloat16)] + [pltpu.VMEM((length, 128), jnp.float32)] * 3,
        count * length * (2 * features * 128 + 5 * PAIR_WORK * length),
        waits,
    )[0]


def exchanged(parts):
    return parts[0], flip_pairs(parts[1], 1)


def model_rows(kernel, name, lefts, pieces, waits=()):
    length, width = lefts[0].shape[0], 2 * MODEL_HALF
    outs = (((length // 2, width), jnp.float32), ((length // 2, width), jnp.bfloat16))
    hidden = sum(left.shape[1] for left in lefts)
    more = {"limit": KERNEL_VMEM, "flops": 2 * length * width * hidden, "waits": waits}
    return exchanged(on_chip(kernel, name, outs, *lefts, *pieces[0], *pieces[1], **more))


def flip_pairs(block, distance):
    size = lax.axis_size("dp")
    return lax.ppermute(block, "dp", [(i, i ^ distance) for i in range(size)])


def passed_on(block, step):
    size = lax.axis_size("tensor")
    return lax.ppermute(block, "tensor", [(i, (i + step) % size) for i in range(size)])


def dot_tn(left, right):
    return lax.dot_general(
        left, right, (((0,), (0,)), ((), ())), preferred_element_type=jnp.float32
    )


def fetch(first_ref, zeros, ones, buffers, sems):
    for section, sources in enumerate((zeros, ones)):

        @pl.when(first_ref[0] == section)
        def _():
            for i, (source, buffer) in enumerate(zip(sources, buffers)):
                pltpu.make_async_copy(source, buffer, sems.at[i]).start()

    def arrived(*places):
        for i in places:
            pltpu.make_async_copy(zeros[i], buffers[i], sems.at[i]).wait()

    return arrived


def mlp_grads_kernel(base, section_ref, *refs):
    (own_one, other_one, own_two, other_two), (rows, d_up, gelu, d_down, sems) = refs[12:16], refs[16:]
    half, size = own_one.shape[0] // 2, own_one.shape[1]
    cols = pl.ds(base * size, 2 * size)

    def parts(own_rows, other_rows, d_up_ref, gelu_ref, own_grad, other_grad):
        whole = (d_up_ref.at[:, cols], gelu_ref.at[:, cols])
        return (own_rows, other_rows, *whole, own_grad, other_grad)

    count = refs[0].shape[0]
    buffers = (
        rows.at[pl.ds(0, count)],
        rows.at[pl.ds(count, count)],
        d_up,
        gelu,
        d_down.at[pl.ds(0, count)],
        d_down.at[pl.ds(count, count)],
    )
    arrived = fetch(section_ref, parts(*refs[:6]), parts(*refs[6:12]), buffers, sems)
    for j, own, other in ((1, own_two, other_two), (0, own_one, other_one)):
        cols = slice(j * size, (j + 1) * size)
        if j == 1:
            arrived(0, 1, 2)
        up = dot_tn(rows[...], d_up[:, cols])
        own[:half] = up[:half]
        other[:half] = up[half:].astype(jnp.bfloat16)
        if j == 1:
            arrived(3, 4, 5)
        down = dot_tn(gelu[:, cols], d_down[...])
        own[half:] = down[:, :half]
        other[half:] = down[:, half:].astype(jnp.bfloat16)


def attn_grads_kernel(base, section_ref, *refs):
    (own_one, other_one, own_two, other_two), (rows, d_qkv, mixed, d_attn, sems) = refs[12:16], refs[16:]
    half, size = own_one.shape[0], d_qkv.shape[1] // 2
    count = refs[0].shape[0]
    cols = pl.ds(base * 128, 256)

    def parts(own_rows, other_rows, d_qkv_ref, mixed_ref, own_grad, other_grad):
        return (own_rows, other_rows, d_qkv_ref, mixed_ref.at[:, cols], own_grad, other_grad)

    buffers = (
        rows.at[pl.ds(0, count)],
        rows.at[pl.ds(count, count)],
        d_qkv,
        mixed,
        d_attn.at[pl.ds(0, count)],
        d_attn.at[pl.ds(count, count)],
    )
    arrived = fetch(section_ref, parts(*refs[:6]), parts(*refs[6:12]), buffers, sems)
    for j, own, other in ((1, own_two, other_two), (0, own_one, other_one)):
        if j == 1:
            arrived(0, 1, 2)
        qkv = dot_tn(rows[...], d_qkv[:, j * size : (j + 1) * size])
        if j == 1:
            arrived(3, 4, 5)
        out = dot_tn(d_attn[...], mixed[:, j * 128 : (j + 1) * 128])
        own[:, :size] = qkv[:half]
        own[:, size:] = out[:half]
        other[:, :size] = qkv[half:].astype(jnp.bfloat16)
        other[:, size:] = out[half:].astype(jnp.bfloat16)


def weight_grads(kernel, name, base, section, zeros, ones, shape, columns, waits=()):
    length = 2 * zeros[0].shape[0]
    width = zeros[0].shape[1]
    every = pl.BlockSpec(memory_space=pl.ANY)
    space = pl.BlockSpec(memory_space=pltpu.VMEM)
    arrays = (*zeros, *ones)
    first, second, third, fourth = pl.pallas_call(
        without(functools.partial(kernel, base), 1 + len(arrays), len(waits)),
        in_specs=[pl.BlockSpec(memory_space=pltpu.SMEM)] + [every] * (len(arrays) + len(waits)),
        out_specs=[space] * 4,
        out_shape=[
            jax.ShapeDtypeStruct(shape, jnp.float32),
            jax.ShapeDtypeStruct(shape, jnp.bfloat16),
        ]
        * 2,
        scratch_shapes=[
            pltpu.VMEM((length, width), jnp.bfloat16),
            pltpu.VMEM((length, columns[0]), jnp.bfloat16),
            pltpu.VMEM((length, columns[1]), jnp.bfloat16),
            pltpu.VMEM((length, width), jnp.bfloat16),
            pltpu.SemaphoreType.DMA((6,)),
        ],
        compiler_params=pltpu.CompilerParams(vmem_limit_bytes=KERNEL_VMEM),
        name=name,
    )(section, *map(far, (*arrays, *waits)))
    return [(first, flip_pairs(second, 2)), (third, flip_pairs(fourth, 2))]


def moved_kernel(own_ref, other_ref, *refs):
    out_ref = refs[-1]

    def body(i, carry):
        spot = pl.ds(pl.multiple_of(i * CHUNK, CHUNK), CHUNK)
        total = own_ref[spot, :]
        for ref in (other_ref, *refs[:-1]):
            total = total + wide(ref, spot)
        out_ref[spot, :] = total.astype(jnp.bfloat16)
        return carry

    lax.fori_loop(0, own_ref.shape[0] // CHUNK, body, 0)


def gates_kernel(up_ref, down_ref, up_out, down_out):
    up_out[...] = up_ref[...]
    down_out[...] = down_ref[...]


def gate_kernel(piece_ref, out_ref):
    out_ref[...] = piece_ref[...]


def mlp_sum_kernel(core_ref, own_ref, other_ref, moved_ref, up_keep, down_keep, up_send, down_send):
    half = own_ref.shape[0] // 2
    size = up_keep.shape[0]

    def total(rows, cols):
        more = other_ref[rows, cols].astype(jnp.float32) + moved_ref[rows, cols].astype(jnp.float32)
        return own_ref[rows, cols] + more

    for core in range(2):

        @pl.when(core_ref[0] == core)
        def _():
            for place, up, down in ((core, up_keep, down_keep), (1 - core, up_send, down_send)):
                spot = slice(place * size, (place + 1) * size)
                up[...] = total(spot, slice(None))
                down[...] = total(slice(half, None), spot)


def mlp_join_kernel(core_ref, up_keep, down_keep, up_sent, down_sent, up_out, down_out):
    size = up_keep.shape[1]
    for core in range(2):

        @pl.when(core_ref[0] == core)
        def _():
            places = ((core, up_keep, down_keep), (1 - core, up_sent, down_sent))
            for place, up, down in places:
                spot = slice(place * size, (place + 1) * size)
                up_out[:, spot] = up[...]
                down_out[spot] = down[...]


def chosen_kernel(place_ref, zero_ref, one_ref, out_ref):
    half = out_ref.shape[1] // 2
    for section, rows_ref in enumerate((zero_ref, one_ref)):
        for upper in range(2):

            @pl.when(jnp.logical_and(place_ref[0] == section, place_ref[1] == upper))
            def _():
                for side in range(2):
                    place = (side + upper) % 2 * half
                    out_ref[:, place : place + half] = rows_ref[:, side * half : (side + 1) * half]


def pick_kernel(core_ref, rows_ref, keep_ref, send_ref):
    count = keep_ref.shape[0]
    keep_ref[...] = rows_ref[pl.ds(core_ref[0] * count, count)]
    send_ref[...] = rows_ref[pl.ds((1 - core_ref[0]) * count, count)]


def in_order_kernel(core_ref, keep_ref, sent_ref, out_ref):
    out_ref[:, pl.ds(core_ref[0], 1)] = keep_ref[...][:, None]
    out_ref[:, pl.ds(1 - core_ref[0], 1)] = sent_ref[...][:, None]


def with_core(kernel, name, core, outs, *operands, waits=()):
    space = pl.BlockSpec(memory_space=pltpu.VMEM)
    return pl.pallas_call(
        without(kernel, 1 + len(operands), len(waits)),
        in_specs=[pl.BlockSpec(memory_space=pltpu.SMEM)]
        + [space] * len(operands)
        + [pl.BlockSpec(memory_space=pl.ANY)] * len(waits),
        out_specs=[space] * len(outs),
        out_shape=[jax.ShapeDtypeStruct(shape, dtype) for shape, dtype in outs],
        compiler_params=pltpu.CompilerParams(vmem_limit_bytes=ROWS_VMEM),
        name=name,
    )(core, *operands, *map(far, waits))


def last_sum_kernel(core_ref, own_ref, other_ref, moved_ref, keep_ref, send_ref):
    rows = keep_ref.shape[0]

    def total(block):
        spot = pl.ds(pl.multiple_of(block * rows, rows), rows)
        return own_ref[spot, :] + wide(other_ref, spot) + wide(moved_ref, spot)

    keep_ref[...] = total(core_ref[0])
    send_ref[...] = total(1 - core_ref[0])


def joined_kernel(spots, core_ref, keep_ref, sent_ref, column_ref, row_ref):
    size = row_ref.shape[0] // 2
    for core in range(2):

        @pl.when(core_ref[0] == core)
        def _():
            for place, source in ((core, keep_ref), (1 - core, sent_ref)):
                for start, stop, to in spots:
                    step = stop - start
                    column_ref[:, to + place * step : to + (place + 1) * step] = source[:, start:stop]
                row_ref[place * size : (place + 1) * size] = source[:, spots[-1][1] :].T


def per_chip(
    inputs,
    out_cotangent,
    group_ids,
    group_weights,
    gains,
    qkv_weight,
    out_weight,
    up_weight,
    down_weight,
):
    micro, row_count, width = inputs.shape
    tensor = lax.axis_size("tensor")
    part = row_count // 2
    wide_half = width // 2
    length = tensor * row_count
    half = length // 2
    first = lax.axis_index("section") == 0
    place = lax.axis_index("dp")
    core = place % 2
    upper = place // 2 % 2
    core_zero = core == 0
    low_half = upper == 0

    def ordered(mine, other):
        return jnp.where(core_zero, mine, other), jnp.where(core_zero, other, mine)

    def own_first(values):
        return jnp.where(low_half, values, jnp.roll(values, wide_half, axis=-1))

    def both_rows(own):
        return own, flip_pairs(own, 1)

    def to_chip(block):
        split = block.reshape((micro, 2, part) + block.shape[2:])
        mine = lax.dynamic_index_in_dim(split, core, 1, keepdims=False)
        other = lax.dynamic_index_in_dim(split, 1 - core, 1, keepdims=False)
        return lax.all_to_all(
            jnp.concatenate(ordered(mine, flip_pairs(other, 1))), "tensor", 0, 0, tiled=True
        )

    def from_chip(spread_out, waits=()):
        piece = ((micro, part, width), jnp.bfloat16)
        keep, send = with_core(
            pick_kernel, "pick", core_word, (piece, piece), spread_out, waits=waits
        )
        outs = (((micro, 2, part, width), jnp.bfloat16),)
        (rows,) = with_core(
            in_order_kernel, "in_order", core_word, outs, keep, flip_pairs(send, 1)
        )
        return rows.reshape(micro, row_count, width)

    def columns(local):
        size = local.shape[-1] // 2
        mid = (0,) * (local.ndim - 2)
        piece = lax.dynamic_slice(
            local,
            (wide_half * upper, *mid, size * core),
            (wide_half, *local.shape[1:-1], size),
        )
        return piece.reshape(wide_half, -1)

    def rows(local):
        size = local.shape[0] // 2
        return lax.dynamic_slice(local, (size * core, wide_half * upper), (size, wide_half))

    core_word = core.astype(jnp.int32).reshape(1)
    attn_piece = jnp.concatenate([columns(qkv_weight[0]), rows(out_weight[0]).T], axis=1)

    def spread(piece):
        pieces = [piece]
        for _ in range(tensor - 1):
            pieces.append(passed_on(pieces[-1], 1))
        return pieces

    up_piece, down_piece = columns(up_weight[0]), rows(down_weight[0])
    up_other, down_other = [flip_pairs(up_piece, 2)], [flip_pairs(down_piece, 2)]
    attn_own = [attn_piece, passed_on(attn_piece, 1)]
    attn_first = flip_pairs(attn_piece, 2)
    outs = ((attn_piece.shape, attn_piece.dtype),)
    attn_own[1] = on_chip(gate_kernel, "gate", outs, attn_own[1], waits=(attn_first, up_other[0]))[0]
    attn_own += spread(attn_own[1])[1:-1]
    attn_other = [attn_first] + [flip_pairs(piece, 2) for piece in attn_own[1:]]
    outs = tuple((piece.shape, piece.dtype) for piece in (up_piece, down_piece))
    up_piece, down_piece = on_chip(
        gates_kernel, "gate", outs, up_piece, down_piece, waits=(attn_own[2], attn_other[0], down_other[0])
    )
    up_own, down_own = spread(up_piece), spread(down_piece)
    up_other += [flip_pairs(piece, 2) for piece in up_own[1:]]
    down_other += [flip_pairs(piece, 2) for piece in down_own[1:]]
    w_attn, w_up, w_down = (attn_own, attn_other), (up_own, up_other), (down_own, down_other)
    unit = up_piece.shape[1]
    units = tensor * unit

    group_count = group_weights.shape[0]
    matches = group_ids[..., None] == jnp.arange(group_count, dtype=jnp.int32)
    row_scale = jnp.sum(jnp.where(matches, group_weights, 0.0), axis=-1)
    weighted = (out_cotangent.astype(jnp.float32) * row_scale[..., None]).astype(jnp.bfloat16)
    start = to_chip(own_first(jnp.where(first, inputs, weighted))).reshape(half, width)
    gain = own_first(gains[0])

    turns = jnp.arange(half, dtype=jnp.int32)
    turns = turns // part * row_count + turns % part
    positions = jnp.concatenate([turns + core * part, turns + (1 - core) * part])
    freqs = 10000.0 ** (-2.0 * jnp.arange(HEAD_DIM // 2, dtype=jnp.float32) / HEAD_DIM)
    angles = positions.astype(jnp.float32)[:, None] * freqs[None, :]
    cos_part, sin_part = jnp.cos(angles), jnp.sin(angles)
    tables = (
        jnp.concatenate([cos_part] * 4, axis=1),
        jnp.concatenate([-sin_part, sin_part] * 2, axis=1),
    )
    row32, row16 = ((half, width), jnp.float32), ((half, width), jnp.bfloat16)
    unit16 = ((length, units), jnp.bfloat16)
    sum32 = ((1, width), jnp.float32)
    mlp_cost = {"limit": KERNEL_VMEM, "flops": 2 * length * width * units}
    every = slice(None)

    def model_kernel(cols, lefts=1):
        return functools.partial(to_model_kernel, lefts, tensor, cols)

    down_kernel = functools.partial(mlp_down_kernel, tensor)

    def forward(layer_input, waits):
        attn_in = both_rows(
            on_chip(norm_in_kernel, "norm_in", (row16,), gain, layer_input, waits=waits[0])[0]
        )
        *heads, mixed = attend(core_word, tables, attn_in, w_attn, waits[1])
        parts = model_rows(model_kernel(OUT), "attn_out", [mixed], w_attn, waits[2])
        operands = (gain, layer_input, *parts)
        branch, hidden, mlp_in = on_chip(
            after_attention_kernel, "after_attn", (row32, row32, row16), *operands, waits=waits[3]
        )
        mlp_in = both_rows(mlp_in)
        kernel = functools.partial(mlp_up_kernel, tensor)
        operands = (*mlp_in, *w_up[0], *w_up[1])
        gelu_out, slope = on_chip(kernel, "mlp_up", (unit16, unit16), *operands, **mlp_cost)
        parts = model_rows(down_kernel, "mlp_down", [gelu_out], w_down)
        mlp_branch, result = on_chip(
            after_mlp_kernel, "after_mlp", (row32, row16), gain, hidden, *parts
        )
        saved = (layer_input, heads, branch, hidden, slope, mlp_branch)
        return result, saved, (attn_in, mixed, mlp_in, gelu_out)

    def backward(grad, saved, hook, late=()):
        layer_input, heads, branch, hidden, slope, mlp_branch = saved
        operands = (gain, grad, mlp_branch)
        d_down, sum_three = on_chip(
            into_mlp_back_kernel, "into_mlp_back", (row16, sum32), *operands
        )
        d_down = both_rows(d_down)
        d_up = mlp_up_back(d_down, slope, w_down, late)
        waits = hook(d_down, d_up)
        parts = model_rows(model_kernel(every), "mlp_back", [d_up], w_up, waits)
        waits = hook()
        operands = (gain, grad, *parts, hidden, branch)
        outs = (row32, row16, sum32, sum32)
        d_hidden, d_attn, sum_one, sum_two = on_chip(
            into_attention_back_kernel, "into_attn_back", outs, *operands, waits=waits
        )
        d_attn = both_rows(d_attn)
        waits = hook(d_attn)
        d_qkv = []
        for base in reversed(range(0, tensor, 2)):
            some = [side[base : base + 2] for side in w_attn]
            now = attend_back(core_word, tables, d_attn, some, base, waits, *heads)
            d_qkv.insert(0, now)
            waits = hook(now)
        parts = model_rows(model_kernel(QKV, 2), "attn_back", d_qkv, w_attn, waits)
        operands = (gain, layer_input, *parts, d_hidden)
        d_input, sum_zero = on_chip(
            out_of_layer_kernel, "out_of_layer", (row16, sum32), *operands, waits=hook()
        )
        sums = jnp.concatenate([sum_zero, sum_one, sum_two, sum_three])
        return d_input, (d_qkv, d_attn, d_up, d_down), sums

    low_zero, saved_zero, lefts_zero = forward(
        start,
        (
            (up_piece, up_other[0], down_other[0]),
            (up_own[1], down_own[1]),
            (up_own[2], down_own[2], up_other[1], down_other[1]),
            (down_own[3], up_other[2], down_other[2], up_other[3]),
        ),
    )
    low_one, saved_one, lefts_one = forward(shifted(low_zero, "section", 1), ((),) * 4)
    grad_one, rights_one, gain_one = backward(start, saved_one, lambda *new: ())
    received = shifted(grad_one, "section", -1)

    lows = lax.optimization_barrier((low_zero, low_one, grad_one))[:2]
    lows = own_first(jnp.where(first, *lows)).reshape(tensor, part, width)
    lows = lax.all_to_all(lows, "tensor", 0, 0, tiled=True)

    section_word = lax.axis_index("section").astype(jnp.int32).reshape(1)

    def mlp_leaves(base, waits=()):
        zeros = (*lefts_zero[2], d_up, lefts_zero[3], *d_down)
        ones = (*lefts_one[2], rights_one[2], lefts_one[3], *rights_one[3])
        mlp_sums[base : base + 2] = weight_grads(
            mlp_grads_kernel,
            "mlp_grads",
            base,
            section_word,
            zeros,
            ones,
            (wide_half + unit, unit),
            (2 * unit, 2 * unit),
            waits,
        )

    def attn_leaves(base, d_qkv, waits):
        zeros = (*lefts_zero[0], d_qkv, lefts_zero[1], *d_attn)
        ones = (*lefts_one[0], rights_one[0][base // 2], lefts_one[1], *rights_one[1])
        attn_sums[base : base + 2] = weight_grads(
            attn_grads_kernel,
            "attn_grads",
            base,
            section_word,
            zeros,
            ones,
            (wide_half, 512),
            (768, 256),
            waits,
        )

    def moves_on(piece, *moved, waits=()):
        outs = ((piece[1].shape, jnp.bfloat16),)
        (total,) = on_chip(moved_kernel, "moved", outs, *piece, *moved, waits=waits)
        return total, passed_on(total, -1)

    mlp_sums, attn_sums = [None] * tensor, [None] * tensor
    mlp_moves, attn_moves = [None] * tensor, [None] * tensor
    hooks = iter(range(6))

    def hook(*new):
        nonlocal d_down, d_up, d_attn, outputs
        turn = next(hooks)
        if turn == 0:
            d_down, d_up = new
            mlp_leaves(2)
            return (mlp_sums[3][0],)
        if turn == 1:
            return ()
        if turn == 2:
            (d_attn,) = new
            outputs = from_chip(lows, d_attn[:1])
            total, mlp_moves[3] = moves_on(mlp_sums[3], waits=(outputs,))
            mlp_leaves(0, (total,))
            return (mlp_sums[1][0],)
        if turn == 3:
            total, mlp_moves[2] = moves_on(mlp_sums[2], mlp_moves[3], waits=new)
            attn_leaves(2, new[0], (total,))
            return (mlp_sums[2][1], mlp_moves[3], attn_sums[3][0])
        if turn == 4:
            total, mlp_moves[1] = moves_on(mlp_sums[1], mlp_moves[2], waits=new)
            attn_leaves(0, new[0], (total,))
            total, attn_moves[3] = moves_on(attn_sums[3], waits=attn_sums[1][:1])
            return (total, mlp_moves[1], mlp_sums[0][1])
        return attn_sums[2][1:]

    d_down = d_up = d_attn = outputs = None
    grad_zero, rights_zero, gain_zero = backward(received, saved_zero, hook, (lows,))
    _, attn_moves[2] = moves_on(attn_sums[2], attn_moves[3])
    place_word = jnp.stack([lax.axis_index("section"), upper]).astype(jnp.int32)
    (grads_chosen,) = with_core(
        chosen_kernel,
        "chosen",
        place_word,
        (row16,),
        grad_zero,
        grad_one,
        waits=(attn_moves[2], attn_sums[1][1]),
    )
    grads = lax.all_to_all(
        grads_chosen.reshape(tensor, part, width), "tensor", 0, 0, tiled=True
    )

    block32 = ((wide_half // 2, unit), jnp.float32)
    down32 = ((unit, wide_half // 2), jnp.float32)
    up_keep, down_keep, up_send, down_send = with_core(
        mlp_sum_kernel,
        "mlp_sum",
        core_word,
        (block32, down32, block32, down32),
        *mlp_sums[0],
        mlp_moves[1],
        waits=(grads_chosen,),
    )
    outs = (
        ((wide_half // 2, 2 * unit), jnp.float32),
        ((2 * unit, wide_half // 2), jnp.float32),
    )
    sent = flip_pairs(up_send, 1), flip_pairs(down_send, 1)
    up_grad, down_grad = with_core(
        mlp_join_kernel, "mlp_join", core_word, outs, up_keep, down_keep, *sent
    )
    waits = (grads_chosen, attn_sums[0][1])
    last, attn_moves[1] = moves_on(attn_sums[1], attn_moves[2], waits=waits)
    grads = from_chip(grads, (attn_moves[1],))
    gain_total = own_first(jnp.where(first, gain_zero, gain_one))
    count = tensor * lax.axis_size("dp")
    gain_parts = gain_total.reshape(4, count, width // count).swapaxes(0, 1)
    outs = ((gain_parts.shape, gain_parts.dtype),)
    (gain_parts,) = on_chip(gate_kernel, "gate", outs, gain_parts, waits=(last,))
    gain_parts = lax.all_to_all(gain_parts, ("dp", "tensor"), 0, 0, tiled=True)
    gains_grad = jnp.sum(gain_parts, axis=0)
    outs = (((wide_half // 2, 512), jnp.float32),) * 2
    keep, send = with_core(
        last_sum_kernel,
        "attn_sum",
        core_word,
        outs,
        *attn_sums[0],
        attn_moves[1],
        waits=(grads, outputs, gains_grad, up_grad),
    )
    spots = tuple((i * 128, (i + 1) * 128, i * 256) for i in range(3))
    outs = (((wide_half // 2, 768), jnp.float32), ((256, wide_half // 2), jnp.float32))
    kernel = functools.partial(joined_kernel, spots)
    qkv_grad, out_grad = with_core(
        kernel, "attn_join", core_word, outs, keep, flip_pairs(send, 1)
    )
    qkv_grad = qkv_grad.reshape(wide_half // 2, 3, -1)

    return (
        outputs[None],
        grads[None],
        gains_grad[None],
        qkv_grad[None],
        out_grad[None],
        up_grad[None],
        down_grad[None],
    )


def takes_chips(sizes):
    return sizes["section"] == 2 and sizes["dp"] == 4 and sizes["tensor"] == 4


def solution(mesh):
    placed = (
        P("dp", "tensor", None),
        P("dp", "tensor", None),
        P("dp", "tensor"),
        P(),
        P("section", None, None),
        P("section", None, None, "tensor"),
        P("section", "tensor", None),
        P("section", None, "tensor"),
        P("section", "tensor", None),
    )
    body = per_chip if takes_chips(dict(mesh.shape)) else per_device
    return jax.shard_map(
        body,
        mesh=mesh,
        in_specs=placed,
        out_specs=(
            P("section", "dp", "tensor", None),
            P("section", "dp", "tensor", None),
            P("section", None, ("dp", "tensor")),
            P("section", "dp", None, "tensor"),
            P("section", "tensor", "dp"),
            P("section", "dp", "tensor"),
            P("section", "tensor", "dp"),
        ),
        check_vma=False,
    )
```

```python
import functools
import math

import jax
import jax.numpy as jnp
from jax import lax
from jax.experimental import pallas as pl
from jax.experimental.pallas import tpu as pltpu
from jax.sharding import PartitionSpec as P

HEAD_DIM = 64


NORM_EPSILON = 1e-06
TILE = 128
PAIR_WORK = 1024
MODEL_HALF = 512
QKV = slice(0, 384)
OUT = slice(384, 512)
CHUNK = 32
KERNEL_VMEM = 20 << 20
ROWS_VMEM = 3 << 20


def shifted(block, axis, distance):
    devices = range(lax.axis_size(axis))
    route = [(i - distance, i) for i in devices if i - distance in devices]
    return lax.ppermute(block, axis, route)


def norm_rows(vector, weight_gain):
    return (
        vector
        * lax.rsqrt(jnp.mean(vector * vector, axis=-1, keepdims=True) + NORM_EPSILON)
        * weight_gain
    )


def rotary_tables(seq_len, head_width):
    half_width = head_width // 2
    freqs = 10000.0 ** (-2.0 * jnp.arange(half_width, dtype=jnp.float32) / head_width)
    angles = jnp.arange(seq_len, dtype=jnp.float32)[:, None] * freqs[None, :]
    return (jnp.cos(angles), jnp.sin(angles))


def rotate(vector, cos_table, sin_table):
    first_half, second_half = jnp.split(vector, 2, axis=-1)
    cos_part = cos_table[:, None, :]
    sin_part = sin_table[:, None, :]
    return jnp.concatenate(
        [
            first_half * cos_part - second_half * sin_part,
            second_half * cos_part + first_half * sin_part,
        ],
        axis=-1,
    )


def contract(left_rows, right_rows):
    return lax.dot_general(
        left_rows, right_rows, (((0,), (0,)), ((), ())), preferred_element_type=jnp.float32
    )


def gather_rows(row_values, weight):

    def project(shard_rows, offset):
        return (shard_rows, jnp.dot(shard_rows, weight, preferred_element_type=jnp.float32))

    return project(lax.all_gather(row_values, "tensor", axis=0, tiled=True), jnp.int32(0))


def scatter_rows(row_values, weight, row_count):

    def partial_term(offset, span):
        return jnp.dot(row_values, weight, preferred_element_type=jnp.float32)

    return lax.psum_scatter(
        partial_term(jnp.int32(0), lax.axis_size("tensor") * row_count),
        "tensor",
        scatter_dimension=0,
        tiled=True,
    )


def gather_grads(row_values, weight):

    def project(shard_rows, offset):
        return (shard_rows, jnp.dot(shard_rows, weight.T, preferred_element_type=jnp.float32))

    return project(lax.all_gather(row_values, "tensor", axis=0, tiled=True), jnp.int32(0))


def scatter_grads(row_values, weight, row_count):

    def partial_term(offset, span):
        return jnp.dot(row_values, weight.T, preferred_element_type=jnp.float32)

    return lax.psum_scatter(
        partial_term(jnp.int32(0), lax.axis_size("tensor") * row_count),
        "tensor",
        scatter_dimension=0,
        tiled=True,
    )


def attention_probs(queries, key_rows):
    scores = jnp.einsum(
        "qhd,khd->hqk", queries, key_rows, preferred_element_type=jnp.float32
    ) * HEAD_DIM ** (-0.5)
    length = queries.shape[0]
    positions = jnp.arange(length, dtype=jnp.int32)
    causal = positions[:, None] >= positions[None, :]
    scores = jnp.where(causal[None], scores, -1e30)
    expos = jnp.exp(scores - jnp.max(scores, axis=-1, keepdims=True))
    return expos / jnp.sum(expos, axis=-1, keepdims=True)


def layer_forward(layer_input, weights):
    gains, w_qkv, w_out, w_up, w_down = weights
    row_count, model_width = layer_input.shape
    attn_in = norm_rows(layer_input, gains[0]).astype(jnp.bfloat16)
    gathered_a, qkv = gather_rows(attn_in, w_qkv.reshape(model_width, -1))
    length = qkv.shape[0]
    head_count = w_qkv.shape[2] // HEAD_DIM
    qkv = qkv.reshape(length, 3, head_count, HEAD_DIM)
    cos_table, sin_table = rotary_tables(length, HEAD_DIM)
    queries = rotate(qkv[:, 0], cos_table, sin_table).astype(jnp.bfloat16)
    key_rows = rotate(qkv[:, 1], cos_table, sin_table).astype(jnp.bfloat16)
    values = qkv[:, 2].astype(jnp.bfloat16)
    attn_probs = attention_probs(queries, key_rows).astype(jnp.bfloat16)
    mixed = jnp.einsum("hqk,khd->qhd", attn_probs, values, preferred_element_type=jnp.float32)
    mixed = mixed.reshape(length, -1).astype(jnp.bfloat16)
    attn_branch = scatter_rows(mixed, w_out, row_count)
    hidden = layer_input + norm_rows(attn_branch, gains[1])
    mlp_in = norm_rows(hidden, gains[2]).astype(jnp.bfloat16)
    gathered_c, up_act = gather_rows(mlp_in, w_up)
    gelu_out = jax.nn.gelu(up_act, approximate=True).astype(jnp.bfloat16)
    down_branch = scatter_rows(gelu_out, w_down, row_count)
    result = hidden + norm_rows(down_branch, gains[3])
    kept_values = (
        gathered_a,
        queries,
        key_rows,
        values,
        mixed,
        attn_branch,
        hidden,
        gathered_c,
        up_act,
        gelu_out,
        down_branch,
    )
    return (result, kept_values)


def layer_backward(layer_input, grad_result, kept_values, weights):
    gains, w_qkv, w_out, w_up, w_down = weights
    (
        gathered_a,
        queries,
        key_rows,
        values,
        mixed,
        attn_branch,
        hidden,
        gathered_c,
        up_act,
        gelu_out,
        down_branch,
    ) = kept_values
    row_count, model_width = layer_input.shape
    pullback = jax.vjp(norm_rows, down_branch, gains[3])[1]
    grad_down, gain_three = pullback(grad_result)
    gathered_dd, grad_gelu = gather_grads(grad_down.astype(jnp.bfloat16), w_down)
    down_total = contract(gelu_out, gathered_dd)
    pullback = jax.vjp(lambda vector: jax.nn.gelu(vector, approximate=True), up_act)[1]
    grad_up = pullback(grad_gelu)[0].astype(jnp.bfloat16)
    up_total = contract(gathered_c, grad_up)
    grad_mlp = scatter_grads(grad_up, w_up, row_count)
    pullback = jax.vjp(norm_rows, hidden, gains[2])[1]
    grad_norm_mlp, gain_two = pullback(grad_mlp)
    grad_hidden = grad_result + grad_norm_mlp
    pullback = jax.vjp(norm_rows, attn_branch, gains[1])[1]
    grad_attn, gain_one = pullback(grad_hidden)
    gathered_da, grad_mixed = gather_grads(grad_attn.astype(jnp.bfloat16), w_out)
    out_total = contract(mixed, gathered_da)
    length = grad_mixed.shape[0]
    head_count = w_qkv.shape[2] // HEAD_DIM
    grad_mixed = grad_mixed.astype(jnp.bfloat16).reshape(length, head_count, HEAD_DIM)
    attn_probs = attention_probs(queries, key_rows)
    probs_low = attn_probs.astype(jnp.bfloat16)
    grad_probs = jnp.einsum("qhd,khd->hqk", grad_mixed, values, preferred_element_type=jnp.float32)
    grad_values = jnp.einsum(
        "hqk,qhd->khd", probs_low, grad_mixed, preferred_element_type=jnp.float32
    )
    row_dots = jnp.sum(grad_probs * attn_probs, axis=-1, keepdims=True)
    grad_scores = (attn_probs * (grad_probs - row_dots)).astype(jnp.bfloat16)
    scale_value = HEAD_DIM ** (-0.5)
    grad_queries = (
        jnp.einsum("hqk,khd->qhd", grad_scores, key_rows, preferred_element_type=jnp.float32)
        * scale_value
    )
    grad_keys = (
        jnp.einsum("hqk,qhd->khd", grad_scores, queries, preferred_element_type=jnp.float32)
        * scale_value
    )
    cos_table, sin_table = rotary_tables(length, HEAD_DIM)
    pullback = jax.vjp(lambda vector: rotate(vector, cos_table, sin_table), grad_queries)[1]
    grad_q_raw = pullback(grad_queries)[0]
    grad_k_raw = pullback(grad_keys)[0]
    grad_qkv = (
        jnp.stack([grad_q_raw, grad_k_raw, grad_values], axis=1)
        .reshape(length, -1)
        .astype(jnp.bfloat16)
    )
    qkv_total = contract(gathered_a, grad_qkv).reshape(model_width, 3, -1)
    grad_attn_in = scatter_grads(grad_qkv, w_qkv.reshape(model_width, -1), row_count)
    pullback = jax.vjp(norm_rows, layer_input, gains[0])[1]
    grad_norm_in, gain_zero = pullback(grad_attn_in)
    grad_input = grad_hidden + grad_norm_in
    gain_total = jnp.stack([gain_zero, gain_one, gain_two, gain_three])
    return (grad_input, (gain_total, qkv_total, out_total, up_total, down_total))


def lagged(first_section, stacked):
    blank = jnp.zeros_like(stacked[:1])
    earlier = jnp.concatenate([blank, stacked[:-1]])
    later = jnp.concatenate([stacked[1:], blank])
    return jnp.where(first_section, earlier, later)


def per_device(
    inputs,
    out_cotangent,
    group_ids,
    group_weights,
    gains,
    qkv_weight,
    out_weight,
    up_weight,
    down_weight,
):
    weights = (gains[0], qkv_weight[0], out_weight[0], up_weight[0], down_weight[0])
    micro_count, row_count, model_width = inputs.shape
    first_section = lax.axis_index("section") == 0
    group_count = group_weights.shape[0]
    matches = group_ids[..., None] == jnp.arange(group_count, dtype=jnp.int32)
    row_scale = jnp.sum(jnp.where(matches, group_weights, 0.0), axis=-1)
    scaled = out_cotangent.astype(jnp.float32) * row_scale[..., None]
    padded = jnp.concatenate([inputs, jnp.zeros((1, row_count, model_width), jnp.bfloat16)])

    def forward_tick(received, fresh_input):
        layer_input = jnp.where(first_section, fresh_input, received)
        result, kept_values = layer_forward(layer_input.astype(jnp.float32), weights)
        result_low = result.astype(jnp.bfloat16)
        outgoing = shifted(result_low, "section", 1)
        stashed = ()
        return (outgoing, (layer_input, result_low, stashed))

    start_rows = jnp.zeros((row_count, model_width), jnp.bfloat16)
    _, (layer_inputs, layer_results, stashed) = lax.scan(forward_tick, start_rows, padded)
    layer_outputs = jnp.where(first_section, layer_results[:-1], layer_results[1:])[None]
    back_inputs = lagged(first_section, layer_inputs)
    back_stash = jax.tree.map(lambda stacked: lagged(first_section, stacked), stashed)
    grad_padded = jnp.concatenate([scaled, jnp.zeros((1, row_count, model_width), jnp.float32)])
    tick_index = jnp.arange(micro_count + 1, dtype=jnp.int32)
    tick_valid = jnp.where(first_section, tick_index >= 1, tick_index < micro_count).astype(
        jnp.float32
    )

    def backward_tick(carry, step_item):
        received, totals = carry
        layer_input, cotangent, valid_now, stash_now = step_item
        grad_now = jnp.where(first_section, received.astype(jnp.float32), cotangent)
        input_now = layer_input.astype(jnp.float32)
        kept_values = layer_forward(input_now, weights)[1]
        grad_input, layer_grads = layer_backward(input_now, grad_now, kept_values, weights)
        totals = jax.tree.map(lambda total, update: total + valid_now * update, totals, layer_grads)
        grad_low = grad_input.astype(jnp.bfloat16)
        outgoing = shifted(grad_low, "section", -1)
        return ((outgoing, totals), grad_low)

    start_totals = (
        jnp.zeros((4, model_width), jnp.float32),
        jnp.zeros(qkv_weight.shape[1:], jnp.float32),
        jnp.zeros(out_weight.shape[1:], jnp.float32),
        jnp.zeros(up_weight.shape[1:], jnp.float32),
        jnp.zeros(down_weight.shape[1:], jnp.float32),
    )
    (_, totals), grad_lows = lax.scan(
        backward_tick,
        (start_rows, start_totals),
        (back_inputs, grad_padded, tick_valid, back_stash),
    )
    input_grads = jnp.where(first_section, grad_lows[1:], grad_lows[:-1])[None]
    gain_total, qkv_total, out_total, up_total, down_total = totals
    gains_grad = lax.psum_scatter(gain_total, ("dp", "tensor"), scatter_dimension=1, tiled=True)
    qkv_grad, out_grad, up_grad, down_grad = (
        lax.psum_scatter(
            qkv_total.astype(jnp.bfloat16), "dp", scatter_dimension=0, tiled=True
        ).astype(jnp.float32),
        lax.psum_scatter(
            out_total.astype(jnp.bfloat16), "dp", scatter_dimension=1, tiled=True
        ).astype(jnp.float32),
        lax.psum_scatter(
            up_total.astype(jnp.bfloat16), "dp", scatter_dimension=0, tiled=True
        ).astype(jnp.float32),
        lax.psum_scatter(
            down_total.astype(jnp.bfloat16), "dp", scatter_dimension=1, tiled=True
        ).astype(jnp.float32),
    )
    return (
        layer_outputs,
        input_grads,
        gains_grad[None],
        qkv_grad[None],
        out_grad[None],
        up_grad[None],
        down_grad[None],
    )


def rotated(block, cos_rows, sin_rows):
    lane = lax.broadcasted_iota(jnp.int32, block.shape, 1)
    ahead = pltpu.roll(block, 96, 1)
    behind = pltpu.roll(block, 32, 1)
    swapped = jnp.where(lane % 64 < 32, ahead, behind)
    return block * cos_rows + swapped * sin_rows


def dot_nt(left, right):
    return lax.dot_general(
        left, right, (((1,), (1,)), ((), ())), preferred_element_type=jnp.float32
    )


def dot_nn(left, right):
    return jnp.dot(left, right, preferred_element_type=jnp.float32)


def model_weight(owns, others, cols):
    sides = [jnp.concatenate([ref[:, cols] for ref in refs], axis=1) for refs in (owns, others)]
    return jnp.concatenate(sides, axis=0)


def stacked_up(values):
    return jnp.concatenate(values, axis=0)


def edge_masks(core, rows):
    key = lax.broadcasted_iota(jnp.int32, (rows, 2 * rows), 0)
    query = lax.broadcasted_iota(jnp.int32, (rows, 2 * rows), 1)
    mine = query < rows
    place = jnp.where(mine, query + core * rows, query - rows + (1 - core) * rows)
    return (key + core * rows <= place, key + (1 - core) * rows <= place)


def both_sides(value, half, start, stop, axis=0):
    if axis == 0:
        return jnp.concatenate([value[start:stop], value[half + start : half + stop]], axis=0)
    return jnp.concatenate([value[:, start:stop], value[:, half + start : half + stop]], axis=1)


def hidden_scores(scores, masks, tile, step):
    seen = step * tile
    pieces = []
    for side in range(2):
        base = side * (seen + tile)
        if seen:
            pieces.append(scores[base : base + seen])
        pieces.append(jnp.where(masks[side], scores[base + seen : base + seen + tile], -1e30))
    return jnp.concatenate(pieces, axis=0)


def one_head(rows, head):
    lane = lax.broadcasted_iota(jnp.int32, rows.shape, 1)
    return jnp.where(lane // 64 == head, rows, jnp.zeros_like(rows))


def pick_piece(weight, owns, others, cols):
    for j, (own, other) in enumerate(zip(owns, others)):

        @pl.when(pl.program_id(0) == j)
        def _():
            size = own.shape[0]
            weight[:size] = own[:, cols]
            weight[size:] = other[:, cols]


def attend_kernel(pieces, core_ref, cos_ref, sin_ref, own_rows, other_rows, *refs):
    owns, others = refs[:pieces], refs[pieces : 2 * pieces]
    q_ref, k_ref, v_ref, lse_ref, mix_ref, weight = refs[2 * pieces :]
    half = own_rows.shape[0]
    tile = TILE
    pick_piece(weight, owns, others, QKV)
    proj = dot_nn(stacked_up([own_rows[...], other_rows[...]]), weight[...])
    cos_rows, sin_rows = cos_ref[...], sin_ref[...]
    q = (rotated(proj[:, :128], cos_rows, sin_rows) * HEAD_DIM ** (-0.5)).astype(jnp.bfloat16)
    k = rotated(proj[:, 128:256], cos_rows, sin_rows).astype(jnp.bfloat16)
    v32 = proj[:, 256:]
    q_ref[0] = q
    k_ref[0] = k
    v_ref[0] = v32.astype(jnp.bfloat16)
    v_flip = v32.T.astype(jnp.bfloat16)
    masks = edge_masks(core_ref[0], tile)

    def scored(step, head):
        stop = (step + 1) * tile
        q_head = one_head(both_sides(q, half, step * tile, stop), head)
        return hidden_scores(dot_nt(both_sides(k, half, 0, stop), q_head), masks, tile, step)

    units = [(step, head) for step in range(half // tile) for head in range(2)]
    ahead = scored(*units[0])
    outs = []
    for spot, (step, head) in enumerate(units):
        scores = ahead
        if spot + 1 < len(units):
            ahead = scored(*units[spot + 1])
        stop = (step + 1) * tile
        top = jnp.max(scores, axis=0, keepdims=True)
        expos = jnp.exp(scores - top)
        total = jnp.sum(expos, axis=0, keepdims=True)
        lse = top + jnp.log(total)
        lse_ref[0, head : head + 1, step * tile : stop] = lse[:, :tile]
        lse_ref[0, head : head + 1, half + step * tile : half + stop] = lse[:, tile:]
        v_cols = both_sides(v_flip, half, 0, stop, axis=1)
        out = dot_nn(v_cols[64 * head : 64 * head + 64], expos.astype(jnp.bfloat16))
        outs.append(out * (1.0 / total))
        if head == 1:
            mixed = jnp.concatenate(outs, axis=0).T.astype(jnp.bfloat16)
            outs = []
            mix_ref[step * tile : stop, :] = mixed[:tile]
            mix_ref[half + step * tile : half + stop, :] = mixed[tile:]


def attend_back_kernel(pieces, core_ref, cos_ref, sin_ref, own_rows, other_rows, *refs):
    owns, others = refs[:pieces], refs[pieces : 2 * pieces]
    q_ref, k_ref, v_ref, lse_ref, out_ref, weight, dq, dk, dv = refs[2 * pieces :]
    half = own_rows.shape[0]
    tile = TILE
    pick_piece(weight, owns, others, OUT)
    rows = stacked_up([own_rows[...], other_rows[...]])
    d_mixed = dot_nn(rows, weight[...]).astype(jnp.bfloat16)
    q, k, v = q_ref[0], k_ref[0], v_ref[0]
    k_flip = k.astype(jnp.float32).T.astype(jnp.bfloat16)
    masks = edge_masks(core_ref[0], tile)
    steps = half // tile

    def scored(step, head):
        stop = (step + 1) * tile
        q_head = one_head(both_sides(q, half, step * tile, stop), head)
        g_head = one_head(both_sides(d_mixed, half, step * tile, stop), head)
        scores = hidden_scores(dot_nt(both_sides(k, half, 0, stop), q_head), masks, tile, step)
        return q_head, g_head, scores, dot_nt(both_sides(v, half, 0, stop), g_head)

    units = [(step, head) for step in reversed(range(steps)) for head in range(2)]
    ahead = scored(*units[0])
    dq_flips = []
    dk_sum = dv_sum = None
    for spot, (step, head) in enumerate(units):
        q_head, g_head, scores, d_probs = ahead
        if spot + 1 < len(units):
            ahead = scored(*units[spot + 1])
        stop = (step + 1) * tile
        lse = both_sides(lse_ref[0], half, step * tile, stop, axis=1)
        probs = jnp.exp(scores - lse[head : head + 1])
        dots = jnp.sum(probs * d_probs, axis=0, keepdims=True)
        d_scores = (probs * (d_probs - dots)).astype(jnp.bfloat16)
        dv_part = dot_nn(probs.astype(jnp.bfloat16), g_head)
        dk_part = dot_nn(d_scores, q_head)
        k_cols = both_sides(k_flip, half, 0, stop, axis=1)
        dq_flips.append(dot_nn(k_cols[64 * head : 64 * head + 64], d_scores))
        if head == 0:
            dv_sum, dk_sum = dv_part, dk_part
            continue
        dv_sum, dk_sum = dv_sum + dv_part, dk_sum + dk_part
        dq_rows = jnp.concatenate(dq_flips, axis=0).T * HEAD_DIM ** (-0.5)
        dq_flips = []
        dq[step * tile : stop] = dq_rows[:tile]
        dq[half + step * tile : half + stop] = dq_rows[tile:]
        for base, part in ((0, slice(0, stop)), (half, slice(stop, 2 * stop))):
            if step == steps - 1:
                dk[base : base + stop] = dk_sum[part]
                dv[base : base + stop] = dv_sum[part]
            else:
                dk[base : base + stop] += dk_sum[part]
                dv[base : base + stop] += dv_sum[part]
    cos_rows, sin_rows = cos_ref[...], -sin_ref[...]
    out_ref[:, :128] = rotated(dq[...], cos_rows, sin_rows).astype(jnp.bfloat16)
    out_ref[:, 128:256] = rotated(dk[...], cos_rows, sin_rows).astype(jnp.bfloat16)
    out_ref[:, 256:] = dv[...].astype(jnp.bfloat16)


def split_rows(total, own_ref, other_ref):
    half = own_ref.shape[0]
    own_ref[...] = total[:half]
    other_ref[...] = total[half:].astype(jnp.bfloat16)


def to_model_kernel(lefts, pieces, cols, *refs):
    left, refs = jnp.concatenate([ref[...] for ref in refs[:lefts]], axis=1), refs[lefts:]
    weight = model_weight(refs[:pieces], refs[pieces : 2 * pieces], cols)
    split_rows(dot_nt(left, weight), *refs[2 * pieces :])


def mlp_down_kernel(pieces, left_ref, *refs):
    sides = [stacked_up([ref[...] for ref in side]) for side in (refs[:pieces], refs[pieces:-2])]
    split_rows(dot_nn(left_ref[...], jnp.concatenate(sides, axis=1)), *refs[-2:])


def gelu_both(up_act):
    root = math.sqrt(2.0 / math.pi)
    square = up_act * up_act
    rise = 0.5 + 0.5 * jnp.tanh(up_act * (root + root * 0.044715 * square))
    value = up_act * rise
    slope = rise + value * (1.0 - rise) * (2.0 * root + 6.0 * root * 0.044715 * square)
    return value, slope


def mlp_up_kernel(pieces, own_rows, other_rows, *refs):
    owns, others = refs[:pieces], refs[pieces : 2 * pieces]
    gelu_ref, slope_ref = refs[2 * pieces :]
    half = own_rows.shape[0]
    size = owns[0].shape[1]
    step = half // 2
    units = [(j, i) for j in range(pieces) for i in range(4)]

    def product(j, i):
        rows = (own_rows, other_rows)[i // 2][i % 2 * step : (i % 2 + 1) * step]
        return dot_nn(rows, stacked_up([owns[j][...], others[j][...]]))

    ahead = product(*units[0])
    for spot, (j, i) in enumerate(units):
        up_act = ahead
        if spot + 1 < len(units):
            ahead = product(*units[spot + 1])
        value, slope = gelu_both(up_act)
        gelu_ref[i * step : (i + 1) * step, j * size : (j + 1) * size] = value.astype(jnp.bfloat16)
        slope_ref[i * step : (i + 1) * step, j * size : (j + 1) * size] = slope.astype(
            jnp.bfloat16
        )


def mlp_up_back_kernel(pieces, own_rows, other_rows, slope_ref, *refs):
    owns, others = refs[:pieces], refs[pieces : 2 * pieces]
    out_ref, weight, slope, sems = refs[2 * pieces :]
    half = own_rows.shape[1] // 2
    size = owns[0].shape[0]
    order = list(reversed(range(pieces)))
    copies = []
    for j in order:
        sources = (owns[j], others[j], slope_ref.at[:, pl.ds(j * size, size)])
        targets = (
            weight.at[j, :, pl.ds(0, half)],
            weight.at[j, :, pl.ds(half, half)],
            slope.at[:, pl.ds(j * size, size)],
        )
        copies.append(
            [
                pltpu.make_async_copy(source, target, sems.at[j, i])
                for i, (source, target) in enumerate(zip(sources, targets))
            ]
        )
        for copy in copies[-1]:
            copy.start()
    rows = stacked_up([own_rows[...], other_rows[...]])
    for j, arriving in zip(order, copies):
        cols = slice(j * size, (j + 1) * size)
        for copy in arriving:
            copy.wait()
        d_gelu = dot_nt(rows, weight[j])
        out_ref[:, cols] = (d_gelu * slope[:, cols].astype(jnp.float32)).astype(jnp.bfloat16)


def inverse_size(rows):
    return lax.rsqrt(jnp.mean(rows * rows, axis=-1, keepdims=True) + NORM_EPSILON)


def norm_back(rows, gain, grad):
    scale = inverse_size(rows)
    weighted = grad * gain
    inner = jnp.mean(rows * weighted, axis=-1, keepdims=True)
    return scale * weighted - rows * (scale * scale * scale * inner), rows * scale * grad


def folded(rows):
    return jnp.sum(rows.reshape(rows.shape[0] // 8, 8, rows.shape[1]), axis=0)


def wide(ref, spot):
    return ref[spot, :].astype(jnp.float32)


def by_chunks(count, body, sums=0, width=0):
    def one(i, carry):
        more = body(pl.ds(pl.multiple_of(i * CHUNK, CHUNK), CHUNK))
        return tuple(old + folded(new) for old, new in zip(carry, more))

    start = tuple(jnp.zeros((8, width), jnp.float32) for _ in range(sums))
    totals = lax.fori_loop(0, count // CHUNK, one, start)
    return [jnp.sum(total, axis=0, keepdims=True) for total in totals]


def norm_in_kernel(gain_ref, rows_ref, out_ref):
    def body(spot):
        rows = wide(rows_ref, spot)
        out_ref[spot, :] = (rows * inverse_size(rows) * gain_ref[0:1]).astype(jnp.bfloat16)
        return ()

    by_chunks(rows_ref.shape[0], body)


def after_attention_kernel(
    gain_ref, rows_ref, own_ref, other_ref, branch_ref, hidden_ref, out_ref
):
    def body(spot):
        branch = own_ref[spot, :] + wide(other_ref, spot)
        hidden = wide(rows_ref, spot) + branch * inverse_size(branch) * gain_ref[1:2]
        branch_ref[spot, :] = branch
        hidden_ref[spot, :] = hidden
        out_ref[spot, :] = (hidden * inverse_size(hidden) * gain_ref[2:3]).astype(jnp.bfloat16)
        return ()

    by_chunks(rows_ref.shape[0], body)


def after_mlp_kernel(gain_ref, hidden_ref, own_ref, other_ref, branch_ref, out_ref):
    def body(spot):
        branch = own_ref[spot, :] + wide(other_ref, spot)
        branch_ref[spot, :] = branch
        result = hidden_ref[spot, :] + branch * inverse_size(branch) * gain_ref[3:4]
        out_ref[spot, :] = result.astype(jnp.bfloat16)
        return ()

    by_chunks(hidden_ref.shape[0], body)


def into_mlp_back_kernel(gain_ref, grad_ref, branch_ref, out_ref, sum_ref):
    def body(spot):
        d_rows, d_gain = norm_back(branch_ref[spot, :], gain_ref[3:4], wide(grad_ref, spot))
        out_ref[spot, :] = d_rows.astype(jnp.bfloat16)
        return (d_gain,)

    (sum_ref[...],) = by_chunks(grad_ref.shape[0], body, 1, grad_ref.shape[1])


def into_attention_back_kernel(
    gain_ref, grad_ref, own_ref, other_ref, hidden_ref, branch_ref, d_hidden_ref, out_ref, *sums
):
    def body(spot):
        d_rows = own_ref[spot, :] + wide(other_ref, spot)
        d_rows, d_gain = norm_back(hidden_ref[spot, :], gain_ref[2:3], d_rows)
        d_hidden = wide(grad_ref, spot) + d_rows
        d_hidden_ref[spot, :] = d_hidden
        d_rows, d_first = norm_back(branch_ref[spot, :], gain_ref[1:2], d_hidden)
        out_ref[spot, :] = d_rows.astype(jnp.bfloat16)
        return (d_first, d_gain)

    totals = by_chunks(grad_ref.shape[0], body, 2, grad_ref.shape[1])
    sums[0][...], sums[1][...] = totals


def out_of_layer_kernel(gain_ref, rows_ref, own_ref, other_ref, d_hidden_ref, out_ref, sum_ref):
    def body(spot):
        d_rows = own_ref[spot, :] + wide(other_ref, spot)
        d_rows, d_gain = norm_back(wide(rows_ref, spot), gain_ref[0:1], d_rows)
        out_ref[spot, :] = (d_hidden_ref[spot, :] + d_rows).astype(jnp.bfloat16)
        return (d_gain,)

    (sum_ref[...],) = by_chunks(rows_ref.shape[0], body, 1, rows_ref.shape[1])


def work(flops, arrays):
    size = sum(math.prod(array.shape) * jnp.dtype(array.dtype).itemsize for array in arrays)
    return pl.CostEstimate(flops=flops, bytes_accessed=size, transcendentals=0)


def far(array):
    return pltpu.with_memory_space_constraint(array, pltpu.HBM)


def without(kernel, first, count):
    return lambda *refs: kernel(*refs[:first], *refs[first + count :])


def on_chip(kernel, name, outs, *operands, limit=ROWS_VMEM, flops=0, waits=()):
    shapes = [jax.ShapeDtypeStruct(shape, dtype) for shape, dtype in outs]
    space = pl.BlockSpec(memory_space=pltpu.VMEM)
    return pl.pallas_call(
        without(kernel, len(operands), len(waits)),
        in_specs=[space] * len(operands) + [pl.BlockSpec(memory_space=pl.ANY)] * len(waits),
        out_specs=[space] * len(outs),
        out_shape=shapes,
        compiler_params=pltpu.CompilerParams(vmem_limit_bytes=limit),
        cost_estimate=work(flops, (*operands, *shapes)),
        name=name,
    )(*operands, *map(far, waits))


def whole_block(array):
    return pl.BlockSpec(array.shape, lambda j: (0,) * array.ndim)


def by_pairs(kernel, name, core, operands, pieces, blocks, outs, scratch, flops, waits):
    shapes = [jax.ShapeDtypeStruct(shape, dtype) for shape, dtype, _ in outs]
    taken = 1 + len(operands) + 2 * len(pieces[0]) + len(blocks)
    return pl.pallas_call(
        without(functools.partial(kernel, len(pieces[0])), taken, len(waits)),
        grid=(len(pieces[0]),),
        in_specs=[pl.BlockSpec(memory_space=pltpu.SMEM)]
        + [whole_block(array) for array in (*operands, *pieces[0], *pieces[1])]
        + [spec for _, spec in blocks]
        + [pl.BlockSpec(memory_space=pl.ANY)] * len(waits),
        out_specs=[spec for _, _, spec in outs],
        out_shape=shapes,
        scratch_shapes=scratch,
        compiler_params=pltpu.CompilerParams(vmem_limit_bytes=KERNEL_VMEM),
        cost_estimate=work(flops, (*operands, *pieces[0], *pieces[1], *shapes)),
        name=name,
    )(core, *operands, *pieces[0], *pieces[1], *[array for array, _ in blocks], *map(far, waits))


def mlp_up_back(rows, slope, pieces, waits):
    length, units = slope.shape
    unit, half = pieces[0][0].shape
    count = len(pieces[0])
    every, space = pl.BlockSpec(memory_space=pl.ANY), pl.BlockSpec(memory_space=pltpu.VMEM)
    return pl.pallas_call(
        without(functools.partial(mlp_up_back_kernel, count), 3 + 2 * count, len(waits)),
        in_specs=[space] * 2 + [every] * (1 + 2 * count + len(waits)),
        out_specs=space,
        out_shape=jax.ShapeDtypeStruct((length, units), jnp.bfloat16),
        scratch_shapes=[
            pltpu.VMEM((count, unit, 2 * half), jnp.bfloat16),
            pltpu.VMEM((length, units), jnp.bfloat16),
            pltpu.SemaphoreType.DMA((count, 3)),
        ],
        compiler_params=pltpu.CompilerParams(vmem_limit_bytes=KERNEL_VMEM),
        name="mlp_up_back",
    )(*rows, *map(far, (slope, *pieces[0], *pieces[1], *waits)))


def attend(core, tables, rows, pieces, waits):
    half, features = rows[0].shape
    length, count = 2 * half, len(pieces[0])
    lanes = ((count, length, 128), jnp.bfloat16, pl.BlockSpec((1, length, 128), lambda j: (j, 0, 0)))
    lse = ((count, 2, length), jnp.float32, pl.BlockSpec((1, 2, length), lambda j: (j, 0, 0)))
    mixed = ((length, count * 128), jnp.bfloat16, pl.BlockSpec((length, 128), lambda j: (0, j)))
    return by_pairs(
        attend_kernel,
        "attend",
        core,
        (*tables, *rows),
        pieces,
        (),
        (lanes, lanes, lanes, lse, mixed),
        [pltpu.VMEM((features, 384), jnp.bfloat16)],
        count * length * (2 * features * 384 + 2 * PAIR_WORK * length),
        waits,
    )


def attend_back(core, tables, rows, pieces, base, waits, q, k, v, lse):
    half, features = rows[0].shape
    length, count = 2 * half, len(pieces[0])
    lanes = pl.BlockSpec((1, length, 128), lambda j: (base + j, 0, 0))
    lse_spec = pl.BlockSpec((1, 2, length), lambda j: (base + j, 0, 0))
    out = ((length, count * 384), jnp.bfloat16, pl.BlockSpec((length, 384), lambda j: (0, j)))
    return by_pairs(
        attend_back_kernel,
        "attend_back",
        core,
        (*tables, *rows),
        pieces,
        ((q, lanes), (k, lanes), (v, lanes), (lse, lse_spec)),
        (out,),
        [pltpu.VMEM((features, 128), jnp.bfloat16)] + [pltpu.VMEM((length, 128), jnp.float32)] * 3,
        count * length * (2 * features * 128 + 5 * PAIR_WORK * length),
        waits,
    )[0]


def exchanged(parts):
    return parts[0], flip_pairs(parts[1], 1)


def model_rows(kernel, name, lefts, pieces, waits=()):
    length, width = lefts[0].shape[0], 2 * MODEL_HALF
    outs = (((length // 2, width), jnp.float32), ((length // 2, width), jnp.bfloat16))
    hidden = sum(left.shape[1] for left in lefts)
    more = {"limit": KERNEL_VMEM, "flops": 2 * length * width * hidden, "waits": waits}
    return exchanged(on_chip(kernel, name, outs, *lefts, *pieces[0], *pieces[1], **more))


def flip_pairs(block, distance):
    size = lax.axis_size("dp")
    return lax.ppermute(block, "dp", [(i, i ^ distance) for i in range(size)])


def passed_on(block, step):
    size = lax.axis_size("tensor")
    return lax.ppermute(block, "tensor", [(i, (i + step) % size) for i in range(size)])


def dot_tn(left, right):
    return lax.dot_general(
        left, right, (((0,), (0,)), ((), ())), preferred_element_type=jnp.float32
    )


def fetch(first_ref, zeros, ones, buffers, sems):
    for section, sources in enumerate((zeros, ones)):

        @pl.when(first_ref[0] == section)
        def _():
            for i, (source, buffer) in enumerate(zip(sources, buffers)):
                pltpu.make_async_copy(source, buffer, sems.at[i]).start()

    def arrived(*places):
        for i in places:
            pltpu.make_async_copy(zeros[i], buffers[i], sems.at[i]).wait()

    return arrived


def mlp_grads_kernel(base, section_ref, *refs):
    (own_one, other_one, own_two, other_two), (rows, d_up, gelu, d_down, sems) = refs[12:16], refs[16:]
    half, size = own_one.shape[0] // 2, own_one.shape[1]
    cols = pl.ds(base * size, 2 * size)

    def parts(own_rows, other_rows, d_up_ref, gelu_ref, own_grad, other_grad):
        whole = (d_up_ref.at[:, cols], gelu_ref.at[:, cols])
        return (own_rows, other_rows, *whole, own_grad, other_grad)

    count = refs[0].shape[0]
    buffers = (
        rows.at[pl.ds(0, count)],
        rows.at[pl.ds(count, count)],
        d_up,
        gelu,
        d_down.at[pl.ds(0, count)],
        d_down.at[pl.ds(count, count)],
    )
    arrived = fetch(section_ref, parts(*refs[:6]), parts(*refs[6:12]), buffers, sems)
    for j, own, other in ((1, own_two, other_two), (0, own_one, other_one)):
        cols = slice(j * size, (j + 1) * size)
        if j == 1:
            arrived(0, 1, 2)
        up = dot_tn(rows[...], d_up[:, cols])
        own[:half] = up[:half]
        other[:half] = up[half:].astype(jnp.bfloat16)
        if j == 1:
            arrived(3, 4, 5)
        down = dot_tn(gelu[:, cols], d_down[...])
        own[half:] = down[:, :half]
        other[half:] = down[:, half:].astype(jnp.bfloat16)


def attn_grads_kernel(base, section_ref, *refs):
    (own_one, other_one, own_two, other_two), (rows, d_qkv, mixed, d_attn, sems) = refs[12:16], refs[16:]
    half, size = own_one.shape[0], d_qkv.shape[1] // 2
    count = refs[0].shape[0]
    cols = pl.ds(base * 128, 256)

    def parts(own_rows, other_rows, d_qkv_ref, mixed_ref, own_grad, other_grad):
        return (own_rows, other_rows, d_qkv_ref, mixed_ref.at[:, cols], own_grad, other_grad)

    buffers = (
        rows.at[pl.ds(0, count)],
        rows.at[pl.ds(count, count)],
        d_qkv,
        mixed,
        d_attn.at[pl.ds(0, count)],
        d_attn.at[pl.ds(count, count)],
    )
    arrived = fetch(section_ref, parts(*refs[:6]), parts(*refs[6:12]), buffers, sems)
    for j, own, other in ((1, own_two, other_two), (0, own_one, other_one)):
        if j == 1:
            arrived(0, 1, 2)
        qkv = dot_tn(rows[...], d_qkv[:, j * size : (j + 1) * size])
        if j == 1:
            arrived(3, 4, 5)
        out = dot_tn(d_attn[...], mixed[:, j * 128 : (j + 1) * 128])
        own[:, :size] = qkv[:half]
        own[:, size:] = out[:half]
        other[:, :size] = qkv[half:].astype(jnp.bfloat16)
        other[:, size:] = out[half:].astype(jnp.bfloat16)


def weight_grads(kernel, name, base, section, zeros, ones, shape, columns, waits=()):
    length = 2 * zeros[0].shape[0]
    width = zeros[0].shape[1]
    every = pl.BlockSpec(memory_space=pl.ANY)
    space = pl.BlockSpec(memory_space=pltpu.VMEM)
    arrays = (*zeros, *ones)
    first, second, third, fourth = pl.pallas_call(
        without(functools.partial(kernel, base), 1 + len(arrays), len(waits)),
        in_specs=[pl.BlockSpec(memory_space=pltpu.SMEM)] + [every] * (len(arrays) + len(waits)),
        out_specs=[space] * 4,
        out_shape=[
            jax.ShapeDtypeStruct(shape, jnp.float32),
            jax.ShapeDtypeStruct(shape, jnp.bfloat16),
        ]
        * 2,
        scratch_shapes=[
            pltpu.VMEM((length, width), jnp.bfloat16),
            pltpu.VMEM((length, columns[0]), jnp.bfloat16),
            pltpu.VMEM((length, columns[1]), jnp.bfloat16),
            pltpu.VMEM((length, width), jnp.bfloat16),
            pltpu.SemaphoreType.DMA((6,)),
        ],
        compiler_params=pltpu.CompilerParams(vmem_limit_bytes=KERNEL_VMEM),
        name=name,
    )(section, *map(far, (*arrays, *waits)))
    return [(first, flip_pairs(second, 2)), (third, flip_pairs(fourth, 2))]


def moved_kernel(own_ref, other_ref, *refs):
    out_ref = refs[-1]

    def body(i, carry):
        spot = pl.ds(pl.multiple_of(i * CHUNK, CHUNK), CHUNK)
        total = own_ref[spot, :]
        for ref in (other_ref, *refs[:-1]):
            total = total + wide(ref, spot)
        out_ref[spot, :] = total.astype(jnp.bfloat16)
        return carry

    lax.fori_loop(0, own_ref.shape[0] // CHUNK, body, 0)


def gates_kernel(up_ref, down_ref, up_out, down_out):
    up_out[...] = up_ref[...]
    down_out[...] = down_ref[...]


def gate_kernel(piece_ref, out_ref):
    out_ref[...] = piece_ref[...]


def mlp_sum_kernel(core_ref, own_ref, other_ref, moved_ref, up_keep, down_keep, up_send, down_send):
    half = own_ref.shape[0] // 2
    size = up_keep.shape[0]

    def total(rows, cols):
        more = other_ref[rows, cols].astype(jnp.float32) + moved_ref[rows, cols].astype(jnp.float32)
        return own_ref[rows, cols] + more

    for core in range(2):

        @pl.when(core_ref[0] == core)
        def _():
            for place, up, down in ((core, up_keep, down_keep), (1 - core, up_send, down_send)):
                spot = slice(place * size, (place + 1) * size)
                up[...] = total(spot, slice(None))
                down[...] = total(slice(half, None), spot)


def mlp_join_kernel(core_ref, up_keep, down_keep, up_sent, down_sent, up_out, down_out):
    size = up_keep.shape[1]
    for core in range(2):

        @pl.when(core_ref[0] == core)
        def _():
            places = ((core, up_keep, down_keep), (1 - core, up_sent, down_sent))
            for place, up, down in places:
                spot = slice(place * size, (place + 1) * size)
                up_out[:, spot] = up[...]
                down_out[spot] = down[...]


def chosen_kernel(place_ref, zero_ref, one_ref, out_ref):
    half = out_ref.shape[1] // 2
    for section, rows_ref in enumerate((zero_ref, one_ref)):
        for upper in range(2):

            @pl.when(jnp.logical_and(place_ref[0] == section, place_ref[1] == upper))
            def _():
                for side in range(2):
                    place = (side + upper) % 2 * half
                    out_ref[:, place : place + half] = rows_ref[:, side * half : (side + 1) * half]


def pick_kernel(core_ref, rows_ref, keep_ref, send_ref):
    count = keep_ref.shape[0]
    keep_ref[...] = rows_ref[pl.ds(core_ref[0] * count, count)]
    send_ref[...] = rows_ref[pl.ds((1 - core_ref[0]) * count, count)]


def in_order_kernel(core_ref, keep_ref, sent_ref, out_ref):
    out_ref[:, pl.ds(core_ref[0], 1)] = keep_ref[...][:, None]
    out_ref[:, pl.ds(1 - core_ref[0], 1)] = sent_ref[...][:, None]


def with_core(kernel, name, core, outs, *operands, waits=()):
    space = pl.BlockSpec(memory_space=pltpu.VMEM)
    return pl.pallas_call(
        without(kernel, 1 + len(operands), len(waits)),
        in_specs=[pl.BlockSpec(memory_space=pltpu.SMEM)]
        + [space] * len(operands)
        + [pl.BlockSpec(memory_space=pl.ANY)] * len(waits),
        out_specs=[space] * len(outs),
        out_shape=[jax.ShapeDtypeStruct(shape, dtype) for shape, dtype in outs],
        compiler_params=pltpu.CompilerParams(vmem_limit_bytes=ROWS_VMEM),
        name=name,
    )(core, *operands, *map(far, waits))


def last_sum_kernel(core_ref, own_ref, other_ref, moved_ref, keep_ref, send_ref):
    rows = keep_ref.shape[0]

    def total(block):
        spot = pl.ds(pl.multiple_of(block * rows, rows), rows)
        return own_ref[spot, :] + wide(other_ref, spot) + wide(moved_ref, spot)

    keep_ref[...] = total(core_ref[0])
    send_ref[...] = total(1 - core_ref[0])


def joined_kernel(spots, core_ref, keep_ref, sent_ref, column_ref, row_ref):
    size = row_ref.shape[0] // 2
    for core in range(2):

        @pl.when(core_ref[0] == core)
        def _():
            for place, source in ((core, keep_ref), (1 - core, sent_ref)):
                for start, stop, to in spots:
                    step = stop - start
                    column_ref[:, to + place * step : to + (place + 1) * step] = source[:, start:stop]
                row_ref[place * size : (place + 1) * size] = source[:, spots[-1][1] :].T


def per_chip(
    inputs,
    out_cotangent,
    group_ids,
    group_weights,
    gains,
    qkv_weight,
    out_weight,
    up_weight,
    down_weight,
):
    micro, row_count, width = inputs.shape
    tensor = lax.axis_size("tensor")
    part = row_count // 2
    wide_half = width // 2
    length = tensor * row_count
    half = length // 2
    first = lax.axis_index("section") == 0
    place = lax.axis_index("dp")
    core = place % 2
    upper = place // 2 % 2
    core_zero = core == 0
    low_half = upper == 0

    def ordered(mine, other):
        return jnp.where(core_zero, mine, other), jnp.where(core_zero, other, mine)

    def own_first(values):
        return jnp.where(low_half, values, jnp.roll(values, wide_half, axis=-1))

    def both_rows(own):
        return own, flip_pairs(own, 1)

    def to_chip(block):
        split = block.reshape((micro, 2, part) + block.shape[2:])
        mine = lax.dynamic_index_in_dim(split, core, 1, keepdims=False)
        other = lax.dynamic_index_in_dim(split, 1 - core, 1, keepdims=False)
        return lax.all_to_all(
            jnp.concatenate(ordered(mine, flip_pairs(other, 1))), "tensor", 0, 0, tiled=True
        )

    def from_chip(spread_out, waits=()):
        piece = ((micro, part, width), jnp.bfloat16)
        keep, send = with_core(
            pick_kernel, "pick", core_word, (piece, piece), spread_out, waits=waits
        )
        outs = (((micro, 2, part, width), jnp.bfloat16),)
        (rows,) = with_core(
            in_order_kernel, "in_order", core_word, outs, keep, flip_pairs(send, 1)
        )
        return rows.reshape(micro, row_count, width)

    def columns(local):
        size = local.shape[-1] // 2
        mid = (0,) * (local.ndim - 2)
        piece = lax.dynamic_slice(
            local,
            (wide_half * upper, *mid, size * core),
            (wide_half, *local.shape[1:-1], size),
        )
        return piece.reshape(wide_half, -1)

    def rows(local):
        size = local.shape[0] // 2
        return lax.dynamic_slice(local, (size * core, wide_half * upper), (size, wide_half))

    core_word = core.astype(jnp.int32).reshape(1)
    attn_piece = jnp.concatenate([columns(qkv_weight[0]), rows(out_weight[0]).T], axis=1)

    def spread(piece):
        pieces = [piece]
        for _ in range(tensor - 1):
            pieces.append(passed_on(pieces[-1], 1))
        return pieces

    up_piece, down_piece = columns(up_weight[0]), rows(down_weight[0])
    up_other, down_other = [flip_pairs(up_piece, 2)], [flip_pairs(down_piece, 2)]
    attn_own = [attn_piece, passed_on(attn_piece, 1)]
    attn_first = flip_pairs(attn_piece, 2)
    outs = ((attn_piece.shape, attn_piece.dtype),)
    attn_own[1] = on_chip(gate_kernel, "gate", outs, attn_own[1], waits=(attn_first, up_other[0]))[0]
    attn_own += spread(attn_own[1])[1:-1]
    attn_other = [attn_first] + [flip_pairs(piece, 2) for piece in attn_own[1:]]
    outs = tuple((piece.shape, piece.dtype) for piece in (up_piece, down_piece))
    up_piece, down_piece = on_chip(
        gates_kernel, "gate", outs, up_piece, down_piece, waits=(attn_own[2], attn_other[0], down_other[0])
    )
    up_own, down_own = spread(up_piece), spread(down_piece)
    up_other += [flip_pairs(piece, 2) for piece in up_own[1:]]
    down_other += [flip_pairs(piece, 2) for piece in down_own[1:]]
    w_attn, w_up, w_down = (attn_own, attn_other), (up_own, up_other), (down_own, down_other)
    unit = up_piece.shape[1]
    units = tensor * unit

    group_count = group_weights.shape[0]
    matches = group_ids[..., None] == jnp.arange(group_count, dtype=jnp.int32)
    row_scale = jnp.sum(jnp.where(matches, group_weights, 0.0), axis=-1)
    weighted = (out_cotangent.astype(jnp.float32) * row_scale[..., None]).astype(jnp.bfloat16)
    start = to_chip(own_first(jnp.where(first, inputs, weighted))).reshape(half, width)
    gain = own_first(gains[0])

    turns = jnp.arange(half, dtype=jnp.int32)
    turns = turns // part * row_count + turns % part
    positions = jnp.concatenate([turns + core * part, turns + (1 - core) * part])
    freqs = 10000.0 ** (-2.0 * jnp.arange(HEAD_DIM // 2, dtype=jnp.float32) / HEAD_DIM)
    angles = positions.astype(jnp.float32)[:, None] * freqs[None, :]
    cos_part, sin_part = jnp.cos(angles), jnp.sin(angles)
    tables = (
        jnp.concatenate([cos_part] * 4, axis=1),
        jnp.concatenate([-sin_part, sin_part] * 2, axis=1),
    )
    row32, row16 = ((half, width), jnp.float32), ((half, width), jnp.bfloat16)
    unit16 = ((length, units), jnp.bfloat16)
    sum32 = ((1, width), jnp.float32)
    mlp_cost = {"limit": KERNEL_VMEM, "flops": 2 * length * width * units}
    every = slice(None)

    def model_kernel(cols, lefts=1):
        return functools.partial(to_model_kernel, lefts, tensor, cols)

    down_kernel = functools.partial(mlp_down_kernel, tensor)

    def forward(layer_input, waits):
        attn_in = both_rows(
            on_chip(norm_in_kernel, "norm_in", (row16,), gain, layer_input, waits=waits[0])[0]
        )
        *heads, mixed = attend(core_word, tables, attn_in, w_attn, waits[1])
        parts = model_rows(model_kernel(OUT), "attn_out", [mixed], w_attn, waits[2])
        operands = (gain, layer_input, *parts)
        branch, hidden, mlp_in = on_chip(
            after_attention_kernel, "after_attn", (row32, row32, row16), *operands, waits=waits[3]
        )
        mlp_in = both_rows(mlp_in)
        kernel = functools.partial(mlp_up_kernel, tensor)
        operands = (*mlp_in, *w_up[0], *w_up[1])
        gelu_out, slope = on_chip(kernel, "mlp_up", (unit16, unit16), *operands, **mlp_cost)
        parts = model_rows(down_kernel, "mlp_down", [gelu_out], w_down)
        mlp_branch, result = on_chip(
            after_mlp_kernel, "after_mlp", (row32, row16), gain, hidden, *parts
        )
        saved = (layer_input, heads, branch, hidden, slope, mlp_branch)
        return result, saved, (attn_in, mixed, mlp_in, gelu_out)

    def backward(grad, saved, hook, late=()):
        layer_input, heads, branch, hidden, slope, mlp_branch = saved
        operands = (gain, grad, mlp_branch)
        d_down, sum_three = on_chip(
            into_mlp_back_kernel, "into_mlp_back", (row16, sum32), *operands
        )
        d_down = both_rows(d_down)
        d_up = mlp_up_back(d_down, slope, w_down, late)
        waits = hook(d_down, d_up)
        parts = model_rows(model_kernel(every), "mlp_back", [d_up], w_up, waits)
        waits = hook()
        operands = (gain, grad, *parts, hidden, branch)
        outs = (row32, row16, sum32, sum32)
        d_hidden, d_attn, sum_one, sum_two = on_chip(
            into_attention_back_kernel, "into_attn_back", outs, *operands, waits=waits
        )
        d_attn = both_rows(d_attn)
        waits = hook(d_attn)
        d_qkv = []
        for base in reversed(range(0, tensor, 2)):
            some = [side[base : base + 2] for side in w_attn]
            now = attend_back(core_word, tables, d_attn, some, base, waits, *heads)
            d_qkv.insert(0, now)
            waits = hook(now)
        parts = model_rows(model_kernel(QKV, 2), "attn_back", d_qkv, w_attn, waits)
        operands = (gain, layer_input, *parts, d_hidden)
        d_input, sum_zero = on_chip(
            out_of_layer_kernel, "out_of_layer", (row16, sum32), *operands, waits=hook()
        )
        sums = jnp.concatenate([sum_zero, sum_one, sum_two, sum_three])
        return d_input, (d_qkv, d_attn, d_up, d_down), sums

    low_zero, saved_zero, lefts_zero = forward(
        start,
        (
            (up_piece, up_other[0], down_other[0]),
            (up_own[1], down_own[1]),
            (up_own[2], down_own[2], up_other[1], down_other[1]),
            (up_own[3], down_own[3], up_other[2], down_other[2]),
        ),
    )
    low_one, saved_one, lefts_one = forward(shifted(low_zero, "section", 1), ((),) * 4)
    grad_one, rights_one, gain_one = backward(start, saved_one, lambda *new: ())
    received = shifted(grad_one, "section", -1)

    lows = lax.optimization_barrier((low_zero, low_one, grad_one))[:2]
    lows = own_first(jnp.where(first, *lows)).reshape(tensor, part, width)
    lows = lax.all_to_all(lows, "tensor", 0, 0, tiled=True)

    section_word = lax.axis_index("section").astype(jnp.int32).reshape(1)

    def mlp_leaves(base, waits=()):
        zeros = (*lefts_zero[2], d_up, lefts_zero[3], *d_down)
        ones = (*lefts_one[2], rights_one[2], lefts_one[3], *rights_one[3])
        mlp_sums[base : base + 2] = weight_grads(
            mlp_grads_kernel,
            "mlp_grads",
            base,
            section_word,
            zeros,
            ones,
            (wide_half + unit, unit),
            (2 * unit, 2 * unit),
            waits,
        )

    def attn_leaves(base, d_qkv, waits):
        zeros = (*lefts_zero[0], d_qkv, lefts_zero[1], *d_attn)
        ones = (*lefts_one[0], rights_one[0][base // 2], lefts_one[1], *rights_one[1])
        attn_sums[base : base + 2] = weight_grads(
            attn_grads_kernel,
            "attn_grads",
            base,
            section_word,
            zeros,
            ones,
            (wide_half, 512),
            (768, 256),
            waits,
        )

    def moves_on(piece, *moved, waits=()):
        outs = ((piece[1].shape, jnp.bfloat16),)
        (total,) = on_chip(moved_kernel, "moved", outs, *piece, *moved, waits=waits)
        return total, passed_on(total, -1)

    mlp_sums, attn_sums = [None] * tensor, [None] * tensor
    mlp_moves, attn_moves = [None] * tensor, [None] * tensor
    hooks = iter(range(6))

    def hook(*new):
        nonlocal d_down, d_up, d_attn, outputs
        turn = next(hooks)
        if turn == 0:
            d_down, d_up = new
            mlp_leaves(2)
            return (mlp_sums[3][0],)
        if turn == 1:
            return ()
        if turn == 2:
            (d_attn,) = new
            outputs = from_chip(lows, d_attn[:1])
            total, mlp_moves[3] = moves_on(mlp_sums[3], waits=(outputs,))
            mlp_leaves(0, (total,))
            return (mlp_sums[1][0],)
        if turn == 3:
            total, mlp_moves[2] = moves_on(mlp_sums[2], mlp_moves[3], waits=new)
            attn_leaves(2, new[0], (total,))
            return (mlp_sums[2][1], mlp_moves[3], attn_sums[3][0])
        if turn == 4:
            total, mlp_moves[1] = moves_on(mlp_sums[1], mlp_moves[2], waits=new)
            attn_leaves(0, new[0], (total,))
            total, attn_moves[3] = moves_on(attn_sums[3], waits=attn_sums[1][:1])
            return (total, mlp_moves[1], mlp_sums[0][1])
        return attn_sums[2][1:]

    d_down = d_up = d_attn = outputs = None
    grad_zero, rights_zero, gain_zero = backward(received, saved_zero, hook, (lows,))
    _, attn_moves[2] = moves_on(attn_sums[2], attn_moves[3])
    place_word = jnp.stack([lax.axis_index("section"), upper]).astype(jnp.int32)
    (grads_chosen,) = with_core(
        chosen_kernel,
        "chosen",
        place_word,
        (row16,),
        grad_zero,
        grad_one,
        waits=(attn_moves[2], attn_sums[1][1]),
    )
    grads = lax.all_to_all(
        grads_chosen.reshape(tensor, part, width), "tensor", 0, 0, tiled=True
    )

    block32 = ((wide_half // 2, unit), jnp.float32)
    down32 = ((unit, wide_half // 2), jnp.float32)
    up_keep, down_keep, up_send, down_send = with_core(
        mlp_sum_kernel,
        "mlp_sum",
        core_word,
        (block32, down32, block32, down32),
        *mlp_sums[0],
        mlp_moves[1],
        waits=(grads_chosen,),
    )
    outs = (
        ((wide_half // 2, 2 * unit), jnp.float32),
        ((2 * unit, wide_half // 2), jnp.float32),
    )
    sent = flip_pairs(up_send, 1), flip_pairs(down_send, 1)
    up_grad, down_grad = with_core(
        mlp_join_kernel, "mlp_join", core_word, outs, up_keep, down_keep, *sent
    )
    waits = (grads_chosen, attn_sums[0][1])
    last, attn_moves[1] = moves_on(attn_sums[1], attn_moves[2], waits=waits)
    gain_total = own_first(jnp.where(first, gain_zero, gain_one))
    count = tensor * lax.axis_size("dp")
    gain_parts = gain_total.reshape(4, count, width // count).swapaxes(0, 1)
    outs = ((gain_parts.shape, gain_parts.dtype),)
    (gain_parts,) = on_chip(gate_kernel, "gate", outs, gain_parts, waits=(last,))
    gain_parts = lax.all_to_all(gain_parts, ("dp", "tensor"), 0, 0, tiled=True)
    gains_grad = jnp.sum(gain_parts, axis=0)
    grads = from_chip(grads, (attn_moves[1], gains_grad))
    outs = (((wide_half // 2, 512), jnp.float32),) * 2
    keep, send = with_core(
        last_sum_kernel,
        "attn_sum",
        core_word,
        outs,
        *attn_sums[0],
        attn_moves[1],
        waits=(grads, outputs, gains_grad, up_grad),
    )
    spots = tuple((i * 128, (i + 1) * 128, i * 256) for i in range(3))
    outs = (((wide_half // 2, 768), jnp.float32), ((256, wide_half // 2), jnp.float32))
    kernel = functools.partial(joined_kernel, spots)
    qkv_grad, out_grad = with_core(
        kernel, "attn_join", core_word, outs, keep, flip_pairs(send, 1)
    )
    qkv_grad = qkv_grad.reshape(wide_half // 2, 3, -1)

    return (
        outputs[None],
        grads[None],
        gains_grad[None],
        qkv_grad[None],
        out_grad[None],
        up_grad[None],
        down_grad[None],
    )


def takes_chips(sizes):
    return sizes["section"] == 2 and sizes["dp"] == 4 and sizes["tensor"] == 4


def solution(mesh):
    placed = (
        P("dp", "tensor", None),
        P("dp", "tensor", None),
        P("dp", "tensor"),
        P(),
        P("section", None, None),
        P("section", None, None, "tensor"),
        P("section", "tensor", None),
        P("section", None, "tensor"),
        P("section", "tensor", None),
    )
    body = per_chip if takes_chips(dict(mesh.shape)) else per_device
    return jax.shard_map(
        body,
        mesh=mesh,
        in_specs=placed,
        out_specs=(
            P("section", "dp", "tensor", None),
            P("section", "dp", "tensor", None),
            P("section", None, ("dp", "tensor")),
            P("section", "dp", None, "tensor"),
            P("section", "tensor", "dp"),
            P("section", "dp", "tensor"),
            P("section", "tensor", "dp"),
        ),
        check_vma=False,
    )
```

```python
import functools
import math

import jax
import jax.numpy as jnp
from jax import lax
from jax.experimental import pallas as pl
from jax.experimental.pallas import tpu as pltpu
from jax.sharding import PartitionSpec as P

HEAD_DIM = 64


NORM_EPSILON = 1e-06
TILE = 128
PAIR_WORK = 1024
MODEL_HALF = 512
QKV = slice(0, 384)
OUT = slice(384, 512)
CHUNK = 32
KERNEL_VMEM = 20 << 20
ROWS_VMEM = 3 << 20


def shifted(block, axis, distance):
    devices = range(lax.axis_size(axis))
    route = [(i - distance, i) for i in devices if i - distance in devices]
    return lax.ppermute(block, axis, route)


def norm_rows(vector, weight_gain):
    return (
        vector
        * lax.rsqrt(jnp.mean(vector * vector, axis=-1, keepdims=True) + NORM_EPSILON)
        * weight_gain
    )


def rotary_tables(seq_len, head_width):
    half_width = head_width // 2
    freqs = 10000.0 ** (-2.0 * jnp.arange(half_width, dtype=jnp.float32) / head_width)
    angles = jnp.arange(seq_len, dtype=jnp.float32)[:, None] * freqs[None, :]
    return (jnp.cos(angles), jnp.sin(angles))


def rotate(vector, cos_table, sin_table):
    first_half, second_half = jnp.split(vector, 2, axis=-1)
    cos_part = cos_table[:, None, :]
    sin_part = sin_table[:, None, :]
    return jnp.concatenate(
        [
            first_half * cos_part - second_half * sin_part,
            second_half * cos_part + first_half * sin_part,
        ],
        axis=-1,
    )


def contract(left_rows, right_rows):
    return lax.dot_general(
        left_rows, right_rows, (((0,), (0,)), ((), ())), preferred_element_type=jnp.float32
    )


def gather_rows(row_values, weight):

    def project(shard_rows, offset):
        return (shard_rows, jnp.dot(shard_rows, weight, preferred_element_type=jnp.float32))

    return project(lax.all_gather(row_values, "tensor", axis=0, tiled=True), jnp.int32(0))


def scatter_rows(row_values, weight, row_count):

    def partial_term(offset, span):
        return jnp.dot(row_values, weight, preferred_element_type=jnp.float32)

    return lax.psum_scatter(
        partial_term(jnp.int32(0), lax.axis_size("tensor") * row_count),
        "tensor",
        scatter_dimension=0,
        tiled=True,
    )


def gather_grads(row_values, weight):

    def project(shard_rows, offset):
        return (shard_rows, jnp.dot(shard_rows, weight.T, preferred_element_type=jnp.float32))

    return project(lax.all_gather(row_values, "tensor", axis=0, tiled=True), jnp.int32(0))


def scatter_grads(row_values, weight, row_count):

    def partial_term(offset, span):
        return jnp.dot(row_values, weight.T, preferred_element_type=jnp.float32)

    return lax.psum_scatter(
        partial_term(jnp.int32(0), lax.axis_size("tensor") * row_count),
        "tensor",
        scatter_dimension=0,
        tiled=True,
    )


def attention_probs(queries, key_rows):
    scores = jnp.einsum(
        "qhd,khd->hqk", queries, key_rows, preferred_element_type=jnp.float32
    ) * HEAD_DIM ** (-0.5)
    length = queries.shape[0]
    positions = jnp.arange(length, dtype=jnp.int32)
    causal = positions[:, None] >= positions[None, :]
    scores = jnp.where(causal[None], scores, -1e30)
    expos = jnp.exp(scores - jnp.max(scores, axis=-1, keepdims=True))
    return expos / jnp.sum(expos, axis=-1, keepdims=True)


def layer_forward(layer_input, weights):
    gains, w_qkv, w_out, w_up, w_down = weights
    row_count, model_width = layer_input.shape
    attn_in = norm_rows(layer_input, gains[0]).astype(jnp.bfloat16)
    gathered_a, qkv = gather_rows(attn_in, w_qkv.reshape(model_width, -1))
    length = qkv.shape[0]
    head_count = w_qkv.shape[2] // HEAD_DIM
    qkv = qkv.reshape(length, 3, head_count, HEAD_DIM)
    cos_table, sin_table = rotary_tables(length, HEAD_DIM)
    queries = rotate(qkv[:, 0], cos_table, sin_table).astype(jnp.bfloat16)
    key_rows = rotate(qkv[:, 1], cos_table, sin_table).astype(jnp.bfloat16)
    values = qkv[:, 2].astype(jnp.bfloat16)
    attn_probs = attention_probs(queries, key_rows).astype(jnp.bfloat16)
    mixed = jnp.einsum("hqk,khd->qhd", attn_probs, values, preferred_element_type=jnp.float32)
    mixed = mixed.reshape(length, -1).astype(jnp.bfloat16)
    attn_branch = scatter_rows(mixed, w_out, row_count)
    hidden = layer_input + norm_rows(attn_branch, gains[1])
    mlp_in = norm_rows(hidden, gains[2]).astype(jnp.bfloat16)
    gathered_c, up_act = gather_rows(mlp_in, w_up)
    gelu_out = jax.nn.gelu(up_act, approximate=True).astype(jnp.bfloat16)
    down_branch = scatter_rows(gelu_out, w_down, row_count)
    result = hidden + norm_rows(down_branch, gains[3])
    kept_values = (
        gathered_a,
        queries,
        key_rows,
        values,
        mixed,
        attn_branch,
        hidden,
        gathered_c,
        up_act,
        gelu_out,
        down_branch,
    )
    return (result, kept_values)


def layer_backward(layer_input, grad_result, kept_values, weights):
    gains, w_qkv, w_out, w_up, w_down = weights
    (
        gathered_a,
        queries,
        key_rows,
        values,
        mixed,
        attn_branch,
        hidden,
        gathered_c,
        up_act,
        gelu_out,
        down_branch,
    ) = kept_values
    row_count, model_width = layer_input.shape
    pullback = jax.vjp(norm_rows, down_branch, gains[3])[1]
    grad_down, gain_three = pullback(grad_result)
    gathered_dd, grad_gelu = gather_grads(grad_down.astype(jnp.bfloat16), w_down)
    down_total = contract(gelu_out, gathered_dd)
    pullback = jax.vjp(lambda vector: jax.nn.gelu(vector, approximate=True), up_act)[1]
    grad_up = pullback(grad_gelu)[0].astype(jnp.bfloat16)
    up_total = contract(gathered_c, grad_up)
    grad_mlp = scatter_grads(grad_up, w_up, row_count)
    pullback = jax.vjp(norm_rows, hidden, gains[2])[1]
    grad_norm_mlp, gain_two = pullback(grad_mlp)
    grad_hidden = grad_result + grad_norm_mlp
    pullback = jax.vjp(norm_rows, attn_branch, gains[1])[1]
    grad_attn, gain_one = pullback(grad_hidden)
    gathered_da, grad_mixed = gather_grads(grad_attn.astype(jnp.bfloat16), w_out)
    out_total = contract(mixed, gathered_da)
    length = grad_mixed.shape[0]
    head_count = w_qkv.shape[2] // HEAD_DIM
    grad_mixed = grad_mixed.astype(jnp.bfloat16).reshape(length, head_count, HEAD_DIM)
    attn_probs = attention_probs(queries, key_rows)
    probs_low = attn_probs.astype(jnp.bfloat16)
    grad_probs = jnp.einsum("qhd,khd->hqk", grad_mixed, values, preferred_element_type=jnp.float32)
    grad_values = jnp.einsum(
        "hqk,qhd->khd", probs_low, grad_mixed, preferred_element_type=jnp.float32
    )
    row_dots = jnp.sum(grad_probs * attn_probs, axis=-1, keepdims=True)
    grad_scores = (attn_probs * (grad_probs - row_dots)).astype(jnp.bfloat16)
    scale_value = HEAD_DIM ** (-0.5)
    grad_queries = (
        jnp.einsum("hqk,khd->qhd", grad_scores, key_rows, preferred_element_type=jnp.float32)
        * scale_value
    )
    grad_keys = (
        jnp.einsum("hqk,qhd->khd", grad_scores, queries, preferred_element_type=jnp.float32)
        * scale_value
    )
    cos_table, sin_table = rotary_tables(length, HEAD_DIM)
    pullback = jax.vjp(lambda vector: rotate(vector, cos_table, sin_table), grad_queries)[1]
    grad_q_raw = pullback(grad_queries)[0]
    grad_k_raw = pullback(grad_keys)[0]
    grad_qkv = (
        jnp.stack([grad_q_raw, grad_k_raw, grad_values], axis=1)
        .reshape(length, -1)
        .astype(jnp.bfloat16)
    )
    qkv_total = contract(gathered_a, grad_qkv).reshape(model_width, 3, -1)
    grad_attn_in = scatter_grads(grad_qkv, w_qkv.reshape(model_width, -1), row_count)
    pullback = jax.vjp(norm_rows, layer_input, gains[0])[1]
    grad_norm_in, gain_zero = pullback(grad_attn_in)
    grad_input = grad_hidden + grad_norm_in
    gain_total = jnp.stack([gain_zero, gain_one, gain_two, gain_three])
    return (grad_input, (gain_total, qkv_total, out_total, up_total, down_total))


def lagged(first_section, stacked):
    blank = jnp.zeros_like(stacked[:1])
    earlier = jnp.concatenate([blank, stacked[:-1]])
    later = jnp.concatenate([stacked[1:], blank])
    return jnp.where(first_section, earlier, later)


def per_device(
    inputs,
    out_cotangent,
    group_ids,
    group_weights,
    gains,
    qkv_weight,
    out_weight,
    up_weight,
    down_weight,
):
    weights = (gains[0], qkv_weight[0], out_weight[0], up_weight[0], down_weight[0])
    micro_count, row_count, model_width = inputs.shape
    first_section = lax.axis_index("section") == 0
    group_count = group_weights.shape[0]
    matches = group_ids[..., None] == jnp.arange(group_count, dtype=jnp.int32)
    row_scale = jnp.sum(jnp.where(matches, group_weights, 0.0), axis=-1)
    scaled = out_cotangent.astype(jnp.float32) * row_scale[..., None]
    padded = jnp.concatenate([inputs, jnp.zeros((1, row_count, model_width), jnp.bfloat16)])

    def forward_tick(received, fresh_input):
        layer_input = jnp.where(first_section, fresh_input, received)
        result, kept_values = layer_forward(layer_input.astype(jnp.float32), weights)
        result_low = result.astype(jnp.bfloat16)
        outgoing = shifted(result_low, "section", 1)
        stashed = ()
        return (outgoing, (layer_input, result_low, stashed))

    start_rows = jnp.zeros((row_count, model_width), jnp.bfloat16)
    _, (layer_inputs, layer_results, stashed) = lax.scan(forward_tick, start_rows, padded)
    layer_outputs = jnp.where(first_section, layer_results[:-1], layer_results[1:])[None]
    back_inputs = lagged(first_section, layer_inputs)
    back_stash = jax.tree.map(lambda stacked: lagged(first_section, stacked), stashed)
    grad_padded = jnp.concatenate([scaled, jnp.zeros((1, row_count, model_width), jnp.float32)])
    tick_index = jnp.arange(micro_count + 1, dtype=jnp.int32)
    tick_valid = jnp.where(first_section, tick_index >= 1, tick_index < micro_count).astype(
        jnp.float32
    )

    def backward_tick(carry, step_item):
        received, totals = carry
        layer_input, cotangent, valid_now, stash_now = step_item
        grad_now = jnp.where(first_section, received.astype(jnp.float32), cotangent)
        input_now = layer_input.astype(jnp.float32)
        kept_values = layer_forward(input_now, weights)[1]
        grad_input, layer_grads = layer_backward(input_now, grad_now, kept_values, weights)
        totals = jax.tree.map(lambda total, update: total + valid_now * update, totals, layer_grads)
        grad_low = grad_input.astype(jnp.bfloat16)
        outgoing = shifted(grad_low, "section", -1)
        return ((outgoing, totals), grad_low)

    start_totals = (
        jnp.zeros((4, model_width), jnp.float32),
        jnp.zeros(qkv_weight.shape[1:], jnp.float32),
        jnp.zeros(out_weight.shape[1:], jnp.float32),
        jnp.zeros(up_weight.shape[1:], jnp.float32),
        jnp.zeros(down_weight.shape[1:], jnp.float32),
    )
    (_, totals), grad_lows = lax.scan(
        backward_tick,
        (start_rows, start_totals),
        (back_inputs, grad_padded, tick_valid, back_stash),
    )
    input_grads = jnp.where(first_section, grad_lows[1:], grad_lows[:-1])[None]
    gain_total, qkv_total, out_total, up_total, down_total = totals
    gains_grad = lax.psum_scatter(gain_total, ("dp", "tensor"), scatter_dimension=1, tiled=True)
    qkv_grad, out_grad, up_grad, down_grad = (
        lax.psum_scatter(
            qkv_total.astype(jnp.bfloat16), "dp", scatter_dimension=0, tiled=True
        ).astype(jnp.float32),
        lax.psum_scatter(
            out_total.astype(jnp.bfloat16), "dp", scatter_dimension=1, tiled=True
        ).astype(jnp.float32),
        lax.psum_scatter(
            up_total.astype(jnp.bfloat16), "dp", scatter_dimension=0, tiled=True
        ).astype(jnp.float32),
        lax.psum_scatter(
            down_total.astype(jnp.bfloat16), "dp", scatter_dimension=1, tiled=True
        ).astype(jnp.float32),
    )
    return (
        layer_outputs,
        input_grads,
        gains_grad[None],
        qkv_grad[None],
        out_grad[None],
        up_grad[None],
        down_grad[None],
    )


def rotated(block, cos_rows, sin_rows):
    lane = lax.broadcasted_iota(jnp.int32, block.shape, 1)
    ahead = pltpu.roll(block, 96, 1)
    behind = pltpu.roll(block, 32, 1)
    swapped = jnp.where(lane % 64 < 32, ahead, behind)
    return block * cos_rows + swapped * sin_rows


def dot_nt(left, right):
    return lax.dot_general(
        left, right, (((1,), (1,)), ((), ())), preferred_element_type=jnp.float32
    )


def dot_nn(left, right):
    return jnp.dot(left, right, preferred_element_type=jnp.float32)


def model_weight(owns, others, cols):
    sides = [jnp.concatenate([ref[:, cols] for ref in refs], axis=1) for refs in (owns, others)]
    return jnp.concatenate(sides, axis=0)


def stacked_up(values):
    return jnp.concatenate(values, axis=0)


def edge_masks(core, rows):
    key = lax.broadcasted_iota(jnp.int32, (rows, 2 * rows), 0)
    query = lax.broadcasted_iota(jnp.int32, (rows, 2 * rows), 1)
    mine = query < rows
    place = jnp.where(mine, query + core * rows, query - rows + (1 - core) * rows)
    return (key + core * rows <= place, key + (1 - core) * rows <= place)


def both_sides(value, half, start, stop, axis=0):
    if axis == 0:
        return jnp.concatenate([value[start:stop], value[half + start : half + stop]], axis=0)
    return jnp.concatenate([value[:, start:stop], value[:, half + start : half + stop]], axis=1)


def hidden_scores(scores, masks, tile, step):
    seen = step * tile
    pieces = []
    for side in range(2):
        base = side * (seen + tile)
        if seen:
            pieces.append(scores[base : base + seen])
        pieces.append(jnp.where(masks[side], scores[base + seen : base + seen + tile], -1e30))
    return jnp.concatenate(pieces, axis=0)


def one_head(rows, head):
    lane = lax.broadcasted_iota(jnp.int32, rows.shape, 1)
    return jnp.where(lane // 64 == head, rows, jnp.zeros_like(rows))


def pick_piece(weight, owns, others, cols):
    for j, (own, other) in enumerate(zip(owns, others)):

        @pl.when(pl.program_id(0) == j)
        def _():
            size = own.shape[0]
            weight[:size] = own[:, cols]
            weight[size:] = other[:, cols]


def attend_kernel(pieces, core_ref, cos_ref, sin_ref, own_rows, other_rows, *refs):
    owns, others = refs[:pieces], refs[pieces : 2 * pieces]
    q_ref, k_ref, v_ref, lse_ref, mix_ref, weight = refs[2 * pieces :]
    half = own_rows.shape[0]
    tile = TILE
    pick_piece(weight, owns, others, QKV)
    proj = dot_nn(stacked_up([own_rows[...], other_rows[...]]), weight[...])
    cos_rows, sin_rows = cos_ref[...], sin_ref[...]
    q = (rotated(proj[:, :128], cos_rows, sin_rows) * HEAD_DIM ** (-0.5)).astype(jnp.bfloat16)
    k = rotated(proj[:, 128:256], cos_rows, sin_rows).astype(jnp.bfloat16)
    v32 = proj[:, 256:]
    q_ref[0] = q
    k_ref[0] = k
    v_ref[0] = v32.astype(jnp.bfloat16)
    v_flip = v32.T.astype(jnp.bfloat16)
    masks = edge_masks(core_ref[0], tile)

    def scored(step, head):
        stop = (step + 1) * tile
        q_head = one_head(both_sides(q, half, step * tile, stop), head)
        return hidden_scores(dot_nt(both_sides(k, half, 0, stop), q_head), masks, tile, step)

    units = [(step, head) for step in range(half // tile) for head in range(2)]
    ahead = scored(*units[0])
    outs = []
    for spot, (step, head) in enumerate(units):
        scores = ahead
        if spot + 1 < len(units):
            ahead = scored(*units[spot + 1])
        stop = (step + 1) * tile
        top = jnp.max(scores, axis=0, keepdims=True)
        expos = jnp.exp(scores - top)
        total = jnp.sum(expos, axis=0, keepdims=True)
        lse = top + jnp.log(total)
        lse_ref[0, head : head + 1, step * tile : stop] = lse[:, :tile]
        lse_ref[0, head : head + 1, half + step * tile : half + stop] = lse[:, tile:]
        v_cols = both_sides(v_flip, half, 0, stop, axis=1)
        out = dot_nn(v_cols[64 * head : 64 * head + 64], expos.astype(jnp.bfloat16))
        outs.append(out * (1.0 / total))
        if head == 1:
            mixed = jnp.concatenate(outs, axis=0).T.astype(jnp.bfloat16)
            outs = []
            mix_ref[step * tile : stop, :] = mixed[:tile]
            mix_ref[half + step * tile : half + stop, :] = mixed[tile:]


def attend_back_kernel(pieces, core_ref, cos_ref, sin_ref, own_rows, other_rows, *refs):
    owns, others = refs[:pieces], refs[pieces : 2 * pieces]
    q_ref, k_ref, v_ref, lse_ref, out_ref, weight, dq, dk, dv = refs[2 * pieces :]
    half = own_rows.shape[0]
    tile = TILE
    pick_piece(weight, owns, others, OUT)
    rows = stacked_up([own_rows[...], other_rows[...]])
    d_mixed = dot_nn(rows, weight[...]).astype(jnp.bfloat16)
    q, k, v = q_ref[0], k_ref[0], v_ref[0]
    k_flip = k.astype(jnp.float32).T.astype(jnp.bfloat16)
    masks = edge_masks(core_ref[0], tile)
    steps = half // tile

    def scored(step, head):
        stop = (step + 1) * tile
        q_head = one_head(both_sides(q, half, step * tile, stop), head)
        g_head = one_head(both_sides(d_mixed, half, step * tile, stop), head)
        scores = hidden_scores(dot_nt(both_sides(k, half, 0, stop), q_head), masks, tile, step)
        return q_head, g_head, scores, dot_nt(both_sides(v, half, 0, stop), g_head)

    units = [(step, head) for step in reversed(range(steps)) for head in range(2)]
    ahead = scored(*units[0])
    dq_flips = []
    dk_sum = dv_sum = None
    for spot, (step, head) in enumerate(units):
        q_head, g_head, scores, d_probs = ahead
        if spot + 1 < len(units):
            ahead = scored(*units[spot + 1])
        stop = (step + 1) * tile
        lse = both_sides(lse_ref[0], half, step * tile, stop, axis=1)
        probs = jnp.exp(scores - lse[head : head + 1])
        dots = jnp.sum(probs * d_probs, axis=0, keepdims=True)
        d_scores = (probs * (d_probs - dots)).astype(jnp.bfloat16)
        dv_part = dot_nn(probs.astype(jnp.bfloat16), g_head)
        dk_part = dot_nn(d_scores, q_head)
        k_cols = both_sides(k_flip, half, 0, stop, axis=1)
        dq_flips.append(dot_nn(k_cols[64 * head : 64 * head + 64], d_scores))
        if head == 0:
            dv_sum, dk_sum = dv_part, dk_part
            continue
        dv_sum, dk_sum = dv_sum + dv_part, dk_sum + dk_part
        dq_rows = jnp.concatenate(dq_flips, axis=0).T * HEAD_DIM ** (-0.5)
        dq_flips = []
        dq[step * tile : stop] = dq_rows[:tile]
        dq[half + step * tile : half + stop] = dq_rows[tile:]
        for base, part in ((0, slice(0, stop)), (half, slice(stop, 2 * stop))):
            if step == steps - 1:
                dk[base : base + stop] = dk_sum[part]
                dv[base : base + stop] = dv_sum[part]
            else:
                dk[base : base + stop] += dk_sum[part]
                dv[base : base + stop] += dv_sum[part]
    cos_rows, sin_rows = cos_ref[...], -sin_ref[...]
    out_ref[:, :128] = rotated(dq[...], cos_rows, sin_rows).astype(jnp.bfloat16)
    out_ref[:, 128:256] = rotated(dk[...], cos_rows, sin_rows).astype(jnp.bfloat16)
    out_ref[:, 256:] = dv[...].astype(jnp.bfloat16)


def split_rows(total, own_ref, other_ref):
    half = own_ref.shape[0]
    own_ref[...] = total[:half]
    other_ref[...] = total[half:].astype(jnp.bfloat16)


def to_model_kernel(lefts, pieces, cols, *refs):
    left, refs = jnp.concatenate([ref[...] for ref in refs[:lefts]], axis=1), refs[lefts:]
    weight = model_weight(refs[:pieces], refs[pieces : 2 * pieces], cols)
    split_rows(dot_nt(left, weight), *refs[2 * pieces :])


def mlp_down_kernel(pieces, left_ref, *refs):
    sides = [stacked_up([ref[...] for ref in side]) for side in (refs[:pieces], refs[pieces:-2])]
    split_rows(dot_nn(left_ref[...], jnp.concatenate(sides, axis=1)), *refs[-2:])


def gelu_both(up_act):
    root = math.sqrt(2.0 / math.pi)
    square = up_act * up_act
    rise = 0.5 + 0.5 * jnp.tanh(up_act * (root + root * 0.044715 * square))
    value = up_act * rise
    slope = rise + value * (1.0 - rise) * (2.0 * root + 6.0 * root * 0.044715 * square)
    return value, slope


def mlp_up_kernel(pieces, own_rows, other_rows, *refs):
    owns, others = refs[:pieces], refs[pieces : 2 * pieces]
    gelu_ref, slope_ref = refs[2 * pieces :]
    half = own_rows.shape[0]
    size = owns[0].shape[1]
    step = half // 2
    units = [(j, i) for j in range(pieces) for i in range(4)]

    def product(j, i):
        rows = (own_rows, other_rows)[i // 2][i % 2 * step : (i % 2 + 1) * step]
        return dot_nn(rows, stacked_up([owns[j][...], others[j][...]]))

    ahead = product(*units[0])
    for spot, (j, i) in enumerate(units):
        up_act = ahead
        if spot + 1 < len(units):
            ahead = product(*units[spot + 1])
        value, slope = gelu_both(up_act)
        gelu_ref[i * step : (i + 1) * step, j * size : (j + 1) * size] = value.astype(jnp.bfloat16)
        slope_ref[i * step : (i + 1) * step, j * size : (j + 1) * size] = slope.astype(
            jnp.bfloat16
        )


def mlp_up_back_near_kernel(pieces, own_rows, other_rows, slope_ref, *refs):
    owns, others = refs[:pieces], refs[pieces : 2 * pieces]
    out_ref = refs[-1]
    size = owns[0].shape[0]
    rows = stacked_up([own_rows[...], other_rows[...]])
    for j in range(pieces):
        cols = slice(j * size, (j + 1) * size)
        weight = jnp.concatenate([owns[j][...], others[j][...]], axis=1)
        d_gelu = dot_nt(rows, weight)
        out_ref[:, cols] = (d_gelu * slope_ref[:, cols].astype(jnp.float32)).astype(jnp.bfloat16)


def mlp_up_back_kernel(pieces, own_rows, other_rows, slope_ref, *refs):
    owns, others = refs[:pieces], refs[pieces : 2 * pieces]
    out_ref, weight, slope, sems = refs[2 * pieces :]
    half = own_rows.shape[1] // 2
    size = owns[0].shape[0]
    order = list(reversed(range(pieces)))
    copies = []
    for j in order:
        sources = (owns[j], others[j], slope_ref.at[:, pl.ds(j * size, size)])
        targets = (
            weight.at[j, :, pl.ds(0, half)],
            weight.at[j, :, pl.ds(half, half)],
            slope.at[:, pl.ds(j * size, size)],
        )
        copies.append(
            [
                pltpu.make_async_copy(source, target, sems.at[j, i])
                for i, (source, target) in enumerate(zip(sources, targets))
            ]
        )
        for copy in copies[-1]:
            copy.start()
    rows = stacked_up([own_rows[...], other_rows[...]])
    for j, arriving in zip(order, copies):
        cols = slice(j * size, (j + 1) * size)
        for copy in arriving:
            copy.wait()
        d_gelu = dot_nt(rows, weight[j])
        out_ref[:, cols] = (d_gelu * slope[:, cols].astype(jnp.float32)).astype(jnp.bfloat16)


def inverse_size(rows):
    return lax.rsqrt(jnp.mean(rows * rows, axis=-1, keepdims=True) + NORM_EPSILON)


def norm_back(rows, gain, grad):
    scale = inverse_size(rows)
    weighted = grad * gain
    inner = jnp.mean(rows * weighted, axis=-1, keepdims=True)
    return scale * weighted - rows * (scale * scale * scale * inner), rows * scale * grad


def folded(rows):
    return jnp.sum(rows.reshape(rows.shape[0] // 8, 8, rows.shape[1]), axis=0)


def wide(ref, spot):
    return ref[spot, :].astype(jnp.float32)


def by_chunks(count, body, sums=0, width=0):
    def one(i, carry):
        more = body(pl.ds(pl.multiple_of(i * CHUNK, CHUNK), CHUNK))
        return tuple(old + folded(new) for old, new in zip(carry, more))

    start = tuple(jnp.zeros((8, width), jnp.float32) for _ in range(sums))
    totals = lax.fori_loop(0, count // CHUNK, one, start)
    return [jnp.sum(total, axis=0, keepdims=True) for total in totals]


def norm_in_kernel(gain_ref, rows_ref, out_ref):
    def body(spot):
        rows = wide(rows_ref, spot)
        out_ref[spot, :] = (rows * inverse_size(rows) * gain_ref[0:1]).astype(jnp.bfloat16)
        return ()

    by_chunks(rows_ref.shape[0], body)


def after_attention_kernel(
    gain_ref, rows_ref, own_ref, other_ref, branch_ref, hidden_ref, out_ref
):
    def body(spot):
        branch = own_ref[spot, :] + wide(other_ref, spot)
        hidden = wide(rows_ref, spot) + branch * inverse_size(branch) * gain_ref[1:2]
        branch_ref[spot, :] = branch
        hidden_ref[spot, :] = hidden
        out_ref[spot, :] = (hidden * inverse_size(hidden) * gain_ref[2:3]).astype(jnp.bfloat16)
        return ()

    by_chunks(rows_ref.shape[0], body)


def after_mlp_kernel(gain_ref, hidden_ref, own_ref, other_ref, branch_ref, out_ref):
    def body(spot):
        branch = own_ref[spot, :] + wide(other_ref, spot)
        branch_ref[spot, :] = branch
        result = hidden_ref[spot, :] + branch * inverse_size(branch) * gain_ref[3:4]
        out_ref[spot, :] = result.astype(jnp.bfloat16)
        return ()

    by_chunks(hidden_ref.shape[0], body)


def into_mlp_back_kernel(gain_ref, grad_ref, branch_ref, out_ref, sum_ref):
    def body(spot):
        d_rows, d_gain = norm_back(branch_ref[spot, :], gain_ref[3:4], wide(grad_ref, spot))
        out_ref[spot, :] = d_rows.astype(jnp.bfloat16)
        return (d_gain,)

    (sum_ref[...],) = by_chunks(grad_ref.shape[0], body, 1, grad_ref.shape[1])


def into_attention_back_kernel(
    gain_ref, grad_ref, own_ref, other_ref, hidden_ref, branch_ref, d_hidden_ref, out_ref, *sums
):
    def body(spot):
        d_rows = own_ref[spot, :] + wide(other_ref, spot)
        d_rows, d_gain = norm_back(hidden_ref[spot, :], gain_ref[2:3], d_rows)
        d_hidden = wide(grad_ref, spot) + d_rows
        d_hidden_ref[spot, :] = d_hidden
        d_rows, d_first = norm_back(branch_ref[spot, :], gain_ref[1:2], d_hidden)
        out_ref[spot, :] = d_rows.astype(jnp.bfloat16)
        return (d_first, d_gain)

    totals = by_chunks(grad_ref.shape[0], body, 2, grad_ref.shape[1])
    sums[0][...], sums[1][...] = totals


def out_of_layer_kernel(gain_ref, rows_ref, own_ref, other_ref, d_hidden_ref, out_ref, sum_ref):
    def body(spot):
        d_rows = own_ref[spot, :] + wide(other_ref, spot)
        d_rows, d_gain = norm_back(wide(rows_ref, spot), gain_ref[0:1], d_rows)
        out_ref[spot, :] = (d_hidden_ref[spot, :] + d_rows).astype(jnp.bfloat16)
        return (d_gain,)

    (sum_ref[...],) = by_chunks(rows_ref.shape[0], body, 1, rows_ref.shape[1])


def work(flops, arrays):
    size = sum(math.prod(array.shape) * jnp.dtype(array.dtype).itemsize for array in arrays)
    return pl.CostEstimate(flops=flops, bytes_accessed=size, transcendentals=0)


def far(array):
    return pltpu.with_memory_space_constraint(array, pltpu.HBM)


def without(kernel, first, count):
    return lambda *refs: kernel(*refs[:first], *refs[first + count :])


def on_chip(kernel, name, outs, *operands, limit=ROWS_VMEM, flops=0, waits=()):
    shapes = [jax.ShapeDtypeStruct(shape, dtype) for shape, dtype in outs]
    space = pl.BlockSpec(memory_space=pltpu.VMEM)
    return pl.pallas_call(
        without(kernel, len(operands), len(waits)),
        in_specs=[space] * len(operands) + [pl.BlockSpec(memory_space=pl.ANY)] * len(waits),
        out_specs=[space] * len(outs),
        out_shape=shapes,
        compiler_params=pltpu.CompilerParams(vmem_limit_bytes=limit),
        cost_estimate=work(flops, (*operands, *shapes)),
        name=name,
    )(*operands, *map(far, waits))


def whole_block(array):
    return pl.BlockSpec(array.shape, lambda j: (0,) * array.ndim)


def by_pairs(kernel, name, core, operands, pieces, blocks, outs, scratch, flops, waits):
    shapes = [jax.ShapeDtypeStruct(shape, dtype) for shape, dtype, _ in outs]
    taken = 1 + len(operands) + 2 * len(pieces[0]) + len(blocks)
    return pl.pallas_call(
        without(functools.partial(kernel, len(pieces[0])), taken, len(waits)),
        grid=(len(pieces[0]),),
        in_specs=[pl.BlockSpec(memory_space=pltpu.SMEM)]
        + [whole_block(array) for array in (*operands, *pieces[0], *pieces[1])]
        + [spec for _, spec in blocks]
        + [pl.BlockSpec(memory_space=pl.ANY)] * len(waits),
        out_specs=[spec for _, _, spec in outs],
        out_shape=shapes,
        scratch_shapes=scratch,
        compiler_params=pltpu.CompilerParams(vmem_limit_bytes=KERNEL_VMEM),
        cost_estimate=work(flops, (*operands, *pieces[0], *pieces[1], *shapes)),
        name=name,
    )(core, *operands, *pieces[0], *pieces[1], *[array for array, _ in blocks], *map(far, waits))


def mlp_up_back(rows, slope, pieces, waits):
    length, units = slope.shape
    unit, half = pieces[0][0].shape
    count = len(pieces[0])
    every, space = pl.BlockSpec(memory_space=pl.ANY), pl.BlockSpec(memory_space=pltpu.VMEM)
    return pl.pallas_call(
        without(functools.partial(mlp_up_back_kernel, count), 3 + 2 * count, len(waits)),
        in_specs=[space] * 2 + [every] * (1 + 2 * count + len(waits)),
        out_specs=space,
        out_shape=jax.ShapeDtypeStruct((length, units), jnp.bfloat16),
        scratch_shapes=[
            pltpu.VMEM((count, unit, 2 * half), jnp.bfloat16),
            pltpu.VMEM((length, units), jnp.bfloat16),
            pltpu.SemaphoreType.DMA((count, 3)),
        ],
        compiler_params=pltpu.CompilerParams(vmem_limit_bytes=KERNEL_VMEM),
        name="mlp_up_back",
    )(*rows, *map(far, (slope, *pieces[0], *pieces[1], *waits)))


def attend(core, tables, rows, pieces, waits):
    half, features = rows[0].shape
    length, count = 2 * half, len(pieces[0])
    lanes = ((count, length, 128), jnp.bfloat16, pl.BlockSpec((1, length, 128), lambda j: (j, 0, 0)))
    lse = ((count, 2, length), jnp.float32, pl.BlockSpec((1, 2, length), lambda j: (j, 0, 0)))
    mixed = ((length, count * 128), jnp.bfloat16, pl.BlockSpec((length, 128), lambda j: (0, j)))
    return by_pairs(
        attend_kernel,
        "attend",
        core,
        (*tables, *rows),
        pieces,
        (),
        (lanes, lanes, lanes, lse, mixed),
        [pltpu.VMEM((features, 384), jnp.bfloat16)],
        count * length * (2 * features * 384 + 2 * PAIR_WORK * length),
        waits,
    )


def attend_back(core, tables, rows, pieces, base, waits, q, k, v, lse):
    half, features = rows[0].shape
    length, count = 2 * half, len(pieces[0])
    lanes = pl.BlockSpec((1, length, 128), lambda j: (base + j, 0, 0))
    lse_spec = pl.BlockSpec((1, 2, length), lambda j: (base + j, 0, 0))
    out = ((length, count * 384), jnp.bfloat16, pl.BlockSpec((length, 384), lambda j: (0, j)))
    return by_pairs(
        attend_back_kernel,
        "attend_back",
        core,
        (*tables, *rows),
        pieces,
        ((q, lanes), (k, lanes), (v, lanes), (lse, lse_spec)),
        (out,),
        [pltpu.VMEM((features, 128), jnp.bfloat16)] + [pltpu.VMEM((length, 128), jnp.float32)] * 3,
        count * length * (2 * features * 128 + 5 * PAIR_WORK * length),
        waits,
    )[0]


def exchanged(parts):
    return parts[0], flip_pairs(parts[1], 1)


def model_rows(kernel, name, lefts, pieces, waits=()):
    length, width = lefts[0].shape[0], 2 * MODEL_HALF
    outs = (((length // 2, width), jnp.float32), ((length // 2, width), jnp.bfloat16))
    hidden = sum(left.shape[1] for left in lefts)
    more = {"limit": KERNEL_VMEM, "flops": 2 * length * width * hidden, "waits": waits}
    return exchanged(on_chip(kernel, name, outs, *lefts, *pieces[0], *pieces[1], **more))


def flip_pairs(block, distance):
    size = lax.axis_size("dp")
    return lax.ppermute(block, "dp", [(i, i ^ distance) for i in range(size)])


def passed_on(block, step):
    size = lax.axis_size("tensor")
    return lax.ppermute(block, "tensor", [(i, (i + step) % size) for i in range(size)])


def dot_tn(left, right):
    return lax.dot_general(
        left, right, (((0,), (0,)), ((), ())), preferred_element_type=jnp.float32
    )


def fetch(first_ref, zeros, ones, buffers, sems):
    for section, sources in enumerate((zeros, ones)):

        @pl.when(first_ref[0] == section)
        def _():
            for i, (source, buffer) in enumerate(zip(sources, buffers)):
                pltpu.make_async_copy(source, buffer, sems.at[i]).start()

    def arrived(*places):
        for i in places:
            pltpu.make_async_copy(zeros[i], buffers[i], sems.at[i]).wait()

    return arrived


def mlp_grads_kernel(base, section_ref, *refs):
    (own_one, other_one, own_two, other_two), (rows, d_up, gelu, d_down, sems) = refs[12:16], refs[16:]
    half, size = own_one.shape[0] // 2, own_one.shape[1]
    cols = pl.ds(base * size, 2 * size)

    def parts(own_rows, other_rows, d_up_ref, gelu_ref, own_grad, other_grad):
        whole = (d_up_ref.at[:, cols], gelu_ref.at[:, cols])
        return (own_rows, other_rows, *whole, own_grad, other_grad)

    count = refs[0].shape[0]
    buffers = (
        rows.at[pl.ds(0, count)],
        rows.at[pl.ds(count, count)],
        d_up,
        gelu,
        d_down.at[pl.ds(0, count)],
        d_down.at[pl.ds(count, count)],
    )
    arrived = fetch(section_ref, parts(*refs[:6]), parts(*refs[6:12]), buffers, sems)
    for j, own, other in ((1, own_two, other_two), (0, own_one, other_one)):
        cols = slice(j * size, (j + 1) * size)
        if j == 1:
            arrived(0, 1, 2)
        up = dot_tn(rows[...], d_up[:, cols])
        own[:half] = up[:half]
        other[:half] = up[half:].astype(jnp.bfloat16)
        if j == 1:
            arrived(3, 4, 5)
        down = dot_tn(gelu[:, cols], d_down[...])
        own[half:] = down[:, :half]
        other[half:] = down[:, half:].astype(jnp.bfloat16)


def attn_grads_kernel(base, section_ref, *refs):
    (own_one, other_one, own_two, other_two), (rows, d_qkv, mixed, d_attn, sems) = refs[12:16], refs[16:]
    half, size = own_one.shape[0], d_qkv.shape[1] // 2
    count = refs[0].shape[0]
    cols = pl.ds(base * 128, 256)

    def parts(own_rows, other_rows, d_qkv_ref, mixed_ref, own_grad, other_grad):
        return (own_rows, other_rows, d_qkv_ref, mixed_ref.at[:, cols], own_grad, other_grad)

    buffers = (
        rows.at[pl.ds(0, count)],
        rows.at[pl.ds(count, count)],
        d_qkv,
        mixed,
        d_attn.at[pl.ds(0, count)],
        d_attn.at[pl.ds(count, count)],
    )
    arrived = fetch(section_ref, parts(*refs[:6]), parts(*refs[6:12]), buffers, sems)
    for j, own, other in ((1, own_two, other_two), (0, own_one, other_one)):
        if j == 1:
            arrived(0, 1, 2)
        qkv = dot_tn(rows[...], d_qkv[:, j * size : (j + 1) * size])
        if j == 1:
            arrived(3, 4, 5)
        out = dot_tn(d_attn[...], mixed[:, j * 128 : (j + 1) * 128])
        own[:, :size] = qkv[:half]
        own[:, size:] = out[:half]
        other[:, :size] = qkv[half:].astype(jnp.bfloat16)
        other[:, size:] = out[half:].astype(jnp.bfloat16)


def weight_grads(kernel, name, base, section, zeros, ones, shape, columns, waits=()):
    length = 2 * zeros[0].shape[0]
    width = zeros[0].shape[1]
    every = pl.BlockSpec(memory_space=pl.ANY)
    space = pl.BlockSpec(memory_space=pltpu.VMEM)
    arrays = (*zeros, *ones)
    first, second, third, fourth = pl.pallas_call(
        without(functools.partial(kernel, base), 1 + len(arrays), len(waits)),
        in_specs=[pl.BlockSpec(memory_space=pltpu.SMEM)] + [every] * (len(arrays) + len(waits)),
        out_specs=[space] * 4,
        out_shape=[
            jax.ShapeDtypeStruct(shape, jnp.float32),
            jax.ShapeDtypeStruct(shape, jnp.bfloat16),
        ]
        * 2,
        scratch_shapes=[
            pltpu.VMEM((length, width), jnp.bfloat16),
            pltpu.VMEM((length, columns[0]), jnp.bfloat16),
            pltpu.VMEM((length, columns[1]), jnp.bfloat16),
            pltpu.VMEM((length, width), jnp.bfloat16),
            pltpu.SemaphoreType.DMA((6,)),
        ],
        compiler_params=pltpu.CompilerParams(vmem_limit_bytes=KERNEL_VMEM),
        name=name,
    )(section, *map(far, (*arrays, *waits)))
    return [(first, flip_pairs(second, 2)), (third, flip_pairs(fourth, 2))]


def moved_kernel(own_ref, other_ref, *refs):
    out_ref = refs[-1]

    def body(i, carry):
        spot = pl.ds(pl.multiple_of(i * CHUNK, CHUNK), CHUNK)
        total = own_ref[spot, :]
        for ref in (other_ref, *refs[:-1]):
            total = total + wide(ref, spot)
        out_ref[spot, :] = total.astype(jnp.bfloat16)
        return carry

    lax.fori_loop(0, own_ref.shape[0] // CHUNK, body, 0)


def gates_kernel(up_ref, down_ref, up_out, down_out):
    up_out[...] = up_ref[...]
    down_out[...] = down_ref[...]


def gate_kernel(piece_ref, out_ref):
    out_ref[...] = piece_ref[...]


def mlp_sum_kernel(core_ref, own_ref, other_ref, moved_ref, up_keep, down_keep, up_send, down_send):
    half = own_ref.shape[0] // 2
    size = up_keep.shape[0]

    def total(rows, cols):
        more = other_ref[rows, cols].astype(jnp.float32) + moved_ref[rows, cols].astype(jnp.float32)
        return own_ref[rows, cols] + more

    for core in range(2):

        @pl.when(core_ref[0] == core)
        def _():
            for place, up, down in ((core, up_keep, down_keep), (1 - core, up_send, down_send)):
                spot = slice(place * size, (place + 1) * size)
                up[...] = total(spot, slice(None))
                down[...] = total(slice(half, None), spot)


def mlp_join_kernel(core_ref, up_keep, down_keep, up_sent, down_sent, up_out, down_out):
    size = up_keep.shape[1]
    for core in range(2):

        @pl.when(core_ref[0] == core)
        def _():
            places = ((core, up_keep, down_keep), (1 - core, up_sent, down_sent))
            for place, up, down in places:
                spot = slice(place * size, (place + 1) * size)
                up_out[:, spot] = up[...]
                down_out[spot] = down[...]


def chosen_kernel(place_ref, zero_ref, one_ref, out_ref):
    half = out_ref.shape[1] // 2
    for section, rows_ref in enumerate((zero_ref, one_ref)):
        for upper in range(2):

            @pl.when(jnp.logical_and(place_ref[0] == section, place_ref[1] == upper))
            def _():
                for side in range(2):
                    place = (side + upper) % 2 * half
                    out_ref[:, place : place + half] = rows_ref[:, side * half : (side + 1) * half]


def pick_kernel(core_ref, rows_ref, keep_ref, send_ref):
    count = keep_ref.shape[0]
    keep_ref[...] = rows_ref[pl.ds(core_ref[0] * count, count)]
    send_ref[...] = rows_ref[pl.ds((1 - core_ref[0]) * count, count)]


def in_order_kernel(core_ref, keep_ref, sent_ref, out_ref):
    out_ref[:, pl.ds(core_ref[0], 1)] = keep_ref[...][:, None]
    out_ref[:, pl.ds(1 - core_ref[0], 1)] = sent_ref[...][:, None]


def with_core(kernel, name, core, outs, *operands, waits=()):
    space = pl.BlockSpec(memory_space=pltpu.VMEM)
    return pl.pallas_call(
        without(kernel, 1 + len(operands), len(waits)),
        in_specs=[pl.BlockSpec(memory_space=pltpu.SMEM)]
        + [space] * len(operands)
        + [pl.BlockSpec(memory_space=pl.ANY)] * len(waits),
        out_specs=[space] * len(outs),
        out_shape=[jax.ShapeDtypeStruct(shape, dtype) for shape, dtype in outs],
        compiler_params=pltpu.CompilerParams(vmem_limit_bytes=ROWS_VMEM),
        name=name,
    )(core, *operands, *map(far, waits))


def last_sum_kernel(core_ref, own_ref, other_ref, moved_ref, keep_ref, send_ref):
    rows = keep_ref.shape[0]

    def total(block):
        spot = pl.ds(pl.multiple_of(block * rows, rows), rows)
        return own_ref[spot, :] + wide(other_ref, spot) + wide(moved_ref, spot)

    keep_ref[...] = total(core_ref[0])
    send_ref[...] = total(1 - core_ref[0])


def joined_kernel(spots, core_ref, keep_ref, sent_ref, column_ref, row_ref):
    size = row_ref.shape[0] // 2
    for core in range(2):

        @pl.when(core_ref[0] == core)
        def _():
            for place, source in ((core, keep_ref), (1 - core, sent_ref)):
                for start, stop, to in spots:
                    step = stop - start
                    column_ref[:, to + place * step : to + (place + 1) * step] = source[:, start:stop]
                row_ref[place * size : (place + 1) * size] = source[:, spots[-1][1] :].T


def per_chip(
    inputs,
    out_cotangent,
    group_ids,
    group_weights,
    gains,
    qkv_weight,
    out_weight,
    up_weight,
    down_weight,
):
    micro, row_count, width = inputs.shape
    tensor = lax.axis_size("tensor")
    part = row_count // 2
    wide_half = width // 2
    length = tensor * row_count
    half = length // 2
    first = lax.axis_index("section") == 0
    place = lax.axis_index("dp")
    core = place % 2
    upper = place // 2 % 2
    core_zero = core == 0
    low_half = upper == 0

    def ordered(mine, other):
        return jnp.where(core_zero, mine, other), jnp.where(core_zero, other, mine)

    def own_first(values):
        return jnp.where(low_half, values, jnp.roll(values, wide_half, axis=-1))

    def both_rows(own):
        return own, flip_pairs(own, 1)

    def to_chip(block):
        split = block.reshape((micro, 2, part) + block.shape[2:])
        mine = lax.dynamic_index_in_dim(split, core, 1, keepdims=False)
        other = lax.dynamic_index_in_dim(split, 1 - core, 1, keepdims=False)
        return lax.all_to_all(
            jnp.concatenate(ordered(mine, flip_pairs(other, 1))), "tensor", 0, 0, tiled=True
        )

    def from_chip(spread_out, waits=()):
        piece = ((micro, part, width), jnp.bfloat16)
        keep, send = with_core(
            pick_kernel, "pick", core_word, (piece, piece), spread_out, waits=waits
        )
        outs = (((micro, 2, part, width), jnp.bfloat16),)
        (rows,) = with_core(
            in_order_kernel, "in_order", core_word, outs, keep, flip_pairs(send, 1)
        )
        return rows.reshape(micro, row_count, width)

    def columns(local):
        size = local.shape[-1] // 2
        mid = (0,) * (local.ndim - 2)
        piece = lax.dynamic_slice(
            local,
            (wide_half * upper, *mid, size * core),
            (wide_half, *local.shape[1:-1], size),
        )
        return piece.reshape(wide_half, -1)

    def rows(local):
        size = local.shape[0] // 2
        return lax.dynamic_slice(local, (size * core, wide_half * upper), (size, wide_half))

    core_word = core.astype(jnp.int32).reshape(1)
    attn_piece = jnp.concatenate([columns(qkv_weight[0]), rows(out_weight[0]).T], axis=1)

    def spread(piece):
        pieces = [piece]
        for _ in range(tensor - 1):
            pieces.append(passed_on(pieces[-1], 1))
        return pieces

    up_piece, down_piece = columns(up_weight[0]), rows(down_weight[0])
    up_other, down_other = [flip_pairs(up_piece, 2)], [flip_pairs(down_piece, 2)]
    attn_own = [attn_piece, passed_on(attn_piece, 1)]
    attn_first = flip_pairs(attn_piece, 2)
    outs = ((attn_piece.shape, attn_piece.dtype),)
    attn_own[1] = on_chip(gate_kernel, "gate", outs, attn_own[1], waits=(attn_first, up_other[0]))[0]
    attn_own += spread(attn_own[1])[1:-1]
    attn_other = [attn_first] + [flip_pairs(piece, 2) for piece in attn_own[1:]]
    outs = tuple((piece.shape, piece.dtype) for piece in (up_piece, down_piece))
    up_piece, down_piece = on_chip(
        gates_kernel, "gate", outs, up_piece, down_piece, waits=(attn_own[2], attn_other[0], down_other[0])
    )
    up_own, down_own = spread(up_piece), spread(down_piece)
    up_other += [flip_pairs(piece, 2) for piece in up_own[1:]]
    down_other += [flip_pairs(piece, 2) for piece in down_own[1:]]
    w_attn, w_up, w_down = (attn_own, attn_other), (up_own, up_other), (down_own, down_other)
    unit = up_piece.shape[1]
    units = tensor * unit

    group_count = group_weights.shape[0]
    matches = group_ids[..., None] == jnp.arange(group_count, dtype=jnp.int32)
    row_scale = jnp.sum(jnp.where(matches, group_weights, 0.0), axis=-1)
    weighted = (out_cotangent.astype(jnp.float32) * row_scale[..., None]).astype(jnp.bfloat16)
    start = to_chip(own_first(jnp.where(first, inputs, weighted))).reshape(half, width)
    gain = own_first(gains[0])

    turns = jnp.arange(half, dtype=jnp.int32)
    turns = turns // part * row_count + turns % part
    positions = jnp.concatenate([turns + core * part, turns + (1 - core) * part])
    freqs = 10000.0 ** (-2.0 * jnp.arange(HEAD_DIM // 2, dtype=jnp.float32) / HEAD_DIM)
    angles = positions.astype(jnp.float32)[:, None] * freqs[None, :]
    cos_part, sin_part = jnp.cos(angles), jnp.sin(angles)
    tables = (
        jnp.concatenate([cos_part] * 4, axis=1),
        jnp.concatenate([-sin_part, sin_part] * 2, axis=1),
    )
    row32, row16 = ((half, width), jnp.float32), ((half, width), jnp.bfloat16)
    unit16 = ((length, units), jnp.bfloat16)
    sum32 = ((1, width), jnp.float32)
    mlp_cost = {"limit": KERNEL_VMEM, "flops": 2 * length * width * units}
    every = slice(None)

    def model_kernel(cols, lefts=1):
        return functools.partial(to_model_kernel, lefts, tensor, cols)

    down_kernel = functools.partial(mlp_down_kernel, tensor)

    def forward(layer_input, waits):
        attn_in = both_rows(
            on_chip(norm_in_kernel, "norm_in", (row16,), gain, layer_input, waits=waits[0])[0]
        )
        *heads, mixed = attend(core_word, tables, attn_in, w_attn, waits[1])
        parts = model_rows(model_kernel(OUT), "attn_out", [mixed], w_attn, waits[2])
        operands = (gain, layer_input, *parts)
        branch, hidden, mlp_in = on_chip(
            after_attention_kernel, "after_attn", (row32, row32, row16), *operands, waits=waits[3]
        )
        mlp_in = both_rows(mlp_in)
        kernel = functools.partial(mlp_up_kernel, tensor)
        operands = (*mlp_in, *w_up[0], *w_up[1])
        gelu_out, slope = on_chip(kernel, "mlp_up", (unit16, unit16), *operands, **mlp_cost)
        parts = model_rows(down_kernel, "mlp_down", [gelu_out], w_down)
        mlp_branch, result = on_chip(
            after_mlp_kernel, "after_mlp", (row32, row16), gain, hidden, *parts
        )
        saved = (layer_input, heads, branch, hidden, slope, mlp_branch)
        return result, saved, (attn_in, mixed, mlp_in, gelu_out)

    def backward(grad, saved, hook, late=()):
        layer_input, heads, branch, hidden, slope, mlp_branch = saved
        operands = (gain, grad, mlp_branch)
        d_down, sum_three = on_chip(
            into_mlp_back_kernel, "into_mlp_back", (row16, sum32), *operands
        )
        d_down = both_rows(d_down)
        if late:
            d_up = mlp_up_back(d_down, slope, w_down, late)
        else:
            kernel = functools.partial(mlp_up_back_near_kernel, tensor)
            operands = (*d_down, slope, *w_down[0], *w_down[1])
            (d_up,) = on_chip(kernel, "mlp_up_back", (unit16,), *operands, **mlp_cost)
        waits = hook(d_down, d_up)
        parts = model_rows(model_kernel(every), "mlp_back", [d_up], w_up, waits)
        waits = hook()
        operands = (gain, grad, *parts, hidden, branch)
        outs = (row32, row16, sum32, sum32)
        d_hidden, d_attn, sum_one, sum_two = on_chip(
            into_attention_back_kernel, "into_attn_back", outs, *operands, waits=waits
        )
        d_attn = both_rows(d_attn)
        waits = hook(d_attn)
        d_qkv = []
        for base in reversed(range(0, tensor, 2)):
            some = [side[base : base + 2] for side in w_attn]
            now = attend_back(core_word, tables, d_attn, some, base, waits, *heads)
            d_qkv.insert(0, now)
            waits = hook(now)
        parts = model_rows(model_kernel(QKV, 2), "attn_back", d_qkv, w_attn, waits)
        operands = (gain, layer_input, *parts, d_hidden)
        d_input, sum_zero = on_chip(
            out_of_layer_kernel, "out_of_layer", (row16, sum32), *operands, waits=hook()
        )
        sums = jnp.concatenate([sum_zero, sum_one, sum_two, sum_three])
        return d_input, (d_qkv, d_attn, d_up, d_down), sums

    low_zero, saved_zero, lefts_zero = forward(
        start,
        (
            (up_piece, up_other[0], down_other[0]),
            (up_own[2], down_own[2], up_other[1], down_other[1]),
            (up_own[3], down_own[3], up_other[2], down_other[2]),
            (up_other[3],),
        ),
    )
    low_one, saved_one, lefts_one = forward(shifted(low_zero, "section", 1), ((),) * 4)
    grad_one, rights_one, gain_one = backward(start, saved_one, lambda *new: ())
    received = shifted(grad_one, "section", -1)

    lows = lax.optimization_barrier((low_zero, low_one, grad_one))[:2]
    lows = own_first(jnp.where(first, *lows)).reshape(tensor, part, width)
    lows = lax.all_to_all(lows, "tensor", 0, 0, tiled=True)

    section_word = lax.axis_index("section").astype(jnp.int32).reshape(1)

    def mlp_leaves(base, waits=()):
        zeros = (*lefts_zero[2], d_up, lefts_zero[3], *d_down)
        ones = (*lefts_one[2], rights_one[2], lefts_one[3], *rights_one[3])
        mlp_sums[base : base + 2] = weight_grads(
            mlp_grads_kernel,
            "mlp_grads",
            base,
            section_word,
            zeros,
            ones,
            (wide_half + unit, unit),
            (2 * unit, 2 * unit),
            waits,
        )

    def attn_leaves(base, d_qkv, waits):
        zeros = (*lefts_zero[0], d_qkv, lefts_zero[1], *d_attn)
        ones = (*lefts_one[0], rights_one[0][base // 2], lefts_one[1], *rights_one[1])
        attn_sums[base : base + 2] = weight_grads(
            attn_grads_kernel,
            "attn_grads",
            base,
            section_word,
            zeros,
            ones,
            (wide_half, 512),
            (768, 256),
            waits,
        )

    def moves_on(piece, *moved, waits=()):
        outs = ((piece[1].shape, jnp.bfloat16),)
        (total,) = on_chip(moved_kernel, "moved", outs, *piece, *moved, waits=waits)
        return total, passed_on(total, -1)

    mlp_sums, attn_sums = [None] * tensor, [None] * tensor
    mlp_moves, attn_moves = [None] * tensor, [None] * tensor
    hooks = iter(range(6))

    def hook(*new):
        nonlocal d_down, d_up, d_attn, outputs
        turn = next(hooks)
        if turn == 0:
            d_down, d_up = new
            mlp_leaves(2)
            return (mlp_sums[3][0],)
        if turn == 1:
            return ()
        if turn == 2:
            (d_attn,) = new
            outputs = from_chip(lows, d_attn[:1])
            total, mlp_moves[3] = moves_on(mlp_sums[3], waits=(outputs,))
            mlp_leaves(0, (total,))
            return (mlp_sums[1][0],)
        if turn == 3:
            total, mlp_moves[2] = moves_on(mlp_sums[2], mlp_moves[3], waits=new)
            attn_leaves(2, new[0], (total,))
            return (mlp_sums[2][1], mlp_moves[3], attn_sums[3][0])
        if turn == 4:
            total, mlp_moves[1] = moves_on(mlp_sums[1], mlp_moves[2], waits=new)
            attn_leaves(0, new[0], (total,))
            total, attn_moves[3] = moves_on(attn_sums[3], waits=attn_sums[1][:1])
            return (total, mlp_moves[1], mlp_sums[0][1])
        return attn_sums[2][1:]

    d_down = d_up = d_attn = outputs = None
    grad_zero, rights_zero, gain_zero = backward(received, saved_zero, hook, (lows,))
    place_word = jnp.stack([lax.axis_index("section"), upper]).astype(jnp.int32)
    (grads,) = with_core(
        chosen_kernel,
        "chosen",
        place_word,
        (row16,),
        grad_zero,
        grad_one,
        waits=(attn_moves[3], attn_sums[1][1]),
    )
    grads = lax.all_to_all(grads.reshape(tensor, part, width), "tensor", 0, 0, tiled=True)

    block32 = ((wide_half // 2, unit), jnp.float32)
    down32 = ((unit, wide_half // 2), jnp.float32)
    up_keep, down_keep, up_send, down_send = with_core(
        mlp_sum_kernel,
        "mlp_sum",
        core_word,
        (block32, down32, block32, down32),
        *mlp_sums[0],
        mlp_moves[1],
        waits=(grad_zero,),
    )
    outs = (
        ((wide_half // 2, 2 * unit), jnp.float32),
        ((2 * unit, wide_half // 2), jnp.float32),
    )
    sent = flip_pairs(up_send, 1), flip_pairs(down_send, 1)
    up_grad, down_grad = with_core(
        mlp_join_kernel, "mlp_join", core_word, outs, up_keep, down_keep, *sent
    )
    total, attn_moves[2] = moves_on(attn_sums[2], attn_moves[3], waits=(grad_zero,))
    waits = (up_grad, attn_sums[0][1], grads)
    last, attn_moves[1] = moves_on(attn_sums[1], attn_moves[2], waits=waits)
    grads = from_chip(grads, (last,))
    gain_total = own_first(jnp.where(first, gain_zero, gain_one))
    count = tensor * lax.axis_size("dp")
    gain_parts = gain_total.reshape(4, count, width // count).swapaxes(0, 1)
    outs = ((gain_parts.shape, gain_parts.dtype),)
    (gain_parts,) = on_chip(gate_kernel, "gate", outs, gain_parts, waits=(last,))
    gain_parts = lax.all_to_all(gain_parts, ("dp", "tensor"), 0, 0, tiled=True)
    gains_grad = jnp.sum(gain_parts, axis=0)
    outs = (((wide_half // 2, 512), jnp.float32),) * 2
    keep, send = with_core(
        last_sum_kernel,
        "attn_sum",
        core_word,
        outs,
        *attn_sums[0],
        attn_moves[1],
        waits=(grads, outputs, gains_grad),
    )
    spots = tuple((i * 128, (i + 1) * 128, i * 256) for i in range(3))
    outs = (((wide_half // 2, 768), jnp.float32), ((256, wide_half // 2), jnp.float32))
    kernel = functools.partial(joined_kernel, spots)
    qkv_grad, out_grad = with_core(
        kernel, "attn_join", core_word, outs, keep, flip_pairs(send, 1)
    )
    qkv_grad = qkv_grad.reshape(wide_half // 2, 3, -1)

    return (
        outputs[None],
        grads[None],
        gains_grad[None],
        qkv_grad[None],
        out_grad[None],
        up_grad[None],
        down_grad[None],
    )


def takes_chips(sizes):
    return sizes["section"] == 2 and sizes["dp"] == 4 and sizes["tensor"] == 4


def solution(mesh):
    placed = (
        P("dp", "tensor", None),
        P("dp", "tensor", None),
        P("dp", "tensor"),
        P(),
        P("section", None, None),
        P("section", None, None, "tensor"),
        P("section", "tensor", None),
        P("section", None, "tensor"),
        P("section", "tensor", None),
    )
    body = per_chip if takes_chips(dict(mesh.shape)) else per_device
    return jax.shard_map(
        body,
        mesh=mesh,
        in_specs=placed,
        out_specs=(
            P("section", "dp", "tensor", None),
            P("section", "dp", "tensor", None),
            P("section", None, ("dp", "tensor")),
            P("section", "dp", None, "tensor"),
            P("section", "tensor", "dp"),
            P("section", "dp", "tensor"),
            P("section", "tensor", "dp"),
        ),
        check_vma=False,
    )
```

```python
import functools
import math

import jax
import jax.numpy as jnp
from jax import lax
from jax.experimental import pallas as pl
from jax.experimental.pallas import tpu as pltpu
from jax.sharding import PartitionSpec as P

HEAD_DIM = 64


NORM_EPSILON = 1e-06
TILE = 128
PAIR_WORK = 1024
MODEL_HALF = 512
QKV = slice(0, 384)
OUT = slice(384, 512)
CHUNK = 32
KERNEL_VMEM = 20 << 20
ROWS_VMEM = 3 << 20


def shifted(block, axis, distance):
    devices = range(lax.axis_size(axis))
    route = [(i - distance, i) for i in devices if i - distance in devices]
    return lax.ppermute(block, axis, route)


def norm_rows(vector, weight_gain):
    return (
        vector
        * lax.rsqrt(jnp.mean(vector * vector, axis=-1, keepdims=True) + NORM_EPSILON)
        * weight_gain
    )


def rotary_tables(seq_len, head_width):
    half_width = head_width // 2
    freqs = 10000.0 ** (-2.0 * jnp.arange(half_width, dtype=jnp.float32) / head_width)
    angles = jnp.arange(seq_len, dtype=jnp.float32)[:, None] * freqs[None, :]
    return (jnp.cos(angles), jnp.sin(angles))


def rotate(vector, cos_table, sin_table):
    first_half, second_half = jnp.split(vector, 2, axis=-1)
    cos_part = cos_table[:, None, :]
    sin_part = sin_table[:, None, :]
    return jnp.concatenate(
        [
            first_half * cos_part - second_half * sin_part,
            second_half * cos_part + first_half * sin_part,
        ],
        axis=-1,
    )


def contract(left_rows, right_rows):
    return lax.dot_general(
        left_rows, right_rows, (((0,), (0,)), ((), ())), preferred_element_type=jnp.float32
    )


def gather_rows(row_values, weight):

    def project(shard_rows, offset):
        return (shard_rows, jnp.dot(shard_rows, weight, preferred_element_type=jnp.float32))

    return project(lax.all_gather(row_values, "tensor", axis=0, tiled=True), jnp.int32(0))


def scatter_rows(row_values, weight, row_count):

    def partial_term(offset, span):
        return jnp.dot(row_values, weight, preferred_element_type=jnp.float32)

    return lax.psum_scatter(
        partial_term(jnp.int32(0), lax.axis_size("tensor") * row_count),
        "tensor",
        scatter_dimension=0,
        tiled=True,
    )


def gather_grads(row_values, weight):

    def project(shard_rows, offset):
        return (shard_rows, jnp.dot(shard_rows, weight.T, preferred_element_type=jnp.float32))

    return project(lax.all_gather(row_values, "tensor", axis=0, tiled=True), jnp.int32(0))


def scatter_grads(row_values, weight, row_count):

    def partial_term(offset, span):
        return jnp.dot(row_values, weight.T, preferred_element_type=jnp.float32)

    return lax.psum_scatter(
        partial_term(jnp.int32(0), lax.axis_size("tensor") * row_count),
        "tensor",
        scatter_dimension=0,
        tiled=True,
    )


def attention_probs(queries, key_rows):
    scores = jnp.einsum(
        "qhd,khd->hqk", queries, key_rows, preferred_element_type=jnp.float32
    ) * HEAD_DIM ** (-0.5)
    length = queries.shape[0]
    positions = jnp.arange(length, dtype=jnp.int32)
    causal = positions[:, None] >= positions[None, :]
    scores = jnp.where(causal[None], scores, -1e30)
    expos = jnp.exp(scores - jnp.max(scores, axis=-1, keepdims=True))
    return expos / jnp.sum(expos, axis=-1, keepdims=True)


def layer_forward(layer_input, weights):
    gains, w_qkv, w_out, w_up, w_down = weights
    row_count, model_width = layer_input.shape
    attn_in = norm_rows(layer_input, gains[0]).astype(jnp.bfloat16)
    gathered_a, qkv = gather_rows(attn_in, w_qkv.reshape(model_width, -1))
    length = qkv.shape[0]
    head_count = w_qkv.shape[2] // HEAD_DIM
    qkv = qkv.reshape(length, 3, head_count, HEAD_DIM)
    cos_table, sin_table = rotary_tables(length, HEAD_DIM)
    queries = rotate(qkv[:, 0], cos_table, sin_table).astype(jnp.bfloat16)
    key_rows = rotate(qkv[:, 1], cos_table, sin_table).astype(jnp.bfloat16)
    values = qkv[:, 2].astype(jnp.bfloat16)
    attn_probs = attention_probs(queries, key_rows).astype(jnp.bfloat16)
    mixed = jnp.einsum("hqk,khd->qhd", attn_probs, values, preferred_element_type=jnp.float32)
    mixed = mixed.reshape(length, -1).astype(jnp.bfloat16)
    attn_branch = scatter_rows(mixed, w_out, row_count)
    hidden = layer_input + norm_rows(attn_branch, gains[1])
    mlp_in = norm_rows(hidden, gains[2]).astype(jnp.bfloat16)
    gathered_c, up_act = gather_rows(mlp_in, w_up)
    gelu_out = jax.nn.gelu(up_act, approximate=True).astype(jnp.bfloat16)
    down_branch = scatter_rows(gelu_out, w_down, row_count)
    result = hidden + norm_rows(down_branch, gains[3])
    kept_values = (
        gathered_a,
        queries,
        key_rows,
        values,
        mixed,
        attn_branch,
        hidden,
        gathered_c,
        up_act,
        gelu_out,
        down_branch,
    )
    return (result, kept_values)


def layer_backward(layer_input, grad_result, kept_values, weights):
    gains, w_qkv, w_out, w_up, w_down = weights
    (
        gathered_a,
        queries,
        key_rows,
        values,
        mixed,
        attn_branch,
        hidden,
        gathered_c,
        up_act,
        gelu_out,
        down_branch,
    ) = kept_values
    row_count, model_width = layer_input.shape
    pullback = jax.vjp(norm_rows, down_branch, gains[3])[1]
    grad_down, gain_three = pullback(grad_result)
    gathered_dd, grad_gelu = gather_grads(grad_down.astype(jnp.bfloat16), w_down)
    down_total = contract(gelu_out, gathered_dd)
    pullback = jax.vjp(lambda vector: jax.nn.gelu(vector, approximate=True), up_act)[1]
    grad_up = pullback(grad_gelu)[0].astype(jnp.bfloat16)
    up_total = contract(gathered_c, grad_up)
    grad_mlp = scatter_grads(grad_up, w_up, row_count)
    pullback = jax.vjp(norm_rows, hidden, gains[2])[1]
    grad_norm_mlp, gain_two = pullback(grad_mlp)
    grad_hidden = grad_result + grad_norm_mlp
    pullback = jax.vjp(norm_rows, attn_branch, gains[1])[1]
    grad_attn, gain_one = pullback(grad_hidden)
    gathered_da, grad_mixed = gather_grads(grad_attn.astype(jnp.bfloat16), w_out)
    out_total = contract(mixed, gathered_da)
    length = grad_mixed.shape[0]
    head_count = w_qkv.shape[2] // HEAD_DIM
    grad_mixed = grad_mixed.astype(jnp.bfloat16).reshape(length, head_count, HEAD_DIM)
    attn_probs = attention_probs(queries, key_rows)
    probs_low = attn_probs.astype(jnp.bfloat16)
    grad_probs = jnp.einsum("qhd,khd->hqk", grad_mixed, values, preferred_element_type=jnp.float32)
    grad_values = jnp.einsum(
        "hqk,qhd->khd", probs_low, grad_mixed, preferred_element_type=jnp.float32
    )
    row_dots = jnp.sum(grad_probs * attn_probs, axis=-1, keepdims=True)
    grad_scores = (attn_probs * (grad_probs - row_dots)).astype(jnp.bfloat16)
    scale_value = HEAD_DIM ** (-0.5)
    grad_queries = (
        jnp.einsum("hqk,khd->qhd", grad_scores, key_rows, preferred_element_type=jnp.float32)
        * scale_value
    )
    grad_keys = (
        jnp.einsum("hqk,qhd->khd", grad_scores, queries, preferred_element_type=jnp.float32)
        * scale_value
    )
    cos_table, sin_table = rotary_tables(length, HEAD_DIM)
    pullback = jax.vjp(lambda vector: rotate(vector, cos_table, sin_table), grad_queries)[1]
    grad_q_raw = pullback(grad_queries)[0]
    grad_k_raw = pullback(grad_keys)[0]
    grad_qkv = (
        jnp.stack([grad_q_raw, grad_k_raw, grad_values], axis=1)
        .reshape(length, -1)
        .astype(jnp.bfloat16)
    )
    qkv_total = contract(gathered_a, grad_qkv).reshape(model_width, 3, -1)
    grad_attn_in = scatter_grads(grad_qkv, w_qkv.reshape(model_width, -1), row_count)
    pullback = jax.vjp(norm_rows, layer_input, gains[0])[1]
    grad_norm_in, gain_zero = pullback(grad_attn_in)
    grad_input = grad_hidden + grad_norm_in
    gain_total = jnp.stack([gain_zero, gain_one, gain_two, gain_three])
    return (grad_input, (gain_total, qkv_total, out_total, up_total, down_total))


def lagged(first_section, stacked):
    blank = jnp.zeros_like(stacked[:1])
    earlier = jnp.concatenate([blank, stacked[:-1]])
    later = jnp.concatenate([stacked[1:], blank])
    return jnp.where(first_section, earlier, later)


def per_device(
    inputs,
    out_cotangent,
    group_ids,
    group_weights,
    gains,
    qkv_weight,
    out_weight,
    up_weight,
    down_weight,
):
    weights = (gains[0], qkv_weight[0], out_weight[0], up_weight[0], down_weight[0])
    micro_count, row_count, model_width = inputs.shape
    first_section = lax.axis_index("section") == 0
    group_count = group_weights.shape[0]
    matches = group_ids[..., None] == jnp.arange(group_count, dtype=jnp.int32)
    row_scale = jnp.sum(jnp.where(matches, group_weights, 0.0), axis=-1)
    scaled = out_cotangent.astype(jnp.float32) * row_scale[..., None]
    padded = jnp.concatenate([inputs, jnp.zeros((1, row_count, model_width), jnp.bfloat16)])

    def forward_tick(received, fresh_input):
        layer_input = jnp.where(first_section, fresh_input, received)
        result, kept_values = layer_forward(layer_input.astype(jnp.float32), weights)
        result_low = result.astype(jnp.bfloat16)
        outgoing = shifted(result_low, "section", 1)
        stashed = ()
        return (outgoing, (layer_input, result_low, stashed))

    start_rows = jnp.zeros((row_count, model_width), jnp.bfloat16)
    _, (layer_inputs, layer_results, stashed) = lax.scan(forward_tick, start_rows, padded)
    layer_outputs = jnp.where(first_section, layer_results[:-1], layer_results[1:])[None]
    back_inputs = lagged(first_section, layer_inputs)
    back_stash = jax.tree.map(lambda stacked: lagged(first_section, stacked), stashed)
    grad_padded = jnp.concatenate([scaled, jnp.zeros((1, row_count, model_width), jnp.float32)])
    tick_index = jnp.arange(micro_count + 1, dtype=jnp.int32)
    tick_valid = jnp.where(first_section, tick_index >= 1, tick_index < micro_count).astype(
        jnp.float32
    )

    def backward_tick(carry, step_item):
        received, totals = carry
        layer_input, cotangent, valid_now, stash_now = step_item
        grad_now = jnp.where(first_section, received.astype(jnp.float32), cotangent)
        input_now = layer_input.astype(jnp.float32)
        kept_values = layer_forward(input_now, weights)[1]
        grad_input, layer_grads = layer_backward(input_now, grad_now, kept_values, weights)
        totals = jax.tree.map(lambda total, update: total + valid_now * update, totals, layer_grads)
        grad_low = grad_input.astype(jnp.bfloat16)
        outgoing = shifted(grad_low, "section", -1)
        return ((outgoing, totals), grad_low)

    start_totals = (
        jnp.zeros((4, model_width), jnp.float32),
        jnp.zeros(qkv_weight.shape[1:], jnp.float32),
        jnp.zeros(out_weight.shape[1:], jnp.float32),
        jnp.zeros(up_weight.shape[1:], jnp.float32),
        jnp.zeros(down_weight.shape[1:], jnp.float32),
    )
    (_, totals), grad_lows = lax.scan(
        backward_tick,
        (start_rows, start_totals),
        (back_inputs, grad_padded, tick_valid, back_stash),
    )
    input_grads = jnp.where(first_section, grad_lows[1:], grad_lows[:-1])[None]
    gain_total, qkv_total, out_total, up_total, down_total = totals
    gains_grad = lax.psum_scatter(gain_total, ("dp", "tensor"), scatter_dimension=1, tiled=True)
    qkv_grad, out_grad, up_grad, down_grad = (
        lax.psum_scatter(
            qkv_total.astype(jnp.bfloat16), "dp", scatter_dimension=0, tiled=True
        ).astype(jnp.float32),
        lax.psum_scatter(
            out_total.astype(jnp.bfloat16), "dp", scatter_dimension=1, tiled=True
        ).astype(jnp.float32),
        lax.psum_scatter(
            up_total.astype(jnp.bfloat16), "dp", scatter_dimension=0, tiled=True
        ).astype(jnp.float32),
        lax.psum_scatter(
            down_total.astype(jnp.bfloat16), "dp", scatter_dimension=1, tiled=True
        ).astype(jnp.float32),
    )
    return (
        layer_outputs,
        input_grads,
        gains_grad[None],
        qkv_grad[None],
        out_grad[None],
        up_grad[None],
        down_grad[None],
    )


def rotated(block, cos_rows, sin_rows):
    lane = lax.broadcasted_iota(jnp.int32, block.shape, 1)
    ahead = pltpu.roll(block, 96, 1)
    behind = pltpu.roll(block, 32, 1)
    swapped = jnp.where(lane % 64 < 32, ahead, behind)
    return block * cos_rows + swapped * sin_rows


def dot_nt(left, right):
    return lax.dot_general(
        left, right, (((1,), (1,)), ((), ())), preferred_element_type=jnp.float32
    )


def dot_nn(left, right):
    return jnp.dot(left, right, preferred_element_type=jnp.float32)


def model_weight(owns, others, cols):
    sides = [jnp.concatenate([ref[:, cols] for ref in refs], axis=1) for refs in (owns, others)]
    return jnp.concatenate(sides, axis=0)


def stacked_up(values):
    return jnp.concatenate(values, axis=0)


def edge_masks(core, rows):
    key = lax.broadcasted_iota(jnp.int32, (rows, 2 * rows), 0)
    query = lax.broadcasted_iota(jnp.int32, (rows, 2 * rows), 1)
    mine = query < rows
    place = jnp.where(mine, query + core * rows, query - rows + (1 - core) * rows)
    return (key + core * rows <= place, key + (1 - core) * rows <= place)


def both_sides(value, half, start, stop, axis=0):
    if axis == 0:
        return jnp.concatenate([value[start:stop], value[half + start : half + stop]], axis=0)
    return jnp.concatenate([value[:, start:stop], value[:, half + start : half + stop]], axis=1)


def hidden_scores(scores, masks, tile, step):
    seen = step * tile
    pieces = []
    for side in range(2):
        base = side * (seen + tile)
        if seen:
            pieces.append(scores[base : base + seen])
        pieces.append(jnp.where(masks[side], scores[base + seen : base + seen + tile], -1e30))
    return jnp.concatenate(pieces, axis=0)


def one_head(rows, head):
    lane = lax.broadcasted_iota(jnp.int32, rows.shape, 1)
    return jnp.where(lane // 64 == head, rows, jnp.zeros_like(rows))


def pick_piece(weight, owns, others, cols):
    for j, (own, other) in enumerate(zip(owns, others)):

        @pl.when(pl.program_id(0) == j)
        def _():
            size = own.shape[0]
            weight[:size] = own[:, cols]
            weight[size:] = other[:, cols]


def attend_kernel(pieces, core_ref, cos_ref, sin_ref, own_rows, other_rows, *refs):
    owns, others = refs[:pieces], refs[pieces : 2 * pieces]
    q_ref, k_ref, v_ref, lse_ref, mix_ref, weight = refs[2 * pieces :]
    half = own_rows.shape[0]
    tile = TILE
    pick_piece(weight, owns, others, QKV)
    proj = dot_nn(stacked_up([own_rows[...], other_rows[...]]), weight[...])
    cos_rows, sin_rows = cos_ref[...], sin_ref[...]
    q = (rotated(proj[:, :128], cos_rows, sin_rows) * HEAD_DIM ** (-0.5)).astype(jnp.bfloat16)
    k = rotated(proj[:, 128:256], cos_rows, sin_rows).astype(jnp.bfloat16)
    v32 = proj[:, 256:]
    q_ref[0] = q
    k_ref[0] = k
    v_ref[0] = v32.astype(jnp.bfloat16)
    v_flip = v32.T.astype(jnp.bfloat16)
    masks = edge_masks(core_ref[0], tile)

    def scored(step, head):
        stop = (step + 1) * tile
        q_head = one_head(both_sides(q, half, step * tile, stop), head)
        return hidden_scores(dot_nt(both_sides(k, half, 0, stop), q_head), masks, tile, step)

    units = [(step, head) for step in range(half // tile) for head in range(2)]
    ahead = scored(*units[0])
    outs = []
    for spot, (step, head) in enumerate(units):
        scores = ahead
        if spot + 1 < len(units):
            ahead = scored(*units[spot + 1])
        stop = (step + 1) * tile
        top = jnp.max(scores, axis=0, keepdims=True)
        expos = jnp.exp(scores - top)
        total = jnp.sum(expos, axis=0, keepdims=True)
        lse = top + jnp.log(total)
        lse_ref[0, head : head + 1, step * tile : stop] = lse[:, :tile]
        lse_ref[0, head : head + 1, half + step * tile : half + stop] = lse[:, tile:]
        v_cols = both_sides(v_flip, half, 0, stop, axis=1)
        out = dot_nn(v_cols[64 * head : 64 * head + 64], expos.astype(jnp.bfloat16))
        outs.append(out * (1.0 / total))
        if head == 1:
            mixed = jnp.concatenate(outs, axis=0).T.astype(jnp.bfloat16)
            outs = []
            mix_ref[step * tile : stop, :] = mixed[:tile]
            mix_ref[half + step * tile : half + stop, :] = mixed[tile:]


def attend_back_kernel(pieces, core_ref, cos_ref, sin_ref, own_rows, other_rows, *refs):
    owns, others = refs[:pieces], refs[pieces : 2 * pieces]
    q_ref, k_ref, v_ref, lse_ref, out_ref, weight, dq, dk, dv = refs[2 * pieces :]
    half = own_rows.shape[0]
    tile = TILE
    pick_piece(weight, owns, others, OUT)
    rows = stacked_up([own_rows[...], other_rows[...]])
    d_mixed = dot_nn(rows, weight[...]).astype(jnp.bfloat16)
    q, k, v = q_ref[0], k_ref[0], v_ref[0]
    k_flip = k.astype(jnp.float32).T.astype(jnp.bfloat16)
    masks = edge_masks(core_ref[0], tile)
    steps = half // tile

    def scored(step, head):
        stop = (step + 1) * tile
        q_head = one_head(both_sides(q, half, step * tile, stop), head)
        g_head = one_head(both_sides(d_mixed, half, step * tile, stop), head)
        scores = hidden_scores(dot_nt(both_sides(k, half, 0, stop), q_head), masks, tile, step)
        return q_head, g_head, scores, dot_nt(both_sides(v, half, 0, stop), g_head)

    units = [(step, head) for step in reversed(range(steps)) for head in range(2)]
    ahead = scored(*units[0])
    dq_flips = []
    dk_sum = dv_sum = None
    for spot, (step, head) in enumerate(units):
        q_head, g_head, scores, d_probs = ahead
        if spot + 1 < len(units):
            ahead = scored(*units[spot + 1])
        stop = (step + 1) * tile
        lse = both_sides(lse_ref[0], half, step * tile, stop, axis=1)
        probs = jnp.exp(scores - lse[head : head + 1])
        dots = jnp.sum(probs * d_probs, axis=0, keepdims=True)
        d_scores = (probs * (d_probs - dots)).astype(jnp.bfloat16)
        dv_part = dot_nn(probs.astype(jnp.bfloat16), g_head)
        dk_part = dot_nn(d_scores, q_head)
        k_cols = both_sides(k_flip, half, 0, stop, axis=1)
        dq_flips.append(dot_nn(k_cols[64 * head : 64 * head + 64], d_scores))
        if head == 0:
            dv_sum, dk_sum = dv_part, dk_part
            continue
        dv_sum, dk_sum = dv_sum + dv_part, dk_sum + dk_part
        dq_rows = jnp.concatenate(dq_flips, axis=0).T * HEAD_DIM ** (-0.5)
        dq_flips = []
        dq[step * tile : stop] = dq_rows[:tile]
        dq[half + step * tile : half + stop] = dq_rows[tile:]
        for base, part in ((0, slice(0, stop)), (half, slice(stop, 2 * stop))):
            if step == steps - 1:
                dk[base : base + stop] = dk_sum[part]
                dv[base : base + stop] = dv_sum[part]
            else:
                dk[base : base + stop] += dk_sum[part]
                dv[base : base + stop] += dv_sum[part]
    cos_rows, sin_rows = cos_ref[...], -sin_ref[...]
    out_ref[:, :128] = rotated(dq[...], cos_rows, sin_rows).astype(jnp.bfloat16)
    out_ref[:, 128:256] = rotated(dk[...], cos_rows, sin_rows).astype(jnp.bfloat16)
    out_ref[:, 256:] = dv[...].astype(jnp.bfloat16)


def split_rows(total, own_ref, other_ref):
    half = own_ref.shape[0]
    own_ref[...] = total[:half]
    other_ref[...] = total[half:].astype(jnp.bfloat16)


def to_model_kernel(lefts, pieces, cols, *refs):
    left, refs = jnp.concatenate([ref[...] for ref in refs[:lefts]], axis=1), refs[lefts:]
    weight = model_weight(refs[:pieces], refs[pieces : 2 * pieces], cols)
    split_rows(dot_nt(left, weight), *refs[2 * pieces :])


def mlp_down_kernel(pieces, left_ref, *refs):
    sides = [stacked_up([ref[...] for ref in side]) for side in (refs[:pieces], refs[pieces:-2])]
    split_rows(dot_nn(left_ref[...], jnp.concatenate(sides, axis=1)), *refs[-2:])


def gelu_both(up_act):
    root = math.sqrt(2.0 / math.pi)
    square = up_act * up_act
    rise = 0.5 + 0.5 * jnp.tanh(up_act * (root + root * 0.044715 * square))
    value = up_act * rise
    slope = rise + value * (1.0 - rise) * (2.0 * root + 6.0 * root * 0.044715 * square)
    return value, slope


def mlp_up_kernel(pieces, own_rows, other_rows, *refs):
    owns, others = refs[:pieces], refs[pieces : 2 * pieces]
    gelu_ref, slope_ref = refs[2 * pieces :]
    half = own_rows.shape[0]
    size = owns[0].shape[1]
    step = half // 2
    units = [(j, i) for j in range(pieces) for i in range(4)]

    def product(j, i):
        rows = (own_rows, other_rows)[i // 2][i % 2 * step : (i % 2 + 1) * step]
        return dot_nn(rows, stacked_up([owns[j][...], others[j][...]]))

    ahead = product(*units[0])
    for spot, (j, i) in enumerate(units):
        up_act = ahead
        if spot + 1 < len(units):
            ahead = product(*units[spot + 1])
        value, slope = gelu_both(up_act)
        gelu_ref[i * step : (i + 1) * step, j * size : (j + 1) * size] = value.astype(jnp.bfloat16)
        slope_ref[i * step : (i + 1) * step, j * size : (j + 1) * size] = slope.astype(
            jnp.bfloat16
        )


def mlp_up_back_kernel(pieces, own_rows, other_rows, slope_ref, *refs):
    owns, others = refs[:pieces], refs[pieces : 2 * pieces]
    out_ref, weight, slope, sems = refs[2 * pieces :]
    half = own_rows.shape[1] // 2
    size = owns[0].shape[0]
    order = list(reversed(range(pieces)))
    copies = []
    for j in order:
        sources = (owns[j], others[j], slope_ref.at[:, pl.ds(j * size, size)])
        targets = (
            weight.at[j, :, pl.ds(0, half)],
            weight.at[j, :, pl.ds(half, half)],
            slope.at[:, pl.ds(j * size, size)],
        )
        copies.append(
            [
                pltpu.make_async_copy(source, target, sems.at[j, i])
                for i, (source, target) in enumerate(zip(sources, targets))
            ]
        )
        for copy in copies[-1]:
            copy.start()
    rows = stacked_up([own_rows[...], other_rows[...]])
    for j, arriving in zip(order, copies):
        cols = slice(j * size, (j + 1) * size)
        for copy in arriving:
            copy.wait()
        d_gelu = dot_nt(rows, weight[j])
        out_ref[:, cols] = (d_gelu * slope[:, cols].astype(jnp.float32)).astype(jnp.bfloat16)


def inverse_size(rows):
    return lax.rsqrt(jnp.mean(rows * rows, axis=-1, keepdims=True) + NORM_EPSILON)


def norm_back(rows, gain, grad):
    scale = inverse_size(rows)
    weighted = grad * gain
    inner = jnp.mean(rows * weighted, axis=-1, keepdims=True)
    return scale * weighted - rows * (scale * scale * scale * inner), rows * scale * grad


def folded(rows):
    return jnp.sum(rows.reshape(rows.shape[0] // 8, 8, rows.shape[1]), axis=0)


def wide(ref, spot):
    return ref[spot, :].astype(jnp.float32)


def by_chunks(count, body, sums=0, width=0):
    def one(i, carry):
        more = body(pl.ds(pl.multiple_of(i * CHUNK, CHUNK), CHUNK))
        return tuple(old + folded(new) for old, new in zip(carry, more))

    start = tuple(jnp.zeros((8, width), jnp.float32) for _ in range(sums))
    totals = lax.fori_loop(0, count // CHUNK, one, start)
    return [jnp.sum(total, axis=0, keepdims=True) for total in totals]


def norm_in_kernel(gain_ref, rows_ref, out_ref):
    def body(spot):
        rows = wide(rows_ref, spot)
        out_ref[spot, :] = (rows * inverse_size(rows) * gain_ref[0:1]).astype(jnp.bfloat16)
        return ()

    by_chunks(rows_ref.shape[0], body)


def after_attention_kernel(
    gain_ref, rows_ref, own_ref, other_ref, branch_ref, hidden_ref, out_ref
):
    def body(spot):
        branch = own_ref[spot, :] + wide(other_ref, spot)
        hidden = wide(rows_ref, spot) + branch * inverse_size(branch) * gain_ref[1:2]
        branch_ref[spot, :] = branch
        hidden_ref[spot, :] = hidden
        out_ref[spot, :] = (hidden * inverse_size(hidden) * gain_ref[2:3]).astype(jnp.bfloat16)
        return ()

    by_chunks(rows_ref.shape[0], body)


def after_mlp_kernel(gain_ref, hidden_ref, own_ref, other_ref, branch_ref, out_ref):
    def body(spot):
        branch = own_ref[spot, :] + wide(other_ref, spot)
        branch_ref[spot, :] = branch
        result = hidden_ref[spot, :] + branch * inverse_size(branch) * gain_ref[3:4]
        out_ref[spot, :] = result.astype(jnp.bfloat16)
        return ()

    by_chunks(hidden_ref.shape[0], body)


def into_mlp_back_kernel(gain_ref, grad_ref, branch_ref, out_ref, sum_ref):
    def body(spot):
        d_rows, d_gain = norm_back(branch_ref[spot, :], gain_ref[3:4], wide(grad_ref, spot))
        out_ref[spot, :] = d_rows.astype(jnp.bfloat16)
        return (d_gain,)

    (sum_ref[...],) = by_chunks(grad_ref.shape[0], body, 1, grad_ref.shape[1])


def into_attention_back_kernel(
    gain_ref, grad_ref, own_ref, other_ref, hidden_ref, branch_ref, d_hidden_ref, out_ref, *sums
):
    def body(spot):
        d_rows = own_ref[spot, :] + wide(other_ref, spot)
        d_rows, d_gain = norm_back(hidden_ref[spot, :], gain_ref[2:3], d_rows)
        d_hidden = wide(grad_ref, spot) + d_rows
        d_hidden_ref[spot, :] = d_hidden
        d_rows, d_first = norm_back(branch_ref[spot, :], gain_ref[1:2], d_hidden)
        out_ref[spot, :] = d_rows.astype(jnp.bfloat16)
        return (d_first, d_gain)

    totals = by_chunks(grad_ref.shape[0], body, 2, grad_ref.shape[1])
    sums[0][...], sums[1][...] = totals


def out_of_layer_kernel(gain_ref, rows_ref, own_ref, other_ref, d_hidden_ref, out_ref, sum_ref):
    def body(spot):
        d_rows = own_ref[spot, :] + wide(other_ref, spot)
        d_rows, d_gain = norm_back(wide(rows_ref, spot), gain_ref[0:1], d_rows)
        out_ref[spot, :] = (d_hidden_ref[spot, :] + d_rows).astype(jnp.bfloat16)
        return (d_gain,)

    (sum_ref[...],) = by_chunks(rows_ref.shape[0], body, 1, rows_ref.shape[1])


def work(flops, arrays):
    size = sum(math.prod(array.shape) * jnp.dtype(array.dtype).itemsize for array in arrays)
    return pl.CostEstimate(flops=flops, bytes_accessed=size, transcendentals=0)


def far(array):
    return pltpu.with_memory_space_constraint(array, pltpu.HBM)


def without(kernel, first, count):
    return lambda *refs: kernel(*refs[:first], *refs[first + count :])


def on_chip(kernel, name, outs, *operands, limit=ROWS_VMEM, flops=0, waits=()):
    shapes = [jax.ShapeDtypeStruct(shape, dtype) for shape, dtype in outs]
    space = pl.BlockSpec(memory_space=pltpu.VMEM)
    return pl.pallas_call(
        without(kernel, len(operands), len(waits)),
        in_specs=[space] * len(operands) + [pl.BlockSpec(memory_space=pl.ANY)] * len(waits),
        out_specs=[space] * len(outs),
        out_shape=shapes,
        compiler_params=pltpu.CompilerParams(vmem_limit_bytes=limit),
        cost_estimate=work(flops, (*operands, *shapes)),
        name=name,
    )(*operands, *map(far, waits))


def whole_block(array):
    return pl.BlockSpec(array.shape, lambda j: (0,) * array.ndim)


def by_pairs(kernel, name, core, operands, pieces, blocks, outs, scratch, flops, waits):
    shapes = [jax.ShapeDtypeStruct(shape, dtype) for shape, dtype, _ in outs]
    taken = 1 + len(operands) + 2 * len(pieces[0]) + len(blocks)
    return pl.pallas_call(
        without(functools.partial(kernel, len(pieces[0])), taken, len(waits)),
        grid=(len(pieces[0]),),
        in_specs=[pl.BlockSpec(memory_space=pltpu.SMEM)]
        + [whole_block(array) for array in (*operands, *pieces[0], *pieces[1])]
        + [spec for _, spec in blocks]
        + [pl.BlockSpec(memory_space=pl.ANY)] * len(waits),
        out_specs=[spec for _, _, spec in outs],
        out_shape=shapes,
        scratch_shapes=scratch,
        compiler_params=pltpu.CompilerParams(vmem_limit_bytes=KERNEL_VMEM),
        cost_estimate=work(flops, (*operands, *pieces[0], *pieces[1], *shapes)),
        name=name,
    )(core, *operands, *pieces[0], *pieces[1], *[array for array, _ in blocks], *map(far, waits))


def mlp_up_back(rows, slope, pieces, waits):
    length, units = slope.shape
    unit, half = pieces[0][0].shape
    count = len(pieces[0])
    every, space = pl.BlockSpec(memory_space=pl.ANY), pl.BlockSpec(memory_space=pltpu.VMEM)
    return pl.pallas_call(
        without(functools.partial(mlp_up_back_kernel, count), 3 + 2 * count, len(waits)),
        in_specs=[space] * 2 + [every] * (1 + 2 * count + len(waits)),
        out_specs=space,
        out_shape=jax.ShapeDtypeStruct((length, units), jnp.bfloat16),
        scratch_shapes=[
            pltpu.VMEM((count, unit, 2 * half), jnp.bfloat16),
            pltpu.VMEM((length, units), jnp.bfloat16),
            pltpu.SemaphoreType.DMA((count, 3)),
        ],
        compiler_params=pltpu.CompilerParams(vmem_limit_bytes=KERNEL_VMEM),
        name="mlp_up_back",
    )(*rows, *map(far, (slope, *pieces[0], *pieces[1], *waits)))


def attend(core, tables, rows, pieces, waits):
    half, features = rows[0].shape
    length, count = 2 * half, len(pieces[0])
    lanes = ((count, length, 128), jnp.bfloat16, pl.BlockSpec((1, length, 128), lambda j: (j, 0, 0)))
    lse = ((count, 2, length), jnp.float32, pl.BlockSpec((1, 2, length), lambda j: (j, 0, 0)))
    mixed = ((length, count * 128), jnp.bfloat16, pl.BlockSpec((length, 128), lambda j: (0, j)))
    return by_pairs(
        attend_kernel,
        "attend",
        core,
        (*tables, *rows),
        pieces,
        (),
        (lanes, lanes, lanes, lse, mixed),
        [pltpu.VMEM((features, 384), jnp.bfloat16)],
        count * length * (2 * features * 384 + 2 * PAIR_WORK * length),
        waits,
    )


def attend_back(core, tables, rows, pieces, base, waits, q, k, v, lse):
    half, features = rows[0].shape
    length, count = 2 * half, len(pieces[0])
    lanes = pl.BlockSpec((1, length, 128), lambda j: (base + j, 0, 0))
    lse_spec = pl.BlockSpec((1, 2, length), lambda j: (base + j, 0, 0))
    out = ((length, count * 384), jnp.bfloat16, pl.BlockSpec((length, 384), lambda j: (0, j)))
    return by_pairs(
        attend_back_kernel,
        "attend_back",
        core,
        (*tables, *rows),
        pieces,
        ((q, lanes), (k, lanes), (v, lanes), (lse, lse_spec)),
        (out,),
        [pltpu.VMEM((features, 128), jnp.bfloat16)] + [pltpu.VMEM((length, 128), jnp.float32)] * 3,
        count * length * (2 * features * 128 + 5 * PAIR_WORK * length),
        waits,
    )[0]


def exchanged(parts):
    return parts[0], flip_pairs(parts[1], 1)


def model_rows(kernel, name, lefts, pieces, waits=()):
    length, width = lefts[0].shape[0], 2 * MODEL_HALF
    outs = (((length // 2, width), jnp.float32), ((length // 2, width), jnp.bfloat16))
    hidden = sum(left.shape[1] for left in lefts)
    more = {"limit": KERNEL_VMEM, "flops": 2 * length * width * hidden, "waits": waits}
    return exchanged(on_chip(kernel, name, outs, *lefts, *pieces[0], *pieces[1], **more))


def flip_pairs(block, distance):
    size = lax.axis_size("dp")
    return lax.ppermute(block, "dp", [(i, i ^ distance) for i in range(size)])


def passed_on(block, step):
    size = lax.axis_size("tensor")
    return lax.ppermute(block, "tensor", [(i, (i + step) % size) for i in range(size)])


def dot_tn(left, right):
    return lax.dot_general(
        left, right, (((0,), (0,)), ((), ())), preferred_element_type=jnp.float32
    )


def fetch(first_ref, zeros, ones, buffers, sems):
    for section, sources in enumerate((zeros, ones)):

        @pl.when(first_ref[0] == section)
        def _():
            for i, (source, buffer) in enumerate(zip(sources, buffers)):
                pltpu.make_async_copy(source, buffer, sems.at[i]).start()

    def arrived(*places):
        for i in places:
            pltpu.make_async_copy(zeros[i], buffers[i], sems.at[i]).wait()

    return arrived


def mlp_grads_kernel(base, section_ref, *refs):
    (own_one, other_one, own_two, other_two), (rows, d_up, gelu, d_down, sems) = refs[12:16], refs[16:]
    half, size = own_one.shape[0] // 2, own_one.shape[1]
    cols = pl.ds(base * size, 2 * size)

    def parts(own_rows, other_rows, d_up_ref, gelu_ref, own_grad, other_grad):
        whole = (d_up_ref.at[:, cols], gelu_ref.at[:, cols])
        return (own_rows, other_rows, *whole, own_grad, other_grad)

    count = refs[0].shape[0]
    buffers = (
        rows.at[pl.ds(0, count)],
        rows.at[pl.ds(count, count)],
        d_up,
        gelu,
        d_down.at[pl.ds(0, count)],
        d_down.at[pl.ds(count, count)],
    )
    arrived = fetch(section_ref, parts(*refs[:6]), parts(*refs[6:12]), buffers, sems)
    for j, own, other in ((1, own_two, other_two), (0, own_one, other_one)):
        cols = slice(j * size, (j + 1) * size)
        if j == 1:
            arrived(0, 1, 2)
        up = dot_tn(rows[...], d_up[:, cols])
        own[:half] = up[:half]
        other[:half] = up[half:].astype(jnp.bfloat16)
        if j == 1:
            arrived(3, 4, 5)
        down = dot_tn(gelu[:, cols], d_down[...])
        own[half:] = down[:, :half]
        other[half:] = down[:, half:].astype(jnp.bfloat16)


def attn_grads_kernel(base, section_ref, *refs):
    (own_one, other_one, own_two, other_two), (rows, d_qkv, mixed, d_attn, sems) = refs[12:16], refs[16:]
    half, size = own_one.shape[0], d_qkv.shape[1] // 2
    count = refs[0].shape[0]
    cols = pl.ds(base * 128, 256)

    def parts(own_rows, other_rows, d_qkv_ref, mixed_ref, own_grad, other_grad):
        return (own_rows, other_rows, d_qkv_ref, mixed_ref.at[:, cols], own_grad, other_grad)

    buffers = (
        rows.at[pl.ds(0, count)],
        rows.at[pl.ds(count, count)],
        d_qkv,
        mixed,
        d_attn.at[pl.ds(0, count)],
        d_attn.at[pl.ds(count, count)],
    )
    arrived = fetch(section_ref, parts(*refs[:6]), parts(*refs[6:12]), buffers, sems)
    for j, own, other in ((1, own_two, other_two), (0, own_one, other_one)):
        if j == 1:
            arrived(0, 1, 2)
        qkv = dot_tn(rows[...], d_qkv[:, j * size : (j + 1) * size])
        if j == 1:
            arrived(3, 4, 5)
        out = dot_tn(d_attn[...], mixed[:, j * 128 : (j + 1) * 128])
        own[:, :size] = qkv[:half]
        own[:, size:] = out[:half]
        other[:, :size] = qkv[half:].astype(jnp.bfloat16)
        other[:, size:] = out[half:].astype(jnp.bfloat16)


def weight_grads(kernel, name, base, section, zeros, ones, shape, columns, waits=()):
    length = 2 * zeros[0].shape[0]
    width = zeros[0].shape[1]
    every = pl.BlockSpec(memory_space=pl.ANY)
    space = pl.BlockSpec(memory_space=pltpu.VMEM)
    arrays = (*zeros, *ones)
    first, second, third, fourth = pl.pallas_call(
        without(functools.partial(kernel, base), 1 + len(arrays), len(waits)),
        in_specs=[pl.BlockSpec(memory_space=pltpu.SMEM)] + [every] * (len(arrays) + len(waits)),
        out_specs=[space] * 4,
        out_shape=[
            jax.ShapeDtypeStruct(shape, jnp.float32),
            jax.ShapeDtypeStruct(shape, jnp.bfloat16),
        ]
        * 2,
        scratch_shapes=[
            pltpu.VMEM((length, width), jnp.bfloat16),
            pltpu.VMEM((length, columns[0]), jnp.bfloat16),
            pltpu.VMEM((length, columns[1]), jnp.bfloat16),
            pltpu.VMEM((length, width), jnp.bfloat16),
            pltpu.SemaphoreType.DMA((6,)),
        ],
        compiler_params=pltpu.CompilerParams(vmem_limit_bytes=KERNEL_VMEM),
        name=name,
    )(section, *map(far, (*arrays, *waits)))
    return [(first, flip_pairs(second, 2)), (third, flip_pairs(fourth, 2))]


def moved_kernel(own_ref, other_ref, *refs):
    out_ref = refs[-1]

    def body(i, carry):
        spot = pl.ds(pl.multiple_of(i * CHUNK, CHUNK), CHUNK)
        total = own_ref[spot, :]
        for ref in (other_ref, *refs[:-1]):
            total = total + wide(ref, spot)
        out_ref[spot, :] = total.astype(jnp.bfloat16)
        return carry

    lax.fori_loop(0, own_ref.shape[0] // CHUNK, body, 0)


def gates_kernel(up_ref, down_ref, up_out, down_out):
    up_out[...] = up_ref[...]
    down_out[...] = down_ref[...]


def gate_kernel(piece_ref, out_ref):
    out_ref[...] = piece_ref[...]


def mlp_sum_kernel(core_ref, own_ref, other_ref, moved_ref, up_keep, down_keep, up_send, down_send):
    half = own_ref.shape[0] // 2
    size = up_keep.shape[0]

    def total(rows, cols):
        more = other_ref[rows, cols].astype(jnp.float32) + moved_ref[rows, cols].astype(jnp.float32)
        return own_ref[rows, cols] + more

    for core in range(2):

        @pl.when(core_ref[0] == core)
        def _():
            for place, up, down in ((core, up_keep, down_keep), (1 - core, up_send, down_send)):
                spot = slice(place * size, (place + 1) * size)
                up[...] = total(spot, slice(None))
                down[...] = total(slice(half, None), spot)


def mlp_join_kernel(core_ref, up_keep, down_keep, up_sent, down_sent, up_out, down_out):
    size = up_keep.shape[1]
    for core in range(2):

        @pl.when(core_ref[0] == core)
        def _():
            places = ((core, up_keep, down_keep), (1 - core, up_sent, down_sent))
            for place, up, down in places:
                spot = slice(place * size, (place + 1) * size)
                up_out[:, spot] = up[...]
                down_out[spot] = down[...]


def chosen_kernel(place_ref, zero_ref, one_ref, out_ref):
    half = out_ref.shape[1] // 2
    for section, rows_ref in enumerate((zero_ref, one_ref)):
        for upper in range(2):

            @pl.when(jnp.logical_and(place_ref[0] == section, place_ref[1] == upper))
            def _():
                for side in range(2):
                    place = (side + upper) % 2 * half
                    out_ref[:, place : place + half] = rows_ref[:, side * half : (side + 1) * half]


def pick_kernel(core_ref, rows_ref, keep_ref, send_ref):
    count = keep_ref.shape[0]
    keep_ref[...] = rows_ref[pl.ds(core_ref[0] * count, count)]
    send_ref[...] = rows_ref[pl.ds((1 - core_ref[0]) * count, count)]


def in_order_kernel(core_ref, keep_ref, sent_ref, out_ref):
    out_ref[:, pl.ds(core_ref[0], 1)] = keep_ref[...][:, None]
    out_ref[:, pl.ds(1 - core_ref[0], 1)] = sent_ref[...][:, None]


def with_core(kernel, name, core, outs, *operands, waits=()):
    space = pl.BlockSpec(memory_space=pltpu.VMEM)
    return pl.pallas_call(
        without(kernel, 1 + len(operands), len(waits)),
        in_specs=[pl.BlockSpec(memory_space=pltpu.SMEM)]
        + [space] * len(operands)
        + [pl.BlockSpec(memory_space=pl.ANY)] * len(waits),
        out_specs=[space] * len(outs),
        out_shape=[jax.ShapeDtypeStruct(shape, dtype) for shape, dtype in outs],
        compiler_params=pltpu.CompilerParams(vmem_limit_bytes=ROWS_VMEM),
        name=name,
    )(core, *operands, *map(far, waits))


def last_sum_kernel(core_ref, own_ref, other_ref, moved_ref, keep_ref, send_ref):
    rows = keep_ref.shape[0]

    def total(block):
        spot = pl.ds(pl.multiple_of(block * rows, rows), rows)
        return own_ref[spot, :] + wide(other_ref, spot) + wide(moved_ref, spot)

    keep_ref[...] = total(core_ref[0])
    send_ref[...] = total(1 - core_ref[0])


def joined_kernel(spots, core_ref, keep_ref, sent_ref, column_ref, row_ref):
    size = row_ref.shape[0] // 2
    for core in range(2):

        @pl.when(core_ref[0] == core)
        def _():
            for place, source in ((core, keep_ref), (1 - core, sent_ref)):
                for start, stop, to in spots:
                    step = stop - start
                    column_ref[:, to + place * step : to + (place + 1) * step] = source[:, start:stop]
                row_ref[place * size : (place + 1) * size] = source[:, spots[-1][1] :].T


def per_chip(
    inputs,
    out_cotangent,
    group_ids,
    group_weights,
    gains,
    qkv_weight,
    out_weight,
    up_weight,
    down_weight,
):
    micro, row_count, width = inputs.shape
    tensor = lax.axis_size("tensor")
    part = row_count // 2
    wide_half = width // 2
    length = tensor * row_count
    half = length // 2
    first = lax.axis_index("section") == 0
    place = lax.axis_index("dp")
    core = place % 2
    upper = place // 2 % 2
    core_zero = core == 0
    low_half = upper == 0

    def ordered(mine, other):
        return jnp.where(core_zero, mine, other), jnp.where(core_zero, other, mine)

    def own_first(values):
        return jnp.where(low_half, values, jnp.roll(values, wide_half, axis=-1))

    def both_rows(own):
        return own, flip_pairs(own, 1)

    def to_chip(block):
        split = block.reshape((micro, 2, part) + block.shape[2:])
        mine = lax.dynamic_index_in_dim(split, core, 1, keepdims=False)
        other = lax.dynamic_index_in_dim(split, 1 - core, 1, keepdims=False)
        return lax.all_to_all(
            jnp.concatenate(ordered(mine, flip_pairs(other, 1))), "tensor", 0, 0, tiled=True
        )

    def from_chip(spread_out, waits=()):
        piece = ((micro, part, width), jnp.bfloat16)
        keep, send = with_core(
            pick_kernel, "pick", core_word, (piece, piece), spread_out, waits=waits
        )
        outs = (((micro, 2, part, width), jnp.bfloat16),)
        (rows,) = with_core(
            in_order_kernel, "in_order", core_word, outs, keep, flip_pairs(send, 1)
        )
        return rows.reshape(micro, row_count, width)

    def columns(local):
        size = local.shape[-1] // 2
        mid = (0,) * (local.ndim - 2)
        piece = lax.dynamic_slice(
            local,
            (wide_half * upper, *mid, size * core),
            (wide_half, *local.shape[1:-1], size),
        )
        return piece.reshape(wide_half, -1)

    def rows(local):
        size = local.shape[0] // 2
        return lax.dynamic_slice(local, (size * core, wide_half * upper), (size, wide_half))

    core_word = core.astype(jnp.int32).reshape(1)
    attn_piece = jnp.concatenate([columns(qkv_weight[0]), rows(out_weight[0]).T], axis=1)

    def spread(piece):
        pieces = [piece]
        for _ in range(tensor - 1):
            pieces.append(passed_on(pieces[-1], 1))
        return pieces

    up_piece, down_piece = columns(up_weight[0]), rows(down_weight[0])
    up_other, down_other = [flip_pairs(up_piece, 2)], [flip_pairs(down_piece, 2)]
    attn_own = [attn_piece, passed_on(attn_piece, 1)]
    attn_first = flip_pairs(attn_piece, 2)
    outs = ((attn_piece.shape, attn_piece.dtype),)
    attn_own[1] = on_chip(gate_kernel, "gate", outs, attn_own[1], waits=(attn_first, up_other[0]))[0]
    attn_own += spread(attn_own[1])[1:-1]
    attn_other = [attn_first] + [flip_pairs(piece, 2) for piece in attn_own[1:]]
    outs = tuple((piece.shape, piece.dtype) for piece in (up_piece, down_piece))
    up_piece, down_piece = on_chip(
        gates_kernel, "gate", outs, up_piece, down_piece, waits=(attn_own[2], attn_other[0], down_other[0])
    )
    up_own, down_own = spread(up_piece), spread(down_piece)
    up_other += [flip_pairs(piece, 2) for piece in up_own[1:]]
    down_other += [flip_pairs(piece, 2) for piece in down_own[1:]]
    w_attn, w_up, w_down = (attn_own, attn_other), (up_own, up_other), (down_own, down_other)
    unit = up_piece.shape[1]
    units = tensor * unit

    group_count = group_weights.shape[0]
    matches = group_ids[..., None] == jnp.arange(group_count, dtype=jnp.int32)
    row_scale = jnp.sum(jnp.where(matches, group_weights, 0.0), axis=-1)
    weighted = (out_cotangent.astype(jnp.float32) * row_scale[..., None]).astype(jnp.bfloat16)
    start = to_chip(own_first(jnp.where(first, inputs, weighted))).reshape(half, width)
    gain = own_first(gains[0])

    turns = jnp.arange(half, dtype=jnp.int32)
    turns = turns // part * row_count + turns % part
    positions = jnp.concatenate([turns + core * part, turns + (1 - core) * part])
    freqs = 10000.0 ** (-2.0 * jnp.arange(HEAD_DIM // 2, dtype=jnp.float32) / HEAD_DIM)
    angles = positions.astype(jnp.float32)[:, None] * freqs[None, :]
    cos_part, sin_part = jnp.cos(angles), jnp.sin(angles)
    tables = (
        jnp.concatenate([cos_part] * 4, axis=1),
        jnp.concatenate([-sin_part, sin_part] * 2, axis=1),
    )
    row32, row16 = ((half, width), jnp.float32), ((half, width), jnp.bfloat16)
    unit16 = ((length, units), jnp.bfloat16)
    sum32 = ((1, width), jnp.float32)
    mlp_cost = {"limit": KERNEL_VMEM, "flops": 2 * length * width * units}
    every = slice(None)

    def model_kernel(cols, lefts=1):
        return functools.partial(to_model_kernel, lefts, tensor, cols)

    down_kernel = functools.partial(mlp_down_kernel, tensor)

    def forward(layer_input, waits):
        attn_in = both_rows(
            on_chip(norm_in_kernel, "norm_in", (row16,), gain, layer_input, waits=waits[0])[0]
        )
        *heads, mixed = attend(core_word, tables, attn_in, w_attn, waits[1])
        parts = model_rows(model_kernel(OUT), "attn_out", [mixed], w_attn, waits[2])
        operands = (gain, layer_input, *parts)
        branch, hidden, mlp_in = on_chip(
            after_attention_kernel, "after_attn", (row32, row32, row16), *operands, waits=waits[3]
        )
        mlp_in = both_rows(mlp_in)
        kernel = functools.partial(mlp_up_kernel, tensor)
        operands = (*mlp_in, *w_up[0], *w_up[1])
        gelu_out, slope = on_chip(kernel, "mlp_up", (unit16, unit16), *operands, **mlp_cost)
        parts = model_rows(down_kernel, "mlp_down", [gelu_out], w_down)
        mlp_branch, result = on_chip(
            after_mlp_kernel, "after_mlp", (row32, row16), gain, hidden, *parts
        )
        saved = (layer_input, heads, branch, hidden, slope, mlp_branch)
        return result, saved, (attn_in, mixed, mlp_in, gelu_out)

    def backward(grad, saved, hook, late=()):
        layer_input, heads, branch, hidden, slope, mlp_branch = saved
        operands = (gain, grad, mlp_branch)
        d_down, sum_three = on_chip(
            into_mlp_back_kernel, "into_mlp_back", (row16, sum32), *operands
        )
        d_down = both_rows(d_down)
        d_up = mlp_up_back(d_down, slope, w_down, late)
        waits = hook(d_down, d_up)
        parts = model_rows(model_kernel(every), "mlp_back", [d_up], w_up, waits)
        waits = hook()
        operands = (gain, grad, *parts, hidden, branch)
        outs = (row32, row16, sum32, sum32)
        d_hidden, d_attn, sum_one, sum_two = on_chip(
            into_attention_back_kernel, "into_attn_back", outs, *operands, waits=waits
        )
        d_attn = both_rows(d_attn)
        waits = hook(d_attn)
        d_qkv = []
        for base in reversed(range(0, tensor, 2)):
            some = [side[base : base + 2] for side in w_attn]
            now = attend_back(core_word, tables, d_attn, some, base, waits, *heads)
            d_qkv.insert(0, now)
            waits = hook(now)
        parts = model_rows(model_kernel(QKV, 2), "attn_back", d_qkv, w_attn, waits)
        operands = (gain, layer_input, *parts, d_hidden)
        d_input, sum_zero = on_chip(
            out_of_layer_kernel, "out_of_layer", (row16, sum32), *operands, waits=hook()
        )
        sums = jnp.concatenate([sum_zero, sum_one, sum_two, sum_three])
        return d_input, (d_qkv, d_attn, d_up, d_down), sums

    low_zero, saved_zero, lefts_zero = forward(
        start,
        (
            (up_piece, up_other[0], down_other[0]),
            (up_own[2], down_own[2], up_other[1], down_other[1]),
            (up_own[3], down_own[3], up_other[2], down_other[2]),
            (up_other[3],),
        ),
    )
    low_one, saved_one, lefts_one = forward(shifted(low_zero, "section", 1), ((),) * 4)
    grad_one, rights_one, gain_one = backward(start, saved_one, lambda *new: ())
    received = shifted(grad_one, "section", -1)

    lows = lax.optimization_barrier((low_zero, low_one, grad_one))[:2]
    lows = own_first(jnp.where(first, *lows)).reshape(tensor, part, width)
    lows = lax.all_to_all(lows, "tensor", 0, 0, tiled=True)

    section_word = lax.axis_index("section").astype(jnp.int32).reshape(1)

    def mlp_leaves(base, waits=()):
        zeros = (*lefts_zero[2], d_up, lefts_zero[3], *d_down)
        ones = (*lefts_one[2], rights_one[2], lefts_one[3], *rights_one[3])
        mlp_sums[base : base + 2] = weight_grads(
            mlp_grads_kernel,
            "mlp_grads",
            base,
            section_word,
            zeros,
            ones,
            (wide_half + unit, unit),
            (2 * unit, 2 * unit),
            waits,
        )

    def attn_leaves(base, d_qkv, waits):
        zeros = (*lefts_zero[0], d_qkv, lefts_zero[1], *d_attn)
        ones = (*lefts_one[0], rights_one[0][base // 2], lefts_one[1], *rights_one[1])
        attn_sums[base : base + 2] = weight_grads(
            attn_grads_kernel,
            "attn_grads",
            base,
            section_word,
            zeros,
            ones,
            (wide_half, 512),
            (768, 256),
            waits,
        )

    def moves_on(piece, *moved, waits=()):
        outs = ((piece[1].shape, jnp.bfloat16),)
        (total,) = on_chip(moved_kernel, "moved", outs, *piece, *moved, waits=waits)
        return total, passed_on(total, -1)

    mlp_sums, attn_sums = [None] * tensor, [None] * tensor
    mlp_moves, attn_moves = [None] * tensor, [None] * tensor
    hooks = iter(range(6))

    def hook(*new):
        nonlocal d_down, d_up, d_attn, outputs
        turn = next(hooks)
        if turn == 0:
            d_down, d_up = new
            mlp_leaves(2)
            return (mlp_sums[3][0],)
        if turn == 1:
            return ()
        if turn == 2:
            (d_attn,) = new
            outputs = from_chip(lows, d_attn[:1])
            total, mlp_moves[3] = moves_on(mlp_sums[3], waits=(outputs,))
            mlp_leaves(0, (total,))
            return (mlp_sums[1][0],)
        if turn == 3:
            total, mlp_moves[2] = moves_on(mlp_sums[2], mlp_moves[3], waits=new)
            attn_leaves(2, new[0], (total,))
            return (mlp_sums[2][1], mlp_moves[3], attn_sums[3][0])
        if turn == 4:
            total, mlp_moves[1] = moves_on(mlp_sums[1], mlp_moves[2], waits=new)
            attn_leaves(0, new[0], (total,))
            total, attn_moves[3] = moves_on(attn_sums[3], waits=attn_sums[1][:1])
            return (total, mlp_moves[1], mlp_sums[0][1])
        return attn_sums[2][1:]

    d_down = d_up = d_attn = outputs = None
    grad_zero, rights_zero, gain_zero = backward(received, saved_zero, hook, (lows,))
    place_word = jnp.stack([lax.axis_index("section"), upper]).astype(jnp.int32)
    (grads,) = with_core(
        chosen_kernel,
        "chosen",
        place_word,
        (row16,),
        grad_zero,
        grad_one,
        waits=(attn_moves[3], attn_sums[1][1]),
    )
    grads = lax.all_to_all(grads.reshape(tensor, part, width), "tensor", 0, 0, tiled=True)

    block32 = ((wide_half // 2, unit), jnp.float32)
    down32 = ((unit, wide_half // 2), jnp.float32)
    up_keep, down_keep, up_send, down_send = with_core(
        mlp_sum_kernel,
        "mlp_sum",
        core_word,
        (block32, down32, block32, down32),
        *mlp_sums[0],
        mlp_moves[1],
        waits=(grad_zero,),
    )
    outs = (
        ((wide_half // 2, 2 * unit), jnp.float32),
        ((2 * unit, wide_half // 2), jnp.float32),
    )
    sent = flip_pairs(up_send, 1), flip_pairs(down_send, 1)
    up_grad, down_grad = with_core(
        mlp_join_kernel, "mlp_join", core_word, outs, up_keep, down_keep, *sent
    )
    total, attn_moves[2] = moves_on(attn_sums[2], attn_moves[3], waits=(grad_zero,))
    waits = (up_grad, attn_sums[0][1], grads)
    last, attn_moves[1] = moves_on(attn_sums[1], attn_moves[2], waits=waits)
    grads = from_chip(grads, (last,))
    gain_total = own_first(jnp.where(first, gain_zero, gain_one))
    count = tensor * lax.axis_size("dp")
    gain_parts = gain_total.reshape(4, count, width // count).swapaxes(0, 1)
    outs = ((gain_parts.shape, gain_parts.dtype),)
    (gain_parts,) = on_chip(gate_kernel, "gate", outs, gain_parts, waits=(last,))
    gain_parts = lax.all_to_all(gain_parts, ("dp", "tensor"), 0, 0, tiled=True)
    gains_grad = jnp.sum(gain_parts, axis=0)
    outs = (((wide_half // 2, 512), jnp.float32),) * 2
    keep, send = with_core(
        last_sum_kernel,
        "attn_sum",
        core_word,
        outs,
        *attn_sums[0],
        attn_moves[1],
        waits=(grads, outputs, gains_grad),
    )
    spots = tuple((i * 128, (i + 1) * 128, i * 256) for i in range(3))
    outs = (((wide_half // 2, 768), jnp.float32), ((256, wide_half // 2), jnp.float32))
    kernel = functools.partial(joined_kernel, spots)
    qkv_grad, out_grad = with_core(
        kernel, "attn_join", core_word, outs, keep, flip_pairs(send, 1)
    )
    qkv_grad = qkv_grad.reshape(wide_half // 2, 3, -1)

    return (
        outputs[None],
        grads[None],
        gains_grad[None],
        qkv_grad[None],
        out_grad[None],
        up_grad[None],
        down_grad[None],
    )


def takes_chips(sizes):
    return sizes["section"] == 2 and sizes["dp"] == 4 and sizes["tensor"] == 4


def solution(mesh):
    placed = (
        P("dp", "tensor", None),
        P("dp", "tensor", None),
        P("dp", "tensor"),
        P(),
        P("section", None, None),
        P("section", None, None, "tensor"),
        P("section", "tensor", None),
        P("section", None, "tensor"),
        P("section", "tensor", None),
    )
    body = per_chip if takes_chips(dict(mesh.shape)) else per_device
    return jax.shard_map(
        body,
        mesh=mesh,
        in_specs=placed,
        out_specs=(
            P("section", "dp", "tensor", None),
            P("section", "dp", "tensor", None),
            P("section", None, ("dp", "tensor")),
            P("section", "dp", None, "tensor"),
            P("section", "tensor", "dp"),
            P("section", "dp", "tensor"),
            P("section", "tensor", "dp"),
        ),
        check_vma=False,
    )
```

```python
import functools
import math

import jax
import jax.numpy as jnp
from jax import lax
from jax.experimental import pallas as pl
from jax.experimental.pallas import tpu as pltpu
from jax.sharding import PartitionSpec as P

HEAD_DIM = 64


NORM_EPSILON = 1e-06
TILE = 128
PAIR_WORK = 1024
MODEL_HALF = 512
QKV = slice(0, 384)
OUT = slice(384, 512)
CHUNK = 16
KERNEL_VMEM = 20 << 20
ROWS_VMEM = 3 << 20


def shifted(block, axis, distance):
    devices = range(lax.axis_size(axis))
    route = [(i - distance, i) for i in devices if i - distance in devices]
    return lax.ppermute(block, axis, route)


def norm_rows(vector, weight_gain):
    return (
        vector
        * lax.rsqrt(jnp.mean(vector * vector, axis=-1, keepdims=True) + NORM_EPSILON)
        * weight_gain
    )


def rotary_tables(seq_len, head_width):
    half_width = head_width // 2
    freqs = 10000.0 ** (-2.0 * jnp.arange(half_width, dtype=jnp.float32) / head_width)
    angles = jnp.arange(seq_len, dtype=jnp.float32)[:, None] * freqs[None, :]
    return (jnp.cos(angles), jnp.sin(angles))


def rotate(vector, cos_table, sin_table):
    first_half, second_half = jnp.split(vector, 2, axis=-1)
    cos_part = cos_table[:, None, :]
    sin_part = sin_table[:, None, :]
    return jnp.concatenate(
        [
            first_half * cos_part - second_half * sin_part,
            second_half * cos_part + first_half * sin_part,
        ],
        axis=-1,
    )


def contract(left_rows, right_rows):
    return lax.dot_general(
        left_rows, right_rows, (((0,), (0,)), ((), ())), preferred_element_type=jnp.float32
    )


def gather_rows(row_values, weight):

    def project(shard_rows, offset):
        return (shard_rows, jnp.dot(shard_rows, weight, preferred_element_type=jnp.float32))

    return project(lax.all_gather(row_values, "tensor", axis=0, tiled=True), jnp.int32(0))


def scatter_rows(row_values, weight, row_count):

    def partial_term(offset, span):
        return jnp.dot(row_values, weight, preferred_element_type=jnp.float32)

    return lax.psum_scatter(
        partial_term(jnp.int32(0), lax.axis_size("tensor") * row_count),
        "tensor",
        scatter_dimension=0,
        tiled=True,
    )


def gather_grads(row_values, weight):

    def project(shard_rows, offset):
        return (shard_rows, jnp.dot(shard_rows, weight.T, preferred_element_type=jnp.float32))

    return project(lax.all_gather(row_values, "tensor", axis=0, tiled=True), jnp.int32(0))


def scatter_grads(row_values, weight, row_count):

    def partial_term(offset, span):
        return jnp.dot(row_values, weight.T, preferred_element_type=jnp.float32)

    return lax.psum_scatter(
        partial_term(jnp.int32(0), lax.axis_size("tensor") * row_count),
        "tensor",
        scatter_dimension=0,
        tiled=True,
    )


def attention_probs(queries, key_rows):
    scores = jnp.einsum(
        "qhd,khd->hqk", queries, key_rows, preferred_element_type=jnp.float32
    ) * HEAD_DIM ** (-0.5)
    length = queries.shape[0]
    positions = jnp.arange(length, dtype=jnp.int32)
    causal = positions[:, None] >= positions[None, :]
    scores = jnp.where(causal[None], scores, -1e30)
    expos = jnp.exp(scores - jnp.max(scores, axis=-1, keepdims=True))
    return expos / jnp.sum(expos, axis=-1, keepdims=True)


def layer_forward(layer_input, weights):
    gains, w_qkv, w_out, w_up, w_down = weights
    row_count, model_width = layer_input.shape
    attn_in = norm_rows(layer_input, gains[0]).astype(jnp.bfloat16)
    gathered_a, qkv = gather_rows(attn_in, w_qkv.reshape(model_width, -1))
    length = qkv.shape[0]
    head_count = w_qkv.shape[2] // HEAD_DIM
    qkv = qkv.reshape(length, 3, head_count, HEAD_DIM)
    cos_table, sin_table = rotary_tables(length, HEAD_DIM)
    queries = rotate(qkv[:, 0], cos_table, sin_table).astype(jnp.bfloat16)
    key_rows = rotate(qkv[:, 1], cos_table, sin_table).astype(jnp.bfloat16)
    values = qkv[:, 2].astype(jnp.bfloat16)
    attn_probs = attention_probs(queries, key_rows).astype(jnp.bfloat16)
    mixed = jnp.einsum("hqk,khd->qhd", attn_probs, values, preferred_element_type=jnp.float32)
    mixed = mixed.reshape(length, -1).astype(jnp.bfloat16)
    attn_branch = scatter_rows(mixed, w_out, row_count)
    hidden = layer_input + norm_rows(attn_branch, gains[1])
    mlp_in = norm_rows(hidden, gains[2]).astype(jnp.bfloat16)
    gathered_c, up_act = gather_rows(mlp_in, w_up)
    gelu_out = jax.nn.gelu(up_act, approximate=True).astype(jnp.bfloat16)
    down_branch = scatter_rows(gelu_out, w_down, row_count)
    result = hidden + norm_rows(down_branch, gains[3])
    kept_values = (
        gathered_a,
        queries,
        key_rows,
        values,
        mixed,
        attn_branch,
        hidden,
        gathered_c,
        up_act,
        gelu_out,
        down_branch,
    )
    return (result, kept_values)


def layer_backward(layer_input, grad_result, kept_values, weights):
    gains, w_qkv, w_out, w_up, w_down = weights
    (
        gathered_a,
        queries,
        key_rows,
        values,
        mixed,
        attn_branch,
        hidden,
        gathered_c,
        up_act,
        gelu_out,
        down_branch,
    ) = kept_values
    row_count, model_width = layer_input.shape
    pullback = jax.vjp(norm_rows, down_branch, gains[3])[1]
    grad_down, gain_three = pullback(grad_result)
    gathered_dd, grad_gelu = gather_grads(grad_down.astype(jnp.bfloat16), w_down)
    down_total = contract(gelu_out, gathered_dd)
    pullback = jax.vjp(lambda vector: jax.nn.gelu(vector, approximate=True), up_act)[1]
    grad_up = pullback(grad_gelu)[0].astype(jnp.bfloat16)
    up_total = contract(gathered_c, grad_up)
    grad_mlp = scatter_grads(grad_up, w_up, row_count)
    pullback = jax.vjp(norm_rows, hidden, gains[2])[1]
    grad_norm_mlp, gain_two = pullback(grad_mlp)
    grad_hidden = grad_result + grad_norm_mlp
    pullback = jax.vjp(norm_rows, attn_branch, gains[1])[1]
    grad_attn, gain_one = pullback(grad_hidden)
    gathered_da, grad_mixed = gather_grads(grad_attn.astype(jnp.bfloat16), w_out)
    out_total = contract(mixed, gathered_da)
    length = grad_mixed.shape[0]
    head_count = w_qkv.shape[2] // HEAD_DIM
    grad_mixed = grad_mixed.astype(jnp.bfloat16).reshape(length, head_count, HEAD_DIM)
    attn_probs = attention_probs(queries, key_rows)
    probs_low = attn_probs.astype(jnp.bfloat16)
    grad_probs = jnp.einsum("qhd,khd->hqk", grad_mixed, values, preferred_element_type=jnp.float32)
    grad_values = jnp.einsum(
        "hqk,qhd->khd", probs_low, grad_mixed, preferred_element_type=jnp.float32
    )
    row_dots = jnp.sum(grad_probs * attn_probs, axis=-1, keepdims=True)
    grad_scores = (attn_probs * (grad_probs - row_dots)).astype(jnp.bfloat16)
    scale_value = HEAD_DIM ** (-0.5)
    grad_queries = (
        jnp.einsum("hqk,khd->qhd", grad_scores, key_rows, preferred_element_type=jnp.float32)
        * scale_value
    )
    grad_keys = (
        jnp.einsum("hqk,qhd->khd", grad_scores, queries, preferred_element_type=jnp.float32)
        * scale_value
    )
    cos_table, sin_table = rotary_tables(length, HEAD_DIM)
    pullback = jax.vjp(lambda vector: rotate(vector, cos_table, sin_table), grad_queries)[1]
    grad_q_raw = pullback(grad_queries)[0]
    grad_k_raw = pullback(grad_keys)[0]
    grad_qkv = (
        jnp.stack([grad_q_raw, grad_k_raw, grad_values], axis=1)
        .reshape(length, -1)
        .astype(jnp.bfloat16)
    )
    qkv_total = contract(gathered_a, grad_qkv).reshape(model_width, 3, -1)
    grad_attn_in = scatter_grads(grad_qkv, w_qkv.reshape(model_width, -1), row_count)
    pullback = jax.vjp(norm_rows, layer_input, gains[0])[1]
    grad_norm_in, gain_zero = pullback(grad_attn_in)
    grad_input = grad_hidden + grad_norm_in
    gain_total = jnp.stack([gain_zero, gain_one, gain_two, gain_three])
    return (grad_input, (gain_total, qkv_total, out_total, up_total, down_total))


def lagged(first_section, stacked):
    blank = jnp.zeros_like(stacked[:1])
    earlier = jnp.concatenate([blank, stacked[:-1]])
    later = jnp.concatenate([stacked[1:], blank])
    return jnp.where(first_section, earlier, later)


def per_device(
    inputs,
    out_cotangent,
    group_ids,
    group_weights,
    gains,
    qkv_weight,
    out_weight,
    up_weight,
    down_weight,
):
    weights = (gains[0], qkv_weight[0], out_weight[0], up_weight[0], down_weight[0])
    micro_count, row_count, model_width = inputs.shape
    first_section = lax.axis_index("section") == 0
    group_count = group_weights.shape[0]
    matches = group_ids[..., None] == jnp.arange(group_count, dtype=jnp.int32)
    row_scale = jnp.sum(jnp.where(matches, group_weights, 0.0), axis=-1)
    scaled = out_cotangent.astype(jnp.float32) * row_scale[..., None]
    padded = jnp.concatenate([inputs, jnp.zeros((1, row_count, model_width), jnp.bfloat16)])

    def forward_tick(received, fresh_input):
        layer_input = jnp.where(first_section, fresh_input, received)
        result, kept_values = layer_forward(layer_input.astype(jnp.float32), weights)
        result_low = result.astype(jnp.bfloat16)
        outgoing = shifted(result_low, "section", 1)
        stashed = ()
        return (outgoing, (layer_input, result_low, stashed))

    start_rows = jnp.zeros((row_count, model_width), jnp.bfloat16)
    _, (layer_inputs, layer_results, stashed) = lax.scan(forward_tick, start_rows, padded)
    layer_outputs = jnp.where(first_section, layer_results[:-1], layer_results[1:])[None]
    back_inputs = lagged(first_section, layer_inputs)
    back_stash = jax.tree.map(lambda stacked: lagged(first_section, stacked), stashed)
    grad_padded = jnp.concatenate([scaled, jnp.zeros((1, row_count, model_width), jnp.float32)])
    tick_index = jnp.arange(micro_count + 1, dtype=jnp.int32)
    tick_valid = jnp.where(first_section, tick_index >= 1, tick_index < micro_count).astype(
        jnp.float32
    )

    def backward_tick(carry, step_item):
        received, totals = carry
        layer_input, cotangent, valid_now, stash_now = step_item
        grad_now = jnp.where(first_section, received.astype(jnp.float32), cotangent)
        input_now = layer_input.astype(jnp.float32)
        kept_values = layer_forward(input_now, weights)[1]
        grad_input, layer_grads = layer_backward(input_now, grad_now, kept_values, weights)
        totals = jax.tree.map(lambda total, update: total + valid_now * update, totals, layer_grads)
        grad_low = grad_input.astype(jnp.bfloat16)
        outgoing = shifted(grad_low, "section", -1)
        return ((outgoing, totals), grad_low)

    start_totals = (
        jnp.zeros((4, model_width), jnp.float32),
        jnp.zeros(qkv_weight.shape[1:], jnp.float32),
        jnp.zeros(out_weight.shape[1:], jnp.float32),
        jnp.zeros(up_weight.shape[1:], jnp.float32),
        jnp.zeros(down_weight.shape[1:], jnp.float32),
    )
    (_, totals), grad_lows = lax.scan(
        backward_tick,
        (start_rows, start_totals),
        (back_inputs, grad_padded, tick_valid, back_stash),
    )
    input_grads = jnp.where(first_section, grad_lows[1:], grad_lows[:-1])[None]
    gain_total, qkv_total, out_total, up_total, down_total = totals
    gains_grad = lax.psum_scatter(gain_total, ("dp", "tensor"), scatter_dimension=1, tiled=True)
    qkv_grad, out_grad, up_grad, down_grad = (
        lax.psum_scatter(
            qkv_total.astype(jnp.bfloat16), "dp", scatter_dimension=0, tiled=True
        ).astype(jnp.float32),
        lax.psum_scatter(
            out_total.astype(jnp.bfloat16), "dp", scatter_dimension=1, tiled=True
        ).astype(jnp.float32),
        lax.psum_scatter(
            up_total.astype(jnp.bfloat16), "dp", scatter_dimension=0, tiled=True
        ).astype(jnp.float32),
        lax.psum_scatter(
            down_total.astype(jnp.bfloat16), "dp", scatter_dimension=1, tiled=True
        ).astype(jnp.float32),
    )
    return (
        layer_outputs,
        input_grads,
        gains_grad[None],
        qkv_grad[None],
        out_grad[None],
        up_grad[None],
        down_grad[None],
    )


def rotated(block, cos_rows, sin_rows):
    lane = lax.broadcasted_iota(jnp.int32, block.shape, 1)
    ahead = pltpu.roll(block, 96, 1)
    behind = pltpu.roll(block, 32, 1)
    swapped = jnp.where(lane % 64 < 32, ahead, behind)
    return block * cos_rows + swapped * sin_rows


def dot_nt(left, right):
    return lax.dot_general(
        left, right, (((1,), (1,)), ((), ())), preferred_element_type=jnp.float32
    )


def dot_nn(left, right):
    return jnp.dot(left, right, preferred_element_type=jnp.float32)


def model_weight(owns, others, cols):
    sides = [jnp.concatenate([ref[:, cols] for ref in refs], axis=1) for refs in (owns, others)]
    return jnp.concatenate(sides, axis=0)


def stacked_up(values):
    return jnp.concatenate(values, axis=0)


def edge_masks(core, rows):
    key = lax.broadcasted_iota(jnp.int32, (rows, 2 * rows), 0)
    query = lax.broadcasted_iota(jnp.int32, (rows, 2 * rows), 1)
    mine = query < rows
    place = jnp.where(mine, query + core * rows, query - rows + (1 - core) * rows)
    return (key + core * rows <= place, key + (1 - core) * rows <= place)


def both_sides(value, half, start, stop, axis=0):
    if axis == 0:
        return jnp.concatenate([value[start:stop], value[half + start : half + stop]], axis=0)
    return jnp.concatenate([value[:, start:stop], value[:, half + start : half + stop]], axis=1)


def hidden_scores(scores, masks, tile, step):
    seen = step * tile
    pieces = []
    for side in range(2):
        base = side * (seen + tile)
        if seen:
            pieces.append(scores[base : base + seen])
        pieces.append(jnp.where(masks[side], scores[base + seen : base + seen + tile], -1e30))
    return jnp.concatenate(pieces, axis=0)


def one_head(rows, head):
    lane = lax.broadcasted_iota(jnp.int32, rows.shape, 1)
    return jnp.where(lane // 64 == head, rows, jnp.zeros_like(rows))


def pick_piece(weight, owns, others, cols):
    for j, (own, other) in enumerate(zip(owns, others)):

        @pl.when(pl.program_id(0) == j)
        def _():
            size = own.shape[0]
            weight[:size] = own[:, cols]
            weight[size:] = other[:, cols]


def attend_kernel(pieces, core_ref, cos_ref, sin_ref, own_rows, other_rows, *refs):
    owns, others = refs[:pieces], refs[pieces : 2 * pieces]
    q_ref, k_ref, v_ref, lse_ref, mix_ref, weight = refs[2 * pieces :]
    half = own_rows.shape[0]
    tile = TILE
    pick_piece(weight, owns, others, QKV)
    proj = dot_nn(stacked_up([own_rows[...], other_rows[...]]), weight[...])
    cos_rows, sin_rows = cos_ref[...], sin_ref[...]
    q = (rotated(proj[:, :128], cos_rows, sin_rows) * HEAD_DIM ** (-0.5)).astype(jnp.bfloat16)
    k = rotated(proj[:, 128:256], cos_rows, sin_rows).astype(jnp.bfloat16)
    v32 = proj[:, 256:]
    q_ref[0] = q
    k_ref[0] = k
    v_ref[0] = v32.astype(jnp.bfloat16)
    v_flip = v32.T.astype(jnp.bfloat16)
    masks = edge_masks(core_ref[0], tile)

    def scored(step, head):
        stop = (step + 1) * tile
        q_head = one_head(both_sides(q, half, step * tile, stop), head)
        return hidden_scores(dot_nt(both_sides(k, half, 0, stop), q_head), masks, tile, step)

    units = [(step, head) for step in range(half // tile) for head in range(2)]
    ahead = scored(*units[0])
    outs = []
    for spot, (step, head) in enumerate(units):
        scores = ahead
        if spot + 1 < len(units):
            ahead = scored(*units[spot + 1])
        stop = (step + 1) * tile
        top = jnp.max(scores, axis=0, keepdims=True)
        expos = jnp.exp(scores - top)
        total = jnp.sum(expos, axis=0, keepdims=True)
        lse = top + jnp.log(total)
        lse_ref[0, head : head + 1, step * tile : stop] = lse[:, :tile]
        lse_ref[0, head : head + 1, half + step * tile : half + stop] = lse[:, tile:]
        v_cols = both_sides(v_flip, half, 0, stop, axis=1)
        out = dot_nn(v_cols[64 * head : 64 * head + 64], expos.astype(jnp.bfloat16))
        outs.append(out * (1.0 / total))
        if head == 1:
            mixed = jnp.concatenate(outs, axis=0).T.astype(jnp.bfloat16)
            outs = []
            mix_ref[step * tile : stop, :] = mixed[:tile]
            mix_ref[half + step * tile : half + stop, :] = mixed[tile:]


def attend_back_kernel(pieces, core_ref, cos_ref, sin_ref, own_rows, other_rows, *refs):
    owns, others = refs[:pieces], refs[pieces : 2 * pieces]
    q_ref, k_ref, v_ref, lse_ref, out_ref, weight, dq, dk, dv = refs[2 * pieces :]
    half = own_rows.shape[0]
    tile = TILE
    pick_piece(weight, owns, others, OUT)
    rows = stacked_up([own_rows[...], other_rows[...]])
    d_mixed = dot_nn(rows, weight[...]).astype(jnp.bfloat16)
    q, k, v = q_ref[0], k_ref[0], v_ref[0]
    k_flip = k.astype(jnp.float32).T.astype(jnp.bfloat16)
    masks = edge_masks(core_ref[0], tile)
    steps = half // tile

    def scored(step, head):
        stop = (step + 1) * tile
        q_head = one_head(both_sides(q, half, step * tile, stop), head)
        g_head = one_head(both_sides(d_mixed, half, step * tile, stop), head)
        scores = hidden_scores(dot_nt(both_sides(k, half, 0, stop), q_head), masks, tile, step)
        return q_head, g_head, scores, dot_nt(both_sides(v, half, 0, stop), g_head)

    units = [(step, head) for step in reversed(range(steps)) for head in range(2)]
    ahead = scored(*units[0])
    dq_flips = []
    dk_sum = dv_sum = None
    for spot, (step, head) in enumerate(units):
        q_head, g_head, scores, d_probs = ahead
        if spot + 1 < len(units):
            ahead = scored(*units[spot + 1])
        stop = (step + 1) * tile
        lse = both_sides(lse_ref[0], half, step * tile, stop, axis=1)
        probs = jnp.exp(scores - lse[head : head + 1])
        dots = jnp.sum(probs * d_probs, axis=0, keepdims=True)
        d_scores = (probs * (d_probs - dots)).astype(jnp.bfloat16)
        dv_part = dot_nn(probs.astype(jnp.bfloat16), g_head)
        dk_part = dot_nn(d_scores, q_head)
        k_cols = both_sides(k_flip, half, 0, stop, axis=1)
        dq_flips.append(dot_nn(k_cols[64 * head : 64 * head + 64], d_scores))
        if head == 0:
            dv_sum, dk_sum = dv_part, dk_part
            continue
        dv_sum, dk_sum = dv_sum + dv_part, dk_sum + dk_part
        dq_rows = jnp.concatenate(dq_flips, axis=0).T * HEAD_DIM ** (-0.5)
        dq_flips = []
        dq[step * tile : stop] = dq_rows[:tile]
        dq[half + step * tile : half + stop] = dq_rows[tile:]
        for base, part in ((0, slice(0, stop)), (half, slice(stop, 2 * stop))):
            if step == steps - 1:
                dk[base : base + stop] = dk_sum[part]
                dv[base : base + stop] = dv_sum[part]
            else:
                dk[base : base + stop] += dk_sum[part]
                dv[base : base + stop] += dv_sum[part]
    cos_rows, sin_rows = cos_ref[...], -sin_ref[...]
    out_ref[:, :128] = rotated(dq[...], cos_rows, sin_rows).astype(jnp.bfloat16)
    out_ref[:, 128:256] = rotated(dk[...], cos_rows, sin_rows).astype(jnp.bfloat16)
    out_ref[:, 256:] = dv[...].astype(jnp.bfloat16)


def split_rows(total, own_ref, other_ref):
    half = own_ref.shape[0]
    own_ref[...] = total[:half]
    other_ref[...] = total[half:].astype(jnp.bfloat16)


def to_model_kernel(lefts, pieces, cols, *refs):
    left, refs = jnp.concatenate([ref[...] for ref in refs[:lefts]], axis=1), refs[lefts:]
    weight = model_weight(refs[:pieces], refs[pieces : 2 * pieces], cols)
    split_rows(dot_nt(left, weight), *refs[2 * pieces :])


def mlp_down_kernel(pieces, left_ref, *refs):
    sides = [stacked_up([ref[...] for ref in side]) for side in (refs[:pieces], refs[pieces:-2])]
    split_rows(dot_nn(left_ref[...], jnp.concatenate(sides, axis=1)), *refs[-2:])


def gelu_both(up_act):
    root = math.sqrt(2.0 / math.pi)
    square = up_act * up_act
    rise = 0.5 + 0.5 * jnp.tanh(up_act * (root + root * 0.044715 * square))
    value = up_act * rise
    slope = rise + value * (1.0 - rise) * (2.0 * root + 6.0 * root * 0.044715 * square)
    return value, slope


def mlp_up_kernel(pieces, own_rows, other_rows, *refs):
    owns, others = refs[:pieces], refs[pieces : 2 * pieces]
    gelu_ref, slope_ref = refs[2 * pieces :]
    half = own_rows.shape[0]
    size = owns[0].shape[1]
    step = half // 2
    units = [(j, i) for j in range(pieces) for i in range(4)]

    def product(j, i):
        rows = (own_rows, other_rows)[i // 2][i % 2 * step : (i % 2 + 1) * step]
        return dot_nn(rows, stacked_up([owns[j][...], others[j][...]]))

    ahead = product(*units[0])
    for spot, (j, i) in enumerate(units):
        up_act = ahead
        if spot + 1 < len(units):
            ahead = product(*units[spot + 1])
        value, slope = gelu_both(up_act)
        gelu_ref[i * step : (i + 1) * step, j * size : (j + 1) * size] = value.astype(jnp.bfloat16)
        slope_ref[i * step : (i + 1) * step, j * size : (j + 1) * size] = slope.astype(
            jnp.bfloat16
        )


def mlp_up_back_kernel(pieces, own_rows, other_rows, slope_ref, *refs):
    owns, others = refs[:pieces], refs[pieces : 2 * pieces]
    out_ref, weight, slope, sems = refs[2 * pieces :]
    half = own_rows.shape[1] // 2
    size = owns[0].shape[0]
    order = list(reversed(range(pieces)))
    copies = []
    for j in order:
        sources = (owns[j], others[j], slope_ref.at[:, pl.ds(j * size, size)])
        targets = (
            weight.at[j, :, pl.ds(0, half)],
            weight.at[j, :, pl.ds(half, half)],
            slope.at[:, pl.ds(j * size, size)],
        )
        copies.append(
            [
                pltpu.make_async_copy(source, target, sems.at[j, i])
                for i, (source, target) in enumerate(zip(sources, targets))
            ]
        )
        for copy in copies[-1]:
            copy.start()
    rows = stacked_up([own_rows[...], other_rows[...]])
    for j, arriving in zip(order, copies):
        cols = slice(j * size, (j + 1) * size)
        for copy in arriving:
            copy.wait()
        d_gelu = dot_nt(rows, weight[j])
        out_ref[:, cols] = (d_gelu * slope[:, cols].astype(jnp.float32)).astype(jnp.bfloat16)


def inverse_size(rows):
    return lax.rsqrt(jnp.mean(rows * rows, axis=-1, keepdims=True) + NORM_EPSILON)


def norm_back(rows, gain, grad):
    scale = inverse_size(rows)
    weighted = grad * gain
    inner = jnp.mean(rows * weighted, axis=-1, keepdims=True)
    return scale * weighted - rows * (scale * scale * scale * inner), rows * scale * grad


def folded(rows):
    return jnp.sum(rows.reshape(rows.shape[0] // 8, 8, rows.shape[1]), axis=0)


def wide(ref, spot):
    return ref[spot, :].astype(jnp.float32)


def by_chunks(count, body, sums=0, width=0):
    def one(i, carry):
        more = body(pl.ds(pl.multiple_of(i * CHUNK, CHUNK), CHUNK))
        return tuple(old + folded(new) for old, new in zip(carry, more))

    start = tuple(jnp.zeros((8, width), jnp.float32) for _ in range(sums))
    totals = lax.fori_loop(0, count // CHUNK, one, start)
    return [jnp.sum(total, axis=0, keepdims=True) for total in totals]


def norm_in_kernel(gain_ref, rows_ref, out_ref):
    def body(spot):
        rows = wide(rows_ref, spot)
        out_ref[spot, :] = (rows * inverse_size(rows) * gain_ref[0:1]).astype(jnp.bfloat16)
        return ()

    by_chunks(rows_ref.shape[0], body)


def after_attention_kernel(
    gain_ref, rows_ref, own_ref, other_ref, branch_ref, hidden_ref, out_ref
):
    def body(spot):
        branch = own_ref[spot, :] + wide(other_ref, spot)
        hidden = wide(rows_ref, spot) + branch * inverse_size(branch) * gain_ref[1:2]
        branch_ref[spot, :] = branch
        hidden_ref[spot, :] = hidden
        out_ref[spot, :] = (hidden * inverse_size(hidden) * gain_ref[2:3]).astype(jnp.bfloat16)
        return ()

    by_chunks(rows_ref.shape[0], body)


def after_mlp_kernel(gain_ref, hidden_ref, own_ref, other_ref, branch_ref, out_ref):
    def body(spot):
        branch = own_ref[spot, :] + wide(other_ref, spot)
        branch_ref[spot, :] = branch
        result = hidden_ref[spot, :] + branch * inverse_size(branch) * gain_ref[3:4]
        out_ref[spot, :] = result.astype(jnp.bfloat16)
        return ()

    by_chunks(hidden_ref.shape[0], body)


def into_mlp_back_kernel(gain_ref, grad_ref, branch_ref, out_ref, sum_ref):
    def body(spot):
        d_rows, d_gain = norm_back(branch_ref[spot, :], gain_ref[3:4], wide(grad_ref, spot))
        out_ref[spot, :] = d_rows.astype(jnp.bfloat16)
        return (d_gain,)

    (sum_ref[...],) = by_chunks(grad_ref.shape[0], body, 1, grad_ref.shape[1])


def into_attention_back_kernel(
    gain_ref, grad_ref, own_ref, other_ref, hidden_ref, branch_ref, d_hidden_ref, out_ref, *sums
):
    def body(spot):
        d_rows = own_ref[spot, :] + wide(other_ref, spot)
        d_rows, d_gain = norm_back(hidden_ref[spot, :], gain_ref[2:3], d_rows)
        d_hidden = wide(grad_ref, spot) + d_rows
        d_hidden_ref[spot, :] = d_hidden
        d_rows, d_first = norm_back(branch_ref[spot, :], gain_ref[1:2], d_hidden)
        out_ref[spot, :] = d_rows.astype(jnp.bfloat16)
        return (d_first, d_gain)

    totals = by_chunks(grad_ref.shape[0], body, 2, grad_ref.shape[1])
    sums[0][...], sums[1][...] = totals


def out_of_layer_kernel(gain_ref, rows_ref, own_ref, other_ref, d_hidden_ref, out_ref, sum_ref):
    def body(spot):
        d_rows = own_ref[spot, :] + wide(other_ref, spot)
        d_rows, d_gain = norm_back(wide(rows_ref, spot), gain_ref[0:1], d_rows)
        out_ref[spot, :] = (d_hidden_ref[spot, :] + d_rows).astype(jnp.bfloat16)
        return (d_gain,)

    (sum_ref[...],) = by_chunks(rows_ref.shape[0], body, 1, rows_ref.shape[1])


def work(flops, arrays):
    size = sum(math.prod(array.shape) * jnp.dtype(array.dtype).itemsize for array in arrays)
    return pl.CostEstimate(flops=flops, bytes_accessed=size, transcendentals=0)


def far(array):
    return pltpu.with_memory_space_constraint(array, pltpu.HBM)


def without(kernel, first, count):
    return lambda *refs: kernel(*refs[:first], *refs[first + count :])


def on_chip(kernel, name, outs, *operands, limit=ROWS_VMEM, flops=0, waits=()):
    shapes = [jax.ShapeDtypeStruct(shape, dtype) for shape, dtype in outs]
    space = pl.BlockSpec(memory_space=pltpu.VMEM)
    return pl.pallas_call(
        without(kernel, len(operands), len(waits)),
        in_specs=[space] * len(operands) + [pl.BlockSpec(memory_space=pl.ANY)] * len(waits),
        out_specs=[space] * len(outs),
        out_shape=shapes,
        compiler_params=pltpu.CompilerParams(vmem_limit_bytes=limit),
        cost_estimate=work(flops, (*operands, *shapes)),
        name=name,
    )(*operands, *map(far, waits))


def whole_block(array):
    return pl.BlockSpec(array.shape, lambda j: (0,) * array.ndim)


def by_pairs(kernel, name, core, operands, pieces, blocks, outs, scratch, flops, waits):
    shapes = [jax.ShapeDtypeStruct(shape, dtype) for shape, dtype, _ in outs]
    taken = 1 + len(operands) + 2 * len(pieces[0]) + len(blocks)
    return pl.pallas_call(
        without(functools.partial(kernel, len(pieces[0])), taken, len(waits)),
        grid=(len(pieces[0]),),
        in_specs=[pl.BlockSpec(memory_space=pltpu.SMEM)]
        + [whole_block(array) for array in (*operands, *pieces[0], *pieces[1])]
        + [spec for _, spec in blocks]
        + [pl.BlockSpec(memory_space=pl.ANY)] * len(waits),
        out_specs=[spec for _, _, spec in outs],
        out_shape=shapes,
        scratch_shapes=scratch,
        compiler_params=pltpu.CompilerParams(vmem_limit_bytes=KERNEL_VMEM),
        cost_estimate=work(flops, (*operands, *pieces[0], *pieces[1], *shapes)),
        name=name,
    )(core, *operands, *pieces[0], *pieces[1], *[array for array, _ in blocks], *map(far, waits))


def mlp_up_back(rows, slope, pieces, waits):
    length, units = slope.shape
    unit, half = pieces[0][0].shape
    count = len(pieces[0])
    every, space = pl.BlockSpec(memory_space=pl.ANY), pl.BlockSpec(memory_space=pltpu.VMEM)
    return pl.pallas_call(
        without(functools.partial(mlp_up_back_kernel, count), 3 + 2 * count, len(waits)),
        in_specs=[space] * 2 + [every] * (1 + 2 * count + len(waits)),
        out_specs=space,
        out_shape=jax.ShapeDtypeStruct((length, units), jnp.bfloat16),
        scratch_shapes=[
            pltpu.VMEM((count, unit, 2 * half), jnp.bfloat16),
            pltpu.VMEM((length, units), jnp.bfloat16),
            pltpu.SemaphoreType.DMA((count, 3)),
        ],
        compiler_params=pltpu.CompilerParams(vmem_limit_bytes=KERNEL_VMEM),
        name="mlp_up_back",
    )(*rows, *map(far, (slope, *pieces[0], *pieces[1], *waits)))


def attend(core, tables, rows, pieces, waits):
    half, features = rows[0].shape
    length, count = 2 * half, len(pieces[0])
    lanes = ((count, length, 128), jnp.bfloat16, pl.BlockSpec((1, length, 128), lambda j: (j, 0, 0)))
    lse = ((count, 2, length), jnp.float32, pl.BlockSpec((1, 2, length), lambda j: (j, 0, 0)))
    mixed = ((length, count * 128), jnp.bfloat16, pl.BlockSpec((length, 128), lambda j: (0, j)))
    return by_pairs(
        attend_kernel,
        "attend",
        core,
        (*tables, *rows),
        pieces,
        (),
        (lanes, lanes, lanes, lse, mixed),
        [pltpu.VMEM((features, 384), jnp.bfloat16)],
        count * length * (2 * features * 384 + 2 * PAIR_WORK * length),
        waits,
    )


def attend_back(core, tables, rows, pieces, base, waits, q, k, v, lse):
    half, features = rows[0].shape
    length, count = 2 * half, len(pieces[0])
    lanes = pl.BlockSpec((1, length, 128), lambda j: (base + j, 0, 0))
    lse_spec = pl.BlockSpec((1, 2, length), lambda j: (base + j, 0, 0))
    out = ((length, count * 384), jnp.bfloat16, pl.BlockSpec((length, 384), lambda j: (0, j)))
    return by_pairs(
        attend_back_kernel,
        "attend_back",
        core,
        (*tables, *rows),
        pieces,
        ((q, lanes), (k, lanes), (v, lanes), (lse, lse_spec)),
        (out,),
        [pltpu.VMEM((features, 128), jnp.bfloat16)] + [pltpu.VMEM((length, 128), jnp.float32)] * 3,
        count * length * (2 * features * 128 + 5 * PAIR_WORK * length),
        waits,
    )[0]


def exchanged(parts):
    return parts[0], flip_pairs(parts[1], 1)


def model_rows(kernel, name, lefts, pieces, waits=()):
    length, width = lefts[0].shape[0], 2 * MODEL_HALF
    outs = (((length // 2, width), jnp.float32), ((length // 2, width), jnp.bfloat16))
    hidden = sum(left.shape[1] for left in lefts)
    more = {"limit": KERNEL_VMEM, "flops": 2 * length * width * hidden, "waits": waits}
    return exchanged(on_chip(kernel, name, outs, *lefts, *pieces[0], *pieces[1], **more))


def flip_pairs(block, distance):
    size = lax.axis_size("dp")
    return lax.ppermute(block, "dp", [(i, i ^ distance) for i in range(size)])


def passed_on(block, step):
    size = lax.axis_size("tensor")
    return lax.ppermute(block, "tensor", [(i, (i + step) % size) for i in range(size)])


def dot_tn(left, right):
    return lax.dot_general(
        left, right, (((0,), (0,)), ((), ())), preferred_element_type=jnp.float32
    )


def fetch(first_ref, zeros, ones, buffers, sems):
    for section, sources in enumerate((zeros, ones)):

        @pl.when(first_ref[0] == section)
        def _():
            for i, (source, buffer) in enumerate(zip(sources, buffers)):
                pltpu.make_async_copy(source, buffer, sems.at[i]).start()

    def arrived(*places):
        for i in places:
            pltpu.make_async_copy(zeros[i], buffers[i], sems.at[i]).wait()

    return arrived


def mlp_grads_kernel(base, section_ref, *refs):
    (own_one, other_one, own_two, other_two), (rows, d_up, gelu, d_down, sems) = refs[12:16], refs[16:]
    half, size = own_one.shape[0] // 2, own_one.shape[1]
    cols = pl.ds(base * size, 2 * size)

    def parts(own_rows, other_rows, d_up_ref, gelu_ref, own_grad, other_grad):
        whole = (d_up_ref.at[:, cols], gelu_ref.at[:, cols])
        return (own_rows, other_rows, *whole, own_grad, other_grad)

    count = refs[0].shape[0]
    buffers = (
        rows.at[pl.ds(0, count)],
        rows.at[pl.ds(count, count)],
        d_up,
        gelu,
        d_down.at[pl.ds(0, count)],
        d_down.at[pl.ds(count, count)],
    )
    arrived = fetch(section_ref, parts(*refs[:6]), parts(*refs[6:12]), buffers, sems)
    for j, own, other in ((1, own_two, other_two), (0, own_one, other_one)):
        cols = slice(j * size, (j + 1) * size)
        if j == 1:
            arrived(0, 1, 2)
        up = dot_tn(rows[...], d_up[:, cols])
        own[:half] = up[:half]
        other[:half] = up[half:].astype(jnp.bfloat16)
        if j == 1:
            arrived(3, 4, 5)
        down = dot_tn(gelu[:, cols], d_down[...])
        own[half:] = down[:, :half]
        other[half:] = down[:, half:].astype(jnp.bfloat16)


def attn_grads_kernel(base, section_ref, *refs):
    (own_one, other_one, own_two, other_two), (rows, d_qkv, mixed, d_attn, sems) = refs[12:16], refs[16:]
    half, size = own_one.shape[0], d_qkv.shape[1] // 2
    count = refs[0].shape[0]
    cols = pl.ds(base * 128, 256)

    def parts(own_rows, other_rows, d_qkv_ref, mixed_ref, own_grad, other_grad):
        return (own_rows, other_rows, d_qkv_ref, mixed_ref.at[:, cols], own_grad, other_grad)

    buffers = (
        rows.at[pl.ds(0, count)],
        rows.at[pl.ds(count, count)],
        d_qkv,
        mixed,
        d_attn.at[pl.ds(0, count)],
        d_attn.at[pl.ds(count, count)],
    )
    arrived = fetch(section_ref, parts(*refs[:6]), parts(*refs[6:12]), buffers, sems)
    for j, own, other in ((1, own_two, other_two), (0, own_one, other_one)):
        if j == 1:
            arrived(0, 1, 2)
        qkv = dot_tn(rows[...], d_qkv[:, j * size : (j + 1) * size])
        if j == 1:
            arrived(3, 4, 5)
        out = dot_tn(d_attn[...], mixed[:, j * 128 : (j + 1) * 128])
        own[:, :size] = qkv[:half]
        own[:, size:] = out[:half]
        other[:, :size] = qkv[half:].astype(jnp.bfloat16)
        other[:, size:] = out[half:].astype(jnp.bfloat16)


def weight_grads(kernel, name, base, section, zeros, ones, shape, columns, waits=()):
    length = 2 * zeros[0].shape[0]
    width = zeros[0].shape[1]
    every = pl.BlockSpec(memory_space=pl.ANY)
    space = pl.BlockSpec(memory_space=pltpu.VMEM)
    arrays = (*zeros, *ones)
    first, second, third, fourth = pl.pallas_call(
        without(functools.partial(kernel, base), 1 + len(arrays), len(waits)),
        in_specs=[pl.BlockSpec(memory_space=pltpu.SMEM)] + [every] * (len(arrays) + len(waits)),
        out_specs=[space] * 4,
        out_shape=[
            jax.ShapeDtypeStruct(shape, jnp.float32),
            jax.ShapeDtypeStruct(shape, jnp.bfloat16),
        ]
        * 2,
        scratch_shapes=[
            pltpu.VMEM((length, width), jnp.bfloat16),
            pltpu.VMEM((length, columns[0]), jnp.bfloat16),
            pltpu.VMEM((length, columns[1]), jnp.bfloat16),
            pltpu.VMEM((length, width), jnp.bfloat16),
            pltpu.SemaphoreType.DMA((6,)),
        ],
        compiler_params=pltpu.CompilerParams(vmem_limit_bytes=KERNEL_VMEM),
        name=name,
    )(section, *map(far, (*arrays, *waits)))
    return [(first, flip_pairs(second, 2)), (third, flip_pairs(fourth, 2))]


def moved_kernel(own_ref, other_ref, *refs):
    out_ref = refs[-1]

    def body(i, carry):
        spot = pl.ds(pl.multiple_of(i * CHUNK, CHUNK), CHUNK)
        total = own_ref[spot, :]
        for ref in (other_ref, *refs[:-1]):
            total = total + wide(ref, spot)
        out_ref[spot, :] = total.astype(jnp.bfloat16)
        return carry

    lax.fori_loop(0, own_ref.shape[0] // CHUNK, body, 0)


def gates_kernel(up_ref, down_ref, up_out, down_out):
    up_out[...] = up_ref[...]
    down_out[...] = down_ref[...]


def gate_kernel(piece_ref, out_ref):
    out_ref[...] = piece_ref[...]


def mlp_sum_kernel(core_ref, own_ref, other_ref, moved_ref, up_keep, down_keep, up_send, down_send):
    half = own_ref.shape[0] // 2
    size = up_keep.shape[0]

    def total(rows, cols):
        more = other_ref[rows, cols].astype(jnp.float32) + moved_ref[rows, cols].astype(jnp.float32)
        return own_ref[rows, cols] + more

    for core in range(2):

        @pl.when(core_ref[0] == core)
        def _():
            for place, up, down in ((core, up_keep, down_keep), (1 - core, up_send, down_send)):
                spot = slice(place * size, (place + 1) * size)
                up[...] = total(spot, slice(None))
                down[...] = total(slice(half, None), spot)


def mlp_join_kernel(core_ref, up_keep, down_keep, up_sent, down_sent, up_out, down_out):
    size = up_keep.shape[1]
    for core in range(2):

        @pl.when(core_ref[0] == core)
        def _():
            places = ((core, up_keep, down_keep), (1 - core, up_sent, down_sent))
            for place, up, down in places:
                spot = slice(place * size, (place + 1) * size)
                up_out[:, spot] = up[...]
                down_out[spot] = down[...]


def chosen_kernel(place_ref, zero_ref, one_ref, out_ref):
    half = out_ref.shape[1] // 2
    for section, rows_ref in enumerate((zero_ref, one_ref)):
        for upper in range(2):

            @pl.when(jnp.logical_and(place_ref[0] == section, place_ref[1] == upper))
            def _():
                for side in range(2):
                    place = (side + upper) % 2 * half
                    out_ref[:, place : place + half] = rows_ref[:, side * half : (side + 1) * half]


def pick_kernel(core_ref, rows_ref, keep_ref, send_ref):
    count = keep_ref.shape[0]
    keep_ref[...] = rows_ref[pl.ds(core_ref[0] * count, count)]
    send_ref[...] = rows_ref[pl.ds((1 - core_ref[0]) * count, count)]


def in_order_kernel(core_ref, keep_ref, sent_ref, out_ref):
    out_ref[:, pl.ds(core_ref[0], 1)] = keep_ref[...][:, None]
    out_ref[:, pl.ds(1 - core_ref[0], 1)] = sent_ref[...][:, None]


def with_core(kernel, name, core, outs, *operands, waits=()):
    space = pl.BlockSpec(memory_space=pltpu.VMEM)
    return pl.pallas_call(
        without(kernel, 1 + len(operands), len(waits)),
        in_specs=[pl.BlockSpec(memory_space=pltpu.SMEM)]
        + [space] * len(operands)
        + [pl.BlockSpec(memory_space=pl.ANY)] * len(waits),
        out_specs=[space] * len(outs),
        out_shape=[jax.ShapeDtypeStruct(shape, dtype) for shape, dtype in outs],
        compiler_params=pltpu.CompilerParams(vmem_limit_bytes=ROWS_VMEM),
        name=name,
    )(core, *operands, *map(far, waits))


def last_sum_kernel(core_ref, own_ref, other_ref, moved_ref, keep_ref, send_ref):
    rows = keep_ref.shape[0]

    def total(block):
        spot = pl.ds(pl.multiple_of(block * rows, rows), rows)
        return own_ref[spot, :] + wide(other_ref, spot) + wide(moved_ref, spot)

    keep_ref[...] = total(core_ref[0])
    send_ref[...] = total(1 - core_ref[0])


def joined_kernel(spots, core_ref, keep_ref, sent_ref, column_ref, row_ref):
    size = row_ref.shape[0] // 2
    for core in range(2):

        @pl.when(core_ref[0] == core)
        def _():
            for place, source in ((core, keep_ref), (1 - core, sent_ref)):
                for start, stop, to in spots:
                    step = stop - start
                    column_ref[:, to + place * step : to + (place + 1) * step] = source[:, start:stop]
                row_ref[place * size : (place + 1) * size] = source[:, spots[-1][1] :].T


def per_chip(
    inputs,
    out_cotangent,
    group_ids,
    group_weights,
    gains,
    qkv_weight,
    out_weight,
    up_weight,
    down_weight,
):
    micro, row_count, width = inputs.shape
    tensor = lax.axis_size("tensor")
    part = row_count // 2
    wide_half = width // 2
    length = tensor * row_count
    half = length // 2
    first = lax.axis_index("section") == 0
    place = lax.axis_index("dp")
    core = place % 2
    upper = place // 2 % 2
    core_zero = core == 0
    low_half = upper == 0

    def ordered(mine, other):
        return jnp.where(core_zero, mine, other), jnp.where(core_zero, other, mine)

    def own_first(values):
        return jnp.where(low_half, values, jnp.roll(values, wide_half, axis=-1))

    def both_rows(own):
        return own, flip_pairs(own, 1)

    def to_chip(block):
        split = block.reshape((micro, 2, part) + block.shape[2:])
        mine = lax.dynamic_index_in_dim(split, core, 1, keepdims=False)
        other = lax.dynamic_index_in_dim(split, 1 - core, 1, keepdims=False)
        return lax.all_to_all(
            jnp.concatenate(ordered(mine, flip_pairs(other, 1))), "tensor", 0, 0, tiled=True
        )

    def from_chip(spread_out, waits=()):
        piece = ((micro, part, width), jnp.bfloat16)
        keep, send = with_core(
            pick_kernel, "pick", core_word, (piece, piece), spread_out, waits=waits
        )
        outs = (((micro, 2, part, width), jnp.bfloat16),)
        (rows,) = with_core(
            in_order_kernel, "in_order", core_word, outs, keep, flip_pairs(send, 1)
        )
        return rows.reshape(micro, row_count, width)

    def columns(local):
        size = local.shape[-1] // 2
        mid = (0,) * (local.ndim - 2)
        piece = lax.dynamic_slice(
            local,
            (wide_half * upper, *mid, size * core),
            (wide_half, *local.shape[1:-1], size),
        )
        return piece.reshape(wide_half, -1)

    def rows(local):
        size = local.shape[0] // 2
        return lax.dynamic_slice(local, (size * core, wide_half * upper), (size, wide_half))

    core_word = core.astype(jnp.int32).reshape(1)
    attn_piece = jnp.concatenate([columns(qkv_weight[0]), rows(out_weight[0]).T], axis=1)

    def spread(piece):
        pieces = [piece]
        for _ in range(tensor - 1):
            pieces.append(passed_on(pieces[-1], 1))
        return pieces

    up_piece, down_piece = columns(up_weight[0]), rows(down_weight[0])
    up_other, down_other = [flip_pairs(up_piece, 2)], [flip_pairs(down_piece, 2)]
    attn_own = [attn_piece, passed_on(attn_piece, 1)]
    attn_first = flip_pairs(attn_piece, 2)
    outs = ((attn_piece.shape, attn_piece.dtype),)
    attn_own[1] = on_chip(gate_kernel, "gate", outs, attn_own[1], waits=(attn_first, up_other[0]))[0]
    attn_own += spread(attn_own[1])[1:-1]
    attn_other = [attn_first] + [flip_pairs(piece, 2) for piece in attn_own[1:]]
    outs = tuple((piece.shape, piece.dtype) for piece in (up_piece, down_piece))
    up_piece, down_piece = on_chip(
        gates_kernel, "gate", outs, up_piece, down_piece, waits=(attn_own[2], attn_other[0], down_other[0])
    )
    up_own, down_own = spread(up_piece), spread(down_piece)
    up_other += [flip_pairs(piece, 2) for piece in up_own[1:]]
    down_other += [flip_pairs(piece, 2) for piece in down_own[1:]]
    w_attn, w_up, w_down = (attn_own, attn_other), (up_own, up_other), (down_own, down_other)
    unit = up_piece.shape[1]
    units = tensor * unit

    group_count = group_weights.shape[0]
    matches = group_ids[..., None] == jnp.arange(group_count, dtype=jnp.int32)
    row_scale = jnp.sum(jnp.where(matches, group_weights, 0.0), axis=-1)
    weighted = (out_cotangent.astype(jnp.float32) * row_scale[..., None]).astype(jnp.bfloat16)
    start = to_chip(own_first(jnp.where(first, inputs, weighted))).reshape(half, width)
    gain = own_first(gains[0])

    turns = jnp.arange(half, dtype=jnp.int32)
    turns = turns // part * row_count + turns % part
    positions = jnp.concatenate([turns + core * part, turns + (1 - core) * part])
    freqs = 10000.0 ** (-2.0 * jnp.arange(HEAD_DIM // 2, dtype=jnp.float32) / HEAD_DIM)
    angles = positions.astype(jnp.float32)[:, None] * freqs[None, :]
    cos_part, sin_part = jnp.cos(angles), jnp.sin(angles)
    tables = (
        jnp.concatenate([cos_part] * 4, axis=1),
        jnp.concatenate([-sin_part, sin_part] * 2, axis=1),
    )
    row32, row16 = ((half, width), jnp.float32), ((half, width), jnp.bfloat16)
    unit16 = ((length, units), jnp.bfloat16)
    sum32 = ((1, width), jnp.float32)
    mlp_cost = {"limit": KERNEL_VMEM, "flops": 2 * length * width * units}
    every = slice(None)

    def model_kernel(cols, lefts=1):
        return functools.partial(to_model_kernel, lefts, tensor, cols)

    down_kernel = functools.partial(mlp_down_kernel, tensor)

    def forward(layer_input, waits):
        attn_in = both_rows(
            on_chip(norm_in_kernel, "norm_in", (row16,), gain, layer_input, waits=waits[0])[0]
        )
        *heads, mixed = attend(core_word, tables, attn_in, w_attn, waits[1])
        parts = model_rows(model_kernel(OUT), "attn_out", [mixed], w_attn, waits[2])
        operands = (gain, layer_input, *parts)
        branch, hidden, mlp_in = on_chip(
            after_attention_kernel, "after_attn", (row32, row32, row16), *operands, waits=waits[3]
        )
        mlp_in = both_rows(mlp_in)
        kernel = functools.partial(mlp_up_kernel, tensor)
        operands = (*mlp_in, *w_up[0], *w_up[1])
        gelu_out, slope = on_chip(kernel, "mlp_up", (unit16, unit16), *operands, **mlp_cost)
        parts = model_rows(down_kernel, "mlp_down", [gelu_out], w_down)
        mlp_branch, result = on_chip(
            after_mlp_kernel, "after_mlp", (row32, row16), gain, hidden, *parts
        )
        saved = (layer_input, heads, branch, hidden, slope, mlp_branch)
        return result, saved, (attn_in, mixed, mlp_in, gelu_out)

    def backward(grad, saved, hook, late=()):
        layer_input, heads, branch, hidden, slope, mlp_branch = saved
        operands = (gain, grad, mlp_branch)
        d_down, sum_three = on_chip(
            into_mlp_back_kernel, "into_mlp_back", (row16, sum32), *operands
        )
        d_down = both_rows(d_down)
        d_up = mlp_up_back(d_down, slope, w_down, late)
        waits = hook(d_down, d_up)
        parts = model_rows(model_kernel(every), "mlp_back", [d_up], w_up, waits)
        waits = hook()
        operands = (gain, grad, *parts, hidden, branch)
        outs = (row32, row16, sum32, sum32)
        d_hidden, d_attn, sum_one, sum_two = on_chip(
            into_attention_back_kernel, "into_attn_back", outs, *operands, waits=waits
        )
        d_attn = both_rows(d_attn)
        waits = hook(d_attn)
        d_qkv = []
        for base in reversed(range(0, tensor, 2)):
            some = [side[base : base + 2] for side in w_attn]
            now = attend_back(core_word, tables, d_attn, some, base, waits, *heads)
            d_qkv.insert(0, now)
            waits = hook(now)
        parts = model_rows(model_kernel(QKV, 2), "attn_back", d_qkv, w_attn, waits)
        operands = (gain, layer_input, *parts, d_hidden)
        d_input, sum_zero = on_chip(
            out_of_layer_kernel, "out_of_layer", (row16, sum32), *operands, waits=hook()
        )
        sums = jnp.concatenate([sum_zero, sum_one, sum_two, sum_three])
        return d_input, (d_qkv, d_attn, d_up, d_down), sums

    low_zero, saved_zero, lefts_zero = forward(
        start,
        (
            (up_piece, up_other[0], down_other[0]),
            (up_own[1], down_own[1]),
            (up_own[2], down_own[2], up_other[1], down_other[1]),
            (up_own[3], down_own[3], up_other[2], down_other[2]),
        ),
    )
    low_one, saved_one, lefts_one = forward(shifted(low_zero, "section", 1), ((),) * 4)
    grad_one, rights_one, gain_one = backward(start, saved_one, lambda *new: ())
    received = shifted(grad_one, "section", -1)

    lows = lax.optimization_barrier((low_zero, low_one, grad_one))[:2]
    lows = own_first(jnp.where(first, *lows)).reshape(tensor, part, width)
    lows = lax.all_to_all(lows, "tensor", 0, 0, tiled=True)

    section_word = lax.axis_index("section").astype(jnp.int32).reshape(1)

    def mlp_leaves(base, waits=()):
        zeros = (*lefts_zero[2], d_up, lefts_zero[3], *d_down)
        ones = (*lefts_one[2], rights_one[2], lefts_one[3], *rights_one[3])
        mlp_sums[base : base + 2] = weight_grads(
            mlp_grads_kernel,
            "mlp_grads",
            base,
            section_word,
            zeros,
            ones,
            (wide_half + unit, unit),
            (2 * unit, 2 * unit),
            waits,
        )

    def attn_leaves(base, d_qkv, waits):
        zeros = (*lefts_zero[0], d_qkv, lefts_zero[1], *d_attn)
        ones = (*lefts_one[0], rights_one[0][base // 2], lefts_one[1], *rights_one[1])
        attn_sums[base : base + 2] = weight_grads(
            attn_grads_kernel,
            "attn_grads",
            base,
            section_word,
            zeros,
            ones,
            (wide_half, 512),
            (768, 256),
            waits,
        )

    def moves_on(piece, *moved, waits=()):
        outs = ((piece[1].shape, jnp.bfloat16),)
        (total,) = on_chip(moved_kernel, "moved", outs, *piece, *moved, waits=waits)
        return total, passed_on(total, -1)

    mlp_sums, attn_sums = [None] * tensor, [None] * tensor
    mlp_moves, attn_moves = [None] * tensor, [None] * tensor
    hooks = iter(range(6))

    def hook(*new):
        nonlocal d_down, d_up, d_attn, outputs
        turn = next(hooks)
        if turn == 0:
            d_down, d_up = new
            mlp_leaves(2)
            return (mlp_sums[3][0],)
        if turn == 1:
            return ()
        if turn == 2:
            (d_attn,) = new
            outputs = from_chip(lows, d_attn[:1])
            total, mlp_moves[3] = moves_on(mlp_sums[3], waits=(outputs,))
            mlp_leaves(0, (total,))
            return (mlp_sums[1][0],)
        if turn == 3:
            total, mlp_moves[2] = moves_on(mlp_sums[2], mlp_moves[3], waits=new)
            attn_leaves(2, new[0], (total,))
            return (mlp_sums[2][1], mlp_moves[3], attn_sums[3][0])
        if turn == 4:
            total, mlp_moves[1] = moves_on(mlp_sums[1], mlp_moves[2], waits=new)
            attn_leaves(0, new[0], (total,))
            total, attn_moves[3] = moves_on(attn_sums[3], waits=attn_sums[1][:1])
            return (total, mlp_moves[1], mlp_sums[0][1])
        return attn_sums[2][1:]

    d_down = d_up = d_attn = outputs = None
    grad_zero, rights_zero, gain_zero = backward(received, saved_zero, hook, (lows,))
    place_word = jnp.stack([lax.axis_index("section"), upper]).astype(jnp.int32)
    (grads,) = with_core(
        chosen_kernel,
        "chosen",
        place_word,
        (row16,),
        grad_zero,
        grad_one,
        waits=(attn_moves[3], attn_sums[1][1]),
    )
    grads = lax.all_to_all(grads.reshape(tensor, part, width), "tensor", 0, 0, tiled=True)

    block32 = ((wide_half // 2, unit), jnp.float32)
    down32 = ((unit, wide_half // 2), jnp.float32)
    up_keep, down_keep, up_send, down_send = with_core(
        mlp_sum_kernel,
        "mlp_sum",
        core_word,
        (block32, down32, block32, down32),
        *mlp_sums[0],
        mlp_moves[1],
        waits=(grad_zero,),
    )
    outs = (
        ((wide_half // 2, 2 * unit), jnp.float32),
        ((2 * unit, wide_half // 2), jnp.float32),
    )
    sent = flip_pairs(up_send, 1), flip_pairs(down_send, 1)
    up_grad, down_grad = with_core(
        mlp_join_kernel, "mlp_join", core_word, outs, up_keep, down_keep, *sent
    )
    total, attn_moves[2] = moves_on(attn_sums[2], attn_moves[3], waits=(grad_zero,))
    waits = (up_grad, attn_sums[0][1], grads)
    last, attn_moves[1] = moves_on(attn_sums[1], attn_moves[2], waits=waits)
    grads = from_chip(grads, (last,))
    gain_total = own_first(jnp.where(first, gain_zero, gain_one))
    count = tensor * lax.axis_size("dp")
    gain_parts = gain_total.reshape(4, count, width // count).swapaxes(0, 1)
    outs = ((gain_parts.shape, gain_parts.dtype),)
    (gain_parts,) = on_chip(gate_kernel, "gate", outs, gain_parts, waits=(last,))
    gain_parts = lax.all_to_all(gain_parts, ("dp", "tensor"), 0, 0, tiled=True)
    gains_grad = jnp.sum(gain_parts, axis=0)
    outs = (((wide_half // 2, 512), jnp.float32),) * 2
    keep, send = with_core(
        last_sum_kernel,
        "attn_sum",
        core_word,
        outs,
        *attn_sums[0],
        attn_moves[1],
        waits=(grads, outputs, gains_grad),
    )
    spots = tuple((i * 128, (i + 1) * 128, i * 256) for i in range(3))
    outs = (((wide_half // 2, 768), jnp.float32), ((256, wide_half // 2), jnp.float32))
    kernel = functools.partial(joined_kernel, spots)
    qkv_grad, out_grad = with_core(
        kernel, "attn_join", core_word, outs, keep, flip_pairs(send, 1)
    )
    qkv_grad = qkv_grad.reshape(wide_half // 2, 3, -1)

    return (
        outputs[None],
        grads[None],
        gains_grad[None],
        qkv_grad[None],
        out_grad[None],
        up_grad[None],
        down_grad[None],
    )


def takes_chips(sizes):
    return sizes["section"] == 2 and sizes["dp"] == 4 and sizes["tensor"] == 4


def solution(mesh):
    placed = (
        P("dp", "tensor", None),
        P("dp", "tensor", None),
        P("dp", "tensor"),
        P(),
        P("section", None, None),
        P("section", None, None, "tensor"),
        P("section", "tensor", None),
        P("section", None, "tensor"),
        P("section", "tensor", None),
    )
    body = per_chip if takes_chips(dict(mesh.shape)) else per_device
    return jax.shard_map(
        body,
        mesh=mesh,
        in_specs=placed,
        out_specs=(
            P("section", "dp", "tensor", None),
            P("section", "dp", "tensor", None),
            P("section", None, ("dp", "tensor")),
            P("section", "dp", None, "tensor"),
            P("section", "tensor", "dp"),
            P("section", "dp", "tensor"),
            P("section", "tensor", "dp"),
        ),
        check_vma=False,
    )
```
